32 devices in a mesh: fsdp: 2 (over x), context: 4 (over z), tensor: 4 (over y, core).
Axes of the slice: x: 2, y: 2, z: 4, core: 2. Of those that a mesh axis runs over, the one named last changes fastest.
Arguments:
- inputs: bfloat16 [4096, 1536], P(('fsdp', 'context')), may hold values from -6 to 6
- cotangent: bfloat16 [4096, 1536], P(('fsdp', 'context')), may hold values from -6 to 6
- blocks: int32 [2, 8], P('fsdp'), may hold values from 0 to 7, each once within a row
- attn_gain: bfloat16 [1536], P('fsdp'), may hold values from 0.25 to 1.75
- w_query: bfloat16 [1536, 1536], P('fsdp', 'tensor'), may hold values from -0.21875 to 0.21875
- b_query: bfloat16 [12, 128], P('tensor', 'fsdp'), may hold values from -3 to 3
- w_key: bfloat16 [1536, 256], P('fsdp'), may hold values from -0.21875 to 0.21875
- b_key: bfloat16 [2, 128], P(None, 'fsdp'), may hold values from -3 to 3
- w_value: bfloat16 [1536, 256], P('fsdp'), may hold values from -0.15625 to 0.15625
- b_value: bfloat16 [2, 128], P(None, 'fsdp'), may hold values from -3 to 3
- w_out: bfloat16 [1536, 1536], P('tensor', 'fsdp'), may hold values from -1 to 1
- ffn_gain: bfloat16 [1536], P('fsdp'), may hold values from 0.25 to 1.75
- w_gate: bfloat16 [1536, 8960], P('fsdp', 'tensor'), may hold values from -0.15625 to 0.15625
- w_up: bfloat16 [1536, 8960], P('fsdp', 'tensor'), may hold values from -0.15625 to 0.15625
- w_down: bfloat16 [8960, 1536], P('tensor', 'fsdp'), may hold values from -0.09375 to 0.09375
Outputs:
- outputs: bfloat16 [4096, 1536], P(('fsdp', 'context'))
- input_grad: bfloat16 [4096, 1536], P(('fsdp', 'context'))
- attn_gain_grad: float32 [1536], P('fsdp')
- w_query_grad: float32 [1536, 1536], P('fsdp', 'tensor')
- b_query_grad: float32 [12, 128], P('tensor', 'fsdp')
- w_key_grad: float32 [1536, 256], P('fsdp')
- b_key_grad: float32 [2, 128], P(None, 'fsdp')
- w_value_grad: float32 [1536, 256], P('fsdp')
- b_value_grad: float32 [2, 128], P(None, 'fsdp')
- w_out_grad: float32 [1536, 1536], P('tensor', 'fsdp')
- ffn_gain_grad: float32 [1536], P('fsdp')
- w_gate_grad: float32 [1536, 8960], P('fsdp', 'tensor')
- w_up_grad: float32 [1536, 8960], P('fsdp', 'tensor')
- w_down_grad: float32 [8960, 1536], P('tensor', 'fsdp')
The draws below stay inside these ranges and needn't reach their ends.
Inputs may be any that keep to these rules, and one draw needn't show every extreme that they name: `blocks`: each row lists every block number of 0 to 7 once.
All inputs are finite; a program needn't handle non-finite values.
Results may differ from the reference program's by a relative error of at most 0.02.
Values may be sent and summed in bfloat16 or wider, within the bound.
A program may use at most 192 MiB of HBM per device.

```python
import jax
import jax.numpy as jnp
from jax import lax

D = 1536
H = 12
KV = 2
HD = 128
FF = 8960
BLOCK = 256
NBLK = 8
SEQS = 2
TOKENS = 4096


def block_scale(own_key, extent, cuts, least, largest):
    def one(dim, shards_of):
        draws = jax.random.uniform(jax.random.fold_in(jax.random.fold_in(own_key, 6), dim), (shards_of,), jnp.float32, least / len(cuts), largest / len(cuts))
        return jnp.repeat(jnp.exp(draws), extent[dim] // shards_of).reshape((-1,) + (1,) * (len(extent) - dim - 1))

    level = one(*cuts[0])
    for cut in cuts[1:]:
        level = level * one(*cut)
    return level


def gaussian(rng, shape, deviation, bound, cuts=(), kind=jnp.bfloat16):
    factor_of = block_scale(rng, shape, cuts, -0.22, 0.18) if cuts else 1.0
    entries = jax.random.normal(rng, shape, jnp.float32) * deviation * factor_of
    return jnp.minimum(jnp.maximum(entries, -bound), bound).astype(kind)


def setup_inputs(seed: int = 0) -> dict:
    seeds = jax.random.split(jax.random.key(seed), 16)
    inputs = gaussian(seeds[0], (TOKENS, D), 1.0, 6.0, ((0, 8),))
    cotangent = gaussian(seeds[1], (TOKENS, D), 1.0, 6.0, ((0, 8),))
    blocks = jax.vmap(lambda own: jax.random.permutation(own, NBLK))(jax.random.split(seeds[2], SEQS)).reshape((SEQS, NBLK)).astype(jnp.int32)
    attn_gain = jnp.clip(1.0 + 0.15 * jax.random.normal(seeds[3], (D,), jnp.float32), 0.25, 1.75).astype(jnp.bfloat16)
    w_query = gaussian(seeds[4], (D, H * HD), (D // 2) ** -0.5, 0.21875, ((0, 2), (1, 4)))
    b_query = gaussian(seeds[5], (H, HD), 0.5, 3.0, ((0, 4), (1, 2)))
    w_key = gaussian(seeds[6], (D, KV * HD), (D // 2) ** -0.5, 0.21875, ((0, 2),))
    b_key = gaussian(seeds[7], (KV, HD), 0.5, 3.0, ((1, 2),))
    w_value = gaussian(seeds[8], (D, KV * HD), D ** -0.5, 0.15625, ((0, 2),))
    b_value = gaussian(seeds[9], (KV, HD), 0.5, 3.0, ((1, 2),))
    w_out = gaussian(seeds[10], (H * HD, D), (max(H * HD // 48, 16)) ** -0.5, 1.0, ((0, 4), (1, 2)))
    ffn_gain = jnp.clip(1.0 + 0.15 * jax.random.normal(seeds[11], (D,), jnp.float32), 0.25, 1.75).astype(jnp.bfloat16)
    w_gate = gaussian(seeds[12], (D, FF), D ** -0.5, 0.15625, ((0, 2), (1, 4)))
    w_up = gaussian(seeds[13], (D, FF), D ** -0.5, 0.15625, ((0, 2), (1, 4)))
    w_down = gaussian(seeds[14], (FF, D), (FF // 2) ** -0.5, 0.09375, ((0, 4), (1, 2)))
    return {"inputs": inputs, "cotangent": cotangent, "blocks": blocks, "attn_gain": attn_gain, "w_query": w_query, "b_query": b_query, "w_key": w_key, "b_key": b_key, "w_value": w_value, "b_value": b_value, "w_out": w_out, "ffn_gain": ffn_gain, "w_gate": w_gate, "w_up": w_up, "w_down": w_down}


@jax.custom_vjp
def low(v):
    return lax.optimization_barrier(v.astype(jnp.bfloat16)).astype(jnp.float32)

@jax.custom_vjp
def low_back(v):
    return v

def low_keep(v):
    return (low(v), None)

def low_pass(kept, grad):
    return (grad,)

def back_keep(v):
    return (v, None)

def back_low(kept, grad):
    return (low(grad),)
low.defvjp(low_keep, low_pass)
low_back.defvjp(back_keep, back_low)
EPSILON = 1e-06
ROPE_BASE = 1000000.0
MASKED = -1e+30

def product(left, right):
    return jnp.dot(left, right, precision=lax.Precision.HIGHEST, preferred_element_type=jnp.float32)

def rope_tables(positions):
    halfway = HD // 2
    frequency = ROPE_BASE ** (-(jnp.arange(halfway, dtype=jnp.float32) * 2.0 / HD))
    angles = positions.astype(jnp.float32)[:, None] * frequency[None, :]
    cosine = jnp.concatenate([jnp.cos(angles), jnp.cos(angles)], axis=1)
    sine = jnp.concatenate([jnp.sin(angles), jnp.sin(angles)], axis=1)
    return (cosine, sine)

def rotate(field, cosine, sine):
    halfway = HD // 2
    turned = jnp.concatenate([-field[..., halfway:], field[..., :halfway]], axis=-1)
    return field * cosine[:, None, :] + turned * sine[:, None, :]

def rms_norm(values, gain):
    return values * lax.rsqrt(lax.optimization_barrier(jnp.mean(values * values, axis=-1, keepdims=True)) + EPSILON) * gain

def attention(queries, keys, values, allowed):
    scaling = HD ** (-0.5)

    def one_head(head_index):
        key_group = head_index // (H // KV)
        query_head = lax.dynamic_index_in_dim(queries, head_index, 1, keepdims=False)
        key_head = lax.dynamic_index_in_dim(keys, key_group, 1, keepdims=False)
        value_head = lax.dynamic_index_in_dim(values, key_group, 1, keepdims=False)
        raw_scores = low_back(product(query_head, key_head.T) * scaling)
        scores = jnp.where(allowed, raw_scores, MASKED)
        row_max = lax.optimization_barrier(jnp.max(scores, axis=1, keepdims=True))
        expo = jnp.exp(scores - row_max)
        probability = expo / lax.optimization_barrier(jnp.sum(expo, axis=1, keepdims=True))
        return product(low(probability), value_head)
    heads_out = lax.map(jax.checkpoint(one_head), jnp.arange(H, dtype=jnp.int32))
    return jnp.transpose(heads_out, (1, 0, 2)).reshape(queries.shape[0], H * HD)

def layer(inputs, block_ids, params):
    attn_gain, w_query, b_query, w_key, b_key, w_value, b_value, w_out, ffn_gain, w_gate, w_up, w_down = params
    length = inputs.shape[0]
    block_of_row = jnp.repeat(block_ids, BLOCK, total_repeat_length=length)
    positions = block_of_row * BLOCK + jnp.arange(length, dtype=jnp.int32) % BLOCK
    cosine, sine = rope_tables(positions)
    normed = low(rms_norm(inputs, attn_gain))
    query_pre = low_back(product(normed, w_query).reshape(length, H, HD) + b_query)
    key_pre = low_back(product(normed, w_key).reshape(length, KV, HD) + b_key)
    value_pre = low_back(product(normed, w_value).reshape(length, KV, HD) + b_value)
    queries = low(rotate(query_pre, cosine, sine))
    keys = low(rotate(key_pre, cosine, sine))
    values = low(value_pre)
    allowed = block_of_row[None, :] <= block_of_row[:, None]
    attended = low(low_back(attention(queries, keys, values, allowed)))
    middle = inputs + low_back(product(attended, w_out))
    normed2 = low(rms_norm(middle, ffn_gain))
    gate_pre = low_back(product(normed2, w_gate))
    up_pre = low_back(product(normed2, w_up))
    hidden = low(gate_pre * jax.nn.sigmoid(gate_pre) * up_pre)
    return middle + product(hidden, w_down)

def reference(inputs, cotangent, blocks, attn_gain, w_query, b_query, w_key, b_key, w_value, b_value, w_out, ffn_gain, w_gate, w_up, w_down):
    weights = tuple((weight_arg.astype(jnp.float32) for weight_arg in (attn_gain, w_query, b_query, w_key, b_key, w_value, b_value, w_out, ffn_gain, w_gate, w_up, w_down)))
    length = inputs.shape[0] // SEQS
    start = inputs.astype(jnp.float32).reshape(SEQS, length, D)

    def forward(whole, *params):

        def per_sequence(ignored, seq_pair):
            return (ignored, layer(seq_pair[0], seq_pair[1], params))
        ignored, result = lax.scan(per_sequence, None, (whole, blocks))
        return result
    result, pullback = jax.vjp(forward, start, *weights)
    grads = pullback(cotangent.astype(jnp.float32).reshape(SEQS, length, D))
    outputs = result.reshape(-1, D).astype(jnp.bfloat16)
    input_grad = grads[0].reshape(-1, D).astype(jnp.bfloat16)
    return (outputs, input_grad, grads[1], grads[2], grads[3], grads[4], grads[5], grads[6], grads[7], grads[8], grads[9], grads[10], grads[11], grads[12])
```

```python
import functools

import jax
import jax.numpy as jnp
from jax import lax
from jax.experimental import pallas as pl
from jax.experimental.pallas import tpu as pltpu
from jax.sharding import PartitionSpec as P

H = 12
KV = 2
HD = 128
BLOCK = 256

EPSILON = 1e-06
ROPE_BASE = 1000000.0
MASKED = -1e30
SCALING = HD ** (-0.5)
LANES = 128
VMEM_LIMIT = 60 << 20

f32 = jnp.float32
bf16 = jnp.bfloat16


def rope_tables(positions):
    halfway = HD // 2
    frequency = ROPE_BASE ** (-(jnp.arange(halfway, dtype=f32) * 2.0 / HD))
    angles = positions.astype(f32)[:, None] * frequency[None, :]
    cosine, sine = jnp.cos(angles), jnp.sin(angles)
    return (jnp.concatenate([cosine, cosine], axis=1), jnp.concatenate([sine, sine], axis=1))


def rotate(field, cosine, sine):
    halfway = HD // 2
    turned = jnp.concatenate([-field[..., halfway:], field[..., :halfway]], axis=-1)
    return field * cosine + turned * sine


def rotate_back(grad_field, cosine, sine):
    halfway = HD // 2
    moved = grad_field * sine
    turned = jnp.concatenate([moved[..., halfway:], -moved[..., :halfway]], axis=-1)
    return grad_field * cosine + turned


def rms_scale(values):
    return lax.rsqrt(jnp.mean(values * values, axis=-1, keepdims=True) + EPSILON)


def norm_back(values, factor, gain, grad_normed):
    gained = gain * grad_normed
    inner = jnp.mean(gained * values, axis=-1, keepdims=True)
    grad_values = factor * gained - values * (factor * factor * factor) * inner
    return (grad_values, jnp.sum(grad_normed * values * factor, axis=0))


def dot(left, right):
    return jnp.dot(left, right, preferred_element_type=f32)


def dot_rows(left, right):
    return lax.dot_general(left, right, (((0,), (0,)), ((), ())), preferred_element_type=f32)


def dot_cols(left, right):
    return lax.dot_general(left, right, (((1,), (1,)), ((), ())), preferred_element_type=f32)


def mask_row(kb_ref, own_block, key_blocks):
    return jnp.concatenate(
        [
            jnp.full((1, BLOCK), jnp.where(kb_ref[j] <= own_block, 0.0, MASKED), f32)
            for j in range(key_blocks)
        ],
        axis=1,
    )


def attention_kernel(key_blocks, kb_ref, q_ref, k_ref, v_ref, o_ref, lse_ref):
    bias = mask_row(kb_ref, kb_ref[pl.program_id(1)], key_blocks)
    scores = dot_cols(q_ref[...], k_ref[...]) * SCALING + bias
    row_max = jnp.max(scores, axis=1, keepdims=True)
    expo = jnp.exp(scores - row_max)
    total = jnp.sum(expo, axis=1, keepdims=True)
    probability = (expo * (1.0 / total)).astype(bf16)
    o_ref[...] = dot(probability, v_ref[...]).astype(bf16)
    lse_ref[0] = row_max + jnp.log(total)


def attention(key_blocks, queries, keys, values):
    rows, width = queries.shape
    heads = width // HD
    whole = pl.BlockSpec(keys.shape, lambda h, i, kb: (0, 0))
    tile = pl.BlockSpec((BLOCK, HD), lambda h, i, kb: (i, h))
    return pl.pallas_call(
        functools.partial(attention_kernel, keys.shape[0] // BLOCK),
        name="attention",
        grid_spec=pltpu.PrefetchScalarGridSpec(
            num_scalar_prefetch=1,
            grid=(heads, rows // BLOCK),
            in_specs=[tile, whole, whole],
            out_specs=[tile, pl.BlockSpec((1, BLOCK, 1), lambda h, i, kb: (h, i, 0))],
        ),
        out_shape=[
            jax.ShapeDtypeStruct((rows, width), bf16),
            jax.ShapeDtypeStruct((heads, rows, 1), f32),
        ],
        compiler_params=pltpu.CompilerParams(vmem_limit_bytes=VMEM_LIMIT),
        cost_estimate=pl.CostEstimate(
            flops=4 * rows * keys.shape[0] * width,
            bytes_accessed=4 * rows * width + 4 * keys.size,
            transcendentals=rows * keys.shape[0] * heads,
        ),
    )(key_blocks, queries, keys, values)


def attention_back_kernel(
    key_blocks,
    kb_ref,
    q_ref,
    do_ref,
    lse_ref,
    cos_ref,
    sin_ref,
    k_ref,
    v_ref,
    dq_ref,
    dk_ref,
    dv_ref,
):
    head, i = pl.program_id(0), pl.program_id(1)

    @pl.when((head == 0) & (i == 0))
    def _():
        dk_ref[...] = jnp.zeros_like(dk_ref)
        dv_ref[...] = jnp.zeros_like(dv_ref)

    bias = mask_row(kb_ref, kb_ref[i], key_blocks)
    scores = dot_cols(q_ref[...], k_ref[...]) * SCALING + bias
    probability = jnp.exp(scores - lse_ref[0])
    grad_probs = dot_cols(do_ref[...], v_ref[...])
    inner = jnp.sum(probability * grad_probs, axis=1, keepdims=True)
    grad_scores = (probability * (grad_probs - inner)).astype(bf16)
    grad_query = dot(grad_scores, k_ref[...]) * SCALING
    moved = grad_query * sin_ref[...]
    sign = jnp.where(lax.broadcasted_iota(jnp.int32, moved.shape, 1) < HD // 2, 1.0, -1.0)
    dq_ref[...] = (
        grad_query * cos_ref[...] + pltpu.roll(moved, HD // 2, 1) * sign
    ).astype(bf16)
    dk_ref[...] += dot_rows(grad_scores, q_ref[...]) * SCALING
    dv_ref[...] += dot_rows(probability.astype(bf16), do_ref[...])


def attention_back(key_blocks, queries, grad_out, lse, cosine, sine, keys, values):
    rows, width = queries.shape
    heads = width // HD
    whole = pl.BlockSpec(keys.shape, lambda h, i, kb: (0, 0))
    tile = pl.BlockSpec((BLOCK, HD), lambda h, i, kb: (i, h))
    table = pl.BlockSpec((BLOCK, HD), lambda h, i, kb: (i, 0))
    return pl.pallas_call(
        functools.partial(attention_back_kernel, keys.shape[0] // BLOCK),
        name="attention_back",
        grid_spec=pltpu.PrefetchScalarGridSpec(
            num_scalar_prefetch=1,
            grid=(heads, rows // BLOCK),
            in_specs=[
                tile,
                tile,
                pl.BlockSpec((1, BLOCK, 1), lambda h, i, kb: (h, i, 0)),
                table,
                table,
                whole,
                whole,
            ],
            out_specs=[tile, whole, whole],
        ),
        out_shape=[
            jax.ShapeDtypeStruct((rows, width), bf16),
            jax.ShapeDtypeStruct(keys.shape, f32),
            jax.ShapeDtypeStruct(keys.shape, f32),
        ],
        compiler_params=pltpu.CompilerParams(vmem_limit_bytes=VMEM_LIMIT),
        cost_estimate=pl.CostEstimate(
            flops=10 * rows * keys.shape[0] * width,
            bytes_accessed=6 * rows * width + 12 * keys.size,
            transcendentals=rows * keys.shape[0] * heads,
        ),
    )(key_blocks, queries, grad_out, lse, cosine, sine, keys, values)


def ffn_kernel(with_dx, base_ref, x_ref, dy_ref, wg_ref, wu_ref, wd_ref, *refs):
    hid_ref, dg_ref, du_ref = refs[-4:-1] if with_dx else refs[-3:]
    gate = dot(x_ref[...], wg_ref[...])
    up = dot(x_ref[...], wu_ref[...])
    grad_hidden = dot_cols(dy_ref[...], wd_ref[...])
    sigma = 1.0 / (1.0 + jnp.exp(-gate))
    gated = gate * sigma
    hid_ref[...] = (gated * up).astype(bf16)
    grad_gate = (grad_hidden * up * (sigma + gated * (1.0 - sigma))).astype(bf16)
    grad_up = (grad_hidden * gated).astype(bf16)
    dg_ref[...] = grad_gate
    du_ref[...] = grad_up
    if with_dx:
        refs[-1][...] = (dot_cols(grad_gate, wg_ref[...]) + dot_cols(grad_up, wu_ref[...])).astype(
            bf16
        )


def ffn(base, normed, grad_out, wg, wu, wd, filled=None):
    rows, width = normed.shape
    units = wg.shape[1]
    tile = 512
    steps = rows // tile
    with_dx = filled is None
    row = lambda n: pl.BlockSpec((tile, n), lambda i, b: (i, 0))
    weight = lambda w: pl.BlockSpec(
        w.shape, lambda i, b: (0, 0), pipeline_mode=pl.Buffered(1)
    )
    out_row = pl.BlockSpec((tile, units), lambda i, b: (i + b[0] * steps, 0))
    out_specs = [out_row] * 3
    out_shape = [jax.ShapeDtypeStruct((2 * rows, units), bf16)] * 3
    in_specs = [row(width), row(width), weight(wg), weight(wu), weight(wd)]
    args = [base, normed, grad_out, wg, wu, wd]
    aliases = {}
    if with_dx:
        out_specs = out_specs + [row(width)]
        out_shape = out_shape + [jax.ShapeDtypeStruct((rows, width), bf16)]
    else:
        in_specs = in_specs + [pl.BlockSpec(memory_space=pl.ANY)] * 3
        args = args + list(filled)
        aliases = {6: 0, 7: 1, 8: 2}
    return pl.pallas_call(
        functools.partial(ffn_kernel, with_dx),
        name="ffn_pair" if with_dx else "ffn_far",
        grid_spec=pltpu.PrefetchScalarGridSpec(
            num_scalar_prefetch=1, grid=(steps,), in_specs=in_specs, out_specs=out_specs
        ),
        out_shape=out_shape,
        input_output_aliases=aliases,
        compiler_params=pltpu.CompilerParams(vmem_limit_bytes=VMEM_LIMIT),
        cost_estimate=pl.CostEstimate(
            flops=2 * rows * width * units * (5 if with_dx else 3),
            bytes_accessed=2 * (3 * width * units + 3 * rows * units + 3 * rows * width),
            transcendentals=rows * units,
        ),
    )(*args)


def build(n_f, n_c, n_t):
    def flip(x, axis, bit):
        size = {"fsdp": n_f, "context": n_c, "tensor": n_t}[axis]
        return lax.ppermute(x, axis, [(i, i ^ bit) for i in range(size)])

    def by_bit(bit, x, other, axis):
        return jnp.where(
            bit == 0,
            jnp.concatenate([x, other], axis=axis),
            jnp.concatenate([other, x], axis=axis),
        )

    def local(
        inputs,
        cotangent,
        blocks,
        attn_gain,
        w_query,
        b_query,
        w_key,
        b_key,
        w_value,
        b_value,
        w_out,
        ffn_gain,
        w_gate,
        w_up,
        w_down,
    ):
        rows, width = inputs.shape
        f = lax.axis_index("fsdp")
        c = lax.axis_index("context")
        t = lax.axis_index("tensor")
        core, parity, pair = t % 2, c % 2, c // 2
        heads = w_query.shape[1] // HD
        group = (t * heads) // (H // KV)
        part = rows // n_t
        units_all = w_gate.shape[1]
        units = -(-units_all // (2 * LANES)) * LANES

        def gather_f(x, axis):
            if n_f == 2:
                return by_bit(f, x, flip(x, "fsdp", 1), axis)
            return lax.all_gather(x, "fsdp", axis=axis, tiled=True)

        def grad_f(left, right, side):
            if n_f == 2:
                half = width // 2
                source = (left, right)[side]
                own = lax.dynamic_slice_in_dim(source, f * half, half, 1)
                far = lax.dynamic_slice_in_dim(source, (1 - f) * half, half, 1)
                pick = lambda x: dot_rows(x, right) if side == 0 else dot_rows(left, x)
                got = flip(pick(far).astype(bf16), "fsdp", 1)
                return pick(own) + got.astype(f32)
            return lax.psum_scatter(
                dot_rows(left, right).astype(bf16), "fsdp", scatter_dimension=side, tiled=True
            ).astype(f32)

        def sum_c(x):
            for bit in (1, 2):
                low = x.astype(bf16)
                x = low.astype(f32) + flip(low, "context", bit).astype(f32)
            return x

        order = (0, 2, 1, 3)

        def mixed(x):
            return jnp.concatenate(
                [lax.dynamic_slice_in_dim(x, (t ^ j) * part, part, 0) for j in order], axis=0
            )

        def natural(x):
            blocks_of = [x[i * part : (i + 1) * part] for i in range(n_t)]
            place = [blocks_of[order.index(j)] for j in range(n_t)]
            out = jnp.stack(place)
            return jnp.concatenate(
                [lax.dynamic_index_in_dim(out, n ^ t, 0, keepdims=False) for n in range(n_t)],
                axis=0,
            )

        def add_half(x, axis, bit):
            half = x.shape[0] // 2
            got = flip(x[half:].astype(bf16), axis, bit)
            return x[:half].astype(f32) + got.astype(f32)

        def scatter_t(x):
            return add_half(add_half(x, "tensor", 1), "tensor", 2)

        def scatter_pair(x):
            return add_half(add_half(add_half(x, "tensor", 1), "context", 1), "tensor", 2)

        def grow(x, axis, bit):
            return jnp.concatenate([x, flip(x, axis, bit)], axis=0)

        def gather_t(x):
            return grow(grow(x, "tensor", 2), "tensor", 1)

        def gather_pair(x):
            return grow(grow(grow(x, "tensor", 2), "context", 1), "tensor", 1)

        small = jnp.concatenate(
            [v.reshape(1, -1) for v in (attn_gain, ffn_gain, b_query, b_key, b_value)], axis=1
        )
        column = lambda w: lax.dynamic_slice_in_dim(w, group * HD, HD, 1)
        w_kv_own = jnp.where(core == 0, column(w_key), column(w_value))
        w_qkv = gather_f(jnp.concatenate([w_query, w_kv_own], axis=1), 0)
        small = gather_f(small, 0)
        w_out_all = gather_f(w_out, 1)
        piece = attn_gain.shape[0]
        gain_first = small[:, :piece].reshape(1, width).astype(f32)
        gain_second = small[:, piece : 2 * piece].reshape(1, width).astype(f32)
        bias_of = lambda lo, n: (
            small[:, lo : lo + n * (HD // n_f)]
            .reshape(n_f, n, HD // n_f)
            .transpose(1, 0, 2)
            .reshape(n, HD)
            .astype(f32)
        )
        at = 2 * piece
        bq = bias_of(at, heads)
        bk = bias_of(at + heads * (HD // n_f), KV)
        bv = bias_of(at + (heads + KV) * (HD // n_f), KV)
        b_kv = lax.dynamic_index_in_dim(jnp.where(core == 0, bk, bv), group, 0)

        def unit_slice(w, axis):
            low = lax.slice_in_dim(w, 0, units, axis=axis)
            high = lax.slice_in_dim(w, units, units_all, axis=axis)
            pad = [(0, 0), (0, 0)]
            pad[axis] = (0, 2 * units - units_all)
            return jnp.where(parity == 0, low, jnp.pad(high, pad))

        wg = gather_f(unit_slice(w_gate, 1), 0)
        wu = gather_f(unit_slice(w_up, 1), 0)
        wd = gather_f(unit_slice(w_down, 0), 1)

        dy_own = mixed(cotangent)[: 2 * part]
        dy_near = jnp.concatenate([dy_own, flip(dy_own, "context", 1)], axis=0)
        dy_pair = grow(dy_near, "tensor", 1)
        dy_far = grow(grow(flip(dy_own, "context", 2), "context", 1), "tensor", 1)

        seq_blocks = blocks[0].reshape(n_c, -1)
        own_blocks = seq_blocks.shape[1]
        key_blocks = jnp.concatenate(
            [lax.dynamic_index_in_dim(seq_blocks, c ^ j, 0, keepdims=False) for j in range(n_c)]
        )
        positions = (
            key_blocks[:own_blocks, None] * BLOCK + jnp.arange(BLOCK, dtype=jnp.int32)[None, :]
        ).reshape(-1)
        cosine, sine = rope_tables(positions)
        inputs_f = inputs.astype(f32)
        factor_first = rms_scale(inputs_f)
        normed = (inputs_f * factor_first * gain_first).astype(bf16)
        qkv_pre = dot(normed, w_qkv)
        query_pre = qkv_pre[:, : heads * HD].reshape(rows, heads, HD) + bq
        queries = (
            rotate(query_pre, cosine[:, None, :], sine[:, None, :])
            .astype(bf16)
            .reshape(rows, heads * HD)
        )
        kv_pre = qkv_pre[:, heads * HD :] + b_kv
        kv_own = jnp.where(core == 0, rotate(kv_pre, cosine, sine), kv_pre).astype(bf16)
        kv_whole = grow(grow(kv_own, "context", 1), "context", 2)
        kv_other = flip(kv_whole, "tensor", 1)
        keys = jnp.where(core == 0, kv_whole, kv_other)
        values = jnp.where(core == 0, kv_other, kv_whole)
        attended, lse = attention(key_blocks, queries, keys, values)

        attended_mixed = mixed(attended)
        attn_sum = scatter_t(dot(attended_mixed, w_out_all))
        middle = lax.dynamic_slice_in_dim(inputs, t * part, part, 0).astype(f32) + attn_sum

        factor_second = rms_scale(middle)
        normed2 = (middle * factor_second * gain_second).astype(bf16)
        normed2_pair = gather_pair(normed2)
        normed2_far = gather_pair(flip(normed2, "context", 2))
        base = pair.reshape(1)
        *half_filled, dx_part = ffn(base, normed2_pair, dy_pair, wg, wu, wd)
        grad_normed2 = scatter_pair(dx_part)
        hidden, grad_gate, grad_up = ffn(
            1 - base, normed2_far, dy_far, wg, wu, wd, filled=half_filled
        )
        hidden_pair = lax.dynamic_slice_in_dim(hidden, pair * 2 * rows, 2 * rows, 0)
        final = middle + scatter_pair(dot(hidden_pair, wd))
        outputs = natural(gather_t(final.astype(bf16)))

        normed2_all = by_bit(pair, normed2_pair, normed2_far, 0)
        dy_all = by_bit(pair, dy_pair, dy_far, 0)

        def unit_grad(left, right, side):
            own = grad_f(left, right, side).astype(bf16)
            other = flip(own, "context", 1)
            whole = by_bit(parity, own, other, 1 - side)
            return lax.slice_in_dim(whole, 0, units_all, axis=1 - side).astype(f32)

        wd_grad = unit_grad(hidden, dy_all, 1)
        wg_grad = unit_grad(normed2_all, grad_gate, 0)
        wu_grad = unit_grad(normed2_all, grad_up, 0)

        grad_mid_norm, ffn_gain_grad = norm_back(middle, factor_second, gain_second, grad_normed2)
        dy_part = lax.dynamic_slice_in_dim(cotangent, t * part, part, 0).astype(f32)
        grad_middle = dy_part + grad_mid_norm
        grad_middle_low = gather_t(grad_middle.astype(bf16))
        wo_grad = sum_c(grad_f(attended_mixed, grad_middle_low, 1))
        grad_attended = natural(dot_cols(grad_middle_low, w_out_all).astype(bf16))

        dq_low, dk, dv = attention_back(
            key_blocks, queries, grad_attended, lse, cosine, sine, keys, values
        )
        dkv_keep = jnp.where(core == 0, dk, dv)
        dkv_send = jnp.where(core == 0, dv, dk).astype(bf16)
        dkv = dkv_keep + flip(dkv_send, "tensor", 1).astype(f32)
        dkv = add_half(add_half(dkv, "context", 2), "context", 1)
        dkv_low = jnp.where(core == 0, rotate_back(dkv, cosine, sine), dkv).astype(bf16)
        wq_grad = sum_c(grad_f(normed, dq_low, 0))
        wkv_own = sum_c(grad_f(normed, dkv_low, 0)).astype(bf16)
        wkv_stack = gather_t(wkv_own)
        depth = wkv_own.shape[0]
        wkv_of = [wkv_stack[order.index(j) * depth : (order.index(j) + 1) * depth] for j in range(n_t)]
        wkv_stack = jnp.stack(wkv_of)
        wkv_rank = [
            lax.dynamic_index_in_dim(wkv_stack, n ^ t, 0, keepdims=False).astype(f32)
            for n in range(n_t)
        ]
        wk_grad = jnp.concatenate(wkv_rank[0::2], axis=1)
        wv_grad = jnp.concatenate(wkv_rank[1::2], axis=1)

        d_qkv = mixed(jnp.concatenate([dq_low, dkv_low], axis=1))
        grad_normed = scatter_t(dot_cols(d_qkv, w_qkv))
        inputs_part = lax.dynamic_slice_in_dim(inputs, t * part, part, 0).astype(f32)
        factor_part = lax.dynamic_slice_in_dim(factor_first, t * part, part, 0)
        grad_in_norm, attn_gain_grad = norm_back(inputs_part, factor_part, gain_first, grad_normed)
        input_grad = natural(gather_t((grad_middle + grad_in_norm).astype(bf16)))

        bq_grad = jnp.sum(dq_low.astype(f32), axis=0)
        bkv_grad = jnp.sum(dkv_low.astype(f32), axis=0)
        slots = jnp.zeros((n_t, (heads + 1) * HD), f32)
        slots = lax.dynamic_update_slice(
            slots, jnp.concatenate([bq_grad, bkv_grad])[None], (t, 0)
        )
        packed = lax.psum(
            jnp.concatenate([attn_gain_grad, ffn_gain_grad, slots.reshape(-1)]),
            ("fsdp", "context", "tensor"),
        )
        attn_gain_grad = lax.dynamic_slice_in_dim(packed, f * piece, piece, 0)
        ffn_gain_grad = lax.dynamic_slice_in_dim(packed, width + f * piece, piece, 0)
        slots = packed[2 * width :].reshape(n_t, heads + 1, HD)
        slots = lax.dynamic_slice_in_dim(slots, f * (HD // n_f), HD // n_f, 2)
        bq_out = lax.dynamic_index_in_dim(slots, t, 0, keepdims=False)[:heads]
        bk_out = slots[0::2, heads]
        bv_out = slots[1::2, heads]

        return (
            outputs,
            input_grad,
            attn_gain_grad,
            wq_grad,
            bq_out,
            wk_grad,
            bk_out,
            wv_grad,
            bv_out,
            wo_grad,
            ffn_gain_grad,
            wg_grad,
            wu_grad,
            wd_grad,
        )

    return local


def solution(mesh):
    in_specs = (
        P(("fsdp", "context"), None),
        P(("fsdp", "context"), None),
        P("fsdp", None),
        P("fsdp"),
        P("fsdp", "tensor"),
        P("tensor", "fsdp"),
        P("fsdp", None),
        P(None, "fsdp"),
        P("fsdp", None),
        P(None, "fsdp"),
        P("tensor", "fsdp"),
        P("fsdp"),
        P("fsdp", "tensor"),
        P("fsdp", "tensor"),
        P("tensor", "fsdp"),
    )
    out_specs = (
        P(("fsdp", "context"), None),
        P(("fsdp", "context"), None),
        P("fsdp"),
        P("fsdp", "tensor"),
        P("tensor", "fsdp"),
        P("fsdp", None),
        P(None, "fsdp"),
        P("fsdp", None),
        P(None, "fsdp"),
        P("tensor", "fsdp"),
        P("fsdp"),
        P("fsdp", "tensor"),
        P("fsdp", "tensor"),
        P("tensor", "fsdp"),
    )
    local = build(mesh.shape["fsdp"], mesh.shape["context"], mesh.shape["tensor"])
    return jax.shard_map(local, mesh=mesh, in_specs=in_specs, out_specs=out_specs, check_vma=False)
```

```python
import functools

import jax
import jax.numpy as jnp
from jax import lax
from jax.experimental import pallas as pl
from jax.experimental.pallas import tpu as pltpu
from jax.sharding import PartitionSpec as P

H = 12
KV = 2
HD = 128
BLOCK = 256

EPSILON = 1e-06
ROPE_BASE = 1000000.0
MASKED = -1e30
SCALING = HD ** (-0.5)
LANES = 128
VMEM_LIMIT = 60 << 20

f32 = jnp.float32
bf16 = jnp.bfloat16


def rope_tables(positions):
    halfway = HD // 2
    frequency = ROPE_BASE ** (-(jnp.arange(halfway, dtype=f32) * 2.0 / HD))
    angles = positions.astype(f32)[:, None] * frequency[None, :]
    cosine, sine = jnp.cos(angles), jnp.sin(angles)
    return (jnp.concatenate([cosine, cosine], axis=1), jnp.concatenate([sine, sine], axis=1))


def rotate(field, cosine, sine):
    halfway = HD // 2
    turned = jnp.concatenate([-field[..., halfway:], field[..., :halfway]], axis=-1)
    return field * cosine + turned * sine


def rotate_back(grad_field, cosine, sine):
    halfway = HD // 2
    moved = grad_field * sine
    turned = jnp.concatenate([moved[..., halfway:], -moved[..., :halfway]], axis=-1)
    return grad_field * cosine + turned


def rms_scale(values):
    return lax.rsqrt(jnp.mean(values * values, axis=-1, keepdims=True) + EPSILON)


def norm_back(values, factor, gain, grad_normed):
    gained = gain * grad_normed
    inner = jnp.mean(gained * values, axis=-1, keepdims=True)
    grad_values = factor * gained - values * (factor * factor * factor) * inner
    return (grad_values, jnp.sum(grad_normed * values * factor, axis=0))


def dot(left, right):
    return jnp.dot(left, right, preferred_element_type=f32)


def dot_rows(left, right):
    return lax.dot_general(left, right, (((0,), (0,)), ((), ())), preferred_element_type=f32)


def dot_cols(left, right):
    return lax.dot_general(left, right, (((1,), (1,)), ((), ())), preferred_element_type=f32)


def mask_row(kb_ref, own_block, key_blocks):
    return jnp.concatenate(
        [
            jnp.full((1, BLOCK), jnp.where(kb_ref[j] <= own_block, 0.0, MASKED), f32)
            for j in range(key_blocks)
        ],
        axis=1,
    )


def attention_kernel(key_blocks, kb_ref, q_ref, k_ref, v_ref, o_ref, lse_ref):
    bias = mask_row(kb_ref, kb_ref[pl.program_id(1)], key_blocks)
    scores = dot_cols(q_ref[...], k_ref[...]) * SCALING + bias
    row_max = jnp.max(scores, axis=1, keepdims=True)
    expo = jnp.exp(scores - row_max)
    total = jnp.sum(expo, axis=1, keepdims=True)
    probability = (expo * (1.0 / total)).astype(bf16)
    o_ref[...] = dot(probability, v_ref[...]).astype(bf16)
    lse_ref[0] = row_max + jnp.log(total)


def attention(key_blocks, queries, keys, values):
    rows, width = queries.shape
    heads = width // HD
    whole = pl.BlockSpec(keys.shape, lambda h, i, kb: (0, 0))
    tile = pl.BlockSpec((BLOCK, HD), lambda h, i, kb: (i, h))
    return pl.pallas_call(
        functools.partial(attention_kernel, keys.shape[0] // BLOCK),
        name="attention",
        grid_spec=pltpu.PrefetchScalarGridSpec(
            num_scalar_prefetch=1,
            grid=(heads, rows // BLOCK),
            in_specs=[tile, whole, whole],
            out_specs=[tile, pl.BlockSpec((1, BLOCK, 1), lambda h, i, kb: (h, i, 0))],
        ),
        out_shape=[
            jax.ShapeDtypeStruct((rows, width), bf16),
            jax.ShapeDtypeStruct((heads, rows, 1), f32),
        ],
        compiler_params=pltpu.CompilerParams(vmem_limit_bytes=VMEM_LIMIT),
        cost_estimate=pl.CostEstimate(
            flops=4 * rows * keys.shape[0] * width,
            bytes_accessed=4 * rows * width + 4 * keys.size,
            transcendentals=rows * keys.shape[0] * heads,
        ),
    )(key_blocks, queries, keys, values)


def attention_back_kernel(
    key_blocks,
    kb_ref,
    q_ref,
    do_ref,
    lse_ref,
    cos_ref,
    sin_ref,
    k_ref,
    v_ref,
    dq_ref,
    dk_ref,
    dv_ref,
):
    head, i = pl.program_id(0), pl.program_id(1)

    @pl.when((head == 0) & (i == 0))
    def _():
        dk_ref[...] = jnp.zeros_like(dk_ref)
        dv_ref[...] = jnp.zeros_like(dv_ref)

    bias = mask_row(kb_ref, kb_ref[i], key_blocks)
    scores = dot_cols(q_ref[...], k_ref[...]) * SCALING + bias
    probability = jnp.exp(scores - lse_ref[0])
    grad_probs = dot_cols(do_ref[...], v_ref[...])
    inner = jnp.sum(probability * grad_probs, axis=1, keepdims=True)
    grad_scores = (probability * (grad_probs - inner)).astype(bf16)
    grad_query = dot(grad_scores, k_ref[...]) * SCALING
    moved = grad_query * sin_ref[...]
    sign = jnp.where(lax.broadcasted_iota(jnp.int32, moved.shape, 1) < HD // 2, 1.0, -1.0)
    dq_ref[...] = (
        grad_query * cos_ref[...] + pltpu.roll(moved, HD // 2, 1) * sign
    ).astype(bf16)
    dk_ref[...] += dot_rows(grad_scores, q_ref[...]) * SCALING
    dv_ref[...] += dot_rows(probability.astype(bf16), do_ref[...])


def attention_back(key_blocks, queries, grad_out, lse, cosine, sine, keys, values):
    rows, width = queries.shape
    heads = width // HD
    whole = pl.BlockSpec(keys.shape, lambda h, i, kb: (0, 0))
    tile = pl.BlockSpec((BLOCK, HD), lambda h, i, kb: (i, h))
    table = pl.BlockSpec((BLOCK, HD), lambda h, i, kb: (i, 0))
    return pl.pallas_call(
        functools.partial(attention_back_kernel, keys.shape[0] // BLOCK),
        name="attention_back",
        grid_spec=pltpu.PrefetchScalarGridSpec(
            num_scalar_prefetch=1,
            grid=(heads, rows // BLOCK),
            in_specs=[
                tile,
                tile,
                pl.BlockSpec((1, BLOCK, 1), lambda h, i, kb: (h, i, 0)),
                table,
                table,
                whole,
                whole,
            ],
            out_specs=[tile, whole, whole],
        ),
        out_shape=[
            jax.ShapeDtypeStruct((rows, width), bf16),
            jax.ShapeDtypeStruct(keys.shape, f32),
            jax.ShapeDtypeStruct(keys.shape, f32),
        ],
        compiler_params=pltpu.CompilerParams(vmem_limit_bytes=VMEM_LIMIT),
        cost_estimate=pl.CostEstimate(
            flops=10 * rows * keys.shape[0] * width,
            bytes_accessed=6 * rows * width + 12 * keys.size,
            transcendentals=rows * keys.shape[0] * heads,
        ),
    )(key_blocks, queries, grad_out, lse, cosine, sine, keys, values)


def qkv_kernel(pieces, meta_ref, x_ref, gain_ref, bias_ref, cos_ref, sin_ref, *refs):
    weights, (xn_ref, factor_ref, q_ref, kv_ref) = refs[:pieces], refs[pieces:]
    values = x_ref[...].astype(f32)
    factor = lax.rsqrt(jnp.mean(values * values, axis=-1, keepdims=True) + EPSILON)
    factor_ref[...] = factor
    xn_ref[...] = (values * factor * gain_ref[...]).astype(bf16)
    total = bias_ref[...]
    for j, weight in enumerate(weights):
        depth = weight.shape[0]
        total = total + dot(xn_ref[:, columns_of(meta_ref, j, depth, pieces)], weight[...])
    cosine, sine = cos_ref[...], sin_ref[...]
    sign = jnp.where(lax.broadcasted_iota(jnp.int32, cosine.shape, 1) < HD // 2, -1.0, 1.0)
    heads = q_ref.shape[1] // HD
    for h in range(heads + 1):
        own = total[:, h * HD : (h + 1) * HD]
        turned = own * cosine + pltpu.roll(own, HD // 2, 1) * sign * sine
        if h < heads:
            q_ref[:, h * HD : (h + 1) * HD] = turned.astype(bf16)
        else:
            kv_ref[...] = jnp.where(meta_ref[2] == 0, turned, own).astype(bf16)


def columns_of(meta_ref, j, depth, pieces):
    if pieces == 1:
        return slice(None)
    return pl.ds(pl.multiple_of(meta_ref[j] * depth, LANES), depth)


def qkv(meta, inputs, gain, bias, cosine, sine, weights):
    rows, width = inputs.shape
    out = weights[0].shape[1]
    tile = 256
    row = lambda n: pl.BlockSpec((tile, n), lambda i, m: (i, 0))
    fixed = lambda w: pl.BlockSpec(w.shape, lambda i, m: (0, 0))
    return pl.pallas_call(
        functools.partial(qkv_kernel, len(weights)),
        name="qkv",
        grid_spec=pltpu.PrefetchScalarGridSpec(
            num_scalar_prefetch=1,
            grid=(rows // tile,),
            in_specs=[row(width), fixed(gain), fixed(bias), row(HD), row(HD)]
            + [fixed(w) for w in weights],
            out_specs=[row(width), row(1), row(out - HD), row(HD)],
        ),
        out_shape=[
            jax.ShapeDtypeStruct((rows, width), bf16),
            jax.ShapeDtypeStruct((rows, 1), f32),
            jax.ShapeDtypeStruct((rows, out - HD), bf16),
            jax.ShapeDtypeStruct((rows, HD), bf16),
        ],
        compiler_params=pltpu.CompilerParams(vmem_limit_bytes=VMEM_LIMIT),
        cost_estimate=pl.CostEstimate(
            flops=2 * rows * width * out,
            bytes_accessed=4 * rows * width + 2 * width * out,
            transcendentals=0,
        ),
    )(meta, inputs, gain, bias, cosine, sine, *weights)


def ffn_kernel(with_dx, pieces, meta_ref, x_ref, dy_ref, *refs):
    wg, wu, wd = (refs[m * pieces : (m + 1) * pieces] for m in range(3))
    outs = refs[-4:] if with_dx else refs[-3:]
    hid_ref, dg_ref, du_ref = outs[:3]
    columns = [columns_of(meta_ref, j, wg[j].shape[1], pieces) for j in range(pieces)]
    gate = sum(dot_cols(x_ref[:, at], w[...]) for at, w in zip(columns, wg))
    up = sum(dot_cols(x_ref[:, at], w[...]) for at, w in zip(columns, wu))
    grad_hidden = sum(dot_cols(dy_ref[:, at], w[...]) for at, w in zip(columns, wd))
    sigma = 1.0 / (1.0 + jnp.exp(-gate))
    gated = gate * sigma
    hid_ref[...] = (gated * up).astype(bf16)
    grad_gate = (grad_hidden * up * (sigma + gated * (1.0 - sigma))).astype(bf16)
    grad_up = (grad_hidden * gated).astype(bf16)
    dg_ref[...] = grad_gate
    du_ref[...] = grad_up
    if with_dx:
        for at, g, u in zip(columns, wg, wu):
            outs[3][:, at] = (dot(grad_gate, g[...]) + dot(grad_up, u[...])).astype(bf16)


def ffn(meta, normed, grad_out, wg, wu, wd, with_dx):
    rows, width = normed.shape
    units = wg[0].shape[0]
    tile = 512
    row = lambda n: pl.BlockSpec((tile, n), lambda i, m: (i, 0))
    weight = lambda w: pl.BlockSpec(w.shape, lambda i, m: (0, 0), pipeline_mode=pl.Buffered(1))
    weights = list(wg) + list(wu) + list(wd)
    widths = [units] * 3 + [width] * with_dx
    return pl.pallas_call(
        functools.partial(ffn_kernel, with_dx, len(wg)),
        name="ffn_pair" if with_dx else "ffn_far",
        grid_spec=pltpu.PrefetchScalarGridSpec(
            num_scalar_prefetch=1,
            grid=(rows // tile,),
            in_specs=[row(width), row(width)] + [weight(w) for w in weights],
            out_specs=[row(n) for n in widths],
        ),
        out_shape=[jax.ShapeDtypeStruct((rows, n), bf16) for n in widths],
        compiler_params=pltpu.CompilerParams(vmem_limit_bytes=VMEM_LIMIT),
        cost_estimate=pl.CostEstimate(
            flops=2 * rows * width * units * (5 if with_dx else 3),
            bytes_accessed=2 * (3 * width * units + 3 * rows * units + 3 * rows * width),
            transcendentals=rows * units,
        ),
    )(meta, normed, grad_out, *weights)


def unit_grads_kernel(meta_ref, xp, xf, yp, yf, hp, hf, gp, gf, up, uf, og, ou, od, ag, au, ad):
    step = pl.program_id(0)

    @pl.when(step == 0)
    def _():
        for acc in (ag, au, ad):
            acc[...] = jnp.zeros_like(acc)

    for use, x, y, h, g, u in ((True, xp, yp, hp, gp, up), (False, xf, yf, hf, gf, uf)):

        @pl.when((step // (pl.num_programs(0) // 2) == meta_ref[3]) == use)
        def _():
            ag[...] += dot_rows(g[...], x[...])
            au[...] += dot_rows(u[...], x[...])
            ad[...] += dot_rows(h[...], y[...])

    @pl.when(step == pl.num_programs(0) - 1)
    def _():
        og[...] = ag[...].astype(bf16)
        ou[...] = au[...].astype(bf16)
        od[...] = ad[...].astype(bf16)


def unit_grads(meta, which, pieces, x, y, hid, dg, du):
    rows, width = x[0].shape
    units = dg[0].shape[1]
    depth = width // pieces
    tile = 512
    steps = rows // tile
    shard = (lambda m: m[which]) if pieces > 1 else (lambda m: 0)
    near = lambda i, m: jnp.clip(i - steps * m[3], 0, steps - 1)
    far = lambda i, m: jnp.clip(i - steps * (1 - m[3]), 0, steps - 1)
    feature = lambda at: pl.BlockSpec((tile, depth), lambda i, m: (at(i, m), shard(m)))
    unit = lambda at: pl.BlockSpec((tile, units), lambda i, m: (at(i, m), 0))
    return pl.pallas_call(
        unit_grads_kernel,
        name=f"unit_grads_{which}",
        grid_spec=pltpu.PrefetchScalarGridSpec(
            num_scalar_prefetch=1,
            grid=(2 * steps,),
            in_specs=[feature(near), feature(far)] * 2 + [unit(near), unit(far)] * 3,
            out_specs=[
                pl.BlockSpec((units, depth), lambda i, m: (0, 0), pipeline_mode=pl.Buffered(1))
            ]
            * 3,
            scratch_shapes=[pltpu.VMEM((units, depth), f32)] * 3,
        ),
        out_shape=[jax.ShapeDtypeStruct((units, depth), bf16)] * 3,
        compiler_params=pltpu.CompilerParams(vmem_limit_bytes=VMEM_LIMIT),
        cost_estimate=pl.CostEstimate(
            flops=12 * rows * depth * units,
            bytes_accessed=2 * (6 * rows * units + 4 * rows * depth + 3 * units * depth),
            transcendentals=0,
        ),
    )(meta, *x, *y, *hid, *dg, *du)


def build(n_f, n_c, n_t):
    def flip(x, axis, bit):
        size = {"fsdp": n_f, "context": n_c, "tensor": n_t}[axis]
        return lax.ppermute(x, axis, [(i, i ^ bit) for i in range(size)])

    def by_bit(bit, x, other, axis):
        return jnp.where(
            bit == 0,
            jnp.concatenate([x, other], axis=axis),
            jnp.concatenate([other, x], axis=axis),
        )

    def local(
        inputs,
        cotangent,
        blocks,
        attn_gain,
        w_query,
        b_query,
        w_key,
        b_key,
        w_value,
        b_value,
        w_out,
        ffn_gain,
        w_gate,
        w_up,
        w_down,
    ):
        rows, width = inputs.shape
        f = lax.axis_index("fsdp")
        c = lax.axis_index("context")
        t = lax.axis_index("tensor")
        core, parity, pair = t % 2, c % 2, c // 2
        heads = w_query.shape[1] // HD
        group = (t * heads) // (H // KV)
        part = rows // n_t
        units_all = w_gate.shape[1]
        units = units_all // 2

        def gather_f(x, axis):
            if n_f == 2:
                return by_bit(f, x, flip(x, "fsdp", 1), axis)
            return lax.all_gather(x, "fsdp", axis=axis, tiled=True)

        def columns_f(parts):
            parts = [x.astype(bf16) for x in parts]
            return by_bit(f, parts[0], parts[1], 1) if n_f == 2 else parts[0]

        def grad_f(left, right, side):
            if n_f == 2:
                half = width // 2
                source = (left, right)[side]
                own = lax.dynamic_slice_in_dim(source, f * half, half, 1)
                far = lax.dynamic_slice_in_dim(source, (1 - f) * half, half, 1)
                pick = lambda x: dot_rows(x, right) if side == 0 else dot_rows(left, x)
                got = flip(pick(far).astype(bf16), "fsdp", 1)
                return pick(own) + got.astype(f32)
            return lax.psum_scatter(
                dot_rows(left, right).astype(bf16), "fsdp", scatter_dimension=side, tiled=True
            ).astype(f32)

        def sum_c(x):
            for bit in (1, 2):
                low = x.astype(bf16)
                x = low.astype(f32) + flip(low, "context", bit).astype(f32)
            return x

        order = (0, 2, 1, 3)

        def mixed(x):
            return jnp.concatenate(
                [lax.dynamic_slice_in_dim(x, (t ^ j) * part, part, 0) for j in order], axis=0
            )

        def natural(x):
            blocks_of = [x[i * part : (i + 1) * part] for i in range(n_t)]
            place = [blocks_of[order.index(j)] for j in range(n_t)]
            out = jnp.stack(place)
            return jnp.concatenate(
                [lax.dynamic_index_in_dim(out, n ^ t, 0, keepdims=False) for n in range(n_t)],
                axis=0,
            )

        def add_half(x, axis, bit):
            half = x.shape[0] // 2
            got = flip(x[half:].astype(bf16), axis, bit)
            return x[:half].astype(f32) + got.astype(f32)

        def scatter_t(x):
            return add_half(add_half(x, "tensor", 1), "tensor", 2)

        def scatter_pair(x):
            return add_half(add_half(add_half(x, "tensor", 1), "context", 1), "tensor", 2)

        def grow(x, axis, bit):
            return jnp.concatenate([x, flip(x, axis, bit)], axis=0)

        def gather_t(x):
            return grow(grow(x, "tensor", 2), "tensor", 1)

        def gather_pair(x):
            return grow(grow(grow(x, "tensor", 2), "context", 1), "tensor", 1)

        small = jnp.concatenate(
            [v.reshape(1, -1) for v in (attn_gain, ffn_gain, b_query, b_key, b_value)], axis=1
        )
        column = lambda w: lax.dynamic_slice_in_dim(w, group * HD, HD, 1)
        w_kv_own = jnp.where(core == 0, column(w_key), column(w_value))
        pieces_f = lambda x, axis: (
            [x, flip(x, "fsdp", 1)]
            if n_f == 2
            else [lax.all_gather(x, "fsdp", axis=axis, tiled=True)]
        )
        meta = jnp.stack([f, 1 - f, core, pair]).astype(jnp.int32)
        w_qkv = pieces_f(jnp.concatenate([w_query, w_kv_own], axis=1), 0)
        small = gather_f(small, 0)
        w_out_all = gather_f(w_out, 1)
        piece = attn_gain.shape[0]
        gain_first = small[:, :piece].reshape(1, width).astype(f32)
        gain_second = small[:, piece : 2 * piece].reshape(1, width).astype(f32)
        bias_of = lambda lo, n: (
            small[:, lo : lo + n * (HD // n_f)]
            .reshape(n_f, n, HD // n_f)
            .transpose(1, 0, 2)
            .reshape(n, HD)
            .astype(f32)
        )
        at = 2 * piece
        bq = bias_of(at, heads)
        bk = bias_of(at + heads * (HD // n_f), KV)
        bv = bias_of(at + (heads + KV) * (HD // n_f), KV)
        b_kv = lax.dynamic_index_in_dim(jnp.where(core == 0, bk, bv), group, 0)

        unit_slice = lambda w: lax.dynamic_slice_in_dim(w, parity * units, units, 0)
        wg = pieces_f(unit_slice(w_gate.T), 1)
        wu = pieces_f(unit_slice(w_up.T), 1)
        wd = pieces_f(unit_slice(w_down), 1)

        dy_own = mixed(cotangent)[: 2 * part]
        dy_near = jnp.concatenate([dy_own, flip(dy_own, "context", 1)], axis=0)
        dy_pair = grow(dy_near, "tensor", 1)
        dy_far = grow(grow(flip(dy_own, "context", 2), "context", 1), "tensor", 1)

        seq_blocks = blocks[0].reshape(n_c, -1)
        own_blocks = seq_blocks.shape[1]
        key_blocks = jnp.concatenate(
            [lax.dynamic_index_in_dim(seq_blocks, c ^ j, 0, keepdims=False) for j in range(n_c)]
        )
        positions = (
            key_blocks[:own_blocks, None] * BLOCK + jnp.arange(BLOCK, dtype=jnp.int32)[None, :]
        ).reshape(-1)
        cosine, sine = rope_tables(positions)
        bias = jnp.concatenate([bq.reshape(1, -1), b_kv], axis=1)
        normed, factor_first, queries, kv_own = qkv(
            meta, inputs, gain_first, bias, cosine, sine, w_qkv
        )
        kv_whole = grow(grow(kv_own, "context", 1), "context", 2)
        kv_other = flip(kv_whole, "tensor", 1)
        keys = jnp.where(core == 0, kv_whole, kv_other)
        values = jnp.where(core == 0, kv_other, kv_whole)
        attended, lse = attention(key_blocks, queries, keys, values)

        attended_mixed = mixed(attended)
        attn_sum = scatter_t(dot(attended_mixed, w_out_all))
        middle = lax.dynamic_slice_in_dim(inputs, t * part, part, 0).astype(f32) + attn_sum

        factor_second = rms_scale(middle)
        normed2 = (middle * factor_second * gain_second).astype(bf16)
        normed2_pair = gather_pair(normed2)
        normed2_far = gather_pair(flip(normed2, "context", 2))
        hid_pair, dg_pair, du_pair, dx_part = ffn(meta, normed2_pair, dy_pair, wg, wu, wd, True)
        grad_normed2 = scatter_pair(dx_part)
        hid_far, dg_far, du_far = ffn(meta, normed2_far, dy_far, wg, wu, wd, False)
        final = middle + scatter_pair(columns_f([dot(hid_pair, w) for w in wd]))
        outputs = natural(gather_t(final.astype(bf16)))

        grad_args = (
            (normed2_pair, normed2_far),
            (dy_pair, dy_far),
            (hid_pair, hid_far),
            (dg_pair, dg_far),
            (du_pair, du_far),
        )
        if n_f == 2:
            unit_sent = unit_grads(meta, 1, 2, *grad_args)
            unit_got = [flip(x, "fsdp", 1) for x in unit_sent]
            unit_own = unit_grads(meta, 0, 2, *grad_args)
        else:
            unit_own = [
                lax.psum_scatter(x, "fsdp", scatter_dimension=1, tiled=True)
                for x in unit_grads(meta, 0, 1, *grad_args)
            ]
            unit_got = [jnp.zeros_like(x) for x in unit_own]

        def unit_done(own, got):
            low = (own.astype(f32) + got.astype(f32)).astype(bf16)
            return by_bit(parity, low, flip(low, "context", 1), 0).astype(f32)

        grad_mid_norm, ffn_gain_grad = norm_back(middle, factor_second, gain_second, grad_normed2)
        dy_part = lax.dynamic_slice_in_dim(cotangent, t * part, part, 0).astype(f32)
        grad_middle = dy_part + grad_mid_norm
        grad_middle_low = gather_t(grad_middle.astype(bf16))
        wo_grad = sum_c(grad_f(attended_mixed, grad_middle_low, 1))
        grad_attended = natural(dot_cols(grad_middle_low, w_out_all).astype(bf16))

        dq_low, dk, dv = attention_back(
            key_blocks, queries, grad_attended, lse, cosine, sine, keys, values
        )
        unit_own, unit_got, dq_low = lax.optimization_barrier((unit_own, unit_got, dq_low))
        wg_grad, wu_grad, wd_grad = (unit_done(a, b) for a, b in zip(unit_own, unit_got))
        wg_grad, wu_grad = wg_grad.T, wu_grad.T
        dkv_keep = jnp.where(core == 0, dk, dv)
        dkv_send = jnp.where(core == 0, dv, dk).astype(bf16)
        dkv = dkv_keep + flip(dkv_send, "tensor", 1).astype(f32)
        dkv = add_half(add_half(dkv, "context", 2), "context", 1)
        dkv_low = jnp.where(core == 0, rotate_back(dkv, cosine, sine), dkv).astype(bf16)
        wq_grad = sum_c(grad_f(normed, dq_low, 0))
        wkv_own = sum_c(grad_f(normed, dkv_low, 0)).astype(bf16)
        wkv_stack = gather_t(wkv_own)
        depth = wkv_own.shape[0]
        wkv_of = [wkv_stack[order.index(j) * depth : (order.index(j) + 1) * depth] for j in range(n_t)]
        wkv_stack = jnp.stack(wkv_of)
        wkv_rank = [
            lax.dynamic_index_in_dim(wkv_stack, n ^ t, 0, keepdims=False).astype(f32)
            for n in range(n_t)
        ]
        wk_grad = jnp.concatenate(wkv_rank[0::2], axis=1)
        wv_grad = jnp.concatenate(wkv_rank[1::2], axis=1)

        d_qkv = mixed(jnp.concatenate([dq_low, dkv_low], axis=1))
        grad_normed = scatter_t(columns_f([dot_cols(d_qkv, w) for w in w_qkv]))
        inputs_part = lax.dynamic_slice_in_dim(inputs, t * part, part, 0).astype(f32)
        factor_part = lax.dynamic_slice_in_dim(factor_first, t * part, part, 0)
        grad_in_norm, attn_gain_grad = norm_back(inputs_part, factor_part, gain_first, grad_normed)
        input_grad = natural(gather_t((grad_middle + grad_in_norm).astype(bf16)))

        bq_grad = jnp.sum(dq_low.astype(f32), axis=0)
        bkv_grad = jnp.sum(dkv_low.astype(f32), axis=0)
        slots = jnp.zeros((n_t, (heads + 1) * HD), f32)
        slots = lax.dynamic_update_slice(
            slots, jnp.concatenate([bq_grad, bkv_grad])[None], (t, 0)
        )
        packed = lax.psum(
            jnp.concatenate([attn_gain_grad, ffn_gain_grad, slots.reshape(-1)]),
            ("fsdp", "context", "tensor"),
        )
        attn_gain_grad = lax.dynamic_slice_in_dim(packed, f * piece, piece, 0)
        ffn_gain_grad = lax.dynamic_slice_in_dim(packed, width + f * piece, piece, 0)
        slots = packed[2 * width :].reshape(n_t, heads + 1, HD)
        slots = lax.dynamic_slice_in_dim(slots, f * (HD // n_f), HD // n_f, 2)
        bq_out = lax.dynamic_index_in_dim(slots, t, 0, keepdims=False)[:heads]
        bk_out = slots[0::2, heads]
        bv_out = slots[1::2, heads]

        return (
            outputs,
            input_grad,
            attn_gain_grad,
            wq_grad,
            bq_out,
            wk_grad,
            bk_out,
            wv_grad,
            bv_out,
            wo_grad,
            ffn_gain_grad,
            wg_grad,
            wu_grad,
            wd_grad,
        )

    return local


def solution(mesh):
    in_specs = (
        P(("fsdp", "context"), None),
        P(("fsdp", "context"), None),
        P("fsdp", None),
        P("fsdp"),
        P("fsdp", "tensor"),
        P("tensor", "fsdp"),
        P("fsdp", None),
        P(None, "fsdp"),
        P("fsdp", None),
        P(None, "fsdp"),
        P("tensor", "fsdp"),
        P("fsdp"),
        P("fsdp", "tensor"),
        P("fsdp", "tensor"),
        P("tensor", "fsdp"),
    )
    out_specs = (
        P(("fsdp", "context"), None),
        P(("fsdp", "context"), None),
        P("fsdp"),
        P("fsdp", "tensor"),
        P("tensor", "fsdp"),
        P("fsdp", None),
        P(None, "fsdp"),
        P("fsdp", None),
        P(None, "fsdp"),
        P("tensor", "fsdp"),
        P("fsdp"),
        P("fsdp", "tensor"),
        P("fsdp", "tensor"),
        P("tensor", "fsdp"),
    )
    local = build(mesh.shape["fsdp"], mesh.shape["context"], mesh.shape["tensor"])
    return jax.shard_map(local, mesh=mesh, in_specs=in_specs, out_specs=out_specs, check_vma=False)
```

```python
import functools

import jax
import jax.numpy as jnp
from jax import lax
from jax.experimental import pallas as pl
from jax.experimental.pallas import tpu as pltpu
from jax.sharding import PartitionSpec as P

H = 12
KV = 2
HD = 128
BLOCK = 256

EPSILON = 1e-06
ROPE_BASE = 1000000.0
MASKED = -1e30
SCALING = HD ** (-0.5)
LANES = 128
VMEM_LIMIT = 60 << 20

f32 = jnp.float32
bf16 = jnp.bfloat16


def rope_tables(positions):
    halfway = HD // 2
    frequency = ROPE_BASE ** (-(jnp.arange(halfway, dtype=f32) * 2.0 / HD))
    angles = positions.astype(f32)[:, None] * frequency[None, :]
    cosine, sine = jnp.cos(angles), jnp.sin(angles)
    return (jnp.concatenate([cosine, cosine], axis=1), jnp.concatenate([sine, sine], axis=1))


def rotate(field, cosine, sine):
    halfway = HD // 2
    turned = jnp.concatenate([-field[..., halfway:], field[..., :halfway]], axis=-1)
    return field * cosine + turned * sine


def rotate_back(grad_field, cosine, sine):
    halfway = HD // 2
    moved = grad_field * sine
    turned = jnp.concatenate([moved[..., halfway:], -moved[..., :halfway]], axis=-1)
    return grad_field * cosine + turned


def dot(left, right):
    return jnp.dot(left, right, preferred_element_type=f32)


def dot_rows(left, right):
    return lax.dot_general(left, right, (((0,), (0,)), ((), ())), preferred_element_type=f32)


def dot_cols(left, right):
    return lax.dot_general(left, right, (((1,), (1,)), ((), ())), preferred_element_type=f32)


def mask_row(kb_ref, own_block, key_blocks):
    return jnp.concatenate(
        [
            jnp.full((1, BLOCK), jnp.where(kb_ref[j] <= own_block, 0.0, MASKED), f32)
            for j in range(key_blocks)
        ],
        axis=1,
    )


def attention_kernel(key_blocks, kb_ref, q_ref, k_ref, v_ref, o_ref, lse_ref):
    bias = mask_row(kb_ref, kb_ref[pl.program_id(1)], key_blocks)
    scores = dot_cols(q_ref[...], k_ref[...]) * SCALING + bias
    row_max = jnp.max(scores, axis=1, keepdims=True)
    expo = jnp.exp(scores - row_max)
    total = jnp.sum(expo, axis=1, keepdims=True)
    probability = (expo * (1.0 / total)).astype(bf16)
    o_ref[...] = dot(probability, v_ref[...]).astype(bf16)
    lse_ref[0] = row_max + jnp.log(total)


def attention(key_blocks, queries, kv):
    rows, width = queries.shape
    heads = width // HD
    whole = lambda kind: pl.BlockSpec((None,) + kv.shape[1:], lambda h, i, kb: (kind, 0, 0))
    tile = pl.BlockSpec((BLOCK, HD), lambda h, i, kb: (i, h))
    return pl.pallas_call(
        functools.partial(attention_kernel, kv.shape[1] // BLOCK),
        name="attention",
        grid_spec=pltpu.PrefetchScalarGridSpec(
            num_scalar_prefetch=1,
            grid=(heads, rows // BLOCK),
            in_specs=[tile, whole(0), whole(1)],
            out_specs=[tile, pl.BlockSpec((1, BLOCK, 1), lambda h, i, kb: (h, i, 0))],
        ),
        out_shape=[
            jax.ShapeDtypeStruct((rows, width), bf16),
            jax.ShapeDtypeStruct((heads, rows, 1), f32),
        ],
        compiler_params=pltpu.CompilerParams(vmem_limit_bytes=VMEM_LIMIT),
    )(key_blocks, queries, kv, kv)


def attention_back_kernel(
    key_blocks,
    kb_ref,
    q_ref,
    do_ref,
    lse_ref,
    cos_ref,
    sin_ref,
    k_ref,
    v_ref,
    dq_ref,
    dkv_ref,
    dk_ref,
    dv_ref,
):
    head, i = pl.program_id(0), pl.program_id(1)

    @pl.when((head == 0) & (i == 0))
    def _():
        dk_ref[...] = jnp.zeros_like(dk_ref)
        dv_ref[...] = jnp.zeros_like(dv_ref)

    bias = mask_row(kb_ref, kb_ref[i], key_blocks)
    scores = dot_cols(q_ref[...], k_ref[...]) * SCALING + bias
    probability = jnp.exp(scores - lse_ref[0])
    grad_probs = dot_cols(do_ref[...], v_ref[...])
    inner = jnp.sum(probability * grad_probs, axis=1, keepdims=True)
    grad_scores = (probability * (grad_probs - inner)).astype(bf16)
    grad_query = dot(grad_scores, k_ref[...]) * SCALING
    moved = grad_query * sin_ref[...]
    sign = jnp.where(lax.broadcasted_iota(jnp.int32, moved.shape, 1) < HD // 2, 1.0, -1.0)
    dq_ref[...] = (
        grad_query * cos_ref[...] + pltpu.roll(moved, HD // 2, 1) * sign
    ).astype(bf16)
    dk_ref[...] += dot_rows(grad_scores, q_ref[...]) * SCALING
    dv_ref[...] += dot_rows(probability.astype(bf16), do_ref[...])

    @pl.when((head == pl.num_programs(0) - 1) & (i == pl.num_programs(1) - 1))
    def _():
        dkv_ref[0] = dk_ref[...].astype(bf16)
        dkv_ref[1] = dv_ref[...].astype(bf16)


def attention_back(key_blocks, queries, grad_out, lse, cosine, sine, kv):
    rows, width = queries.shape
    heads = width // HD
    whole = lambda kind: pl.BlockSpec((None,) + kv.shape[1:], lambda h, i, kb: (kind, 0, 0))
    tile = pl.BlockSpec((BLOCK, HD), lambda h, i, kb: (i, h))
    table = pl.BlockSpec((BLOCK, HD), lambda h, i, kb: (i, 0))
    return pl.pallas_call(
        functools.partial(attention_back_kernel, kv.shape[1] // BLOCK),
        name="attention_back",
        grid_spec=pltpu.PrefetchScalarGridSpec(
            num_scalar_prefetch=1,
            grid=(heads, rows // BLOCK),
            in_specs=[
                tile,
                tile,
                pl.BlockSpec((1, BLOCK, 1), lambda h, i, kb: (h, i, 0)),
                table,
                table,
                whole(0),
                whole(1),
            ],
            out_specs=[tile, pl.BlockSpec(kv.shape, lambda h, i, kb: (0, 0, 0))],
            scratch_shapes=[pltpu.VMEM(kv.shape[1:], f32)] * 2,
        ),
        out_shape=[
            jax.ShapeDtypeStruct((rows, width), bf16),
            jax.ShapeDtypeStruct(kv.shape, bf16),
        ],
        compiler_params=pltpu.CompilerParams(vmem_limit_bytes=VMEM_LIMIT),
    )(key_blocks, queries, grad_out, lse, cosine, sine, kv, kv)


def qkv_kernel(pieces, meta_ref, x_ref, gain_ref, bias_ref, cos_ref, sin_ref, *refs):
    weights, (xn_ref, factor_ref, q_ref, kv_ref) = refs[:pieces], refs[pieces:]
    values = x_ref[...].astype(f32)
    factor = lax.rsqrt(jnp.mean(values * values, axis=-1, keepdims=True) + EPSILON)
    factor_ref[...] = factor
    xn_ref[...] = (values * factor * gain_ref[...]).astype(bf16)
    total = bias_ref[...]
    for j, weight in enumerate(weights):
        depth = weight.shape[0]
        total = total + dot(xn_ref[:, columns_of(meta_ref, j, depth, pieces)], weight[...])
    cosine, sine = cos_ref[...], sin_ref[...]
    sign = jnp.where(lax.broadcasted_iota(jnp.int32, cosine.shape, 1) < HD // 2, -1.0, 1.0)
    heads = q_ref.shape[1] // HD
    for h in range(heads + 1):
        own = total[:, h * HD : (h + 1) * HD]
        turned = own * cosine + pltpu.roll(own, HD // 2, 1) * sign * sine
        if h < heads:
            q_ref[:, h * HD : (h + 1) * HD] = turned.astype(bf16)
        else:
            kv_ref[...] = jnp.where(meta_ref[2] == 0, turned, own).astype(bf16)


def columns_of(meta_ref, j, depth, pieces):
    if pieces == 1:
        return slice(None)
    return pl.ds(pl.multiple_of(meta_ref[j] * depth, LANES), depth)


def qkv(meta, inputs, gain, bias, cosine, sine, weights):
    rows, width = inputs.shape
    out = weights[0].shape[1]
    tile = 256
    row = lambda n: pl.BlockSpec((tile, n), lambda i, m: (i, 0))
    fixed = lambda w: pl.BlockSpec(w.shape, lambda i, m: (0, 0))
    return pl.pallas_call(
        functools.partial(qkv_kernel, len(weights)),
        name="qkv",
        grid_spec=pltpu.PrefetchScalarGridSpec(
            num_scalar_prefetch=1,
            grid=(rows // tile,),
            in_specs=[row(width), fixed(gain), fixed(bias), row(HD), row(HD)]
            + [fixed(w) for w in weights],
            out_specs=[row(width), row(1), row(out - HD), row(HD)],
        ),
        out_shape=[
            jax.ShapeDtypeStruct((rows, width), bf16),
            jax.ShapeDtypeStruct((rows, 1), f32),
            jax.ShapeDtypeStruct((rows, out - HD), bf16),
            jax.ShapeDtypeStruct((rows, HD), bf16),
        ],
        compiler_params=pltpu.CompilerParams(vmem_limit_bytes=VMEM_LIMIT),
    )(meta, inputs, gain, bias, cosine, sine, *weights)


def ffn_kernel(with_dx, pieces, meta_ref, x_ref, dy_ref, *refs):
    wg, wu, wd = (refs[m * pieces : (m + 1) * pieces] for m in range(3))
    outs = refs[-4:] if with_dx else refs[-3:]
    hid_ref, dg_ref, du_ref = outs[:3]
    columns = [columns_of(meta_ref, j, wg[j].shape[1], pieces) for j in range(pieces)]
    gate = sum(dot_cols(x_ref[:, at], w[...]) for at, w in zip(columns, wg))
    up = sum(dot_cols(x_ref[:, at], w[...]) for at, w in zip(columns, wu))
    grad_hidden = sum(dot_cols(dy_ref[:, at], w[...]) for at, w in zip(columns, wd))
    sigma = 1.0 / (1.0 + jnp.exp(-gate))
    gated = gate * sigma
    hid_ref[...] = (gated * up).astype(bf16)
    grad_gate = (grad_hidden * up * (sigma + gated * (1.0 - sigma))).astype(bf16)
    grad_up = (grad_hidden * gated).astype(bf16)
    dg_ref[...] = grad_gate
    du_ref[...] = grad_up
    if with_dx:
        for at, g, u in zip(columns, wg, wu):
            outs[3][:, at] = (dot(grad_gate, g[...]) + dot(grad_up, u[...])).astype(bf16)


def ffn(meta, normed, grad_out, weights, with_dx):
    width = normed.shape[-1]
    half = 0 if with_dx else 1
    rows = normed.shape[1] * normed.shape[2]
    units = weights[0].shape[0] // 3
    tile = 512
    steps = rows // tile
    flat = lambda x: x.reshape(-1, width)
    row = lambda n: pl.BlockSpec((tile, n), lambda i, m: (i, 0))
    read = pl.BlockSpec((tile, width), lambda i, m: (i + half * steps, 0))
    weight = lambda w, k: pl.BlockSpec(
        (units, w.shape[1]), lambda i, m: (k, 0), pipeline_mode=pl.Buffered(1)
    )
    widths = [units] * 3 + [width] * with_dx
    return pl.pallas_call(
        functools.partial(ffn_kernel, with_dx, len(weights)),
        name="ffn_pair" if with_dx else "ffn_far",
        grid_spec=pltpu.PrefetchScalarGridSpec(
            num_scalar_prefetch=1,
            grid=(steps,),
            in_specs=[read, read] + [weight(w, k) for k in range(3) for w in weights],
            out_specs=[row(n) for n in widths],
        ),
        out_shape=[jax.ShapeDtypeStruct((rows, n), bf16) for n in widths],
        compiler_params=pltpu.CompilerParams(vmem_limit_bytes=VMEM_LIMIT),
    )(meta, flat(normed), flat(grad_out), *(list(weights) * 3))


def unit_grads_kernel(meta_ref, x, y, hp, hf, gp, gf, up, uf, og, ou, od, ag, au, ad):
    step = pl.program_id(0)

    @pl.when(step == 0)
    def _():
        for acc in (ag, au, ad):
            acc[...] = jnp.zeros_like(acc)

    for use, h, g, u in ((True, hp, gp, up), (False, hf, gf, uf)):

        @pl.when((step // (pl.num_programs(0) // 2) == meta_ref[3]) == use)
        def _():
            ag[...] += dot_rows(g[...], x[...])
            au[...] += dot_rows(u[...], x[...])
            ad[...] += dot_rows(h[...], y[...])

    @pl.when(step == pl.num_programs(0) - 1)
    def _():
        og[...] = ag[...].astype(bf16)
        ou[...] = au[...].astype(bf16)
        od[...] = ad[...].astype(bf16)


def unit_grads(meta, which, pieces, x, y, hid, dg, du):
    width = x.shape[-1]
    rows, units = dg[0].shape
    depth = width // pieces
    tile = 512
    steps = rows // tile
    shard = (lambda m: m[which]) if pieces > 1 else (lambda m: 0)
    near = lambda i, m: jnp.clip(i - steps * m[3], 0, steps - 1)
    far = lambda i, m: jnp.clip(i - steps * (1 - m[3]), 0, steps - 1)
    feature = pl.BlockSpec(
        (tile, depth), lambda i, m: (lax.rem(i + steps * m[3], 2 * steps), shard(m))
    )
    unit = lambda at: pl.BlockSpec((tile, units), lambda i, m: (at(i, m), 0))
    return pl.pallas_call(
        unit_grads_kernel,
        name=f"unit_grads_{which}",
        grid_spec=pltpu.PrefetchScalarGridSpec(
            num_scalar_prefetch=1,
            grid=(2 * steps,),
            in_specs=[feature] * 2 + [unit(near), unit(far)] * 3,
            out_specs=[
                pl.BlockSpec((units, depth), lambda i, m: (0, 0), pipeline_mode=pl.Buffered(1))
            ]
            * 3,
            scratch_shapes=[pltpu.VMEM((units, depth), f32)] * 3,
        ),
        out_shape=[jax.ShapeDtypeStruct((units, depth), bf16)] * 3,
        compiler_params=pltpu.CompilerParams(vmem_limit_bytes=VMEM_LIMIT),
    )(meta, x.reshape(-1, width), y.reshape(-1, width), *hid, *dg, *du)


class Wires:
    def __init__(self, sends, receives, locals_):
        self.sends, self.receives, self.locals = sends, receives, locals_
        self.used = self.used_local = 0
        self.started = []

    def copy(self, source, target, device):
        k = self.used
        self.used += 1
        one = pltpu.make_async_remote_copy(
            source,
            target,
            self.sends.at[k],
            self.receives.at[k],
            device_id=device,
            device_id_type=pl.DeviceIdType.MESH,
        )
        one.start()
        self.started.append(one)
        return one

    def here(self, source, target):
        k = self.used_local
        self.used_local += 1
        one = pltpu.make_async_copy(source, target, self.locals.at[k])
        one.start()
        return one

    def finish(self):
        for one in self.started:
            one.wait_send()


def meet(devices):
    barrier = pltpu.get_barrier_semaphore()
    for device in devices:
        pl.semaphore_signal(barrier, inc=1, device_id=device, device_id_type=pl.DeviceIdType.MESH)
    pl.semaphore_wait(barrier, len(devices))


def partners():
    c, t = lax.axis_index("context"), lax.axis_index("tensor")
    flip = lambda x, bit: x + bit * (1 - 2 * lax.rem(x // bit, 2))
    return {
        "core": {"tensor": flip(t, 1)},
        "y": {"tensor": flip(t, 2)},
        "z": {"context": flip(c, 1)},
        "far": {"context": flip(c, 2)},
        "last": {"context": flip(flip(c, 1), 2)},
    }


def wide(x):
    return x.astype(f32)


def scatter_rank(wires, to, part, own, got_core, sent, got_y):
    size = part.shape[1] // 2
    halves = [pl.ds(0, size), pl.ds(size, size)]
    from_core = {}
    for block in (1, 0):
        for k, at in enumerate(halves):
            from_core[block, k] = wires.copy(
                part.at[2 + block, at], got_core.at[block, at], to["core"]
            )
    mine = wires.here(part.at[pl.ds(0, 2)], own)
    mine.wait()
    from_y = []
    for k, at in enumerate(halves):
        from_core[1, k].wait_recv()
        sent[at] = (wide(own[1, at]) + wide(got_core[1, at])).astype(bf16)
        from_y.append(wires.copy(sent.at[at], got_y.at[at], to["y"]))
    for k in range(2):
        from_core[0, k].wait_recv()
    total = wide(own[0]) + wide(got_core[0])
    for one in from_y:
        one.wait_recv()
    return total + wide(got_y[...])


def scatter_pair(wires, to, part, own, got_core, sent, got_y, got_z, diag_y, diag_z):
    size = part.shape[1] // 2
    low, high = pl.ds(0, size), pl.ds(size, size)
    from_core = {j: wires.copy(part.at[4 + j], got_core.at[j], to["core"]) for j in (3, 1, 2, 0)}
    mine = wires.here(part.at[pl.ds(0, 4)], own)
    mine.wait()
    both = lambda j, at: wide(own[j, at]) + wide(got_core[j, at])
    from_core[3].wait_recv()
    sent[2] = (wide(own[3]) + wide(got_core[3])).astype(bf16)
    via_z = wires.copy(sent.at[2, low], diag_z, to["z"])
    via_y = wires.copy(sent.at[2, high], diag_y, to["y"])
    from_core[1].wait_recv()
    sent[0, high] = both(1, high).astype(bf16)
    y_high = wires.copy(sent.at[0, high], got_y.at[high], to["y"])
    from_core[2].wait_recv()
    sent[1, low] = both(2, low).astype(bf16)
    z_low = wires.copy(sent.at[1, low], got_z.at[low], to["z"])
    via_z.wait_recv()
    sent[0, low] = (both(1, low) + wide(diag_z[...])).astype(bf16)
    y_low = wires.copy(sent.at[0, low], got_y.at[low], to["y"])
    via_y.wait_recv()
    sent[1, high] = (both(2, high) + wide(diag_y[...])).astype(bf16)
    z_high = wires.copy(sent.at[1, high], got_z.at[high], to["z"])
    from_core[0].wait_recv()
    total = wide(own[0]) + wide(got_core[0])
    for one in (y_high, z_low, y_low, z_high):
        one.wait_recv()
    return total + wide(got_y[...]) + wide(got_z[...])


def gather_rank(wires, to, block, out, at):
    size = block.shape[0] // 2
    halves = [pl.ds(0, size), pl.ds(size, size)]
    mine = wires.here(block, out.at[at(0, 0)])
    from_y = [wires.copy(block.at[h], out.at[at(0, 2), h], to["y"]) for h in halves]
    from_core = [wires.copy(block, out.at[at(0, 1)], to["core"])]
    for h, one in zip(halves, from_y):
        one.wait_recv()
        from_core.append(wires.copy(out.at[at(2, 0), h], out.at[at(2, 1), h], to["core"]))
    for one in from_core:
        one.wait_recv()
    mine.wait()


def gather_pair(wires, to, block, out, base):
    size = block.shape[0] // 2
    low, high = pl.ds(0, size), pl.ds(size, size)
    at = lambda j: out.at[base + j]
    from_y = wires.copy(block, at(1), to["y"])
    from_z = wires.copy(block, at(2), to["z"])
    from_core = [wires.copy(block, at(4), to["core"])]
    from_y.wait_recv()
    via_z = wires.copy(out.at[base + 1, low], out.at[base + 3, low], to["z"])
    from_core.append(wires.copy(at(1), at(5), to["core"]))
    from_z.wait_recv()
    via_y = wires.copy(out.at[base + 2, high], out.at[base + 3, high], to["y"])
    from_core.append(wires.copy(at(2), at(6), to["core"]))
    via_z.wait_recv()
    via_y.wait_recv()
    from_core.append(wires.copy(at(3), at(7), to["core"]))
    return from_core


def remote_call(kernel, name, key, args, outs, scratch, copies, in_vmem):
    ins, out_in = in_vmem
    spec = lambda inside: pl.BlockSpec(memory_space=pltpu.VMEM if inside else pl.ANY)
    return pl.pallas_call(
        kernel,
        name=name,
        out_shape=outs,
        in_specs=[spec(x) for x in ins],
        out_specs=[spec(x) for x in out_in],
        scratch_shapes=list(scratch)
        + [
            pltpu.SemaphoreType.DMA((copies,)),
            pltpu.SemaphoreType.DMA((copies,)),
            pltpu.SemaphoreType.DMA((4,)),
        ],
        compiler_params=pltpu.CompilerParams(
            collective_id=key, has_side_effects=True, vmem_limit_bytes=VMEM_LIMIT
        ),
    )(*args)


def kv_gather_kernel(own_ref, out_ref, *sems):
    wires, to = Wires(*sems), partners()
    kind = lax.rem(lax.axis_index("tensor"), 2)
    rows = own_ref.shape[0]
    block = lambda j: out_ref.at[kind, pl.ds(j * rows, rows)]
    meet([to[k] for k in ("core", "z", "far", "last")])
    mine = wires.here(own_ref, block(0))
    arrive = [wires.copy(own_ref, block(j), to[k]) for j, k in ((3, "last"), (2, "far"), (1, "z"))]
    from_core = [wires.copy(own_ref, block(0), to["core"])]
    for j, one in ((1, arrive[2]), (2, arrive[1]), (3, arrive[0])):
        one.wait_recv()
        from_core.append(wires.copy(block(j), block(j), to["core"]))
    for one in from_core:
        one.wait_recv()
    mine.wait()
    wires.finish()


def kv_gather(own):
    rows, width = own.shape
    n_c = lax.axis_size("context")
    return remote_call(
        kv_gather_kernel,
        "kv_gather",
        0,
        [own],
        [jax.ShapeDtypeStruct((2, n_c * rows, width), bf16)],
        [],
        8,
        ([False], [False]),
    )[0]


def kv_scatter_kernel(part_ref, out_ref, own, got_core, sent, got, *sems):
    wires, to = Wires(*sems), partners()
    kind = lax.rem(lax.axis_index("tensor"), 2)
    rows = out_ref.shape[0]
    block = lambda j: pl.ds(j * rows, rows)
    meet([to[k] for k in ("core", "z", "far", "last")])
    steps = ((3, "last"), (2, "far"), (1, "z"), (0, None))
    from_core = {
        j: wires.copy(part_ref.at[1 - kind, block(j)], got_core.at[block(j)], to["core"])
        for j, _ in steps
    }
    mine = wires.here(part_ref.at[kind], own)
    mine.wait()
    arrive = []
    for j, k in steps[:3]:
        from_core[j].wait_recv()
        sent[block(j)] = (wide(own[block(j)]) + wide(got_core[block(j)])).astype(bf16)
        arrive.append(wires.copy(sent.at[block(j)], got.at[block(j)], to[k]))
    from_core[0].wait_recv()
    total = wide(own[block(0)]) + wide(got_core[block(0)])
    for one in arrive:
        one.wait_recv()
    for j in (1, 2, 3):
        total = total + wide(got[block(j)])
    out_ref[...] = total
    wires.finish()


def kv_scatter(part):
    _, rows, width = part.shape
    n_c = lax.axis_size("context")
    return remote_call(
        kv_scatter_kernel,
        "kv_scatter",
        1,
        [part],
        [jax.ShapeDtypeStruct((rows // n_c, width), f32)],
        [pltpu.VMEM((rows, width), bf16)] * 4,
        7,
        ([False], [True]),
    )[0]


def middle_kernel(part, x_ref, gain_ref, mid_ref, factor_ref, out, own, core, sent, got, xn, *sems):
    wires, to = Wires(*sems), partners()
    meet([to[k] for k in ("core", "y", "z", "far")])
    middle = wide(x_ref[...]) + scatter_rank(wires, to, part, own, core, sent, got)
    mid_ref[...] = middle
    factor = lax.rsqrt(jnp.mean(middle * middle, axis=-1, keepdims=True) + EPSILON)
    factor_ref[...] = factor
    xn[...] = (middle * factor * gain_ref[...]).astype(bf16)
    blocks = out.shape[0] // 2
    mine = wires.here(xn, out.at[0])
    from_far = wires.copy(xn, out.at[blocks], to["far"])
    last = gather_pair(wires, to, xn, out, 0)
    from_far.wait_recv()
    last += gather_pair(wires, to, out.at[blocks], out, blocks)
    for one in last:
        one.wait_recv()
    mine.wait()
    wires.finish()


def middle_norm(part, inputs_part, gain):
    rows, width = inputs_part.shape
    return remote_call(
        middle_kernel,
        "middle_norm",
        2,
        [part.reshape(4, rows, width), inputs_part, gain],
        [
            jax.ShapeDtypeStruct((rows, width), f32),
            jax.ShapeDtypeStruct((rows, 1), f32),
            jax.ShapeDtypeStruct((16, rows, width), bf16),
        ],
        [
            pltpu.VMEM((2, rows, width), bf16),
            pltpu.VMEM((2, rows, width), bf16),
            pltpu.VMEM((rows, width), bf16),
            pltpu.VMEM((rows, width), bf16),
            pltpu.VMEM((rows, width), bf16),
        ],
        32,
        ([False, True, True], [True, True, False]),
    )


def norm_back_rows(values, factor, gain, grad_normed):
    gained = gain * grad_normed
    inner = jnp.mean(gained * values, axis=-1, keepdims=True)
    grad_values = factor * gained - values * (factor * factor * factor) * inner
    return grad_values, jnp.sum(grad_normed * values * factor, axis=0, keepdims=True)


MIXED = (0, 2, 1, 3)


def middle_back_kernel(part, mid_ref, factor_ref, gain_ref, dy_ref, dmid_ref, dgain_ref, out, *rest):
    low, rest = rest[0], rest[1:]
    wires, to = Wires(*rest[-3:]), partners()
    meet([to[k] for k in ("core", "y", "z")])
    grad_normed = scatter_pair(wires, to, part, *rest[:-3])
    du, dgain = norm_back_rows(mid_ref[...], factor_ref[...], gain_ref[...], grad_normed)
    dgain_ref[...] = dgain
    dmid = wide(dy_ref[...]) + du
    dmid_ref[...] = dmid
    low[...] = dmid.astype(bf16)
    gather_rank(wires, to, low, out, lambda j, flip: MIXED.index(j ^ flip))
    wires.finish()


def pair_scratch(rows, width):
    return [
        pltpu.VMEM((4, rows, width), bf16),
        pltpu.VMEM((4, rows, width), bf16),
        pltpu.VMEM((3, rows, width), bf16),
        pltpu.VMEM((rows, width), bf16),
        pltpu.VMEM((rows, width), bf16),
        pltpu.VMEM((rows // 2, width), bf16),
        pltpu.VMEM((rows // 2, width), bf16),
    ]


def middle_back(part, middle, factor, gain, dy_part):
    rows, width = middle.shape
    return remote_call(
        middle_back_kernel,
        "middle_back",
        3,
        [part.reshape(8, rows, width), middle, factor, gain, dy_part],
        [
            jax.ShapeDtypeStruct((rows, width), f32),
            jax.ShapeDtypeStruct((1, width), f32),
            jax.ShapeDtypeStruct((4, rows, width), bf16),
        ],
        [pltpu.VMEM((rows, width), bf16)] + pair_scratch(rows, width),
        16,
        ([False, True, True, True, True], [True, True, False]),
    )


def outputs_kernel(part, mid_ref, out, low, *rest):
    wires, to = Wires(*rest[-3:]), partners()
    t = lax.axis_index("tensor")
    flip = lambda x, bit: x + bit * (1 - 2 * lax.rem(x // bit, 2))
    meet([to[k] for k in ("core", "y", "z")])
    low[...] = (mid_ref[...] + scatter_pair(wires, to, part, *rest[:-3])).astype(bf16)
    gather_rank(wires, to, low, out, lambda j, _: t if j == 0 else flip(t, j))
    wires.finish()


def final_outputs(part, middle):
    rows, width = middle.shape
    return remote_call(
        outputs_kernel,
        "final_outputs",
        4,
        [part.reshape(8, rows, width), middle],
        [jax.ShapeDtypeStruct((4, rows, width), bf16)],
        [pltpu.VMEM((rows, width), bf16)] + pair_scratch(rows, width),
        16,
        ([False, True], [False]),
    )[0].reshape(4 * rows, width)


def input_back_kernel(part, x_ref, factor_ref, gain_ref, dmid_ref, dgain_ref, out, *rest):
    low, own, core, sent, got = rest[:-3]
    wires, to = Wires(*rest[-3:]), partners()
    t = lax.axis_index("tensor")
    flip = lambda x, bit: x + bit * (1 - 2 * lax.rem(x // bit, 2))
    meet([to[k] for k in ("core", "y")])
    grad_normed = scatter_rank(wires, to, part, own, core, sent, got)
    du, dgain = norm_back_rows(wide(x_ref[...]), factor_ref[...], gain_ref[...], grad_normed)
    dgain_ref[...] = dgain
    low[...] = (dmid_ref[...] + du).astype(bf16)
    gather_rank(wires, to, low, out, lambda j, _: t if j == 0 else flip(t, j))
    wires.finish()


def input_back(part, inputs_part, factor, gain, grad_middle):
    rows, width = inputs_part.shape
    return remote_call(
        input_back_kernel,
        "input_back",
        5,
        [part.reshape(4, rows, width), inputs_part, factor, gain, grad_middle],
        [
            jax.ShapeDtypeStruct((1, width), f32),
            jax.ShapeDtypeStruct((4, rows, width), bf16),
        ],
        [
            pltpu.VMEM((rows, width), bf16),
            pltpu.VMEM((2, rows, width), bf16),
            pltpu.VMEM((2, rows, width), bf16),
            pltpu.VMEM((rows, width), bf16),
            pltpu.VMEM((rows, width), bf16),
        ],
        16,
        ([False, True, True, True, True], [True, False]),
    )


def build(n_f, n_c, n_t):
    def flip(x, axis, bit):
        size = {"fsdp": n_f, "context": n_c, "tensor": n_t}[axis]
        return lax.ppermute(x, axis, [(i, i ^ bit) for i in range(size)])

    def by_bit(bit, x, other, axis):
        return jnp.where(
            bit == 0,
            jnp.concatenate([x, other], axis=axis),
            jnp.concatenate([other, x], axis=axis),
        )

    def local(
        inputs,
        cotangent,
        blocks,
        attn_gain,
        w_query,
        b_query,
        w_key,
        b_key,
        w_value,
        b_value,
        w_out,
        ffn_gain,
        w_gate,
        w_up,
        w_down,
    ):
        rows, width = inputs.shape
        f = lax.axis_index("fsdp")
        c = lax.axis_index("context")
        t = lax.axis_index("tensor")
        core, parity, pair = t % 2, c % 2, c // 2
        heads = w_query.shape[1] // HD
        group = (t * heads) // (H // KV)
        part = rows // n_t
        units_all = w_gate.shape[1]
        units = units_all // 2

        def gather_f(x, axis):
            if n_f == 2:
                return by_bit(f, x, flip(x, "fsdp", 1), axis)
            return lax.all_gather(x, "fsdp", axis=axis, tiled=True)

        def columns_f(parts):
            parts = [x.astype(bf16) for x in parts]
            return by_bit(f, parts[0], parts[1], 1) if n_f == 2 else parts[0]

        def grad_f(left, right, side):
            if n_f == 2:
                half = width // 2
                source = (left, right)[side]
                own = lax.dynamic_slice_in_dim(source, f * half, half, 1)
                far = lax.dynamic_slice_in_dim(source, (1 - f) * half, half, 1)
                pick = lambda x: dot_rows(x, right) if side == 0 else dot_rows(left, x)
                got = flip(pick(far).astype(bf16), "fsdp", 1)
                return pick(own) + got.astype(f32)
            return lax.psum_scatter(
                dot_rows(left, right).astype(bf16), "fsdp", scatter_dimension=side, tiled=True
            ).astype(f32)

        def sum_c(x):
            for bit in (1, 2):
                low = x.astype(bf16)
                x = low.astype(f32) + flip(low, "context", bit).astype(f32)
            return x

        order = MIXED

        def mixed(x):
            return jnp.concatenate(
                [lax.dynamic_slice_in_dim(x, (t ^ j) * part, part, 0) for j in order], axis=0
            )

        def natural(x):
            blocks_of = [x[i * part : (i + 1) * part] for i in range(n_t)]
            place = [blocks_of[order.index(j)] for j in range(n_t)]
            out = jnp.stack(place)
            return jnp.concatenate(
                [lax.dynamic_index_in_dim(out, n ^ t, 0, keepdims=False) for n in range(n_t)],
                axis=0,
            )

        def grow(x, axis, bit):
            return jnp.concatenate([x, flip(x, axis, bit)], axis=0)

        def gather_t(x):
            return grow(grow(x, "tensor", 2), "tensor", 1)

        small = jnp.concatenate(
            [v.reshape(1, -1) for v in (attn_gain, ffn_gain, b_query, b_key, b_value)], axis=1
        )
        column = lambda w: lax.dynamic_slice_in_dim(w, group * HD, HD, 1)
        w_kv_own = jnp.where(core == 0, column(w_key), column(w_value))
        pieces_f = lambda x, axis: (
            [x, flip(x, "fsdp", 1)]
            if n_f == 2
            else [lax.all_gather(x, "fsdp", axis=axis, tiled=True)]
        )
        meta = jnp.stack([f, 1 - f, core, pair]).astype(jnp.int32)
        w_qkv = pieces_f(jnp.concatenate([w_query, w_kv_own], axis=1), 0)
        small = gather_f(small, 0)
        w_out_all = gather_f(w_out, 1)
        piece = attn_gain.shape[0]
        gain_first = small[:, :piece].reshape(1, width).astype(f32)
        gain_second = small[:, piece : 2 * piece].reshape(1, width).astype(f32)
        bias_of = lambda lo, n: (
            small[:, lo : lo + n * (HD // n_f)]
            .reshape(n_f, n, HD // n_f)
            .transpose(1, 0, 2)
            .reshape(n, HD)
            .astype(f32)
        )
        at = 2 * piece
        bq = bias_of(at, heads)
        bk = bias_of(at + heads * (HD // n_f), KV)
        bv = bias_of(at + (heads + KV) * (HD // n_f), KV)
        b_kv = lax.dynamic_index_in_dim(jnp.where(core == 0, bk, bv), group, 0)

        unit_slice = lambda w: lax.dynamic_slice_in_dim(w, parity * units, units, 0)
        w_units = pieces_f(
            jnp.concatenate([unit_slice(w) for w in (w_gate.T, w_up.T, w_down)], axis=0), 1
        )

        dy_own = mixed(cotangent)[: 2 * part]
        dy_near = jnp.concatenate([dy_own, flip(dy_own, "context", 1)], axis=0)
        dy_pair = grow(dy_near, "tensor", 1)
        dy_far = grow(grow(flip(dy_own, "context", 2), "context", 1), "tensor", 1)
        dy_all = jnp.concatenate([dy_pair, dy_far], axis=0).reshape(2, -1, part, width)

        seq_blocks = blocks[0].reshape(n_c, -1)
        own_blocks = seq_blocks.shape[1]
        key_blocks = jnp.concatenate(
            [lax.dynamic_index_in_dim(seq_blocks, c ^ j, 0, keepdims=False) for j in range(n_c)]
        )
        positions = (
            key_blocks[:own_blocks, None] * BLOCK + jnp.arange(BLOCK, dtype=jnp.int32)[None, :]
        ).reshape(-1)
        cosine, sine = rope_tables(positions)
        bias = jnp.concatenate([bq.reshape(1, -1), b_kv], axis=1)
        normed, factor_first, queries, kv_own = qkv(
            meta, inputs, gain_first, bias, cosine, sine, w_qkv
        )
        kv = kv_gather(kv_own)
        attended, lse = attention(key_blocks, queries, kv)
        attended_mixed = mixed(attended)
        inputs_part = lax.dynamic_slice_in_dim(inputs, t * part, part, 0)
        middle, factor_second, normed2 = middle_norm(
            dot(attended_mixed, w_out_all).astype(bf16), inputs_part, gain_second
        )

        normed2 = normed2.reshape(2, -1, part, width)
        hid_pair, dg_pair, du_pair, dx_part = ffn(meta, normed2, dy_all, w_units, True)
        hid_far, dg_far, du_far = ffn(meta, normed2, dy_all, w_units, False)
        grad_args = (normed2, dy_all, (hid_pair, hid_far), (dg_pair, dg_far), (du_pair, du_far))
        if n_f == 2:
            unit_sent = unit_grads(meta, 1, 2, *grad_args)
            unit_got = [flip(x, "fsdp", 1) for x in unit_sent]
            dx_part, _ = lax.optimization_barrier((dx_part, unit_sent))
        else:
            unit_own = [
                lax.psum_scatter(x, "fsdp", scatter_dimension=1, tiled=True)
                for x in unit_grads(meta, 0, 1, *grad_args)
            ]
            unit_got = [jnp.zeros_like(x) for x in unit_own]

        def unit_done(own, got):
            low = (own.astype(f32) + got.astype(f32)).astype(bf16)
            return by_bit(parity, low, flip(low, "context", 1), 0).astype(f32)

        dy_part = lax.dynamic_slice_in_dim(cotangent, t * part, part, 0)
        grad_middle, ffn_gain_grad, grad_middle_low = middle_back(
            dx_part, middle, factor_second, gain_second, dy_part
        )
        grad_middle_low = grad_middle_low.reshape(rows, width)
        wo_grad = sum_c(grad_f(attended_mixed, grad_middle_low, 1))
        grad_attended = natural(dot_cols(grad_middle_low, w_out_all).astype(bf16))

        dq_low, dkv = attention_back(key_blocks, queries, grad_attended, lse, cosine, sine, kv)
        dkv = kv_scatter(dkv)
        if n_f == 2:
            late_args, _ = lax.optimization_barrier((grad_args, dkv))
            unit_own = unit_grads(meta, 0, 2, *late_args)
            unit_got, _ = lax.optimization_barrier((unit_got, dkv))
        dkv_low = jnp.where(core == 0, rotate_back(dkv, cosine, sine), dkv).astype(bf16)
        wq_grad = sum_c(grad_f(normed, dq_low, 0))
        wkv_own = sum_c(grad_f(normed, dkv_low, 0)).astype(bf16)
        wkv_stack = gather_t(wkv_own)
        depth = wkv_own.shape[0]
        wkv_of = [wkv_stack[order.index(j) * depth : (order.index(j) + 1) * depth] for j in range(n_t)]
        wkv_stack = jnp.stack(wkv_of)
        wkv_rank = [
            lax.dynamic_index_in_dim(wkv_stack, n ^ t, 0, keepdims=False).astype(f32)
            for n in range(n_t)
        ]
        wk_grad = jnp.concatenate(wkv_rank[0::2], axis=1)
        wv_grad = jnp.concatenate(wkv_rank[1::2], axis=1)

        d_qkv = mixed(jnp.concatenate([dq_low, dkv_low], axis=1))
        factor_part = lax.dynamic_slice_in_dim(factor_first, t * part, part, 0)
        attn_gain_grad, input_grad = input_back(
            columns_f([dot_cols(d_qkv, w) for w in w_qkv]),
            inputs_part,
            factor_part,
            gain_first,
            grad_middle,
        )
        input_grad = input_grad.reshape(rows, width)
        outputs = final_outputs(
            columns_f([dot(hid_pair, w[2 * units :]) for w in w_units]), middle
        )
        wg_grad, wu_grad, wd_grad = (unit_done(a, b) for a, b in zip(unit_own, unit_got))
        wg_grad, wu_grad = wg_grad.T, wu_grad.T

        bq_grad = jnp.sum(dq_low.astype(f32), axis=0)
        bkv_grad = jnp.sum(dkv_low.astype(f32), axis=0)
        slots = jnp.zeros((n_t, (heads + 1) * HD), f32)
        slots = lax.dynamic_update_slice(
            slots, jnp.concatenate([bq_grad, bkv_grad])[None], (t, 0)
        )
        packed = lax.psum(
            jnp.concatenate([attn_gain_grad[0], ffn_gain_grad[0], slots.reshape(-1)]),
            ("fsdp", "context", "tensor"),
        )
        attn_gain_grad = lax.dynamic_slice_in_dim(packed, f * piece, piece, 0)
        ffn_gain_grad = lax.dynamic_slice_in_dim(packed, width + f * piece, piece, 0)
        slots = packed[2 * width :].reshape(n_t, heads + 1, HD)
        slots = lax.dynamic_slice_in_dim(slots, f * (HD // n_f), HD // n_f, 2)
        bq_out = lax.dynamic_index_in_dim(slots, t, 0, keepdims=False)[:heads]
        bk_out = slots[0::2, heads]
        bv_out = slots[1::2, heads]

        return (
            outputs,
            input_grad,
            attn_gain_grad,
            wq_grad,
            bq_out,
            wk_grad,
            bk_out,
            wv_grad,
            bv_out,
            wo_grad,
            ffn_gain_grad,
            wg_grad,
            wu_grad,
            wd_grad,
        )

    return local


def solution(mesh):
    in_specs = (
        P(("fsdp", "context"), None),
        P(("fsdp", "context"), None),
        P("fsdp", None),
        P("fsdp"),
        P("fsdp", "tensor"),
        P("tensor", "fsdp"),
        P("fsdp", None),
        P(None, "fsdp"),
        P("fsdp", None),
        P(None, "fsdp"),
        P("tensor", "fsdp"),
        P("fsdp"),
        P("fsdp", "tensor"),
        P("fsdp", "tensor"),
        P("tensor", "fsdp"),
    )
    out_specs = (
        P(("fsdp", "context"), None),
        P(("fsdp", "context"), None),
        P("fsdp"),
        P("fsdp", "tensor"),
        P("tensor", "fsdp"),
        P("fsdp", None),
        P(None, "fsdp"),
        P("fsdp", None),
        P(None, "fsdp"),
        P("tensor", "fsdp"),
        P("fsdp"),
        P("fsdp", "tensor"),
        P("fsdp", "tensor"),
        P("tensor", "fsdp"),
    )
    local = build(mesh.shape["fsdp"], mesh.shape["context"], mesh.shape["tensor"])
    return jax.shard_map(local, mesh=mesh, in_specs=in_specs, out_specs=out_specs, check_vma=False)
```

```python
import functools

import jax
import jax.numpy as jnp
from jax import lax
from jax.experimental import pallas as pl
from jax.experimental.pallas import tpu as pltpu
from jax.sharding import PartitionSpec as P

H = 12
KV = 2
HD = 128
BLOCK = 256

EPSILON = 1e-06
ROPE_BASE = 1000000.0
MASKED = -1e30
SCALING = HD ** (-0.5)
LANES = 128
VMEM_LIMIT = 60 << 20

f32 = jnp.float32
bf16 = jnp.bfloat16


def rope_tables(positions):
    halfway = HD // 2
    frequency = ROPE_BASE ** (-(jnp.arange(halfway, dtype=f32) * 2.0 / HD))
    angles = positions.astype(f32)[:, None] * frequency[None, :]
    cosine, sine = jnp.cos(angles), jnp.sin(angles)
    return (jnp.concatenate([cosine, cosine], axis=1), jnp.concatenate([sine, sine], axis=1))


def rotate(field, cosine, sine):
    halfway = HD // 2
    turned = jnp.concatenate([-field[..., halfway:], field[..., :halfway]], axis=-1)
    return field * cosine + turned * sine


def rotate_back(grad_field, cosine, sine):
    halfway = HD // 2
    moved = grad_field * sine
    turned = jnp.concatenate([moved[..., halfway:], -moved[..., :halfway]], axis=-1)
    return grad_field * cosine + turned


def dot(left, right):
    return jnp.dot(left, right, preferred_element_type=f32)


def dot_rows(left, right):
    return lax.dot_general(left, right, (((0,), (0,)), ((), ())), preferred_element_type=f32)


def dot_cols(left, right):
    return lax.dot_general(left, right, (((1,), (1,)), ((), ())), preferred_element_type=f32)


def mask_row(kb_ref, own_block, key_blocks):
    return jnp.concatenate(
        [
            jnp.full((1, BLOCK), jnp.where(kb_ref[j] <= own_block, 0.0, MASKED), f32)
            for j in range(key_blocks)
        ],
        axis=1,
    )


def attention_kernel(key_blocks, kb_ref, q_ref, k_ref, v_ref, o_ref, lse_ref):
    bias = mask_row(kb_ref, kb_ref[pl.program_id(1)], key_blocks)
    scores = dot_cols(q_ref[...], k_ref[...]) * SCALING + bias
    row_max = jnp.max(scores, axis=1, keepdims=True)
    expo = jnp.exp(scores - row_max)
    total = jnp.sum(expo, axis=1, keepdims=True)
    probability = (expo * (1.0 / total)).astype(bf16)
    o_ref[...] = dot(probability, v_ref[...]).astype(bf16)
    lse_ref[0] = row_max + jnp.log(total)


def attention(key_blocks, queries, kv):
    rows, width = queries.shape
    heads = width // HD
    whole = lambda kind: pl.BlockSpec((None,) + kv.shape[1:], lambda h, i, kb: (kind, 0, 0))
    tile = pl.BlockSpec((BLOCK, HD), lambda h, i, kb: (i, h))
    return pl.pallas_call(
        functools.partial(attention_kernel, kv.shape[1] // BLOCK),
        name="attention",
        grid_spec=pltpu.PrefetchScalarGridSpec(
            num_scalar_prefetch=1,
            grid=(heads, rows // BLOCK),
            in_specs=[tile, whole(0), whole(1)],
            out_specs=[tile, pl.BlockSpec((1, BLOCK, 1), lambda h, i, kb: (h, i, 0))],
        ),
        out_shape=[
            jax.ShapeDtypeStruct((rows, width), bf16),
            jax.ShapeDtypeStruct((heads, rows, 1), f32),
        ],
        compiler_params=pltpu.CompilerParams(vmem_limit_bytes=VMEM_LIMIT),
    )(key_blocks, queries, kv, kv)


def attention_back_kernel(
    key_blocks,
    kb_ref,
    q_ref,
    do_ref,
    lse_ref,
    cos_ref,
    sin_ref,
    k_ref,
    v_ref,
    dq_ref,
    dkv_ref,
    dk_ref,
    dv_ref,
):
    head, i = pl.program_id(0), pl.program_id(1)

    @pl.when((head == 0) & (i == 0))
    def _():
        dk_ref[...] = jnp.zeros_like(dk_ref)
        dv_ref[...] = jnp.zeros_like(dv_ref)

    bias = mask_row(kb_ref, kb_ref[i], key_blocks)
    scores = dot_cols(q_ref[...], k_ref[...]) * SCALING + bias
    probability = jnp.exp(scores - lse_ref[0])
    grad_probs = dot_cols(do_ref[...], v_ref[...])
    inner = jnp.sum(probability * grad_probs, axis=1, keepdims=True)
    grad_scores = (probability * (grad_probs - inner)).astype(bf16)
    grad_query = dot(grad_scores, k_ref[...]) * SCALING
    moved = grad_query * sin_ref[...]
    sign = jnp.where(lax.broadcasted_iota(jnp.int32, moved.shape, 1) < HD // 2, 1.0, -1.0)
    dq_ref[...] = (
        grad_query * cos_ref[...] + pltpu.roll(moved, HD // 2, 1) * sign
    ).astype(bf16)
    dk_ref[...] += dot_rows(grad_scores, q_ref[...]) * SCALING
    dv_ref[...] += dot_rows(probability.astype(bf16), do_ref[...])

    @pl.when((head == pl.num_programs(0) - 1) & (i == pl.num_programs(1) - 1))
    def _():
        dkv_ref[0] = dk_ref[...].astype(bf16)
        dkv_ref[1] = dv_ref[...].astype(bf16)


def attention_back(key_blocks, queries, grad_out, lse, cosine, sine, kv):
    rows, width = queries.shape
    heads = width // HD
    whole = lambda kind: pl.BlockSpec((None,) + kv.shape[1:], lambda h, i, kb: (kind, 0, 0))
    tile = pl.BlockSpec((BLOCK, HD), lambda h, i, kb: (i, h))
    table = pl.BlockSpec((BLOCK, HD), lambda h, i, kb: (i, 0))
    return pl.pallas_call(
        functools.partial(attention_back_kernel, kv.shape[1] // BLOCK),
        name="attention_back",
        grid_spec=pltpu.PrefetchScalarGridSpec(
            num_scalar_prefetch=1,
            grid=(heads, rows // BLOCK),
            in_specs=[
                tile,
                tile,
                pl.BlockSpec((1, BLOCK, 1), lambda h, i, kb: (h, i, 0)),
                table,
                table,
                whole(0),
                whole(1),
            ],
            out_specs=[tile, pl.BlockSpec(kv.shape, lambda h, i, kb: (0, 0, 0))],
            scratch_shapes=[pltpu.VMEM(kv.shape[1:], f32)] * 2,
        ),
        out_shape=[
            jax.ShapeDtypeStruct((rows, width), bf16),
            jax.ShapeDtypeStruct(kv.shape, bf16),
        ],
        compiler_params=pltpu.CompilerParams(vmem_limit_bytes=VMEM_LIMIT),
    )(key_blocks, queries, grad_out, lse, cosine, sine, kv, kv)


def qkv_kernel(pieces, meta_ref, x_ref, gain_ref, bias_ref, cos_ref, sin_ref, *refs):
    weights, (xn_ref, factor_ref, q_ref, kv_ref) = refs[:pieces], refs[pieces:]
    values = x_ref[...].astype(f32)
    factor = lax.rsqrt(jnp.mean(values * values, axis=-1, keepdims=True) + EPSILON)
    factor_ref[...] = factor
    xn_ref[...] = (values * factor * gain_ref[...]).astype(bf16)
    total = bias_ref[...]
    for j, weight in enumerate(weights):
        depth = weight.shape[0]
        total = total + dot(xn_ref[:, columns_of(meta_ref, j, depth, pieces)], weight[...])
    cosine, sine = cos_ref[...], sin_ref[...]
    sign = jnp.where(lax.broadcasted_iota(jnp.int32, cosine.shape, 1) < HD // 2, -1.0, 1.0)
    heads = q_ref.shape[1] // HD
    for h in range(heads + 1):
        own = total[:, h * HD : (h + 1) * HD]
        turned = own * cosine + pltpu.roll(own, HD // 2, 1) * sign * sine
        if h < heads:
            q_ref[:, h * HD : (h + 1) * HD] = turned.astype(bf16)
        else:
            kv_ref[...] = jnp.where(meta_ref[2] == 0, turned, own).astype(bf16)


def columns_of(meta_ref, j, depth, pieces):
    if pieces == 1:
        return slice(None)
    return pl.ds(pl.multiple_of(meta_ref[j] * depth, LANES), depth)


def qkv(meta, inputs, gain, bias, cosine, sine, weights):
    rows, width = inputs.shape
    out = weights[0].shape[1]
    tile = 256
    row = lambda n: pl.BlockSpec((tile, n), lambda i, m: (i, 0))
    fixed = lambda w: pl.BlockSpec(w.shape, lambda i, m: (0, 0))
    return pl.pallas_call(
        functools.partial(qkv_kernel, len(weights)),
        name="qkv",
        grid_spec=pltpu.PrefetchScalarGridSpec(
            num_scalar_prefetch=1,
            grid=(rows // tile,),
            in_specs=[row(width), fixed(gain), fixed(bias), row(HD), row(HD)]
            + [fixed(w) for w in weights],
            out_specs=[row(width), row(1), row(out - HD), row(HD)],
        ),
        out_shape=[
            jax.ShapeDtypeStruct((rows, width), bf16),
            jax.ShapeDtypeStruct((rows, 1), f32),
            jax.ShapeDtypeStruct((rows, out - HD), bf16),
            jax.ShapeDtypeStruct((rows, HD), bf16),
        ],
        compiler_params=pltpu.CompilerParams(vmem_limit_bytes=VMEM_LIMIT),
    )(meta, inputs, gain, bias, cosine, sine, *weights)


def ffn_kernel(with_dx, pieces, meta_ref, x_ref, dy_ref, *refs):
    wg, wu, wd = (refs[m * pieces : (m + 1) * pieces] for m in range(3))
    outs = refs[-5:] if with_dx else refs[-3:]
    hid_ref, dg_ref, du_ref = outs[:3]
    columns = [columns_of(meta_ref, j, wg[j].shape[1], pieces) for j in range(pieces)]
    gate = sum(dot_cols(x_ref[:, at], w[...]) for at, w in zip(columns, wg))
    up = sum(dot_cols(x_ref[:, at], w[...]) for at, w in zip(columns, wu))
    grad_hidden = sum(dot_cols(dy_ref[:, at], w[...]) for at, w in zip(columns, wd))
    sigma = 1.0 / (1.0 + jnp.exp(-gate))
    gated = gate * sigma
    hidden = (gated * up).astype(bf16)
    hid_ref[...] = hidden
    grad_gate = (grad_hidden * up * (sigma + gated * (1.0 - sigma))).astype(bf16)
    grad_up = (grad_hidden * gated).astype(bf16)
    dg_ref[...] = grad_gate
    du_ref[...] = grad_up
    if with_dx:
        for at, g, u in zip(columns, wg, wu):
            outs[3][:, at] = (dot(grad_gate, g[...]) + dot(grad_up, u[...])).astype(bf16)
        for at, d in zip(columns, wd):
            outs[4][:, at] = dot(hidden, d[...]).astype(bf16)


def ffn(meta, normed, grad_out, weights, with_dx):
    width = normed.shape[-1]
    half = 0 if with_dx else 1
    rows = normed.shape[1] * normed.shape[2]
    units = weights[0].shape[0] // 3
    tile = 512
    steps = rows // tile
    flat = lambda x: x.reshape(-1, width)
    row = lambda n: pl.BlockSpec((tile, n), lambda i, m: (i, 0))
    read = pl.BlockSpec((tile, width), lambda i, m: (i + half * steps, 0))
    weight = lambda w, k: pl.BlockSpec(
        (units, w.shape[1]), lambda i, m: (k, 0), pipeline_mode=pl.Buffered(1)
    )
    widths = [units] * 3 + [width] * (2 * with_dx)
    return pl.pallas_call(
        functools.partial(ffn_kernel, with_dx, len(weights)),
        name="ffn_pair" if with_dx else "ffn_far",
        grid_spec=pltpu.PrefetchScalarGridSpec(
            num_scalar_prefetch=1,
            grid=(steps,),
            in_specs=[read, read] + [weight(w, k) for k in range(3) for w in weights],
            out_specs=[row(n) for n in widths],
        ),
        out_shape=[jax.ShapeDtypeStruct((rows, n), bf16) for n in widths],
        compiler_params=pltpu.CompilerParams(vmem_limit_bytes=VMEM_LIMIT),
    )(meta, flat(normed), flat(grad_out), *(list(weights) * 3))


def unit_grads_kernel(meta_ref, x, y, hp, hf, gp, gf, up, uf, og, oud, ag, au, ad):
    step = pl.program_id(0)

    @pl.when(step == 0)
    def _():
        for acc in (ag, au, ad):
            acc[...] = jnp.zeros_like(acc)

    for use, h, g, u in ((True, hp, gp, up), (False, hf, gf, uf)):

        @pl.when((step // (pl.num_programs(0) // 2) == meta_ref[3]) == use)
        def _():
            ag[...] += dot_rows(g[...], x[...])
            au[...] += dot_rows(u[...], x[...])
            ad[...] += dot_rows(h[...], y[...])

    @pl.when(step == pl.num_programs(0) - 1)
    def _():
        units = og.shape[0]
        og[...] = ag[...].astype(bf16)
        oud[:units] = au[...].astype(bf16)
        oud[units:] = ad[...].astype(bf16)


def unit_grads(meta, which, pieces, x, y, hid, dg, du):
    width = x.shape[-1]
    rows, units = dg[0].shape
    depth = width // pieces
    tile = 512
    steps = rows // tile
    shard = (lambda m: m[which]) if pieces > 1 else (lambda m: 0)
    near = lambda i, m: jnp.clip(i - steps * m[3], 0, steps - 1)
    far = lambda i, m: jnp.clip(i - steps * (1 - m[3]), 0, steps - 1)
    feature = pl.BlockSpec(
        (tile, depth), lambda i, m: (lax.rem(i + steps * m[3], 2 * steps), shard(m))
    )
    unit = lambda at: pl.BlockSpec((tile, units), lambda i, m: (at(i, m), 0))
    return pl.pallas_call(
        unit_grads_kernel,
        name=f"unit_grads_{which}",
        grid_spec=pltpu.PrefetchScalarGridSpec(
            num_scalar_prefetch=1,
            grid=(2 * steps,),
            in_specs=[feature] * 2 + [unit(near), unit(far)] * 3,
            out_specs=[
                pl.BlockSpec((k * units, depth), lambda i, m: (0, 0), pipeline_mode=pl.Buffered(1))
                for k in (1, 2)
            ],
            scratch_shapes=[pltpu.VMEM((units, depth), f32)] * 3,
        ),
        out_shape=[jax.ShapeDtypeStruct((k * units, depth), bf16) for k in (1, 2)],
        compiler_params=pltpu.CompilerParams(vmem_limit_bytes=VMEM_LIMIT),
    )(meta, x.reshape(-1, width), y.reshape(-1, width), *hid, *dg, *du)


class Wires:
    def __init__(self, sends, receives, locals_):
        self.sends, self.receives, self.locals = sends, receives, locals_
        self.used = self.used_local = 0
        self.started = []

    def copy(self, source, target, device):
        k = self.used
        self.used += 1
        one = pltpu.make_async_remote_copy(
            source,
            target,
            self.sends.at[k],
            self.receives.at[k],
            device_id=device,
            device_id_type=pl.DeviceIdType.MESH,
        )
        one.start()
        self.started.append(one)
        return one

    def here(self, source, target):
        k = self.used_local
        self.used_local += 1
        one = pltpu.make_async_copy(source, target, self.locals.at[k])
        one.start()
        return one

    def finish(self):
        for one in self.started:
            one.wait_send()


def meet(devices):
    barrier = pltpu.get_barrier_semaphore()
    for device in devices:
        pl.semaphore_signal(barrier, inc=1, device_id=device, device_id_type=pl.DeviceIdType.MESH)
    pl.semaphore_wait(barrier, len(devices))


def partners():
    c, t = lax.axis_index("context"), lax.axis_index("tensor")
    flip = lambda x, bit: x + bit * (1 - 2 * lax.rem(x // bit, 2))
    return {
        "core": {"tensor": flip(t, 1)},
        "y": {"tensor": flip(t, 2)},
        "z": {"context": flip(c, 1)},
        "far": {"context": flip(c, 2)},
        "last": {"context": flip(flip(c, 1), 2)},
    }


def wide(x):
    return x.astype(f32)


def scatter_rank(wires, to, part, own, got_core, sent, got_y):
    size = part.shape[1] // 2
    halves = [pl.ds(0, size), pl.ds(size, size)]
    from_core = {}
    for block in (1, 0):
        for k, at in enumerate(halves):
            from_core[block, k] = wires.copy(
                part.at[2 + block, at], got_core.at[block, at], to["core"]
            )
    mine = wires.here(part.at[pl.ds(0, 2)], own)
    mine.wait()
    from_y = []
    for k, at in enumerate(halves):
        from_core[1, k].wait_recv()
        sent[at] = (wide(own[1, at]) + wide(got_core[1, at])).astype(bf16)
        from_y.append(wires.copy(sent.at[at], got_y.at[at], to["y"]))
    for k in range(2):
        from_core[0, k].wait_recv()
    total = wide(own[0]) + wide(got_core[0])
    for one in from_y:
        one.wait_recv()
    return total + wide(got_y[...])


def scatter_pair(wires, to, part, own, got_core, sent, got_y, got_z, diag_y, diag_z):
    size = part.shape[1] // 2
    low, high = pl.ds(0, size), pl.ds(size, size)
    from_core = {j: wires.copy(part.at[4 + j], got_core.at[j], to["core"]) for j in (3, 1, 2, 0)}
    mine = wires.here(part.at[pl.ds(0, 4)], own)
    yield
    mine.wait()
    both = lambda j, at: wide(own[j, at]) + wide(got_core[j, at])
    from_core[3].wait_recv()
    sent[2] = (wide(own[3]) + wide(got_core[3])).astype(bf16)
    via_z = wires.copy(sent.at[2, low], diag_z, to["z"])
    via_y = wires.copy(sent.at[2, high], diag_y, to["y"])
    from_core[1].wait_recv()
    sent[0, high] = both(1, high).astype(bf16)
    y_high = wires.copy(sent.at[0, high], got_y.at[high], to["y"])
    from_core[2].wait_recv()
    sent[1, low] = both(2, low).astype(bf16)
    z_low = wires.copy(sent.at[1, low], got_z.at[low], to["z"])
    yield
    via_z.wait_recv()
    sent[0, low] = (both(1, low) + wide(diag_z[...])).astype(bf16)
    y_low = wires.copy(sent.at[0, low], got_y.at[low], to["y"])
    via_y.wait_recv()
    sent[1, high] = (both(2, high) + wide(diag_y[...])).astype(bf16)
    z_high = wires.copy(sent.at[1, high], got_z.at[high], to["z"])
    yield
    from_core[0].wait_recv()
    total = wide(own[0]) + wide(got_core[0])
    for one in (y_high, z_low, y_low, z_high):
        one.wait_recv()
    return total + wide(got_y[...]) + wide(got_z[...])


def result_of(steps):
    while True:
        try:
            next(steps)
        except StopIteration as done:
            return done.value


def gather_rank(wires, to, block, out, at):
    size = block.shape[0] // 2
    halves = [pl.ds(0, size), pl.ds(size, size)]
    mine = wires.here(block, out.at[at(0, 0)])
    from_y = [wires.copy(block.at[h], out.at[at(0, 2), h], to["y"]) for h in halves]
    from_core = [wires.copy(block, out.at[at(0, 1)], to["core"])]
    yield
    for h, one in zip(halves, from_y):
        one.wait_recv()
        from_core.append(wires.copy(out.at[at(2, 0), h], out.at[at(2, 1), h], to["core"]))
    for one in from_core:
        one.wait_recv()
    mine.wait()


def gather_pair(wires, to, block, out, base):
    size = block.shape[0] // 2
    low, high = pl.ds(0, size), pl.ds(size, size)
    at = lambda j: out.at[base + j]
    from_y = wires.copy(block, at(1), to["y"])
    from_z = wires.copy(block, at(2), to["z"])
    from_core = [wires.copy(block, at(4), to["core"])]
    from_y.wait_recv()
    via_z = wires.copy(out.at[base + 1, low], out.at[base + 3, low], to["z"])
    from_core.append(wires.copy(at(1), at(5), to["core"]))
    from_z.wait_recv()
    via_y = wires.copy(out.at[base + 2, high], out.at[base + 3, high], to["y"])
    from_core.append(wires.copy(at(2), at(6), to["core"]))
    via_z.wait_recv()
    via_y.wait_recv()
    from_core.append(wires.copy(at(3), at(7), to["core"]))
    return from_core


def remote_call(kernel, name, key, args, outs, scratch, copies, in_vmem):
    ins, out_in = in_vmem
    spec = lambda inside: pl.BlockSpec(memory_space=pltpu.VMEM if inside else pl.ANY)
    return pl.pallas_call(
        kernel,
        name=name,
        out_shape=outs,
        in_specs=[spec(x) for x in ins],
        out_specs=[spec(x) for x in out_in],
        scratch_shapes=list(scratch)
        + [
            pltpu.SemaphoreType.DMA((copies,)),
            pltpu.SemaphoreType.DMA((copies,)),
            pltpu.SemaphoreType.DMA((4,)),
        ],
        compiler_params=pltpu.CompilerParams(
            collective_id=key, has_side_effects=True, vmem_limit_bytes=VMEM_LIMIT
        ),
    )(*args)


def kv_gather_kernel(own_ref, out_ref, *sems):
    wires, to = Wires(*sems), partners()
    kind = lax.rem(lax.axis_index("tensor"), 2)
    rows = own_ref.shape[0]
    block = lambda j: out_ref.at[kind, pl.ds(j * rows, rows)]
    meet([to[k] for k in ("core", "z", "far", "last")])
    mine = wires.here(own_ref, block(0))
    arrive = [wires.copy(own_ref, block(j), to[k]) for j, k in ((3, "last"), (2, "far"), (1, "z"))]
    from_core = [wires.copy(own_ref, block(0), to["core"])]
    for j, one in ((1, arrive[2]), (2, arrive[1]), (3, arrive[0])):
        one.wait_recv()
        from_core.append(wires.copy(block(j), block(j), to["core"]))
    for one in from_core:
        one.wait_recv()
    mine.wait()
    wires.finish()


def kv_gather(own):
    rows, width = own.shape
    n_c = lax.axis_size("context")
    return remote_call(
        kv_gather_kernel,
        "kv_gather",
        0,
        [own],
        [jax.ShapeDtypeStruct((2, n_c * rows, width), bf16)],
        [],
        8,
        ([False], [False]),
    )[0]


def kv_scatter_kernel(part_ref, out_ref, own, got_core, sent, got, *sems):
    wires, to = Wires(*sems), partners()
    kind = lax.rem(lax.axis_index("tensor"), 2)
    rows = out_ref.shape[0]
    block = lambda j: pl.ds(j * rows, rows)
    meet([to[k] for k in ("core", "z", "far", "last")])
    steps = ((3, "last"), (2, "far"), (1, "z"), (0, None))
    from_core = {
        j: wires.copy(part_ref.at[1 - kind, block(j)], got_core.at[block(j)], to["core"])
        for j, _ in steps
    }
    mine = wires.here(part_ref.at[kind], own)
    mine.wait()
    arrive = []
    for j, k in steps[:3]:
        from_core[j].wait_recv()
        sent[block(j)] = (wide(own[block(j)]) + wide(got_core[block(j)])).astype(bf16)
        arrive.append(wires.copy(sent.at[block(j)], got.at[block(j)], to[k]))
    from_core[0].wait_recv()
    total = wide(own[block(0)]) + wide(got_core[block(0)])
    for one in arrive:
        one.wait_recv()
    for j in (1, 2, 3):
        total = total + wide(got[block(j)])
    out_ref[...] = total
    wires.finish()


def kv_scatter(part):
    _, rows, width = part.shape
    n_c = lax.axis_size("context")
    return remote_call(
        kv_scatter_kernel,
        "kv_scatter",
        1,
        [part],
        [jax.ShapeDtypeStruct((rows // n_c, width), f32)],
        [pltpu.VMEM((rows, width), bf16)] * 4,
        7,
        ([False], [True]),
    )[0]


def middle_kernel(part, x_ref, gain_ref, mid_ref, factor_ref, out, own, core, sent, got, xn, *sems):
    wires, to = Wires(*sems), partners()
    meet([to[k] for k in ("core", "y", "z", "far")])
    middle = wide(x_ref[...]) + scatter_rank(wires, to, part, own, core, sent, got)
    mid_ref[...] = middle
    factor = lax.rsqrt(jnp.mean(middle * middle, axis=-1, keepdims=True) + EPSILON)
    factor_ref[...] = factor
    xn[...] = (middle * factor * gain_ref[...]).astype(bf16)
    blocks = out.shape[0] // 2
    mine = wires.here(xn, out.at[0])
    from_far = wires.copy(xn, out.at[blocks], to["far"])
    last = gather_pair(wires, to, xn, out, 0)
    from_far.wait_recv()
    last += gather_pair(wires, to, out.at[blocks], out, blocks)
    for one in last:
        one.wait_recv()
    mine.wait()
    wires.finish()


def middle_norm(part, inputs_part, gain):
    rows, width = inputs_part.shape
    return remote_call(
        middle_kernel,
        "middle_norm",
        2,
        [part.reshape(4, rows, width), inputs_part, gain],
        [
            jax.ShapeDtypeStruct((rows, width), f32),
            jax.ShapeDtypeStruct((rows, 1), f32),
            jax.ShapeDtypeStruct((16, rows, width), bf16),
        ],
        [
            pltpu.VMEM((2, rows, width), bf16),
            pltpu.VMEM((2, rows, width), bf16),
            pltpu.VMEM((rows, width), bf16),
            pltpu.VMEM((rows, width), bf16),
            pltpu.VMEM((rows, width), bf16),
        ],
        32,
        ([False, True, True], [True, True, False]),
    )


def norm_back_rows(values, factor, gain, grad_normed):
    gained = gain * grad_normed
    inner = jnp.mean(gained * values, axis=-1, keepdims=True)
    grad_values = factor * gained - values * (factor * factor * factor) * inner
    return grad_values, jnp.sum(grad_normed * values * factor, axis=0, keepdims=True)


MIXED = (0, 2, 1, 3)


def natural_place(t):
    flip = lambda x, bit: x + bit * (1 - 2 * lax.rem(x // bit, 2))
    return lambda j, _: t if j == 0 else flip(t, j)


def middle_back_kernel(
    part, out_part, mid_ref, factor_ref, gain_ref, dy_ref, dmid_ref, dgain_ref, out, outputs, *rest
):
    low, out_low, first, second, wires = rest[0], rest[1], rest[2:9], rest[9:16], Wires(*rest[16:])
    to = partners()
    meet([to[k] for k in ("core", "y", "z")])
    back = scatter_pair(wires, to, part, *first)
    ahead = scatter_pair(wires, to, out_part, *second)
    next(back)
    next(ahead)
    next(back)
    next(back)
    next(ahead)
    grad_normed = result_of(back)
    du, dgain = norm_back_rows(mid_ref[...], factor_ref[...], gain_ref[...], grad_normed)
    dgain_ref[...] = dgain
    dmid = wide(dy_ref[...]) + du
    dmid_ref[...] = dmid
    low[...] = dmid.astype(bf16)
    share = gather_rank(wires, to, low, out, lambda j, flip: MIXED.index(j ^ flip))
    next(share)
    next(ahead)
    out_low[...] = (mid_ref[...] + result_of(ahead)).astype(bf16)
    place = natural_place(lax.axis_index("tensor"))
    out_share = gather_rank(wires, to, out_low, outputs, place)
    next(out_share)
    result_of(share)
    result_of(out_share)
    wires.finish()


def pair_scratch(rows, width):
    return [
        pltpu.VMEM((4, rows, width), bf16),
        pltpu.VMEM((4, rows, width), bf16),
        pltpu.VMEM((3, rows, width), bf16),
        pltpu.VMEM((rows, width), bf16),
        pltpu.VMEM((rows, width), bf16),
        pltpu.VMEM((rows // 2, width), bf16),
        pltpu.VMEM((rows // 2, width), bf16),
    ]


def middle_back(part, out_part, middle, factor, gain, dy_part):
    rows, width = middle.shape
    return remote_call(
        middle_back_kernel,
        "middle_back",
        3,
        [part.reshape(8, rows, width), out_part.reshape(8, rows, width)]
        + [middle, factor, gain, dy_part],
        [
            jax.ShapeDtypeStruct((rows, width), f32),
            jax.ShapeDtypeStruct((1, width), f32),
            jax.ShapeDtypeStruct((4, rows, width), bf16),
            jax.ShapeDtypeStruct((4, rows, width), bf16),
        ],
        [pltpu.VMEM((rows, width), bf16)] * 2 + pair_scratch(rows, width) * 2,
        32,
        ([False, False, True, True, True, True], [True, True, False, False]),
    )


def add_all(wires, ways, value, slots):
    for k, device in enumerate(ways):
        one = wires.copy(value, slots.at[k], device)
        one.wait()
        wires.started = [x for x in wires.started if x is not one]
        value[...] = value[...] + slots[k]


def input_back_kernel(
    part, x_ref, factor_ref, gain_ref, dmid_ref, small_ref, sum_ref, out, *rest
):
    low, own, core, sent, got, slots = rest[:-3]
    wires, to = Wires(*rest[-3:]), partners()
    meet([to[k] for k in ("core", "y")])
    grad_normed = scatter_rank(wires, to, part, own, core, sent, got)
    du, dgain = norm_back_rows(wide(x_ref[...]), factor_ref[...], gain_ref[...], grad_normed)
    low[...] = (dmid_ref[...] + du).astype(bf16)
    share = gather_rank(wires, to, low, out, natural_place(lax.axis_index("tensor")))
    next(share)
    width = dgain.shape[1]
    sum_ref[:, width:] = small_ref[:, width:]
    sum_ref[:, :width] = dgain
    add_all(wires, [to["core"], to["y"]], sum_ref, slots)
    result_of(share)
    wires.finish()


def input_back(part, inputs_part, factor, gain, grad_middle, small):
    rows, width = inputs_part.shape
    return remote_call(
        input_back_kernel,
        "input_back",
        5,
        [part.reshape(4, rows, width), inputs_part, factor, gain, grad_middle, small],
        [
            jax.ShapeDtypeStruct(small.shape, f32),
            jax.ShapeDtypeStruct((4, rows, width), bf16),
        ],
        [
            pltpu.VMEM((rows, width), bf16),
            pltpu.VMEM((2, rows, width), bf16),
            pltpu.VMEM((2, rows, width), bf16),
            pltpu.VMEM((rows, width), bf16),
            pltpu.VMEM((rows, width), bf16),
            pltpu.VMEM((2,) + small.shape, f32),
        ],
        16,
        ([False, True, True, True, True, True], [True, False]),
    )


def context_sum_kernel(over_f, *refs):
    (parts, refs), (small_ref, refs) = (refs[:3], refs[3:]), (refs[3], refs[4:])
    (outs, refs), (sum_ref, shared, refs) = (refs[:3], refs[3:]), (refs[3], refs[4], refs[5:])
    gots, slots, wires = refs[:3], refs[3], Wires(*refs[4:])
    to, c = partners(), lax.axis_index("context")
    ways = ((1, "z"), (2, "far"), (3, "last"))
    greet = ["core", "y", "z", "far", "last"]
    flip = lambda x, bit: x + bit * (1 - 2 * lax.rem(x // bit, 2))
    if over_f:
        to["f"] = {"fsdp": 1 - lax.axis_index("fsdp")}
        greet.append("f")
    meet([to[k] for k in greet])
    rank = {1: flip(c, 1), 2: flip(c, 2), 3: flip(flip(c, 1), 2)}
    arrive = []
    order = (2, 0, 1)
    quarter = lambda ref, k: pl.ds(
        pl.multiple_of(k * (ref.shape[0] // 4), ref.shape[0] // 4), ref.shape[0] // 4
    )
    for i in order:
        part, got = parts[i], gots[i]
        arrive.append(
            [
                wires.copy(part.at[quarter(part, rank[j])], got.at[j - 1], to[way])
                for j, way in ways
            ]
        )
    sum_ref[...] = small_ref[...]
    sent = []
    for i, copies in zip(order, arrive):
        part, got, out = parts[i], gots[i], outs[i]
        for one in copies:
            one.wait_recv()
        at = quarter(part, c)
        out[at] = (
            wide(part[at]) + wide(got[0]) + wide(got[1]) + wide(got[2])
        ).astype(bf16)
        sent.append([wires.copy(out.at[at], out.at[at], to[way]) for _, way in ways])
    add_all(wires, [to[k] for k in (("f",) if over_f else ()) + ("z", "far")], sum_ref, slots)
    for one in sent[0]:
        one.wait_recv()
    share = gather_rank(wires, to, outs[2], shared, natural_place(lax.axis_index("tensor")))
    next(share)
    for one in sent[1] + sent[2]:
        one.wait_recv()
    result_of(share)
    wires.finish()


def context_sum(over_f, parts, small):
    shape = lambda x: jax.ShapeDtypeStruct(x.shape, x.dtype)
    return remote_call(
        functools.partial(context_sum_kernel, over_f),
        "context_sum",
        6,
        [*parts, small],
        [shape(x) for x in parts]
        + [shape(small), jax.ShapeDtypeStruct((4,) + parts[2].shape, bf16)],
        [pltpu.VMEM((3, x.shape[0] // 4, x.shape[1]), bf16) for x in parts]
        + [pltpu.VMEM((3,) + small.shape, f32)],
        32,
        ([True] * 4, [True] * 4 + [False]),
    )


def build(n_f, n_c, n_t):
    def flip(x, axis, bit):
        size = {"fsdp": n_f, "context": n_c, "tensor": n_t}[axis]
        return lax.ppermute(x, axis, [(i, i ^ bit) for i in range(size)])

    def by_bit(bit, x, other, axis):
        return jnp.where(
            bit == 0,
            jnp.concatenate([x, other], axis=axis),
            jnp.concatenate([other, x], axis=axis),
        )

    def after(x, *others):
        return lax.optimization_barrier((x, others))[0]

    def local(
        inputs,
        cotangent,
        blocks,
        attn_gain,
        w_query,
        b_query,
        w_key,
        b_key,
        w_value,
        b_value,
        w_out,
        ffn_gain,
        w_gate,
        w_up,
        w_down,
    ):
        rows, width = inputs.shape
        f = lax.axis_index("fsdp")
        c = lax.axis_index("context")
        t = lax.axis_index("tensor")
        core, parity, pair = t % 2, c % 2, c // 2
        heads = w_query.shape[1] // HD
        group = (t * heads) // (H // KV)
        part = rows // n_t
        units_all = w_gate.shape[1]
        units = units_all // 2

        def gather_f(x, axis):
            if n_f == 2:
                return by_bit(f, x, flip(x, "fsdp", 1), axis)
            return lax.all_gather(x, "fsdp", axis=axis, tiled=True)

        def columns_f(parts):
            parts = [x.astype(bf16) for x in parts]
            return by_bit(f, parts[0], parts[1], 1) if n_f == 2 else parts[0]

        def grad_f(left, right, side):
            if n_f == 2:
                half = width // 2
                source = (left, right)[side]
                own = lax.dynamic_slice_in_dim(source, f * half, half, 1)
                far = lax.dynamic_slice_in_dim(source, (1 - f) * half, half, 1)
                pick = lambda x: dot_rows(x, right) if side == 0 else dot_rows(left, x)
                got = flip(pick(far).astype(bf16), "fsdp", 1)
                return pick(own) + got.astype(f32)
            return lax.psum_scatter(
                dot_rows(left, right).astype(bf16), "fsdp", scatter_dimension=side, tiled=True
            ).astype(f32)

        order = MIXED

        def mixed(x):
            return jnp.concatenate(
                [lax.dynamic_slice_in_dim(x, (t ^ j) * part, part, 0) for j in order], axis=0
            )

        def natural(x):
            blocks_of = [x[i * part : (i + 1) * part] for i in range(n_t)]
            place = [blocks_of[order.index(j)] for j in range(n_t)]
            out = jnp.stack(place)
            return jnp.concatenate(
                [lax.dynamic_index_in_dim(out, n ^ t, 0, keepdims=False) for n in range(n_t)],
                axis=0,
            )

        def grow(x, axis, bit):
            return jnp.concatenate([x, flip(x, axis, bit)], axis=0)

        small = jnp.concatenate(
            [v.reshape(1, -1) for v in (attn_gain, ffn_gain, b_query, b_key, b_value)], axis=1
        )
        column = lambda w: lax.dynamic_slice_in_dim(w, group * HD, HD, 1)
        w_kv_own = jnp.where(core == 0, column(w_key), column(w_value))
        pieces_f = lambda x, axis: (
            [x, flip(x, "fsdp", 1)]
            if n_f == 2
            else [lax.all_gather(x, "fsdp", axis=axis, tiled=True)]
        )
        meta = jnp.stack([f, 1 - f, core, pair]).astype(jnp.int32)
        w_qkv = pieces_f(jnp.concatenate([w_query, w_kv_own], axis=1), 0)
        small = gather_f(small, 0)
        w_out_all = gather_f(w_out, 1)
        piece = attn_gain.shape[0]
        gain_first = small[:, :piece].reshape(1, width).astype(f32)
        gain_second = small[:, piece : 2 * piece].reshape(1, width).astype(f32)
        bias_of = lambda lo, n: (
            small[:, lo : lo + n * (HD // n_f)]
            .reshape(n_f, n, HD // n_f)
            .transpose(1, 0, 2)
            .reshape(n, HD)
            .astype(f32)
        )
        at = 2 * piece
        bq = bias_of(at, heads)
        bk = bias_of(at + heads * (HD // n_f), KV)
        bv = bias_of(at + (heads + KV) * (HD // n_f), KV)
        b_kv = lax.dynamic_index_in_dim(jnp.where(core == 0, bk, bv), group, 0)

        unit_slice = lambda w: lax.dynamic_slice_in_dim(w, parity * units, units, 0)
        own_units = jnp.concatenate([unit_slice(w) for w in (w_gate.T, w_up.T, w_down)], axis=0)
        w_units = pieces_f(after(own_units, w_qkv, small), 1)

        dy_own = mixed(cotangent)[: 2 * part]
        dy_near = jnp.concatenate([dy_own, flip(dy_own, "context", 1)], axis=0)
        dy_pair = grow(dy_near, "tensor", 1)
        dy_far = grow(grow(flip(dy_own, "context", 2), "context", 1), "tensor", 1)
        dy_all = jnp.concatenate([dy_pair, dy_far], axis=0).reshape(2, -1, part, width)

        seq_blocks = blocks[0].reshape(n_c, -1)
        own_blocks = seq_blocks.shape[1]
        key_blocks = jnp.concatenate(
            [lax.dynamic_index_in_dim(seq_blocks, c ^ j, 0, keepdims=False) for j in range(n_c)]
        )
        positions = (
            key_blocks[:own_blocks, None] * BLOCK + jnp.arange(BLOCK, dtype=jnp.int32)[None, :]
        ).reshape(-1)
        cosine, sine = rope_tables(positions)
        bias = jnp.concatenate([bq.reshape(1, -1), b_kv], axis=1)
        normed, factor_first, queries, kv_own = qkv(
            meta, inputs, gain_first, bias, cosine, sine, w_qkv
        )
        kv = kv_gather(kv_own)
        attended, lse = attention(key_blocks, queries, kv)
        attended_mixed = mixed(attended)
        inputs_part = lax.dynamic_slice_in_dim(inputs, t * part, part, 0)
        middle, factor_second, normed2 = middle_norm(
            dot(attended_mixed, w_out_all).astype(bf16), inputs_part, gain_second
        )

        normed2 = normed2.reshape(2, -1, part, width)
        hid_pair, dg_pair, du_pair, dx_part, out_part = ffn(meta, normed2, dy_all, w_units, True)
        hid_far, dg_far, du_far = ffn(meta, after(normed2, dx_part), dy_all, w_units, False)
        grad_args = (normed2, dy_all, (hid_pair, hid_far), (dg_pair, dg_far), (du_pair, du_far))
        if n_f == 2:
            unit_sent = unit_grads(meta, 1, 2, *grad_args)
            unit_got = [flip(x, "fsdp", 1) for x in unit_sent]
            unit_own = unit_grads(meta, 0, 2, *after(grad_args, unit_sent))
            dx_part = after(dx_part, unit_own)
        else:
            unit_own = [
                lax.psum_scatter(x, "fsdp", scatter_dimension=1, tiled=True)
                for x in unit_grads(meta, 0, 1, *grad_args)
            ]
            unit_got = [jnp.zeros_like(x) for x in unit_own]

        unit_sum = lambda own, got: (own.astype(f32) + got.astype(f32)).astype(bf16)
        unit_whole = lambda low, other: by_bit(parity, low, other, 0).astype(f32)

        dy_part = lax.dynamic_slice_in_dim(cotangent, t * part, part, 0)
        grad_middle, ffn_gain_grad, grad_middle_low, outputs = middle_back(
            dx_part, out_part, middle, factor_second, gain_second, dy_part
        )
        outputs = outputs.reshape(rows, width)
        grad_middle_low = grad_middle_low.reshape(rows, width)
        unit_low = [unit_sum(unit_own[0], after(unit_got[0], grad_middle_low))]
        unit_other = [flip(unit_low[0], "context", 1)]
        grad_attended = natural(
            dot_cols(after(grad_middle_low, unit_low), w_out_all).astype(bf16)
        )

        dq_low, dkv = attention_back(key_blocks, queries, grad_attended, lse, cosine, sine, kv)
        dkv = kv_scatter(dkv)
        unit_low.append(unit_sum(unit_own[1], after(unit_got[1], dkv)))
        unit_other.append(flip(unit_low[1], "context", 1))
        wo_part = grad_f(attended_mixed, after(grad_middle_low, dkv), 1).astype(bf16)
        dkv_low = jnp.where(core == 0, rotate_back(dkv, cosine, sine), dkv).astype(bf16)
        wq_part = grad_f(normed, dq_low, 0).astype(bf16)
        wkv_part = grad_f(normed, dkv_low, 0).astype(bf16)
        d_qkv = mixed(jnp.concatenate([dq_low, dkv_low], axis=1))
        factor_part = lax.dynamic_slice_in_dim(factor_first, t * part, part, 0)
        own_biases = jnp.sum(
            jnp.concatenate([dq_low, dkv_low], axis=1).astype(f32), axis=0, keepdims=True
        )
        slots = lax.dynamic_update_slice(
            jnp.zeros((n_t, (heads + 1) * HD), f32), own_biases, (t, 0)
        )
        small_grads = jnp.concatenate(
            [jnp.zeros((1, width), f32), ffn_gain_grad, slots.reshape(1, -1)], axis=1
        )
        small_grads, input_grad = input_back(
            columns_f([dot_cols(d_qkv, w) for w in w_qkv]),
            inputs_part,
            factor_part,
            gain_first,
            grad_middle,
            small_grads,
        )
        input_grad = input_grad.reshape(rows, width)
        if n_f > 2:
            small_grads = lax.psum(small_grads, "fsdp")
        wo_grad, wq_grad, _, packed, wkv_all = context_sum(
            n_f == 2, (wo_part, wq_part, wkv_part), small_grads
        )
        wo_grad, wq_grad, wkv_all = (x.astype(f32) for x in (wo_grad, wq_grad, wkv_all))
        wk_grad = jnp.concatenate([wkv_all[0], wkv_all[2]], axis=1)
        wv_grad = jnp.concatenate([wkv_all[1], wkv_all[3]], axis=1)
        packed = packed[0]
        attn_gain_grad = lax.dynamic_slice_in_dim(packed, f * piece, piece, 0)
        ffn_gain_grad = lax.dynamic_slice_in_dim(packed, width + f * piece, piece, 0)
        slots = packed[2 * width :].reshape(n_t, heads + 1, HD)
        slots = lax.dynamic_slice_in_dim(slots, f * (HD // n_f), HD // n_f, 2)
        bq_out = lax.dynamic_index_in_dim(slots, t, 0, keepdims=False)[:heads]
        bk_out = slots[0::2, heads]
        bv_out = slots[1::2, heads]

        shares = [
            (low[k : k + units], other[k : k + units])
            for low, other in zip(unit_low, unit_other)
            for k in range(0, low.shape[0], units)
        ]
        wg_grad, wu_grad, wd_grad = (unit_whole(*share) for share in shares)
        wg_grad, wu_grad = wg_grad.T, wu_grad.T

        return (
            outputs,
            input_grad,
            attn_gain_grad,
            wq_grad,
            bq_out,
            wk_grad,
            bk_out,
            wv_grad,
            bv_out,
            wo_grad,
            ffn_gain_grad,
            wg_grad,
            wu_grad,
            wd_grad,
        )

    return local


def solution(mesh):
    in_specs = (
        P(("fsdp", "context"), None),
        P(("fsdp", "context"), None),
        P("fsdp", None),
        P("fsdp"),
        P("fsdp", "tensor"),
        P("tensor", "fsdp"),
        P("fsdp", None),
        P(None, "fsdp"),
        P("fsdp", None),
        P(None, "fsdp"),
        P("tensor", "fsdp"),
        P("fsdp"),
        P("fsdp", "tensor"),
        P("fsdp", "tensor"),
        P("tensor", "fsdp"),
    )
    out_specs = (
        P(("fsdp", "context"), None),
        P(("fsdp", "context"), None),
        P("fsdp"),
        P("fsdp", "tensor"),
        P("tensor", "fsdp"),
        P("fsdp", None),
        P(None, "fsdp"),
        P("fsdp", None),
        P(None, "fsdp"),
        P("tensor", "fsdp"),
        P("fsdp"),
        P("fsdp", "tensor"),
        P("fsdp", "tensor"),
        P("tensor", "fsdp"),
    )
    local = build(mesh.shape["fsdp"], mesh.shape["context"], mesh.shape["tensor"])
    return jax.shard_map(local, mesh=mesh, in_specs=in_specs, out_specs=out_specs, check_vma=False)
```

```python
import functools

import jax
import jax.numpy as jnp
from jax import lax
from jax.experimental import pallas as pl
from jax.experimental.pallas import tpu as pltpu
from jax.sharding import PartitionSpec as P

H = 12
KV = 2
HD = 128
BLOCK = 256

EPSILON = 1e-06
ROPE_BASE = 1000000.0
MASKED = -1e30
SCALING = HD ** (-0.5)
LANES = 128
VMEM_LIMIT = 60 << 20

f32 = jnp.float32
bf16 = jnp.bfloat16


def rope_tables(positions):
    halfway = HD // 2
    frequency = ROPE_BASE ** (-(jnp.arange(halfway, dtype=f32) * 2.0 / HD))
    angles = positions.astype(f32)[:, None] * frequency[None, :]
    cosine, sine = jnp.cos(angles), jnp.sin(angles)
    return (jnp.concatenate([cosine, cosine], axis=1), jnp.concatenate([sine, sine], axis=1))


def rotate(field, cosine, sine):
    halfway = HD // 2
    turned = jnp.concatenate([-field[..., halfway:], field[..., :halfway]], axis=-1)
    return field * cosine + turned * sine


def rotate_back(grad_field, cosine, sine):
    halfway = HD // 2
    moved = grad_field * sine
    turned = jnp.concatenate([moved[..., halfway:], -moved[..., :halfway]], axis=-1)
    return grad_field * cosine + turned


def dot(left, right):
    return jnp.dot(left, right, preferred_element_type=f32)


def dot_rows(left, right):
    return lax.dot_general(left, right, (((0,), (0,)), ((), ())), preferred_element_type=f32)


def dot_cols(left, right):
    return lax.dot_general(left, right, (((1,), (1,)), ((), ())), preferred_element_type=f32)


def mask_row(kb_ref, own_block, key_blocks):
    return jnp.concatenate(
        [
            jnp.full((1, BLOCK), jnp.where(kb_ref[j] <= own_block, 0.0, MASKED), f32)
            for j in range(key_blocks)
        ],
        axis=1,
    )


def attention_kernel(key_blocks, kb_ref, q_ref, k_ref, v_ref, o_ref, lse_ref):
    bias = mask_row(kb_ref, kb_ref[pl.program_id(1)], key_blocks)
    scores = dot_cols(q_ref[...], k_ref[...]) * SCALING + bias
    row_max = jnp.max(scores, axis=1, keepdims=True)
    expo = jnp.exp(scores - row_max)
    total = jnp.sum(expo, axis=1, keepdims=True)
    probability = (expo * (1.0 / total)).astype(bf16)
    o_ref[...] = dot(probability, v_ref[...]).astype(bf16)
    lse_ref[0] = row_max + jnp.log(total)


def attention(key_blocks, queries, kv):
    rows, width = queries.shape
    heads = width // HD
    whole = lambda kind: pl.BlockSpec((None,) + kv.shape[1:], lambda h, i, kb: (kind, 0, 0))
    tile = pl.BlockSpec((BLOCK, HD), lambda h, i, kb: (i, h))
    return pl.pallas_call(
        functools.partial(attention_kernel, kv.shape[1] // BLOCK),
        name="attention",
        grid_spec=pltpu.PrefetchScalarGridSpec(
            num_scalar_prefetch=1,
            grid=(heads, rows // BLOCK),
            in_specs=[tile, whole(0), whole(1)],
            out_specs=[tile, pl.BlockSpec((1, BLOCK, 1), lambda h, i, kb: (h, i, 0))],
        ),
        out_shape=[
            jax.ShapeDtypeStruct((rows, width), bf16),
            jax.ShapeDtypeStruct((heads, rows, 1), f32),
        ],
        compiler_params=pltpu.CompilerParams(vmem_limit_bytes=VMEM_LIMIT),
    )(key_blocks, queries, kv, kv)


def attention_back_kernel(
    key_blocks,
    kb_ref,
    q_ref,
    do_ref,
    lse_ref,
    cos_ref,
    sin_ref,
    k_ref,
    v_ref,
    dq_ref,
    dkv_ref,
    dk_ref,
    dv_ref,
):
    head, i = pl.program_id(0), pl.program_id(1)

    @pl.when((head == 0) & (i == 0))
    def _():
        dk_ref[...] = jnp.zeros_like(dk_ref)
        dv_ref[...] = jnp.zeros_like(dv_ref)

    bias = mask_row(kb_ref, kb_ref[i], key_blocks)
    scores = dot_cols(q_ref[...], k_ref[...]) * SCALING + bias
    probability = jnp.exp(scores - lse_ref[0])
    grad_probs = dot_cols(do_ref[...], v_ref[...])
    inner = jnp.sum(probability * grad_probs, axis=1, keepdims=True)
    grad_scores = (probability * (grad_probs - inner)).astype(bf16)
    grad_query = dot(grad_scores, k_ref[...]) * SCALING
    moved = grad_query * sin_ref[...]
    sign = jnp.where(lax.broadcasted_iota(jnp.int32, moved.shape, 1) < HD // 2, 1.0, -1.0)
    dq_ref[...] = (
        grad_query * cos_ref[...] + pltpu.roll(moved, HD // 2, 1) * sign
    ).astype(bf16)
    dk_ref[...] += dot_rows(grad_scores, q_ref[...]) * SCALING
    dv_ref[...] += dot_rows(probability.astype(bf16), do_ref[...])

    @pl.when((head == pl.num_programs(0) - 1) & (i == pl.num_programs(1) - 1))
    def _():
        dkv_ref[0] = dk_ref[...].astype(bf16)
        dkv_ref[1] = dv_ref[...].astype(bf16)


def attention_back(key_blocks, queries, grad_out, lse, cosine, sine, kv):
    rows, width = queries.shape
    heads = width // HD
    whole = lambda kind: pl.BlockSpec((None,) + kv.shape[1:], lambda h, i, kb: (kind, 0, 0))
    tile = pl.BlockSpec((BLOCK, HD), lambda h, i, kb: (i, h))
    table = pl.BlockSpec((BLOCK, HD), lambda h, i, kb: (i, 0))
    return pl.pallas_call(
        functools.partial(attention_back_kernel, kv.shape[1] // BLOCK),
        name="attention_back",
        grid_spec=pltpu.PrefetchScalarGridSpec(
            num_scalar_prefetch=1,
            grid=(heads, rows // BLOCK),
            in_specs=[
                tile,
                tile,
                pl.BlockSpec((1, BLOCK, 1), lambda h, i, kb: (h, i, 0)),
                table,
                table,
                whole(0),
                whole(1),
            ],
            out_specs=[tile, pl.BlockSpec(kv.shape, lambda h, i, kb: (0, 0, 0))],
            scratch_shapes=[pltpu.VMEM(kv.shape[1:], f32)] * 2,
        ),
        out_shape=[
            jax.ShapeDtypeStruct((rows, width), bf16),
            jax.ShapeDtypeStruct(kv.shape, bf16),
        ],
        compiler_params=pltpu.CompilerParams(vmem_limit_bytes=VMEM_LIMIT),
    )(key_blocks, queries, grad_out, lse, cosine, sine, kv, kv)


def qkv_kernel(pieces, meta_ref, x_ref, gain_ref, bias_ref, cos_ref, sin_ref, *refs):
    weights, (xn_ref, factor_ref, q_ref, kv_ref) = refs[: 2 * pieces], refs[2 * pieces :]
    values = x_ref[...].astype(f32)
    factor = lax.rsqrt(jnp.mean(values * values, axis=-1, keepdims=True) + EPSILON)
    factor_ref[...] = factor
    xn_ref[...] = (values * factor * gain_ref[...]).astype(bf16)
    depth = weights[0].shape[0]
    normed = [xn_ref[:, columns_of(meta_ref, j, depth, pieces)] for j in range(pieces)]
    cosine, sine = cos_ref[...], sin_ref[...]
    sign = jnp.where(lax.broadcasted_iota(jnp.int32, cosine.shape, 1) < HD // 2, -1.0, 1.0)
    sine = sine * sign
    width = q_ref.shape[1]
    total = bias_ref[:, :width] + sum(dot(x, w[...]) for x, w in zip(normed, weights[:pieces]))
    turn = lambda own: own * cosine + pltpu.roll(own, HD // 2, 1) * sine
    for h in range(width // HD):
        q_ref[:, h * HD : (h + 1) * HD] = turn(total[:, h * HD : (h + 1) * HD]).astype(bf16)
    own = bias_ref[:, width:] + sum(dot(x, w[...]) for x, w in zip(normed, weights[pieces:]))
    kv_ref[...] = jnp.where(meta_ref[2] == 0, turn(own), own).astype(bf16)


def columns_of(meta_ref, j, depth, pieces):
    if pieces == 1:
        return slice(None)
    return pl.ds(pl.multiple_of(meta_ref[j] * depth, LANES), depth)


def qkv(meta, inputs, gain, bias, cosine, sine, w_q, w_kv):
    rows, width = inputs.shape
    out = w_q[0].shape[1]
    tile = 256
    row = lambda n: pl.BlockSpec((tile, n), lambda i, m: (i, 0))
    fixed = lambda w: pl.BlockSpec(w.shape, lambda i, m: (0, 0))
    return pl.pallas_call(
        functools.partial(qkv_kernel, len(w_q)),
        name="qkv",
        grid_spec=pltpu.PrefetchScalarGridSpec(
            num_scalar_prefetch=1,
            grid=(rows // tile,),
            in_specs=[row(width), fixed(gain), fixed(bias), row(HD), row(HD)]
            + [fixed(w) for w in (*w_q, *w_kv)],
            out_specs=[row(width), row(1), row(out), row(HD)],
        ),
        out_shape=[
            jax.ShapeDtypeStruct((rows, width), bf16),
            jax.ShapeDtypeStruct((rows, 1), f32),
            jax.ShapeDtypeStruct((rows, out), bf16),
            jax.ShapeDtypeStruct((rows, HD), bf16),
        ],
        compiler_params=pltpu.CompilerParams(vmem_limit_bytes=VMEM_LIMIT),
    )(meta, inputs, gain, bias, cosine, sine, *w_q, *w_kv)


def qkv_back_kernel(pieces, meta_ref, dq_ref, dkv_ref, *refs):
    w_q, w_kv, out_ref = refs[:pieces], refs[pieces : 2 * pieces], refs[-1]
    for j in range(pieces):
        out_ref[:, columns_of(meta_ref, j, w_q[j].shape[0], pieces)] = (
            dot_cols(dq_ref[...], w_q[j][...]) + dot_cols(dkv_ref[...], w_kv[j][...])
        ).astype(bf16)


def qkv_back(meta, grad_q, grad_kv, w_q, w_kv):
    rows, width = grad_q.shape[0], sum(w.shape[0] for w in w_q)
    tile = 256
    row = lambda n: pl.BlockSpec((tile, n), lambda i, m: (i, 0))
    fixed = lambda w: pl.BlockSpec(w.shape, lambda i, m: (0, 0))
    return pl.pallas_call(
        functools.partial(qkv_back_kernel, len(w_q)),
        name="qkv_back",
        grid_spec=pltpu.PrefetchScalarGridSpec(
            num_scalar_prefetch=1,
            grid=(rows // tile,),
            in_specs=[row(grad_q.shape[1]), row(HD)] + [fixed(w) for w in (*w_q, *w_kv)],
            out_specs=row(width),
        ),
        out_shape=jax.ShapeDtypeStruct((rows, width), bf16),
        compiler_params=pltpu.CompilerParams(vmem_limit_bytes=VMEM_LIMIT),
    )(meta, grad_q, grad_kv, *w_q, *w_kv)


def ffn_kernel(pieces, meta_ref, x_ref, dy_ref, *refs):
    wg, wu, wd = (refs[m * pieces : (m + 1) * pieces] for m in range(3))
    hid_ref, dg_ref, du_ref, dx_ref, out_ref = refs[-5:]
    columns = [columns_of(meta_ref, j, wg[j].shape[1], pieces) for j in range(pieces)]
    gate = sum(dot_cols(x_ref[:, at], w[...]) for at, w in zip(columns, wg))
    up = sum(dot_cols(x_ref[:, at], w[...]) for at, w in zip(columns, wu))
    grad_hidden = sum(dot_cols(dy_ref[:, at], w[...]) for at, w in zip(columns, wd))
    sigma = 1.0 / (1.0 + jnp.exp(-gate))
    gated = gate * sigma
    hid_ref[...] = (gated * up).astype(bf16)
    dg_ref[...] = (grad_hidden * up * (sigma + gated * (1.0 - sigma))).astype(bf16)
    du_ref[...] = (grad_hidden * gated).astype(bf16)

    @pl.when(pl.program_id(0) < pl.num_programs(0) // 2)
    def _():
        for at, g, u, d in zip(columns, wg, wu, wd):
            dx_ref[:, at] = (dot(dg_ref[...], g[...]) + dot(du_ref[...], u[...])).astype(bf16)
            out_ref[:, at] = dot(hid_ref[...], d[...]).astype(bf16)


def ffn(meta, normed, grad_out, weights):
    width = normed.shape[-1]
    rows = normed.shape[0] * normed.shape[1]
    units = weights[0].shape[0] // 3
    tile = 512
    steps = rows // tile
    flat = lambda x: x.reshape(-1, width)
    read = pl.BlockSpec((tile, width), lambda i, m: (i, 0))
    weight = lambda w, k: pl.BlockSpec(
        (units, w.shape[1]), lambda i, m: (k, 0), pipeline_mode=pl.Buffered(1)
    )
    placed = pl.BlockSpec(
        (tile, units), lambda i, m: (lax.rem(i + m[3] * (steps // 2), steps), 0)
    )
    near = pl.BlockSpec((tile, width), lambda i, m: (jnp.minimum(i, steps // 2 - 1), 0))
    return pl.pallas_call(
        functools.partial(ffn_kernel, len(weights)),
        name="ffn",
        grid_spec=pltpu.PrefetchScalarGridSpec(
            num_scalar_prefetch=1,
            grid=(steps,),
            in_specs=[read, read] + [weight(w, k) for k in range(3) for w in weights],
            out_specs=[placed] * 3 + [near] * 2,
        ),
        out_shape=[jax.ShapeDtypeStruct((rows, units), bf16)] * 3
        + [jax.ShapeDtypeStruct((rows // 2, width), bf16)] * 2,
        compiler_params=pltpu.CompilerParams(vmem_limit_bytes=VMEM_LIMIT),
    )(meta, flat(normed), flat(grad_out), *(list(weights) * 3))


def unit_grads_kernel(count, meta_ref, near_ref, far_ref, *refs):
    units, out_ref, x_ref = refs[:count], refs[-2], refs[-1]
    half = near_ref.shape[0]
    x_ref[pl.ds(pl.multiple_of(meta_ref[3] * half, half), half)] = near_ref[...]
    x_ref[pl.ds(pl.multiple_of((1 - meta_ref[3]) * half, half), half)] = far_ref[...]
    for k, unit in enumerate(units):
        depth = unit.shape[1]
        out_ref[k * depth : (k + 1) * depth] = dot_rows(unit[...], x_ref[...]).astype(bf16)


def unit_grads(meta, which, pieces, x, units_of):
    width = x.shape[-1]
    count, (rows, units) = len(units_of), units_of[0].shape
    depth = width // pieces
    tile = 256
    steps = depth // tile
    shard = (lambda m: m[which]) if pieces > 1 else (lambda m: 0)
    feature = lambda half: pl.BlockSpec(
        (rows // 2, tile), lambda i, m: (half, shard(m) * steps + i)
    )
    unit = pl.BlockSpec((rows, units), lambda i, m: (0, 0), pipeline_mode=pl.Buffered(1))
    x = x.reshape(-1, width)
    return pl.pallas_call(
        functools.partial(unit_grads_kernel, count),
        name=f"unit_grads_{which}_{count}",
        grid_spec=pltpu.PrefetchScalarGridSpec(
            num_scalar_prefetch=1,
            grid=(steps,),
            in_specs=[feature(0), feature(1)] + [unit] * count,
            out_specs=pl.BlockSpec((count * units, tile), lambda i, m: (0, i)),
            scratch_shapes=[pltpu.VMEM((rows, tile), bf16)],
        ),
        out_shape=jax.ShapeDtypeStruct((count * units, depth), bf16),
        compiler_params=pltpu.CompilerParams(vmem_limit_bytes=VMEM_LIMIT),
    )(meta, x, x, *units_of)


class Wires:
    def __init__(self, sends, receives, locals_):
        self.sends, self.receives, self.locals = sends, receives, locals_
        self.used = self.used_local = 0
        self.started = []

    def plan(self, source, target, device):
        k = self.used
        self.used += 1
        return pltpu.make_async_remote_copy(
            source,
            target,
            self.sends.at[k],
            self.receives.at[k],
            device_id=device,
            device_id_type=pl.DeviceIdType.MESH,
        )

    def copy(self, source, target, device):
        one = self.plan(source, target, device)
        one.start()
        self.started.append(one)
        return one

    def here(self, source, target):
        k = self.used_local
        self.used_local += 1
        one = pltpu.make_async_copy(source, target, self.locals.at[k])
        one.start()
        return one

    def finish(self):
        for one in self.started:
            one.wait_send()


def meet(devices):
    barrier = pltpu.get_barrier_semaphore()
    for device in devices:
        pl.semaphore_signal(barrier, inc=1, device_id=device, device_id_type=pl.DeviceIdType.MESH)
    pl.semaphore_wait(barrier, len(devices))


def partners():
    c, t = lax.axis_index("context"), lax.axis_index("tensor")
    flip = lambda x, bit: x + bit * (1 - 2 * lax.rem(x // bit, 2))
    return {
        "core": {"tensor": flip(t, 1)},
        "y": {"tensor": flip(t, 2)},
        "z": {"context": flip(c, 1)},
        "far": {"context": flip(c, 2)},
        "last": {"context": flip(flip(c, 1), 2)},
    }


def wide(x):
    return x.astype(f32)


def ranks():
    t = lax.axis_index("tensor")
    flip = lambda x, bit: x + bit * (1 - 2 * lax.rem(x // bit, 2))
    return (t, flip(t, 1), flip(t, 2), flip(flip(t, 1), 2))


def scatter_rank(wires, to, part, own, got_core, sent, got_y):
    size = part.shape[1] // 2
    halves = [pl.ds(0, size), pl.ds(size, size)]
    rank = ranks()
    from_core = {}
    for block in (1, 0):
        for k, at in enumerate(halves):
            from_core[block, k] = wires.copy(
                part.at[rank[1 + 2 * block], at], got_core.at[block, at], to["core"]
            )
    mine = [wires.here(part.at[rank[2 * block]], own.at[block]) for block in (0, 1)]
    yield
    for one in mine:
        one.wait()
    from_y = []
    for k, at in enumerate(halves):
        from_core[1, k].wait_recv()
        sent[at] = (wide(own[1, at]) + wide(got_core[1, at])).astype(bf16)
        from_y.append(wires.copy(sent.at[at], got_y.at[at], to["y"]))
    yield
    for k in range(2):
        from_core[0, k].wait_recv()
    total = wide(own[0]) + wide(got_core[0])
    for one in from_y:
        one.wait_recv()
    return total + wide(got_y[...])


def scatter_pair(wires, to, part, own, got_core, sent, got_y, got_z, diag_y, diag_z):
    size = part.shape[1] // 2
    low, high = pl.ds(0, size), pl.ds(size, size)
    from_core = {j: wires.copy(part.at[4 + j], got_core.at[j], to["core"]) for j in (3, 1, 2, 0)}
    mine = wires.here(part.at[pl.ds(0, 4)], own)
    yield
    mine.wait()
    both = lambda j, at: wide(own[j, at]) + wide(got_core[j, at])
    from_core[3].wait_recv()
    sent[2] = (wide(own[3]) + wide(got_core[3])).astype(bf16)
    via_z = wires.copy(sent.at[2, low], diag_z, to["z"])
    via_y = wires.copy(sent.at[2, high], diag_y, to["y"])
    from_core[1].wait_recv()
    sent[0, high] = both(1, high).astype(bf16)
    y_high = wires.copy(sent.at[0, high], got_y.at[high], to["y"])
    from_core[2].wait_recv()
    sent[1, low] = both(2, low).astype(bf16)
    z_low = wires.copy(sent.at[1, low], got_z.at[low], to["z"])
    yield
    via_z.wait_recv()
    sent[0, low] = (both(1, low) + wide(diag_z[...])).astype(bf16)
    y_low = wires.copy(sent.at[0, low], got_y.at[low], to["y"])
    via_y.wait_recv()
    sent[1, high] = (both(2, high) + wide(diag_y[...])).astype(bf16)
    z_high = wires.copy(sent.at[1, high], got_z.at[high], to["z"])
    yield
    from_core[0].wait_recv()
    total = wide(own[0]) + wide(got_core[0])
    for one in (y_high, z_low, y_low, z_high):
        one.wait_recv()
    return total + wide(got_y[...]) + wide(got_z[...])


def result_of(steps):
    while True:
        try:
            next(steps)
        except StopIteration as done:
            return done.value


def gather_rank(wires, to, block, out):
    size = block.shape[0] // 2
    halves = [pl.ds(0, size), pl.ds(size, size)]
    rank = ranks()
    mine = wires.here(block, out.at[rank[0]])
    from_y = [wires.copy(block.at[h], out.at[rank[0], h], to["y"]) for h in halves]
    from_core = [wires.copy(block, out.at[rank[0]], to["core"])]
    yield
    for h, one in zip(halves, from_y):
        one.wait_recv()
        from_core.append(wires.copy(out.at[rank[2], h], out.at[rank[2], h], to["core"]))
    for one in from_core:
        one.wait_recv()
    mine.wait()


def gather_pair(wires, to, block, out, base):
    size = block.shape[0] // 2
    low, high = pl.ds(0, size), pl.ds(size, size)
    at = lambda j: out.at[base + j]
    from_z = wires.copy(block, at(2), to["z"])
    yield
    from_y = wires.copy(block, at(1), to["y"])
    from_core = [wires.copy(block, at(4), to["core"])]
    yield
    from_y.wait_recv()
    via_z = wires.copy(out.at[base + 1, low], out.at[base + 3, low], to["z"])
    from_core.append(wires.copy(at(1), at(5), to["core"]))
    from_z.wait_recv()
    via_y = wires.copy(out.at[base + 2, high], out.at[base + 3, high], to["y"])
    from_core.append(wires.copy(at(2), at(6), to["core"]))
    yield
    via_z.wait_recv()
    via_y.wait_recv()
    from_core.append(wires.copy(at(3), at(7), to["core"]))
    return from_core


def remote_call(kernel, name, key, args, outs, scratch, copies, in_vmem):
    ins, out_in = in_vmem
    spec = lambda inside: pl.BlockSpec(memory_space=pltpu.VMEM if inside else pl.ANY)
    return pl.pallas_call(
        kernel,
        name=name,
        out_shape=outs,
        in_specs=[spec(x) for x in ins],
        out_specs=[spec(x) for x in out_in],
        scratch_shapes=list(scratch)
        + [
            pltpu.SemaphoreType.DMA((copies,)),
            pltpu.SemaphoreType.DMA((copies,)),
            pltpu.SemaphoreType.DMA((6,)),
        ],
        compiler_params=pltpu.CompilerParams(
            collective_id=key, has_side_effects=True, vmem_limit_bytes=VMEM_LIMIT
        ),
    )(*args)


def kv_gather_kernel(own_ref, out_ref, *sems):
    wires, to = Wires(*sems), partners()
    kind = lax.rem(lax.axis_index("tensor"), 2)
    rows = own_ref.shape[0]
    block = lambda j: out_ref.at[kind, pl.ds(j * rows, rows)]
    meet([to[k] for k in ("core", "z", "far", "last")])
    mine = wires.here(own_ref, block(0))
    arrive = [wires.copy(own_ref, block(j), to[k]) for j, k in ((3, "last"), (2, "far"), (1, "z"))]
    from_core = [wires.copy(own_ref, block(0), to["core"])]
    for j, one in ((1, arrive[2]), (2, arrive[1]), (3, arrive[0])):
        one.wait_recv()
        from_core.append(wires.copy(block(j), block(j), to["core"]))
    for one in from_core:
        one.wait_recv()
    mine.wait()
    wires.finish()


def kv_gather(own):
    rows, width = own.shape
    n_c = lax.axis_size("context")
    return remote_call(
        kv_gather_kernel,
        "kv_gather",
        0,
        [own],
        [jax.ShapeDtypeStruct((2, n_c * rows, width), bf16)],
        [],
        8,
        ([False], [False]),
    )[0]


def kv_scatter_kernel(
    part_ref, out_part, mid_ref, dkv_ref, outputs, own, got_core, sent, got, low, *rest
):
    first, wires, to = rest[:7], Wires(*rest[7:]), partners()
    kind = lax.rem(lax.axis_index("tensor"), 2)
    rows = dkv_ref.shape[0]
    block = lambda j: pl.ds(j * rows, rows)
    meet([to[k] for k in ("core", "y", "z", "far", "last")])
    steps = ((3, "last"), (2, "far"), (1, "z"), (0, None))
    from_core = {
        j: wires.copy(part_ref.at[1 - kind, block(j)], got_core.at[block(j)], to["core"])
        for j, _ in steps
    }
    mine = wires.here(part_ref.at[kind], own)
    ahead = scatter_pair(wires, to, out_part, *first)
    next(ahead)
    mine.wait()
    arrive = []
    for j, k in steps[:3]:
        from_core[j].wait_recv()
        sent[block(j)] = (wide(own[block(j)]) + wide(got_core[block(j)])).astype(bf16)
        arrive.append(wires.copy(sent.at[block(j)], got.at[block(j)], to[k]))
    next(ahead)
    from_core[0].wait_recv()
    total = wide(own[block(0)]) + wide(got_core[block(0)])
    for one in arrive:
        one.wait_recv()
    for j in (1, 2, 3):
        total = total + wide(got[block(j)])
    dkv_ref[...] = total
    low[...] = (mid_ref[...] + result_of(ahead)).astype(bf16)
    result_of(gather_rank(wires, to, low, outputs))
    wires.finish()


def kv_scatter(part, out_part, middle):
    _, rows, width = part.shape
    n_c = lax.axis_size("context")
    out_rows, out_width = middle.shape
    return remote_call(
        kv_scatter_kernel,
        "kv_scatter",
        1,
        [part, out_part.reshape(8, out_rows, out_width), middle],
        [
            jax.ShapeDtypeStruct((rows // n_c, width), f32),
            jax.ShapeDtypeStruct((4, out_rows, out_width), bf16),
        ],
        [pltpu.VMEM((rows, width), bf16)] * 4
        + [pltpu.VMEM((out_rows, out_width), bf16)]
        + pair_scratch(out_rows, out_width),
        24,
        ([False, False, True], [True, False]),
    )


def middle_kernel(
    part, x_ref, gain_ref, dy_ref, mid_ref, factor_ref, out, dys, own, core, sent, got, xn, *sems
):
    wires, to = Wires(*sems), partners()
    blocks = out.shape[0] // 2
    meet([to[k] for k in ("core", "y", "z", "far")])
    summed = scatter_rank(wires, to, part, own, core, sent, got)
    next(summed)
    dy_far = wires.copy(dy_ref, dys.at[blocks], to["far"])
    mine = [wires.here(dy_ref, dys.at[0])]
    dy_near = gather_pair(wires, to, dy_ref, dys, 0)
    next(dy_near)
    next(summed)
    next(dy_near)
    middle = wide(x_ref[...]) + result_of(summed)
    mid_ref[...] = middle
    factor = lax.rsqrt(jnp.mean(middle * middle, axis=-1, keepdims=True) + EPSILON)
    factor_ref[...] = factor
    xn[...] = (middle * factor * gain_ref[...]).astype(bf16)
    mine.append(wires.here(xn, out.at[0]))
    xn_far = wires.copy(xn, out.at[blocks], to["far"])
    xn_near = gather_pair(wires, to, xn, out, 0)
    next(xn_near)
    next(xn_near)
    next(dy_near)
    next(xn_near)
    dy_far.wait_recv()
    dy_last = gather_pair(wires, to, dys.at[blocks], dys, blocks)
    next(dy_last)
    next(dy_last)
    xn_far.wait_recv()
    xn_last = gather_pair(wires, to, out.at[blocks], out, blocks)
    next(xn_last)
    next(xn_last)
    ends = result_of(dy_near) + result_of(xn_near)
    next(dy_last)
    next(xn_last)
    ends += result_of(dy_last) + result_of(xn_last)
    for one in ends:
        one.wait_recv()
    for one in mine:
        one.wait()
    wires.finish()


def middle_norm(part, inputs_part, gain, dy_part):
    rows, width = inputs_part.shape
    return remote_call(
        middle_kernel,
        "middle_norm",
        2,
        [part.reshape(4, rows, width), inputs_part, gain, dy_part],
        [
            jax.ShapeDtypeStruct((rows, width), f32),
            jax.ShapeDtypeStruct((rows, 1), f32),
            jax.ShapeDtypeStruct((16, rows, width), bf16),
            jax.ShapeDtypeStruct((16, rows, width), bf16),
        ],
        [
            pltpu.VMEM((2, rows, width), bf16),
            pltpu.VMEM((2, rows, width), bf16),
            pltpu.VMEM((rows, width), bf16),
            pltpu.VMEM((rows, width), bf16),
            pltpu.VMEM((rows, width), bf16),
        ],
        48,
        ([False, True, True, True], [True, True, False, False]),
    )


def norm_back_rows(values, factor, gain, grad_normed):
    gained = gain * grad_normed
    inner = jnp.mean(gained * values, axis=-1, keepdims=True)
    grad_values = factor * gained - values * (factor * factor * factor) * inner
    return grad_values, jnp.sum(grad_normed * values * factor, axis=0, keepdims=True)


def middle_back_kernel(
    part, mid_ref, factor_ref, gain_ref, dy_ref, dmid_ref, dgain_ref, out, low, *rest
):
    first, wires, to = rest[:7], Wires(*rest[7:]), partners()
    meet([to[k] for k in ("core", "y", "z")])
    grad_normed = result_of(scatter_pair(wires, to, part, *first))
    du, dgain = norm_back_rows(mid_ref[...], factor_ref[...], gain_ref[...], grad_normed)
    dgain_ref[...] = dgain
    dmid = wide(dy_ref[...]) + du
    low[...] = dmid.astype(bf16)
    share = gather_rank(wires, to, low, out)
    next(share)
    dmid_ref[...] = dmid
    result_of(share)
    wires.finish()


def pair_scratch(rows, width):
    return [
        pltpu.VMEM((4, rows, width), bf16),
        pltpu.VMEM((4, rows, width), bf16),
        pltpu.VMEM((3, rows, width), bf16),
        pltpu.VMEM((rows, width), bf16),
        pltpu.VMEM((rows, width), bf16),
        pltpu.VMEM((rows // 2, width), bf16),
        pltpu.VMEM((rows // 2, width), bf16),
    ]


def middle_back(part, middle, factor, gain, dy_part):
    rows, width = middle.shape
    return remote_call(
        middle_back_kernel,
        "middle_back",
        3,
        [part.reshape(8, rows, width), middle, factor, gain, dy_part],
        [
            jax.ShapeDtypeStruct((rows, width), f32),
            jax.ShapeDtypeStruct((1, width), f32),
            jax.ShapeDtypeStruct((4, rows, width), bf16),
        ],
        [pltpu.VMEM((rows, width), bf16)] + pair_scratch(rows, width),
        16,
        ([False, True, True, True, True], [True, True, False]),
    )


def add_all(wires, ways, value, slots):
    for k, device in enumerate(ways):
        one = wires.copy(value, slots.at[k], device)
        one.wait()
        wires.started = [x for x in wires.started if x is not one]
        value[...] = value[...] + slots[k]


def input_back_kernel(
    part, x_ref, factor_ref, gain_ref, dmid_ref, small_ref, sum_ref, out, *rest
):
    low, own, core, sent, got, slots = rest[:-3]
    wires, to = Wires(*rest[-3:]), partners()
    meet([to[k] for k in ("core", "y")])
    grad_normed = result_of(scatter_rank(wires, to, part, own, core, sent, got))
    du, dgain = norm_back_rows(wide(x_ref[...]), factor_ref[...], gain_ref[...], grad_normed)
    low[...] = (dmid_ref[...] + du).astype(bf16)
    share = gather_rank(wires, to, low, out)
    next(share)
    width = dgain.shape[1]
    sum_ref[:, width:] = small_ref[:, width:]
    sum_ref[:, :width] = dgain
    add_all(wires, [to["core"], to["y"]], sum_ref, slots)
    result_of(share)
    wires.finish()


def input_back(part, inputs_part, factor, gain, grad_middle, small):
    rows, width = inputs_part.shape
    return remote_call(
        input_back_kernel,
        "input_back",
        5,
        [part.reshape(4, rows, width), inputs_part, factor, gain, grad_middle, small],
        [
            jax.ShapeDtypeStruct(small.shape, f32),
            jax.ShapeDtypeStruct((4, rows, width), bf16),
        ],
        [
            pltpu.VMEM((rows, width), bf16),
            pltpu.VMEM((2, rows, width), bf16),
            pltpu.VMEM((2, rows, width), bf16),
            pltpu.VMEM((rows, width), bf16),
            pltpu.VMEM((rows, width), bf16),
            pltpu.VMEM((2,) + small.shape, f32),
        ],
        16,
        ([False, True, True, True, True, True], [True, False]),
    )


def context_sum_kernel(over_f, *refs):
    parts, small_ref, outs, sum_ref, shared = refs[:3], refs[3], refs[4:6], refs[6], refs[7]
    lows, from_end, from_middle, slots = refs[8:11], refs[11:14], refs[14:17], refs[17]
    wires, to, c = Wires(*refs[18:]), partners(), lax.axis_index("context")
    last = lax.axis_size("context") - 1
    end = (c == 0) | (c == last)
    greet = ["core", "y", "z", "far", "last"]
    if over_f:
        to["f"] = {"fsdp": 1 - lax.axis_index("fsdp")}
        greet.append("f")
    meet([to[k] for k in greet])
    chunks = []
    for i, cuts in ((2, 1), (0, 2), (1, 2)):
        size = parts[i].shape[0] // cuts
        chunks += [(i, pl.ds(k * size, size)) for k in range(cuts)]
    inward = [wires.plan(parts[i].at[at], from_end[i].at[at], to["z"]) for i, at in chunks]
    across = [wires.plan(lows[i].at[at], from_middle[i].at[at], to["last"]) for i, at in chunks]
    outward = [wires.plan(lows[i].at[at], lows[i].at[at], to["z"]) for i, at in chunks]

    @pl.when(end)
    def _():
        for one in inward:
            one.start()

    @pl.when(jnp.logical_not(end))
    def _():
        for k, (i, at) in enumerate(chunks):
            inward[k].wait_recv()
            lows[i][at] = (wide(parts[i][at]) + wide(from_end[i][at])).astype(bf16)
            across[k].start()

    sum_ref[...] = small_ref[...]
    add_all(wires, [to[k] for k in (("f",) if over_f else ()) + ("z", "far")], sum_ref, slots)

    @pl.when(jnp.logical_not(end))
    def _():
        for k, (i, at) in enumerate(chunks):
            across[k].wait_recv()
            across[k].wait_send()
            lows[i][at] = (wide(lows[i][at]) + wide(from_middle[i][at])).astype(bf16)
            outward[k].start()

    def arrived(k):
        @pl.when(end)
        def _():
            outward[k].wait_recv()

    arrived(0)
    share = gather_rank(wires, to, lows[2], shared)
    next(share)
    for k in range(1, len(chunks)):
        arrived(k)
    for i in (0, 1):
        outs[i][...] = wide(lows[i][...])
    result_of(share)

    @pl.when(end)
    def _():
        for one in inward:
            one.wait_send()

    @pl.when(jnp.logical_not(end))
    def _():
        for one in outward:
            one.wait_send()

    wires.finish()


def context_sum(over_f, parts, small):
    like = lambda x: pltpu.VMEM(x.shape, bf16)
    return remote_call(
        functools.partial(context_sum_kernel, over_f),
        "context_sum",
        6,
        [*parts, small],
        [jax.ShapeDtypeStruct(x.shape, f32) for x in parts[:2]]
        + [jax.ShapeDtypeStruct(small.shape, f32)]
        + [jax.ShapeDtypeStruct((4,) + parts[2].shape, bf16)],
        [like(x) for x in parts] * 3 + [pltpu.VMEM((3,) + small.shape, f32)],
        32,
        ([True] * 4, [True] * 3 + [False]),
    )


def build(n_f, n_c, n_t):
    def flip(x, axis, bit):
        size = {"fsdp": n_f, "context": n_c, "tensor": n_t}[axis]
        return lax.ppermute(x, axis, [(i, i ^ bit) for i in range(size)])

    def by_bit(bit, x, other, axis):
        return jnp.where(
            bit == 0,
            jnp.concatenate([x, other], axis=axis),
            jnp.concatenate([other, x], axis=axis),
        )

    def after(x, *others):
        return lax.optimization_barrier((x, others))[0]

    def local(
        inputs,
        cotangent,
        blocks,
        attn_gain,
        w_query,
        b_query,
        w_key,
        b_key,
        w_value,
        b_value,
        w_out,
        ffn_gain,
        w_gate,
        w_up,
        w_down,
    ):
        rows, width = inputs.shape
        f = lax.axis_index("fsdp")
        c = lax.axis_index("context")
        t = lax.axis_index("tensor")
        core, parity, pair = t % 2, c % 2, c // 2
        heads = w_query.shape[1] // HD
        group = (t * heads) // (H // KV)
        part = rows // n_t
        units_all = w_gate.shape[1]
        units = units_all // 2

        def gather_f(x, axis):
            if n_f == 2:
                return by_bit(f, x, flip(x, "fsdp", 1), axis)
            return lax.all_gather(x, "fsdp", axis=axis, tiled=True)

        def grad_far(left, right, side):
            if n_f > 2:
                return None
            source = (left, right)[side]
            half = width // 2
            far = lax.dynamic_slice_in_dim(source, (1 - f) * half, half, 1)
            return (dot_rows(far, right) if side == 0 else dot_rows(left, far)).astype(bf16)

        def grad_sum(left, right, side, far):
            if n_f > 2:
                return lax.psum_scatter(
                    dot_rows(left, right).astype(bf16), "fsdp", scatter_dimension=side, tiled=True
                )
            source = (left, right)[side]
            half = width // 2
            own = lax.dynamic_slice_in_dim(source, f * half, half, 1)
            own = dot_rows(own, right) if side == 0 else dot_rows(left, own)
            return (own + flip(far, "fsdp", 1).astype(f32)).astype(bf16)

        small = jnp.concatenate(
            [v.reshape(1, -1) for v in (attn_gain, ffn_gain, b_query, b_key, b_value)], axis=1
        )
        column = lambda w: lax.dynamic_slice_in_dim(w, group * HD, HD, 1)
        w_kv_own = jnp.where(core == 0, column(w_key), column(w_value))
        pieces_f = lambda x, axis: (
            [x, flip(x, "fsdp", 1)]
            if n_f == 2
            else [lax.all_gather(x, "fsdp", axis=axis, tiled=True)]
        )
        meta = jnp.stack([f, 1 - f, core, pair]).astype(jnp.int32)
        w_q = pieces_f(w_query, 0)
        w_kv = pieces_f(w_kv_own, 0)
        small = gather_f(small, 0)
        w_out_all = gather_f(w_out, 1)
        piece = attn_gain.shape[0]
        gain_first = small[:, :piece].reshape(1, width).astype(f32)
        gain_second = small[:, piece : 2 * piece].reshape(1, width).astype(f32)
        bias_of = lambda lo, n: (
            small[:, lo : lo + n * (HD // n_f)]
            .reshape(n_f, n, HD // n_f)
            .transpose(1, 0, 2)
            .reshape(n, HD)
            .astype(f32)
        )
        at = 2 * piece
        bq = bias_of(at, heads)
        bk = bias_of(at + heads * (HD // n_f), KV)
        bv = bias_of(at + (heads + KV) * (HD // n_f), KV)
        b_kv = lax.dynamic_index_in_dim(jnp.where(core == 0, bk, bv), group, 0)

        unit_slice = lambda w: lax.dynamic_slice_in_dim(w, parity * units, units, 0)
        own_units = jnp.concatenate([unit_slice(w) for w in (w_gate.T, w_up.T, w_down)], axis=0)
        w_units = pieces_f(after(own_units, w_q, w_kv, small, w_out_all), 1)

        dy_part = lax.dynamic_slice_in_dim(cotangent, t * part, part, 0)

        seq_blocks = blocks[0].reshape(n_c, -1)
        own_blocks = seq_blocks.shape[1]
        key_blocks = jnp.concatenate(
            [lax.dynamic_index_in_dim(seq_blocks, c ^ j, 0, keepdims=False) for j in range(n_c)]
        )
        positions = (
            key_blocks[:own_blocks, None] * BLOCK + jnp.arange(BLOCK, dtype=jnp.int32)[None, :]
        ).reshape(-1)
        cosine, sine = rope_tables(positions)
        bias = jnp.concatenate([bq.reshape(1, -1), b_kv], axis=1)
        normed, factor_first, queries, kv_own = qkv(
            meta, inputs, gain_first, bias, cosine, sine, w_q, w_kv
        )
        kv = kv_gather(kv_own)
        attended, lse = attention(key_blocks, queries, kv)
        inputs_part = lax.dynamic_slice_in_dim(inputs, t * part, part, 0)
        middle, factor_second, normed2, dy_all = middle_norm(
            dot(attended, w_out_all).astype(bf16), inputs_part, gain_second, dy_part
        )

        hidden, grad_gate, grad_up, dx_part, out_part = ffn(meta, normed2, dy_all, w_units)
        down, gate_up = [hidden], [grad_gate, grad_up]
        if n_f == 2:
            down_sent = unit_grads(meta, 1, 2, dy_all, down)
            down_got = flip(down_sent, "fsdp", 1)
            gate_up_sent = unit_grads(meta, 1, 2, *after((normed2, gate_up), down_sent))
            gate_up_got = flip(gate_up_sent, "fsdp", 1)
            dx_part = after(dx_part, gate_up_sent)
        else:
            over_f = lambda x: lax.psum_scatter(x, "fsdp", scatter_dimension=1, tiled=True)
            down_own = over_f(unit_grads(meta, 0, 1, dy_all, down))
            gate_up_own = over_f(unit_grads(meta, 0, 1, normed2, gate_up))
            down_got, gate_up_got = jnp.zeros_like(down_own), jnp.zeros_like(gate_up_own)

        def unit_done(own, got):
            low = (own.astype(f32) + got.astype(f32)).astype(bf16)
            return low, flip(low, "context", 1)

        unit_whole = lambda low, other: by_bit(parity, low, other, 0).astype(f32)

        grad_middle, ffn_gain_grad, grad_middle_low = middle_back(
            dx_part, middle, factor_second, gain_second, dy_part
        )
        grad_middle_low = grad_middle_low.reshape(rows, width)
        if n_f == 2:
            down_own = unit_grads(meta, 0, 2, *after((dy_all, down), grad_middle_low))
        down_done = unit_done(down_own, after(down_got, grad_middle_low))
        grad_attended = dot_cols(after(grad_middle_low, down_done[0]), w_out_all).astype(bf16)

        dq_low, dkv = attention_back(key_blocks, queries, grad_attended, lse, cosine, sine, kv)
        if n_f == 2:
            gate_up_own = unit_grads(meta, 0, 2, *after((normed2, gate_up), dkv))
            dkv = after(dkv, gate_up_own)
        dkv, outputs = kv_scatter(after(dkv, down_done), out_part, middle)
        outputs = outputs.reshape(rows, width)
        gate_up_got = after(gate_up_got, dkv)
        gate_done, up_done = (
            unit_done(gate_up_own[k : k + units], gate_up_got[k : k + units]) for k in (0, units)
        )
        dkv = after(dkv, gate_done[0], up_done[0])
        dkv_low = jnp.where(core == 0, rotate_back(dkv, cosine, sine), dkv).astype(bf16)
        attention_args = (
            (attended, after(grad_middle_low, dkv), 1),
            (normed, after(dq_low, dkv), 0),
            (normed, dkv_low, 0),
        )
        fars = [grad_far(*args) for args in attention_args]
        dkv_low = after(dkv_low, fars)
        factor_part = lax.dynamic_slice_in_dim(factor_first, t * part, part, 0)
        own_biases = jnp.sum(
            jnp.concatenate([dq_low, dkv_low], axis=1).astype(f32), axis=0, keepdims=True
        )
        slots = lax.dynamic_update_slice(
            jnp.zeros((n_t, (heads + 1) * HD), f32), own_biases, (t, 0)
        )
        small_grads = jnp.concatenate(
            [jnp.zeros((1, width), f32), ffn_gain_grad, slots.reshape(1, -1)], axis=1
        )
        small_grads, input_grad = input_back(
            qkv_back(meta, dq_low, dkv_low, w_q, w_kv),
            inputs_part,
            factor_part,
            gain_first,
            grad_middle,
            small_grads,
        )
        input_grad = input_grad.reshape(rows, width)
        if n_f > 2:
            small_grads = lax.psum(small_grads, "fsdp")
        attention_parts = [grad_sum(*args, far) for args, far in zip(attention_args, fars)]
        wd_grad = unit_whole(*after(down_done, small_grads))
        small_grads, gate_done, up_done = lax.optimization_barrier(
            (small_grads, gate_done, up_done)
        )
        wo_grad, wq_grad, packed, wkv_all = context_sum(
            n_f == 2, attention_parts, after(small_grads, wd_grad)
        )
        wkv_all = wkv_all.astype(f32)
        wk_grad = jnp.concatenate([wkv_all[0], wkv_all[2]], axis=1)
        wv_grad = jnp.concatenate([wkv_all[1], wkv_all[3]], axis=1)
        packed = packed[0]
        attn_gain_grad = lax.dynamic_slice_in_dim(packed, f * piece, piece, 0)
        ffn_gain_grad = lax.dynamic_slice_in_dim(packed, width + f * piece, piece, 0)
        slots = packed[2 * width :].reshape(n_t, heads + 1, HD)
        slots = lax.dynamic_slice_in_dim(slots, f * (HD // n_f), HD // n_f, 2)
        bq_out = lax.dynamic_index_in_dim(slots, t, 0, keepdims=False)[:heads]
        bk_out = slots[0::2, heads]
        bv_out = slots[1::2, heads]

        wg_grad, wu_grad = unit_whole(*gate_done), unit_whole(*up_done)
        wg_grad, wu_grad = wg_grad.T, wu_grad.T

        return (
            outputs,
            input_grad,
            attn_gain_grad,
            wq_grad,
            bq_out,
            wk_grad,
            bk_out,
            wv_grad,
            bv_out,
            wo_grad,
            ffn_gain_grad,
            wg_grad,
            wu_grad,
            wd_grad,
        )

    return local


def solution(mesh):
    in_specs = (
        P(("fsdp", "context"), None),
        P(("fsdp", "context"), None),
        P("fsdp", None),
        P("fsdp"),
        P("fsdp", "tensor"),
        P("tensor", "fsdp"),
        P("fsdp", None),
        P(None, "fsdp"),
        P("fsdp", None),
        P(None, "fsdp"),
        P("tensor", "fsdp"),
        P("fsdp"),
        P("fsdp", "tensor"),
        P("fsdp", "tensor"),
        P("tensor", "fsdp"),
    )
    out_specs = (
        P(("fsdp", "context"), None),
        P(("fsdp", "context"), None),
        P("fsdp"),
        P("fsdp", "tensor"),
        P("tensor", "fsdp"),
        P("fsdp", None),
        P(None, "fsdp"),
        P("fsdp", None),
        P(None, "fsdp"),
        P("tensor", "fsdp"),
        P("fsdp"),
        P("fsdp", "tensor"),
        P("fsdp", "tensor"),
        P("tensor", "fsdp"),
    )
    local = build(mesh.shape["fsdp"], mesh.shape["context"], mesh.shape["tensor"])
    return jax.shard_map(local, mesh=mesh, in_specs=in_specs, out_specs=out_specs, check_vma=False)
```

```python
import functools

import jax
import jax.numpy as jnp
from jax import lax
from jax.experimental import pallas as pl
from jax.experimental.pallas import tpu as pltpu
from jax.sharding import PartitionSpec as P

H = 12
KV = 2
HD = 128
BLOCK = 256

EPSILON = 1e-06
ROPE_BASE = 1000000.0
MASKED = -1e30
SCALING = HD ** (-0.5)
LANES = 128
VMEM_LIMIT = 60 << 20
FFN_VMEM_LIMIT = 63 << 20

f32 = jnp.float32
bf16 = jnp.bfloat16


def rope_tables(positions):
    halfway = HD // 2
    frequency = ROPE_BASE ** (-(jnp.arange(halfway, dtype=f32) * 2.0 / HD))
    angles = positions.astype(f32)[:, None] * frequency[None, :]
    cosine, sine = jnp.cos(angles), jnp.sin(angles)
    return (jnp.concatenate([cosine, cosine], axis=1), jnp.concatenate([sine, sine], axis=1))


def rotate(field, cosine, sine):
    halfway = HD // 2
    turned = jnp.concatenate([-field[..., halfway:], field[..., :halfway]], axis=-1)
    return field * cosine + turned * sine


def rotate_back(grad_field, cosine, sine):
    halfway = HD // 2
    moved = grad_field * sine
    turned = jnp.concatenate([moved[..., halfway:], -moved[..., :halfway]], axis=-1)
    return grad_field * cosine + turned


def dot(left, right):
    return jnp.dot(left, right, preferred_element_type=f32)


def dot_rows(left, right):
    return lax.dot_general(left, right, (((0,), (0,)), ((), ())), preferred_element_type=f32)


def dot_cols(left, right):
    return lax.dot_general(left, right, (((1,), (1,)), ((), ())), preferred_element_type=f32)


def mask_row(kb_ref, own_block, key_blocks):
    return jnp.concatenate(
        [
            jnp.full((1, BLOCK), jnp.where(kb_ref[j] <= own_block, 0.0, MASKED), f32)
            for j in range(key_blocks)
        ],
        axis=1,
    )


def attention_kernel(key_blocks, kb_ref, q_ref, k_ref, v_ref, o_ref, lse_ref):
    bias = mask_row(kb_ref, kb_ref[pl.program_id(1)], key_blocks)
    scores = dot_cols(q_ref[...], k_ref[...]) * SCALING + bias
    row_max = jnp.max(scores, axis=1, keepdims=True)
    expo = jnp.exp(scores - row_max)
    total = jnp.sum(expo, axis=1, keepdims=True)
    probability = (expo * (1.0 / total)).astype(bf16)
    o_ref[...] = dot(probability, v_ref[...]).astype(bf16)
    lse_ref[0] = row_max + jnp.log(total)


def attention(key_blocks, queries, kv):
    rows, width = queries.shape
    heads = width // HD
    whole = lambda kind: pl.BlockSpec((None,) + kv.shape[1:], lambda h, i, kb: (kind, 0, 0))
    tile = pl.BlockSpec((BLOCK, HD), lambda h, i, kb: (i, h))
    return pl.pallas_call(
        functools.partial(attention_kernel, kv.shape[1] // BLOCK),
        name="attention",
        grid_spec=pltpu.PrefetchScalarGridSpec(
            num_scalar_prefetch=1,
            grid=(heads, rows // BLOCK),
            in_specs=[tile, whole(0), whole(1)],
            out_specs=[tile, pl.BlockSpec((1, BLOCK, 1), lambda h, i, kb: (h, i, 0))],
        ),
        out_shape=[
            jax.ShapeDtypeStruct((rows, width), bf16),
            jax.ShapeDtypeStruct((heads, rows, 1), f32),
        ],
        compiler_params=pltpu.CompilerParams(vmem_limit_bytes=VMEM_LIMIT),
    )(key_blocks, queries, kv, kv)


def attention_back_kernel(
    key_blocks,
    kb_ref,
    q_ref,
    do_ref,
    lse_ref,
    cos_ref,
    sin_ref,
    k_ref,
    v_ref,
    dq_ref,
    dkv_ref,
    dk_ref,
    dv_ref,
):
    head, i = pl.program_id(0), pl.program_id(1)

    @pl.when((head == 0) & (i == 0))
    def _():
        dk_ref[...] = jnp.zeros_like(dk_ref)
        dv_ref[...] = jnp.zeros_like(dv_ref)

    bias = mask_row(kb_ref, kb_ref[i], key_blocks)
    scores = dot_cols(q_ref[...], k_ref[...]) * SCALING + bias
    probability = jnp.exp(scores - lse_ref[0])
    grad_probs = dot_cols(do_ref[...], v_ref[...])
    inner = jnp.sum(probability * grad_probs, axis=1, keepdims=True)
    grad_scores = (probability * (grad_probs - inner)).astype(bf16)
    grad_query = dot(grad_scores, k_ref[...]) * SCALING
    moved = grad_query * sin_ref[...]
    sign = jnp.where(lax.broadcasted_iota(jnp.int32, moved.shape, 1) < HD // 2, 1.0, -1.0)
    dq_ref[...] = (
        grad_query * cos_ref[...] + pltpu.roll(moved, HD // 2, 1) * sign
    ).astype(bf16)
    dk_ref[...] += dot_rows(grad_scores, q_ref[...]) * SCALING
    dv_ref[...] += dot_rows(probability.astype(bf16), do_ref[...])

    @pl.when((head == pl.num_programs(0) - 1) & (i == pl.num_programs(1) - 1))
    def _():
        dkv_ref[0] = dk_ref[...].astype(bf16)
        dkv_ref[1] = dv_ref[...].astype(bf16)


def attention_back(key_blocks, queries, grad_out, lse, cosine, sine, kv):
    rows, width = queries.shape
    heads = width // HD
    whole = lambda kind: pl.BlockSpec((None,) + kv.shape[1:], lambda h, i, kb: (kind, 0, 0))
    tile = pl.BlockSpec((BLOCK, HD), lambda h, i, kb: (i, h))
    table = pl.BlockSpec((BLOCK, HD), lambda h, i, kb: (i, 0))
    return pl.pallas_call(
        functools.partial(attention_back_kernel, kv.shape[1] // BLOCK),
        name="attention_back",
        grid_spec=pltpu.PrefetchScalarGridSpec(
            num_scalar_prefetch=1,
            grid=(heads, rows // BLOCK),
            in_specs=[
                tile,
                tile,
                pl.BlockSpec((1, BLOCK, 1), lambda h, i, kb: (h, i, 0)),
                table,
                table,
                whole(0),
                whole(1),
            ],
            out_specs=[tile, pl.BlockSpec(kv.shape, lambda h, i, kb: (0, 0, 0))],
            scratch_shapes=[pltpu.VMEM(kv.shape[1:], f32)] * 2,
        ),
        out_shape=[
            jax.ShapeDtypeStruct((rows, width), bf16),
            jax.ShapeDtypeStruct(kv.shape, bf16),
        ],
        compiler_params=pltpu.CompilerParams(vmem_limit_bytes=VMEM_LIMIT),
    )(key_blocks, queries, grad_out, lse, cosine, sine, kv, kv)


def qkv_kernel(pieces, meta_ref, x_ref, gain_ref, bias_ref, cos_ref, sin_ref, *refs):
    weights, (xn_ref, factor_ref, q_ref, kv_ref) = refs[: 2 * pieces], refs[2 * pieces :]
    values = x_ref[...].astype(f32)
    factor = lax.rsqrt(jnp.mean(values * values, axis=-1, keepdims=True) + EPSILON)
    factor_ref[...] = factor
    xn_ref[...] = (values * factor * gain_ref[...]).astype(bf16)
    depth = weights[0].shape[0]
    normed = [xn_ref[:, columns_of(meta_ref, j, depth, pieces)] for j in range(pieces)]
    cosine, sine = cos_ref[...], sin_ref[...]
    sign = jnp.where(lax.broadcasted_iota(jnp.int32, cosine.shape, 1) < HD // 2, -1.0, 1.0)
    sine = sine * sign
    width = q_ref.shape[1]
    total = bias_ref[:, :width] + sum(dot(x, w[...]) for x, w in zip(normed, weights[:pieces]))
    turn = lambda own: own * cosine + pltpu.roll(own, HD // 2, 1) * sine
    for h in range(width // HD):
        q_ref[:, h * HD : (h + 1) * HD] = turn(total[:, h * HD : (h + 1) * HD]).astype(bf16)
    own = bias_ref[:, width:] + sum(dot(x, w[...]) for x, w in zip(normed, weights[pieces:]))
    kv_ref[...] = jnp.where(meta_ref[2] == 0, turn(own), own).astype(bf16)


def columns_of(meta_ref, j, depth, pieces):
    if pieces == 1:
        return slice(None)
    return pl.ds(pl.multiple_of(meta_ref[j] * depth, LANES), depth)


def qkv(meta, inputs, gain, bias, cosine, sine, w_q, w_kv):
    rows, width = inputs.shape
    out = w_q[0].shape[1]
    tile = 256
    row = lambda n: pl.BlockSpec((tile, n), lambda i, m: (i, 0))
    fixed = lambda w: pl.BlockSpec(w.shape, lambda i, m: (0, 0))
    return pl.pallas_call(
        functools.partial(qkv_kernel, len(w_q)),
        name="qkv",
        grid_spec=pltpu.PrefetchScalarGridSpec(
            num_scalar_prefetch=1,
            grid=(rows // tile,),
            in_specs=[row(width), fixed(gain), fixed(bias), row(HD), row(HD)]
            + [fixed(w) for w in (*w_q, *w_kv)],
            out_specs=[row(width), row(1), row(out), row(HD)],
        ),
        out_shape=[
            jax.ShapeDtypeStruct((rows, width), bf16),
            jax.ShapeDtypeStruct((rows, 1), f32),
            jax.ShapeDtypeStruct((rows, out), bf16),
            jax.ShapeDtypeStruct((rows, HD), bf16),
        ],
        compiler_params=pltpu.CompilerParams(vmem_limit_bytes=VMEM_LIMIT),
    )(meta, inputs, gain, bias, cosine, sine, *w_q, *w_kv)


def qkv_back_kernel(pieces, meta_ref, dq_ref, dkv_ref, *refs):
    w_q, w_kv, out_ref = refs[:pieces], refs[pieces : 2 * pieces], refs[-1]
    for j in range(pieces):
        out_ref[:, columns_of(meta_ref, j, w_q[j].shape[0], pieces)] = (
            dot_cols(dq_ref[...], w_q[j][...]) + dot_cols(dkv_ref[...], w_kv[j][...])
        ).astype(bf16)


def qkv_back(meta, grad_q, grad_kv, w_q, w_kv):
    rows, width = grad_q.shape[0], sum(w.shape[0] for w in w_q)
    tile = 256
    row = lambda n: pl.BlockSpec((tile, n), lambda i, m: (i, 0))
    fixed = lambda w: pl.BlockSpec(w.shape, lambda i, m: (0, 0))
    return pl.pallas_call(
        functools.partial(qkv_back_kernel, len(w_q)),
        name="qkv_back",
        grid_spec=pltpu.PrefetchScalarGridSpec(
            num_scalar_prefetch=1,
            grid=(rows // tile,),
            in_specs=[row(grad_q.shape[1]), row(HD)] + [fixed(w) for w in (*w_q, *w_kv)],
            out_specs=row(width),
        ),
        out_shape=jax.ShapeDtypeStruct((rows, width), bf16),
        compiler_params=pltpu.CompilerParams(vmem_limit_bytes=VMEM_LIMIT),
    )(meta, grad_q, grad_kv, *w_q, *w_kv)


def ffn_kernel(pieces, meta_ref, x_ref, dy_ref, *refs):
    wg, wu, wd = (refs[m * pieces : (m + 1) * pieces] for m in range(3))
    refs = refs[3 * pieces :]
    hid_ref, dg_ref, du_ref, dx_ref, out_ref = refs[:5]
    columns = [columns_of(meta_ref, j, wg[j].shape[1], pieces) for j in range(pieces)]
    gate = sum(dot_cols(x_ref[:, at], w[...]) for at, w in zip(columns, wg))
    up = sum(dot_cols(x_ref[:, at], w[...]) for at, w in zip(columns, wu))
    grad_hidden = sum(dot_cols(dy_ref[:, at], w[...]) for at, w in zip(columns, wd))
    sigma = 1.0 / (1.0 + jnp.exp(-gate))
    gated = gate * sigma
    hid_ref[...] = (gated * up).astype(bf16)
    dg_ref[...] = (grad_hidden * up * (sigma + gated * (1.0 - sigma))).astype(bf16)
    du_ref[...] = (grad_hidden * gated).astype(bf16)
    step, steps = pl.program_id(0), pl.num_programs(0)

    @pl.when(step // (steps // 2) == meta_ref[3])
    def _():
        for at, g, u, d in zip(columns, wg, wu, wd):
            dx_ref[:, at] = (dot(dg_ref[...], g[...]) + dot(du_ref[...], u[...])).astype(bf16)
            out_ref[:, at] = dot(hid_ref[...], d[...]).astype(bf16)

    if pieces == 2:
        outs, totals = refs[5:8], refs[8:11]
        sources = ((hid_ref, dy_ref), (dg_ref, x_ref), (du_ref, x_ref))

        @pl.when(step == 0)
        def _():
            for total in totals:
                total[...] = jnp.zeros_like(total)

        for total, (unit, row) in zip(totals, sources):
            total[...] += dot_rows(unit[...], row[:, columns[1]])

        @pl.when(step == steps - 1)
        def _():
            for out, total in zip(outs, totals):
                out[...] = total[...].astype(bf16)


def ffn(meta, normed, grad_out, weights):
    width = normed.shape[-1]
    rows = normed.shape[0] * normed.shape[1]
    pieces = len(weights)
    units, depth = weights[0].shape[0] // 3, weights[0].shape[1]
    tile = 512
    steps = rows // tile
    half = steps // 2
    flat = lambda x: x.reshape(-1, width)
    read = pl.BlockSpec((tile, width), lambda i, m: (lax.rem(i + m[3] * half, steps), 0))
    once = pl.Buffered(1)
    weight = lambda w, k: pl.BlockSpec((units, depth), lambda i, m: (k, 0), pipeline_mode=once)
    placed = pl.BlockSpec((tile, units), lambda i, m: (i, 0))
    near = pl.BlockSpec((tile, width), lambda i, m: (jnp.clip(i - m[3] * half, 0, half - 1), 0))
    grads = [pl.BlockSpec((units, depth), lambda i, m: (0, 0), pipeline_mode=once)] * 3
    grads = grads if pieces == 2 else []
    shapes = [(rows, units)] * 3 + [(rows // 2, width)] * 2 + [(units, depth)] * len(grads)
    return pl.pallas_call(
        functools.partial(ffn_kernel, pieces),
        name="ffn",
        grid_spec=pltpu.PrefetchScalarGridSpec(
            num_scalar_prefetch=1,
            grid=(steps,),
            in_specs=[read, read] + [weight(w, k) for k in range(3) for w in weights],
            out_specs=[placed] * 3 + [near] * 2 + grads,
            scratch_shapes=[pltpu.VMEM((units, depth), f32)] * len(grads),
        ),
        out_shape=[jax.ShapeDtypeStruct(shape, bf16) for shape in shapes],
        compiler_params=pltpu.CompilerParams(vmem_limit_bytes=FFN_VMEM_LIMIT),
    )(meta, flat(normed), flat(grad_out), *(list(weights) * 3))


def unit_grads_kernel(count, meta_ref, near_ref, far_ref, *refs):
    units, out_ref, x_ref = refs[:count], refs[-2], refs[-1]
    half = near_ref.shape[0]
    x_ref[pl.ds(pl.multiple_of(meta_ref[3] * half, half), half)] = near_ref[...]
    x_ref[pl.ds(pl.multiple_of((1 - meta_ref[3]) * half, half), half)] = far_ref[...]
    for k, unit in enumerate(units):
        depth = unit.shape[1]
        out_ref[k * depth : (k + 1) * depth] = dot_rows(unit[...], x_ref[...]).astype(bf16)


def unit_grads(meta, which, pieces, x, units_of):
    width = x.shape[-1]
    count, (rows, units) = len(units_of), units_of[0].shape
    depth = width // pieces
    tile = 256
    steps = depth // tile
    shard = (lambda m: m[which]) if pieces > 1 else (lambda m: 0)
    feature = lambda half: pl.BlockSpec(
        (rows // 2, tile), lambda i, m: (half, shard(m) * steps + i)
    )
    unit = pl.BlockSpec((rows, units), lambda i, m: (0, 0), pipeline_mode=pl.Buffered(1))
    x = x.reshape(-1, width)
    return pl.pallas_call(
        functools.partial(unit_grads_kernel, count),
        name=f"unit_grads_{which}_{count}",
        grid_spec=pltpu.PrefetchScalarGridSpec(
            num_scalar_prefetch=1,
            grid=(steps,),
            in_specs=[feature(0), feature(1)] + [unit] * count,
            out_specs=pl.BlockSpec((count * units, tile), lambda i, m: (0, i)),
            scratch_shapes=[pltpu.VMEM((rows, tile), bf16)],
        ),
        out_shape=jax.ShapeDtypeStruct((count * units, depth), bf16),
        compiler_params=pltpu.CompilerParams(vmem_limit_bytes=VMEM_LIMIT),
    )(meta, x, x, *units_of)


class Wires:
    def __init__(self, sends, receives, locals_):
        self.sends, self.receives, self.locals = sends, receives, locals_
        self.used = self.used_local = 0
        self.started = []

    def plan(self, source, target, device):
        k = self.used
        self.used += 1
        return pltpu.make_async_remote_copy(
            source,
            target,
            self.sends.at[k],
            self.receives.at[k],
            device_id=device,
            device_id_type=pl.DeviceIdType.MESH,
        )

    def copy(self, source, target, device):
        one = self.plan(source, target, device)
        one.start()
        self.started.append(one)
        return one

    def here(self, source, target):
        k = self.used_local
        self.used_local += 1
        one = pltpu.make_async_copy(source, target, self.locals.at[k])
        one.start()
        return one

    def finish(self):
        for one in self.started:
            one.wait_send()


def meet(devices):
    barrier = pltpu.get_barrier_semaphore()
    for device in devices:
        pl.semaphore_signal(barrier, inc=1, device_id=device, device_id_type=pl.DeviceIdType.MESH)
    pl.semaphore_wait(barrier, len(devices))


def partners():
    c, t = lax.axis_index("context"), lax.axis_index("tensor")
    flip = lambda x, bit: x + bit * (1 - 2 * lax.rem(x // bit, 2))
    return {
        "core": {"tensor": flip(t, 1)},
        "y": {"tensor": flip(t, 2)},
        "z": {"context": flip(c, 1)},
        "far": {"context": flip(c, 2)},
        "last": {"context": flip(flip(c, 1), 2)},
    }


def wide(x):
    return x.astype(f32)


def ranks():
    t = lax.axis_index("tensor")
    flip = lambda x, bit: x + bit * (1 - 2 * lax.rem(x // bit, 2))
    return (t, flip(t, 1), flip(t, 2), flip(flip(t, 1), 2))


def scatter_rank(wires, to, part, own, got_core, sent, got_y):
    size = part.shape[1] // 2
    halves = [pl.ds(0, size), pl.ds(size, size)]
    rank = ranks()
    from_core = {}
    for block in (1, 0):
        for k, at in enumerate(halves):
            from_core[block, k] = wires.copy(
                part.at[rank[1 + 2 * block], at], got_core.at[block, at], to["core"]
            )
    mine = [wires.here(part.at[rank[2 * block]], own.at[block]) for block in (0, 1)]
    yield
    for one in mine:
        one.wait()
    from_y = []
    for k, at in enumerate(halves):
        from_core[1, k].wait_recv()
        sent[at] = (wide(own[1, at]) + wide(got_core[1, at])).astype(bf16)
        from_y.append(wires.copy(sent.at[at], got_y.at[at], to["y"]))
    yield
    for k in range(2):
        from_core[0, k].wait_recv()
    total = wide(own[0]) + wide(got_core[0])
    for one in from_y:
        one.wait_recv()
    return total + wide(got_y[...])


def scatter_pair(wires, to, part, own, got_core, sent, got_y, got_z, diag_y, diag_z):
    size = part.shape[1] // 2
    low, high = pl.ds(0, size), pl.ds(size, size)
    from_core = {j: wires.copy(part.at[4 + j], got_core.at[j], to["core"]) for j in (3, 1, 2, 0)}
    mine = wires.here(part.at[pl.ds(0, 4)], own)
    yield
    mine.wait()
    both = lambda j, at: wide(own[j, at]) + wide(got_core[j, at])
    from_core[3].wait_recv()
    sent[2] = (wide(own[3]) + wide(got_core[3])).astype(bf16)
    via_z = wires.copy(sent.at[2, low], diag_z, to["z"])
    via_y = wires.copy(sent.at[2, high], diag_y, to["y"])
    from_core[1].wait_recv()
    sent[0, high] = both(1, high).astype(bf16)
    y_high = wires.copy(sent.at[0, high], got_y.at[high], to["y"])
    from_core[2].wait_recv()
    sent[1, low] = both(2, low).astype(bf16)
    z_low = wires.copy(sent.at[1, low], got_z.at[low], to["z"])
    yield
    via_z.wait_recv()
    sent[0, low] = (both(1, low) + wide(diag_z[...])).astype(bf16)
    y_low = wires.copy(sent.at[0, low], got_y.at[low], to["y"])
    via_y.wait_recv()
    sent[1, high] = (both(2, high) + wide(diag_y[...])).astype(bf16)
    z_high = wires.copy(sent.at[1, high], got_z.at[high], to["z"])
    yield
    from_core[0].wait_recv()
    total = wide(own[0]) + wide(got_core[0])
    for one in (y_high, z_low, y_low, z_high):
        one.wait_recv()
    return total + wide(got_y[...]) + wide(got_z[...])


def result_of(steps):
    while True:
        try:
            next(steps)
        except StopIteration as done:
            return done.value


def gather_rank(wires, to, block, out):
    size = block.shape[0] // 2
    halves = [pl.ds(0, size), pl.ds(size, size)]
    rank = ranks()
    mine = wires.here(block, out.at[rank[0]])
    from_y = [wires.copy(block.at[h], out.at[rank[0], h], to["y"]) for h in halves]
    from_core = [wires.copy(block, out.at[rank[0]], to["core"])]
    yield
    for h, one in zip(halves, from_y):
        one.wait_recv()
        from_core.append(wires.copy(out.at[rank[2], h], out.at[rank[2], h], to["core"]))
    for one in from_core:
        one.wait_recv()
    mine.wait()


def gather_pair(wires, to, block, out, base):
    size = block.shape[0] // 2
    low, high = pl.ds(0, size), pl.ds(size, size)
    at = lambda j: out.at[base + j]
    from_z = wires.copy(block, at(2), to["z"])
    yield
    from_y = wires.copy(block, at(1), to["y"])
    from_core = [wires.copy(block, at(4), to["core"])]
    yield
    from_y.wait_recv()
    via_z = wires.copy(out.at[base + 1, low], out.at[base + 3, low], to["z"])
    from_core.append(wires.copy(at(1), at(5), to["core"]))
    from_z.wait_recv()
    via_y = wires.copy(out.at[base + 2, high], out.at[base + 3, high], to["y"])
    from_core.append(wires.copy(at(2), at(6), to["core"]))
    yield
    via_z.wait_recv()
    via_y.wait_recv()
    from_core.append(wires.copy(at(3), at(7), to["core"]))
    return from_core


def remote_call(kernel, name, key, args, outs, scratch, copies, in_vmem):
    ins, out_in = in_vmem
    spec = lambda inside: pl.BlockSpec(memory_space=pltpu.VMEM if inside else pl.ANY)
    return pl.pallas_call(
        kernel,
        name=name,
        out_shape=outs,
        in_specs=[spec(x) for x in ins],
        out_specs=[spec(x) for x in out_in],
        scratch_shapes=list(scratch)
        + [
            pltpu.SemaphoreType.DMA((copies,)),
            pltpu.SemaphoreType.DMA((copies,)),
            pltpu.SemaphoreType.DMA((6,)),
        ],
        compiler_params=pltpu.CompilerParams(
            collective_id=key, has_side_effects=True, vmem_limit_bytes=VMEM_LIMIT
        ),
    )(*args)


def kv_gather_kernel(own_ref, out_ref, *sems):
    wires, to = Wires(*sems), partners()
    kind = lax.rem(lax.axis_index("tensor"), 2)
    rows = own_ref.shape[0]
    block = lambda j: out_ref.at[kind, pl.ds(j * rows, rows)]
    meet([to[k] for k in ("core", "z", "far", "last")])
    mine = wires.here(own_ref, block(0))
    arrive = [wires.copy(own_ref, block(j), to[k]) for j, k in ((3, "last"), (2, "far"), (1, "z"))]
    from_core = [wires.copy(own_ref, block(0), to["core"])]
    for j, one in ((1, arrive[2]), (2, arrive[1]), (3, arrive[0])):
        one.wait_recv()
        from_core.append(wires.copy(block(j), block(j), to["core"]))
    for one in from_core:
        one.wait_recv()
    mine.wait()
    wires.finish()


def kv_gather(own):
    rows, width = own.shape
    n_c = lax.axis_size("context")
    return remote_call(
        kv_gather_kernel,
        "kv_gather",
        0,
        [own],
        [jax.ShapeDtypeStruct((2, n_c * rows, width), bf16)],
        [],
        8,
        ([False], [False]),
    )[0]


def kv_scatter_kernel(part_ref, dkv_ref, own, got_core, sent, got, *sems):
    wires, to = Wires(*sems), partners()
    kind = lax.rem(lax.axis_index("tensor"), 2)
    rows = dkv_ref.shape[0]
    block = lambda j: pl.ds(j * rows, rows)
    meet([to[k] for k in ("core", "z", "far", "last")])
    steps = ((3, "last"), (2, "far"), (1, "z"), (0, None))
    from_core = {
        j: wires.copy(part_ref.at[1 - kind, block(j)], got_core.at[block(j)], to["core"])
        for j, _ in steps
    }
    mine = wires.here(part_ref.at[kind], own)
    mine.wait()
    arrive = []
    for j, k in steps[:3]:
        from_core[j].wait_recv()
        sent[block(j)] = (wide(own[block(j)]) + wide(got_core[block(j)])).astype(bf16)
        arrive.append(wires.copy(sent.at[block(j)], got.at[block(j)], to[k]))
    from_core[0].wait_recv()
    total = wide(own[block(0)]) + wide(got_core[block(0)])
    for one in arrive:
        one.wait_recv()
    for j in (1, 2, 3):
        total = total + wide(got[block(j)])
    dkv_ref[...] = total
    wires.finish()


def kv_scatter(part):
    _, rows, width = part.shape
    n_c = lax.axis_size("context")
    return remote_call(
        kv_scatter_kernel,
        "kv_scatter",
        1,
        [part],
        [jax.ShapeDtypeStruct((rows // n_c, width), f32)],
        [pltpu.VMEM((rows, width), bf16)] * 4,
        7,
        ([False], [True]),
    )[0]


def middle_kernel(
    part, x_ref, gain_ref, dy_ref, mid_ref, factor_ref, out, dys, own, core, sent, got, xn, *sems
):
    wires, to = Wires(*sems), partners()
    blocks = out.shape[0] // 2
    meet([to[k] for k in ("core", "y", "z", "far")])
    summed = scatter_rank(wires, to, part, own, core, sent, got)
    next(summed)
    dy_far = wires.copy(dy_ref, dys.at[blocks], to["far"])
    mine = [wires.here(dy_ref, dys.at[0])]
    dy_near = gather_pair(wires, to, dy_ref, dys, 0)
    next(dy_near)
    next(summed)
    next(dy_near)
    middle = wide(x_ref[...]) + result_of(summed)
    mid_ref[...] = middle
    factor = lax.rsqrt(jnp.mean(middle * middle, axis=-1, keepdims=True) + EPSILON)
    factor_ref[...] = factor
    xn[...] = (middle * factor * gain_ref[...]).astype(bf16)
    mine.append(wires.here(xn, out.at[0]))
    xn_far = wires.copy(xn, out.at[blocks], to["far"])
    xn_near = gather_pair(wires, to, xn, out, 0)
    next(xn_near)
    next(xn_near)
    next(dy_near)
    next(xn_near)
    dy_far.wait_recv()
    dy_last = gather_pair(wires, to, dys.at[blocks], dys, blocks)
    next(dy_last)
    next(dy_last)
    xn_far.wait_recv()
    xn_last = gather_pair(wires, to, out.at[blocks], out, blocks)
    next(xn_last)
    next(xn_last)
    ends = result_of(dy_near) + result_of(xn_near)
    next(dy_last)
    next(xn_last)
    ends += result_of(dy_last) + result_of(xn_last)
    for one in ends:
        one.wait_recv()
    for one in mine:
        one.wait()
    wires.finish()


def middle_norm(part, inputs_part, gain, dy_part):
    rows, width = inputs_part.shape
    return remote_call(
        middle_kernel,
        "middle_norm",
        2,
        [part.reshape(4, rows, width), inputs_part, gain, dy_part],
        [
            jax.ShapeDtypeStruct((rows, width), f32),
            jax.ShapeDtypeStruct((rows, 1), f32),
            jax.ShapeDtypeStruct((16, rows, width), bf16),
            jax.ShapeDtypeStruct((16, rows, width), bf16),
        ],
        [
            pltpu.VMEM((2, rows, width), bf16),
            pltpu.VMEM((2, rows, width), bf16),
            pltpu.VMEM((rows, width), bf16),
            pltpu.VMEM((rows, width), bf16),
            pltpu.VMEM((rows, width), bf16),
        ],
        48,
        ([False, True, True, True], [True, True, False, False]),
    )


def norm_back_rows(values, factor, gain, grad_normed):
    gained = gain * grad_normed
    inner = jnp.mean(gained * values, axis=-1, keepdims=True)
    grad_values = factor * gained - values * (factor * factor * factor) * inner
    return grad_values, jnp.sum(grad_normed * values * factor, axis=0, keepdims=True)


def middle_back_kernel(
    part, mid_ref, factor_ref, gain_ref, dy_ref, dmid_ref, dgain_ref, out, low, *rest
):
    first, wires, to = rest[:7], Wires(*rest[7:]), partners()
    meet([to[k] for k in ("core", "y", "z")])
    grad_normed = result_of(scatter_pair(wires, to, part, *first))
    du, dgain = norm_back_rows(mid_ref[...], factor_ref[...], gain_ref[...], grad_normed)
    dgain_ref[...] = dgain
    dmid = wide(dy_ref[...]) + du
    low[...] = dmid.astype(bf16)
    share = gather_rank(wires, to, low, out)
    next(share)
    dmid_ref[...] = dmid
    result_of(share)
    wires.finish()


def pair_scratch(rows, width):
    return [
        pltpu.VMEM((4, rows, width), bf16),
        pltpu.VMEM((4, rows, width), bf16),
        pltpu.VMEM((3, rows, width), bf16),
        pltpu.VMEM((rows, width), bf16),
        pltpu.VMEM((rows, width), bf16),
        pltpu.VMEM((rows // 2, width), bf16),
        pltpu.VMEM((rows // 2, width), bf16),
    ]


def middle_back(part, middle, factor, gain, dy_part):
    rows, width = middle.shape
    return remote_call(
        middle_back_kernel,
        "middle_back",
        3,
        [part.reshape(8, rows, width), middle, factor, gain, dy_part],
        [
            jax.ShapeDtypeStruct((rows, width), f32),
            jax.ShapeDtypeStruct((1, width), f32),
            jax.ShapeDtypeStruct((4, rows, width), bf16),
        ],
        [pltpu.VMEM((rows, width), bf16)] + pair_scratch(rows, width),
        16,
        ([False, True, True, True, True], [True, True, False]),
    )


def add_all(wires, ways, value, slots):
    for k, device in enumerate(ways):
        one = wires.copy(value, slots.at[k], device)
        one.wait()
        wires.started = [x for x in wires.started if x is not one]
        value[...] = value[...] + slots[k]


def input_back_kernel(
    part, x_ref, factor_ref, gain_ref, dmid_ref, small_ref, sum_ref, out, *rest
):
    low, own, core, sent, got, slots = rest[:-3]
    wires, to = Wires(*rest[-3:]), partners()
    meet([to[k] for k in ("core", "y")])
    grad_normed = result_of(scatter_rank(wires, to, part, own, core, sent, got))
    du, dgain = norm_back_rows(wide(x_ref[...]), factor_ref[...], gain_ref[...], grad_normed)
    low[...] = (dmid_ref[...] + du).astype(bf16)
    share = gather_rank(wires, to, low, out)
    next(share)
    width = dgain.shape[1]
    sum_ref[:, width:] = small_ref[:, width:]
    sum_ref[:, :width] = dgain
    add_all(wires, [to["core"], to["y"]], sum_ref, slots)
    result_of(share)
    wires.finish()


def input_back(part, inputs_part, factor, gain, grad_middle, small):
    rows, width = inputs_part.shape
    return remote_call(
        input_back_kernel,
        "input_back",
        5,
        [part.reshape(4, rows, width), inputs_part, factor, gain, grad_middle, small],
        [
            jax.ShapeDtypeStruct(small.shape, f32),
            jax.ShapeDtypeStruct((4, rows, width), bf16),
        ],
        [
            pltpu.VMEM((rows, width), bf16),
            pltpu.VMEM((2, rows, width), bf16),
            pltpu.VMEM((2, rows, width), bf16),
            pltpu.VMEM((rows, width), bf16),
            pltpu.VMEM((rows, width), bf16),
            pltpu.VMEM((2,) + small.shape, f32),
        ],
        16,
        ([False, True, True, True, True, True], [True, False]),
    )


def context_sum_kernel(over_f, *refs):
    parts, small_ref, out_part, mid_ref = refs[:3], refs[3], refs[4], refs[5]
    outs, sum_ref, shared, outputs = refs[6:8], refs[8], refs[9], refs[10]
    lows, from_end, from_middle = refs[11:15], refs[15:19], refs[19:23]
    out_low, slot, scratch = refs[23], refs[24], refs[25:32]
    wires, to, c = Wires(*refs[32:]), partners(), lax.axis_index("context")
    end = (c == 0) | (c == lax.axis_size("context") - 1)
    inner = jnp.logical_not(end)
    greet = ["core", "y", "z", "last"]
    if over_f:
        to["f"] = {"fsdp": 1 - lax.axis_index("fsdp")}
        greet.append("f")
    meet([to[k] for k in greet])
    ahead = scatter_pair(wires, to, out_part, *scratch)
    next(ahead)
    sum_ref[...] = small_ref[...]
    from_f = wires.copy(small_ref, slot, to["f"]) if over_f else None
    next(ahead)
    sources = [*parts, sum_ref]
    chunks = []
    for i, cuts in ((2, 1), (0, 2), (1, 2), (3, 1)):
        size = sources[i].shape[0] // cuts
        chunks += [(i, pl.ds(k * size, size)) for k in range(cuts)]
    inward = [wires.plan(sources[i].at[at], from_end[i].at[at], to["z"]) for i, at in chunks]
    across = [wires.plan(lows[i].at[at], from_middle[i].at[at], to["last"]) for i, at in chunks]
    outward = [wires.plan(lows[i].at[at], lows[i].at[at], to["z"]) for i, at in chunks]
    small = len(chunks) - 1

    def send_in(k):
        @pl.when(end)
        def _():
            inward[k].start()

    for k in range(small):
        send_in(k)
    next(ahead)
    if over_f:
        from_f.wait_recv()
        sum_ref[...] = sum_ref[...] + slot[...]
    send_in(small)
    out_low[...] = (mid_ref[...] + result_of(ahead)).astype(bf16)
    out_share = gather_rank(wires, to, out_low, outputs)
    next(out_share)

    @pl.when(inner)
    def _():
        def send_out(k):
            i, at = chunks[k]
            across[k].wait()
            lows[i][at] = (wide(lows[i][at]) + wide(from_middle[i][at])).astype(lows[i].dtype)
            outward[k].start()

        for k, (i, at) in enumerate(chunks):
            inward[k].wait_recv()
            total = wide(sources[i][at]) + wide(from_end[i][at])
            lows[i][at] = total.astype(lows[i].dtype)
            across[k].start()
            if k:
                send_out(k - 1)
        send_out(small)

    result_of(out_share)

    def arrived(k):
        @pl.when(end)
        def _():
            outward[k].wait_recv()

    arrived(0)
    share = gather_rank(wires, to, lows[2], shared)
    next(share)
    for k in range(1, len(chunks)):
        arrived(k)

    @pl.when(end)
    def _():
        for one in inward:
            one.wait_send()

    for i in (0, 1):
        outs[i][...] = wide(lows[i][...])
    sum_ref[...] = lows[3][...]
    result_of(share)

    @pl.when(inner)
    def _():
        for one in outward:
            one.wait_send()

    wires.finish()


def context_sum(over_f, parts, small, out_part, middle):
    rows, width = middle.shape
    lines = [pltpu.VMEM(x.shape, x.dtype) for x in (*parts, small)]
    return remote_call(
        functools.partial(context_sum_kernel, over_f),
        "context_sum",
        6,
        [*parts, small, out_part.reshape(8, rows, width), middle],
        [jax.ShapeDtypeStruct(x.shape, f32) for x in parts[:2]]
        + [jax.ShapeDtypeStruct(small.shape, f32)]
        + [jax.ShapeDtypeStruct((4,) + parts[2].shape, bf16)]
        + [jax.ShapeDtypeStruct((4, rows, width), bf16)],
        lines * 3
        + [pltpu.VMEM((rows, width), bf16), pltpu.VMEM(small.shape, f32)]
        + pair_scratch(rows, width),
        48,
        ([True] * 4 + [False, True], [True] * 3 + [False] * 2),
    )


def build(n_f, n_c, n_t):
    def flip(x, axis, bit):
        size = {"fsdp": n_f, "context": n_c, "tensor": n_t}[axis]
        return lax.ppermute(x, axis, [(i, i ^ bit) for i in range(size)])

    def by_bit(bit, x, other, axis):
        return jnp.where(
            bit == 0,
            jnp.concatenate([x, other], axis=axis),
            jnp.concatenate([other, x], axis=axis),
        )

    def after(x, *others):
        return lax.optimization_barrier((x, others))[0]

    def local(
        inputs,
        cotangent,
        blocks,
        attn_gain,
        w_query,
        b_query,
        w_key,
        b_key,
        w_value,
        b_value,
        w_out,
        ffn_gain,
        w_gate,
        w_up,
        w_down,
    ):
        rows, width = inputs.shape
        f = lax.axis_index("fsdp")
        c = lax.axis_index("context")
        t = lax.axis_index("tensor")
        core, parity, pair = t % 2, c % 2, c // 2
        heads = w_query.shape[1] // HD
        group = (t * heads) // (H // KV)
        part = rows // n_t
        units_all = w_gate.shape[1]
        units = units_all // 2

        def gather_f(x, axis):
            if n_f == 2:
                return by_bit(f, x, flip(x, "fsdp", 1), axis)
            return lax.all_gather(x, "fsdp", axis=axis, tiled=True)

        def grad_far(left, right, side):
            if n_f > 2:
                return None
            source = (left, right)[side]
            half = width // 2
            far = lax.dynamic_slice_in_dim(source, (1 - f) * half, half, 1)
            return (dot_rows(far, right) if side == 0 else dot_rows(left, far)).astype(bf16)

        def grad_sum(left, right, side, far):
            if n_f > 2:
                return lax.psum_scatter(
                    dot_rows(left, right).astype(bf16), "fsdp", scatter_dimension=side, tiled=True
                )
            source = (left, right)[side]
            half = width // 2
            own = lax.dynamic_slice_in_dim(source, f * half, half, 1)
            own = dot_rows(own, right) if side == 0 else dot_rows(left, own)
            return (own + flip(far, "fsdp", 1).astype(f32)).astype(bf16)

        small = jnp.concatenate(
            [v.reshape(1, -1) for v in (attn_gain, ffn_gain, b_query, b_key, b_value)], axis=1
        )
        column = lambda w: lax.dynamic_slice_in_dim(w, group * HD, HD, 1)
        w_kv_own = jnp.where(core == 0, column(w_key), column(w_value))
        pieces_f = lambda x, axis: (
            [x, flip(x, "fsdp", 1)]
            if n_f == 2
            else [lax.all_gather(x, "fsdp", axis=axis, tiled=True)]
        )
        meta = jnp.stack([f, 1 - f, core, pair]).astype(jnp.int32)
        w_q = pieces_f(w_query, 0)
        w_kv = pieces_f(w_kv_own, 0)
        small = gather_f(small, 0)
        w_out_all = gather_f(after(w_out, small), 1)
        piece = attn_gain.shape[0]
        gain_first = small[:, :piece].reshape(1, width).astype(f32)
        gain_second = small[:, piece : 2 * piece].reshape(1, width).astype(f32)
        bias_of = lambda lo, n: (
            small[:, lo : lo + n * (HD // n_f)]
            .reshape(n_f, n, HD // n_f)
            .transpose(1, 0, 2)
            .reshape(n, HD)
            .astype(f32)
        )
        at = 2 * piece
        bq = bias_of(at, heads)
        bk = bias_of(at + heads * (HD // n_f), KV)
        bv = bias_of(at + (heads + KV) * (HD // n_f), KV)
        b_kv = lax.dynamic_index_in_dim(jnp.where(core == 0, bk, bv), group, 0)

        unit_slice = lambda w: lax.dynamic_slice_in_dim(w, parity * units, units, 0)
        own_units = jnp.concatenate([unit_slice(w) for w in (w_gate.T, w_up.T, w_down)], axis=0)

        dy_part = lax.dynamic_slice_in_dim(cotangent, t * part, part, 0)

        seq_blocks = blocks[0].reshape(n_c, -1)
        own_blocks = seq_blocks.shape[1]
        key_blocks = jnp.concatenate(
            [lax.dynamic_index_in_dim(seq_blocks, c ^ j, 0, keepdims=False) for j in range(n_c)]
        )
        positions = (
            key_blocks[:own_blocks, None] * BLOCK + jnp.arange(BLOCK, dtype=jnp.int32)[None, :]
        ).reshape(-1)
        cosine, sine = rope_tables(positions)
        bias = jnp.concatenate([bq.reshape(1, -1), b_kv], axis=1)
        normed, factor_first, queries, kv_own = qkv(
            meta, inputs, gain_first, bias, cosine, sine, w_q, w_kv
        )
        w_units = pieces_f(after(own_units, kv_own, w_out_all), 1)
        kv = kv_gather(after(kv_own, w_out_all))
        attended, lse = attention(key_blocks, queries, kv)
        inputs_part = lax.dynamic_slice_in_dim(inputs, t * part, part, 0)
        middle, factor_second, normed2, dy_all = middle_norm(
            dot(attended, w_out_all).astype(bf16), inputs_part, gain_second, dy_part
        )

        hidden, grad_gate, grad_up, dx_part, out_part, *unit_far = ffn(
            meta, normed2, dy_all, w_units
        )
        if n_f == 2:
            down_got, gate_got, up_got = (flip(x, "fsdp", 1) for x in unit_far)
        else:
            over_f = lambda x: lax.psum_scatter(x, "fsdp", scatter_dimension=1, tiled=True)
            down_own = over_f(unit_grads(meta, 0, 1, dy_all, [hidden]))
            gate_up_own = over_f(unit_grads(meta, 0, 1, normed2, [grad_gate, grad_up]))
            down_got = gate_got = up_got = jnp.zeros_like(down_own)

        def unit_done(own, got):
            low = (own.astype(f32) + got.astype(f32)).astype(bf16)
            return low, flip(low, "context", 1)

        unit_whole = lambda low, other: by_bit(parity, low, other, 0).astype(f32)

        grad_middle, ffn_gain_grad, grad_middle_low = middle_back(
            dx_part, middle, factor_second, gain_second, dy_part
        )
        grad_middle_low = grad_middle_low.reshape(rows, width)
        if n_f == 2:
            down_own = unit_grads(meta, 0, 2, *after((dy_all, [hidden]), grad_middle_low))
        down_done = unit_done(down_own, after(down_got, grad_middle_low))
        grad_attended = dot_cols(after(grad_middle_low, down_done[0]), w_out_all).astype(bf16)

        dq_low, dkv = attention_back(key_blocks, queries, grad_attended, lse, cosine, sine, kv)
        if n_f == 2:
            gate_up_own = unit_grads(meta, 0, 2, *after((normed2, [grad_gate, grad_up]), dkv))
            dkv = after(dkv, gate_up_own)
        dkv = kv_scatter(after(dkv, down_done))
        gate_done = unit_done(gate_up_own[:units], after(gate_got, dkv))
        up_done = unit_done(gate_up_own[units:], after(up_got, gate_done[0]))
        dkv = after(dkv, gate_done[0], up_done[0])
        dkv_low = jnp.where(core == 0, rotate_back(dkv, cosine, sine), dkv).astype(bf16)
        attention_args = (
            (attended, after(grad_middle_low, dkv), 1),
            (normed, after(dq_low, dkv), 0),
            (normed, dkv_low, 0),
        )
        fars = [grad_far(*args) for args in attention_args]
        dkv_low = after(dkv_low, fars)
        factor_part = lax.dynamic_slice_in_dim(factor_first, t * part, part, 0)
        own_biases = jnp.sum(
            jnp.concatenate([dq_low, dkv_low], axis=1).astype(f32), axis=0, keepdims=True
        )
        slots = lax.dynamic_update_slice(
            jnp.zeros((n_t, (heads + 1) * HD), f32), own_biases, (t, 0)
        )
        small_grads = jnp.concatenate(
            [jnp.zeros((1, width), f32), ffn_gain_grad, slots.reshape(1, -1)], axis=1
        )
        small_grads, input_grad = input_back(
            qkv_back(meta, dq_low, dkv_low, w_q, w_kv),
            inputs_part,
            factor_part,
            gain_first,
            grad_middle,
            small_grads,
        )
        input_grad = input_grad.reshape(rows, width)
        if n_f > 2:
            small_grads = lax.psum(small_grads, "fsdp")
        attention_parts = [grad_sum(*args, far) for args, far in zip(attention_args, fars)]
        wd_grad = unit_whole(*after(down_done, small_grads))
        wg_grad = unit_whole(*after(gate_done, small_grads))
        small_grads, up_done, wg_grad, wd_grad = lax.optimization_barrier(
            (small_grads, up_done, wg_grad, wd_grad)
        )
        wo_grad, wq_grad, packed, wkv_all, outputs = context_sum(
            n_f == 2, attention_parts, small_grads, out_part, middle
        )
        outputs = outputs.reshape(rows, width)
        wkv_all = wkv_all.astype(f32)
        wk_grad = jnp.concatenate([wkv_all[0], wkv_all[2]], axis=1)
        wv_grad = jnp.concatenate([wkv_all[1], wkv_all[3]], axis=1)
        packed = packed[0]
        attn_gain_grad = lax.dynamic_slice_in_dim(packed, f * piece, piece, 0)
        ffn_gain_grad = lax.dynamic_slice_in_dim(packed, width + f * piece, piece, 0)
        slots = packed[2 * width :].reshape(n_t, heads + 1, HD)
        slots = lax.dynamic_slice_in_dim(slots, f * (HD // n_f), HD // n_f, 2)
        bq_out = lax.dynamic_index_in_dim(slots, t, 0, keepdims=False)[:heads]
        bk_out = slots[0::2, heads]
        bv_out = slots[1::2, heads]

        wu_grad = unit_whole(*up_done)
        wg_grad, wu_grad = wg_grad.T, wu_grad.T

        return (
            outputs,
            input_grad,
            attn_gain_grad,
            wq_grad,
            bq_out,
            wk_grad,
            bk_out,
            wv_grad,
            bv_out,
            wo_grad,
            ffn_gain_grad,
            wg_grad,
            wu_grad,
            wd_grad,
        )

    return local


def solution(mesh):
    in_specs = (
        P(("fsdp", "context"), None),
        P(("fsdp", "context"), None),
        P("fsdp", None),
        P("fsdp"),
        P("fsdp", "tensor"),
        P("tensor", "fsdp"),
        P("fsdp", None),
        P(None, "fsdp"),
        P("fsdp", None),
        P(None, "fsdp"),
        P("tensor", "fsdp"),
        P("fsdp"),
        P("fsdp", "tensor"),
        P("fsdp", "tensor"),
        P("tensor", "fsdp"),
    )
    out_specs = (
        P(("fsdp", "context"), None),
        P(("fsdp", "context"), None),
        P("fsdp"),
        P("fsdp", "tensor"),
        P("tensor", "fsdp"),
        P("fsdp", None),
        P(None, "fsdp"),
        P("fsdp", None),
        P(None, "fsdp"),
        P("tensor", "fsdp"),
        P("fsdp"),
        P("fsdp", "tensor"),
        P("fsdp", "tensor"),
        P("tensor", "fsdp"),
    )
    local = build(mesh.shape["fsdp"], mesh.shape["context"], mesh.shape["tensor"])
    return jax.shard_map(local, mesh=mesh, in_specs=in_specs, out_specs=out_specs, check_vma=False)
```

```python
import functools

import jax
import jax.numpy as jnp
from jax import lax
from jax.experimental import pallas as pl
from jax.experimental.pallas import tpu as pltpu
from jax.sharding import PartitionSpec as P

H = 12
KV = 2
HD = 128
BLOCK = 256

EPSILON = 1e-06
ROPE_BASE = 1000000.0
MASKED = -1e30
SCALING = HD ** (-0.5)
LANES = 128
VMEM_LIMIT = 60 << 20

f32 = jnp.float32
bf16 = jnp.bfloat16


def rope_tables(positions):
    halfway = HD // 2
    frequency = ROPE_BASE ** (-(jnp.arange(halfway, dtype=f32) * 2.0 / HD))
    angles = positions.astype(f32)[:, None] * frequency[None, :]
    cosine, sine = jnp.cos(angles), jnp.sin(angles)
    return (jnp.concatenate([cosine, cosine], axis=1), jnp.concatenate([sine, sine], axis=1))


def rotate(field, cosine, sine):
    halfway = HD // 2
    turned = jnp.concatenate([-field[..., halfway:], field[..., :halfway]], axis=-1)
    return field * cosine + turned * sine


def rotate_back(grad_field, cosine, sine):
    halfway = HD // 2
    moved = grad_field * sine
    turned = jnp.concatenate([moved[..., halfway:], -moved[..., :halfway]], axis=-1)
    return grad_field * cosine + turned


def dot(left, right):
    return jnp.dot(left, right, preferred_element_type=f32)


def dot_rows(left, right):
    return lax.dot_general(left, right, (((0,), (0,)), ((), ())), preferred_element_type=f32)


def dot_cols(left, right):
    return lax.dot_general(left, right, (((1,), (1,)), ((), ())), preferred_element_type=f32)


def mask_row(kb_ref, own_block, key_blocks):
    return jnp.concatenate(
        [
            jnp.full((1, BLOCK), jnp.where(kb_ref[j] <= own_block, 0.0, MASKED), f32)
            for j in range(key_blocks)
        ],
        axis=1,
    )


def attention_kernel(key_blocks, kb_ref, q_ref, k_ref, v_ref, o_ref, lse_ref):
    bias = mask_row(kb_ref, kb_ref[pl.program_id(1)], key_blocks)
    scores = dot_cols(q_ref[...], k_ref[...]) * SCALING + bias
    row_max = jnp.max(scores, axis=1, keepdims=True)
    expo = jnp.exp(scores - row_max)
    total = jnp.sum(expo, axis=1, keepdims=True)
    probability = (expo * (1.0 / total)).astype(bf16)
    o_ref[...] = dot(probability, v_ref[...]).astype(bf16)
    lse_ref[0] = row_max + jnp.log(total)


def attention(key_blocks, queries, kv):
    rows, width = queries.shape
    heads = width // HD
    whole = lambda kind: pl.BlockSpec((None,) + kv.shape[1:], lambda h, i, kb: (kind, 0, 0))
    tile = pl.BlockSpec((BLOCK, HD), lambda h, i, kb: (i, h))
    return pl.pallas_call(
        functools.partial(attention_kernel, kv.shape[1] // BLOCK),
        name="attention",
        grid_spec=pltpu.PrefetchScalarGridSpec(
            num_scalar_prefetch=1,
            grid=(heads, rows // BLOCK),
            in_specs=[tile, whole(0), whole(1)],
            out_specs=[tile, pl.BlockSpec((1, BLOCK, 1), lambda h, i, kb: (h, i, 0))],
        ),
        out_shape=[
            jax.ShapeDtypeStruct((rows, width), bf16),
            jax.ShapeDtypeStruct((heads, rows, 1), f32),
        ],
        compiler_params=pltpu.CompilerParams(vmem_limit_bytes=VMEM_LIMIT),
    )(key_blocks, queries, kv, kv)


def attention_back_kernel(
    key_blocks,
    kb_ref,
    q_ref,
    do_ref,
    lse_ref,
    cos_ref,
    sin_ref,
    k_ref,
    v_ref,
    dq_ref,
    dkv_ref,
    dk_ref,
    dv_ref,
):
    head, i = pl.program_id(0), pl.program_id(1)

    @pl.when((head == 0) & (i == 0))
    def _():
        dk_ref[...] = jnp.zeros_like(dk_ref)
        dv_ref[...] = jnp.zeros_like(dv_ref)

    bias = mask_row(kb_ref, kb_ref[i], key_blocks)
    scores = dot_cols(q_ref[...], k_ref[...]) * SCALING + bias
    probability = jnp.exp(scores - lse_ref[0])
    grad_probs = dot_cols(do_ref[...], v_ref[...])
    inner = jnp.sum(probability * grad_probs, axis=1, keepdims=True)
    grad_scores = (probability * (grad_probs - inner)).astype(bf16)
    grad_query = dot(grad_scores, k_ref[...]) * SCALING
    moved = grad_query * sin_ref[...]
    sign = jnp.where(lax.broadcasted_iota(jnp.int32, moved.shape, 1) < HD // 2, 1.0, -1.0)
    dq_ref[...] = (
        grad_query * cos_ref[...] + pltpu.roll(moved, HD // 2, 1) * sign
    ).astype(bf16)
    dk_ref[...] += dot_rows(grad_scores, q_ref[...]) * SCALING
    dv_ref[...] += dot_rows(probability.astype(bf16), do_ref[...])

    @pl.when((head == pl.num_programs(0) - 1) & (i == pl.num_programs(1) - 1))
    def _():
        dkv_ref[0] = dk_ref[...].astype(bf16)
        dkv_ref[1] = dv_ref[...].astype(bf16)


def attention_back(key_blocks, queries, grad_out, lse, cosine, sine, kv):
    rows, width = queries.shape
    heads = width // HD
    whole = lambda kind: pl.BlockSpec((None,) + kv.shape[1:], lambda h, i, kb: (kind, 0, 0))
    tile = pl.BlockSpec((BLOCK, HD), lambda h, i, kb: (i, h))
    table = pl.BlockSpec((BLOCK, HD), lambda h, i, kb: (i, 0))
    return pl.pallas_call(
        functools.partial(attention_back_kernel, kv.shape[1] // BLOCK),
        name="attention_back",
        grid_spec=pltpu.PrefetchScalarGridSpec(
            num_scalar_prefetch=1,
            grid=(heads, rows // BLOCK),
            in_specs=[
                tile,
                tile,
                pl.BlockSpec((1, BLOCK, 1), lambda h, i, kb: (h, i, 0)),
                table,
                table,
                whole(0),
                whole(1),
            ],
            out_specs=[tile, pl.BlockSpec(kv.shape, lambda h, i, kb: (0, 0, 0))],
            scratch_shapes=[pltpu.VMEM(kv.shape[1:], f32)] * 2,
        ),
        out_shape=[
            jax.ShapeDtypeStruct((rows, width), bf16),
            jax.ShapeDtypeStruct(kv.shape, bf16),
        ],
        compiler_params=pltpu.CompilerParams(vmem_limit_bytes=VMEM_LIMIT),
    )(key_blocks, queries, grad_out, lse, cosine, sine, kv, kv)


def qkv_kernel(pieces, meta_ref, x_ref, gain_ref, bias_ref, cos_ref, sin_ref, *refs):
    weights, (xn_ref, factor_ref, q_ref, kv_ref) = refs[: 2 * pieces], refs[2 * pieces :]
    values = x_ref[...].astype(f32)
    factor = lax.rsqrt(jnp.mean(values * values, axis=-1, keepdims=True) + EPSILON)
    factor_ref[...] = factor
    xn_ref[...] = (values * factor * gain_ref[...]).astype(bf16)
    depth = weights[0].shape[0]
    normed = [xn_ref[:, columns_of(meta_ref, j, depth, pieces)] for j in range(pieces)]
    cosine, sine = cos_ref[...], sin_ref[...]
    sign = jnp.where(lax.broadcasted_iota(jnp.int32, cosine.shape, 1) < HD // 2, -1.0, 1.0)
    sine = sine * sign
    width = q_ref.shape[1]
    total = bias_ref[:, :width] + sum(dot(x, w[...]) for x, w in zip(normed, weights[:pieces]))
    turn = lambda own: own * cosine + pltpu.roll(own, HD // 2, 1) * sine
    for h in range(width // HD):
        q_ref[:, h * HD : (h + 1) * HD] = turn(total[:, h * HD : (h + 1) * HD]).astype(bf16)
    own = bias_ref[:, width:] + sum(dot(x, w[...]) for x, w in zip(normed, weights[pieces:]))
    kv_ref[...] = jnp.where(meta_ref[2] == 0, turn(own), own).astype(bf16)


def columns_of(meta_ref, j, depth, pieces):
    if pieces == 1:
        return slice(None)
    return pl.ds(pl.multiple_of(meta_ref[j] * depth, LANES), depth)


def qkv(meta, inputs, gain, bias, cosine, sine, w_q, w_kv):
    rows, width = inputs.shape
    out = w_q[0].shape[1]
    tile = 256
    row = lambda n: pl.BlockSpec((tile, n), lambda i, m: (i, 0))
    fixed = lambda w: pl.BlockSpec(w.shape, lambda i, m: (0, 0))
    return pl.pallas_call(
        functools.partial(qkv_kernel, len(w_q)),
        name="qkv",
        grid_spec=pltpu.PrefetchScalarGridSpec(
            num_scalar_prefetch=1,
            grid=(rows // tile,),
            in_specs=[row(width), fixed(gain), fixed(bias), row(HD), row(HD)]
            + [fixed(w) for w in (*w_q, *w_kv)],
            out_specs=[row(width), row(1), row(out), row(HD)],
        ),
        out_shape=[
            jax.ShapeDtypeStruct((rows, width), bf16),
            jax.ShapeDtypeStruct((rows, 1), f32),
            jax.ShapeDtypeStruct((rows, out), bf16),
            jax.ShapeDtypeStruct((rows, HD), bf16),
        ],
        compiler_params=pltpu.CompilerParams(vmem_limit_bytes=VMEM_LIMIT),
    )(meta, inputs, gain, bias, cosine, sine, *w_q, *w_kv)


def qkv_back_kernel(pieces, meta_ref, dq_ref, dkv_ref, *refs):
    w_q, w_kv, out_ref = refs[:pieces], refs[pieces : 2 * pieces], refs[-1]
    for j in range(pieces):
        out_ref[:, columns_of(meta_ref, j, w_q[j].shape[0], pieces)] = (
            dot_cols(dq_ref[...], w_q[j][...]) + dot_cols(dkv_ref[...], w_kv[j][...])
        ).astype(bf16)


def qkv_back(meta, grad_q, grad_kv, w_q, w_kv):
    rows, width = grad_q.shape[0], sum(w.shape[0] for w in w_q)
    tile = 256
    row = lambda n: pl.BlockSpec((tile, n), lambda i, m: (i, 0))
    fixed = lambda w: pl.BlockSpec(w.shape, lambda i, m: (0, 0))
    return pl.pallas_call(
        functools.partial(qkv_back_kernel, len(w_q)),
        name="qkv_back",
        grid_spec=pltpu.PrefetchScalarGridSpec(
            num_scalar_prefetch=1,
            grid=(rows // tile,),
            in_specs=[row(grad_q.shape[1]), row(HD)] + [fixed(w) for w in (*w_q, *w_kv)],
            out_specs=row(width),
        ),
        out_shape=jax.ShapeDtypeStruct((rows, width), bf16),
        compiler_params=pltpu.CompilerParams(vmem_limit_bytes=VMEM_LIMIT),
    )(meta, grad_q, grad_kv, *w_q, *w_kv)


def add_rows(unit_refs, row_refs, columns, totals, outs):
    step = pl.program_id(0)

    @pl.when(step == 0)
    def _():
        for total in totals:
            total[...] = jnp.zeros_like(total)

    for total, unit, row in zip(totals, unit_refs, row_refs):
        total[...] += dot_rows(unit[...], row[:, columns])

    @pl.when(step == pl.num_programs(0) - 1)
    def _():
        for out, total in zip(outs, totals):
            out[...] = total[...].astype(bf16)


def hidden_kernel(pieces, meta_ref, x_ref, dy_ref, *refs):
    wg, wu, refs = refs[:pieces], refs[pieces : 2 * pieces], refs[2 * pieces :]
    hid_ref, slope_ref, gated_ref = refs[:3]
    columns = [columns_of(meta_ref, j, wg[j].shape[1], pieces) for j in range(pieces)]
    gate = sum(dot_cols(x_ref[:, at], w[...]) for at, w in zip(columns, wg))
    up = sum(dot_cols(x_ref[:, at], w[...]) for at, w in zip(columns, wu))
    sigma = 1.0 / (1.0 + jnp.exp(-gate))
    gated = gate * sigma
    hid_ref[...] = (gated * up).astype(bf16)
    slope_ref[...] = (up * (sigma + gated * (1.0 - sigma))).astype(bf16)
    gated_ref[...] = gated.astype(bf16)
    if pieces == 2:
        add_rows([hid_ref], [dy_ref], columns[1], refs[4:], refs[3:4])


def hidden_back_kernel(pieces, meta_ref, x_ref, dy_ref, hid_ref, slope_ref, gated_ref, *refs):
    wg, wu, wd = (refs[m * pieces : (m + 1) * pieces] for m in range(3))
    refs = refs[3 * pieces :]
    dg_ref, du_ref, dx_ref, out_ref = refs[:4]
    columns = [columns_of(meta_ref, j, wg[j].shape[1], pieces) for j in range(pieces)]
    grad_hidden = sum(dot_cols(dy_ref[:, at], w[...]) for at, w in zip(columns, wd))
    dg_ref[...] = (grad_hidden * slope_ref[...].astype(f32)).astype(bf16)
    du_ref[...] = (grad_hidden * gated_ref[...].astype(f32)).astype(bf16)

    @pl.when(pl.program_id(0) // (pl.num_programs(0) // 2) == meta_ref[3])
    def _():
        for at, g, u, d in zip(columns, wg, wu, wd):
            dx_ref[:, at] = (dot(dg_ref[...], g[...]) + dot(du_ref[...], u[...])).astype(bf16)
            out_ref[:, at] = dot(hid_ref[...], d[...]).astype(bf16)

    if pieces == 2:
        add_rows([dg_ref, du_ref], [x_ref, x_ref], columns[1], refs[6:], refs[4:6])


def hidden_specs(meta, normed, weights):
    width = normed.shape[-1]
    rows = normed.shape[0] * normed.shape[1]
    units, depth = weights[0].shape[0] // 3, weights[0].shape[1]
    tile = 512
    steps = rows // tile
    half = steps // 2
    once = pl.Buffered(1)
    inside = lambda i, m: jnp.clip(i - m[3] * half, 0, half - 1)
    return {
        "steps": steps,
        "flat": lambda x: x.reshape(-1, width),
        "row": pl.BlockSpec((tile, width), lambda i, m: (lax.rem(i + m[3] * half, steps), 0)),
        "unit": pl.BlockSpec((tile, units), lambda i, m: (i, 0)),
        "near_unit": pl.BlockSpec((tile, units), lambda i, m: (inside(i, m) + m[3] * half, 0)),
        "near_row": pl.BlockSpec((tile, width), lambda i, m: (inside(i, m), 0)),
        "weight": lambda k: pl.BlockSpec((units, depth), lambda i, m: (k, 0), pipeline_mode=once),
        "grad": pl.BlockSpec((units, depth), lambda i, m: (0, 0), pipeline_mode=once),
        "unit_shape": jax.ShapeDtypeStruct((rows, units), bf16),
        "near_shape": jax.ShapeDtypeStruct((rows // 2, width), bf16),
        "grad_shape": jax.ShapeDtypeStruct((units, depth), bf16),
        "total": pltpu.VMEM((units, depth), f32),
    }


def hidden_call(kernel, name, meta, args, in_specs, outs, grads, specs):
    return pl.pallas_call(
        kernel,
        name=name,
        grid_spec=pltpu.PrefetchScalarGridSpec(
            num_scalar_prefetch=1,
            grid=(specs["steps"],),
            in_specs=in_specs,
            out_specs=[specs[x] for x in outs] + [specs["grad"]] * grads,
            scratch_shapes=[specs["total"]] * grads,
        ),
        out_shape=[specs[x.split("_")[0] + "_shape"] for x in outs]
        + [specs["grad_shape"]] * grads,
        compiler_params=pltpu.CompilerParams(vmem_limit_bytes=VMEM_LIMIT),
    )(meta, *args)


def hidden_units(meta, normed, grad_out, weights):
    specs, pieces = hidden_specs(meta, normed, weights), len(weights)
    return hidden_call(
        functools.partial(hidden_kernel, pieces),
        "hidden_units",
        meta,
        [specs["flat"](normed), specs["flat"](grad_out)] + list(weights) * 2,
        [specs["row"]] * 2 + [specs["weight"](k) for k in range(2) for _ in weights],
        ["unit"] * 3,
        pieces == 2,
        specs,
    )


def hidden_back(meta, normed, grad_out, hidden, slope, gated, weights):
    specs, pieces = hidden_specs(meta, normed, weights), len(weights)
    return hidden_call(
        functools.partial(hidden_back_kernel, pieces),
        "hidden_back",
        meta,
        [specs["flat"](normed), specs["flat"](grad_out), hidden, slope, gated]
        + list(weights) * 3,
        [specs["row"]] * 2
        + [specs["near_unit"], specs["unit"], specs["unit"]]
        + [specs["weight"](k) for k in range(3) for _ in weights],
        ["unit", "unit", "near_row", "near_row"],
        2 * (pieces == 2),
        specs,
    )


def unit_grads_kernel(count, meta_ref, near_ref, far_ref, *refs):
    units, out_ref, x_ref = refs[:count], refs[-2], refs[-1]
    half = near_ref.shape[0]
    x_ref[pl.ds(pl.multiple_of(meta_ref[3] * half, half), half)] = near_ref[...]
    x_ref[pl.ds(pl.multiple_of((1 - meta_ref[3]) * half, half), half)] = far_ref[...]
    for k, unit in enumerate(units):
        depth = unit.shape[1]
        out_ref[k * depth : (k + 1) * depth] = dot_rows(unit[...], x_ref[...]).astype(bf16)


def unit_grads(meta, which, pieces, x, units_of):
    width = x.shape[-1]
    count, (rows, units) = len(units_of), units_of[0].shape
    depth = width // pieces
    tile = 256
    steps = depth // tile
    shard = (lambda m: m[which]) if pieces > 1 else (lambda m: 0)
    feature = lambda half: pl.BlockSpec(
        (rows // 2, tile), lambda i, m: (half, shard(m) * steps + i)
    )
    unit = pl.BlockSpec((rows, units), lambda i, m: (0, 0), pipeline_mode=pl.Buffered(1))
    x = x.reshape(-1, width)
    return pl.pallas_call(
        functools.partial(unit_grads_kernel, count),
        name=f"unit_grads_{which}_{count}",
        grid_spec=pltpu.PrefetchScalarGridSpec(
            num_scalar_prefetch=1,
            grid=(steps,),
            in_specs=[feature(0), feature(1)] + [unit] * count,
            out_specs=pl.BlockSpec((count * units, tile), lambda i, m: (0, i)),
            scratch_shapes=[pltpu.VMEM((rows, tile), bf16)],
        ),
        out_shape=jax.ShapeDtypeStruct((count * units, depth), bf16),
        compiler_params=pltpu.CompilerParams(vmem_limit_bytes=VMEM_LIMIT),
    )(meta, x, x, *units_of)


class Wires:
    def __init__(self, sends, receives, locals_):
        self.sends, self.receives, self.locals = sends, receives, locals_
        self.used = self.used_local = 0
        self.started = []

    def plan(self, source, target, device):
        k = self.used
        self.used += 1
        return pltpu.make_async_remote_copy(
            source,
            target,
            self.sends.at[k],
            self.receives.at[k],
            device_id=device,
            device_id_type=pl.DeviceIdType.MESH,
        )

    def copy(self, source, target, device):
        one = self.plan(source, target, device)
        one.start()
        self.started.append(one)
        return one

    def here(self, source, target):
        k = self.used_local
        self.used_local += 1
        one = pltpu.make_async_copy(source, target, self.locals.at[k])
        one.start()
        return one

    def finish(self):
        for one in self.started:
            one.wait_send()


def meet(devices):
    barrier = pltpu.get_barrier_semaphore()
    for device in devices:
        pl.semaphore_signal(barrier, inc=1, device_id=device, device_id_type=pl.DeviceIdType.MESH)
    pl.semaphore_wait(barrier, len(devices))


def partners():
    c, t = lax.axis_index("context"), lax.axis_index("tensor")
    flip = lambda x, bit: x + bit * (1 - 2 * lax.rem(x // bit, 2))
    return {
        "core": {"tensor": flip(t, 1)},
        "y": {"tensor": flip(t, 2)},
        "z": {"context": flip(c, 1)},
        "far": {"context": flip(c, 2)},
        "last": {"context": flip(flip(c, 1), 2)},
    }


def wide(x):
    return x.astype(f32)


def ranks():
    t = lax.axis_index("tensor")
    flip = lambda x, bit: x + bit * (1 - 2 * lax.rem(x // bit, 2))
    return (t, flip(t, 1), flip(t, 2), flip(flip(t, 1), 2))


def scatter_rank(wires, to, part, own, got_core, sent, got_y):
    size = part.shape[1] // 2
    halves = [pl.ds(0, size), pl.ds(size, size)]
    rank = ranks()
    from_core = {}
    for block in (1, 0):
        for k, at in enumerate(halves):
            from_core[block, k] = wires.copy(
                part.at[rank[1 + 2 * block], at], got_core.at[block, at], to["core"]
            )
    mine = [wires.here(part.at[rank[2 * block]], own.at[block]) for block in (0, 1)]
    yield
    for one in mine:
        one.wait()
    from_y = []
    for k, at in enumerate(halves):
        from_core[1, k].wait_recv()
        sent[at] = (wide(own[1, at]) + wide(got_core[1, at])).astype(bf16)
        from_y.append(wires.copy(sent.at[at], got_y.at[at], to["y"]))
    yield
    for k in range(2):
        from_core[0, k].wait_recv()
    total = wide(own[0]) + wide(got_core[0])
    for one in from_y:
        one.wait_recv()
    return total + wide(got_y[...])


def scatter_pair(wires, to, part, own, got_core, sent, got_y, got_z, diag_y, diag_z):
    size = part.shape[1] // 2
    low, high = pl.ds(0, size), pl.ds(size, size)
    from_core = {j: wires.copy(part.at[4 + j], got_core.at[j], to["core"]) for j in (3, 1, 2, 0)}
    mine = wires.here(part.at[pl.ds(0, 4)], own)
    yield
    mine.wait()
    both = lambda j, at: wide(own[j, at]) + wide(got_core[j, at])
    from_core[3].wait_recv()
    sent[2] = (wide(own[3]) + wide(got_core[3])).astype(bf16)
    via_z = wires.copy(sent.at[2, low], diag_z, to["z"])
    via_y = wires.copy(sent.at[2, high], diag_y, to["y"])
    from_core[1].wait_recv()
    sent[0, high] = both(1, high).astype(bf16)
    y_high = wires.copy(sent.at[0, high], got_y.at[high], to["y"])
    from_core[2].wait_recv()
    sent[1, low] = both(2, low).astype(bf16)
    z_low = wires.copy(sent.at[1, low], got_z.at[low], to["z"])
    yield
    via_z.wait_recv()
    sent[0, low] = (both(1, low) + wide(diag_z[...])).astype(bf16)
    y_low = wires.copy(sent.at[0, low], got_y.at[low], to["y"])
    via_y.wait_recv()
    sent[1, high] = (both(2, high) + wide(diag_y[...])).astype(bf16)
    z_high = wires.copy(sent.at[1, high], got_z.at[high], to["z"])
    yield
    from_core[0].wait_recv()
    total = wide(own[0]) + wide(got_core[0])
    for one in (y_high, z_low, y_low, z_high):
        one.wait_recv()
    return total + wide(got_y[...]) + wide(got_z[...])


def result_of(steps):
    while True:
        try:
            next(steps)
        except StopIteration as done:
            return done.value


def gather_rank(wires, to, block, out):
    size = block.shape[0] // 2
    halves = [pl.ds(0, size), pl.ds(size, size)]
    rank = ranks()
    mine = wires.here(block, out.at[rank[0]])
    from_y = [wires.copy(block.at[h], out.at[rank[0], h], to["y"]) for h in halves]
    from_core = [wires.copy(block, out.at[rank[0]], to["core"])]
    yield
    for h, one in zip(halves, from_y):
        one.wait_recv()
        from_core.append(wires.copy(out.at[rank[2], h], out.at[rank[2], h], to["core"]))
    for one in from_core:
        one.wait_recv()
    mine.wait()


def gather_pair(wires, to, block, out, base):
    size = block.shape[0] // 2
    low, high = pl.ds(0, size), pl.ds(size, size)
    at = lambda j: out.at[base + j]
    from_z = wires.copy(block, at(2), to["z"])
    yield
    from_y = wires.copy(block, at(1), to["y"])
    from_core = [wires.copy(block, at(4), to["core"])]
    yield
    from_y.wait_recv()
    via_z = wires.copy(out.at[base + 1, low], out.at[base + 3, low], to["z"])
    from_core.append(wires.copy(at(1), at(5), to["core"]))
    from_z.wait_recv()
    via_y = wires.copy(out.at[base + 2, high], out.at[base + 3, high], to["y"])
    from_core.append(wires.copy(at(2), at(6), to["core"]))
    yield
    via_z.wait_recv()
    via_y.wait_recv()
    from_core.append(wires.copy(at(3), at(7), to["core"]))
    return from_core


def remote_call(kernel, name, key, args, outs, scratch, copies, in_vmem):
    ins, out_in = in_vmem
    spec = lambda inside: pl.BlockSpec(memory_space=pltpu.VMEM if inside else pl.ANY)
    return pl.pallas_call(
        kernel,
        name=name,
        out_shape=outs,
        in_specs=[spec(x) for x in ins],
        out_specs=[spec(x) for x in out_in],
        scratch_shapes=list(scratch)
        + [
            pltpu.SemaphoreType.DMA((copies,)),
            pltpu.SemaphoreType.DMA((copies,)),
            pltpu.SemaphoreType.DMA((6,)),
        ],
        compiler_params=pltpu.CompilerParams(
            collective_id=key, has_side_effects=True, vmem_limit_bytes=VMEM_LIMIT
        ),
    )(*args)


def kv_gather_kernel(own_ref, out_ref, *sems):
    wires, to = Wires(*sems), partners()
    kind = lax.rem(lax.axis_index("tensor"), 2)
    rows = own_ref.shape[0]
    block = lambda j: out_ref.at[kind, pl.ds(j * rows, rows)]
    meet([to[k] for k in ("core", "z", "far", "last")])
    mine = wires.here(own_ref, block(0))
    arrive = [wires.copy(own_ref, block(j), to[k]) for j, k in ((3, "last"), (2, "far"), (1, "z"))]
    from_core = [wires.copy(own_ref, block(0), to["core"])]
    for j, one in ((1, arrive[2]), (2, arrive[1]), (3, arrive[0])):
        one.wait_recv()
        from_core.append(wires.copy(block(j), block(j), to["core"]))
    for one in from_core:
        one.wait_recv()
    mine.wait()
    wires.finish()


def kv_gather(own):
    rows, width = own.shape
    n_c = lax.axis_size("context")
    return remote_call(
        kv_gather_kernel,
        "kv_gather",
        0,
        [own],
        [jax.ShapeDtypeStruct((2, n_c * rows, width), bf16)],
        [],
        8,
        ([False], [False]),
    )[0]


def kv_scatter_kernel(part_ref, dkv_ref, own, got_core, sent, got, *sems):
    wires, to = Wires(*sems), partners()
    kind = lax.rem(lax.axis_index("tensor"), 2)
    rows = dkv_ref.shape[0]
    block = lambda j: pl.ds(j * rows, rows)
    meet([to[k] for k in ("core", "z", "far", "last")])
    steps = ((3, "last"), (2, "far"), (1, "z"), (0, None))
    from_core = {
        j: wires.copy(part_ref.at[1 - kind, block(j)], got_core.at[block(j)], to["core"])
        for j, _ in steps
    }
    mine = wires.here(part_ref.at[kind], own)
    mine.wait()
    arrive = []
    for j, k in steps[:3]:
        from_core[j].wait_recv()
        sent[block(j)] = (wide(own[block(j)]) + wide(got_core[block(j)])).astype(bf16)
        arrive.append(wires.copy(sent.at[block(j)], got.at[block(j)], to[k]))
    from_core[0].wait_recv()
    total = wide(own[block(0)]) + wide(got_core[block(0)])
    for one in arrive:
        one.wait_recv()
    for j in (1, 2, 3):
        total = total + wide(got[block(j)])
    dkv_ref[...] = total
    wires.finish()


def kv_scatter(part):
    _, rows, width = part.shape
    n_c = lax.axis_size("context")
    return remote_call(
        kv_scatter_kernel,
        "kv_scatter",
        1,
        [part],
        [jax.ShapeDtypeStruct((rows // n_c, width), f32)],
        [pltpu.VMEM((rows, width), bf16)] * 4,
        7,
        ([False], [True]),
    )[0]


def middle_kernel(
    part, x_ref, gain_ref, dy_ref, mid_ref, factor_ref, out, dys, own, core, sent, got, xn, *sems
):
    wires, to = Wires(*sems), partners()
    blocks = out.shape[0] // 2
    meet([to[k] for k in ("core", "y", "z", "far")])
    summed = scatter_rank(wires, to, part, own, core, sent, got)
    next(summed)
    dy_far = wires.copy(dy_ref, dys.at[blocks], to["far"])
    mine = [wires.here(dy_ref, dys.at[0])]
    dy_near = gather_pair(wires, to, dy_ref, dys, 0)
    next(dy_near)
    next(summed)
    next(dy_near)
    middle = wide(x_ref[...]) + result_of(summed)
    mid_ref[...] = middle
    factor = lax.rsqrt(jnp.mean(middle * middle, axis=-1, keepdims=True) + EPSILON)
    factor_ref[...] = factor
    xn[...] = (middle * factor * gain_ref[...]).astype(bf16)
    mine.append(wires.here(xn, out.at[0]))
    xn_far = wires.copy(xn, out.at[blocks], to["far"])
    xn_near = gather_pair(wires, to, xn, out, 0)
    next(xn_near)
    next(xn_near)
    next(dy_near)
    next(xn_near)
    dy_far.wait_recv()
    dy_last = gather_pair(wires, to, dys.at[blocks], dys, blocks)
    next(dy_last)
    next(dy_last)
    xn_far.wait_recv()
    xn_last = gather_pair(wires, to, out.at[blocks], out, blocks)
    next(xn_last)
    next(xn_last)
    ends = result_of(dy_near) + result_of(xn_near)
    next(dy_last)
    next(xn_last)
    ends += result_of(dy_last) + result_of(xn_last)
    for one in ends:
        one.wait_recv()
    for one in mine:
        one.wait()
    wires.finish()


def middle_norm(part, inputs_part, gain, dy_part):
    rows, width = inputs_part.shape
    return remote_call(
        middle_kernel,
        "middle_norm",
        2,
        [part.reshape(4, rows, width), inputs_part, gain, dy_part],
        [
            jax.ShapeDtypeStruct((rows, width), f32),
            jax.ShapeDtypeStruct((rows, 1), f32),
            jax.ShapeDtypeStruct((16, rows, width), bf16),
            jax.ShapeDtypeStruct((16, rows, width), bf16),
        ],
        [
            pltpu.VMEM((2, rows, width), bf16),
            pltpu.VMEM((2, rows, width), bf16),
            pltpu.VMEM((rows, width), bf16),
            pltpu.VMEM((rows, width), bf16),
            pltpu.VMEM((rows, width), bf16),
        ],
        48,
        ([False, True, True, True], [True, True, False, False]),
    )


def norm_back_rows(values, factor, gain, grad_normed):
    gained = gain * grad_normed
    inner = jnp.mean(gained * values, axis=-1, keepdims=True)
    grad_values = factor * gained - values * (factor * factor * factor) * inner
    return grad_values, jnp.sum(grad_normed * values * factor, axis=0, keepdims=True)


def middle_back_kernel(
    part, mid_ref, factor_ref, gain_ref, dy_ref, dmid_ref, dgain_ref, out, low, *rest
):
    first, wires, to = rest[:7], Wires(*rest[7:]), partners()
    meet([to[k] for k in ("core", "y", "z")])
    grad_normed = result_of(scatter_pair(wires, to, part, *first))
    du, dgain = norm_back_rows(mid_ref[...], factor_ref[...], gain_ref[...], grad_normed)
    dgain_ref[...] = dgain
    dmid = wide(dy_ref[...]) + du
    low[...] = dmid.astype(bf16)
    share = gather_rank(wires, to, low, out)
    next(share)
    dmid_ref[...] = dmid
    result_of(share)
    wires.finish()


def pair_scratch(rows, width):
    return [
        pltpu.VMEM((4, rows, width), bf16),
        pltpu.VMEM((4, rows, width), bf16),
        pltpu.VMEM((3, rows, width), bf16),
        pltpu.VMEM((rows, width), bf16),
        pltpu.VMEM((rows, width), bf16),
        pltpu.VMEM((rows // 2, width), bf16),
        pltpu.VMEM((rows // 2, width), bf16),
    ]


def middle_back(part, middle, factor, gain, dy_part):
    rows, width = middle.shape
    return remote_call(
        middle_back_kernel,
        "middle_back",
        3,
        [part.reshape(8, rows, width), middle, factor, gain, dy_part],
        [
            jax.ShapeDtypeStruct((rows, width), f32),
            jax.ShapeDtypeStruct((1, width), f32),
            jax.ShapeDtypeStruct((4, rows, width), bf16),
        ],
        [pltpu.VMEM((rows, width), bf16)] + pair_scratch(rows, width),
        16,
        ([False, True, True, True, True], [True, True, False]),
    )


def add_all(wires, ways, value, slots):
    for k, device in enumerate(ways):
        one = wires.copy(value, slots.at[k], device)
        one.wait()
        wires.started = [x for x in wires.started if x is not one]
        value[...] = value[...] + slots[k]


def input_back_kernel(
    part, x_ref, factor_ref, gain_ref, dmid_ref, small_ref, sum_ref, out, *rest
):
    low, own, core, sent, got, slots = rest[:-3]
    wires, to = Wires(*rest[-3:]), partners()
    meet([to[k] for k in ("core", "y")])
    grad_normed = result_of(scatter_rank(wires, to, part, own, core, sent, got))
    du, dgain = norm_back_rows(wide(x_ref[...]), factor_ref[...], gain_ref[...], grad_normed)
    low[...] = (dmid_ref[...] + du).astype(bf16)
    share = gather_rank(wires, to, low, out)
    next(share)
    width = dgain.shape[1]
    sum_ref[:, width:] = small_ref[:, width:]
    sum_ref[:, :width] = dgain
    add_all(wires, [to["core"], to["y"]], sum_ref, slots)
    result_of(share)
    wires.finish()


def input_back(part, inputs_part, factor, gain, grad_middle, small):
    rows, width = inputs_part.shape
    return remote_call(
        input_back_kernel,
        "input_back",
        5,
        [part.reshape(4, rows, width), inputs_part, factor, gain, grad_middle, small],
        [
            jax.ShapeDtypeStruct(small.shape, f32),
            jax.ShapeDtypeStruct((4, rows, width), bf16),
        ],
        [
            pltpu.VMEM((rows, width), bf16),
            pltpu.VMEM((2, rows, width), bf16),
            pltpu.VMEM((2, rows, width), bf16),
            pltpu.VMEM((rows, width), bf16),
            pltpu.VMEM((rows, width), bf16),
            pltpu.VMEM((2,) + small.shape, f32),
        ],
        16,
        ([False, True, True, True, True, True], [True, False]),
    )


def context_sum_kernel(over_f, *refs):
    parts, small_ref, out_part, mid_ref = refs[:3], refs[3], refs[4], refs[5]
    outs, sum_ref, shared, outputs = refs[6:8], refs[8], refs[9], refs[10]
    lows, from_end, from_middle = refs[11:15], refs[15:19], refs[19:23]
    out_low, slot, scratch = refs[23], refs[24], refs[25:32]
    wires, to, c = Wires(*refs[32:]), partners(), lax.axis_index("context")
    end = (c == 0) | (c == lax.axis_size("context") - 1)
    inner = jnp.logical_not(end)
    greet = ["core", "y", "z", "last"]
    if over_f:
        to["f"] = {"fsdp": 1 - lax.axis_index("fsdp")}
        greet.append("f")
    meet([to[k] for k in greet])
    ahead = scatter_pair(wires, to, out_part, *scratch)
    next(ahead)
    sum_ref[...] = small_ref[...]
    from_f = wires.copy(small_ref, slot, to["f"]) if over_f else None
    next(ahead)
    sources = [*parts, sum_ref]
    chunks = []
    for i, cuts in ((2, 1), (0, 2), (1, 2), (3, 1)):
        size = sources[i].shape[0] // cuts
        chunks += [(i, pl.ds(k * size, size)) for k in range(cuts)]
    inward = [wires.plan(sources[i].at[at], from_end[i].at[at], to["z"]) for i, at in chunks]
    across = [wires.plan(lows[i].at[at], from_middle[i].at[at], to["last"]) for i, at in chunks]
    outward = [wires.plan(lows[i].at[at], lows[i].at[at], to["z"]) for i, at in chunks]
    small = len(chunks) - 1

    def send_in(k):
        @pl.when(end)
        def _():
            inward[k].start()

    def pass_on(first, past):
        @pl.when(inner)
        def _():
            for k in range(first, past):
                i, at = chunks[k]
                inward[k].wait_recv()
                total = wide(sources[i][at]) + wide(from_end[i][at])
                lows[i][at] = total.astype(lows[i].dtype)
                across[k].start()
                if k:
                    send_out(k - 1)

    def send_out(k):
        i, at = chunks[k]
        across[k].wait()
        lows[i][at] = (wide(lows[i][at]) + wide(from_middle[i][at])).astype(lows[i].dtype)
        outward[k].start()

    send_in(0)
    send_in(1)
    next(ahead)
    if over_f:
        from_f.wait_recv()
        sum_ref[...] = sum_ref[...] + slot[...]
    for k in range(2, small + 1):
        send_in(k)
    pass_on(0, 2)
    out_low[...] = (mid_ref[...] + result_of(ahead)).astype(bf16)
    out_share = gather_rank(wires, to, out_low, outputs)
    next(out_share)
    pass_on(2, small + 1)

    @pl.when(inner)
    def _():
        send_out(small)

    result_of(out_share)

    def arrived(k):
        @pl.when(end)
        def _():
            outward[k].wait_recv()

    arrived(0)
    share = gather_rank(wires, to, lows[2], shared)
    next(share)
    for k in range(1, len(chunks)):
        arrived(k)

    @pl.when(end)
    def _():
        for one in inward:
            one.wait_send()

    for i in (0, 1):
        outs[i][...] = wide(lows[i][...])
    sum_ref[...] = lows[3][...]
    result_of(share)

    @pl.when(inner)
    def _():
        for one in outward:
            one.wait_send()

    wires.finish()


def context_sum(over_f, parts, small, out_part, middle):
    rows, width = middle.shape
    lines = [pltpu.VMEM(x.shape, x.dtype) for x in (*parts, small)]
    return remote_call(
        functools.partial(context_sum_kernel, over_f),
        "context_sum",
        6,
        [*parts, small, out_part.reshape(8, rows, width), middle],
        [jax.ShapeDtypeStruct(x.shape, f32) for x in parts[:2]]
        + [jax.ShapeDtypeStruct(small.shape, f32)]
        + [jax.ShapeDtypeStruct((4,) + parts[2].shape, bf16)]
        + [jax.ShapeDtypeStruct((4, rows, width), bf16)],
        lines * 3
        + [pltpu.VMEM((rows, width), bf16), pltpu.VMEM(small.shape, f32)]
        + pair_scratch(rows, width),
        48,
        ([True] * 4 + [False, True], [True] * 3 + [False] * 2),
    )


def build(n_f, n_c, n_t):
    def flip(x, axis, bit):
        size = {"fsdp": n_f, "context": n_c, "tensor": n_t}[axis]
        return lax.ppermute(x, axis, [(i, i ^ bit) for i in range(size)])

    def by_bit(bit, x, other, axis):
        return jnp.where(
            bit == 0,
            jnp.concatenate([x, other], axis=axis),
            jnp.concatenate([other, x], axis=axis),
        )

    def after(x, *others):
        return lax.optimization_barrier((x, others))[0]

    def local(
        inputs,
        cotangent,
        blocks,
        attn_gain,
        w_query,
        b_query,
        w_key,
        b_key,
        w_value,
        b_value,
        w_out,
        ffn_gain,
        w_gate,
        w_up,
        w_down,
    ):
        rows, width = inputs.shape
        f = lax.axis_index("fsdp")
        c = lax.axis_index("context")
        t = lax.axis_index("tensor")
        core, parity, pair = t % 2, c % 2, c // 2
        heads = w_query.shape[1] // HD
        group = (t * heads) // (H // KV)
        part = rows // n_t
        units_all = w_gate.shape[1]
        units = units_all // 2

        def gather_f(x, axis):
            if n_f == 2:
                return by_bit(f, x, flip(x, "fsdp", 1), axis)
            return lax.all_gather(x, "fsdp", axis=axis, tiled=True)

        def grad_far(left, right, side):
            if n_f > 2:
                return None
            source = (left, right)[side]
            half = width // 2
            far = lax.dynamic_slice_in_dim(source, (1 - f) * half, half, 1)
            return (dot_rows(far, right) if side == 0 else dot_rows(left, far)).astype(bf16)

        def grad_sum(left, right, side, far):
            if n_f > 2:
                return lax.psum_scatter(
                    dot_rows(left, right).astype(bf16), "fsdp", scatter_dimension=side, tiled=True
                )
            source = (left, right)[side]
            half = width // 2
            own = lax.dynamic_slice_in_dim(source, f * half, half, 1)
            own = dot_rows(own, right) if side == 0 else dot_rows(left, own)
            return (own + flip(far, "fsdp", 1).astype(f32)).astype(bf16)

        small = jnp.concatenate(
            [v.reshape(1, -1) for v in (attn_gain, ffn_gain, b_query, b_key, b_value)], axis=1
        )
        column = lambda w: lax.dynamic_slice_in_dim(w, group * HD, HD, 1)
        w_kv_own = jnp.where(core == 0, column(w_key), column(w_value))
        pieces_f = lambda x, axis: (
            [x, flip(x, "fsdp", 1)]
            if n_f == 2
            else [lax.all_gather(x, "fsdp", axis=axis, tiled=True)]
        )
        meta = jnp.stack([f, 1 - f, core, pair]).astype(jnp.int32)
        w_q = pieces_f(w_query, 0)
        w_kv = pieces_f(w_kv_own, 0)
        small = gather_f(small, 0)
        w_out_all = gather_f(after(w_out, small), 1)
        piece = attn_gain.shape[0]
        gain_first = small[:, :piece].reshape(1, width).astype(f32)
        gain_second = small[:, piece : 2 * piece].reshape(1, width).astype(f32)
        bias_of = lambda lo, n: (
            small[:, lo : lo + n * (HD // n_f)]
            .reshape(n_f, n, HD // n_f)
            .transpose(1, 0, 2)
            .reshape(n, HD)
            .astype(f32)
        )
        at = 2 * piece
        bq = bias_of(at, heads)
        bk = bias_of(at + heads * (HD // n_f), KV)
        bv = bias_of(at + (heads + KV) * (HD // n_f), KV)
        b_kv = lax.dynamic_index_in_dim(jnp.where(core == 0, bk, bv), group, 0)

        unit_slice = lambda w: lax.dynamic_slice_in_dim(w, parity * units, units, 0)
        own_units = jnp.concatenate([unit_slice(w) for w in (w_gate.T, w_up.T, w_down)], axis=0)

        dy_part = lax.dynamic_slice_in_dim(cotangent, t * part, part, 0)

        seq_blocks = blocks[0].reshape(n_c, -1)
        own_blocks = seq_blocks.shape[1]
        key_blocks = jnp.concatenate(
            [lax.dynamic_index_in_dim(seq_blocks, c ^ j, 0, keepdims=False) for j in range(n_c)]
        )
        positions = (
            key_blocks[:own_blocks, None] * BLOCK + jnp.arange(BLOCK, dtype=jnp.int32)[None, :]
        ).reshape(-1)
        cosine, sine = rope_tables(positions)
        bias = jnp.concatenate([bq.reshape(1, -1), b_kv], axis=1)
        normed, factor_first, queries, kv_own = qkv(
            meta, inputs, gain_first, bias, cosine, sine, w_q, w_kv
        )
        w_units = pieces_f(after(own_units, kv_own, w_out_all), 1)
        kv = kv_gather(after(kv_own, w_out_all))
        attended, lse = attention(key_blocks, queries, kv)
        inputs_part = lax.dynamic_slice_in_dim(inputs, t * part, part, 0)
        middle, factor_second, normed2, dy_all = middle_norm(
            dot(attended, w_out_all).astype(bf16), inputs_part, gain_second, dy_part
        )

        hidden, slope, gated, *down_far = hidden_units(meta, normed2, dy_all, w_units)
        grad_gate, grad_up, dx_part, out_part, *unit_far = hidden_back(
            meta, normed2, dy_all, hidden, slope, gated, w_units
        )

        def unit_done(own, got):
            low = (own.astype(f32) + got.astype(f32)).astype(bf16)
            return low, flip(low, "context", 1)

        if n_f == 2:
            down_got, gate_got, up_got = (flip(x, "fsdp", 1) for x in (*down_far, *unit_far))
            down_own = unit_grads(meta, 0, 2, *after((dy_all, [hidden]), dx_part))
            down_done = unit_done(down_own, after(down_got, down_own))
            gate_up_own = unit_grads(
                meta, 0, 2, *after((normed2, [grad_gate, grad_up]), down_done[0])
            )
            dx_part = after(dx_part, gate_up_own)
        else:
            over_f = lambda x: lax.psum_scatter(x, "fsdp", scatter_dimension=1, tiled=True)
            down_own = over_f(unit_grads(meta, 0, 1, dy_all, [hidden]))
            gate_up_own = over_f(unit_grads(meta, 0, 1, normed2, [grad_gate, grad_up]))
            gate_got = up_got = jnp.zeros_like(down_own)
            down_done = unit_done(down_own, gate_got)

        unit_whole = lambda low, other: by_bit(parity, low, other, 0).astype(f32)

        grad_middle, ffn_gain_grad, grad_middle_low = middle_back(
            dx_part, middle, factor_second, gain_second, dy_part
        )
        grad_middle_low = grad_middle_low.reshape(rows, width)
        gate_done = unit_done(gate_up_own[:units], after(gate_got, grad_middle_low))
        grad_attended = dot_cols(
            after(grad_middle_low, gate_done[0], down_done), w_out_all
        ).astype(bf16)

        dq_low, dkv = attention_back(key_blocks, queries, grad_attended, lse, cosine, sine, kv)
        dkv = kv_scatter(after(dkv, gate_done))
        up_done = unit_done(gate_up_own[units:], after(up_got, dkv))
        dkv = after(dkv, up_done[0])
        dkv_low = jnp.where(core == 0, rotate_back(dkv, cosine, sine), dkv).astype(bf16)
        attention_args = (
            (attended, after(grad_middle_low, dkv), 1),
            (normed, after(dq_low, dkv), 0),
            (normed, dkv_low, 0),
        )
        fars = [grad_far(*args) for args in attention_args]
        dkv_low = after(dkv_low, fars)
        factor_part = lax.dynamic_slice_in_dim(factor_first, t * part, part, 0)
        own_biases = jnp.sum(
            jnp.concatenate([dq_low, dkv_low], axis=1).astype(f32), axis=0, keepdims=True
        )
        slots = lax.dynamic_update_slice(
            jnp.zeros((n_t, (heads + 1) * HD), f32), own_biases, (t, 0)
        )
        small_grads = jnp.concatenate(
            [jnp.zeros((1, width), f32), ffn_gain_grad, slots.reshape(1, -1)], axis=1
        )
        small_grads, input_grad = input_back(
            qkv_back(meta, dq_low, dkv_low, w_q, w_kv),
            inputs_part,
            factor_part,
            gain_first,
            grad_middle,
            small_grads,
        )
        input_grad = input_grad.reshape(rows, width)
        if n_f > 2:
            small_grads = lax.psum(small_grads, "fsdp")
        attention_parts = [grad_sum(*args, far) for args, far in zip(attention_args, fars)]
        wd_grad = unit_whole(*after(down_done, small_grads))
        wg_grad = unit_whole(*after(gate_done, small_grads))
        small_grads, up_done, wg_grad, wd_grad = lax.optimization_barrier(
            (small_grads, up_done, wg_grad, wd_grad)
        )
        wo_grad, wq_grad, packed, wkv_all, outputs = context_sum(
            n_f == 2, attention_parts, small_grads, out_part, middle
        )
        outputs = outputs.reshape(rows, width)
        wkv_all = wkv_all.astype(f32)
        wk_grad = jnp.concatenate([wkv_all[0], wkv_all[2]], axis=1)
        wv_grad = jnp.concatenate([wkv_all[1], wkv_all[3]], axis=1)
        packed = packed[0]
        attn_gain_grad = lax.dynamic_slice_in_dim(packed, f * piece, piece, 0)
        ffn_gain_grad = lax.dynamic_slice_in_dim(packed, width + f * piece, piece, 0)
        slots = packed[2 * width :].reshape(n_t, heads + 1, HD)
        slots = lax.dynamic_slice_in_dim(slots, f * (HD // n_f), HD // n_f, 2)
        bq_out = lax.dynamic_index_in_dim(slots, t, 0, keepdims=False)[:heads]
        bk_out = slots[0::2, heads]
        bv_out = slots[1::2, heads]

        wu_grad = unit_whole(*up_done)
        wg_grad, wu_grad = wg_grad.T, wu_grad.T

        return (
            outputs,
            input_grad,
            attn_gain_grad,
            wq_grad,
            bq_out,
            wk_grad,
            bk_out,
            wv_grad,
            bv_out,
            wo_grad,
            ffn_gain_grad,
            wg_grad,
            wu_grad,
            wd_grad,
        )

    return local


def solution(mesh):
    in_specs = (
        P(("fsdp", "context"), None),
        P(("fsdp", "context"), None),
        P("fsdp", None),
        P("fsdp"),
        P("fsdp", "tensor"),
        P("tensor", "fsdp"),
        P("fsdp", None),
        P(None, "fsdp"),
        P("fsdp", None),
        P(None, "fsdp"),
        P("tensor", "fsdp"),
        P("fsdp"),
        P("fsdp", "tensor"),
        P("fsdp", "tensor"),
        P("tensor", "fsdp"),
    )
    out_specs = (
        P(("fsdp", "context"), None),
        P(("fsdp", "context"), None),
        P("fsdp"),
        P("fsdp", "tensor"),
        P("tensor", "fsdp"),
        P("fsdp", None),
        P(None, "fsdp"),
        P("fsdp", None),
        P(None, "fsdp"),
        P("tensor", "fsdp"),
        P("fsdp"),
        P("fsdp", "tensor"),
        P("fsdp", "tensor"),
        P("tensor", "fsdp"),
    )
    local = build(mesh.shape["fsdp"], mesh.shape["context"], mesh.shape["tensor"])
    return jax.shard_map(local, mesh=mesh, in_specs=in_specs, out_specs=out_specs, check_vma=False)
```

```python
import functools

import jax
import jax.numpy as jnp
from jax import lax
from jax.experimental import pallas as pl
from jax.experimental.pallas import tpu as pltpu
from jax.sharding import PartitionSpec as P

H = 12
KV = 2
HD = 128
BLOCK = 256

EPSILON = 1e-06
ROPE_BASE = 1000000.0
MASKED = -1e30
SCALING = HD ** (-0.5)
LANES = 128
VMEM_LIMIT = 60 << 20
FFN_VMEM_LIMIT = 63 << 20

f32 = jnp.float32
bf16 = jnp.bfloat16


def rope_tables(positions):
    halfway = HD // 2
    frequency = ROPE_BASE ** (-(jnp.arange(halfway, dtype=f32) * 2.0 / HD))
    angles = positions.astype(f32)[:, None] * frequency[None, :]
    cosine, sine = jnp.cos(angles), jnp.sin(angles)
    return (jnp.concatenate([cosine, cosine], axis=1), jnp.concatenate([sine, sine], axis=1))


def rotate(field, cosine, sine):
    halfway = HD // 2
    turned = jnp.concatenate([-field[..., halfway:], field[..., :halfway]], axis=-1)
    return field * cosine + turned * sine


def rotate_back(grad_field, cosine, sine):
    halfway = HD // 2
    moved = grad_field * sine
    turned = jnp.concatenate([moved[..., halfway:], -moved[..., :halfway]], axis=-1)
    return grad_field * cosine + turned


def dot(left, right):
    return jnp.dot(left, right, preferred_element_type=f32)


def dot_rows(left, right):
    return lax.dot_general(left, right, (((0,), (0,)), ((), ())), preferred_element_type=f32)


def dot_cols(left, right):
    return lax.dot_general(left, right, (((1,), (1,)), ((), ())), preferred_element_type=f32)


def mask_row(kb_ref, own_block, key_blocks):
    return jnp.concatenate(
        [
            jnp.full((1, BLOCK), jnp.where(kb_ref[j] <= own_block, 0.0, MASKED), f32)
            for j in range(key_blocks)
        ],
        axis=1,
    )


def attention_kernel(key_blocks, kb_ref, q_ref, k_ref, v_ref, o_ref, lse_ref):
    bias = mask_row(kb_ref, kb_ref[pl.program_id(1)], key_blocks)
    scores = dot_cols(q_ref[...], k_ref[...]) * SCALING + bias
    row_max = jnp.max(scores, axis=1, keepdims=True)
    expo = jnp.exp(scores - row_max)
    total = jnp.sum(expo, axis=1, keepdims=True)
    probability = (expo * (1.0 / total)).astype(bf16)
    o_ref[...] = dot(probability, v_ref[...]).astype(bf16)
    lse_ref[0] = row_max + jnp.log(total)


def attention(key_blocks, queries, kv):
    rows, width = queries.shape
    heads = width // HD
    whole = lambda kind: pl.BlockSpec((None,) + kv.shape[1:], lambda h, i, kb: (kind, 0, 0))
    tile = pl.BlockSpec((BLOCK, HD), lambda h, i, kb: (i, h))
    return pl.pallas_call(
        functools.partial(attention_kernel, kv.shape[1] // BLOCK),
        name="attention",
        grid_spec=pltpu.PrefetchScalarGridSpec(
            num_scalar_prefetch=1,
            grid=(heads, rows // BLOCK),
            in_specs=[tile, whole(0), whole(1)],
            out_specs=[tile, pl.BlockSpec((1, BLOCK, 1), lambda h, i, kb: (h, i, 0))],
        ),
        out_shape=[
            jax.ShapeDtypeStruct((rows, width), bf16),
            jax.ShapeDtypeStruct((heads, rows, 1), f32),
        ],
        compiler_params=pltpu.CompilerParams(vmem_limit_bytes=VMEM_LIMIT),
    )(key_blocks, queries, kv, kv)


def attention_back_kernel(
    key_blocks,
    kb_ref,
    q_ref,
    do_ref,
    lse_ref,
    cos_ref,
    sin_ref,
    k_ref,
    v_ref,
    dq_ref,
    dkv_ref,
    dk_ref,
    dv_ref,
):
    head, i = pl.program_id(0), pl.program_id(1)

    @pl.when((head == 0) & (i == 0))
    def _():
        dk_ref[...] = jnp.zeros_like(dk_ref)
        dv_ref[...] = jnp.zeros_like(dv_ref)

    bias = mask_row(kb_ref, kb_ref[i], key_blocks)
    scores = dot_cols(q_ref[...], k_ref[...]) * SCALING + bias
    probability = jnp.exp(scores - lse_ref[0])
    grad_probs = dot_cols(do_ref[...], v_ref[...])
    inner = jnp.sum(probability * grad_probs, axis=1, keepdims=True)
    grad_scores = (probability * (grad_probs - inner)).astype(bf16)
    grad_query = dot(grad_scores, k_ref[...]) * SCALING
    moved = grad_query * sin_ref[...]
    sign = jnp.where(lax.broadcasted_iota(jnp.int32, moved.shape, 1) < HD // 2, 1.0, -1.0)
    dq_ref[...] = (
        grad_query * cos_ref[...] + pltpu.roll(moved, HD // 2, 1) * sign
    ).astype(bf16)
    dk_ref[...] += dot_rows(grad_scores, q_ref[...]) * SCALING
    dv_ref[...] += dot_rows(probability.astype(bf16), do_ref[...])

    @pl.when((head == pl.num_programs(0) - 1) & (i == pl.num_programs(1) - 1))
    def _():
        dkv_ref[0] = dk_ref[...].astype(bf16)
        dkv_ref[1] = dv_ref[...].astype(bf16)


def attention_back(key_blocks, queries, grad_out, lse, cosine, sine, kv):
    rows, width = queries.shape
    heads = width // HD
    whole = lambda kind: pl.BlockSpec((None,) + kv.shape[1:], lambda h, i, kb: (kind, 0, 0))
    tile = pl.BlockSpec((BLOCK, HD), lambda h, i, kb: (i, h))
    table = pl.BlockSpec((BLOCK, HD), lambda h, i, kb: (i, 0))
    return pl.pallas_call(
        functools.partial(attention_back_kernel, kv.shape[1] // BLOCK),
        name="attention_back",
        grid_spec=pltpu.PrefetchScalarGridSpec(
            num_scalar_prefetch=1,
            grid=(heads, rows // BLOCK),
            in_specs=[
                tile,
                tile,
                pl.BlockSpec((1, BLOCK, 1), lambda h, i, kb: (h, i, 0)),
                table,
                table,
                whole(0),
                whole(1),
            ],
            out_specs=[tile, pl.BlockSpec(kv.shape, lambda h, i, kb: (0, 0, 0))],
            scratch_shapes=[pltpu.VMEM(kv.shape[1:], f32)] * 2,
        ),
        out_shape=[
            jax.ShapeDtypeStruct((rows, width), bf16),
            jax.ShapeDtypeStruct(kv.shape, bf16),
        ],
        compiler_params=pltpu.CompilerParams(vmem_limit_bytes=VMEM_LIMIT),
    )(key_blocks, queries, grad_out, lse, cosine, sine, kv, kv)


def qkv_kernel(pieces, meta_ref, x_ref, gain_ref, bias_ref, cos_ref, sin_ref, *refs):
    weights, (xn_ref, factor_ref, q_ref, kv_ref) = refs[: 2 * pieces], refs[2 * pieces :]
    values = x_ref[...].astype(f32)
    factor = lax.rsqrt(jnp.mean(values * values, axis=-1, keepdims=True) + EPSILON)
    factor_ref[...] = factor
    xn_ref[...] = (values * factor * gain_ref[...]).astype(bf16)
    depth = weights[0].shape[0]
    normed = [xn_ref[:, columns_of(meta_ref, j, depth, pieces)] for j in range(pieces)]
    cosine, sine = cos_ref[...], sin_ref[...]
    sign = jnp.where(lax.broadcasted_iota(jnp.int32, cosine.shape, 1) < HD // 2, -1.0, 1.0)
    sine = sine * sign
    width = q_ref.shape[1]
    total = bias_ref[:, :width] + sum(dot(x, w[...]) for x, w in zip(normed, weights[:pieces]))
    turn = lambda own: own * cosine + pltpu.roll(own, HD // 2, 1) * sine
    for h in range(width // HD):
        q_ref[:, h * HD : (h + 1) * HD] = turn(total[:, h * HD : (h + 1) * HD]).astype(bf16)
    own = bias_ref[:, width:] + sum(dot(x, w[...]) for x, w in zip(normed, weights[pieces:]))
    kv_ref[...] = jnp.where(meta_ref[2] == 0, turn(own), own).astype(bf16)


def columns_of(meta_ref, j, depth, pieces):
    if pieces == 1:
        return slice(None)
    return pl.ds(pl.multiple_of(meta_ref[j] * depth, LANES), depth)


def qkv(meta, inputs, gain, bias, cosine, sine, w_q, w_kv):
    rows, width = inputs.shape
    out = w_q[0].shape[1]
    tile = 256
    row = lambda n: pl.BlockSpec((tile, n), lambda i, m: (i, 0))
    fixed = lambda w: pl.BlockSpec(w.shape, lambda i, m: (0, 0))
    return pl.pallas_call(
        functools.partial(qkv_kernel, len(w_q)),
        name="qkv",
        grid_spec=pltpu.PrefetchScalarGridSpec(
            num_scalar_prefetch=1,
            grid=(rows // tile,),
            in_specs=[row(width), fixed(gain), fixed(bias), row(HD), row(HD)]
            + [fixed(w) for w in (*w_q, *w_kv)],
            out_specs=[row(width), row(1), row(out), row(HD)],
        ),
        out_shape=[
            jax.ShapeDtypeStruct((rows, width), bf16),
            jax.ShapeDtypeStruct((rows, 1), f32),
            jax.ShapeDtypeStruct((rows, out), bf16),
            jax.ShapeDtypeStruct((rows, HD), bf16),
        ],
        compiler_params=pltpu.CompilerParams(vmem_limit_bytes=VMEM_LIMIT),
    )(meta, inputs, gain, bias, cosine, sine, *w_q, *w_kv)


def qkv_back_kernel(pieces, meta_ref, dq_ref, dkv_ref, *refs):
    w_q, w_kv, out_ref = refs[:pieces], refs[pieces : 2 * pieces], refs[-1]
    for j in range(pieces):
        out_ref[:, columns_of(meta_ref, j, w_q[j].shape[0], pieces)] = (
            dot_cols(dq_ref[...], w_q[j][...]) + dot_cols(dkv_ref[...], w_kv[j][...])
        ).astype(bf16)


def qkv_back(meta, grad_q, grad_kv, w_q, w_kv):
    rows, width = grad_q.shape[0], sum(w.shape[0] for w in w_q)
    tile = 256
    row = lambda n: pl.BlockSpec((tile, n), lambda i, m: (i, 0))
    fixed = lambda w: pl.BlockSpec(w.shape, lambda i, m: (0, 0))
    return pl.pallas_call(
        functools.partial(qkv_back_kernel, len(w_q)),
        name="qkv_back",
        grid_spec=pltpu.PrefetchScalarGridSpec(
            num_scalar_prefetch=1,
            grid=(rows // tile,),
            in_specs=[row(grad_q.shape[1]), row(HD)] + [fixed(w) for w in (*w_q, *w_kv)],
            out_specs=row(width),
        ),
        out_shape=jax.ShapeDtypeStruct((rows, width), bf16),
        compiler_params=pltpu.CompilerParams(vmem_limit_bytes=VMEM_LIMIT),
    )(meta, grad_q, grad_kv, *w_q, *w_kv)


def ffn_kernel(pieces, meta_ref, x_ref, dy_ref, *refs):
    wg, wu, wd = (refs[m * pieces : (m + 1) * pieces] for m in range(3))
    refs = refs[3 * pieces :]
    hid_ref, dg_ref, du_ref, dx_ref, out_ref = refs[:5]
    columns = [columns_of(meta_ref, j, wg[j].shape[1], pieces) for j in range(pieces)]
    gate = sum(dot_cols(x_ref[:, at], w[...]) for at, w in zip(columns, wg))
    up = sum(dot_cols(x_ref[:, at], w[...]) for at, w in zip(columns, wu))
    grad_hidden = sum(dot_cols(dy_ref[:, at], w[...]) for at, w in zip(columns, wd))
    sigma = 1.0 / (1.0 + jnp.exp(-gate))
    gated = gate * sigma
    hid_ref[...] = (gated * up).astype(bf16)
    dg_ref[...] = (grad_hidden * up * (sigma + gated * (1.0 - sigma))).astype(bf16)
    du_ref[...] = (grad_hidden * gated).astype(bf16)
    step, steps = pl.program_id(0), pl.num_programs(0)

    @pl.when(step // (steps // 2) == meta_ref[3])
    def _():
        for at, g, u, d in zip(columns, wg, wu, wd):
            dx_ref[:, at] = (dot(dg_ref[...], g[...]) + dot(du_ref[...], u[...])).astype(bf16)
            out_ref[:, at] = dot(hid_ref[...], d[...]).astype(bf16)

    if pieces == 2:
        outs, totals = refs[5:8], refs[8:11]
        sources = ((hid_ref, dy_ref), (dg_ref, x_ref), (du_ref, x_ref))

        @pl.when(step == 0)
        def _():
            for total in totals:
                total[...] = jnp.zeros_like(total)

        for total, (unit, row) in zip(totals, sources):
            total[...] += dot_rows(unit[...], row[:, columns[1]])

        @pl.when(step == steps - 1)
        def _():
            for out, total in zip(outs, totals):
                out[...] = total[...].astype(bf16)


def ffn(meta, normed, grad_out, weights):
    width = normed.shape[-1]
    rows = normed.shape[0] * normed.shape[1]
    pieces = len(weights)
    units, depth = weights[0].shape[0] // 3, weights[0].shape[1]
    tile = 512
    steps = rows // tile
    half = steps // 2
    flat = lambda x: x.reshape(-1, width)
    read = pl.BlockSpec((tile, width), lambda i, m: (lax.rem(i + m[3] * half, steps), 0))
    once = pl.Buffered(1)
    weight = lambda w, k: pl.BlockSpec((units, depth), lambda i, m: (k, 0), pipeline_mode=once)
    placed = pl.BlockSpec((tile, units), lambda i, m: (i, 0))
    near = pl.BlockSpec((tile, width), lambda i, m: (jnp.clip(i - m[3] * half, 0, half - 1), 0))
    grads = [pl.BlockSpec((units, depth), lambda i, m: (0, 0), pipeline_mode=once)] * 3
    grads = grads if pieces == 2 else []
    shapes = [(rows, units)] * 3 + [(rows // 2, width)] * 2 + [(units, depth)] * len(grads)
    return pl.pallas_call(
        functools.partial(ffn_kernel, pieces),
        name="ffn",
        grid_spec=pltpu.PrefetchScalarGridSpec(
            num_scalar_prefetch=1,
            grid=(steps,),
            in_specs=[read, read] + [weight(w, k) for k in range(3) for w in weights],
            out_specs=[placed] * 3 + [near] * 2 + grads,
            scratch_shapes=[pltpu.VMEM((units, depth), f32)] * len(grads),
        ),
        out_shape=[jax.ShapeDtypeStruct(shape, bf16) for shape in shapes],
        compiler_params=pltpu.CompilerParams(vmem_limit_bytes=FFN_VMEM_LIMIT),
    )(meta, flat(normed), flat(grad_out), *(list(weights) * 3))


def unit_grads_kernel(count, meta_ref, near_ref, far_ref, *refs):
    units, out_ref, x_ref = refs[:count], refs[-2], refs[-1]
    half = near_ref.shape[0]
    x_ref[pl.ds(pl.multiple_of(meta_ref[3] * half, half), half)] = near_ref[...]
    x_ref[pl.ds(pl.multiple_of((1 - meta_ref[3]) * half, half), half)] = far_ref[...]
    for k, unit in enumerate(units):
        depth = unit.shape[1]
        out_ref[k * depth : (k + 1) * depth] = dot_rows(unit[...], x_ref[...]).astype(bf16)


def unit_grads(meta, which, pieces, x, units_of):
    width = x.shape[-1]
    count, (rows, units) = len(units_of), units_of[0].shape
    depth = width // pieces
    tile = 256
    steps = depth // tile
    shard = (lambda m: m[which]) if pieces > 1 else (lambda m: 0)
    feature = lambda half: pl.BlockSpec(
        (rows // 2, tile), lambda i, m: (half, shard(m) * steps + i)
    )
    unit = pl.BlockSpec((rows, units), lambda i, m: (0, 0), pipeline_mode=pl.Buffered(1))
    x = x.reshape(-1, width)
    return pl.pallas_call(
        functools.partial(unit_grads_kernel, count),
        name=f"unit_grads_{which}_{count}",
        grid_spec=pltpu.PrefetchScalarGridSpec(
            num_scalar_prefetch=1,
            grid=(steps,),
            in_specs=[feature(0), feature(1)] + [unit] * count,
            out_specs=pl.BlockSpec((count * units, tile), lambda i, m: (0, i)),
            scratch_shapes=[pltpu.VMEM((rows, tile), bf16)],
        ),
        out_shape=jax.ShapeDtypeStruct((count * units, depth), bf16),
        compiler_params=pltpu.CompilerParams(vmem_limit_bytes=VMEM_LIMIT),
    )(meta, x, x, *units_of)


class Wires:
    def __init__(self, sends, receives, locals_):
        self.sends, self.receives, self.locals = sends, receives, locals_
        self.used = self.used_local = 0
        self.started = []

    def plan(self, source, target, device):
        k = self.used
        self.used += 1
        return pltpu.make_async_remote_copy(
            source,
            target,
            self.sends.at[k],
            self.receives.at[k],
            device_id=device,
            device_id_type=pl.DeviceIdType.MESH,
        )

    def copy(self, source, target, device):
        one = self.plan(source, target, device)
        one.start()
        self.started.append(one)
        return one

    def here(self, source, target):
        k = self.used_local
        self.used_local += 1
        one = pltpu.make_async_copy(source, target, self.locals.at[k])
        one.start()
        return one

    def finish(self):
        for one in self.started:
            one.wait_send()


def meet(devices):
    barrier = pltpu.get_barrier_semaphore()
    for device in devices:
        pl.semaphore_signal(barrier, inc=1, device_id=device, device_id_type=pl.DeviceIdType.MESH)
    pl.semaphore_wait(barrier, len(devices))


def partners():
    c, t = lax.axis_index("context"), lax.axis_index("tensor")
    flip = lambda x, bit: x + bit * (1 - 2 * lax.rem(x // bit, 2))
    return {
        "core": {"tensor": flip(t, 1)},
        "y": {"tensor": flip(t, 2)},
        "z": {"context": flip(c, 1)},
        "far": {"context": flip(c, 2)},
        "last": {"context": flip(flip(c, 1), 2)},
    }


def wide(x):
    return x.astype(f32)


def ranks():
    t = lax.axis_index("tensor")
    flip = lambda x, bit: x + bit * (1 - 2 * lax.rem(x // bit, 2))
    return (t, flip(t, 1), flip(t, 2), flip(flip(t, 1), 2))


def scatter_rank(wires, to, part, own, got_core, sent, got_y):
    size = part.shape[1] // 2
    halves = [pl.ds(0, size), pl.ds(size, size)]
    rank = ranks()
    from_core = {}
    for block in (1, 0):
        for k, at in enumerate(halves):
            from_core[block, k] = wires.copy(
                part.at[rank[1 + 2 * block], at], got_core.at[block, at], to["core"]
            )
    mine = [wires.here(part.at[rank[2 * block]], own.at[block]) for block in (0, 1)]
    yield
    for one in mine:
        one.wait()
    from_y = []
    for k, at in enumerate(halves):
        from_core[1, k].wait_recv()
        sent[at] = (wide(own[1, at]) + wide(got_core[1, at])).astype(bf16)
        from_y.append(wires.copy(sent.at[at], got_y.at[at], to["y"]))
    yield
    for k in range(2):
        from_core[0, k].wait_recv()
    total = wide(own[0]) + wide(got_core[0])
    for one in from_y:
        one.wait_recv()
    return total + wide(got_y[...])


def scatter_pair(wires, to, part, own, got_core, sent, got_y, got_z, diag_y, diag_z):
    size = part.shape[1] // 2
    low, high = pl.ds(0, size), pl.ds(size, size)
    from_core = {j: wires.copy(part.at[4 + j], got_core.at[j], to["core"]) for j in (3, 1, 2, 0)}
    mine = wires.here(part.at[pl.ds(0, 4)], own)
    yield
    mine.wait()
    both = lambda j, at: wide(own[j, at]) + wide(got_core[j, at])
    from_core[3].wait_recv()
    sent[2] = (wide(own[3]) + wide(got_core[3])).astype(bf16)
    via_z = wires.copy(sent.at[2, low], diag_z, to["z"])
    via_y = wires.copy(sent.at[2, high], diag_y, to["y"])
    from_core[1].wait_recv()
    sent[0, high] = both(1, high).astype(bf16)
    y_high = wires.copy(sent.at[0, high], got_y.at[high], to["y"])
    from_core[2].wait_recv()
    sent[1, low] = both(2, low).astype(bf16)
    z_low = wires.copy(sent.at[1, low], got_z.at[low], to["z"])
    yield
    via_z.wait_recv()
    sent[0, low] = (both(1, low) + wide(diag_z[...])).astype(bf16)
    y_low = wires.copy(sent.at[0, low], got_y.at[low], to["y"])
    via_y.wait_recv()
    sent[1, high] = (both(2, high) + wide(diag_y[...])).astype(bf16)
    z_high = wires.copy(sent.at[1, high], got_z.at[high], to["z"])
    yield
    from_core[0].wait_recv()
    total = wide(own[0]) + wide(got_core[0])
    for one in (y_high, z_low, y_low, z_high):
        one.wait_recv()
    return total + wide(got_y[...]) + wide(got_z[...])


def result_of(steps):
    while True:
        try:
            next(steps)
        except StopIteration as done:
            return done.value


def gather_rank(wires, to, block, out):
    size = block.shape[0] // 2
    halves = [pl.ds(0, size), pl.ds(size, size)]
    rank = ranks()
    mine = wires.here(block, out.at[rank[0]])
    from_y = [wires.copy(block.at[h], out.at[rank[0], h], to["y"]) for h in halves]
    from_core = [wires.copy(block, out.at[rank[0]], to["core"])]
    yield
    for h, one in zip(halves, from_y):
        one.wait_recv()
        from_core.append(wires.copy(out.at[rank[2], h], out.at[rank[2], h], to["core"]))
    for one in from_core:
        one.wait_recv()
    mine.wait()


def gather_pair(wires, to, block, out, base):
    size = block.shape[0] // 2
    low, high = pl.ds(0, size), pl.ds(size, size)
    at = lambda j: out.at[base + j]
    from_z = wires.copy(block, at(2), to["z"])
    yield
    from_y = wires.copy(block, at(1), to["y"])
    from_core = [wires.copy(block, at(4), to["core"])]
    yield
    from_y.wait_recv()
    via_z = wires.copy(out.at[base + 1, low], out.at[base + 3, low], to["z"])
    from_core.append(wires.copy(at(1), at(5), to["core"]))
    from_z.wait_recv()
    via_y = wires.copy(out.at[base + 2, high], out.at[base + 3, high], to["y"])
    from_core.append(wires.copy(at(2), at(6), to["core"]))
    yield
    via_z.wait_recv()
    via_y.wait_recv()
    from_core.append(wires.copy(at(3), at(7), to["core"]))
    return from_core


def remote_call(kernel, name, key, args, outs, scratch, copies, in_vmem):
    ins, out_in = in_vmem
    spec = lambda inside: pl.BlockSpec(memory_space=pltpu.VMEM if inside else pl.ANY)
    return pl.pallas_call(
        kernel,
        name=name,
        out_shape=outs,
        in_specs=[spec(x) for x in ins],
        out_specs=[spec(x) for x in out_in],
        scratch_shapes=list(scratch)
        + [
            pltpu.SemaphoreType.DMA((copies,)),
            pltpu.SemaphoreType.DMA((copies,)),
            pltpu.SemaphoreType.DMA((8,)),
        ],
        compiler_params=pltpu.CompilerParams(
            collective_id=key, has_side_effects=True, vmem_limit_bytes=VMEM_LIMIT
        ),
    )(*args)


def kv_gather_kernel(own_ref, out_ref, *sems):
    wires, to = Wires(*sems), partners()
    kind = lax.rem(lax.axis_index("tensor"), 2)
    rows = own_ref.shape[0]
    block = lambda j: out_ref.at[kind, pl.ds(j * rows, rows)]
    meet([to[k] for k in ("core", "z", "far", "last")])
    mine = wires.here(own_ref, block(0))
    arrive = [wires.copy(own_ref, block(j), to[k]) for j, k in ((3, "last"), (2, "far"), (1, "z"))]
    from_core = [wires.copy(own_ref, block(0), to["core"])]
    for j, one in ((1, arrive[2]), (2, arrive[1]), (3, arrive[0])):
        one.wait_recv()
        from_core.append(wires.copy(block(j), block(j), to["core"]))
    for one in from_core:
        one.wait_recv()
    mine.wait()
    wires.finish()


def kv_gather(own):
    rows, width = own.shape
    n_c = lax.axis_size("context")
    return remote_call(
        kv_gather_kernel,
        "kv_gather",
        0,
        [own],
        [jax.ShapeDtypeStruct((2, n_c * rows, width), bf16)],
        [],
        8,
        ([False], [False]),
    )[0]


def kv_scatter_kernel(part_ref, dkv_ref, own, got_core, sent, got, *sems):
    wires, to = Wires(*sems), partners()
    kind = lax.rem(lax.axis_index("tensor"), 2)
    rows = dkv_ref.shape[0]
    block = lambda j: pl.ds(j * rows, rows)
    meet([to[k] for k in ("core", "z", "far", "last")])
    steps = ((3, "last"), (2, "far"), (1, "z"), (0, None))
    from_core = {
        j: wires.copy(part_ref.at[1 - kind, block(j)], got_core.at[block(j)], to["core"])
        for j, _ in steps
    }
    mine = wires.here(part_ref.at[kind], own)
    mine.wait()
    arrive = []
    for j, k in steps[:3]:
        from_core[j].wait_recv()
        sent[block(j)] = (wide(own[block(j)]) + wide(got_core[block(j)])).astype(bf16)
        arrive.append(wires.copy(sent.at[block(j)], got.at[block(j)], to[k]))
    from_core[0].wait_recv()
    total = wide(own[block(0)]) + wide(got_core[block(0)])
    for one in arrive:
        one.wait_recv()
    for j in (1, 2, 3):
        total = total + wide(got[block(j)])
    dkv_ref[...] = total
    wires.finish()


def kv_scatter(part):
    _, rows, width = part.shape
    n_c = lax.axis_size("context")
    return remote_call(
        kv_scatter_kernel,
        "kv_scatter",
        1,
        [part],
        [jax.ShapeDtypeStruct((rows // n_c, width), f32)],
        [pltpu.VMEM((rows, width), bf16)] * 4,
        7,
        ([False], [True]),
    )[0]


def middle_kernel(
    part,
    x_ref,
    gain_ref,
    dy_ref,
    dy_y,
    dy_z,
    dy_far,
    mid_ref,
    factor_ref,
    out,
    dys,
    own,
    core,
    sent,
    got,
    xn,
    *sems,
):
    wires, to = Wires(*sems), partners()
    blocks = out.shape[0] // 2
    size = xn.shape[0] // 2
    low, high = pl.ds(0, size), pl.ds(size, size)
    meet([to[k] for k in ("core", "y", "z", "far")])
    summed = scatter_rank(wires, to, part, own, core, sent, got)
    next(summed)
    mine = [
        wires.here(block, dys.at[k])
        for block, k in ((dy_ref, 0), (dy_y, 1), (dy_z, 2), (dy_far, blocks))
    ]
    via_z = wires.copy(dy_y.at[low], dys.at[3, low], to["z"])
    dy_last = gather_pair(wires, to, dy_far, dys, blocks)
    next(dy_last)
    next(summed)
    via_y = wires.copy(dy_z.at[high], dys.at[3, high], to["y"])
    ends = [
        wires.copy(block, dys.at[4 + k], to["core"])
        for k, block in enumerate((dy_ref, dy_y, dy_z))
    ]
    next(dy_last)
    middle = wide(x_ref[...]) + result_of(summed)
    mid_ref[...] = middle
    factor = lax.rsqrt(jnp.mean(middle * middle, axis=-1, keepdims=True) + EPSILON)
    factor_ref[...] = factor
    xn[...] = (middle * factor * gain_ref[...]).astype(bf16)
    mine.append(wires.here(xn, out.at[0]))
    xn_far = wires.copy(xn, out.at[blocks], to["far"])
    xn_near = gather_pair(wires, to, xn, out, 0)
    next(xn_near)
    next(xn_near)
    via_z.wait_recv()
    via_y.wait_recv()
    ends.append(wires.copy(dys.at[3], dys.at[7], to["core"]))
    next(dy_last)
    next(xn_near)
    xn_far.wait_recv()
    xn_last = gather_pair(wires, to, out.at[blocks], out, blocks)
    next(xn_last)
    next(xn_last)
    ends += result_of(dy_last) + result_of(xn_near)
    next(xn_last)
    ends += result_of(xn_last)
    for one in ends:
        one.wait_recv()
    for one in mine:
        one.wait()
    wires.finish()


def middle_norm(part, inputs_part, gain, dy_blocks):
    rows, width = inputs_part.shape
    return remote_call(
        middle_kernel,
        "middle_norm",
        2,
        [part.reshape(4, rows, width), inputs_part, gain, *dy_blocks],
        [
            jax.ShapeDtypeStruct((rows, width), f32),
            jax.ShapeDtypeStruct((rows, 1), f32),
            jax.ShapeDtypeStruct((16, rows, width), bf16),
            jax.ShapeDtypeStruct((16, rows, width), bf16),
        ],
        [
            pltpu.VMEM((2, rows, width), bf16),
            pltpu.VMEM((2, rows, width), bf16),
            pltpu.VMEM((rows, width), bf16),
            pltpu.VMEM((rows, width), bf16),
            pltpu.VMEM((rows, width), bf16),
        ],
        48,
        ([False] + [True] * 6, [True, True, False, False]),
    )


def norm_back_rows(values, factor, gain, grad_normed):
    gained = gain * grad_normed
    inner = jnp.mean(gained * values, axis=-1, keepdims=True)
    grad_values = factor * gained - values * (factor * factor * factor) * inner
    return grad_values, jnp.sum(grad_normed * values * factor, axis=0, keepdims=True)


def middle_back_kernel(
    part, mid_ref, factor_ref, gain_ref, dy_ref, dmid_ref, dgain_ref, out, low, *rest
):
    first, wires, to = rest[:7], Wires(*rest[7:]), partners()
    meet([to[k] for k in ("core", "y", "z")])
    grad_normed = result_of(scatter_pair(wires, to, part, *first))
    du, dgain = norm_back_rows(mid_ref[...], factor_ref[...], gain_ref[...], grad_normed)
    dgain_ref[...] = dgain
    dmid = wide(dy_ref[...]) + du
    low[...] = dmid.astype(bf16)
    share = gather_rank(wires, to, low, out)
    next(share)
    dmid_ref[...] = dmid
    result_of(share)
    wires.finish()


def pair_scratch(rows, width):
    return [
        pltpu.VMEM((4, rows, width), bf16),
        pltpu.VMEM((4, rows, width), bf16),
        pltpu.VMEM((3, rows, width), bf16),
        pltpu.VMEM((rows, width), bf16),
        pltpu.VMEM((rows, width), bf16),
        pltpu.VMEM((rows // 2, width), bf16),
        pltpu.VMEM((rows // 2, width), bf16),
    ]


def middle_back(part, middle, factor, gain, dy_part):
    rows, width = middle.shape
    return remote_call(
        middle_back_kernel,
        "middle_back",
        3,
        [part.reshape(8, rows, width), middle, factor, gain, dy_part],
        [
            jax.ShapeDtypeStruct((rows, width), f32),
            jax.ShapeDtypeStruct((1, width), f32),
            jax.ShapeDtypeStruct((4, rows, width), bf16),
        ],
        [pltpu.VMEM((rows, width), bf16)] + pair_scratch(rows, width),
        16,
        ([False, True, True, True, True], [True, True, False]),
    )


def add_all(wires, ways, value, slots):
    for k, device in enumerate(ways):
        one = wires.copy(value, slots.at[k], device)
        one.wait()
        wires.started = [x for x in wires.started if x is not one]
        value[...] = value[...] + slots[k]


def input_back_kernel(
    part, x_ref, factor_ref, gain_ref, dmid_ref, small_ref, sum_ref, out, *rest
):
    low, own, core, sent, got, slots = rest[:-3]
    wires, to = Wires(*rest[-3:]), partners()
    meet([to[k] for k in ("core", "y")])
    grad_normed = result_of(scatter_rank(wires, to, part, own, core, sent, got))
    du, dgain = norm_back_rows(wide(x_ref[...]), factor_ref[...], gain_ref[...], grad_normed)
    low[...] = (dmid_ref[...] + du).astype(bf16)
    share = gather_rank(wires, to, low, out)
    next(share)
    width = dgain.shape[1]
    sum_ref[:, width:] = small_ref[:, width:]
    sum_ref[:, :width] = dgain
    add_all(wires, [to["core"], to["y"]], sum_ref, slots)
    result_of(share)
    wires.finish()


def input_back(part, inputs_part, factor, gain, grad_middle, small):
    rows, width = inputs_part.shape
    return remote_call(
        input_back_kernel,
        "input_back",
        5,
        [part.reshape(4, rows, width), inputs_part, factor, gain, grad_middle, small],
        [
            jax.ShapeDtypeStruct(small.shape, f32),
            jax.ShapeDtypeStruct((4, rows, width), bf16),
        ],
        [
            pltpu.VMEM((rows, width), bf16),
            pltpu.VMEM((2, rows, width), bf16),
            pltpu.VMEM((2, rows, width), bf16),
            pltpu.VMEM((rows, width), bf16),
            pltpu.VMEM((rows, width), bf16),
            pltpu.VMEM((2,) + small.shape, f32),
        ],
        16,
        ([False, True, True, True, True, True], [True, False]),
    )


def context_sum_kernel(over_f, *refs):
    parts, small_ref, out_part, mid_ref = refs[:3], refs[3], refs[4], refs[5]
    outs, sum_ref, shared, outputs = refs[6:8], refs[8], refs[9], refs[10]
    lows, from_end, from_middle = refs[11:15], refs[15:19], refs[19:23]
    out_low, slot, scratch = refs[23], refs[24], refs[25:32]
    wires, to, c = Wires(*refs[32:]), partners(), lax.axis_index("context")
    end = (c == 0) | (c == lax.axis_size("context") - 1)
    inner = jnp.logical_not(end)
    greet = ["core", "y", "z", "last"]
    if over_f:
        to["f"] = {"fsdp": 1 - lax.axis_index("fsdp")}
        greet.append("f")
    meet([to[k] for k in greet])
    ahead = scatter_pair(wires, to, out_part, *scratch)
    next(ahead)
    sum_ref[...] = small_ref[...]
    from_f = wires.copy(small_ref, slot, to["f"]) if over_f else None
    next(ahead)
    sources = [*parts, sum_ref]
    chunks = []
    for i, cuts in ((2, 1), (0, 2), (1, 2), (3, 1)):
        size = sources[i].shape[0] // cuts
        chunks += [(i, pl.ds(k * size, size)) for k in range(cuts)]
    inward = [wires.plan(sources[i].at[at], from_end[i].at[at], to["z"]) for i, at in chunks]
    across = [wires.plan(lows[i].at[at], from_middle[i].at[at], to["last"]) for i, at in chunks]
    outward = [wires.plan(lows[i].at[at], lows[i].at[at], to["z"]) for i, at in chunks]
    small = len(chunks) - 1

    def send_in(k):
        @pl.when(end)
        def _():
            inward[k].start()

    def pass_on(first, past):
        @pl.when(inner)
        def _():
            for k in range(first, past):
                i, at = chunks[k]
                inward[k].wait_recv()
                total = wide(sources[i][at]) + wide(from_end[i][at])
                lows[i][at] = total.astype(lows[i].dtype)
                across[k].start()
                if k:
                    send_out(k - 1)

    def send_out(k):
        i, at = chunks[k]
        across[k].wait()
        lows[i][at] = (wide(lows[i][at]) + wide(from_middle[i][at])).astype(lows[i].dtype)
        outward[k].start()

    send_in(0)
    send_in(1)
    next(ahead)
    if over_f:
        from_f.wait_recv()
        sum_ref[...] = sum_ref[...] + slot[...]
    for k in range(2, small + 1):
        send_in(k)
    pass_on(0, 2)
    out_low[...] = (mid_ref[...] + result_of(ahead)).astype(bf16)
    out_share = gather_rank(wires, to, out_low, outputs)
    next(out_share)
    pass_on(2, small + 1)

    @pl.when(inner)
    def _():
        send_out(small)

    result_of(out_share)

    def arrived(k):
        @pl.when(end)
        def _():
            outward[k].wait_recv()

    arrived(0)
    share = gather_rank(wires, to, lows[2], shared)
    next(share)
    for k in range(1, len(chunks)):
        arrived(k)

    @pl.when(end)
    def _():
        for one in inward:
            one.wait_send()

    for i in (0, 1):
        outs[i][...] = wide(lows[i][...])
    sum_ref[...] = lows[3][...]
    result_of(share)

    @pl.when(inner)
    def _():
        for one in outward:
            one.wait_send()

    wires.finish()


def context_sum(over_f, parts, small, out_part, middle):
    rows, width = middle.shape
    lines = [pltpu.VMEM(x.shape, x.dtype) for x in (*parts, small)]
    return remote_call(
        functools.partial(context_sum_kernel, over_f),
        "context_sum",
        6,
        [*parts, small, out_part.reshape(8, rows, width), middle],
        [jax.ShapeDtypeStruct(x.shape, f32) for x in parts[:2]]
        + [jax.ShapeDtypeStruct(small.shape, f32)]
        + [jax.ShapeDtypeStruct((4,) + parts[2].shape, bf16)]
        + [jax.ShapeDtypeStruct((4, rows, width), bf16)],
        lines * 3
        + [pltpu.VMEM((rows, width), bf16), pltpu.VMEM(small.shape, f32)]
        + pair_scratch(rows, width),
        48,
        ([True] * 4 + [False, True], [True] * 3 + [False] * 2),
    )


def build(n_f, n_c, n_t):
    def flip(x, axis, bit):
        size = {"fsdp": n_f, "context": n_c, "tensor": n_t}[axis]
        return lax.ppermute(x, axis, [(i, i ^ bit) for i in range(size)])

    def by_bit(bit, x, other, axis):
        return jnp.where(
            bit == 0,
            jnp.concatenate([x, other], axis=axis),
            jnp.concatenate([other, x], axis=axis),
        )

    def after(x, *others):
        return lax.optimization_barrier((x, others))[0]

    def local(
        inputs,
        cotangent,
        blocks,
        attn_gain,
        w_query,
        b_query,
        w_key,
        b_key,
        w_value,
        b_value,
        w_out,
        ffn_gain,
        w_gate,
        w_up,
        w_down,
    ):
        rows, width = inputs.shape
        f = lax.axis_index("fsdp")
        c = lax.axis_index("context")
        t = lax.axis_index("tensor")
        core, parity, pair = t % 2, c % 2, c // 2
        heads = w_query.shape[1] // HD
        group = (t * heads) // (H // KV)
        part = rows // n_t
        units_all = w_gate.shape[1]
        units = units_all // 2

        def gather_f(x, axis):
            if n_f == 2:
                return by_bit(f, x, flip(x, "fsdp", 1), axis)
            return lax.all_gather(x, "fsdp", axis=axis, tiled=True)

        def grad_far(left, right, side):
            if n_f > 2:
                return None
            source = (left, right)[side]
            half = width // 2
            far = lax.dynamic_slice_in_dim(source, (1 - f) * half, half, 1)
            return (dot_rows(far, right) if side == 0 else dot_rows(left, far)).astype(bf16)

        def grad_sum(left, right, side, far):
            if n_f > 2:
                return lax.psum_scatter(
                    dot_rows(left, right).astype(bf16), "fsdp", scatter_dimension=side, tiled=True
                )
            source = (left, right)[side]
            half = width // 2
            own = lax.dynamic_slice_in_dim(source, f * half, half, 1)
            own = dot_rows(own, right) if side == 0 else dot_rows(left, own)
            return (own + flip(far, "fsdp", 1).astype(f32)).astype(bf16)

        small = jnp.concatenate(
            [v.reshape(1, -1) for v in (attn_gain, ffn_gain, b_query, b_key, b_value)], axis=1
        )
        column = lambda w: lax.dynamic_slice_in_dim(w, group * HD, HD, 1)
        w_kv_own = jnp.where(core == 0, column(w_key), column(w_value))
        pieces_f = lambda x, axis: (
            [x, flip(x, "fsdp", 1)]
            if n_f == 2
            else [lax.all_gather(x, "fsdp", axis=axis, tiled=True)]
        )
        meta = jnp.stack([f, 1 - f, core, pair]).astype(jnp.int32)
        w_q = pieces_f(w_query, 0)
        w_kv = pieces_f(w_kv_own, 0)
        small = gather_f(small, 0)
        w_out_all = gather_f(after(w_out, small, w_q, w_kv), 1)
        piece = attn_gain.shape[0]
        gain_first = small[:, :piece].reshape(1, width).astype(f32)
        gain_second = small[:, piece : 2 * piece].reshape(1, width).astype(f32)
        bias_of = lambda lo, n: (
            small[:, lo : lo + n * (HD // n_f)]
            .reshape(n_f, n, HD // n_f)
            .transpose(1, 0, 2)
            .reshape(n, HD)
            .astype(f32)
        )
        at = 2 * piece
        bq = bias_of(at, heads)
        bk = bias_of(at + heads * (HD // n_f), KV)
        bv = bias_of(at + (heads + KV) * (HD // n_f), KV)
        b_kv = lax.dynamic_index_in_dim(jnp.where(core == 0, bk, bv), group, 0)

        unit_slice = lambda w: lax.dynamic_slice_in_dim(w, parity * units, units, 0)
        own_units = jnp.concatenate([unit_slice(w) for w in (w_gate.T, w_up.T, w_down)], axis=0)

        dy_part = lax.dynamic_slice_in_dim(cotangent, t * part, part, 0)

        seq_blocks = blocks[0].reshape(n_c, -1)
        own_blocks = seq_blocks.shape[1]
        key_blocks = jnp.concatenate(
            [lax.dynamic_index_in_dim(seq_blocks, c ^ j, 0, keepdims=False) for j in range(n_c)]
        )
        positions = (
            key_blocks[:own_blocks, None] * BLOCK + jnp.arange(BLOCK, dtype=jnp.int32)[None, :]
        ).reshape(-1)
        cosine, sine = rope_tables(positions)
        bias = jnp.concatenate([bq.reshape(1, -1), b_kv], axis=1)
        dy_blocks = [
            dy_part,
            flip(dy_part, "tensor", 2),
            flip(dy_part, "context", 1),
            flip(dy_part, "context", 2),
        ]
        bias = after(bias, dy_blocks)
        normed, factor_first, queries, kv_own = qkv(
            meta, inputs, gain_first, bias, cosine, sine, w_q, w_kv
        )
        w_units = pieces_f(after(own_units, kv_own, w_out_all), 1)
        kv = kv_gather(after(kv_own, w_out_all))
        attended, lse = attention(key_blocks, queries, kv)
        inputs_part = lax.dynamic_slice_in_dim(inputs, t * part, part, 0)
        middle, factor_second, normed2, dy_all = middle_norm(
            dot(attended, w_out_all).astype(bf16), inputs_part, gain_second, dy_blocks
        )

        hidden, grad_gate, grad_up, dx_part, out_part, *unit_far = ffn(
            meta, normed2, dy_all, w_units
        )
        if n_f == 2:
            down_got, gate_got, up_got = (flip(x, "fsdp", 1) for x in unit_far)
        else:
            over_f = lambda x: lax.psum_scatter(x, "fsdp", scatter_dimension=1, tiled=True)
            down_own = over_f(unit_grads(meta, 0, 1, dy_all, [hidden]))
            gate_up_own = over_f(unit_grads(meta, 0, 1, normed2, [grad_gate, grad_up]))
            down_got = gate_got = up_got = jnp.zeros_like(down_own)

        def unit_done(own, got):
            low = (own.astype(f32) + got.astype(f32)).astype(bf16)
            return low, flip(low, "context", 1)

        unit_whole = lambda low, other: by_bit(parity, low, other, 0).astype(f32)

        grad_middle, ffn_gain_grad, grad_middle_low = middle_back(
            dx_part, middle, factor_second, gain_second, dy_part
        )
        grad_middle_low = grad_middle_low.reshape(rows, width)
        if n_f == 2:
            down_own = unit_grads(meta, 0, 2, *after((dy_all, [hidden]), grad_middle_low))
        down_done = unit_done(down_own, after(down_got, grad_middle_low))
        grad_attended = dot_cols(after(grad_middle_low, down_done[0]), w_out_all).astype(bf16)

        dq_low, dkv = attention_back(key_blocks, queries, grad_attended, lse, cosine, sine, kv)
        if n_f == 2:
            gate_up_own = unit_grads(meta, 0, 2, *after((normed2, [grad_gate, grad_up]), dkv))
            dkv = after(dkv, gate_up_own)
        dkv = kv_scatter(after(dkv, down_done, gate_got))
        gate_done = unit_done(gate_up_own[:units], after(gate_got, dkv))
        up_done = unit_done(gate_up_own[units:], after(up_got, gate_done[0]))
        dkv = after(dkv, gate_done[0], up_done[0])
        dkv_low = jnp.where(core == 0, rotate_back(dkv, cosine, sine), dkv).astype(bf16)
        attention_args = (
            (attended, after(grad_middle_low, dkv), 1),
            (normed, after(dq_low, dkv), 0),
            (normed, dkv_low, 0),
        )
        fars = [grad_far(*args) for args in attention_args]
        dkv_low = after(dkv_low, fars)
        factor_part = lax.dynamic_slice_in_dim(factor_first, t * part, part, 0)
        own_biases = jnp.sum(
            jnp.concatenate([dq_low, dkv_low], axis=1).astype(f32), axis=0, keepdims=True
        )
        slots = lax.dynamic_update_slice(
            jnp.zeros((n_t, (heads + 1) * HD), f32), own_biases, (t, 0)
        )
        small_grads = jnp.concatenate(
            [jnp.zeros((1, width), f32), ffn_gain_grad, slots.reshape(1, -1)], axis=1
        )
        small_grads, input_grad = input_back(
            qkv_back(meta, dq_low, dkv_low, w_q, w_kv),
            inputs_part,
            factor_part,
            gain_first,
            grad_middle,
            small_grads,
        )
        input_grad = input_grad.reshape(rows, width)
        if n_f > 2:
            small_grads = lax.psum(small_grads, "fsdp")
        attention_parts = [grad_sum(*args, far) for args, far in zip(attention_args, fars)]
        wd_grad = unit_whole(*after(down_done, small_grads))
        wg_grad = unit_whole(*after(gate_done, small_grads))
        small_grads, up_done, wg_grad, wd_grad = lax.optimization_barrier(
            (small_grads, up_done, wg_grad, wd_grad)
        )
        wo_grad, wq_grad, packed, wkv_all, outputs = context_sum(
            n_f == 2, attention_parts, small_grads, out_part, middle
        )
        outputs = outputs.reshape(rows, width)
        wkv_all = wkv_all.astype(f32)
        wk_grad = jnp.concatenate([wkv_all[0], wkv_all[2]], axis=1)
        wv_grad = jnp.concatenate([wkv_all[1], wkv_all[3]], axis=1)
        packed = packed[0]
        attn_gain_grad = lax.dynamic_slice_in_dim(packed, f * piece, piece, 0)
        ffn_gain_grad = lax.dynamic_slice_in_dim(packed, width + f * piece, piece, 0)
        slots = packed[2 * width :].reshape(n_t, heads + 1, HD)
        slots = lax.dynamic_slice_in_dim(slots, f * (HD // n_f), HD // n_f, 2)
        bq_out = lax.dynamic_index_in_dim(slots, t, 0, keepdims=False)[:heads]
        bk_out = slots[0::2, heads]
        bv_out = slots[1::2, heads]

        wu_grad = unit_whole(*up_done)
        wg_grad, wu_grad = wg_grad.T, wu_grad.T

        return (
            outputs,
            input_grad,
            attn_gain_grad,
            wq_grad,
            bq_out,
            wk_grad,
            bk_out,
            wv_grad,
            bv_out,
            wo_grad,
            ffn_gain_grad,
            wg_grad,
            wu_grad,
            wd_grad,
        )

    return local


def solution(mesh):
    in_specs = (
        P(("fsdp", "context"), None),
        P(("fsdp", "context"), None),
        P("fsdp", None),
        P("fsdp"),
        P("fsdp", "tensor"),
        P("tensor", "fsdp"),
        P("fsdp", None),
        P(None, "fsdp"),
        P("fsdp", None),
        P(None, "fsdp"),
        P("tensor", "fsdp"),
        P("fsdp"),
        P("fsdp", "tensor"),
        P("fsdp", "tensor"),
        P("tensor", "fsdp"),
    )
    out_specs = (
        P(("fsdp", "context"), None),
        P(("fsdp", "context"), None),
        P("fsdp"),
        P("fsdp", "tensor"),
        P("tensor", "fsdp"),
        P("fsdp", None),
        P(None, "fsdp"),
        P("fsdp", None),
        P(None, "fsdp"),
        P("tensor", "fsdp"),
        P("fsdp"),
        P("fsdp", "tensor"),
        P("fsdp", "tensor"),
        P("tensor", "fsdp"),
    )
    local = build(mesh.shape["fsdp"], mesh.shape["context"], mesh.shape["tensor"])
    return jax.shard_map(local, mesh=mesh, in_specs=in_specs, out_specs=out_specs, check_vma=False)
```

```python
import functools

import jax
import jax.numpy as jnp
from jax import lax
from jax.experimental import pallas as pl
from jax.experimental.pallas import tpu as pltpu
from jax.sharding import PartitionSpec as P

H = 12
KV = 2
HD = 128
BLOCK = 256

EPSILON = 1e-06
ROPE_BASE = 1000000.0
MASKED = -1e30
SCALING = HD ** (-0.5)
LANES = 128
VMEM_LIMIT = 60 << 20
FFN_VMEM_LIMIT = 63 << 20

f32 = jnp.float32
bf16 = jnp.bfloat16


def rope_tables(positions):
    halfway = HD // 2
    frequency = ROPE_BASE ** (-(jnp.arange(halfway, dtype=f32) * 2.0 / HD))
    angles = positions.astype(f32)[:, None] * frequency[None, :]
    cosine, sine = jnp.cos(angles), jnp.sin(angles)
    return (jnp.concatenate([cosine, cosine], axis=1), jnp.concatenate([sine, sine], axis=1))


def rotate(field, cosine, sine):
    halfway = HD // 2
    turned = jnp.concatenate([-field[..., halfway:], field[..., :halfway]], axis=-1)
    return field * cosine + turned * sine


def rotate_back(grad_field, cosine, sine):
    halfway = HD // 2
    moved = grad_field * sine
    turned = jnp.concatenate([moved[..., halfway:], -moved[..., :halfway]], axis=-1)
    return grad_field * cosine + turned


def dot(left, right):
    return jnp.dot(left, right, preferred_element_type=f32)


def dot_rows(left, right):
    return lax.dot_general(left, right, (((0,), (0,)), ((), ())), preferred_element_type=f32)


def dot_cols(left, right):
    return lax.dot_general(left, right, (((1,), (1,)), ((), ())), preferred_element_type=f32)


def mask_row(kb_ref, own_block, key_blocks):
    return jnp.concatenate(
        [
            jnp.full((1, BLOCK), jnp.where(kb_ref[j] <= own_block, 0.0, MASKED), f32)
            for j in range(key_blocks)
        ],
        axis=1,
    )


def attention_kernel(key_blocks, kb_ref, q_ref, k_ref, v_ref, o_ref, lse_ref):
    bias = mask_row(kb_ref, kb_ref[pl.program_id(1)], key_blocks)
    scores = dot_cols(q_ref[...], k_ref[...]) * SCALING + bias
    row_max = jnp.max(scores, axis=1, keepdims=True)
    expo = jnp.exp(scores - row_max)
    total = jnp.sum(expo, axis=1, keepdims=True)
    probability = (expo * (1.0 / total)).astype(bf16)
    o_ref[...] = dot(probability, v_ref[...]).astype(bf16)
    lse_ref[0] = row_max + jnp.log(total)


def attention(key_blocks, queries, kv):
    rows, width = queries.shape
    heads = width // HD
    whole = lambda kind: pl.BlockSpec((None,) + kv.shape[1:], lambda h, i, kb: (kind, 0, 0))
    tile = pl.BlockSpec((BLOCK, HD), lambda h, i, kb: (i, h))
    return pl.pallas_call(
        functools.partial(attention_kernel, kv.shape[1] // BLOCK),
        name="attention",
        grid_spec=pltpu.PrefetchScalarGridSpec(
            num_scalar_prefetch=1,
            grid=(heads, rows // BLOCK),
            in_specs=[tile, whole(0), whole(1)],
            out_specs=[tile, pl.BlockSpec((1, BLOCK, 1), lambda h, i, kb: (h, i, 0))],
        ),
        out_shape=[
            jax.ShapeDtypeStruct((rows, width), bf16),
            jax.ShapeDtypeStruct((heads, rows, 1), f32),
        ],
        compiler_params=pltpu.CompilerParams(vmem_limit_bytes=VMEM_LIMIT),
    )(key_blocks, queries, kv, kv)


def attention_back_kernel(
    key_blocks,
    kb_ref,
    q_ref,
    do_ref,
    lse_ref,
    cos_ref,
    sin_ref,
    k_ref,
    v_ref,
    dq_ref,
    dkv_ref,
    dk_ref,
    dv_ref,
):
    head, i = pl.program_id(0), pl.program_id(1)

    @pl.when((head == 0) & (i == 0))
    def _():
        dk_ref[...] = jnp.zeros_like(dk_ref)
        dv_ref[...] = jnp.zeros_like(dv_ref)

    bias = mask_row(kb_ref, kb_ref[i], key_blocks)
    scores = dot_cols(q_ref[...], k_ref[...]) * SCALING + bias
    probability = jnp.exp(scores - lse_ref[0])
    grad_probs = dot_cols(do_ref[...], v_ref[...])
    inner = jnp.sum(probability * grad_probs, axis=1, keepdims=True)
    grad_scores = (probability * (grad_probs - inner)).astype(bf16)
    grad_query = dot(grad_scores, k_ref[...]) * SCALING
    moved = grad_query * sin_ref[...]
    sign = jnp.where(lax.broadcasted_iota(jnp.int32, moved.shape, 1) < HD // 2, 1.0, -1.0)
    dq_ref[...] = (
        grad_query * cos_ref[...] + pltpu.roll(moved, HD // 2, 1) * sign
    ).astype(bf16)
    dk_ref[...] += dot_rows(grad_scores, q_ref[...]) * SCALING
    dv_ref[...] += dot_rows(probability.astype(bf16), do_ref[...])

    @pl.when((head == pl.num_programs(0) - 1) & (i == pl.num_programs(1) - 1))
    def _():
        dkv_ref[0] = dk_ref[...].astype(bf16)
        dkv_ref[1] = dv_ref[...].astype(bf16)


def attention_back(key_blocks, queries, grad_out, lse, cosine, sine, kv):
    rows, width = queries.shape
    heads = width // HD
    whole = lambda kind: pl.BlockSpec((None,) + kv.shape[1:], lambda h, i, kb: (kind, 0, 0))
    tile = pl.BlockSpec((BLOCK, HD), lambda h, i, kb: (i, h))
    table = pl.BlockSpec((BLOCK, HD), lambda h, i, kb: (i, 0))
    return pl.pallas_call(
        functools.partial(attention_back_kernel, kv.shape[1] // BLOCK),
        name="attention_back",
        grid_spec=pltpu.PrefetchScalarGridSpec(
            num_scalar_prefetch=1,
            grid=(heads, rows // BLOCK),
            in_specs=[
                tile,
                tile,
                pl.BlockSpec((1, BLOCK, 1), lambda h, i, kb: (h, i, 0)),
                table,
                table,
                whole(0),
                whole(1),
            ],
            out_specs=[tile, pl.BlockSpec(kv.shape, lambda h, i, kb: (0, 0, 0))],
            scratch_shapes=[pltpu.VMEM(kv.shape[1:], f32)] * 2,
        ),
        out_shape=[
            jax.ShapeDtypeStruct((rows, width), bf16),
            jax.ShapeDtypeStruct(kv.shape, bf16),
        ],
        compiler_params=pltpu.CompilerParams(vmem_limit_bytes=VMEM_LIMIT),
    )(key_blocks, queries, grad_out, lse, cosine, sine, kv, kv)


def qkv_kernel(pieces, meta_ref, x_ref, gain_ref, bias_ref, cos_ref, sin_ref, *refs):
    weights, (xn_ref, factor_ref, q_ref, kv_ref) = refs[: 2 * pieces], refs[2 * pieces :]
    values = x_ref[...].astype(f32)
    factor = lax.rsqrt(jnp.mean(values * values, axis=-1, keepdims=True) + EPSILON)
    factor_ref[...] = factor
    xn_ref[...] = (values * factor * gain_ref[...]).astype(bf16)
    depth = weights[0].shape[0]
    normed = [xn_ref[:, columns_of(meta_ref, j, depth, pieces)] for j in range(pieces)]
    cosine, sine = cos_ref[...], sin_ref[...]
    sign = jnp.where(lax.broadcasted_iota(jnp.int32, cosine.shape, 1) < HD // 2, -1.0, 1.0)
    sine = sine * sign
    width = q_ref.shape[1]
    total = bias_ref[:, :width] + sum(dot(x, w[...]) for x, w in zip(normed, weights[:pieces]))
    turn = lambda own: own * cosine + pltpu.roll(own, HD // 2, 1) * sine
    for h in range(width // HD):
        q_ref[:, h * HD : (h + 1) * HD] = turn(total[:, h * HD : (h + 1) * HD]).astype(bf16)
    own = bias_ref[:, width:] + sum(dot(x, w[...]) for x, w in zip(normed, weights[pieces:]))
    kv_ref[...] = jnp.where(meta_ref[2] == 0, turn(own), own).astype(bf16)


def columns_of(meta_ref, j, depth, pieces):
    if pieces == 1:
        return slice(None)
    return pl.ds(pl.multiple_of(meta_ref[j] * depth, LANES), depth)


def qkv(meta, inputs, gain, bias, cosine, sine, w_q, w_kv):
    rows, width = inputs.shape
    out = w_q[0].shape[1]
    tile = 256
    row = lambda n: pl.BlockSpec((tile, n), lambda i, m: (i, 0))
    fixed = lambda w: pl.BlockSpec(w.shape, lambda i, m: (0, 0))
    return pl.pallas_call(
        functools.partial(qkv_kernel, len(w_q)),
        name="qkv",
        grid_spec=pltpu.PrefetchScalarGridSpec(
            num_scalar_prefetch=1,
            grid=(rows // tile,),
            in_specs=[row(width), fixed(gain), fixed(bias), row(HD), row(HD)]
            + [fixed(w) for w in (*w_q, *w_kv)],
            out_specs=[row(width), row(1), row(out), row(HD)],
        ),
        out_shape=[
            jax.ShapeDtypeStruct((rows, width), bf16),
            jax.ShapeDtypeStruct((rows, 1), f32),
            jax.ShapeDtypeStruct((rows, out), bf16),
            jax.ShapeDtypeStruct((rows, HD), bf16),
        ],
        compiler_params=pltpu.CompilerParams(vmem_limit_bytes=VMEM_LIMIT),
    )(meta, inputs, gain, bias, cosine, sine, *w_q, *w_kv)


def qkv_back_kernel(pieces, meta_ref, dq_ref, dkv_ref, *refs):
    w_q, w_kv, out_ref = refs[:pieces], refs[pieces : 2 * pieces], refs[-1]
    for j in range(pieces):
        out_ref[:, columns_of(meta_ref, j, w_q[j].shape[0], pieces)] = (
            dot_cols(dq_ref[...], w_q[j][...]) + dot_cols(dkv_ref[...], w_kv[j][...])
        ).astype(bf16)


def qkv_back(meta, grad_q, grad_kv, w_q, w_kv):
    rows, width = grad_q.shape[0], sum(w.shape[0] for w in w_q)
    tile = 256
    row = lambda n: pl.BlockSpec((tile, n), lambda i, m: (i, 0))
    fixed = lambda w: pl.BlockSpec(w.shape, lambda i, m: (0, 0))
    return pl.pallas_call(
        functools.partial(qkv_back_kernel, len(w_q)),
        name="qkv_back",
        grid_spec=pltpu.PrefetchScalarGridSpec(
            num_scalar_prefetch=1,
            grid=(rows // tile,),
            in_specs=[row(grad_q.shape[1]), row(HD)] + [fixed(w) for w in (*w_q, *w_kv)],
            out_specs=row(width),
        ),
        out_shape=jax.ShapeDtypeStruct((rows, width), bf16),
        compiler_params=pltpu.CompilerParams(vmem_limit_bytes=VMEM_LIMIT),
    )(meta, grad_q, grad_kv, *w_q, *w_kv)


def ffn_kernel(pieces, meta_ref, x_ref, dy_ref, *refs):
    wg, wu, wd = (refs[m * pieces : (m + 1) * pieces] for m in range(3))
    refs = refs[3 * pieces :]
    hid_ref, dg_ref, du_ref, dx_ref, out_ref = refs[:5]
    columns = [columns_of(meta_ref, j, wg[j].shape[1], pieces) for j in range(pieces)]
    gate = sum(dot_cols(x_ref[:, at], w[...]) for at, w in zip(columns, wg))
    up = sum(dot_cols(x_ref[:, at], w[...]) for at, w in zip(columns, wu))
    grad_hidden = sum(dot_cols(dy_ref[:, at], w[...]) for at, w in zip(columns, wd))
    sigma = 1.0 / (1.0 + jnp.exp(-gate))
    gated = gate * sigma
    hid_ref[...] = (gated * up).astype(bf16)
    dg_ref[...] = (grad_hidden * up * (sigma + gated * (1.0 - sigma))).astype(bf16)
    du_ref[...] = (grad_hidden * gated).astype(bf16)
    step, steps = pl.program_id(0), pl.num_programs(0)

    @pl.when(step // (steps // 2) == meta_ref[3])
    def _():
        for at, g, u, d in zip(columns, wg, wu, wd):
            dx_ref[:, at] = (dot(dg_ref[...], g[...]) + dot(du_ref[...], u[...])).astype(bf16)
            out_ref[:, at] = dot(hid_ref[...], d[...]).astype(bf16)

    if pieces == 2:
        outs, totals = refs[5:8], refs[8:11]
        sources = ((hid_ref, dy_ref), (dg_ref, x_ref), (du_ref, x_ref))

        @pl.when(step == 0)
        def _():
            for total in totals:
                total[...] = jnp.zeros_like(total)

        for total, (unit, row) in zip(totals, sources):
            total[...] += dot_rows(unit[...], row[:, columns[1]])

        @pl.when(step == steps - 1)
        def _():
            for out, total in zip(outs, totals):
                out[...] = total[...].astype(bf16)


def ffn(meta, normed, grad_out, weights):
    width = normed.shape[-1]
    rows = normed.shape[0] * normed.shape[1]
    pieces = len(weights)
    units, depth = weights[0][1].shape
    tile = 512
    steps = rows // tile
    half = steps // 2
    flat = lambda x: x.reshape(-1, width)
    read = pl.BlockSpec((tile, width), lambda i, m: (lax.rem(i + m[3] * half, steps), 0))
    once = pl.Buffered(1)
    weight = lambda k: pl.BlockSpec((units, depth), lambda i, m: (k, 0), pipeline_mode=once)
    placed = pl.BlockSpec((tile, units), lambda i, m: (i, 0))
    near = pl.BlockSpec((tile, width), lambda i, m: (jnp.clip(i - m[3] * half, 0, half - 1), 0))
    grads = [pl.BlockSpec((units, depth), lambda i, m: (0, 0), pipeline_mode=once)] * 3
    grads = grads if pieces == 2 else []
    shapes = [(rows, units)] * 3 + [(rows // 2, width)] * 2 + [(units, depth)] * len(grads)
    return pl.pallas_call(
        functools.partial(ffn_kernel, pieces),
        name="ffn",
        grid_spec=pltpu.PrefetchScalarGridSpec(
            num_scalar_prefetch=1,
            grid=(steps,),
            in_specs=[read, read] + [weight(k) for k in (0, 1, 0) for _ in weights],
            out_specs=[placed] * 3 + [near] * 2 + grads,
            scratch_shapes=[pltpu.VMEM((units, depth), f32)] * len(grads),
        ),
        out_shape=[jax.ShapeDtypeStruct(shape, bf16) for shape in shapes],
        compiler_params=pltpu.CompilerParams(vmem_limit_bytes=FFN_VMEM_LIMIT),
    )(meta, flat(normed), flat(grad_out), *[w[k] for k in (0, 0, 1) for w in weights])


def unit_grads_kernel(count, meta_ref, near_ref, far_ref, *refs):
    units, out_ref, x_ref = refs[:count], refs[-2], refs[-1]
    half = near_ref.shape[0]
    x_ref[pl.ds(pl.multiple_of(meta_ref[3] * half, half), half)] = near_ref[...]
    x_ref[pl.ds(pl.multiple_of((1 - meta_ref[3]) * half, half), half)] = far_ref[...]
    for k, unit in enumerate(units):
        depth = unit.shape[1]
        out_ref[k * depth : (k + 1) * depth] = dot_rows(unit[...], x_ref[...]).astype(bf16)


def unit_grads(meta, which, pieces, x, units_of):
    width = x.shape[-1]
    count, (rows, units) = len(units_of), units_of[0].shape
    depth = width // pieces
    tile = 256
    steps = depth // tile
    shard = (lambda m: m[which]) if pieces > 1 else (lambda m: 0)
    feature = lambda half: pl.BlockSpec(
        (rows // 2, tile), lambda i, m: (half, shard(m) * steps + i)
    )
    unit = pl.BlockSpec((rows, units), lambda i, m: (0, 0), pipeline_mode=pl.Buffered(1))
    x = x.reshape(-1, width)
    return pl.pallas_call(
        functools.partial(unit_grads_kernel, count),
        name=f"unit_grads_{which}_{count}",
        grid_spec=pltpu.PrefetchScalarGridSpec(
            num_scalar_prefetch=1,
            grid=(steps,),
            in_specs=[feature(0), feature(1)] + [unit] * count,
            out_specs=pl.BlockSpec((count * units, tile), lambda i, m: (0, i)),
            scratch_shapes=[pltpu.VMEM((rows, tile), bf16)],
        ),
        out_shape=jax.ShapeDtypeStruct((count * units, depth), bf16),
        compiler_params=pltpu.CompilerParams(vmem_limit_bytes=VMEM_LIMIT),
    )(meta, x, x, *units_of)


class Wires:
    def __init__(self, sends, receives, locals_):
        self.sends, self.receives, self.locals = sends, receives, locals_
        self.used = self.used_local = 0
        self.started = []

    def plan(self, source, target, device):
        k = self.used
        self.used += 1
        return pltpu.make_async_remote_copy(
            source,
            target,
            self.sends.at[k],
            self.receives.at[k],
            device_id=device,
            device_id_type=pl.DeviceIdType.MESH,
        )

    def copy(self, source, target, device):
        one = self.plan(source, target, device)
        one.start()
        self.started.append(one)
        return one

    def here(self, source, target):
        k = self.used_local
        self.used_local += 1
        one = pltpu.make_async_copy(source, target, self.locals.at[k])
        one.start()
        return one

    def finish(self):
        for one in self.started:
            one.wait_send()


def meet(devices):
    barrier = pltpu.get_barrier_semaphore()
    for device in devices:
        pl.semaphore_signal(barrier, inc=1, device_id=device, device_id_type=pl.DeviceIdType.MESH)
    pl.semaphore_wait(barrier, len(devices))


def partners():
    c, t = lax.axis_index("context"), lax.axis_index("tensor")
    flip = lambda x, bit: x + bit * (1 - 2 * lax.rem(x // bit, 2))
    return {
        "core": {"tensor": flip(t, 1)},
        "y": {"tensor": flip(t, 2)},
        "z": {"context": flip(c, 1)},
        "far": {"context": flip(c, 2)},
        "last": {"context": flip(flip(c, 1), 2)},
    }


def wide(x):
    return x.astype(f32)


def ranks():
    t = lax.axis_index("tensor")
    flip = lambda x, bit: x + bit * (1 - 2 * lax.rem(x // bit, 2))
    return (t, flip(t, 1), flip(t, 2), flip(flip(t, 1), 2))


def scatter_rank(wires, to, part, own, got_core, sent, got_y):
    size = part.shape[1] // 2
    halves = [pl.ds(0, size), pl.ds(size, size)]
    rank = ranks()
    from_core = {}
    for block in (1, 0):
        for k, at in enumerate(halves):
            from_core[block, k] = wires.copy(
                part.at[rank[1 + 2 * block], at], got_core.at[block, at], to["core"]
            )
    mine = [wires.here(part.at[rank[2 * block]], own.at[block]) for block in (0, 1)]
    yield
    for one in mine:
        one.wait()
    from_y = []
    for k, at in enumerate(halves):
        from_core[1, k].wait_recv()
        sent[at] = (wide(own[1, at]) + wide(got_core[1, at])).astype(bf16)
        from_y.append(wires.copy(sent.at[at], got_y.at[at], to["y"]))
    yield
    for k in range(2):
        from_core[0, k].wait_recv()
    total = wide(own[0]) + wide(got_core[0])
    for one in from_y:
        one.wait_recv()
    return total + wide(got_y[...])


def scatter_pair(wires, to, part, own, got_core, sent, got_y, got_z, diag_y, diag_z):
    size = part.shape[1] // 2
    low, high = pl.ds(0, size), pl.ds(size, size)
    from_core = {j: wires.copy(part.at[4 + j], got_core.at[j], to["core"]) for j in (3, 1, 2, 0)}
    mine = wires.here(part.at[pl.ds(0, 4)], own)
    yield
    mine.wait()
    both = lambda j, at: wide(own[j, at]) + wide(got_core[j, at])
    from_core[3].wait_recv()
    sent[2] = (wide(own[3]) + wide(got_core[3])).astype(bf16)
    via_z = wires.copy(sent.at[2, low], diag_z, to["z"])
    via_y = wires.copy(sent.at[2, high], diag_y, to["y"])
    from_core[1].wait_recv()
    sent[0, high] = both(1, high).astype(bf16)
    y_high = wires.copy(sent.at[0, high], got_y.at[high], to["y"])
    from_core[2].wait_recv()
    sent[1, low] = both(2, low).astype(bf16)
    z_low = wires.copy(sent.at[1, low], got_z.at[low], to["z"])
    yield
    via_z.wait_recv()
    sent[0, low] = (both(1, low) + wide(diag_z[...])).astype(bf16)
    y_low = wires.copy(sent.at[0, low], got_y.at[low], to["y"])
    via_y.wait_recv()
    sent[1, high] = (both(2, high) + wide(diag_y[...])).astype(bf16)
    z_high = wires.copy(sent.at[1, high], got_z.at[high], to["z"])
    yield
    from_core[0].wait_recv()
    total = wide(own[0]) + wide(got_core[0])
    for one in (y_high, z_low, y_low, z_high):
        one.wait_recv()
    return total + wide(got_y[...]) + wide(got_z[...])


def result_of(steps):
    while True:
        try:
            next(steps)
        except StopIteration as done:
            return done.value


def gather_rank(wires, to, block, out):
    size = block.shape[0] // 2
    halves = [pl.ds(0, size), pl.ds(size, size)]
    rank = ranks()
    mine = wires.here(block, out.at[rank[0]])
    from_y = [wires.copy(block.at[h], out.at[rank[0], h], to["y"]) for h in halves]
    from_core = [wires.copy(block, out.at[rank[0]], to["core"])]
    yield
    for h, one in zip(halves, from_y):
        one.wait_recv()
        from_core.append(wires.copy(out.at[rank[2], h], out.at[rank[2], h], to["core"]))
    for one in from_core:
        one.wait_recv()
    mine.wait()


def gather_pair(wires, to, block, out, base):
    size = block.shape[0] // 2
    low, high = pl.ds(0, size), pl.ds(size, size)
    at = lambda j: out.at[base + j]
    from_z = wires.copy(block, at(2), to["z"])
    yield
    from_y = wires.copy(block, at(1), to["y"])
    from_core = [wires.copy(block, at(4), to["core"])]
    yield
    from_y.wait_recv()
    via_z = wires.copy(out.at[base + 1, low], out.at[base + 3, low], to["z"])
    from_core.append(wires.copy(at(1), at(5), to["core"]))
    from_z.wait_recv()
    via_y = wires.copy(out.at[base + 2, high], out.at[base + 3, high], to["y"])
    from_core.append(wires.copy(at(2), at(6), to["core"]))
    yield
    via_z.wait_recv()
    via_y.wait_recv()
    from_core.append(wires.copy(at(3), at(7), to["core"]))
    return from_core


def remote_call(kernel, name, key, args, outs, scratch, copies, in_vmem):
    ins, out_in = in_vmem
    spec = lambda inside: pl.BlockSpec(memory_space=pltpu.VMEM if inside else pl.ANY)
    return pl.pallas_call(
        kernel,
        name=name,
        out_shape=outs,
        in_specs=[spec(x) for x in ins],
        out_specs=[spec(x) for x in out_in],
        scratch_shapes=list(scratch)
        + [
            pltpu.SemaphoreType.DMA((copies,)),
            pltpu.SemaphoreType.DMA((copies,)),
            pltpu.SemaphoreType.DMA((8,)),
        ],
        compiler_params=pltpu.CompilerParams(
            collective_id=key, has_side_effects=True, vmem_limit_bytes=VMEM_LIMIT
        ),
    )(*args)


def kv_gather_kernel(own_ref, out_ref, *sems):
    wires, to = Wires(*sems), partners()
    kind = lax.rem(lax.axis_index("tensor"), 2)
    rows = own_ref.shape[0]
    block = lambda j: out_ref.at[kind, pl.ds(j * rows, rows)]
    meet([to[k] for k in ("core", "z", "far", "last")])
    mine = wires.here(own_ref, block(0))
    arrive = [wires.copy(own_ref, block(j), to[k]) for j, k in ((3, "last"), (2, "far"), (1, "z"))]
    from_core = [wires.copy(own_ref, block(0), to["core"])]
    for j, one in ((1, arrive[2]), (2, arrive[1]), (3, arrive[0])):
        one.wait_recv()
        from_core.append(wires.copy(block(j), block(j), to["core"]))
    for one in from_core:
        one.wait_recv()
    mine.wait()
    wires.finish()


def kv_gather(own):
    rows, width = own.shape
    n_c = lax.axis_size("context")
    return remote_call(
        kv_gather_kernel,
        "kv_gather",
        0,
        [own],
        [jax.ShapeDtypeStruct((2, n_c * rows, width), bf16)],
        [],
        8,
        ([False], [False]),
    )[0]


def kv_scatter_kernel(part_ref, dkv_ref, own, got_core, sent, got, *sems):
    wires, to = Wires(*sems), partners()
    kind = lax.rem(lax.axis_index("tensor"), 2)
    rows = dkv_ref.shape[0]
    block = lambda j: pl.ds(j * rows, rows)
    meet([to[k] for k in ("core", "z", "far", "last")])
    steps = ((3, "last"), (2, "far"), (1, "z"), (0, None))
    from_core = {
        j: wires.copy(part_ref.at[1 - kind, block(j)], got_core.at[block(j)], to["core"])
        for j, _ in steps
    }
    mine = wires.here(part_ref.at[kind], own)
    mine.wait()
    arrive = []
    for j, k in steps[:3]:
        from_core[j].wait_recv()
        sent[block(j)] = (wide(own[block(j)]) + wide(got_core[block(j)])).astype(bf16)
        arrive.append(wires.copy(sent.at[block(j)], got.at[block(j)], to[k]))
    from_core[0].wait_recv()
    total = wide(own[block(0)]) + wide(got_core[block(0)])
    for one in arrive:
        one.wait_recv()
    for j in (1, 2, 3):
        total = total + wide(got[block(j)])
    dkv_ref[...] = total
    wires.finish()


def kv_scatter(part):
    _, rows, width = part.shape
    n_c = lax.axis_size("context")
    return remote_call(
        kv_scatter_kernel,
        "kv_scatter",
        1,
        [part],
        [jax.ShapeDtypeStruct((rows // n_c, width), f32)],
        [pltpu.VMEM((rows, width), bf16)] * 4,
        7,
        ([False], [True]),
    )[0]


def middle_kernel(
    part,
    x_ref,
    gain_ref,
    dy_ref,
    dy_y,
    dy_z,
    mid_ref,
    factor_ref,
    out,
    dys,
    own,
    core,
    sent,
    got,
    xn,
    *sems,
):
    wires, to = Wires(*sems), partners()
    blocks = out.shape[0] // 2
    size = xn.shape[0] // 2
    low, high = pl.ds(0, size), pl.ds(size, size)
    meet([to[k] for k in ("core", "y", "z", "far")])
    summed = scatter_rank(wires, to, part, own, core, sent, got)
    next(summed)
    mine = [
        wires.here(block, dys.at[k])
        for block, k in ((dy_ref, 0), (dy_y, 1), (dy_z, 2))
    ]
    dy_far = wires.copy(dy_ref, dys.at[blocks], to["far"])
    via_z = wires.copy(dy_y.at[low], dys.at[3, low], to["z"])
    next(summed)
    via_y = wires.copy(dy_z.at[high], dys.at[3, high], to["y"])
    ends = [
        wires.copy(block, dys.at[4 + k], to["core"])
        for k, block in enumerate((dy_ref, dy_y, dy_z))
    ]
    middle = wide(x_ref[...]) + result_of(summed)
    mid_ref[...] = middle
    factor = lax.rsqrt(jnp.mean(middle * middle, axis=-1, keepdims=True) + EPSILON)
    factor_ref[...] = factor
    xn[...] = (middle * factor * gain_ref[...]).astype(bf16)
    mine.append(wires.here(xn, out.at[0]))
    xn_far = wires.copy(xn, out.at[blocks], to["far"])
    xn_near = gather_pair(wires, to, xn, out, 0)
    next(xn_near)
    next(xn_near)
    via_z.wait_recv()
    via_y.wait_recv()
    ends.append(wires.copy(dys.at[3], dys.at[7], to["core"]))
    next(xn_near)
    dy_far.wait_recv()
    dy_last = gather_pair(wires, to, dys.at[blocks], dys, blocks)
    next(dy_last)
    next(dy_last)
    xn_far.wait_recv()
    xn_last = gather_pair(wires, to, out.at[blocks], out, blocks)
    next(xn_last)
    next(xn_last)
    ends += result_of(xn_near)
    next(dy_last)
    next(xn_last)
    ends += result_of(dy_last) + result_of(xn_last)
    for one in ends:
        one.wait_recv()
    for one in mine:
        one.wait()
    wires.finish()


def middle_norm(part, inputs_part, gain, dy_blocks):
    rows, width = inputs_part.shape
    return remote_call(
        middle_kernel,
        "middle_norm",
        2,
        [part.reshape(4, rows, width), inputs_part, gain, *dy_blocks],
        [
            jax.ShapeDtypeStruct((rows, width), f32),
            jax.ShapeDtypeStruct((rows, 1), f32),
            jax.ShapeDtypeStruct((16, rows, width), bf16),
            jax.ShapeDtypeStruct((16, rows, width), bf16),
        ],
        [
            pltpu.VMEM((2, rows, width), bf16),
            pltpu.VMEM((2, rows, width), bf16),
            pltpu.VMEM((rows, width), bf16),
            pltpu.VMEM((rows, width), bf16),
            pltpu.VMEM((rows, width), bf16),
        ],
        48,
        ([False] + [True] * 5, [True, True, False, False]),
    )


def norm_back_rows(values, factor, gain, grad_normed):
    gained = gain * grad_normed
    inner = jnp.mean(gained * values, axis=-1, keepdims=True)
    grad_values = factor * gained - values * (factor * factor * factor) * inner
    return grad_values, jnp.sum(grad_normed * values * factor, axis=0, keepdims=True)


def middle_back_kernel(
    part, mid_ref, factor_ref, gain_ref, dy_ref, dmid_ref, dgain_ref, out, low, *rest
):
    first, wires, to = rest[:7], Wires(*rest[7:]), partners()
    meet([to[k] for k in ("core", "y", "z")])
    grad_normed = result_of(scatter_pair(wires, to, part, *first))
    du, dgain = norm_back_rows(mid_ref[...], factor_ref[...], gain_ref[...], grad_normed)
    dgain_ref[...] = dgain
    dmid = wide(dy_ref[...]) + du
    low[...] = dmid.astype(bf16)
    share = gather_rank(wires, to, low, out)
    next(share)
    dmid_ref[...] = dmid
    result_of(share)
    wires.finish()


def pair_scratch(rows, width):
    return [
        pltpu.VMEM((4, rows, width), bf16),
        pltpu.VMEM((4, rows, width), bf16),
        pltpu.VMEM((3, rows, width), bf16),
        pltpu.VMEM((rows, width), bf16),
        pltpu.VMEM((rows, width), bf16),
        pltpu.VMEM((rows // 2, width), bf16),
        pltpu.VMEM((rows // 2, width), bf16),
    ]


def middle_back(part, middle, factor, gain, dy_part):
    rows, width = middle.shape
    return remote_call(
        middle_back_kernel,
        "middle_back",
        3,
        [part.reshape(8, rows, width), middle, factor, gain, dy_part],
        [
            jax.ShapeDtypeStruct((rows, width), f32),
            jax.ShapeDtypeStruct((1, width), f32),
            jax.ShapeDtypeStruct((4, rows, width), bf16),
        ],
        [pltpu.VMEM((rows, width), bf16)] + pair_scratch(rows, width),
        16,
        ([False, True, True, True, True], [True, True, False]),
    )


def add_all(wires, ways, value, slots):
    for k, device in enumerate(ways):
        one = wires.copy(value, slots.at[k], device)
        one.wait()
        wires.started = [x for x in wires.started if x is not one]
        value[...] = value[...] + slots[k]


def input_back_kernel(
    part, x_ref, factor_ref, gain_ref, dmid_ref, small_ref, sum_ref, out, *rest
):
    low, own, core, sent, got, slots = rest[:-3]
    wires, to = Wires(*rest[-3:]), partners()
    meet([to[k] for k in ("core", "y")])
    grad_normed = result_of(scatter_rank(wires, to, part, own, core, sent, got))
    du, dgain = norm_back_rows(wide(x_ref[...]), factor_ref[...], gain_ref[...], grad_normed)
    low[...] = (dmid_ref[...] + du).astype(bf16)
    share = gather_rank(wires, to, low, out)
    next(share)
    width = dgain.shape[1]
    sum_ref[:, width:] = small_ref[:, width:]
    sum_ref[:, :width] = dgain
    add_all(wires, [to["core"], to["y"]], sum_ref, slots)
    result_of(share)
    wires.finish()


def input_back(part, inputs_part, factor, gain, grad_middle, small):
    rows, width = inputs_part.shape
    return remote_call(
        input_back_kernel,
        "input_back",
        5,
        [part.reshape(4, rows, width), inputs_part, factor, gain, grad_middle, small],
        [
            jax.ShapeDtypeStruct(small.shape, f32),
            jax.ShapeDtypeStruct((4, rows, width), bf16),
        ],
        [
            pltpu.VMEM((rows, width), bf16),
            pltpu.VMEM((2, rows, width), bf16),
            pltpu.VMEM((2, rows, width), bf16),
            pltpu.VMEM((rows, width), bf16),
            pltpu.VMEM((rows, width), bf16),
            pltpu.VMEM((2,) + small.shape, f32),
        ],
        16,
        ([False, True, True, True, True, True], [True, False]),
    )


def context_sum_kernel(over_f, *refs):
    parts, small_ref, out_part, mid_ref = refs[:3], refs[3], refs[4], refs[5]
    outs, sum_ref, shared, outputs = refs[6:8], refs[8], refs[9], refs[10]
    lows, from_end, from_middle = refs[11:15], refs[15:19], refs[19:23]
    out_low, slot, scratch = refs[23], refs[24], refs[25:32]
    wires, to, c = Wires(*refs[32:]), partners(), lax.axis_index("context")
    end = (c == 0) | (c == lax.axis_size("context") - 1)
    inner = jnp.logical_not(end)
    greet = ["core", "y", "z", "last"]
    if over_f:
        to["f"] = {"fsdp": 1 - lax.axis_index("fsdp")}
        greet.append("f")
    meet([to[k] for k in greet])
    ahead = scatter_pair(wires, to, out_part, *scratch)
    next(ahead)
    sum_ref[...] = small_ref[...]
    from_f = wires.copy(small_ref, slot, to["f"]) if over_f else None
    next(ahead)
    sources = [*parts, sum_ref]
    chunks = []
    for i, cuts in ((2, 1), (0, 2), (1, 2), (3, 1)):
        size = sources[i].shape[0] // cuts
        chunks += [(i, pl.ds(k * size, size)) for k in range(cuts)]
    inward = [wires.plan(sources[i].at[at], from_end[i].at[at], to["z"]) for i, at in chunks]
    across = [wires.plan(lows[i].at[at], from_middle[i].at[at], to["last"]) for i, at in chunks]
    outward = [wires.plan(lows[i].at[at], lows[i].at[at], to["z"]) for i, at in chunks]
    small = len(chunks) - 1

    def send_in(k):
        @pl.when(end)
        def _():
            inward[k].start()

    def pass_on(first, past):
        @pl.when(inner)
        def _():
            for k in range(first, past):
                i, at = chunks[k]
                inward[k].wait_recv()
                total = wide(sources[i][at]) + wide(from_end[i][at])
                lows[i][at] = total.astype(lows[i].dtype)
                across[k].start()
                if k:
                    send_out(k - 1)

    def send_out(k):
        i, at = chunks[k]
        across[k].wait()
        lows[i][at] = (wide(lows[i][at]) + wide(from_middle[i][at])).astype(lows[i].dtype)
        outward[k].start()

    send_in(0)
    send_in(1)
    next(ahead)
    if over_f:
        from_f.wait_recv()
        sum_ref[...] = sum_ref[...] + slot[...]
    for k in range(2, small + 1):
        send_in(k)
    pass_on(0, 2)
    out_low[...] = (mid_ref[...] + result_of(ahead)).astype(bf16)
    out_share = gather_rank(wires, to, out_low, outputs)
    next(out_share)
    pass_on(2, small + 1)

    @pl.when(inner)
    def _():
        send_out(small)

    result_of(out_share)

    def arrived(k):
        @pl.when(end)
        def _():
            outward[k].wait_recv()

    arrived(0)
    share = gather_rank(wires, to, lows[2], shared)
    next(share)
    for k in range(1, len(chunks)):
        arrived(k)

    @pl.when(end)
    def _():
        for one in inward:
            one.wait_send()

    for i in (0, 1):
        outs[i][...] = wide(lows[i][...])
    sum_ref[...] = lows[3][...]
    result_of(share)

    @pl.when(inner)
    def _():
        for one in outward:
            one.wait_send()

    wires.finish()


def context_sum(over_f, parts, small, out_part, middle):
    rows, width = middle.shape
    lines = [pltpu.VMEM(x.shape, x.dtype) for x in (*parts, small)]
    return remote_call(
        functools.partial(context_sum_kernel, over_f),
        "context_sum",
        6,
        [*parts, small, out_part.reshape(8, rows, width), middle],
        [jax.ShapeDtypeStruct(x.shape, f32) for x in parts[:2]]
        + [jax.ShapeDtypeStruct(small.shape, f32)]
        + [jax.ShapeDtypeStruct((4,) + parts[2].shape, bf16)]
        + [jax.ShapeDtypeStruct((4, rows, width), bf16)],
        lines * 3
        + [pltpu.VMEM((rows, width), bf16), pltpu.VMEM(small.shape, f32)]
        + pair_scratch(rows, width),
        48,
        ([True] * 4 + [False, True], [True] * 3 + [False] * 2),
    )


def build(n_f, n_c, n_t):
    def flip(x, axis, bit):
        size = {"fsdp": n_f, "context": n_c, "tensor": n_t}[axis]
        return lax.ppermute(x, axis, [(i, i ^ bit) for i in range(size)])

    def by_bit(bit, x, other, axis):
        return jnp.where(
            bit == 0,
            jnp.concatenate([x, other], axis=axis),
            jnp.concatenate([other, x], axis=axis),
        )

    def after(x, *others):
        return lax.optimization_barrier((x, others))[0]

    def local(
        inputs,
        cotangent,
        blocks,
        attn_gain,
        w_query,
        b_query,
        w_key,
        b_key,
        w_value,
        b_value,
        w_out,
        ffn_gain,
        w_gate,
        w_up,
        w_down,
    ):
        rows, width = inputs.shape
        f = lax.axis_index("fsdp")
        c = lax.axis_index("context")
        t = lax.axis_index("tensor")
        core, parity, pair = t % 2, c % 2, c // 2
        heads = w_query.shape[1] // HD
        group = (t * heads) // (H // KV)
        part = rows // n_t
        units_all = w_gate.shape[1]
        units = units_all // 2

        def gather_f(x, axis):
            if n_f == 2:
                return by_bit(f, x, flip(x, "fsdp", 1), axis)
            return lax.all_gather(x, "fsdp", axis=axis, tiled=True)

        def grad_far(left, right, side):
            if n_f > 2:
                return None
            source = (left, right)[side]
            half = width // 2
            far = lax.dynamic_slice_in_dim(source, (1 - f) * half, half, 1)
            return (dot_rows(far, right) if side == 0 else dot_rows(left, far)).astype(bf16)

        def grad_sum(left, right, side, far):
            if n_f > 2:
                return lax.psum_scatter(
                    dot_rows(left, right).astype(bf16), "fsdp", scatter_dimension=side, tiled=True
                )
            source = (left, right)[side]
            half = width // 2
            own = lax.dynamic_slice_in_dim(source, f * half, half, 1)
            own = dot_rows(own, right) if side == 0 else dot_rows(left, own)
            return (own + flip(far, "fsdp", 1).astype(f32)).astype(bf16)

        small = jnp.concatenate(
            [v.reshape(1, -1) for v in (attn_gain, ffn_gain, b_query, b_key, b_value)], axis=1
        )
        column = lambda w: lax.dynamic_slice_in_dim(w, group * HD, HD, 1)
        w_kv_own = jnp.where(core == 0, column(w_key), column(w_value))
        pieces_f = lambda x, axis: (
            [x, flip(x, "fsdp", 1)]
            if n_f == 2
            else [lax.all_gather(x, "fsdp", axis=axis, tiled=True)]
        )
        meta = jnp.stack([f, 1 - f, core, pair]).astype(jnp.int32)
        w_q = pieces_f(w_query, 0)
        w_kv = pieces_f(w_kv_own, 0)
        small = gather_f(small, 0)
        w_out_all = gather_f(after(w_out, small, w_q, w_kv), 1)
        piece = attn_gain.shape[0]
        gain_first = small[:, :piece].reshape(1, width).astype(f32)
        gain_second = small[:, piece : 2 * piece].reshape(1, width).astype(f32)
        bias_of = lambda lo, n: (
            small[:, lo : lo + n * (HD // n_f)]
            .reshape(n_f, n, HD // n_f)
            .transpose(1, 0, 2)
            .reshape(n, HD)
            .astype(f32)
        )
        at = 2 * piece
        bq = bias_of(at, heads)
        bk = bias_of(at + heads * (HD // n_f), KV)
        bv = bias_of(at + (heads + KV) * (HD // n_f), KV)
        b_kv = lax.dynamic_index_in_dim(jnp.where(core == 0, bk, bv), group, 0)

        unit_slice = lambda w: lax.dynamic_slice_in_dim(w, parity * units, units, 0)
        own_gate_up = jnp.concatenate([unit_slice(w) for w in (w_gate.T, w_up.T)], axis=0)
        own_down = unit_slice(w_down)

        dy_part = after(lax.dynamic_slice_in_dim(cotangent, t * part, part, 0), small)

        seq_blocks = blocks[0].reshape(n_c, -1)
        own_blocks = seq_blocks.shape[1]
        key_blocks = jnp.concatenate(
            [lax.dynamic_index_in_dim(seq_blocks, c ^ j, 0, keepdims=False) for j in range(n_c)]
        )
        positions = (
            key_blocks[:own_blocks, None] * BLOCK + jnp.arange(BLOCK, dtype=jnp.int32)[None, :]
        ).reshape(-1)
        cosine, sine = rope_tables(positions)
        bias = jnp.concatenate([bq.reshape(1, -1), b_kv], axis=1)
        dy_blocks = [
            dy_part,
            flip(dy_part, "tensor", 2),
            flip(dy_part, "context", 1),
        ]
        bias = after(bias, dy_blocks)
        normed, factor_first, queries, kv_own = qkv(
            meta, inputs, gain_first, bias, cosine, sine, w_q, w_kv
        )
        if n_f == 2:
            half_down = lax.dynamic_slice_in_dim(own_down, pair * (units // 2), units // 2, 0)
            got_half = flip(after(half_down, w_q, w_kv, small), "fsdp", 1)
        else:
            w_units = [tuple(pieces_f(w, 1)[0] for w in (own_gate_up, own_down))]
        kv = kv_gather(after(kv_own, w_out_all))
        if n_f == 2:
            far_half = flip(after(got_half, kv), "context", 2)
            got_gate_up = flip(after(own_gate_up, kv, got_half), "fsdp", 1)
            got_down = by_bit(pair, got_half, far_half, 0)
            w_units = [(own_gate_up, own_down), (got_gate_up, got_down)]
        attended, lse = attention(key_blocks, queries, kv)
        inputs_part = lax.dynamic_slice_in_dim(inputs, t * part, part, 0)
        middle, factor_second, normed2, dy_all = middle_norm(
            dot(attended, w_out_all).astype(bf16), inputs_part, gain_second, dy_blocks
        )

        hidden, grad_gate, grad_up, dx_part, out_part, *unit_far = ffn(
            meta, normed2, dy_all, w_units
        )
        if n_f == 2:
            down_got, gate_got, up_got = (flip(x, "fsdp", 1) for x in unit_far)
        else:
            over_f = lambda x: lax.psum_scatter(x, "fsdp", scatter_dimension=1, tiled=True)
            down_own = over_f(unit_grads(meta, 0, 1, dy_all, [hidden]))
            gate_up_own = over_f(unit_grads(meta, 0, 1, normed2, [grad_gate, grad_up]))
            down_got = gate_got = up_got = jnp.zeros_like(down_own)

        def unit_done(own, got):
            low = (own.astype(f32) + got.astype(f32)).astype(bf16)
            return low, flip(low, "context", 1)

        unit_whole = lambda low, other: by_bit(parity, low, other, 0).astype(f32)

        grad_middle, ffn_gain_grad, grad_middle_low = middle_back(
            dx_part, middle, factor_second, gain_second, dy_part
        )
        grad_middle_low = grad_middle_low.reshape(rows, width)
        if n_f == 2:
            down_own = unit_grads(meta, 0, 2, *after((dy_all, [hidden]), grad_middle_low))
        down_done = unit_done(down_own, after(down_got, grad_middle_low))
        grad_attended = dot_cols(after(grad_middle_low, down_done[0]), w_out_all).astype(bf16)

        dq_low, dkv = attention_back(key_blocks, queries, grad_attended, lse, cosine, sine, kv)
        if n_f == 2:
            gate_up_own = unit_grads(meta, 0, 2, *after((normed2, [grad_gate, grad_up]), dkv))
            dkv = after(dkv, gate_up_own)
        dkv = kv_scatter(after(dkv, down_done, gate_got))
        gate_done = unit_done(gate_up_own[:units], after(gate_got, dkv))
        up_done = unit_done(gate_up_own[units:], after(up_got, gate_done[0]))
        dkv = after(dkv, gate_done[0], up_done[0])
        dkv_low = jnp.where(core == 0, rotate_back(dkv, cosine, sine), dkv).astype(bf16)
        attention_args = (
            (attended, after(grad_middle_low, dkv), 1),
            (normed, after(dq_low, dkv), 0),
            (normed, dkv_low, 0),
        )
        fars = [grad_far(*args) for args in attention_args]
        dkv_low = after(dkv_low, fars)
        factor_part = lax.dynamic_slice_in_dim(factor_first, t * part, part, 0)
        own_biases = jnp.sum(
            jnp.concatenate([dq_low, dkv_low], axis=1).astype(f32), axis=0, keepdims=True
        )
        slots = lax.dynamic_update_slice(
            jnp.zeros((n_t, (heads + 1) * HD), f32), own_biases, (t, 0)
        )
        small_grads = jnp.concatenate(
            [jnp.zeros((1, width), f32), ffn_gain_grad, slots.reshape(1, -1)], axis=1
        )
        small_grads, input_grad = input_back(
            qkv_back(meta, dq_low, dkv_low, w_q, w_kv),
            inputs_part,
            factor_part,
            gain_first,
            grad_middle,
            small_grads,
        )
        input_grad = input_grad.reshape(rows, width)
        if n_f > 2:
            small_grads = lax.psum(small_grads, "fsdp")
        attention_parts = [grad_sum(*args, far) for args, far in zip(attention_args, fars)]
        wd_grad = unit_whole(*after(down_done, small_grads))
        wg_grad = unit_whole(*after(gate_done, small_grads))
        small_grads, up_done, wg_grad, wd_grad = lax.optimization_barrier(
            (small_grads, up_done, wg_grad, wd_grad)
        )
        wo_grad, wq_grad, packed, wkv_all, outputs = context_sum(
            n_f == 2, attention_parts, small_grads, out_part, middle
        )
        outputs = outputs.reshape(rows, width)
        wkv_all = wkv_all.astype(f32)
        wk_grad = jnp.concatenate([wkv_all[0], wkv_all[2]], axis=1)
        wv_grad = jnp.concatenate([wkv_all[1], wkv_all[3]], axis=1)
        packed = packed[0]
        attn_gain_grad = lax.dynamic_slice_in_dim(packed, f * piece, piece, 0)
        ffn_gain_grad = lax.dynamic_slice_in_dim(packed, width + f * piece, piece, 0)
        slots = packed[2 * width :].reshape(n_t, heads + 1, HD)
        slots = lax.dynamic_slice_in_dim(slots, f * (HD // n_f), HD // n_f, 2)
        bq_out = lax.dynamic_index_in_dim(slots, t, 0, keepdims=False)[:heads]
        bk_out = slots[0::2, heads]
        bv_out = slots[1::2, heads]

        wu_grad = unit_whole(*up_done)
        wg_grad, wu_grad = wg_grad.T, wu_grad.T

        return (
            outputs,
            input_grad,
            attn_gain_grad,
            wq_grad,
            bq_out,
            wk_grad,
            bk_out,
            wv_grad,
            bv_out,
            wo_grad,
            ffn_gain_grad,
            wg_grad,
            wu_grad,
            wd_grad,
        )

    return local


def solution(mesh):
    in_specs = (
        P(("fsdp", "context"), None),
        P(("fsdp", "context"), None),
        P("fsdp", None),
        P("fsdp"),
        P("fsdp", "tensor"),
        P("tensor", "fsdp"),
        P("fsdp", None),
        P(None, "fsdp"),
        P("fsdp", None),
        P(None, "fsdp"),
        P("tensor", "fsdp"),
        P("fsdp"),
        P("fsdp", "tensor"),
        P("fsdp", "tensor"),
        P("tensor", "fsdp"),
    )
    out_specs = (
        P(("fsdp", "context"), None),
        P(("fsdp", "context"), None),
        P("fsdp"),
        P("fsdp", "tensor"),
        P("tensor", "fsdp"),
        P("fsdp", None),
        P(None, "fsdp"),
        P("fsdp", None),
        P(None, "fsdp"),
        P("tensor", "fsdp"),
        P("fsdp"),
        P("fsdp", "tensor"),
        P("fsdp", "tensor"),
        P("tensor", "fsdp"),
    )
    local = build(mesh.shape["fsdp"], mesh.shape["context"], mesh.shape["tensor"])
    return jax.shard_map(local, mesh=mesh, in_specs=in_specs, out_specs=out_specs, check_vma=False)
```

```python
import functools

import jax
import jax.numpy as jnp
from jax import lax
from jax.experimental import pallas as pl
from jax.experimental.pallas import tpu as pltpu
from jax.sharding import PartitionSpec as P

H = 12
KV = 2
HD = 128
BLOCK = 256

EPSILON = 1e-06
ROPE_BASE = 1000000.0
MASKED = -1e30
SCALING = HD ** (-0.5)
LANES = 128
VMEM_LIMIT = 60 << 20

f32 = jnp.float32
bf16 = jnp.bfloat16


def rope_tables(positions):
    halfway = HD // 2
    frequency = ROPE_BASE ** (-(jnp.arange(halfway, dtype=f32) * 2.0 / HD))
    angles = positions.astype(f32)[:, None] * frequency[None, :]
    cosine, sine = jnp.cos(angles), jnp.sin(angles)
    return (jnp.concatenate([cosine, cosine], axis=1), jnp.concatenate([sine, sine], axis=1))


def rotate(field, cosine, sine):
    halfway = HD // 2
    turned = jnp.concatenate([-field[..., halfway:], field[..., :halfway]], axis=-1)
    return field * cosine + turned * sine


def rotate_back(grad_field, cosine, sine):
    halfway = HD // 2
    moved = grad_field * sine
    turned = jnp.concatenate([moved[..., halfway:], -moved[..., :halfway]], axis=-1)
    return grad_field * cosine + turned


def dot(left, right):
    return jnp.dot(left, right, preferred_element_type=f32)


def dot_rows(left, right):
    return lax.dot_general(left, right, (((0,), (0,)), ((), ())), preferred_element_type=f32)


def dot_cols(left, right):
    return lax.dot_general(left, right, (((1,), (1,)), ((), ())), preferred_element_type=f32)


def mask_row(kb_ref, own_block, key_blocks):
    return jnp.concatenate(
        [
            jnp.full((1, BLOCK), jnp.where(kb_ref[j] <= own_block, 0.0, MASKED), f32)
            for j in range(key_blocks)
        ],
        axis=1,
    )


def attention_kernel(key_blocks, kb_ref, q_ref, k_ref, v_ref, o_ref, lse_ref):
    bias = mask_row(kb_ref, kb_ref[pl.program_id(1)], key_blocks)
    scores = dot_cols(q_ref[...], k_ref[...]) * SCALING + bias
    row_max = jnp.max(scores, axis=1, keepdims=True)
    expo = jnp.exp(scores - row_max)
    total = jnp.sum(expo, axis=1, keepdims=True)
    probability = (expo * (1.0 / total)).astype(bf16)
    o_ref[...] = dot(probability, v_ref[...]).astype(bf16)
    lse_ref[0] = row_max + jnp.log(total)


def attention(key_blocks, queries, kv):
    rows, width = queries.shape
    heads = width // HD
    whole = lambda kind: pl.BlockSpec((None,) + kv.shape[1:], lambda h, i, kb: (kind, 0, 0))
    tile = pl.BlockSpec((BLOCK, HD), lambda h, i, kb: (i, h))
    return pl.pallas_call(
        functools.partial(attention_kernel, kv.shape[1] // BLOCK),
        name="attention",
        grid_spec=pltpu.PrefetchScalarGridSpec(
            num_scalar_prefetch=1,
            grid=(heads, rows // BLOCK),
            in_specs=[tile, whole(0), whole(1)],
            out_specs=[tile, pl.BlockSpec((1, BLOCK, 1), lambda h, i, kb: (h, i, 0))],
        ),
        out_shape=[
            jax.ShapeDtypeStruct((rows, width), bf16),
            jax.ShapeDtypeStruct((heads, rows, 1), f32),
        ],
        compiler_params=pltpu.CompilerParams(vmem_limit_bytes=VMEM_LIMIT),
    )(key_blocks, queries, kv, kv)


def attention_back_kernel(
    key_blocks,
    kb_ref,
    q_ref,
    do_ref,
    lse_ref,
    cos_ref,
    sin_ref,
    k_ref,
    v_ref,
    dq_ref,
    dkv_ref,
    dk_ref,
    dv_ref,
):
    head, i = pl.program_id(0), pl.program_id(1)

    @pl.when((head == 0) & (i == 0))
    def _():
        dk_ref[...] = jnp.zeros_like(dk_ref)
        dv_ref[...] = jnp.zeros_like(dv_ref)

    bias = mask_row(kb_ref, kb_ref[i], key_blocks)
    scores = dot_cols(q_ref[...], k_ref[...]) * SCALING + bias
    probability = jnp.exp(scores - lse_ref[0])
    grad_probs = dot_cols(do_ref[...], v_ref[...])
    inner = jnp.sum(probability * grad_probs, axis=1, keepdims=True)
    grad_scores = (probability * (grad_probs - inner)).astype(bf16)
    grad_query = dot(grad_scores, k_ref[...]) * SCALING
    moved = grad_query * sin_ref[...]
    sign = jnp.where(lax.broadcasted_iota(jnp.int32, moved.shape, 1) < HD // 2, 1.0, -1.0)
    dq_ref[...] = (
        grad_query * cos_ref[...] + pltpu.roll(moved, HD // 2, 1) * sign
    ).astype(bf16)
    dk_ref[...] += dot_rows(grad_scores, q_ref[...]) * SCALING
    dv_ref[...] += dot_rows(probability.astype(bf16), do_ref[...])

    @pl.when((head == pl.num_programs(0) - 1) & (i == pl.num_programs(1) - 1))
    def _():
        dkv_ref[0] = dk_ref[...].astype(bf16)
        dkv_ref[1] = dv_ref[...].astype(bf16)


def attention_back(key_blocks, queries, grad_out, lse, cosine, sine, kv):
    rows, width = queries.shape
    heads = width // HD
    whole = lambda kind: pl.BlockSpec((None,) + kv.shape[1:], lambda h, i, kb: (kind, 0, 0))
    tile = pl.BlockSpec((BLOCK, HD), lambda h, i, kb: (i, h))
    table = pl.BlockSpec((BLOCK, HD), lambda h, i, kb: (i, 0))
    return pl.pallas_call(
        functools.partial(attention_back_kernel, kv.shape[1] // BLOCK),
        name="attention_back",
        grid_spec=pltpu.PrefetchScalarGridSpec(
            num_scalar_prefetch=1,
            grid=(heads, rows // BLOCK),
            in_specs=[
                tile,
                tile,
                pl.BlockSpec((1, BLOCK, 1), lambda h, i, kb: (h, i, 0)),
                table,
                table,
                whole(0),
                whole(1),
            ],
            out_specs=[tile, pl.BlockSpec(kv.shape, lambda h, i, kb: (0, 0, 0))],
            scratch_shapes=[pltpu.VMEM(kv.shape[1:], f32)] * 2,
        ),
        out_shape=[
            jax.ShapeDtypeStruct((rows, width), bf16),
            jax.ShapeDtypeStruct(kv.shape, bf16),
        ],
        compiler_params=pltpu.CompilerParams(vmem_limit_bytes=VMEM_LIMIT),
    )(key_blocks, queries, grad_out, lse, cosine, sine, kv, kv)


def qkv_kernel(pieces, meta_ref, x_ref, gain_ref, bias_ref, cos_ref, sin_ref, *refs):
    weights, (xn_ref, factor_ref, q_ref, kv_ref) = refs[: 2 * pieces], refs[2 * pieces :]
    values = x_ref[...].astype(f32)
    factor = lax.rsqrt(jnp.mean(values * values, axis=-1, keepdims=True) + EPSILON)
    factor_ref[...] = factor
    xn_ref[...] = (values * factor * gain_ref[...]).astype(bf16)
    depth = weights[0].shape[0]
    normed = [xn_ref[:, columns_of(meta_ref, j, depth, pieces)] for j in range(pieces)]
    cosine, sine = cos_ref[...], sin_ref[...]
    sign = jnp.where(lax.broadcasted_iota(jnp.int32, cosine.shape, 1) < HD // 2, -1.0, 1.0)
    sine = sine * sign
    width = q_ref.shape[1]
    total = bias_ref[:, :width] + sum(dot(x, w[...]) for x, w in zip(normed, weights[:pieces]))
    turn = lambda own: own * cosine + pltpu.roll(own, HD // 2, 1) * sine
    for h in range(width // HD):
        q_ref[:, h * HD : (h + 1) * HD] = turn(total[:, h * HD : (h + 1) * HD]).astype(bf16)
    own = bias_ref[:, width:] + sum(dot(x, w[...]) for x, w in zip(normed, weights[pieces:]))
    kv_ref[...] = jnp.where(meta_ref[2] == 0, turn(own), own).astype(bf16)


def columns_of(meta_ref, j, depth, pieces):
    if pieces == 1:
        return slice(None)
    return pl.ds(pl.multiple_of(meta_ref[j] * depth, LANES), depth)


def qkv(meta, inputs, gain, bias, cosine, sine, w_q, w_kv):
    rows, width = inputs.shape
    out = w_q[0].shape[1]
    tile = 256
    row = lambda n: pl.BlockSpec((tile, n), lambda i, m: (i, 0))
    fixed = lambda w: pl.BlockSpec(w.shape, lambda i, m: (0, 0))
    return pl.pallas_call(
        functools.partial(qkv_kernel, len(w_q)),
        name="qkv",
        grid_spec=pltpu.PrefetchScalarGridSpec(
            num_scalar_prefetch=1,
            grid=(rows // tile,),
            in_specs=[row(width), fixed(gain), fixed(bias), row(HD), row(HD)]
            + [fixed(w) for w in (*w_q, *w_kv)],
            out_specs=[row(width), row(1), row(out), row(HD)],
        ),
        out_shape=[
            jax.ShapeDtypeStruct((rows, width), bf16),
            jax.ShapeDtypeStruct((rows, 1), f32),
            jax.ShapeDtypeStruct((rows, out), bf16),
            jax.ShapeDtypeStruct((rows, HD), bf16),
        ],
        compiler_params=pltpu.CompilerParams(vmem_limit_bytes=VMEM_LIMIT),
    )(meta, inputs, gain, bias, cosine, sine, *w_q, *w_kv)


def qkv_back_kernel(pieces, meta_ref, dq_ref, dkv_ref, *refs):
    w_q, w_kv, out_ref = refs[:pieces], refs[pieces : 2 * pieces], refs[-1]
    for j in range(pieces):
        out_ref[:, columns_of(meta_ref, j, w_q[j].shape[0], pieces)] = (
            dot_cols(dq_ref[...], w_q[j][...]) + dot_cols(dkv_ref[...], w_kv[j][...])
        ).astype(bf16)


def qkv_back(meta, grad_q, grad_kv, w_q, w_kv):
    rows, width = grad_q.shape[0], sum(w.shape[0] for w in w_q)
    tile = 256
    row = lambda n: pl.BlockSpec((tile, n), lambda i, m: (i, 0))
    fixed = lambda w: pl.BlockSpec(w.shape, lambda i, m: (0, 0))
    return pl.pallas_call(
        functools.partial(qkv_back_kernel, len(w_q)),
        name="qkv_back",
        grid_spec=pltpu.PrefetchScalarGridSpec(
            num_scalar_prefetch=1,
            grid=(rows // tile,),
            in_specs=[row(grad_q.shape[1]), row(HD)] + [fixed(w) for w in (*w_q, *w_kv)],
            out_specs=row(width),
        ),
        out_shape=jax.ShapeDtypeStruct((rows, width), bf16),
        compiler_params=pltpu.CompilerParams(vmem_limit_bytes=VMEM_LIMIT),
    )(meta, grad_q, grad_kv, *w_q, *w_kv)


def add_rows(unit_refs, row_refs, columns, totals, outs):
    step = pl.program_id(0)

    @pl.when(step == 0)
    def _():
        for total in totals:
            total[...] = jnp.zeros_like(total)

    for total, unit, row in zip(totals, unit_refs, row_refs):
        total[...] += dot_rows(unit[...], row[:, columns])

    @pl.when(step == pl.num_programs(0) - 1)
    def _():
        for out, total in zip(outs, totals):
            out[...] = total[...].astype(bf16)


def hidden_kernel(pieces, meta_ref, x_ref, dy_ref, *refs):
    wg, wu, refs = refs[:pieces], refs[pieces : 2 * pieces], refs[2 * pieces :]
    hid_ref, slope_ref, gated_ref = refs[:3]
    columns = [columns_of(meta_ref, j, wg[j].shape[1], pieces) for j in range(pieces)]
    gate = sum(dot_cols(x_ref[:, at], w[...]) for at, w in zip(columns, wg))
    up = sum(dot_cols(x_ref[:, at], w[...]) for at, w in zip(columns, wu))
    sigma = 1.0 / (1.0 + jnp.exp(-gate))
    gated = gate * sigma
    hid_ref[...] = (gated * up).astype(bf16)
    slope_ref[...] = (up * (sigma + gated * (1.0 - sigma))).astype(bf16)
    gated_ref[...] = gated.astype(bf16)
    if pieces == 2:
        add_rows([hid_ref], [dy_ref], columns[1], refs[4:], refs[3:4])


def hidden_back_kernel(pieces, meta_ref, x_ref, dy_ref, hid_ref, slope_ref, gated_ref, *refs):
    wg, wu, wd = (refs[m * pieces : (m + 1) * pieces] for m in range(3))
    refs = refs[3 * pieces :]
    dg_ref, du_ref, dx_ref, out_ref = refs[:4]
    columns = [columns_of(meta_ref, j, wg[j].shape[1], pieces) for j in range(pieces)]
    grad_hidden = sum(dot_cols(dy_ref[:, at], w[...]) for at, w in zip(columns, wd))
    dg_ref[...] = (grad_hidden * slope_ref[...].astype(f32)).astype(bf16)
    du_ref[...] = (grad_hidden * gated_ref[...].astype(f32)).astype(bf16)

    @pl.when(pl.program_id(0) // (pl.num_programs(0) // 2) == meta_ref[3])
    def _():
        for at, g, u, d in zip(columns, wg, wu, wd):
            dx_ref[:, at] = (dot(dg_ref[...], g[...]) + dot(du_ref[...], u[...])).astype(bf16)
            out_ref[:, at] = dot(hid_ref[...], d[...]).astype(bf16)

    if pieces == 2:
        add_rows([dg_ref, du_ref], [x_ref, x_ref], columns[1], refs[6:], refs[4:6])


def hidden_specs(meta, normed, weights):
    width = normed.shape[-1]
    rows = normed.shape[0] * normed.shape[1]
    units, depth = weights[0].shape[0] // 2, weights[0].shape[1]
    tile = 512
    steps = rows // tile
    half = steps // 2
    once = pl.Buffered(1)
    inside = lambda i, m: jnp.clip(i - m[3] * half, 0, half - 1)
    return {
        "steps": steps,
        "flat": lambda x: x.reshape(-1, width),
        "row": pl.BlockSpec((tile, width), lambda i, m: (lax.rem(i + m[3] * half, steps), 0)),
        "unit": pl.BlockSpec((tile, units), lambda i, m: (i, 0)),
        "near_unit": pl.BlockSpec((tile, units), lambda i, m: (inside(i, m) + m[3] * half, 0)),
        "near_row": pl.BlockSpec((tile, width), lambda i, m: (inside(i, m), 0)),
        "weight": lambda k: pl.BlockSpec((units, depth), lambda i, m: (k, 0), pipeline_mode=once),
        "grad": pl.BlockSpec((units, depth), lambda i, m: (0, 0), pipeline_mode=once),
        "unit_shape": jax.ShapeDtypeStruct((rows, units), bf16),
        "near_shape": jax.ShapeDtypeStruct((rows // 2, width), bf16),
        "grad_shape": jax.ShapeDtypeStruct((units, depth), bf16),
        "total": pltpu.VMEM((units, depth), f32),
    }


def hidden_call(kernel, name, meta, args, in_specs, outs, grads, specs):
    return pl.pallas_call(
        kernel,
        name=name,
        grid_spec=pltpu.PrefetchScalarGridSpec(
            num_scalar_prefetch=1,
            grid=(specs["steps"],),
            in_specs=in_specs,
            out_specs=[specs[x] for x in outs] + [specs["grad"]] * grads,
            scratch_shapes=[specs["total"]] * grads,
        ),
        out_shape=[specs[x.split("_")[0] + "_shape"] for x in outs]
        + [specs["grad_shape"]] * grads,
        compiler_params=pltpu.CompilerParams(vmem_limit_bytes=VMEM_LIMIT),
    )(meta, *args)


def hidden_units(meta, normed, grad_out, weights):
    specs, pieces = hidden_specs(meta, normed, weights), len(weights)
    return hidden_call(
        functools.partial(hidden_kernel, pieces),
        "hidden_units",
        meta,
        [specs["flat"](normed), specs["flat"](grad_out)] + list(weights) * 2,
        [specs["row"]] * 2 + [specs["weight"](k) for k in range(2) for _ in weights],
        ["unit"] * 3,
        pieces == 2,
        specs,
    )


def hidden_back(meta, normed, grad_out, hidden, slope, gated, weights, down_weights):
    specs, pieces = hidden_specs(meta, normed, weights), len(weights)
    return hidden_call(
        functools.partial(hidden_back_kernel, pieces),
        "hidden_back",
        meta,
        [specs["flat"](normed), specs["flat"](grad_out), hidden, slope, gated]
        + list(weights) * 2
        + list(down_weights),
        [specs["row"]] * 2
        + [specs["near_unit"], specs["unit"], specs["unit"]]
        + [specs["weight"](k) for k in (0, 1, 0) for _ in weights],
        ["unit", "unit", "near_row", "near_row"],
        2 * (pieces == 2),
        specs,
    )


def unit_grads_kernel(count, meta_ref, near_ref, far_ref, *refs):
    units, out_ref, x_ref = refs[:count], refs[-2], refs[-1]
    half = near_ref.shape[0]
    x_ref[pl.ds(pl.multiple_of(meta_ref[3] * half, half), half)] = near_ref[...]
    x_ref[pl.ds(pl.multiple_of((1 - meta_ref[3]) * half, half), half)] = far_ref[...]
    for k, unit in enumerate(units):
        depth = unit.shape[1]
        out_ref[k * depth : (k + 1) * depth] = dot_rows(unit[...], x_ref[...]).astype(bf16)


def unit_grads(meta, which, pieces, x, units_of):
    width = x.shape[-1]
    count, (rows, units) = len(units_of), units_of[0].shape
    depth = width // pieces
    tile = 256
    steps = depth // tile
    shard = (lambda m: m[which]) if pieces > 1 else (lambda m: 0)
    feature = lambda half: pl.BlockSpec(
        (rows // 2, tile), lambda i, m: (half, shard(m) * steps + i)
    )
    unit = pl.BlockSpec((rows, units), lambda i, m: (0, 0), pipeline_mode=pl.Buffered(1))
    x = x.reshape(-1, width)
    return pl.pallas_call(
        functools.partial(unit_grads_kernel, count),
        name=f"unit_grads_{which}_{count}",
        grid_spec=pltpu.PrefetchScalarGridSpec(
            num_scalar_prefetch=1,
            grid=(steps,),
            in_specs=[feature(0), feature(1)] + [unit] * count,
            out_specs=pl.BlockSpec((count * units, tile), lambda i, m: (0, i)),
            scratch_shapes=[pltpu.VMEM((rows, tile), bf16)],
        ),
        out_shape=jax.ShapeDtypeStruct((count * units, depth), bf16),
        compiler_params=pltpu.CompilerParams(vmem_limit_bytes=VMEM_LIMIT),
    )(meta, x, x, *units_of)


class Wires:
    def __init__(self, sends, receives, locals_):
        self.sends, self.receives, self.locals = sends, receives, locals_
        self.used = self.used_local = 0
        self.started = []

    def plan(self, source, target, device):
        k = self.used
        self.used += 1
        return pltpu.make_async_remote_copy(
            source,
            target,
            self.sends.at[k],
            self.receives.at[k],
            device_id=device,
            device_id_type=pl.DeviceIdType.MESH,
        )

    def copy(self, source, target, device):
        one = self.plan(source, target, device)
        one.start()
        self.started.append(one)
        return one

    def here(self, source, target):
        k = self.used_local
        self.used_local += 1
        one = pltpu.make_async_copy(source, target, self.locals.at[k])
        one.start()
        return one

    def finish(self):
        for one in self.started:
            one.wait_send()


def meet(devices):
    barrier = pltpu.get_barrier_semaphore()
    for device in devices:
        pl.semaphore_signal(barrier, inc=1, device_id=device, device_id_type=pl.DeviceIdType.MESH)
    pl.semaphore_wait(barrier, len(devices))


def partners():
    c, t = lax.axis_index("context"), lax.axis_index("tensor")
    flip = lambda x, bit: x + bit * (1 - 2 * lax.rem(x // bit, 2))
    return {
        "core": {"tensor": flip(t, 1)},
        "y": {"tensor": flip(t, 2)},
        "z": {"context": flip(c, 1)},
        "far": {"context": flip(c, 2)},
        "last": {"context": flip(flip(c, 1), 2)},
    }


def wide(x):
    return x.astype(f32)


def ranks():
    t = lax.axis_index("tensor")
    flip = lambda x, bit: x + bit * (1 - 2 * lax.rem(x // bit, 2))
    return (t, flip(t, 1), flip(t, 2), flip(flip(t, 1), 2))


def scatter_rank(wires, to, part, own, got_core, sent, got_y):
    size = part.shape[1] // 2
    halves = [pl.ds(0, size), pl.ds(size, size)]
    rank = ranks()
    from_core = {}
    for block in (1, 0):
        for k, at in enumerate(halves):
            from_core[block, k] = wires.copy(
                part.at[rank[1 + 2 * block], at], got_core.at[block, at], to["core"]
            )
    mine = [wires.here(part.at[rank[2 * block]], own.at[block]) for block in (0, 1)]
    yield
    for one in mine:
        one.wait()
    from_y = []
    for k, at in enumerate(halves):
        from_core[1, k].wait_recv()
        sent[at] = (wide(own[1, at]) + wide(got_core[1, at])).astype(bf16)
        from_y.append(wires.copy(sent.at[at], got_y.at[at], to["y"]))
    yield
    for k in range(2):
        from_core[0, k].wait_recv()
    total = wide(own[0]) + wide(got_core[0])
    for one in from_y:
        one.wait_recv()
    return total + wide(got_y[...])


def scatter_pair(wires, to, part, own, got_core, sent, got_y, got_z, diag_y, diag_z):
    size = part.shape[1] // 2
    low, high = pl.ds(0, size), pl.ds(size, size)
    from_core = {j: wires.copy(part.at[4 + j], got_core.at[j], to["core"]) for j in (3, 1, 2, 0)}
    mine = wires.here(part.at[pl.ds(0, 4)], own)
    yield
    mine.wait()
    both = lambda j, at: wide(own[j, at]) + wide(got_core[j, at])
    from_core[3].wait_recv()
    sent[2] = (wide(own[3]) + wide(got_core[3])).astype(bf16)
    via_z = wires.copy(sent.at[2, low], diag_z, to["z"])
    via_y = wires.copy(sent.at[2, high], diag_y, to["y"])
    from_core[1].wait_recv()
    sent[0, high] = both(1, high).astype(bf16)
    y_high = wires.copy(sent.at[0, high], got_y.at[high], to["y"])
    from_core[2].wait_recv()
    sent[1, low] = both(2, low).astype(bf16)
    z_low = wires.copy(sent.at[1, low], got_z.at[low], to["z"])
    yield
    via_z.wait_recv()
    sent[0, low] = (both(1, low) + wide(diag_z[...])).astype(bf16)
    y_low = wires.copy(sent.at[0, low], got_y.at[low], to["y"])
    via_y.wait_recv()
    sent[1, high] = (both(2, high) + wide(diag_y[...])).astype(bf16)
    z_high = wires.copy(sent.at[1, high], got_z.at[high], to["z"])
    yield
    from_core[0].wait_recv()
    total = wide(own[0]) + wide(got_core[0])
    for one in (y_high, z_low, y_low, z_high):
        one.wait_recv()
    return total + wide(got_y[...]) + wide(got_z[...])


def result_of(steps):
    while True:
        try:
            next(steps)
        except StopIteration as done:
            return done.value


def gather_rank(wires, to, block, out):
    size = block.shape[0] // 2
    halves = [pl.ds(0, size), pl.ds(size, size)]
    rank = ranks()
    mine = wires.here(block, out.at[rank[0]])
    from_y = [wires.copy(block.at[h], out.at[rank[0], h], to["y"]) for h in halves]
    from_core = [wires.copy(block, out.at[rank[0]], to["core"])]
    yield
    for h, one in zip(halves, from_y):
        one.wait_recv()
        from_core.append(wires.copy(out.at[rank[2], h], out.at[rank[2], h], to["core"]))
    for one in from_core:
        one.wait_recv()
    mine.wait()


def gather_pair(wires, to, block, out, base):
    size = block.shape[0] // 2
    low, high = pl.ds(0, size), pl.ds(size, size)
    at = lambda j: out.at[base + j]
    from_z = wires.copy(block, at(2), to["z"])
    yield
    from_y = wires.copy(block, at(1), to["y"])
    from_core = [wires.copy(block, at(4), to["core"])]
    yield
    from_y.wait_recv()
    via_z = wires.copy(out.at[base + 1, low], out.at[base + 3, low], to["z"])
    from_core.append(wires.copy(at(1), at(5), to["core"]))
    from_z.wait_recv()
    via_y = wires.copy(out.at[base + 2, high], out.at[base + 3, high], to["y"])
    from_core.append(wires.copy(at(2), at(6), to["core"]))
    yield
    via_z.wait_recv()
    via_y.wait_recv()
    from_core.append(wires.copy(at(3), at(7), to["core"]))
    return from_core


def remote_call(kernel, name, key, args, outs, scratch, copies, in_vmem):
    ins, out_in = in_vmem
    spec = lambda inside: pl.BlockSpec(memory_space=pltpu.VMEM if inside else pl.ANY)
    return pl.pallas_call(
        kernel,
        name=name,
        out_shape=outs,
        in_specs=[spec(x) for x in ins],
        out_specs=[spec(x) for x in out_in],
        scratch_shapes=list(scratch)
        + [
            pltpu.SemaphoreType.DMA((copies,)),
            pltpu.SemaphoreType.DMA((copies,)),
            pltpu.SemaphoreType.DMA((8,)),
        ],
        compiler_params=pltpu.CompilerParams(
            collective_id=key, has_side_effects=True, vmem_limit_bytes=VMEM_LIMIT
        ),
    )(*args)


def kv_gather_kernel(own_ref, out_ref, *sems):
    wires, to = Wires(*sems), partners()
    kind = lax.rem(lax.axis_index("tensor"), 2)
    rows = own_ref.shape[0]
    block = lambda j: out_ref.at[kind, pl.ds(j * rows, rows)]
    meet([to[k] for k in ("core", "z", "far", "last")])
    mine = wires.here(own_ref, block(0))
    arrive = [wires.copy(own_ref, block(j), to[k]) for j, k in ((3, "last"), (2, "far"), (1, "z"))]
    from_core = [wires.copy(own_ref, block(0), to["core"])]
    for j, one in ((1, arrive[2]), (2, arrive[1]), (3, arrive[0])):
        one.wait_recv()
        from_core.append(wires.copy(block(j), block(j), to["core"]))
    for one in from_core:
        one.wait_recv()
    mine.wait()
    wires.finish()


def kv_gather(own):
    rows, width = own.shape
    n_c = lax.axis_size("context")
    return remote_call(
        kv_gather_kernel,
        "kv_gather",
        0,
        [own],
        [jax.ShapeDtypeStruct((2, n_c * rows, width), bf16)],
        [],
        8,
        ([False], [False]),
    )[0]


def kv_scatter_kernel(part_ref, dkv_ref, own, got_core, sent, got, *sems):
    wires, to = Wires(*sems), partners()
    kind = lax.rem(lax.axis_index("tensor"), 2)
    rows = dkv_ref.shape[0]
    block = lambda j: pl.ds(j * rows, rows)
    meet([to[k] for k in ("core", "z", "far", "last")])
    steps = ((3, "last"), (2, "far"), (1, "z"), (0, None))
    from_core = {
        j: wires.copy(part_ref.at[1 - kind, block(j)], got_core.at[block(j)], to["core"])
        for j, _ in steps
    }
    mine = wires.here(part_ref.at[kind], own)
    mine.wait()
    arrive = []
    for j, k in steps[:3]:
        from_core[j].wait_recv()
        sent[block(j)] = (wide(own[block(j)]) + wide(got_core[block(j)])).astype(bf16)
        arrive.append(wires.copy(sent.at[block(j)], got.at[block(j)], to[k]))
    from_core[0].wait_recv()
    total = wide(own[block(0)]) + wide(got_core[block(0)])
    for one in arrive:
        one.wait_recv()
    for j in (1, 2, 3):
        total = total + wide(got[block(j)])
    dkv_ref[...] = total
    wires.finish()


def kv_scatter(part):
    _, rows, width = part.shape
    n_c = lax.axis_size("context")
    return remote_call(
        kv_scatter_kernel,
        "kv_scatter",
        1,
        [part],
        [jax.ShapeDtypeStruct((rows // n_c, width), f32)],
        [pltpu.VMEM((rows, width), bf16)] * 4,
        7,
        ([False], [True]),
    )[0]


def middle_kernel(
    part,
    x_ref,
    gain_ref,
    dy_ref,
    dy_y,
    dy_z,
    dy_far,
    mid_ref,
    factor_ref,
    out,
    dys,
    own,
    core,
    sent,
    got,
    xn,
    *sems,
):
    wires, to = Wires(*sems), partners()
    blocks = out.shape[0] // 2
    size = xn.shape[0] // 2
    low, high = pl.ds(0, size), pl.ds(size, size)
    meet([to[k] for k in ("core", "y", "z", "far")])
    summed = scatter_rank(wires, to, part, own, core, sent, got)
    next(summed)
    mine = [
        wires.here(block, dys.at[k])
        for block, k in ((dy_ref, 0), (dy_y, 1), (dy_z, 2), (dy_far, blocks))
    ]
    via_z = wires.copy(dy_y.at[low], dys.at[3, low], to["z"])
    dy_last = gather_pair(wires, to, dy_far, dys, blocks)
    next(dy_last)
    next(summed)
    via_y = wires.copy(dy_z.at[high], dys.at[3, high], to["y"])
    ends = [
        wires.copy(block, dys.at[4 + k], to["core"])
        for k, block in enumerate((dy_ref, dy_y, dy_z))
    ]
    next(dy_last)
    middle = wide(x_ref[...]) + result_of(summed)
    mid_ref[...] = middle
    factor = lax.rsqrt(jnp.mean(middle * middle, axis=-1, keepdims=True) + EPSILON)
    factor_ref[...] = factor
    xn[...] = (middle * factor * gain_ref[...]).astype(bf16)
    mine.append(wires.here(xn, out.at[0]))
    xn_far = wires.copy(xn, out.at[blocks], to["far"])
    xn_near = gather_pair(wires, to, xn, out, 0)
    next(xn_near)
    next(xn_near)
    via_z.wait_recv()
    via_y.wait_recv()
    ends.append(wires.copy(dys.at[3], dys.at[7], to["core"]))
    next(dy_last)
    next(xn_near)
    xn_far.wait_recv()
    xn_last = gather_pair(wires, to, out.at[blocks], out, blocks)
    next(xn_last)
    next(xn_last)
    ends += result_of(dy_last) + result_of(xn_near)
    next(xn_last)
    ends += result_of(xn_last)
    for one in ends:
        one.wait_recv()
    for one in mine:
        one.wait()
    wires.finish()


def middle_norm(part, inputs_part, gain, dy_blocks):
    rows, width = inputs_part.shape
    return remote_call(
        middle_kernel,
        "middle_norm",
        2,
        [part.reshape(4, rows, width), inputs_part, gain, *dy_blocks],
        [
            jax.ShapeDtypeStruct((rows, width), f32),
            jax.ShapeDtypeStruct((rows, 1), f32),
            jax.ShapeDtypeStruct((16, rows, width), bf16),
            jax.ShapeDtypeStruct((16, rows, width), bf16),
        ],
        [
            pltpu.VMEM((2, rows, width), bf16),
            pltpu.VMEM((2, rows, width), bf16),
            pltpu.VMEM((rows, width), bf16),
            pltpu.VMEM((rows, width), bf16),
            pltpu.VMEM((rows, width), bf16),
        ],
        48,
        ([False] + [True] * 6, [True, True, False, False]),
    )


def norm_back_rows(values, factor, gain, grad_normed):
    gained = gain * grad_normed
    inner = jnp.mean(gained * values, axis=-1, keepdims=True)
    grad_values = factor * gained - values * (factor * factor * factor) * inner
    return grad_values, jnp.sum(grad_normed * values * factor, axis=0, keepdims=True)


def middle_back_kernel(
    part, mid_ref, factor_ref, gain_ref, dy_ref, dmid_ref, dgain_ref, out, low, *rest
):
    first, wires, to = rest[:7], Wires(*rest[7:]), partners()
    meet([to[k] for k in ("core", "y", "z")])
    grad_normed = result_of(scatter_pair(wires, to, part, *first))
    du, dgain = norm_back_rows(mid_ref[...], factor_ref[...], gain_ref[...], grad_normed)
    dgain_ref[...] = dgain
    dmid = wide(dy_ref[...]) + du
    low[...] = dmid.astype(bf16)
    share = gather_rank(wires, to, low, out)
    next(share)
    dmid_ref[...] = dmid
    result_of(share)
    wires.finish()


def pair_scratch(rows, width):
    return [
        pltpu.VMEM((4, rows, width), bf16),
        pltpu.VMEM((4, rows, width), bf16),
        pltpu.VMEM((3, rows, width), bf16),
        pltpu.VMEM((rows, width), bf16),
        pltpu.VMEM((rows, width), bf16),
        pltpu.VMEM((rows // 2, width), bf16),
        pltpu.VMEM((rows // 2, width), bf16),
    ]


def middle_back(part, middle, factor, gain, dy_part):
    rows, width = middle.shape
    return remote_call(
        middle_back_kernel,
        "middle_back",
        3,
        [part.reshape(8, rows, width), middle, factor, gain, dy_part],
        [
            jax.ShapeDtypeStruct((rows, width), f32),
            jax.ShapeDtypeStruct((1, width), f32),
            jax.ShapeDtypeStruct((4, rows, width), bf16),
        ],
        [pltpu.VMEM((rows, width), bf16)] + pair_scratch(rows, width),
        16,
        ([False, True, True, True, True], [True, True, False]),
    )


def add_all(wires, ways, value, slots):
    for k, device in enumerate(ways):
        one = wires.copy(value, slots.at[k], device)
        one.wait()
        wires.started = [x for x in wires.started if x is not one]
        value[...] = value[...] + slots[k]


def input_back_kernel(
    part, x_ref, factor_ref, gain_ref, dmid_ref, small_ref, sum_ref, out, *rest
):
    low, own, core, sent, got, slots = rest[:-3]
    wires, to = Wires(*rest[-3:]), partners()
    meet([to[k] for k in ("core", "y")])
    grad_normed = result_of(scatter_rank(wires, to, part, own, core, sent, got))
    du, dgain = norm_back_rows(wide(x_ref[...]), factor_ref[...], gain_ref[...], grad_normed)
    low[...] = (dmid_ref[...] + du).astype(bf16)
    share = gather_rank(wires, to, low, out)
    next(share)
    width = dgain.shape[1]
    sum_ref[:, width:] = small_ref[:, width:]
    sum_ref[:, :width] = dgain
    add_all(wires, [to["core"], to["y"]], sum_ref, slots)
    result_of(share)
    wires.finish()


def input_back(part, inputs_part, factor, gain, grad_middle, small):
    rows, width = inputs_part.shape
    return remote_call(
        input_back_kernel,
        "input_back",
        5,
        [part.reshape(4, rows, width), inputs_part, factor, gain, grad_middle, small],
        [
            jax.ShapeDtypeStruct(small.shape, f32),
            jax.ShapeDtypeStruct((4, rows, width), bf16),
        ],
        [
            pltpu.VMEM((rows, width), bf16),
            pltpu.VMEM((2, rows, width), bf16),
            pltpu.VMEM((2, rows, width), bf16),
            pltpu.VMEM((rows, width), bf16),
            pltpu.VMEM((rows, width), bf16),
            pltpu.VMEM((2,) + small.shape, f32),
        ],
        16,
        ([False, True, True, True, True, True], [True, False]),
    )


def context_sum_kernel(over_f, *refs):
    parts, small_ref, out_part, mid_ref = refs[:3], refs[3], refs[4], refs[5]
    outs, sum_ref, shared, outputs = refs[6:8], refs[8], refs[9], refs[10]
    lows, from_end, from_middle = refs[11:15], refs[15:19], refs[19:23]
    out_low, slot, scratch = refs[23], refs[24], refs[25:32]
    wires, to, c = Wires(*refs[32:]), partners(), lax.axis_index("context")
    end = (c == 0) | (c == lax.axis_size("context") - 1)
    inner = jnp.logical_not(end)
    greet = ["core", "y", "z", "last"]
    if over_f:
        to["f"] = {"fsdp": 1 - lax.axis_index("fsdp")}
        greet.append("f")
    meet([to[k] for k in greet])
    ahead = scatter_pair(wires, to, out_part, *scratch)
    next(ahead)
    sum_ref[...] = small_ref[...]
    from_f = wires.copy(small_ref, slot, to["f"]) if over_f else None
    next(ahead)
    sources = [*parts, sum_ref]
    chunks = []
    for i, cuts in ((2, 1), (0, 2), (1, 2), (3, 1)):
        size = sources[i].shape[0] // cuts
        chunks += [(i, pl.ds(k * size, size)) for k in range(cuts)]
    inward = [wires.plan(sources[i].at[at], from_end[i].at[at], to["z"]) for i, at in chunks]
    across = [wires.plan(lows[i].at[at], from_middle[i].at[at], to["last"]) for i, at in chunks]
    outward = [wires.plan(lows[i].at[at], lows[i].at[at], to["z"]) for i, at in chunks]
    small = len(chunks) - 1

    def send_in(k):
        @pl.when(end)
        def _():
            inward[k].start()

    def pass_on(first, past):
        @pl.when(inner)
        def _():
            for k in range(first, past):
                i, at = chunks[k]
                inward[k].wait_recv()
                total = wide(sources[i][at]) + wide(from_end[i][at])
                lows[i][at] = total.astype(lows[i].dtype)
                across[k].start()
                if k:
                    send_out(k - 1)

    def send_out(k):
        i, at = chunks[k]
        across[k].wait()
        lows[i][at] = (wide(lows[i][at]) + wide(from_middle[i][at])).astype(lows[i].dtype)
        outward[k].start()

    send_in(0)
    send_in(1)
    next(ahead)
    if over_f:
        from_f.wait_recv()
        sum_ref[...] = sum_ref[...] + slot[...]
    for k in range(2, small + 1):
        send_in(k)
    pass_on(0, 2)
    out_low[...] = (mid_ref[...] + result_of(ahead)).astype(bf16)
    out_share = gather_rank(wires, to, out_low, outputs)
    next(out_share)
    pass_on(2, small + 1)

    @pl.when(inner)
    def _():
        send_out(small)

    result_of(out_share)

    def arrived(k):
        @pl.when(end)
        def _():
            outward[k].wait_recv()

    arrived(0)
    share = gather_rank(wires, to, lows[2], shared)
    next(share)
    for k in range(1, len(chunks)):
        arrived(k)

    @pl.when(end)
    def _():
        for one in inward:
            one.wait_send()

    for i in (0, 1):
        outs[i][...] = wide(lows[i][...])
    sum_ref[...] = lows[3][...]
    result_of(share)

    @pl.when(inner)
    def _():
        for one in outward:
            one.wait_send()

    wires.finish()


def context_sum(over_f, parts, small, out_part, middle):
    rows, width = middle.shape
    lines = [pltpu.VMEM(x.shape, x.dtype) for x in (*parts, small)]
    return remote_call(
        functools.partial(context_sum_kernel, over_f),
        "context_sum",
        6,
        [*parts, small, out_part.reshape(8, rows, width), middle],
        [jax.ShapeDtypeStruct(x.shape, f32) for x in parts[:2]]
        + [jax.ShapeDtypeStruct(small.shape, f32)]
        + [jax.ShapeDtypeStruct((4,) + parts[2].shape, bf16)]
        + [jax.ShapeDtypeStruct((4, rows, width), bf16)],
        lines * 3
        + [pltpu.VMEM((rows, width), bf16), pltpu.VMEM(small.shape, f32)]
        + pair_scratch(rows, width),
        48,
        ([True] * 4 + [False, True], [True] * 3 + [False] * 2),
    )


def build(n_f, n_c, n_t):
    def flip(x, axis, bit):
        size = {"fsdp": n_f, "context": n_c, "tensor": n_t}[axis]
        return lax.ppermute(x, axis, [(i, i ^ bit) for i in range(size)])

    def by_bit(bit, x, other, axis):
        return jnp.where(
            bit == 0,
            jnp.concatenate([x, other], axis=axis),
            jnp.concatenate([other, x], axis=axis),
        )

    def after(x, *others):
        return lax.optimization_barrier((x, others))[0]

    def local(
        inputs,
        cotangent,
        blocks,
        attn_gain,
        w_query,
        b_query,
        w_key,
        b_key,
        w_value,
        b_value,
        w_out,
        ffn_gain,
        w_gate,
        w_up,
        w_down,
    ):
        rows, width = inputs.shape
        f = lax.axis_index("fsdp")
        c = lax.axis_index("context")
        t = lax.axis_index("tensor")
        core, parity, pair = t % 2, c % 2, c // 2
        heads = w_query.shape[1] // HD
        group = (t * heads) // (H // KV)
        part = rows // n_t
        units_all = w_gate.shape[1]
        units = units_all // 2

        def gather_f(x, axis):
            if n_f == 2:
                return by_bit(f, x, flip(x, "fsdp", 1), axis)
            return lax.all_gather(x, "fsdp", axis=axis, tiled=True)

        def grad_far(left, right, side):
            if n_f > 2:
                return None
            source = (left, right)[side]
            half = width // 2
            far = lax.dynamic_slice_in_dim(source, (1 - f) * half, half, 1)
            return (dot_rows(far, right) if side == 0 else dot_rows(left, far)).astype(bf16)

        def grad_sum(left, right, side, far, late):
            if n_f > 2:
                return lax.psum_scatter(
                    dot_rows(left, right).astype(bf16), "fsdp", scatter_dimension=side, tiled=True
                )
            source = (left, right)[side]
            half = width // 2
            own = lax.dynamic_slice_in_dim(source, f * half, half, 1)
            own = dot_rows(own, right) if side == 0 else dot_rows(left, own)
            return (own + after(flip(far, "fsdp", 1), late).astype(f32)).astype(bf16)

        small = jnp.concatenate(
            [v.reshape(1, -1) for v in (attn_gain, ffn_gain, b_query, b_key, b_value)], axis=1
        )
        column = lambda w: lax.dynamic_slice_in_dim(w, group * HD, HD, 1)
        w_kv_own = jnp.where(core == 0, column(w_key), column(w_value))
        pieces_f = lambda x, axis: (
            [x, flip(x, "fsdp", 1)]
            if n_f == 2
            else [lax.all_gather(x, "fsdp", axis=axis, tiled=True)]
        )
        meta = jnp.stack([f, 1 - f, core, pair]).astype(jnp.int32)
        w_q = pieces_f(w_query, 0)
        w_kv = pieces_f(w_kv_own, 0)
        small = gather_f(small, 0)
        w_out_all = gather_f(after(w_out, small, w_q, w_kv), 1)
        piece = attn_gain.shape[0]
        gain_first = small[:, :piece].reshape(1, width).astype(f32)
        gain_second = small[:, piece : 2 * piece].reshape(1, width).astype(f32)
        bias_of = lambda lo, n: (
            small[:, lo : lo + n * (HD // n_f)]
            .reshape(n_f, n, HD // n_f)
            .transpose(1, 0, 2)
            .reshape(n, HD)
            .astype(f32)
        )
        at = 2 * piece
        bq = bias_of(at, heads)
        bk = bias_of(at + heads * (HD // n_f), KV)
        bv = bias_of(at + (heads + KV) * (HD // n_f), KV)
        b_kv = lax.dynamic_index_in_dim(jnp.where(core == 0, bk, bv), group, 0)

        unit_slice = lambda w: lax.dynamic_slice_in_dim(w, parity * units, units, 0)
        own_gate_up = jnp.concatenate([unit_slice(w) for w in (w_gate.T, w_up.T)], axis=0)
        own_down = unit_slice(w_down)

        dy_part = lax.dynamic_slice_in_dim(cotangent, t * part, part, 0)

        seq_blocks = blocks[0].reshape(n_c, -1)
        own_blocks = seq_blocks.shape[1]
        key_blocks = jnp.concatenate(
            [lax.dynamic_index_in_dim(seq_blocks, c ^ j, 0, keepdims=False) for j in range(n_c)]
        )
        positions = (
            key_blocks[:own_blocks, None] * BLOCK + jnp.arange(BLOCK, dtype=jnp.int32)[None, :]
        ).reshape(-1)
        cosine, sine = rope_tables(positions)
        bias = jnp.concatenate([bq.reshape(1, -1), b_kv], axis=1)
        dy_blocks = [
            dy_part,
            flip(dy_part, "tensor", 2),
            flip(dy_part, "context", 1),
            flip(dy_part, "context", 2),
        ]
        bias = after(bias, dy_blocks)
        normed, factor_first, queries, kv_own = qkv(
            meta, inputs, gain_first, bias, cosine, sine, w_q, w_kv
        )
        far_gate_up = pieces_f(after(own_gate_up, kv_own, w_out_all), 1)[-1]
        w_gate_up = [own_gate_up, far_gate_up] if n_f == 2 else [far_gate_up]
        kv = kv_gather(after(kv_own, w_out_all))
        far_down = pieces_f(after(own_down, kv), 1)[-1]
        w_downs = [own_down, far_down] if n_f == 2 else [far_down]
        attended, lse = attention(key_blocks, queries, kv)
        inputs_part = lax.dynamic_slice_in_dim(inputs, t * part, part, 0)
        middle, factor_second, normed2, dy_all = middle_norm(
            dot(attended, w_out_all).astype(bf16), inputs_part, gain_second, dy_blocks
        )

        hidden, slope, gated, *down_far = hidden_units(meta, normed2, dy_all, w_gate_up)
        grad_gate, grad_up, dx_part, out_part, *unit_far = hidden_back(
            meta, normed2, dy_all, hidden, slope, gated, w_gate_up, w_downs
        )
        unit_far = [*down_far, *unit_far]
        if n_f == 2:
            down_got, gate_got, up_got = (flip(x, "fsdp", 1) for x in unit_far)
        else:
            over_f = lambda x: lax.psum_scatter(x, "fsdp", scatter_dimension=1, tiled=True)
            down_own = over_f(unit_grads(meta, 0, 1, dy_all, [hidden]))
            gate_up_own = over_f(unit_grads(meta, 0, 1, normed2, [grad_gate, grad_up]))
            down_got = gate_got = up_got = jnp.zeros_like(down_own)

        def unit_done(own, got):
            low = (own.astype(f32) + got.astype(f32)).astype(bf16)
            return low, flip(low, "context", 1)

        unit_whole = lambda low, other: by_bit(parity, low, other, 0).astype(f32)

        grad_middle, ffn_gain_grad, grad_middle_low = middle_back(
            dx_part, middle, factor_second, gain_second, dy_part
        )
        grad_middle_low = grad_middle_low.reshape(rows, width)
        if n_f == 2:
            down_own = unit_grads(meta, 0, 2, *after((dy_all, [hidden]), grad_middle_low))
        down_done = unit_done(down_own, after(down_got, grad_middle_low))
        grad_attended = dot_cols(after(grad_middle_low, down_done[0]), w_out_all).astype(bf16)

        dq_low, dkv = attention_back(key_blocks, queries, grad_attended, lse, cosine, sine, kv)
        if n_f == 2:
            gate_up_own = unit_grads(meta, 0, 2, *after((normed2, [grad_gate, grad_up]), dkv))
            dkv = after(dkv, gate_up_own)
        attention_args = [(attended, grad_middle_low, 1), (normed, dq_low, 0)]
        fars = [grad_far(*args) for args in attention_args]
        dkv = kv_scatter(after(dkv, down_done, gate_got, fars))
        gate_done = unit_done(gate_up_own[:units], after(gate_got, dkv))
        dkv = after(dkv, gate_done[0])
        dkv_low = jnp.where(core == 0, rotate_back(dkv, cosine, sine), dkv).astype(bf16)
        attention_args.append((normed, dkv_low, 0))
        fars.append(grad_far(*attention_args[-1]))
        dkv_low = after(dkv_low, fars)
        factor_part = lax.dynamic_slice_in_dim(factor_first, t * part, part, 0)
        own_biases = jnp.sum(
            jnp.concatenate([dq_low, dkv_low], axis=1).astype(f32), axis=0, keepdims=True
        )
        slots = lax.dynamic_update_slice(
            jnp.zeros((n_t, (heads + 1) * HD), f32), own_biases, (t, 0)
        )
        small_grads = jnp.concatenate(
            [jnp.zeros((1, width), f32), ffn_gain_grad, slots.reshape(1, -1)], axis=1
        )
        grad_qkv = qkv_back(meta, dq_low, dkv_low, w_q, w_kv)
        up_done = unit_done(gate_up_own[units:], after(up_got, grad_qkv))
        small_grads, input_grad = input_back(
            after(grad_qkv, up_done[0]),
            inputs_part,
            factor_part,
            gain_first,
            grad_middle,
            small_grads,
        )
        input_grad = input_grad.reshape(rows, width)
        if n_f > 2:
            small_grads = lax.psum(small_grads, "fsdp")
        attention_parts = [
            grad_sum(*args, far, small_grads) for args, far in zip(attention_args, fars)
        ]
        wd_grad = unit_whole(*after(down_done, small_grads))
        wg_grad = unit_whole(*after(gate_done, small_grads))
        small_grads, up_done, wg_grad, wd_grad = lax.optimization_barrier(
            (small_grads, up_done, wg_grad, wd_grad)
        )
        wo_grad, wq_grad, packed, wkv_all, outputs = context_sum(
            n_f == 2, attention_parts, small_grads, out_part, middle
        )
        outputs = outputs.reshape(rows, width)
        wkv_all = wkv_all.astype(f32)
        wk_grad = jnp.concatenate([wkv_all[0], wkv_all[2]], axis=1)
        wv_grad = jnp.concatenate([wkv_all[1], wkv_all[3]], axis=1)
        packed = packed[0]
        attn_gain_grad = lax.dynamic_slice_in_dim(packed, f * piece, piece, 0)
        ffn_gain_grad = lax.dynamic_slice_in_dim(packed, width + f * piece, piece, 0)
        slots = packed[2 * width :].reshape(n_t, heads + 1, HD)
        slots = lax.dynamic_slice_in_dim(slots, f * (HD // n_f), HD // n_f, 2)
        bq_out = lax.dynamic_index_in_dim(slots, t, 0, keepdims=False)[:heads]
        bk_out = slots[0::2, heads]
        bv_out = slots[1::2, heads]

        wu_grad = unit_whole(*up_done)
        wg_grad, wu_grad = wg_grad.T, wu_grad.T

        return (
            outputs,
            input_grad,
            attn_gain_grad,
            wq_grad,
            bq_out,
            wk_grad,
            bk_out,
            wv_grad,
            bv_out,
            wo_grad,
            ffn_gain_grad,
            wg_grad,
            wu_grad,
            wd_grad,
        )

    return local


def solution(mesh):
    in_specs = (
        P(("fsdp", "context"), None),
        P(("fsdp", "context"), None),
        P("fsdp", None),
        P("fsdp"),
        P("fsdp", "tensor"),
        P("tensor", "fsdp"),
        P("fsdp", None),
        P(None, "fsdp"),
        P("fsdp", None),
        P(None, "fsdp"),
        P("tensor", "fsdp"),
        P("fsdp"),
        P("fsdp", "tensor"),
        P("fsdp", "tensor"),
        P("tensor", "fsdp"),
    )
    out_specs = (
        P(("fsdp", "context"), None),
        P(("fsdp", "context"), None),
        P("fsdp"),
        P("fsdp", "tensor"),
        P("tensor", "fsdp"),
        P("fsdp", None),
        P(None, "fsdp"),
        P("fsdp", None),
        P(None, "fsdp"),
        P("tensor", "fsdp"),
        P("fsdp"),
        P("fsdp", "tensor"),
        P("fsdp", "tensor"),
        P("tensor", "fsdp"),
    )
    local = build(mesh.shape["fsdp"], mesh.shape["context"], mesh.shape["tensor"])
    return jax.shard_map(local, mesh=mesh, in_specs=in_specs, out_specs=out_specs, check_vma=False)
```

```python
import functools

import jax
import jax.numpy as jnp
from jax import lax
from jax.experimental import pallas as pl
from jax.experimental.pallas import tpu as pltpu
from jax.sharding import PartitionSpec as P

H = 12
KV = 2
HD = 128
BLOCK = 256

EPSILON = 1e-06
ROPE_BASE = 1000000.0
MASKED = -1e30
SCALING = HD ** (-0.5)
LANES = 128
VMEM_LIMIT = 60 << 20
FFN_VMEM_LIMIT = 63 << 20

f32 = jnp.float32
bf16 = jnp.bfloat16


def rope_tables(positions):
    halfway = HD // 2
    frequency = ROPE_BASE ** (-(jnp.arange(halfway, dtype=f32) * 2.0 / HD))
    angles = positions.astype(f32)[:, None] * frequency[None, :]
    cosine, sine = jnp.cos(angles), jnp.sin(angles)
    return (jnp.concatenate([cosine, cosine], axis=1), jnp.concatenate([sine, sine], axis=1))


def rotate(field, cosine, sine):
    halfway = HD // 2
    turned = jnp.concatenate([-field[..., halfway:], field[..., :halfway]], axis=-1)
    return field * cosine + turned * sine


def rotate_back(grad_field, cosine, sine):
    halfway = HD // 2
    moved = grad_field * sine
    turned = jnp.concatenate([moved[..., halfway:], -moved[..., :halfway]], axis=-1)
    return grad_field * cosine + turned


def dot(left, right):
    return jnp.dot(left, right, preferred_element_type=f32)


def dot_rows(left, right):
    return lax.dot_general(left, right, (((0,), (0,)), ((), ())), preferred_element_type=f32)


def dot_cols(left, right):
    return lax.dot_general(left, right, (((1,), (1,)), ((), ())), preferred_element_type=f32)


def mask_row(kb_ref, own_block, key_blocks):
    return jnp.concatenate(
        [
            jnp.full((1, BLOCK), jnp.where(kb_ref[j] <= own_block, 0.0, MASKED), f32)
            for j in range(key_blocks)
        ],
        axis=1,
    )


def attention_kernel(key_blocks, kb_ref, q_ref, k_ref, v_ref, o_ref, lse_ref):
    bias = mask_row(kb_ref, kb_ref[pl.program_id(1)], key_blocks)
    scores = dot_cols(q_ref[...], k_ref[...]) * SCALING + bias
    row_max = jnp.max(scores, axis=1, keepdims=True)
    expo = jnp.exp(scores - row_max)
    total = jnp.sum(expo, axis=1, keepdims=True)
    probability = (expo * (1.0 / total)).astype(bf16)
    o_ref[...] = dot(probability, v_ref[...]).astype(bf16)
    lse_ref[0] = row_max + jnp.log(total)


def attention(key_blocks, queries, kv):
    rows, width = queries.shape
    heads = width // HD
    whole = lambda kind: pl.BlockSpec((None,) + kv.shape[1:], lambda h, i, kb: (kind, 0, 0))
    tile = pl.BlockSpec((BLOCK, HD), lambda h, i, kb: (i, h))
    return pl.pallas_call(
        functools.partial(attention_kernel, kv.shape[1] // BLOCK),
        name="attention",
        grid_spec=pltpu.PrefetchScalarGridSpec(
            num_scalar_prefetch=1,
            grid=(heads, rows // BLOCK),
            in_specs=[tile, whole(0), whole(1)],
            out_specs=[tile, pl.BlockSpec((1, BLOCK, 1), lambda h, i, kb: (h, i, 0))],
        ),
        out_shape=[
            jax.ShapeDtypeStruct((rows, width), bf16),
            jax.ShapeDtypeStruct((heads, rows, 1), f32),
        ],
        compiler_params=pltpu.CompilerParams(vmem_limit_bytes=VMEM_LIMIT),
    )(key_blocks, queries, kv, kv)


def attention_back_kernel(
    key_blocks,
    kb_ref,
    q_ref,
    do_ref,
    lse_ref,
    cos_ref,
    sin_ref,
    k_ref,
    v_ref,
    dq_ref,
    dkv_ref,
    dk_ref,
    dv_ref,
):
    head, i = pl.program_id(0), pl.program_id(1)

    @pl.when((head == 0) & (i == 0))
    def _():
        dk_ref[...] = jnp.zeros_like(dk_ref)
        dv_ref[...] = jnp.zeros_like(dv_ref)

    bias = mask_row(kb_ref, kb_ref[i], key_blocks)
    scores = dot_cols(q_ref[...], k_ref[...]) * SCALING + bias
    probability = jnp.exp(scores - lse_ref[0])
    grad_probs = dot_cols(do_ref[...], v_ref[...])
    inner = jnp.sum(probability * grad_probs, axis=1, keepdims=True)
    grad_scores = (probability * (grad_probs - inner)).astype(bf16)
    grad_query = dot(grad_scores, k_ref[...]) * SCALING
    moved = grad_query * sin_ref[...]
    sign = jnp.where(lax.broadcasted_iota(jnp.int32, moved.shape, 1) < HD // 2, 1.0, -1.0)
    dq_ref[...] = (
        grad_query * cos_ref[...] + pltpu.roll(moved, HD // 2, 1) * sign
    ).astype(bf16)
    dk_ref[...] += dot_rows(grad_scores, q_ref[...]) * SCALING
    dv_ref[...] += dot_rows(probability.astype(bf16), do_ref[...])

    @pl.when((head == pl.num_programs(0) - 1) & (i == pl.num_programs(1) - 1))
    def _():
        dkv_ref[0] = dk_ref[...].astype(bf16)
        dkv_ref[1] = dv_ref[...].astype(bf16)


def attention_back(key_blocks, queries, grad_out, lse, cosine, sine, kv):
    rows, width = queries.shape
    heads = width // HD
    whole = lambda kind: pl.BlockSpec((None,) + kv.shape[1:], lambda h, i, kb: (kind, 0, 0))
    tile = pl.BlockSpec((BLOCK, HD), lambda h, i, kb: (i, h))
    table = pl.BlockSpec((BLOCK, HD), lambda h, i, kb: (i, 0))
    return pl.pallas_call(
        functools.partial(attention_back_kernel, kv.shape[1] // BLOCK),
        name="attention_back",
        grid_spec=pltpu.PrefetchScalarGridSpec(
            num_scalar_prefetch=1,
            grid=(heads, rows // BLOCK),
            in_specs=[
                tile,
                tile,
                pl.BlockSpec((1, BLOCK, 1), lambda h, i, kb: (h, i, 0)),
                table,
                table,
                whole(0),
                whole(1),
            ],
            out_specs=[tile, pl.BlockSpec(kv.shape, lambda h, i, kb: (0, 0, 0))],
            scratch_shapes=[pltpu.VMEM(kv.shape[1:], f32)] * 2,
        ),
        out_shape=[
            jax.ShapeDtypeStruct((rows, width), bf16),
            jax.ShapeDtypeStruct(kv.shape, bf16),
        ],
        compiler_params=pltpu.CompilerParams(vmem_limit_bytes=VMEM_LIMIT),
    )(key_blocks, queries, grad_out, lse, cosine, sine, kv, kv)


def qkv_kernel(pieces, meta_ref, x_ref, gain_ref, bias_ref, cos_ref, sin_ref, *refs):
    weights, (xn_ref, factor_ref, q_ref, kv_ref) = refs[: 2 * pieces], refs[2 * pieces :]
    values = x_ref[...].astype(f32)
    factor = lax.rsqrt(jnp.mean(values * values, axis=-1, keepdims=True) + EPSILON)
    factor_ref[...] = factor
    xn_ref[...] = (values * factor * gain_ref[...]).astype(bf16)
    depth = weights[0].shape[0]
    normed = [xn_ref[:, columns_of(meta_ref, j, depth, pieces)] for j in range(pieces)]
    cosine, sine = cos_ref[...], sin_ref[...]
    sign = jnp.where(lax.broadcasted_iota(jnp.int32, cosine.shape, 1) < HD // 2, -1.0, 1.0)
    sine = sine * sign
    width = q_ref.shape[1]
    total = bias_ref[:, :width] + sum(dot(x, w[...]) for x, w in zip(normed, weights[:pieces]))
    turn = lambda own: own * cosine + pltpu.roll(own, HD // 2, 1) * sine
    for h in range(width // HD):
        q_ref[:, h * HD : (h + 1) * HD] = turn(total[:, h * HD : (h + 1) * HD]).astype(bf16)
    own = bias_ref[:, width:] + sum(dot(x, w[...]) for x, w in zip(normed, weights[pieces:]))
    kv_ref[...] = jnp.where(meta_ref[2] == 0, turn(own), own).astype(bf16)


def columns_of(meta_ref, j, depth, pieces):
    if pieces == 1:
        return slice(None)
    return pl.ds(pl.multiple_of(meta_ref[j] * depth, LANES), depth)


def qkv(meta, inputs, gain, bias, cosine, sine, w_q, w_kv):
    rows, width = inputs.shape
    out = w_q[0].shape[1]
    tile = 256
    row = lambda n: pl.BlockSpec((tile, n), lambda i, m: (i, 0))
    fixed = lambda w: pl.BlockSpec(w.shape, lambda i, m: (0, 0))
    return pl.pallas_call(
        functools.partial(qkv_kernel, len(w_q)),
        name="qkv",
        grid_spec=pltpu.PrefetchScalarGridSpec(
            num_scalar_prefetch=1,
            grid=(rows // tile,),
            in_specs=[row(width), fixed(gain), fixed(bias), row(HD), row(HD)]
            + [fixed(w) for w in (*w_q, *w_kv)],
            out_specs=[row(width), row(1), row(out), row(HD)],
        ),
        out_shape=[
            jax.ShapeDtypeStruct((rows, width), bf16),
            jax.ShapeDtypeStruct((rows, 1), f32),
            jax.ShapeDtypeStruct((rows, out), bf16),
            jax.ShapeDtypeStruct((rows, HD), bf16),
        ],
        compiler_params=pltpu.CompilerParams(vmem_limit_bytes=VMEM_LIMIT),
    )(meta, inputs, gain, bias, cosine, sine, *w_q, *w_kv)


def qkv_back_kernel(pieces, meta_ref, dq_ref, dkv_ref, *refs):
    w_q, w_kv, out_ref = refs[:pieces], refs[pieces : 2 * pieces], refs[-1]
    for j in range(pieces):
        out_ref[:, columns_of(meta_ref, j, w_q[j].shape[0], pieces)] = (
            dot_cols(dq_ref[...], w_q[j][...]) + dot_cols(dkv_ref[...], w_kv[j][...])
        ).astype(bf16)


def qkv_back(meta, grad_q, grad_kv, w_q, w_kv):
    rows, width = grad_q.shape[0], sum(w.shape[0] for w in w_q)
    tile = 256
    row = lambda n: pl.BlockSpec((tile, n), lambda i, m: (i, 0))
    fixed = lambda w: pl.BlockSpec(w.shape, lambda i, m: (0, 0))
    return pl.pallas_call(
        functools.partial(qkv_back_kernel, len(w_q)),
        name="qkv_back",
        grid_spec=pltpu.PrefetchScalarGridSpec(
            num_scalar_prefetch=1,
            grid=(rows // tile,),
            in_specs=[row(grad_q.shape[1]), row(HD)] + [fixed(w) for w in (*w_q, *w_kv)],
            out_specs=row(width),
        ),
        out_shape=jax.ShapeDtypeStruct((rows, width), bf16),
        compiler_params=pltpu.CompilerParams(vmem_limit_bytes=VMEM_LIMIT),
    )(meta, grad_q, grad_kv, *w_q, *w_kv)


def ffn_kernel(pieces, meta_ref, x_ref, dy_ref, *refs):
    wg, wu, wd = (refs[m * pieces : (m + 1) * pieces] for m in range(3))
    refs = refs[3 * pieces :]
    hid_ref, dg_ref, du_ref, dx_ref, out_ref = refs[:5]
    columns = [columns_of(meta_ref, j, wg[j].shape[1], pieces) for j in range(pieces)]
    gate = sum(dot_cols(x_ref[:, at], w[...]) for at, w in zip(columns, wg))
    up = sum(dot_cols(x_ref[:, at], w[...]) for at, w in zip(columns, wu))
    grad_hidden = sum(dot_cols(dy_ref[:, at], w[...]) for at, w in zip(columns, wd))
    sigma = 1.0 / (1.0 + jnp.exp(-gate))
    gated = gate * sigma
    hid_ref[...] = (gated * up).astype(bf16)
    dg_ref[...] = (grad_hidden * up * (sigma + gated * (1.0 - sigma))).astype(bf16)
    du_ref[...] = (grad_hidden * gated).astype(bf16)
    step, steps = pl.program_id(0), pl.num_programs(0)

    @pl.when(step // (steps // 2) == meta_ref[3])
    def _():
        for at, g, u, d in zip(columns, wg, wu, wd):
            dx_ref[:, at] = (dot(dg_ref[...], g[...]) + dot(du_ref[...], u[...])).astype(bf16)
            out_ref[:, at] = dot(hid_ref[...], d[...]).astype(bf16)

    if pieces == 2:
        outs, totals = refs[5:8], refs[8:11]
        sources = ((hid_ref, dy_ref), (dg_ref, x_ref), (du_ref, x_ref))

        @pl.when(step == 0)
        def _():
            for total in totals:
                total[...] = jnp.zeros_like(total)

        for total, (unit, row) in zip(totals, sources):
            total[...] += dot_rows(unit[...], row[:, columns[1]])

        @pl.when(step == steps - 1)
        def _():
            for out, total in zip(outs, totals):
                out[...] = total[...].astype(bf16)


def ffn(meta, normed, grad_out, weights):
    width = normed.shape[-1]
    rows = normed.shape[0] * normed.shape[1]
    pieces = len(weights)
    units, depth = weights[0].shape[0] // 3, weights[0].shape[1]
    tile = 512
    steps = rows // tile
    half = steps // 2
    flat = lambda x: x.reshape(-1, width)
    read = pl.BlockSpec((tile, width), lambda i, m: (lax.rem(i + m[3] * half, steps), 0))
    once = pl.Buffered(1)
    weight = lambda w, k: pl.BlockSpec((units, depth), lambda i, m: (k, 0), pipeline_mode=once)
    placed = pl.BlockSpec((tile, units), lambda i, m: (i, 0))
    near = pl.BlockSpec((tile, width), lambda i, m: (jnp.clip(i - m[3] * half, 0, half - 1), 0))
    grads = [pl.BlockSpec((units, depth), lambda i, m: (0, 0), pipeline_mode=once)] * 3
    grads = grads if pieces == 2 else []
    shapes = [(rows, units)] * 3 + [(rows // 2, width)] * 2 + [(units, depth)] * len(grads)
    return pl.pallas_call(
        functools.partial(ffn_kernel, pieces),
        name="ffn",
        grid_spec=pltpu.PrefetchScalarGridSpec(
            num_scalar_prefetch=1,
            grid=(steps,),
            in_specs=[read, read] + [weight(w, k) for k in range(3) for w in weights],
            out_specs=[placed] * 3 + [near] * 2 + grads,
            scratch_shapes=[pltpu.VMEM((units, depth), f32)] * len(grads),
        ),
        out_shape=[jax.ShapeDtypeStruct(shape, bf16) for shape in shapes],
        compiler_params=pltpu.CompilerParams(vmem_limit_bytes=FFN_VMEM_LIMIT),
    )(meta, flat(normed), flat(grad_out), *(list(weights) * 3))


def unit_grads_kernel(count, meta_ref, near_ref, far_ref, *refs):
    units, out_ref, x_ref = refs[:count], refs[-2], refs[-1]
    half = near_ref.shape[0]
    x_ref[pl.ds(pl.multiple_of(meta_ref[3] * half, half), half)] = near_ref[...]
    x_ref[pl.ds(pl.multiple_of((1 - meta_ref[3]) * half, half), half)] = far_ref[...]
    for k, unit in enumerate(units):
        depth = unit.shape[1]
        out_ref[k * depth : (k + 1) * depth] = dot_rows(unit[...], x_ref[...]).astype(bf16)


def unit_grads(meta, which, pieces, x, units_of):
    width = x.shape[-1]
    count, (rows, units) = len(units_of), units_of[0].shape
    depth = width // pieces
    tile = 256
    steps = depth // tile
    shard = (lambda m: m[which]) if pieces > 1 else (lambda m: 0)
    feature = lambda half: pl.BlockSpec(
        (rows // 2, tile), lambda i, m: (half, shard(m) * steps + i)
    )
    unit = pl.BlockSpec((rows, units), lambda i, m: (0, 0), pipeline_mode=pl.Buffered(1))
    x = x.reshape(-1, width)
    return pl.pallas_call(
        functools.partial(unit_grads_kernel, count),
        name=f"unit_grads_{which}_{count}",
        grid_spec=pltpu.PrefetchScalarGridSpec(
            num_scalar_prefetch=1,
            grid=(steps,),
            in_specs=[feature(0), feature(1)] + [unit] * count,
            out_specs=pl.BlockSpec((count * units, tile), lambda i, m: (0, i)),
            scratch_shapes=[pltpu.VMEM((rows, tile), bf16)],
        ),
        out_shape=jax.ShapeDtypeStruct((count * units, depth), bf16),
        compiler_params=pltpu.CompilerParams(vmem_limit_bytes=VMEM_LIMIT),
    )(meta, x, x, *units_of)


class Wires:
    def __init__(self, sends, receives, locals_):
        self.sends, self.receives, self.locals = sends, receives, locals_
        self.used = self.used_local = 0
        self.started = []

    def plan(self, source, target, device):
        k = self.used
        self.used += 1
        return pltpu.make_async_remote_copy(
            source,
            target,
            self.sends.at[k],
            self.receives.at[k],
            device_id=device,
            device_id_type=pl.DeviceIdType.MESH,
        )

    def copy(self, source, target, device):
        one = self.plan(source, target, device)
        one.start()
        self.started.append(one)
        return one

    def here(self, source, target):
        k = self.used_local
        self.used_local += 1
        one = pltpu.make_async_copy(source, target, self.locals.at[k])
        one.start()
        return one

    def finish(self):
        for one in self.started:
            one.wait_send()


class OwnGrad:
    TILE = 256

    def __init__(self, units, rows, out, units_here, rows_here):
        self.units, self.rows, self.out = units, rows, out
        self.units_here, self.rows_here = units_here, rows_here
        self.tiles = out.shape[1] // self.TILE
        self.copies = None

    def fetch(self, wires):
        half, depth = self.rows.shape[0] // 2, self.out.shape[1]
        column = pl.multiple_of(lax.axis_index("fsdp") * depth, LANES)
        pair = lax.axis_index("context") // 2
        self.copies = [wires.here(self.units, self.units_here)]
        for k, place in ((0, pair), (1, 1 - pair)):
            self.copies.append(
                wires.here(
                    self.rows.at[pl.ds(k * half, half), pl.ds(column, depth)],
                    self.rows_here.at[pl.ds(pl.multiple_of(place * half, half), half)],
                )
            )

    def make(self, first, past):
        for one in self.copies:
            one.wait()
        self.copies = []

        @pl.loop(first, past)
        def _(k):
            at = pl.ds(pl.multiple_of(k * self.TILE, self.TILE), self.TILE)
            self.out[:, at] = dot_rows(self.units_here[...], self.rows_here[:, at]).astype(bf16)


def own_grad_call(fill, width):
    args = [x for pair in fill for x in pair]
    outs = [jax.ShapeDtypeStruct((units.shape[1], width), bf16) for units, _ in fill]
    scratch = []
    for units, rows in fill:
        scratch += [pltpu.VMEM(units.shape, bf16), pltpu.VMEM((rows.shape[0], width), bf16)]
    return args, outs, scratch


def own_grads(count, args, outs, scratch):
    return [
        OwnGrad(args[2 * k], args[2 * k + 1], outs[k], scratch[2 * k], scratch[2 * k + 1])
        for k in range(count)
    ]


def meet(devices):
    barrier = pltpu.get_barrier_semaphore()
    for device in devices:
        pl.semaphore_signal(barrier, inc=1, device_id=device, device_id_type=pl.DeviceIdType.MESH)
    pl.semaphore_wait(barrier, len(devices))


def partners():
    c, t = lax.axis_index("context"), lax.axis_index("tensor")
    flip = lambda x, bit: x + bit * (1 - 2 * lax.rem(x // bit, 2))
    return {
        "core": {"tensor": flip(t, 1)},
        "y": {"tensor": flip(t, 2)},
        "z": {"context": flip(c, 1)},
        "far": {"context": flip(c, 2)},
        "last": {"context": flip(flip(c, 1), 2)},
    }


def wide(x):
    return x.astype(f32)


def ranks():
    t = lax.axis_index("tensor")
    flip = lambda x, bit: x + bit * (1 - 2 * lax.rem(x // bit, 2))
    return (t, flip(t, 1), flip(t, 2), flip(flip(t, 1), 2))


def scatter_rank(wires, to, part, own, got_core, sent, got_y):
    size = part.shape[1] // 2
    halves = [pl.ds(0, size), pl.ds(size, size)]
    rank = ranks()
    from_core = {}
    for block in (1, 0):
        for k, at in enumerate(halves):
            from_core[block, k] = wires.copy(
                part.at[rank[1 + 2 * block], at], got_core.at[block, at], to["core"]
            )
    mine = [wires.here(part.at[rank[2 * block]], own.at[block]) for block in (0, 1)]
    yield
    for one in mine:
        one.wait()
    from_y = []
    for k, at in enumerate(halves):
        from_core[1, k].wait_recv()
        sent[at] = (wide(own[1, at]) + wide(got_core[1, at])).astype(bf16)
        from_y.append(wires.copy(sent.at[at], got_y.at[at], to["y"]))
    yield
    for k in range(2):
        from_core[0, k].wait_recv()
    total = wide(own[0]) + wide(got_core[0])
    for one in from_y:
        one.wait_recv()
    return total + wide(got_y[...])


def scatter_pair(wires, to, part, own, got_core, sent, got_y, got_z, diag_y, diag_z):
    size = part.shape[1] // 2
    low, high = pl.ds(0, size), pl.ds(size, size)
    from_core = {j: wires.copy(part.at[4 + j], got_core.at[j], to["core"]) for j in (3, 1, 2, 0)}
    mine = wires.here(part.at[pl.ds(0, 4)], own)
    yield
    mine.wait()
    both = lambda j, at: wide(own[j, at]) + wide(got_core[j, at])
    from_core[3].wait_recv()
    sent[2] = (wide(own[3]) + wide(got_core[3])).astype(bf16)
    via_z = wires.copy(sent.at[2, low], diag_z, to["z"])
    via_y = wires.copy(sent.at[2, high], diag_y, to["y"])
    from_core[1].wait_recv()
    sent[0, high] = both(1, high).astype(bf16)
    y_high = wires.copy(sent.at[0, high], got_y.at[high], to["y"])
    from_core[2].wait_recv()
    sent[1, low] = both(2, low).astype(bf16)
    z_low = wires.copy(sent.at[1, low], got_z.at[low], to["z"])
    yield
    via_z.wait_recv()
    sent[0, low] = (both(1, low) + wide(diag_z[...])).astype(bf16)
    y_low = wires.copy(sent.at[0, low], got_y.at[low], to["y"])
    via_y.wait_recv()
    sent[1, high] = (both(2, high) + wide(diag_y[...])).astype(bf16)
    z_high = wires.copy(sent.at[1, high], got_z.at[high], to["z"])
    yield
    from_core[0].wait_recv()
    total = wide(own[0]) + wide(got_core[0])
    for one in (y_high, z_low, y_low, z_high):
        one.wait_recv()
    return total + wide(got_y[...]) + wide(got_z[...])


def result_of(steps):
    while True:
        try:
            next(steps)
        except StopIteration as done:
            return done.value


def gather_rank(wires, to, block, out):
    size = block.shape[0] // 2
    halves = [pl.ds(0, size), pl.ds(size, size)]
    rank = ranks()
    mine = wires.here(block, out.at[rank[0]])
    from_y = [wires.copy(block.at[h], out.at[rank[0], h], to["y"]) for h in halves]
    from_core = [wires.copy(block, out.at[rank[0]], to["core"])]
    yield
    for h, one in zip(halves, from_y):
        one.wait_recv()
        from_core.append(wires.copy(out.at[rank[2], h], out.at[rank[2], h], to["core"]))
    for one in from_core:
        one.wait_recv()
    mine.wait()


def gather_pair(wires, to, block, out, base):
    size = block.shape[0] // 2
    low, high = pl.ds(0, size), pl.ds(size, size)
    at = lambda j: out.at[base + j]
    from_z = wires.copy(block, at(2), to["z"])
    yield
    from_y = wires.copy(block, at(1), to["y"])
    from_core = [wires.copy(block, at(4), to["core"])]
    yield
    from_y.wait_recv()
    via_z = wires.copy(out.at[base + 1, low], out.at[base + 3, low], to["z"])
    from_core.append(wires.copy(at(1), at(5), to["core"]))
    from_z.wait_recv()
    via_y = wires.copy(out.at[base + 2, high], out.at[base + 3, high], to["y"])
    from_core.append(wires.copy(at(2), at(6), to["core"]))
    yield
    via_z.wait_recv()
    via_y.wait_recv()
    from_core.append(wires.copy(at(3), at(7), to["core"]))
    return from_core


def remote_call(kernel, name, key, args, outs, scratch, copies, in_vmem):
    ins, out_in = in_vmem
    spec = lambda inside: pl.BlockSpec(memory_space=pltpu.VMEM if inside else pl.ANY)
    return pl.pallas_call(
        kernel,
        name=name,
        out_shape=outs,
        in_specs=[spec(x) for x in ins],
        out_specs=[spec(x) for x in out_in],
        scratch_shapes=list(scratch)
        + [
            pltpu.SemaphoreType.DMA((copies,)),
            pltpu.SemaphoreType.DMA((copies,)),
            pltpu.SemaphoreType.DMA((8,)),
        ],
        compiler_params=pltpu.CompilerParams(
            collective_id=key, has_side_effects=True, vmem_limit_bytes=VMEM_LIMIT
        ),
    )(*args)


def kv_gather_kernel(own_ref, out_ref, *sems):
    wires, to = Wires(*sems), partners()
    kind = lax.rem(lax.axis_index("tensor"), 2)
    rows = own_ref.shape[0]
    block = lambda j: out_ref.at[kind, pl.ds(j * rows, rows)]
    meet([to[k] for k in ("core", "z", "far", "last")])
    mine = wires.here(own_ref, block(0))
    arrive = [wires.copy(own_ref, block(j), to[k]) for j, k in ((3, "last"), (2, "far"), (1, "z"))]
    from_core = [wires.copy(own_ref, block(0), to["core"])]
    for j, one in ((1, arrive[2]), (2, arrive[1]), (3, arrive[0])):
        one.wait_recv()
        from_core.append(wires.copy(block(j), block(j), to["core"]))
    for one in from_core:
        one.wait_recv()
    mine.wait()
    wires.finish()


def kv_gather(own):
    rows, width = own.shape
    n_c = lax.axis_size("context")
    return remote_call(
        kv_gather_kernel,
        "kv_gather",
        0,
        [own],
        [jax.ShapeDtypeStruct((2, n_c * rows, width), bf16)],
        [],
        8,
        ([False], [False]),
    )[0]


def kv_scatter_kernel(count, part_ref, *refs):
    args, dkv_ref, outs = refs[: 2 * count], refs[2 * count], refs[2 * count + 1 : 3 * count + 1]
    own, got_core, sent, got = refs[3 * count + 1 : 3 * count + 5]
    wires, to = Wires(*refs[-3:]), partners()
    fill = own_grads(count, args, outs, refs[3 * count + 5 : -3])
    kind = lax.rem(lax.axis_index("tensor"), 2)
    rows = dkv_ref.shape[0]
    block = lambda j: pl.ds(j * rows, rows)
    meet([to[k] for k in ("core", "z", "far", "last")])
    steps = ((3, "last"), (2, "far"), (1, "z"), (0, None))
    from_core = {
        j: wires.copy(part_ref.at[1 - kind, block(j)], got_core.at[block(j)], to["core"])
        for j, _ in steps
    }
    mine = wires.here(part_ref.at[kind], own)
    for one in fill:
        one.fetch(wires)
    mine.wait()
    arrive = []
    for j, k in steps[:3]:
        from_core[j].wait_recv()
        sent[block(j)] = (wide(own[block(j)]) + wide(got_core[block(j)])).astype(bf16)
        arrive.append(wires.copy(sent.at[block(j)], got.at[block(j)], to[k]))
    for one in fill:
        one.make(0, one.tiles)
    from_core[0].wait_recv()
    total = wide(own[block(0)]) + wide(got_core[block(0)])
    for one in arrive:
        one.wait_recv()
    for j in (1, 2, 3):
        total = total + wide(got[block(j)])
    dkv_ref[...] = total
    wires.finish()


def kv_scatter(part, fill, width):
    _, rows, depth = part.shape
    n_c = lax.axis_size("context")
    args, outs, scratch = own_grad_call(fill, width)
    return remote_call(
        functools.partial(kv_scatter_kernel, len(fill)),
        "kv_scatter",
        1,
        [part, *args],
        [jax.ShapeDtypeStruct((rows // n_c, depth), f32), *outs],
        [pltpu.VMEM((rows, depth), bf16)] * 4 + scratch,
        7,
        ([False] * (1 + len(args)), [True] * (1 + len(outs))),
    )


def middle_kernel(
    part,
    x_ref,
    gain_ref,
    dy_ref,
    dy_y,
    dy_z,
    dy_far,
    mid_ref,
    factor_ref,
    out,
    dys,
    own,
    core,
    sent,
    got,
    xn,
    *sems,
):
    wires, to = Wires(*sems), partners()
    blocks = out.shape[0] // 2
    size = xn.shape[0] // 2
    low, high = pl.ds(0, size), pl.ds(size, size)
    meet([to[k] for k in ("core", "y", "z", "far")])
    summed = scatter_rank(wires, to, part, own, core, sent, got)
    next(summed)
    mine = [
        wires.here(block, dys.at[k])
        for block, k in ((dy_ref, 0), (dy_y, 1), (dy_z, 2), (dy_far, blocks))
    ]
    via_z = wires.copy(dy_y.at[low], dys.at[3, low], to["z"])
    dy_last = gather_pair(wires, to, dy_far, dys, blocks)
    next(dy_last)
    next(summed)
    via_y = wires.copy(dy_z.at[high], dys.at[3, high], to["y"])
    ends = [
        wires.copy(block, dys.at[4 + k], to["core"])
        for k, block in enumerate((dy_ref, dy_y, dy_z))
    ]
    next(dy_last)
    middle = wide(x_ref[...]) + result_of(summed)
    mid_ref[...] = middle
    factor = lax.rsqrt(jnp.mean(middle * middle, axis=-1, keepdims=True) + EPSILON)
    factor_ref[...] = factor
    xn[...] = (middle * factor * gain_ref[...]).astype(bf16)
    mine.append(wires.here(xn, out.at[0]))
    xn_far = wires.copy(xn, out.at[blocks], to["far"])
    xn_near = gather_pair(wires, to, xn, out, 0)
    next(xn_near)
    next(xn_near)
    via_z.wait_recv()
    via_y.wait_recv()
    ends.append(wires.copy(dys.at[3], dys.at[7], to["core"]))
    next(dy_last)
    next(xn_near)
    xn_far.wait_recv()
    xn_last = gather_pair(wires, to, out.at[blocks], out, blocks)
    next(xn_last)
    next(xn_last)
    ends += result_of(dy_last) + result_of(xn_near)
    next(xn_last)
    ends += result_of(xn_last)
    for one in ends:
        one.wait_recv()
    for one in mine:
        one.wait()
    wires.finish()


def middle_norm(part, inputs_part, gain, dy_blocks):
    rows, width = inputs_part.shape
    return remote_call(
        middle_kernel,
        "middle_norm",
        2,
        [part.reshape(4, rows, width), inputs_part, gain, *dy_blocks],
        [
            jax.ShapeDtypeStruct((rows, width), f32),
            jax.ShapeDtypeStruct((rows, 1), f32),
            jax.ShapeDtypeStruct((16, rows, width), bf16),
            jax.ShapeDtypeStruct((16, rows, width), bf16),
        ],
        [
            pltpu.VMEM((2, rows, width), bf16),
            pltpu.VMEM((2, rows, width), bf16),
            pltpu.VMEM((rows, width), bf16),
            pltpu.VMEM((rows, width), bf16),
            pltpu.VMEM((rows, width), bf16),
        ],
        48,
        ([False] + [True] * 6, [True, True, False, False]),
    )


def norm_back_rows(values, factor, gain, grad_normed):
    gained = gain * grad_normed
    inner = jnp.mean(gained * values, axis=-1, keepdims=True)
    grad_values = factor * gained - values * (factor * factor * factor) * inner
    return grad_values, jnp.sum(grad_normed * values * factor, axis=0, keepdims=True)


def middle_back_kernel(count, part, mid_ref, factor_ref, gain_ref, dy_ref, *refs):
    args, (dmid_ref, dgain_ref, out) = refs[: 2 * count], refs[2 * count : 2 * count + 3]
    outs, refs = refs[2 * count + 3 : 3 * count + 3], refs[3 * count + 3 :]
    low, first, wires, to = refs[0], refs[1:8], Wires(*refs[-3:]), partners()
    fill = own_grads(count, args, outs, refs[8:-3])
    meet([to[k] for k in ("core", "y", "z")])
    back = scatter_pair(wires, to, part, *first)
    next(back)
    for one in fill:
        one.fetch(wires)
    next(back)
    if fill:
        fill[0].make(0, 1)
    next(back)
    if fill:
        fill[0].make(1, fill[0].tiles)
    grad_normed = result_of(back)
    du, dgain = norm_back_rows(mid_ref[...], factor_ref[...], gain_ref[...], grad_normed)
    dgain_ref[...] = dgain
    dmid = wide(dy_ref[...]) + du
    low[...] = dmid.astype(bf16)
    share = gather_rank(wires, to, low, out)
    next(share)
    dmid_ref[...] = dmid
    for one in fill[1:]:
        one.make(0, one.tiles)
    result_of(share)
    wires.finish()


def pair_scratch(rows, width):
    return [
        pltpu.VMEM((4, rows, width), bf16),
        pltpu.VMEM((4, rows, width), bf16),
        pltpu.VMEM((3, rows, width), bf16),
        pltpu.VMEM((rows, width), bf16),
        pltpu.VMEM((rows, width), bf16),
        pltpu.VMEM((rows // 2, width), bf16),
        pltpu.VMEM((rows // 2, width), bf16),
    ]


def middle_back(part, middle, factor, gain, dy_part, fill, shard):
    rows, width = middle.shape
    args, outs, scratch = own_grad_call(fill, shard)
    return remote_call(
        functools.partial(middle_back_kernel, len(fill)),
        "middle_back",
        3,
        [part.reshape(8, rows, width), middle, factor, gain, dy_part, *args],
        [
            jax.ShapeDtypeStruct((rows, width), f32),
            jax.ShapeDtypeStruct((1, width), f32),
            jax.ShapeDtypeStruct((4, rows, width), bf16),
            *outs,
        ],
        [pltpu.VMEM((rows, width), bf16)] + pair_scratch(rows, width) + scratch,
        16,
        (
            [False, True, True, True, True] + [False] * len(args),
            [True, True, False] + [True] * len(outs),
        ),
    )


def add_all(wires, ways, value, slots):
    for k, device in enumerate(ways):
        one = wires.copy(value, slots.at[k], device)
        one.wait()
        wires.started = [x for x in wires.started if x is not one]
        value[...] = value[...] + slots[k]


def input_back_kernel(
    part, x_ref, factor_ref, gain_ref, dmid_ref, small_ref, sum_ref, out, *rest
):
    low, own, core, sent, got, slots = rest[:-3]
    wires, to = Wires(*rest[-3:]), partners()
    meet([to[k] for k in ("core", "y")])
    grad_normed = result_of(scatter_rank(wires, to, part, own, core, sent, got))
    du, dgain = norm_back_rows(wide(x_ref[...]), factor_ref[...], gain_ref[...], grad_normed)
    low[...] = (dmid_ref[...] + du).astype(bf16)
    share = gather_rank(wires, to, low, out)
    next(share)
    width = dgain.shape[1]
    sum_ref[:, width:] = small_ref[:, width:]
    sum_ref[:, :width] = dgain
    add_all(wires, [to["core"], to["y"]], sum_ref, slots)
    result_of(share)
    wires.finish()


def input_back(part, inputs_part, factor, gain, grad_middle, small):
    rows, width = inputs_part.shape
    return remote_call(
        input_back_kernel,
        "input_back",
        5,
        [part.reshape(4, rows, width), inputs_part, factor, gain, grad_middle, small],
        [
            jax.ShapeDtypeStruct(small.shape, f32),
            jax.ShapeDtypeStruct((4, rows, width), bf16),
        ],
        [
            pltpu.VMEM((rows, width), bf16),
            pltpu.VMEM((2, rows, width), bf16),
            pltpu.VMEM((2, rows, width), bf16),
            pltpu.VMEM((rows, width), bf16),
            pltpu.VMEM((rows, width), bf16),
            pltpu.VMEM((2,) + small.shape, f32),
        ],
        16,
        ([False, True, True, True, True, True], [True, False]),
    )


def context_sum_kernel(over_f, *refs):
    parts, small_ref, out_part, mid_ref = refs[:3], refs[3], refs[4], refs[5]
    outs, sum_ref, shared, outputs = refs[6:8], refs[8], refs[9], refs[10]
    lows, from_end, from_middle = refs[11:15], refs[15:19], refs[19:23]
    out_low, slot, scratch = refs[23], refs[24], refs[25:32]
    wires, to, c = Wires(*refs[32:]), partners(), lax.axis_index("context")
    end = (c == 0) | (c == lax.axis_size("context") - 1)
    inner = jnp.logical_not(end)
    greet = ["core", "y", "z", "last"]
    if over_f:
        to["f"] = {"fsdp": 1 - lax.axis_index("fsdp")}
        greet.append("f")
    meet([to[k] for k in greet])
    ahead = scatter_pair(wires, to, out_part, *scratch)
    next(ahead)
    sum_ref[...] = small_ref[...]
    from_f = wires.copy(small_ref, slot, to["f"]) if over_f else None
    next(ahead)
    sources = [*parts, sum_ref]
    chunks = []
    for i, cuts in ((2, 1), (0, 2), (1, 2), (3, 1)):
        size = sources[i].shape[0] // cuts
        chunks += [(i, pl.ds(k * size, size)) for k in range(cuts)]
    inward = [wires.plan(sources[i].at[at], from_end[i].at[at], to["z"]) for i, at in chunks]
    across = [wires.plan(lows[i].at[at], from_middle[i].at[at], to["last"]) for i, at in chunks]
    outward = [wires.plan(lows[i].at[at], lows[i].at[at], to["z"]) for i, at in chunks]
    small = len(chunks) - 1

    def send_in(k):
        @pl.when(end)
        def _():
            inward[k].start()

    def pass_on(first, past):
        @pl.when(inner)
        def _():
            for k in range(first, past):
                i, at = chunks[k]
                inward[k].wait_recv()
                total = wide(sources[i][at]) + wide(from_end[i][at])
                lows[i][at] = total.astype(lows[i].dtype)
                across[k].start()
                if k:
                    send_out(k - 1)

    def send_out(k):
        i, at = chunks[k]
        across[k].wait()
        lows[i][at] = (wide(lows[i][at]) + wide(from_middle[i][at])).astype(lows[i].dtype)
        outward[k].start()

    send_in(0)
    send_in(1)
    next(ahead)
    if over_f:
        from_f.wait_recv()
        sum_ref[...] = sum_ref[...] + slot[...]
    for k in range(2, small + 1):
        send_in(k)
    pass_on(0, 2)
    out_low[...] = (mid_ref[...] + result_of(ahead)).astype(bf16)
    out_share = gather_rank(wires, to, out_low, outputs)
    next(out_share)
    pass_on(2, small + 1)

    @pl.when(inner)
    def _():
        send_out(small)

    result_of(out_share)

    def arrived(k):
        @pl.when(end)
        def _():
            outward[k].wait_recv()

    arrived(0)
    share = gather_rank(wires, to, lows[2], shared)
    next(share)
    for k in range(1, len(chunks)):
        arrived(k)

    @pl.when(end)
    def _():
        for one in inward:
            one.wait_send()

    for i in (0, 1):
        outs[i][...] = wide(lows[i][...])
    sum_ref[...] = lows[3][...]
    result_of(share)

    @pl.when(inner)
    def _():
        for one in outward:
            one.wait_send()

    wires.finish()


def context_sum(over_f, parts, small, out_part, middle):
    rows, width = middle.shape
    lines = [pltpu.VMEM(x.shape, x.dtype) for x in (*parts, small)]
    return remote_call(
        functools.partial(context_sum_kernel, over_f),
        "context_sum",
        6,
        [*parts, small, out_part.reshape(8, rows, width), middle],
        [jax.ShapeDtypeStruct(x.shape, f32) for x in parts[:2]]
        + [jax.ShapeDtypeStruct(small.shape, f32)]
        + [jax.ShapeDtypeStruct((4,) + parts[2].shape, bf16)]
        + [jax.ShapeDtypeStruct((4, rows, width), bf16)],
        lines * 3
        + [pltpu.VMEM((rows, width), bf16), pltpu.VMEM(small.shape, f32)]
        + pair_scratch(rows, width),
        48,
        ([True] * 4 + [False, True], [True] * 3 + [False] * 2),
    )


def build(n_f, n_c, n_t):
    def flip(x, axis, bit):
        size = {"fsdp": n_f, "context": n_c, "tensor": n_t}[axis]
        return lax.ppermute(x, axis, [(i, i ^ bit) for i in range(size)])

    def by_bit(bit, x, other, axis):
        return jnp.where(
            bit == 0,
            jnp.concatenate([x, other], axis=axis),
            jnp.concatenate([other, x], axis=axis),
        )

    def after(x, *others):
        return lax.optimization_barrier((x, others))[0]

    def local(
        inputs,
        cotangent,
        blocks,
        attn_gain,
        w_query,
        b_query,
        w_key,
        b_key,
        w_value,
        b_value,
        w_out,
        ffn_gain,
        w_gate,
        w_up,
        w_down,
    ):
        rows, width = inputs.shape
        f = lax.axis_index("fsdp")
        c = lax.axis_index("context")
        t = lax.axis_index("tensor")
        core, parity, pair = t % 2, c % 2, c // 2
        heads = w_query.shape[1] // HD
        group = (t * heads) // (H // KV)
        part = rows // n_t
        units_all = w_gate.shape[1]
        units = units_all // 2

        def gather_f(x, axis):
            if n_f == 2:
                return by_bit(f, x, flip(x, "fsdp", 1), axis)
            return lax.all_gather(x, "fsdp", axis=axis, tiled=True)

        def grad_far(left, right, side):
            if n_f > 2:
                return None
            source = (left, right)[side]
            half = width // 2
            far = lax.dynamic_slice_in_dim(source, (1 - f) * half, half, 1)
            return (dot_rows(far, right) if side == 0 else dot_rows(left, far)).astype(bf16)

        def grad_sum(left, right, side, far, late):
            if n_f > 2:
                return lax.psum_scatter(
                    dot_rows(left, right).astype(bf16), "fsdp", scatter_dimension=side, tiled=True
                )
            source = (left, right)[side]
            half = width // 2
            own = lax.dynamic_slice_in_dim(source, f * half, half, 1)
            own = dot_rows(own, right) if side == 0 else dot_rows(left, own)
            return (own + after(flip(far, "fsdp", 1), late).astype(f32)).astype(bf16)

        small = jnp.concatenate(
            [v.reshape(1, -1) for v in (attn_gain, ffn_gain, b_query, b_key, b_value)], axis=1
        )
        column = lambda w: lax.dynamic_slice_in_dim(w, group * HD, HD, 1)
        w_kv_own = jnp.where(core == 0, column(w_key), column(w_value))
        pieces_f = lambda x, axis: (
            [x, flip(x, "fsdp", 1)]
            if n_f == 2
            else [lax.all_gather(x, "fsdp", axis=axis, tiled=True)]
        )
        meta = jnp.stack([f, 1 - f, core, pair]).astype(jnp.int32)
        w_q = pieces_f(w_query, 0)
        w_kv = pieces_f(w_kv_own, 0)
        small = gather_f(small, 0)
        w_out_all = gather_f(after(w_out, small, w_q, w_kv), 1)
        piece = attn_gain.shape[0]
        gain_first = small[:, :piece].reshape(1, width).astype(f32)
        gain_second = small[:, piece : 2 * piece].reshape(1, width).astype(f32)
        bias_of = lambda lo, n: (
            small[:, lo : lo + n * (HD // n_f)]
            .reshape(n_f, n, HD // n_f)
            .transpose(1, 0, 2)
            .reshape(n, HD)
            .astype(f32)
        )
        at = 2 * piece
        bq = bias_of(at, heads)
        bk = bias_of(at + heads * (HD // n_f), KV)
        bv = bias_of(at + (heads + KV) * (HD // n_f), KV)
        b_kv = lax.dynamic_index_in_dim(jnp.where(core == 0, bk, bv), group, 0)

        unit_slice = lambda w: lax.dynamic_slice_in_dim(w, parity * units, units, 0)
        own_units = jnp.concatenate([unit_slice(w) for w in (w_gate.T, w_up.T, w_down)], axis=0)

        dy_part = lax.dynamic_slice_in_dim(cotangent, t * part, part, 0)

        seq_blocks = blocks[0].reshape(n_c, -1)
        own_blocks = seq_blocks.shape[1]
        key_blocks = jnp.concatenate(
            [lax.dynamic_index_in_dim(seq_blocks, c ^ j, 0, keepdims=False) for j in range(n_c)]
        )
        positions = (
            key_blocks[:own_blocks, None] * BLOCK + jnp.arange(BLOCK, dtype=jnp.int32)[None, :]
        ).reshape(-1)
        cosine, sine = rope_tables(positions)
        bias = jnp.concatenate([bq.reshape(1, -1), b_kv], axis=1)
        dy_blocks = [
            dy_part,
            flip(dy_part, "tensor", 2),
            flip(dy_part, "context", 1),
            flip(dy_part, "context", 2),
        ]
        bias = after(bias, dy_blocks)
        normed, factor_first, queries, kv_own = qkv(
            meta, inputs, gain_first, bias, cosine, sine, w_q, w_kv
        )
        w_units = pieces_f(after(own_units, kv_own, w_out_all), 1)
        kv = kv_gather(after(kv_own, w_out_all))
        attended, lse = attention(key_blocks, queries, kv)
        inputs_part = lax.dynamic_slice_in_dim(inputs, t * part, part, 0)
        middle, factor_second, normed2, dy_all = middle_norm(
            dot(attended, w_out_all).astype(bf16), inputs_part, gain_second, dy_blocks
        )

        hidden, grad_gate, grad_up, dx_part, out_part, *unit_far = ffn(
            meta, normed2, dy_all, w_units
        )
        flat = lambda x: x.reshape(-1, width)
        if n_f == 2:
            down_got, gate_got, up_got = (flip(x, "fsdp", 1) for x in unit_far)
            early = [(hidden, flat(dy_all)), (grad_gate, flat(normed2))]
            later = [(grad_up, flat(normed2))]
        else:
            over_f = lambda x: lax.psum_scatter(x, "fsdp", scatter_dimension=1, tiled=True)
            owns = [
                over_f(unit_grads(meta, 0, 1, x, [unit]))
                for x, unit in ((dy_all, hidden), (normed2, grad_gate), (normed2, grad_up))
            ]
            down_got = gate_got = up_got = jnp.zeros_like(owns[0])
            early = later = []

        def unit_done(own, got):
            low = (own.astype(f32) + got.astype(f32)).astype(bf16)
            return low, flip(low, "context", 1)

        unit_whole = lambda low, other: by_bit(parity, low, other, 0).astype(f32)

        grad_middle, ffn_gain_grad, grad_middle_low, *first_owns = middle_back(
            dx_part, middle, factor_second, gain_second, dy_part, early, width // n_f
        )
        grad_middle_low = grad_middle_low.reshape(rows, width)
        down_own, gate_own = first_owns or owns[:2]
        down_done = unit_done(down_own, after(down_got, grad_middle_low))
        grad_attended = dot_cols(after(grad_middle_low, down_done[0]), w_out_all).astype(bf16)

        dq_low, dkv = attention_back(key_blocks, queries, grad_attended, lse, cosine, sine, kv)
        attention_args = [(attended, after(grad_middle_low, dq_low), 1), (normed, dq_low, 0)]
        fars = [grad_far(*args) for args in attention_args]
        dkv, *last_owns = kv_scatter(
            after(dkv, gate_got, fars), later, width // n_f
        )
        (up_own,) = last_owns or owns[2:]
        gate_done = unit_done(gate_own, after(gate_got, dkv, down_done))
        dkv = after(dkv, gate_done[0])
        dkv_low = jnp.where(core == 0, rotate_back(dkv, cosine, sine), dkv).astype(bf16)
        attention_args.append((normed, dkv_low, 0))
        fars.append(grad_far(*attention_args[-1]))
        dkv_low = after(dkv_low, fars)
        factor_part = lax.dynamic_slice_in_dim(factor_first, t * part, part, 0)
        own_biases = jnp.sum(
            jnp.concatenate([dq_low, dkv_low], axis=1).astype(f32), axis=0, keepdims=True
        )
        slots = lax.dynamic_update_slice(
            jnp.zeros((n_t, (heads + 1) * HD), f32), own_biases, (t, 0)
        )
        small_grads = jnp.concatenate(
            [jnp.zeros((1, width), f32), ffn_gain_grad, slots.reshape(1, -1)], axis=1
        )
        grad_qkv = qkv_back(meta, dq_low, dkv_low, w_q, w_kv)
        up_done = unit_done(up_own, after(up_got, grad_qkv))
        small_grads, input_grad = input_back(
            after(grad_qkv, up_done[0]),
            inputs_part,
            factor_part,
            gain_first,
            grad_middle,
            small_grads,
        )
        input_grad = input_grad.reshape(rows, width)
        if n_f > 2:
            small_grads = lax.psum(small_grads, "fsdp")
        attention_parts = [
            grad_sum(*args, far, small_grads) for args, far in zip(attention_args, fars)
        ]
        wd_grad = unit_whole(*after(down_done, small_grads))
        wg_grad = unit_whole(*after(gate_done, small_grads))
        small_grads, up_done, wg_grad, wd_grad = lax.optimization_barrier(
            (small_grads, up_done, wg_grad, wd_grad)
        )
        wo_grad, wq_grad, packed, wkv_all, outputs = context_sum(
            n_f == 2, attention_parts, small_grads, out_part, middle
        )
        outputs = outputs.reshape(rows, width)
        wkv_all = wkv_all.astype(f32)
        wk_grad = jnp.concatenate([wkv_all[0], wkv_all[2]], axis=1)
        wv_grad = jnp.concatenate([wkv_all[1], wkv_all[3]], axis=1)
        packed = packed[0]
        attn_gain_grad = lax.dynamic_slice_in_dim(packed, f * piece, piece, 0)
        ffn_gain_grad = lax.dynamic_slice_in_dim(packed, width + f * piece, piece, 0)
        slots = packed[2 * width :].reshape(n_t, heads + 1, HD)
        slots = lax.dynamic_slice_in_dim(slots, f * (HD // n_f), HD // n_f, 2)
        bq_out = lax.dynamic_index_in_dim(slots, t, 0, keepdims=False)[:heads]
        bk_out = slots[0::2, heads]
        bv_out = slots[1::2, heads]

        wu_grad = unit_whole(*up_done)
        wg_grad, wu_grad = wg_grad.T, wu_grad.T

        return (
            outputs,
            input_grad,
            attn_gain_grad,
            wq_grad,
            bq_out,
            wk_grad,
            bk_out,
            wv_grad,
            bv_out,
            wo_grad,
            ffn_gain_grad,
            wg_grad,
            wu_grad,
            wd_grad,
        )

    return local


def solution(mesh):
    in_specs = (
        P(("fsdp", "context"), None),
        P(("fsdp", "context"), None),
        P("fsdp", None),
        P("fsdp"),
        P("fsdp", "tensor"),
        P("tensor", "fsdp"),
        P("fsdp", None),
        P(None, "fsdp"),
        P("fsdp", None),
        P(None, "fsdp"),
        P("tensor", "fsdp"),
        P("fsdp"),
        P("fsdp", "tensor"),
        P("fsdp", "tensor"),
        P("tensor", "fsdp"),
    )
    out_specs = (
        P(("fsdp", "context"), None),
        P(("fsdp", "context"), None),
        P("fsdp"),
        P("fsdp", "tensor"),
        P("tensor", "fsdp"),
        P("fsdp", None),
        P(None, "fsdp"),
        P("fsdp", None),
        P(None, "fsdp"),
        P("tensor", "fsdp"),
        P("fsdp"),
        P("fsdp", "tensor"),
        P("fsdp", "tensor"),
        P("tensor", "fsdp"),
    )
    local = build(mesh.shape["fsdp"], mesh.shape["context"], mesh.shape["tensor"])
    return jax.shard_map(local, mesh=mesh, in_specs=in_specs, out_specs=out_specs, check_vma=False)
```

```python
import functools

import jax
import jax.numpy as jnp
from jax import lax
from jax.experimental import pallas as pl
from jax.experimental.pallas import tpu as pltpu
from jax.sharding import PartitionSpec as P

H = 12
KV = 2
HD = 128
BLOCK = 256

EPSILON = 1e-06
ROPE_BASE = 1000000.0
MASKED = -1e30
SCALING = HD ** (-0.5)
LANES = 128
VMEM_LIMIT = 60 << 20

f32 = jnp.float32
bf16 = jnp.bfloat16


def rope_tables(positions):
    halfway = HD // 2
    frequency = ROPE_BASE ** (-(jnp.arange(halfway, dtype=f32) * 2.0 / HD))
    angles = positions.astype(f32)[:, None] * frequency[None, :]
    cosine, sine = jnp.cos(angles), jnp.sin(angles)
    return (jnp.concatenate([cosine, cosine], axis=1), jnp.concatenate([sine, sine], axis=1))


def rotate(field, cosine, sine):
    halfway = HD // 2
    turned = jnp.concatenate([-field[..., halfway:], field[..., :halfway]], axis=-1)
    return field * cosine + turned * sine


def rotate_back(grad_field, cosine, sine):
    halfway = HD // 2
    moved = grad_field * sine
    turned = jnp.concatenate([moved[..., halfway:], -moved[..., :halfway]], axis=-1)
    return grad_field * cosine + turned


def dot(left, right):
    return jnp.dot(left, right, preferred_element_type=f32)


def dot_rows(left, right):
    return lax.dot_general(left, right, (((0,), (0,)), ((), ())), preferred_element_type=f32)


def dot_cols(left, right):
    return lax.dot_general(left, right, (((1,), (1,)), ((), ())), preferred_element_type=f32)


def mask_row(kb_ref, own_block, key_blocks):
    return jnp.concatenate(
        [
            jnp.full((1, BLOCK), jnp.where(kb_ref[j] <= own_block, 0.0, MASKED), f32)
            for j in range(key_blocks)
        ],
        axis=1,
    )


def attention_kernel(key_blocks, kb_ref, q_ref, k_ref, v_ref, o_ref, lse_ref):
    bias = mask_row(kb_ref, kb_ref[pl.program_id(1)], key_blocks)
    scores = dot_cols(q_ref[...], k_ref[...]) * SCALING + bias
    row_max = jnp.max(scores, axis=1, keepdims=True)
    expo = jnp.exp(scores - row_max)
    total = jnp.sum(expo, axis=1, keepdims=True)
    probability = (expo * (1.0 / total)).astype(bf16)
    o_ref[...] = dot(probability, v_ref[...]).astype(bf16)
    lse_ref[0] = row_max + jnp.log(total)


def attention(key_blocks, queries, kv):
    rows, width = queries.shape
    heads = width // HD
    whole = lambda kind: pl.BlockSpec((None,) + kv.shape[1:], lambda h, i, kb: (kind, 0, 0))
    tile = pl.BlockSpec((BLOCK, HD), lambda h, i, kb: (i, h))
    return pl.pallas_call(
        functools.partial(attention_kernel, kv.shape[1] // BLOCK),
        name="attention",
        grid_spec=pltpu.PrefetchScalarGridSpec(
            num_scalar_prefetch=1,
            grid=(heads, rows // BLOCK),
            in_specs=[tile, whole(0), whole(1)],
            out_specs=[tile, pl.BlockSpec((1, BLOCK, 1), lambda h, i, kb: (h, i, 0))],
        ),
        out_shape=[
            jax.ShapeDtypeStruct((rows, width), bf16),
            jax.ShapeDtypeStruct((heads, rows, 1), f32),
        ],
        compiler_params=pltpu.CompilerParams(vmem_limit_bytes=VMEM_LIMIT),
    )(key_blocks, queries, kv, kv)


def attention_back_kernel(
    key_blocks,
    kb_ref,
    q_ref,
    do_ref,
    lse_ref,
    cos_ref,
    sin_ref,
    k_ref,
    v_ref,
    dq_ref,
    dkv_ref,
    dk_ref,
    dv_ref,
):
    head, i = pl.program_id(0), pl.program_id(1)

    @pl.when((head == 0) & (i == 0))
    def _():
        dk_ref[...] = jnp.zeros_like(dk_ref)
        dv_ref[...] = jnp.zeros_like(dv_ref)

    bias = mask_row(kb_ref, kb_ref[i], key_blocks)
    scores = dot_cols(q_ref[...], k_ref[...]) * SCALING + bias
    probability = jnp.exp(scores - lse_ref[0])
    grad_probs = dot_cols(do_ref[...], v_ref[...])
    inner = jnp.sum(probability * grad_probs, axis=1, keepdims=True)
    grad_scores = (probability * (grad_probs - inner)).astype(bf16)
    grad_query = dot(grad_scores, k_ref[...]) * SCALING
    moved = grad_query * sin_ref[...]
    sign = jnp.where(lax.broadcasted_iota(jnp.int32, moved.shape, 1) < HD // 2, 1.0, -1.0)
    dq_ref[...] = (
        grad_query * cos_ref[...] + pltpu.roll(moved, HD // 2, 1) * sign
    ).astype(bf16)
    dk_ref[...] += dot_rows(grad_scores, q_ref[...]) * SCALING
    dv_ref[...] += dot_rows(probability.astype(bf16), do_ref[...])

    @pl.when((head == pl.num_programs(0) - 1) & (i == pl.num_programs(1) - 1))
    def _():
        dkv_ref[0] = dk_ref[...].astype(bf16)
        dkv_ref[1] = dv_ref[...].astype(bf16)


def attention_back(key_blocks, queries, grad_out, lse, cosine, sine, kv):
    rows, width = queries.shape
    heads = width // HD
    whole = lambda kind: pl.BlockSpec((None,) + kv.shape[1:], lambda h, i, kb: (kind, 0, 0))
    tile = pl.BlockSpec((BLOCK, HD), lambda h, i, kb: (i, h))
    table = pl.BlockSpec((BLOCK, HD), lambda h, i, kb: (i, 0))
    return pl.pallas_call(
        functools.partial(attention_back_kernel, kv.shape[1] // BLOCK),
        name="attention_back",
        grid_spec=pltpu.PrefetchScalarGridSpec(
            num_scalar_prefetch=1,
            grid=(heads, rows // BLOCK),
            in_specs=[
                tile,
                tile,
                pl.BlockSpec((1, BLOCK, 1), lambda h, i, kb: (h, i, 0)),
                table,
                table,
                whole(0),
                whole(1),
            ],
            out_specs=[tile, pl.BlockSpec(kv.shape, lambda h, i, kb: (0, 0, 0))],
            scratch_shapes=[pltpu.VMEM(kv.shape[1:], f32)] * 2,
        ),
        out_shape=[
            jax.ShapeDtypeStruct((rows, width), bf16),
            jax.ShapeDtypeStruct(kv.shape, bf16),
        ],
        compiler_params=pltpu.CompilerParams(vmem_limit_bytes=VMEM_LIMIT),
    )(key_blocks, queries, grad_out, lse, cosine, sine, kv, kv)


def qkv_kernel(pieces, meta_ref, x_ref, gain_ref, bias_ref, cos_ref, sin_ref, *refs):
    weights, (xn_ref, factor_ref, q_ref, kv_ref) = refs[: 2 * pieces], refs[2 * pieces :]
    values = x_ref[...].astype(f32)
    factor = lax.rsqrt(jnp.mean(values * values, axis=-1, keepdims=True) + EPSILON)
    factor_ref[...] = factor
    xn_ref[...] = (values * factor * gain_ref[...]).astype(bf16)
    depth = weights[0].shape[0]
    normed = [xn_ref[:, columns_of(meta_ref, j, depth, pieces)] for j in range(pieces)]
    cosine, sine = cos_ref[...], sin_ref[...]
    sign = jnp.where(lax.broadcasted_iota(jnp.int32, cosine.shape, 1) < HD // 2, -1.0, 1.0)
    sine = sine * sign
    width = q_ref.shape[1]
    total = bias_ref[:, :width] + sum(dot(x, w[...]) for x, w in zip(normed, weights[:pieces]))
    turn = lambda own: own * cosine + pltpu.roll(own, HD // 2, 1) * sine
    for h in range(width // HD):
        q_ref[:, h * HD : (h + 1) * HD] = turn(total[:, h * HD : (h + 1) * HD]).astype(bf16)
    own = bias_ref[:, width:] + sum(dot(x, w[...]) for x, w in zip(normed, weights[pieces:]))
    kv_ref[...] = jnp.where(meta_ref[2] == 0, turn(own), own).astype(bf16)


def columns_of(meta_ref, j, depth, pieces):
    if pieces == 1:
        return slice(None)
    return pl.ds(pl.multiple_of(meta_ref[j] * depth, LANES), depth)


def qkv(meta, inputs, gain, bias, cosine, sine, w_q, w_kv):
    rows, width = inputs.shape
    out = w_q[0].shape[1]
    tile = 256
    row = lambda n: pl.BlockSpec((tile, n), lambda i, m: (i, 0))
    fixed = lambda w: pl.BlockSpec(w.shape, lambda i, m: (0, 0))
    return pl.pallas_call(
        functools.partial(qkv_kernel, len(w_q)),
        name="qkv",
        grid_spec=pltpu.PrefetchScalarGridSpec(
            num_scalar_prefetch=1,
            grid=(rows // tile,),
            in_specs=[row(width), fixed(gain), fixed(bias), row(HD), row(HD)]
            + [fixed(w) for w in (*w_q, *w_kv)],
            out_specs=[row(width), row(1), row(out), row(HD)],
        ),
        out_shape=[
            jax.ShapeDtypeStruct((rows, width), bf16),
            jax.ShapeDtypeStruct((rows, 1), f32),
            jax.ShapeDtypeStruct((rows, out), bf16),
            jax.ShapeDtypeStruct((rows, HD), bf16),
        ],
        compiler_params=pltpu.CompilerParams(vmem_limit_bytes=VMEM_LIMIT),
    )(meta, inputs, gain, bias, cosine, sine, *w_q, *w_kv)


def qkv_back_kernel(pieces, meta_ref, dq_ref, dkv_ref, *refs):
    w_q, w_kv, out_ref = refs[:pieces], refs[pieces : 2 * pieces], refs[-1]
    for j in range(pieces):
        out_ref[:, columns_of(meta_ref, j, w_q[j].shape[0], pieces)] = (
            dot_cols(dq_ref[...], w_q[j][...]) + dot_cols(dkv_ref[...], w_kv[j][...])
        ).astype(bf16)


def qkv_back(meta, grad_q, grad_kv, w_q, w_kv):
    rows, width = grad_q.shape[0], sum(w.shape[0] for w in w_q)
    tile = 256
    row = lambda n: pl.BlockSpec((tile, n), lambda i, m: (i, 0))
    fixed = lambda w: pl.BlockSpec(w.shape, lambda i, m: (0, 0))
    return pl.pallas_call(
        functools.partial(qkv_back_kernel, len(w_q)),
        name="qkv_back",
        grid_spec=pltpu.PrefetchScalarGridSpec(
            num_scalar_prefetch=1,
            grid=(rows // tile,),
            in_specs=[row(grad_q.shape[1]), row(HD)] + [fixed(w) for w in (*w_q, *w_kv)],
            out_specs=row(width),
        ),
        out_shape=jax.ShapeDtypeStruct((rows, width), bf16),
        compiler_params=pltpu.CompilerParams(vmem_limit_bytes=VMEM_LIMIT),
    )(meta, grad_q, grad_kv, *w_q, *w_kv)


def add_rows(unit_refs, row_refs, columns, totals, outs):
    step = pl.program_id(0)

    @pl.when(step == 0)
    def _():
        for total in totals:
            total[...] = jnp.zeros_like(total)

    for total, unit, row in zip(totals, unit_refs, row_refs):
        total[...] += dot_rows(unit[...], row[:, columns])

    @pl.when(step == pl.num_programs(0) - 1)
    def _():
        for out, total in zip(outs, totals):
            out[...] = total[...].astype(bf16)


def hidden_kernel(pieces, meta_ref, x_ref, dy_ref, *refs):
    wg, wu, refs = refs[:pieces], refs[pieces : 2 * pieces], refs[2 * pieces :]
    hid_ref, slope_ref, gated_ref = refs[:3]
    columns = [columns_of(meta_ref, j, wg[j].shape[1], pieces) for j in range(pieces)]
    gate = sum(dot_cols(x_ref[:, at], w[...]) for at, w in zip(columns, wg))
    up = sum(dot_cols(x_ref[:, at], w[...]) for at, w in zip(columns, wu))
    sigma = 1.0 / (1.0 + jnp.exp(-gate))
    gated = gate * sigma
    hid_ref[...] = (gated * up).astype(bf16)
    slope_ref[...] = (up * (sigma + gated * (1.0 - sigma))).astype(bf16)
    gated_ref[...] = gated.astype(bf16)
    if pieces == 2:
        add_rows([hid_ref], [dy_ref], columns[1], refs[4:], refs[3:4])


def hidden_back_kernel(pieces, meta_ref, x_ref, dy_ref, hid_ref, slope_ref, gated_ref, *refs):
    wg, wu, wd = (refs[m * pieces : (m + 1) * pieces] for m in range(3))
    refs = refs[3 * pieces :]
    dg_ref, du_ref, dx_ref, out_ref = refs[:4]
    columns = [columns_of(meta_ref, j, wg[j].shape[1], pieces) for j in range(pieces)]
    grad_hidden = sum(dot_cols(dy_ref[:, at], w[...]) for at, w in zip(columns, wd))
    dg_ref[...] = (grad_hidden * slope_ref[...].astype(f32)).astype(bf16)
    du_ref[...] = (grad_hidden * gated_ref[...].astype(f32)).astype(bf16)

    @pl.when(pl.program_id(0) // (pl.num_programs(0) // 2) == meta_ref[3])
    def _():
        for at, g, u, d in zip(columns, wg, wu, wd):
            dx_ref[:, at] = (dot(dg_ref[...], g[...]) + dot(du_ref[...], u[...])).astype(bf16)
            out_ref[:, at] = dot(hid_ref[...], d[...]).astype(bf16)

    if pieces == 2:
        add_rows([dg_ref, du_ref], [x_ref, x_ref], columns[1], refs[6:], refs[4:6])


def hidden_specs(meta, normed, weights):
    width = normed.shape[-1]
    rows = normed.shape[0] * normed.shape[1]
    units, depth = weights[0].shape[0] // 2, weights[0].shape[1]
    tile = 512
    steps = rows // tile
    half = steps // 2
    once = pl.Buffered(1)
    inside = lambda i, m: jnp.clip(i - m[3] * half, 0, half - 1)
    return {
        "steps": steps,
        "flat": lambda x: x.reshape(-1, width),
        "row": pl.BlockSpec((tile, width), lambda i, m: (lax.rem(i + m[3] * half, steps), 0)),
        "unit": pl.BlockSpec((tile, units), lambda i, m: (i, 0)),
        "near_unit": pl.BlockSpec((tile, units), lambda i, m: (inside(i, m) + m[3] * half, 0)),
        "near_row": pl.BlockSpec((tile, width), lambda i, m: (inside(i, m), 0)),
        "weight": lambda k: pl.BlockSpec((units, depth), lambda i, m: (k, 0), pipeline_mode=once),
        "grad": pl.BlockSpec((units, depth), lambda i, m: (0, 0), pipeline_mode=once),
        "unit_shape": jax.ShapeDtypeStruct((rows, units), bf16),
        "near_shape": jax.ShapeDtypeStruct((rows // 2, width), bf16),
        "grad_shape": jax.ShapeDtypeStruct((units, depth), bf16),
        "total": pltpu.VMEM((units, depth), f32),
    }


def hidden_call(kernel, name, meta, args, in_specs, outs, grads, specs):
    return pl.pallas_call(
        kernel,
        name=name,
        grid_spec=pltpu.PrefetchScalarGridSpec(
            num_scalar_prefetch=1,
            grid=(specs["steps"],),
            in_specs=in_specs,
            out_specs=[specs[x] for x in outs] + [specs["grad"]] * grads,
            scratch_shapes=[specs["total"]] * grads,
        ),
        out_shape=[specs[x.split("_")[0] + "_shape"] for x in outs]
        + [specs["grad_shape"]] * grads,
        compiler_params=pltpu.CompilerParams(vmem_limit_bytes=VMEM_LIMIT),
    )(meta, *args)


def hidden_units(meta, normed, grad_out, weights):
    specs, pieces = hidden_specs(meta, normed, weights), len(weights)
    return hidden_call(
        functools.partial(hidden_kernel, pieces),
        "hidden_units",
        meta,
        [specs["flat"](normed), specs["flat"](grad_out)] + list(weights) * 2,
        [specs["row"]] * 2 + [specs["weight"](k) for k in range(2) for _ in weights],
        ["unit"] * 3,
        pieces == 2,
        specs,
    )


def hidden_back(meta, normed, grad_out, hidden, slope, gated, weights, down_weights):
    specs, pieces = hidden_specs(meta, normed, weights), len(weights)
    return hidden_call(
        functools.partial(hidden_back_kernel, pieces),
        "hidden_back",
        meta,
        [specs["flat"](normed), specs["flat"](grad_out), hidden, slope, gated]
        + list(weights) * 2
        + list(down_weights),
        [specs["row"]] * 2
        + [specs["near_unit"], specs["unit"], specs["unit"]]
        + [specs["weight"](k) for k in (0, 1, 0) for _ in weights],
        ["unit", "unit", "near_row", "near_row"],
        2 * (pieces == 2),
        specs,
    )


def unit_grads_kernel(count, meta_ref, near_ref, far_ref, *refs):
    units, out_ref, x_ref = refs[:count], refs[-2], refs[-1]
    half = near_ref.shape[0]
    x_ref[pl.ds(pl.multiple_of(meta_ref[3] * half, half), half)] = near_ref[...]
    x_ref[pl.ds(pl.multiple_of((1 - meta_ref[3]) * half, half), half)] = far_ref[...]
    for k, unit in enumerate(units):
        depth = unit.shape[1]
        out_ref[k * depth : (k + 1) * depth] = dot_rows(unit[...], x_ref[...]).astype(bf16)


def unit_grads(meta, which, pieces, x, units_of):
    width = x.shape[-1]
    count, (rows, units) = len(units_of), units_of[0].shape
    depth = width // pieces
    tile = 256
    steps = depth // tile
    shard = (lambda m: m[which]) if pieces > 1 else (lambda m: 0)
    feature = lambda half: pl.BlockSpec(
        (rows // 2, tile), lambda i, m: (half, shard(m) * steps + i)
    )
    unit = pl.BlockSpec((rows, units), lambda i, m: (0, 0), pipeline_mode=pl.Buffered(1))
    x = x.reshape(-1, width)
    return pl.pallas_call(
        functools.partial(unit_grads_kernel, count),
        name=f"unit_grads_{which}_{count}",
        grid_spec=pltpu.PrefetchScalarGridSpec(
            num_scalar_prefetch=1,
            grid=(steps,),
            in_specs=[feature(0), feature(1)] + [unit] * count,
            out_specs=pl.BlockSpec((count * units, tile), lambda i, m: (0, i)),
            scratch_shapes=[pltpu.VMEM((rows, tile), bf16)],
        ),
        out_shape=jax.ShapeDtypeStruct((count * units, depth), bf16),
        compiler_params=pltpu.CompilerParams(vmem_limit_bytes=VMEM_LIMIT),
    )(meta, x, x, *units_of)


class Wires:
    def __init__(self, sends, receives, locals_):
        self.sends, self.receives, self.locals = sends, receives, locals_
        self.used = self.used_local = 0
        self.started = []

    def plan(self, source, target, device):
        k = self.used
        self.used += 1
        return pltpu.make_async_remote_copy(
            source,
            target,
            self.sends.at[k],
            self.receives.at[k],
            device_id=device,
            device_id_type=pl.DeviceIdType.MESH,
        )

    def copy(self, source, target, device):
        one = self.plan(source, target, device)
        one.start()
        self.started.append(one)
        return one

    def here(self, source, target):
        k = self.used_local
        self.used_local += 1
        one = pltpu.make_async_copy(source, target, self.locals.at[k])
        one.start()
        return one

    def finish(self):
        for one in self.started:
            one.wait_send()


class OwnGrad:
    TILE = 256

    def __init__(self, units, rows, out, units_here, rows_here):
        self.units, self.rows, self.out = units, rows, out
        self.units_here, self.rows_here = units_here, rows_here
        self.tiles = out.shape[1] // self.TILE
        self.copies = None

    def fetch(self, wires):
        half, depth = self.rows.shape[0] // 2, self.out.shape[1]
        column = pl.multiple_of(lax.axis_index("fsdp") * depth, LANES)
        pair = lax.axis_index("context") // 2
        self.copies = [wires.here(self.units, self.units_here)]
        for k, place in ((0, pair), (1, 1 - pair)):
            self.copies.append(
                wires.here(
                    self.rows.at[pl.ds(k * half, half), pl.ds(column, depth)],
                    self.rows_here.at[pl.ds(pl.multiple_of(place * half, half), half)],
                )
            )

    def make(self, first, past):
        for one in self.copies:
            one.wait()
        self.copies = []

        @pl.loop(first, past)
        def _(k):
            at = pl.ds(pl.multiple_of(k * self.TILE, self.TILE), self.TILE)
            self.out[:, at] = dot_rows(self.units_here[...], self.rows_here[:, at]).astype(bf16)


def own_grad_call(fill, width):
    args = [x for pair in fill for x in pair]
    outs = [jax.ShapeDtypeStruct((units.shape[1], width), bf16) for units, _ in fill]
    scratch = []
    for units, rows in fill:
        scratch += [pltpu.VMEM(units.shape, bf16), pltpu.VMEM((rows.shape[0], width), bf16)]
    return args, outs, scratch


def own_grads(count, args, outs, scratch):
    return [
        OwnGrad(args[2 * k], args[2 * k + 1], outs[k], scratch[2 * k], scratch[2 * k + 1])
        for k in range(count)
    ]


def meet(devices):
    barrier = pltpu.get_barrier_semaphore()
    for device in devices:
        pl.semaphore_signal(barrier, inc=1, device_id=device, device_id_type=pl.DeviceIdType.MESH)
    pl.semaphore_wait(barrier, len(devices))


def partners():
    c, t = lax.axis_index("context"), lax.axis_index("tensor")
    flip = lambda x, bit: x + bit * (1 - 2 * lax.rem(x // bit, 2))
    return {
        "core": {"tensor": flip(t, 1)},
        "y": {"tensor": flip(t, 2)},
        "z": {"context": flip(c, 1)},
        "far": {"context": flip(c, 2)},
        "last": {"context": flip(flip(c, 1), 2)},
    }


def wide(x):
    return x.astype(f32)


def ranks():
    t = lax.axis_index("tensor")
    flip = lambda x, bit: x + bit * (1 - 2 * lax.rem(x // bit, 2))
    return (t, flip(t, 1), flip(t, 2), flip(flip(t, 1), 2))


def scatter_rank(wires, to, part, own, got_core, sent, got_y):
    size = part.shape[1] // 2
    halves = [pl.ds(0, size), pl.ds(size, size)]
    rank = ranks()
    from_core = {}
    for block in (1, 0):
        for k, at in enumerate(halves):
            from_core[block, k] = wires.copy(
                part.at[rank[1 + 2 * block], at], got_core.at[block, at], to["core"]
            )
    mine = [wires.here(part.at[rank[2 * block]], own.at[block]) for block in (0, 1)]
    yield
    for one in mine:
        one.wait()
    from_y = []
    for k, at in enumerate(halves):
        from_core[1, k].wait_recv()
        sent[at] = (wide(own[1, at]) + wide(got_core[1, at])).astype(bf16)
        from_y.append(wires.copy(sent.at[at], got_y.at[at], to["y"]))
    yield
    for k in range(2):
        from_core[0, k].wait_recv()
    total = wide(own[0]) + wide(got_core[0])
    for one in from_y:
        one.wait_recv()
    return total + wide(got_y[...])


def scatter_pair(wires, to, part, own, got_core, sent, got_y, got_z, diag_y, diag_z):
    size = part.shape[1] // 2
    low, high = pl.ds(0, size), pl.ds(size, size)
    from_core = {j: wires.copy(part.at[4 + j], got_core.at[j], to["core"]) for j in (3, 1, 2, 0)}
    mine = wires.here(part.at[pl.ds(0, 4)], own)
    yield
    mine.wait()
    both = lambda j, at: wide(own[j, at]) + wide(got_core[j, at])
    from_core[3].wait_recv()
    sent[2] = (wide(own[3]) + wide(got_core[3])).astype(bf16)
    via_z = wires.copy(sent.at[2, low], diag_z, to["z"])
    via_y = wires.copy(sent.at[2, high], diag_y, to["y"])
    from_core[1].wait_recv()
    sent[0, high] = both(1, high).astype(bf16)
    y_high = wires.copy(sent.at[0, high], got_y.at[high], to["y"])
    from_core[2].wait_recv()
    sent[1, low] = both(2, low).astype(bf16)
    z_low = wires.copy(sent.at[1, low], got_z.at[low], to["z"])
    yield
    via_z.wait_recv()
    sent[0, low] = (both(1, low) + wide(diag_z[...])).astype(bf16)
    y_low = wires.copy(sent.at[0, low], got_y.at[low], to["y"])
    via_y.wait_recv()
    sent[1, high] = (both(2, high) + wide(diag_y[...])).astype(bf16)
    z_high = wires.copy(sent.at[1, high], got_z.at[high], to["z"])
    yield
    from_core[0].wait_recv()
    total = wide(own[0]) + wide(got_core[0])
    for one in (y_high, z_low, y_low, z_high):
        one.wait_recv()
    return total + wide(got_y[...]) + wide(got_z[...])


def result_of(steps):
    while True:
        try:
            next(steps)
        except StopIteration as done:
            return done.value


def gather_rank(wires, to, block, out):
    size = block.shape[0] // 2
    halves = [pl.ds(0, size), pl.ds(size, size)]
    rank = ranks()
    mine = wires.here(block, out.at[rank[0]])
    from_y = [wires.copy(block.at[h], out.at[rank[0], h], to["y"]) for h in halves]
    from_core = [wires.copy(block, out.at[rank[0]], to["core"])]
    yield
    for h, one in zip(halves, from_y):
        one.wait_recv()
        from_core.append(wires.copy(out.at[rank[2], h], out.at[rank[2], h], to["core"]))
    for one in from_core:
        one.wait_recv()
    mine.wait()


def gather_pair(wires, to, block, out, base):
    size = block.shape[0] // 2
    low, high = pl.ds(0, size), pl.ds(size, size)
    at = lambda j: out.at[base + j]
    from_z = wires.copy(block, at(2), to["z"])
    yield
    from_y = wires.copy(block, at(1), to["y"])
    from_core = [wires.copy(block, at(4), to["core"])]
    yield
    from_y.wait_recv()
    via_z = wires.copy(out.at[base + 1, low], out.at[base + 3, low], to["z"])
    from_core.append(wires.copy(at(1), at(5), to["core"]))
    from_z.wait_recv()
    via_y = wires.copy(out.at[base + 2, high], out.at[base + 3, high], to["y"])
    from_core.append(wires.copy(at(2), at(6), to["core"]))
    yield
    via_z.wait_recv()
    via_y.wait_recv()
    from_core.append(wires.copy(at(3), at(7), to["core"]))
    return from_core


def remote_call(kernel, name, key, args, outs, scratch, copies, in_vmem):
    ins, out_in = in_vmem
    spec = lambda inside: pl.BlockSpec(memory_space=pltpu.VMEM if inside else pl.ANY)
    return pl.pallas_call(
        kernel,
        name=name,
        out_shape=outs,
        in_specs=[spec(x) for x in ins],
        out_specs=[spec(x) for x in out_in],
        scratch_shapes=list(scratch)
        + [
            pltpu.SemaphoreType.DMA((copies,)),
            pltpu.SemaphoreType.DMA((copies,)),
            pltpu.SemaphoreType.DMA((8,)),
        ],
        compiler_params=pltpu.CompilerParams(
            collective_id=key, has_side_effects=True, vmem_limit_bytes=VMEM_LIMIT
        ),
    )(*args)


def kv_gather_kernel(own_ref, out_ref, *sems):
    wires, to = Wires(*sems), partners()
    kind = lax.rem(lax.axis_index("tensor"), 2)
    rows = own_ref.shape[0]
    block = lambda j: out_ref.at[kind, pl.ds(j * rows, rows)]
    meet([to[k] for k in ("core", "z", "far", "last")])
    mine = wires.here(own_ref, block(0))
    arrive = [wires.copy(own_ref, block(j), to[k]) for j, k in ((3, "last"), (2, "far"), (1, "z"))]
    from_core = [wires.copy(own_ref, block(0), to["core"])]
    for j, one in ((1, arrive[2]), (2, arrive[1]), (3, arrive[0])):
        one.wait_recv()
        from_core.append(wires.copy(block(j), block(j), to["core"]))
    for one in from_core:
        one.wait_recv()
    mine.wait()
    wires.finish()


def kv_gather(own):
    rows, width = own.shape
    n_c = lax.axis_size("context")
    return remote_call(
        kv_gather_kernel,
        "kv_gather",
        0,
        [own],
        [jax.ShapeDtypeStruct((2, n_c * rows, width), bf16)],
        [],
        8,
        ([False], [False]),
    )[0]


def kv_scatter_kernel(count, part_ref, *refs):
    args, dkv_ref, outs = refs[: 2 * count], refs[2 * count], refs[2 * count + 1 : 3 * count + 1]
    own, got_core, sent, got = refs[3 * count + 1 : 3 * count + 5]
    wires, to = Wires(*refs[-3:]), partners()
    fill = own_grads(count, args, outs, refs[3 * count + 5 : -3])
    kind = lax.rem(lax.axis_index("tensor"), 2)
    rows = dkv_ref.shape[0]
    block = lambda j: pl.ds(j * rows, rows)
    meet([to[k] for k in ("core", "z", "far", "last")])
    steps = ((3, "last"), (2, "far"), (1, "z"), (0, None))
    from_core = {
        j: wires.copy(part_ref.at[1 - kind, block(j)], got_core.at[block(j)], to["core"])
        for j, _ in steps
    }
    mine = wires.here(part_ref.at[kind], own)
    for one in fill:
        one.fetch(wires)
    mine.wait()
    arrive = []
    for j, k in steps[:3]:
        from_core[j].wait_recv()
        sent[block(j)] = (wide(own[block(j)]) + wide(got_core[block(j)])).astype(bf16)
        arrive.append(wires.copy(sent.at[block(j)], got.at[block(j)], to[k]))
    for one in fill:
        one.make(0, one.tiles)
    from_core[0].wait_recv()
    total = wide(own[block(0)]) + wide(got_core[block(0)])
    for one in arrive:
        one.wait_recv()
    for j in (1, 2, 3):
        total = total + wide(got[block(j)])
    dkv_ref[...] = total
    wires.finish()


def kv_scatter(part, fill, width):
    _, rows, depth = part.shape
    n_c = lax.axis_size("context")
    args, outs, scratch = own_grad_call(fill, width)
    return remote_call(
        functools.partial(kv_scatter_kernel, len(fill)),
        "kv_scatter",
        1,
        [part, *args],
        [jax.ShapeDtypeStruct((rows // n_c, depth), f32), *outs],
        [pltpu.VMEM((rows, depth), bf16)] * 4 + scratch,
        7,
        ([False] * (1 + len(args)), [True] * (1 + len(outs))),
    )


def middle_kernel(
    part,
    x_ref,
    gain_ref,
    dy_ref,
    dy_y,
    dy_z,
    dy_far,
    mid_ref,
    factor_ref,
    out,
    dys,
    own,
    core,
    sent,
    got,
    xn,
    *sems,
):
    wires, to = Wires(*sems), partners()
    blocks = out.shape[0] // 2
    size = xn.shape[0] // 2
    low, high = pl.ds(0, size), pl.ds(size, size)
    meet([to[k] for k in ("core", "y", "z", "far")])
    summed = scatter_rank(wires, to, part, own, core, sent, got)
    next(summed)
    mine = [
        wires.here(block, dys.at[k])
        for block, k in ((dy_ref, 0), (dy_y, 1), (dy_z, 2), (dy_far, blocks))
    ]
    via_z = wires.copy(dy_y.at[low], dys.at[3, low], to["z"])
    dy_last = gather_pair(wires, to, dy_far, dys, blocks)
    next(dy_last)
    next(summed)
    via_y = wires.copy(dy_z.at[high], dys.at[3, high], to["y"])
    ends = [
        wires.copy(block, dys.at[4 + k], to["core"])
        for k, block in enumerate((dy_ref, dy_y, dy_z))
    ]
    next(dy_last)
    middle = wide(x_ref[...]) + result_of(summed)
    mid_ref[...] = middle
    factor = lax.rsqrt(jnp.mean(middle * middle, axis=-1, keepdims=True) + EPSILON)
    factor_ref[...] = factor
    xn[...] = (middle * factor * gain_ref[...]).astype(bf16)
    mine.append(wires.here(xn, out.at[0]))
    xn_far = wires.copy(xn, out.at[blocks], to["far"])
    xn_near = gather_pair(wires, to, xn, out, 0)
    next(xn_near)
    next(xn_near)
    via_z.wait_recv()
    via_y.wait_recv()
    ends.append(wires.copy(dys.at[3], dys.at[7], to["core"]))
    next(dy_last)
    next(xn_near)
    xn_far.wait_recv()
    xn_last = gather_pair(wires, to, out.at[blocks], out, blocks)
    next(xn_last)
    next(xn_last)
    ends += result_of(dy_last) + result_of(xn_near)
    next(xn_last)
    ends += result_of(xn_last)
    for one in ends:
        one.wait_recv()
    for one in mine:
        one.wait()
    wires.finish()


def middle_norm(part, inputs_part, gain, dy_blocks):
    rows, width = inputs_part.shape
    return remote_call(
        middle_kernel,
        "middle_norm",
        2,
        [part.reshape(4, rows, width), inputs_part, gain, *dy_blocks],
        [
            jax.ShapeDtypeStruct((rows, width), f32),
            jax.ShapeDtypeStruct((rows, 1), f32),
            jax.ShapeDtypeStruct((16, rows, width), bf16),
            jax.ShapeDtypeStruct((16, rows, width), bf16),
        ],
        [
            pltpu.VMEM((2, rows, width), bf16),
            pltpu.VMEM((2, rows, width), bf16),
            pltpu.VMEM((rows, width), bf16),
            pltpu.VMEM((rows, width), bf16),
            pltpu.VMEM((rows, width), bf16),
        ],
        48,
        ([False] + [True] * 6, [True, True, False, False]),
    )


def norm_back_rows(values, factor, gain, grad_normed):
    gained = gain * grad_normed
    inner = jnp.mean(gained * values, axis=-1, keepdims=True)
    grad_values = factor * gained - values * (factor * factor * factor) * inner
    return grad_values, jnp.sum(grad_normed * values * factor, axis=0, keepdims=True)


def middle_back_kernel(count, part, mid_ref, factor_ref, gain_ref, dy_ref, *refs):
    args, (dmid_ref, dgain_ref, out) = refs[: 2 * count], refs[2 * count : 2 * count + 3]
    outs, refs = refs[2 * count + 3 : 3 * count + 3], refs[3 * count + 3 :]
    low, first, wires, to = refs[0], refs[1:8], Wires(*refs[-3:]), partners()
    fill = own_grads(count, args, outs, refs[8:-3])
    meet([to[k] for k in ("core", "y", "z")])
    back = scatter_pair(wires, to, part, *first)
    next(back)
    for one in fill:
        one.fetch(wires)
    next(back)
    if fill:
        fill[0].make(0, 1)
    next(back)
    if fill:
        fill[0].make(1, fill[0].tiles)
    grad_normed = result_of(back)
    du, dgain = norm_back_rows(mid_ref[...], factor_ref[...], gain_ref[...], grad_normed)
    dgain_ref[...] = dgain
    dmid = wide(dy_ref[...]) + du
    low[...] = dmid.astype(bf16)
    share = gather_rank(wires, to, low, out)
    next(share)
    dmid_ref[...] = dmid
    for one in fill[1:]:
        one.make(0, one.tiles)
    result_of(share)
    wires.finish()


def pair_scratch(rows, width):
    return [
        pltpu.VMEM((4, rows, width), bf16),
        pltpu.VMEM((4, rows, width), bf16),
        pltpu.VMEM((3, rows, width), bf16),
        pltpu.VMEM((rows, width), bf16),
        pltpu.VMEM((rows, width), bf16),
        pltpu.VMEM((rows // 2, width), bf16),
        pltpu.VMEM((rows // 2, width), bf16),
    ]


def middle_back(part, middle, factor, gain, dy_part, fill, shard):
    rows, width = middle.shape
    args, outs, scratch = own_grad_call(fill, shard)
    return remote_call(
        functools.partial(middle_back_kernel, len(fill)),
        "middle_back",
        3,
        [part.reshape(8, rows, width), middle, factor, gain, dy_part, *args],
        [
            jax.ShapeDtypeStruct((rows, width), f32),
            jax.ShapeDtypeStruct((1, width), f32),
            jax.ShapeDtypeStruct((4, rows, width), bf16),
            *outs,
        ],
        [pltpu.VMEM((rows, width), bf16)] + pair_scratch(rows, width) + scratch,
        16,
        (
            [False, True, True, True, True] + [False] * len(args),
            [True, True, False] + [True] * len(outs),
        ),
    )


def add_all(wires, ways, value, slots):
    for k, device in enumerate(ways):
        one = wires.copy(value, slots.at[k], device)
        one.wait()
        wires.started = [x for x in wires.started if x is not one]
        value[...] = value[...] + slots[k]


def input_back_kernel(
    part, x_ref, factor_ref, gain_ref, dmid_ref, small_ref, sum_ref, out, *rest
):
    low, own, core, sent, got, slots = rest[:-3]
    wires, to = Wires(*rest[-3:]), partners()
    meet([to[k] for k in ("core", "y")])
    grad_normed = result_of(scatter_rank(wires, to, part, own, core, sent, got))
    du, dgain = norm_back_rows(wide(x_ref[...]), factor_ref[...], gain_ref[...], grad_normed)
    low[...] = (dmid_ref[...] + du).astype(bf16)
    share = gather_rank(wires, to, low, out)
    next(share)
    width = dgain.shape[1]
    sum_ref[:, width:] = small_ref[:, width:]
    sum_ref[:, :width] = dgain
    add_all(wires, [to["core"], to["y"]], sum_ref, slots)
    result_of(share)
    wires.finish()


def input_back(part, inputs_part, factor, gain, grad_middle, small):
    rows, width = inputs_part.shape
    return remote_call(
        input_back_kernel,
        "input_back",
        5,
        [part.reshape(4, rows, width), inputs_part, factor, gain, grad_middle, small],
        [
            jax.ShapeDtypeStruct(small.shape, f32),
            jax.ShapeDtypeStruct((4, rows, width), bf16),
        ],
        [
            pltpu.VMEM((rows, width), bf16),
            pltpu.VMEM((2, rows, width), bf16),
            pltpu.VMEM((2, rows, width), bf16),
            pltpu.VMEM((rows, width), bf16),
            pltpu.VMEM((rows, width), bf16),
            pltpu.VMEM((2,) + small.shape, f32),
        ],
        16,
        ([False, True, True, True, True, True], [True, False]),
    )


def context_sum_kernel(over_f, *refs):
    parts, small_ref, out_part, mid_ref = refs[:3], refs[3], refs[4], refs[5]
    outs, sum_ref, shared, outputs = refs[6:8], refs[8], refs[9], refs[10]
    lows, from_end, from_middle = refs[11:15], refs[15:19], refs[19:23]
    out_low, slot, scratch = refs[23], refs[24], refs[25:32]
    wires, to, c = Wires(*refs[32:]), partners(), lax.axis_index("context")
    end = (c == 0) | (c == lax.axis_size("context") - 1)
    inner = jnp.logical_not(end)
    greet = ["core", "y", "z", "last"]
    if over_f:
        to["f"] = {"fsdp": 1 - lax.axis_index("fsdp")}
        greet.append("f")
    meet([to[k] for k in greet])
    ahead = scatter_pair(wires, to, out_part, *scratch)
    next(ahead)
    sum_ref[...] = small_ref[...]
    from_f = wires.copy(small_ref, slot, to["f"]) if over_f else None
    next(ahead)
    sources = [*parts, sum_ref]
    chunks = []
    for i, cuts in ((2, 1), (0, 2), (1, 2), (3, 1)):
        size = sources[i].shape[0] // cuts
        chunks += [(i, pl.ds(k * size, size)) for k in range(cuts)]
    inward = [wires.plan(sources[i].at[at], from_end[i].at[at], to["z"]) for i, at in chunks]
    across = [wires.plan(lows[i].at[at], from_middle[i].at[at], to["last"]) for i, at in chunks]
    outward = [wires.plan(lows[i].at[at], lows[i].at[at], to["z"]) for i, at in chunks]
    small = len(chunks) - 1

    def send_in(k):
        @pl.when(end)
        def _():
            inward[k].start()

    def pass_on(first, past):
        @pl.when(inner)
        def _():
            for k in range(first, past):
                i, at = chunks[k]
                inward[k].wait_recv()
                total = wide(sources[i][at]) + wide(from_end[i][at])
                lows[i][at] = total.astype(lows[i].dtype)
                across[k].start()
                if k:
                    send_out(k - 1)

    def send_out(k):
        i, at = chunks[k]
        across[k].wait()
        lows[i][at] = (wide(lows[i][at]) + wide(from_middle[i][at])).astype(lows[i].dtype)
        outward[k].start()

    send_in(0)
    send_in(1)
    next(ahead)
    if over_f:
        from_f.wait_recv()
        sum_ref[...] = sum_ref[...] + slot[...]
    for k in range(2, small + 1):
        send_in(k)
    pass_on(0, 2)
    out_low[...] = (mid_ref[...] + result_of(ahead)).astype(bf16)
    out_share = gather_rank(wires, to, out_low, outputs)
    next(out_share)
    pass_on(2, small + 1)

    @pl.when(inner)
    def _():
        send_out(small)

    result_of(out_share)

    def arrived(k):
        @pl.when(end)
        def _():
            outward[k].wait_recv()

    arrived(0)
    share = gather_rank(wires, to, lows[2], shared)
    next(share)
    for k in range(1, len(chunks)):
        arrived(k)

    @pl.when(end)
    def _():
        for one in inward:
            one.wait_send()

    for i in (0, 1):
        outs[i][...] = wide(lows[i][...])
    sum_ref[...] = lows[3][...]
    result_of(share)

    @pl.when(inner)
    def _():
        for one in outward:
            one.wait_send()

    wires.finish()


def context_sum(over_f, parts, small, out_part, middle):
    rows, width = middle.shape
    lines = [pltpu.VMEM(x.shape, x.dtype) for x in (*parts, small)]
    return remote_call(
        functools.partial(context_sum_kernel, over_f),
        "context_sum",
        6,
        [*parts, small, out_part.reshape(8, rows, width), middle],
        [jax.ShapeDtypeStruct(x.shape, f32) for x in parts[:2]]
        + [jax.ShapeDtypeStruct(small.shape, f32)]
        + [jax.ShapeDtypeStruct((4,) + parts[2].shape, bf16)]
        + [jax.ShapeDtypeStruct((4, rows, width), bf16)],
        lines * 3
        + [pltpu.VMEM((rows, width), bf16), pltpu.VMEM(small.shape, f32)]
        + pair_scratch(rows, width),
        48,
        ([True] * 4 + [False, True], [True] * 3 + [False] * 2),
    )


def build(n_f, n_c, n_t):
    def flip(x, axis, bit):
        size = {"fsdp": n_f, "context": n_c, "tensor": n_t}[axis]
        return lax.ppermute(x, axis, [(i, i ^ bit) for i in range(size)])

    def by_bit(bit, x, other, axis):
        return jnp.where(
            bit == 0,
            jnp.concatenate([x, other], axis=axis),
            jnp.concatenate([other, x], axis=axis),
        )

    def after(x, *others):
        return lax.optimization_barrier((x, others))[0]

    def local(
        inputs,
        cotangent,
        blocks,
        attn_gain,
        w_query,
        b_query,
        w_key,
        b_key,
        w_value,
        b_value,
        w_out,
        ffn_gain,
        w_gate,
        w_up,
        w_down,
    ):
        rows, width = inputs.shape
        f = lax.axis_index("fsdp")
        c = lax.axis_index("context")
        t = lax.axis_index("tensor")
        core, parity, pair = t % 2, c % 2, c // 2
        heads = w_query.shape[1] // HD
        group = (t * heads) // (H // KV)
        part = rows // n_t
        units_all = w_gate.shape[1]
        units = units_all // 2

        def gather_f(x, axis):
            if n_f == 2:
                return by_bit(f, x, flip(x, "fsdp", 1), axis)
            return lax.all_gather(x, "fsdp", axis=axis, tiled=True)

        def grad_far(left, right, side):
            if n_f > 2:
                return None
            source = (left, right)[side]
            half = width // 2
            far = lax.dynamic_slice_in_dim(source, (1 - f) * half, half, 1)
            return (dot_rows(far, right) if side == 0 else dot_rows(left, far)).astype(bf16)

        def grad_sum(left, right, side, far, late):
            if n_f > 2:
                return lax.psum_scatter(
                    dot_rows(left, right).astype(bf16), "fsdp", scatter_dimension=side, tiled=True
                )
            source = (left, right)[side]
            half = width // 2
            own = lax.dynamic_slice_in_dim(source, f * half, half, 1)
            own = dot_rows(own, right) if side == 0 else dot_rows(left, own)
            return (own + after(flip(far, "fsdp", 1), late).astype(f32)).astype(bf16)

        small = jnp.concatenate(
            [v.reshape(1, -1) for v in (attn_gain, ffn_gain, b_query, b_key, b_value)], axis=1
        )
        column = lambda w: lax.dynamic_slice_in_dim(w, group * HD, HD, 1)
        w_kv_own = jnp.where(core == 0, column(w_key), column(w_value))
        pieces_f = lambda x, axis: (
            [x, flip(x, "fsdp", 1)]
            if n_f == 2
            else [lax.all_gather(x, "fsdp", axis=axis, tiled=True)]
        )
        meta = jnp.stack([f, 1 - f, core, pair]).astype(jnp.int32)
        w_q = pieces_f(w_query, 0)
        w_kv = pieces_f(w_kv_own, 0)
        small = gather_f(small, 0)
        w_out_all = gather_f(after(w_out, small, w_q, w_kv), 1)
        piece = attn_gain.shape[0]
        gain_first = small[:, :piece].reshape(1, width).astype(f32)
        gain_second = small[:, piece : 2 * piece].reshape(1, width).astype(f32)
        bias_of = lambda lo, n: (
            small[:, lo : lo + n * (HD // n_f)]
            .reshape(n_f, n, HD // n_f)
            .transpose(1, 0, 2)
            .reshape(n, HD)
            .astype(f32)
        )
        at = 2 * piece
        bq = bias_of(at, heads)
        bk = bias_of(at + heads * (HD // n_f), KV)
        bv = bias_of(at + (heads + KV) * (HD // n_f), KV)
        b_kv = lax.dynamic_index_in_dim(jnp.where(core == 0, bk, bv), group, 0)

        unit_slice = lambda w: lax.dynamic_slice_in_dim(w, parity * units, units, 0)
        own_gate_up = jnp.concatenate(
            [unit_slice(after(w, w_kv_own)) for w in (w_gate.T, w_up.T)], axis=0
        )
        own_down = unit_slice(w_down)

        dy_part = lax.dynamic_slice_in_dim(cotangent, t * part, part, 0)

        seq_blocks = blocks[0].reshape(n_c, -1)
        own_blocks = seq_blocks.shape[1]
        key_blocks = jnp.concatenate(
            [lax.dynamic_index_in_dim(seq_blocks, c ^ j, 0, keepdims=False) for j in range(n_c)]
        )
        positions = (
            key_blocks[:own_blocks, None] * BLOCK + jnp.arange(BLOCK, dtype=jnp.int32)[None, :]
        ).reshape(-1)
        cosine, sine = rope_tables(positions)
        bias = jnp.concatenate([bq.reshape(1, -1), b_kv], axis=1)
        dy_blocks = [
            dy_part,
            flip(dy_part, "tensor", 2),
            flip(dy_part, "context", 1),
            flip(dy_part, "context", 2),
        ]
        inputs_part = lax.dynamic_slice_in_dim(inputs, t * part, part, 0)
        bias = after(bias, dy_blocks[2:], own_gate_up, own_down, inputs_part)
        normed, factor_first, queries, kv_own = qkv(
            meta, inputs, gain_first, bias, cosine, sine, w_q, w_kv
        )
        far_gate_up = pieces_f(after(own_gate_up, kv_own, w_out_all), 1)[-1]
        w_gate_up = [own_gate_up, far_gate_up] if n_f == 2 else [far_gate_up]
        kv = kv_gather(after(kv_own, w_out_all))
        far_down = pieces_f(after(own_down, kv), 1)[-1]
        w_downs = [own_down, far_down] if n_f == 2 else [far_down]
        attended, lse = attention(key_blocks, queries, kv)
        middle, factor_second, normed2, dy_all = middle_norm(
            dot(attended, w_out_all).astype(bf16), inputs_part, gain_second, dy_blocks
        )

        hidden, slope, gated, *down_far = hidden_units(meta, normed2, dy_all, w_gate_up)
        grad_gate, grad_up, dx_part, out_part, *unit_far = hidden_back(
            meta, normed2, dy_all, hidden, slope, gated, w_gate_up, w_downs
        )
        unit_far = [*down_far, *unit_far]
        flat = lambda x: x.reshape(-1, width)
        if n_f == 2:
            down_got, gate_got, up_got = (flip(x, "fsdp", 1) for x in unit_far)
            early = [(hidden, flat(dy_all)), (grad_gate, flat(normed2))]
            later = [(grad_up, flat(normed2))]
        else:
            over_f = lambda x: lax.psum_scatter(x, "fsdp", scatter_dimension=1, tiled=True)
            owns = [
                over_f(unit_grads(meta, 0, 1, x, [unit]))
                for x, unit in ((dy_all, hidden), (normed2, grad_gate), (normed2, grad_up))
            ]
            down_got = gate_got = up_got = jnp.zeros_like(owns[0])
            early = later = []

        def unit_done(own, got):
            low = (own.astype(f32) + got.astype(f32)).astype(bf16)
            return low, flip(low, "context", 1)

        unit_whole = lambda low, other: by_bit(parity, low, other, 0).astype(f32)

        grad_middle, ffn_gain_grad, grad_middle_low, *first_owns = middle_back(
            dx_part, middle, factor_second, gain_second, dy_part, early, width // n_f
        )
        grad_middle_low = grad_middle_low.reshape(rows, width)
        down_own, gate_own = first_owns or owns[:2]
        down_done = unit_done(down_own, after(down_got, grad_middle_low))
        grad_attended = dot_cols(after(grad_middle_low, down_done[0]), w_out_all).astype(bf16)

        dq_low, dkv = attention_back(key_blocks, queries, grad_attended, lse, cosine, sine, kv)
        attention_args = [(attended, after(grad_middle_low, dq_low), 1), (normed, dq_low, 0)]
        fars = [grad_far(*args) for args in attention_args]
        dkv, *last_owns = kv_scatter(
            after(dkv, gate_got, fars), later, width // n_f
        )
        (up_own,) = last_owns or owns[2:]
        gate_done = unit_done(gate_own, after(gate_got, dkv, down_done))
        dkv = after(dkv, gate_done[0])
        dkv_low = jnp.where(core == 0, rotate_back(dkv, cosine, sine), dkv).astype(bf16)
        attention_args.append((normed, dkv_low, 0))
        fars.append(grad_far(*attention_args[-1]))
        dkv_low = after(dkv_low, fars)
        factor_part = lax.dynamic_slice_in_dim(factor_first, t * part, part, 0)
        own_biases = jnp.sum(
            jnp.concatenate([dq_low, dkv_low], axis=1).astype(f32), axis=0, keepdims=True
        )
        slots = lax.dynamic_update_slice(
            jnp.zeros((n_t, (heads + 1) * HD), f32), own_biases, (t, 0)
        )
        small_grads = jnp.concatenate(
            [jnp.zeros((1, width), f32), ffn_gain_grad, slots.reshape(1, -1)], axis=1
        )
        grad_qkv = qkv_back(meta, dq_low, dkv_low, w_q, w_kv)
        up_done = unit_done(up_own, after(up_got, grad_qkv))
        small_grads, input_grad = input_back(
            after(grad_qkv, up_done[0]),
            inputs_part,
            factor_part,
            gain_first,
            grad_middle,
            small_grads,
        )
        input_grad = input_grad.reshape(rows, width)
        if n_f > 2:
            small_grads = lax.psum(small_grads, "fsdp")
        attention_parts = [
            grad_sum(*args, far, small_grads) for args, far in zip(attention_args, fars)
        ]
        wd_grad = unit_whole(*after(down_done, small_grads))
        wg_grad = unit_whole(*after(gate_done, small_grads))
        small_grads, up_done, wg_grad, wd_grad = lax.optimization_barrier(
            (small_grads, up_done, wg_grad, wd_grad)
        )
        wo_grad, wq_grad, packed, wkv_all, outputs = context_sum(
            n_f == 2, attention_parts, small_grads, out_part, middle
        )
        outputs = outputs.reshape(rows, width)
        wkv_all = wkv_all.astype(f32)
        wk_grad = jnp.concatenate([wkv_all[0], wkv_all[2]], axis=1)
        wv_grad = jnp.concatenate([wkv_all[1], wkv_all[3]], axis=1)
        packed = packed[0]
        attn_gain_grad = lax.dynamic_slice_in_dim(packed, f * piece, piece, 0)
        ffn_gain_grad = lax.dynamic_slice_in_dim(packed, width + f * piece, piece, 0)
        slots = packed[2 * width :].reshape(n_t, heads + 1, HD)
        slots = lax.dynamic_slice_in_dim(slots, f * (HD // n_f), HD // n_f, 2)
        bq_out = lax.dynamic_index_in_dim(slots, t, 0, keepdims=False)[:heads]
        bk_out = slots[0::2, heads]
        bv_out = slots[1::2, heads]

        wu_grad = unit_whole(*up_done)
        wg_grad, wu_grad = wg_grad.T, wu_grad.T

        return (
            outputs,
            input_grad,
            attn_gain_grad,
            wq_grad,
            bq_out,
            wk_grad,
            bk_out,
            wv_grad,
            bv_out,
            wo_grad,
            ffn_gain_grad,
            wg_grad,
            wu_grad,
            wd_grad,
        )

    return local


def solution(mesh):
    in_specs = (
        P(("fsdp", "context"), None),
        P(("fsdp", "context"), None),
        P("fsdp", None),
        P("fsdp"),
        P("fsdp", "tensor"),
        P("tensor", "fsdp"),
        P("fsdp", None),
        P(None, "fsdp"),
        P("fsdp", None),
        P(None, "fsdp"),
        P("tensor", "fsdp"),
        P("fsdp"),
        P("fsdp", "tensor"),
        P("fsdp", "tensor"),
        P("tensor", "fsdp"),
    )
    out_specs = (
        P(("fsdp", "context"), None),
        P(("fsdp", "context"), None),
        P("fsdp"),
        P("fsdp", "tensor"),
        P("tensor", "fsdp"),
        P("fsdp", None),
        P(None, "fsdp"),
        P("fsdp", None),
        P(None, "fsdp"),
        P("tensor", "fsdp"),
        P("fsdp"),
        P("fsdp", "tensor"),
        P("fsdp", "tensor"),
        P("tensor", "fsdp"),
    )
    local = build(mesh.shape["fsdp"], mesh.shape["context"], mesh.shape["tensor"])
    return jax.shard_map(local, mesh=mesh, in_specs=in_specs, out_specs=out_specs, check_vma=False)
```

```python
import functools

import jax
import jax.numpy as jnp
from jax import lax
from jax.experimental import pallas as pl
from jax.experimental.pallas import tpu as pltpu
from jax.sharding import PartitionSpec as P

H = 12
KV = 2
HD = 128
BLOCK = 256

EPSILON = 1e-06
ROPE_BASE = 1000000.0
MASKED = -1e30
SCALING = HD ** (-0.5)
LANES = 128
VMEM_LIMIT = 60 << 20

f32 = jnp.float32
bf16 = jnp.bfloat16


def rope_tables(positions):
    halfway = HD // 2
    frequency = ROPE_BASE ** (-(jnp.arange(halfway, dtype=f32) * 2.0 / HD))
    angles = positions.astype(f32)[:, None] * frequency[None, :]
    cosine, sine = jnp.cos(angles), jnp.sin(angles)
    return (jnp.concatenate([cosine, cosine], axis=1), jnp.concatenate([sine, sine], axis=1))


def rotate(field, cosine, sine):
    halfway = HD // 2
    turned = jnp.concatenate([-field[..., halfway:], field[..., :halfway]], axis=-1)
    return field * cosine + turned * sine


def rotate_back(grad_field, cosine, sine):
    halfway = HD // 2
    moved = grad_field * sine
    turned = jnp.concatenate([moved[..., halfway:], -moved[..., :halfway]], axis=-1)
    return grad_field * cosine + turned


def dot(left, right):
    return jnp.dot(left, right, preferred_element_type=f32)


def dot_rows(left, right):
    return lax.dot_general(left, right, (((0,), (0,)), ((), ())), preferred_element_type=f32)


def dot_cols(left, right):
    return lax.dot_general(left, right, (((1,), (1,)), ((), ())), preferred_element_type=f32)


def mask_row(kb_ref, own_block, key_blocks):
    return jnp.concatenate(
        [
            jnp.full((1, BLOCK), jnp.where(kb_ref[j] <= own_block, 0.0, MASKED), f32)
            for j in range(key_blocks)
        ],
        axis=1,
    )


def attention_kernel(key_blocks, kb_ref, q_ref, k_ref, v_ref, o_ref, lse_ref):
    bias = mask_row(kb_ref, kb_ref[pl.program_id(1)], key_blocks)
    scores = dot_cols(q_ref[...], k_ref[...]) * SCALING + bias
    row_max = jnp.max(scores, axis=1, keepdims=True)
    expo = jnp.exp(scores - row_max)
    total = jnp.sum(expo, axis=1, keepdims=True)
    probability = (expo * (1.0 / total)).astype(bf16)
    o_ref[...] = dot(probability, v_ref[...]).astype(bf16)
    lse_ref[0] = row_max + jnp.log(total)


def attention(key_blocks, queries, kv):
    rows, width = queries.shape
    heads = width // HD
    whole = lambda kind: pl.BlockSpec((None,) + kv.shape[1:], lambda h, i, kb: (kind, 0, 0))
    tile = pl.BlockSpec((BLOCK, HD), lambda h, i, kb: (i, h))
    return pl.pallas_call(
        functools.partial(attention_kernel, kv.shape[1] // BLOCK),
        name="attention",
        grid_spec=pltpu.PrefetchScalarGridSpec(
            num_scalar_prefetch=1,
            grid=(heads, rows // BLOCK),
            in_specs=[tile, whole(0), whole(1)],
            out_specs=[tile, pl.BlockSpec((1, BLOCK, 1), lambda h, i, kb: (h, i, 0))],
        ),
        out_shape=[
            jax.ShapeDtypeStruct((rows, width), bf16),
            jax.ShapeDtypeStruct((heads, rows, 1), f32),
        ],
        compiler_params=pltpu.CompilerParams(vmem_limit_bytes=VMEM_LIMIT),
    )(key_blocks, queries, kv, kv)


def attention_back_kernel(
    key_blocks,
    kb_ref,
    q_ref,
    do_ref,
    lse_ref,
    cos_ref,
    sin_ref,
    k_ref,
    v_ref,
    dq_ref,
    dkv_ref,
    dk_ref,
    dv_ref,
):
    head, i = pl.program_id(0), pl.program_id(1)

    @pl.when((head == 0) & (i == 0))
    def _():
        dk_ref[...] = jnp.zeros_like(dk_ref)
        dv_ref[...] = jnp.zeros_like(dv_ref)

    bias = mask_row(kb_ref, kb_ref[i], key_blocks)
    scores = dot_cols(q_ref[...], k_ref[...]) * SCALING + bias
    probability = jnp.exp(scores - lse_ref[0])
    grad_probs = dot_cols(do_ref[...], v_ref[...])
    inner = jnp.sum(probability * grad_probs, axis=1, keepdims=True)
    grad_scores = (probability * (grad_probs - inner)).astype(bf16)
    grad_query = dot(grad_scores, k_ref[...]) * SCALING
    moved = grad_query * sin_ref[...]
    sign = jnp.where(lax.broadcasted_iota(jnp.int32, moved.shape, 1) < HD // 2, 1.0, -1.0)
    dq_ref[...] = (
        grad_query * cos_ref[...] + pltpu.roll(moved, HD // 2, 1) * sign
    ).astype(bf16)
    dk_ref[...] += dot_rows(grad_scores, q_ref[...]) * SCALING
    dv_ref[...] += dot_rows(probability.astype(bf16), do_ref[...])

    @pl.when((head == pl.num_programs(0) - 1) & (i == pl.num_programs(1) - 1))
    def _():
        dkv_ref[0] = dk_ref[...].astype(bf16)
        dkv_ref[1] = dv_ref[...].astype(bf16)


def attention_back(key_blocks, queries, grad_out, lse, cosine, sine, kv):
    rows, width = queries.shape
    heads = width // HD
    whole = lambda kind: pl.BlockSpec((None,) + kv.shape[1:], lambda h, i, kb: (kind, 0, 0))
    tile = pl.BlockSpec((BLOCK, HD), lambda h, i, kb: (i, h))
    table = pl.BlockSpec((BLOCK, HD), lambda h, i, kb: (i, 0))
    return pl.pallas_call(
        functools.partial(attention_back_kernel, kv.shape[1] // BLOCK),
        name="attention_back",
        grid_spec=pltpu.PrefetchScalarGridSpec(
            num_scalar_prefetch=1,
            grid=(heads, rows // BLOCK),
            in_specs=[
                tile,
                tile,
                pl.BlockSpec((1, BLOCK, 1), lambda h, i, kb: (h, i, 0)),
                table,
                table,
                whole(0),
                whole(1),
            ],
            out_specs=[tile, pl.BlockSpec(kv.shape, lambda h, i, kb: (0, 0, 0))],
            scratch_shapes=[pltpu.VMEM(kv.shape[1:], f32)] * 2,
        ),
        out_shape=[
            jax.ShapeDtypeStruct((rows, width), bf16),
            jax.ShapeDtypeStruct(kv.shape, bf16),
        ],
        compiler_params=pltpu.CompilerParams(vmem_limit_bytes=VMEM_LIMIT),
    )(key_blocks, queries, grad_out, lse, cosine, sine, kv, kv)


def qkv_kernel(pieces, meta_ref, x_ref, gain_ref, bias_ref, cos_ref, sin_ref, *refs):
    weights, (xn_ref, factor_ref, q_ref, kv_ref) = refs[: 2 * pieces], refs[2 * pieces :]
    values = x_ref[...].astype(f32)
    factor = lax.rsqrt(jnp.mean(values * values, axis=-1, keepdims=True) + EPSILON)
    factor_ref[...] = factor
    xn_ref[...] = (values * factor * gain_ref[...]).astype(bf16)
    depth = weights[0].shape[0]
    normed = [xn_ref[:, columns_of(meta_ref, j, depth, pieces)] for j in range(pieces)]
    cosine, sine = cos_ref[...], sin_ref[...]
    sign = jnp.where(lax.broadcasted_iota(jnp.int32, cosine.shape, 1) < HD // 2, -1.0, 1.0)
    sine = sine * sign
    width = q_ref.shape[1]
    total = bias_ref[:, :width] + sum(dot(x, w[...]) for x, w in zip(normed, weights[:pieces]))
    turn = lambda own: own * cosine + pltpu.roll(own, HD // 2, 1) * sine
    for h in range(width // HD):
        q_ref[:, h * HD : (h + 1) * HD] = turn(total[:, h * HD : (h + 1) * HD]).astype(bf16)
    own = bias_ref[:, width:] + sum(dot(x, w[...]) for x, w in zip(normed, weights[pieces:]))
    kv_ref[...] = jnp.where(meta_ref[2] == 0, turn(own), own).astype(bf16)


def columns_of(meta_ref, j, depth, pieces):
    if pieces == 1:
        return slice(None)
    return pl.ds(pl.multiple_of(meta_ref[j] * depth, LANES), depth)


def qkv(meta, inputs, gain, bias, cosine, sine, w_q, w_kv):
    rows, width = inputs.shape
    out = w_q[0].shape[1]
    tile = 256
    row = lambda n: pl.BlockSpec((tile, n), lambda i, m: (i, 0))
    fixed = lambda w: pl.BlockSpec(w.shape, lambda i, m: (0, 0))
    return pl.pallas_call(
        functools.partial(qkv_kernel, len(w_q)),
        name="qkv",
        grid_spec=pltpu.PrefetchScalarGridSpec(
            num_scalar_prefetch=1,
            grid=(rows // tile,),
            in_specs=[row(width), fixed(gain), fixed(bias), row(HD), row(HD)]
            + [fixed(w) for w in (*w_q, *w_kv)],
            out_specs=[row(width), row(1), row(out), row(HD)],
        ),
        out_shape=[
            jax.ShapeDtypeStruct((rows, width), bf16),
            jax.ShapeDtypeStruct((rows, 1), f32),
            jax.ShapeDtypeStruct((rows, out), bf16),
            jax.ShapeDtypeStruct((rows, HD), bf16),
        ],
        compiler_params=pltpu.CompilerParams(vmem_limit_bytes=VMEM_LIMIT),
    )(meta, inputs, gain, bias, cosine, sine, *w_q, *w_kv)


def qkv_back_kernel(pieces, meta_ref, dq_ref, dkv_ref, *refs):
    w_q, w_kv, out_ref = refs[:pieces], refs[pieces : 2 * pieces], refs[-1]
    for j in range(pieces):
        out_ref[:, columns_of(meta_ref, j, w_q[j].shape[0], pieces)] = (
            dot_cols(dq_ref[...], w_q[j][...]) + dot_cols(dkv_ref[...], w_kv[j][...])
        ).astype(bf16)


def qkv_back(meta, grad_q, grad_kv, w_q, w_kv):
    rows, width = grad_q.shape[0], sum(w.shape[0] for w in w_q)
    tile = 256
    row = lambda n: pl.BlockSpec((tile, n), lambda i, m: (i, 0))
    fixed = lambda w: pl.BlockSpec(w.shape, lambda i, m: (0, 0))
    return pl.pallas_call(
        functools.partial(qkv_back_kernel, len(w_q)),
        name="qkv_back",
        grid_spec=pltpu.PrefetchScalarGridSpec(
            num_scalar_prefetch=1,
            grid=(rows // tile,),
            in_specs=[row(grad_q.shape[1]), row(HD)] + [fixed(w) for w in (*w_q, *w_kv)],
            out_specs=row(width),
        ),
        out_shape=jax.ShapeDtypeStruct((rows, width), bf16),
        compiler_params=pltpu.CompilerParams(vmem_limit_bytes=VMEM_LIMIT),
    )(meta, grad_q, grad_kv, *w_q, *w_kv)


def add_rows(unit_refs, row_refs, columns, totals, outs):
    step = pl.program_id(0)

    @pl.when(step == 0)
    def _():
        for total in totals:
            total[...] = jnp.zeros_like(total)

    for total, unit, row in zip(totals, unit_refs, row_refs):
        total[...] += dot_rows(unit[...], row[:, columns])

    @pl.when(step == pl.num_programs(0) - 1)
    def _():
        for out, total in zip(outs, totals):
            out[...] = total[...].astype(bf16)


def hidden_kernel(pieces, meta_ref, x_ref, dy_ref, *refs):
    wg, wu, refs = refs[:pieces], refs[pieces : 2 * pieces], refs[2 * pieces :]
    hid_ref, slope_ref, gated_ref = refs[:3]
    columns = [columns_of(meta_ref, j, wg[j].shape[1], pieces) for j in range(pieces)]
    gate = sum(dot_cols(x_ref[:, at], w[...]) for at, w in zip(columns, wg))
    up = sum(dot_cols(x_ref[:, at], w[...]) for at, w in zip(columns, wu))
    sigma = 1.0 / (1.0 + jnp.exp(-gate))
    gated = gate * sigma
    hid_ref[...] = (gated * up).astype(bf16)
    slope_ref[...] = (up * (sigma + gated * (1.0 - sigma))).astype(bf16)
    gated_ref[...] = gated.astype(bf16)
    if pieces == 2:
        add_rows([hid_ref], [dy_ref], columns[1], refs[4:], refs[3:4])


def hidden_back_kernel(pieces, meta_ref, x_ref, dy_ref, hid_ref, slope_ref, gated_ref, *refs):
    wg, wu, wd = (refs[m * pieces : (m + 1) * pieces] for m in range(3))
    refs = refs[3 * pieces :]
    dg_ref, du_ref, dx_ref, out_ref = refs[:4]
    columns = [columns_of(meta_ref, j, wg[j].shape[1], pieces) for j in range(pieces)]
    grad_hidden = sum(dot_cols(dy_ref[:, at], w[...]) for at, w in zip(columns, wd))
    dg_ref[...] = (grad_hidden * slope_ref[...].astype(f32)).astype(bf16)
    du_ref[...] = (grad_hidden * gated_ref[...].astype(f32)).astype(bf16)

    @pl.when(pl.program_id(0) // (pl.num_programs(0) // 2) == meta_ref[3])
    def _():
        for at, g, u, d in zip(columns, wg, wu, wd):
            dx_ref[:, at] = (dot(dg_ref[...], g[...]) + dot(du_ref[...], u[...])).astype(bf16)
            out_ref[:, at] = dot(hid_ref[...], d[...]).astype(bf16)

    if pieces == 2:
        add_rows([dg_ref, du_ref], [x_ref, x_ref], columns[1], refs[6:], refs[4:6])


def hidden_specs(meta, normed, weights):
    width = normed.shape[-1]
    rows = normed.shape[0] * normed.shape[1]
    units, depth = weights[0].shape[0] // 2, weights[0].shape[1]
    tile = 512
    steps = rows // tile
    half = steps // 2
    once = pl.Buffered(1)
    inside = lambda i, m: jnp.clip(i - m[3] * half, 0, half - 1)
    return {
        "steps": steps,
        "flat": lambda x: x.reshape(-1, width),
        "row": pl.BlockSpec((tile, width), lambda i, m: (lax.rem(i + m[3] * half, steps), 0)),
        "unit": pl.BlockSpec((tile, units), lambda i, m: (i, 0)),
        "near_unit": pl.BlockSpec((tile, units), lambda i, m: (inside(i, m) + m[3] * half, 0)),
        "near_row": pl.BlockSpec((tile, width), lambda i, m: (inside(i, m), 0)),
        "weight": lambda k: pl.BlockSpec((units, depth), lambda i, m: (k, 0), pipeline_mode=once),
        "grad": pl.BlockSpec((units, depth), lambda i, m: (0, 0), pipeline_mode=once),
        "unit_shape": jax.ShapeDtypeStruct((rows, units), bf16),
        "near_shape": jax.ShapeDtypeStruct((rows // 2, width), bf16),
        "grad_shape": jax.ShapeDtypeStruct((units, depth), bf16),
        "total": pltpu.VMEM((units, depth), f32),
    }


def hidden_call(kernel, name, meta, args, in_specs, outs, grads, specs):
    return pl.pallas_call(
        kernel,
        name=name,
        grid_spec=pltpu.PrefetchScalarGridSpec(
            num_scalar_prefetch=1,
            grid=(specs["steps"],),
            in_specs=in_specs,
            out_specs=[specs[x] for x in outs] + [specs["grad"]] * grads,
            scratch_shapes=[specs["total"]] * grads,
        ),
        out_shape=[specs[x.split("_")[0] + "_shape"] for x in outs]
        + [specs["grad_shape"]] * grads,
        compiler_params=pltpu.CompilerParams(vmem_limit_bytes=VMEM_LIMIT),
    )(meta, *args)


def hidden_units(meta, normed, grad_out, weights):
    specs, pieces = hidden_specs(meta, normed, weights), len(weights)
    return hidden_call(
        functools.partial(hidden_kernel, pieces),
        "hidden_units",
        meta,
        [specs["flat"](normed), specs["flat"](grad_out)] + list(weights) * 2,
        [specs["row"]] * 2 + [specs["weight"](k) for k in range(2) for _ in weights],
        ["unit"] * 3,
        pieces == 2,
        specs,
    )


def hidden_back(meta, normed, grad_out, hidden, slope, gated, weights, down_weights):
    specs, pieces = hidden_specs(meta, normed, weights), len(weights)
    return hidden_call(
        functools.partial(hidden_back_kernel, pieces),
        "hidden_back",
        meta,
        [specs["flat"](normed), specs["flat"](grad_out), hidden, slope, gated]
        + list(weights) * 2
        + list(down_weights),
        [specs["row"]] * 2
        + [specs["near_unit"], specs["unit"], specs["unit"]]
        + [specs["weight"](k) for k in (0, 1, 0) for _ in weights],
        ["unit", "unit", "near_row", "near_row"],
        2 * (pieces == 2),
        specs,
    )


def unit_grads_kernel(count, meta_ref, near_ref, far_ref, *refs):
    units, out_ref, x_ref = refs[:count], refs[-2], refs[-1]
    half = near_ref.shape[0]
    x_ref[pl.ds(pl.multiple_of(meta_ref[3] * half, half), half)] = near_ref[...]
    x_ref[pl.ds(pl.multiple_of((1 - meta_ref[3]) * half, half), half)] = far_ref[...]
    for k, unit in enumerate(units):
        depth = unit.shape[1]
        out_ref[k * depth : (k + 1) * depth] = dot_rows(unit[...], x_ref[...]).astype(bf16)


def unit_grads(meta, which, pieces, x, units_of):
    width = x.shape[-1]
    count, (rows, units) = len(units_of), units_of[0].shape
    depth = width // pieces
    tile = 256
    steps = depth // tile
    shard = (lambda m: m[which]) if pieces > 1 else (lambda m: 0)
    feature = lambda half: pl.BlockSpec(
        (rows // 2, tile), lambda i, m: (half, shard(m) * steps + i)
    )
    unit = pl.BlockSpec((rows, units), lambda i, m: (0, 0), pipeline_mode=pl.Buffered(1))
    x = x.reshape(-1, width)
    return pl.pallas_call(
        functools.partial(unit_grads_kernel, count),
        name=f"unit_grads_{which}_{count}",
        grid_spec=pltpu.PrefetchScalarGridSpec(
            num_scalar_prefetch=1,
            grid=(steps,),
            in_specs=[feature(0), feature(1)] + [unit] * count,
            out_specs=pl.BlockSpec((count * units, tile), lambda i, m: (0, i)),
            scratch_shapes=[pltpu.VMEM((rows, tile), bf16)],
        ),
        out_shape=jax.ShapeDtypeStruct((count * units, depth), bf16),
        compiler_params=pltpu.CompilerParams(vmem_limit_bytes=VMEM_LIMIT),
    )(meta, x, x, *units_of)


class Wires:
    def __init__(self, sends, receives, locals_):
        self.sends, self.receives, self.locals = sends, receives, locals_
        self.used = self.used_local = 0
        self.started = []

    def plan(self, source, target, device):
        k = self.used
        self.used += 1
        return pltpu.make_async_remote_copy(
            source,
            target,
            self.sends.at[k],
            self.receives.at[k],
            device_id=device,
            device_id_type=pl.DeviceIdType.MESH,
        )

    def copy(self, source, target, device):
        one = self.plan(source, target, device)
        one.start()
        self.started.append(one)
        return one

    def here(self, source, target):
        k = self.used_local
        self.used_local += 1
        one = pltpu.make_async_copy(source, target, self.locals.at[k])
        one.start()
        return one

    def finish(self):
        for one in self.started:
            one.wait_send()


class OwnGrad:
    TILE = 256

    def __init__(self, units, rows, out, units_here, rows_here):
        self.units, self.rows, self.out = units, rows, out
        self.units_here, self.rows_here = units_here, rows_here
        self.tiles = out.shape[1] // self.TILE
        self.copies = None

    def fetch(self, wires):
        half, depth = self.rows.shape[0] // 2, self.out.shape[1]
        column = pl.multiple_of(lax.axis_index("fsdp") * depth, LANES)
        pair = lax.axis_index("context") // 2
        self.copies = [wires.here(self.units, self.units_here)]
        for k, place in ((0, pair), (1, 1 - pair)):
            self.copies.append(
                wires.here(
                    self.rows.at[pl.ds(k * half, half), pl.ds(column, depth)],
                    self.rows_here.at[pl.ds(pl.multiple_of(place * half, half), half)],
                )
            )

    def make(self, first, past):
        for one in self.copies:
            one.wait()
        self.copies = []

        @pl.loop(first, past)
        def _(k):
            at = pl.ds(pl.multiple_of(k * self.TILE, self.TILE), self.TILE)
            self.out[:, at] = dot_rows(self.units_here[...], self.rows_here[:, at]).astype(bf16)


def own_grad_call(fill, width):
    args = [x for pair in fill for x in pair]
    outs = [jax.ShapeDtypeStruct((units.shape[1], width), bf16) for units, _ in fill]
    scratch = []
    for units, rows in fill:
        scratch += [pltpu.VMEM(units.shape, bf16), pltpu.VMEM((rows.shape[0], width), bf16)]
    return args, outs, scratch


def own_grads(count, args, outs, scratch):
    return [
        OwnGrad(args[2 * k], args[2 * k + 1], outs[k], scratch[2 * k], scratch[2 * k + 1])
        for k in range(count)
    ]


def meet(devices):
    barrier = pltpu.get_barrier_semaphore()
    for device in devices:
        pl.semaphore_signal(barrier, inc=1, device_id=device, device_id_type=pl.DeviceIdType.MESH)
    pl.semaphore_wait(barrier, len(devices))


def partners():
    c, t = lax.axis_index("context"), lax.axis_index("tensor")
    flip = lambda x, bit: x + bit * (1 - 2 * lax.rem(x // bit, 2))
    return {
        "core": {"tensor": flip(t, 1)},
        "y": {"tensor": flip(t, 2)},
        "z": {"context": flip(c, 1)},
        "far": {"context": flip(c, 2)},
        "last": {"context": flip(flip(c, 1), 2)},
    }


def wide(x):
    return x.astype(f32)


def ranks():
    t = lax.axis_index("tensor")
    flip = lambda x, bit: x + bit * (1 - 2 * lax.rem(x // bit, 2))
    return (t, flip(t, 1), flip(t, 2), flip(flip(t, 1), 2))


def scatter_rank(wires, to, part, own, got_core, sent, got_y):
    size = part.shape[1] // 2
    halves = [pl.ds(0, size), pl.ds(size, size)]
    rank = ranks()
    from_core = {}
    for block in (1, 0):
        for k, at in enumerate(halves):
            from_core[block, k] = wires.copy(
                part.at[rank[1 + 2 * block], at], got_core.at[block, at], to["core"]
            )
    mine = [wires.here(part.at[rank[2 * block]], own.at[block]) for block in (0, 1)]
    yield
    for one in mine:
        one.wait()
    from_y = []
    for k, at in enumerate(halves):
        from_core[1, k].wait_recv()
        sent[at] = (wide(own[1, at]) + wide(got_core[1, at])).astype(bf16)
        from_y.append(wires.copy(sent.at[at], got_y.at[at], to["y"]))
    yield
    for k in range(2):
        from_core[0, k].wait_recv()
    total = wide(own[0]) + wide(got_core[0])
    for one in from_y:
        one.wait_recv()
    return total + wide(got_y[...])


def scatter_pair(wires, to, part, own, got_core, sent, got_y, got_z, diag_y, diag_z):
    size = part.shape[1] // 2
    low, high = pl.ds(0, size), pl.ds(size, size)
    from_core = {j: wires.copy(part.at[4 + j], got_core.at[j], to["core"]) for j in (3, 1, 2, 0)}
    mine = wires.here(part.at[pl.ds(0, 4)], own)
    yield
    mine.wait()
    both = lambda j, at: wide(own[j, at]) + wide(got_core[j, at])
    from_core[3].wait_recv()
    sent[2] = (wide(own[3]) + wide(got_core[3])).astype(bf16)
    via_z = wires.copy(sent.at[2, low], diag_z, to["z"])
    via_y = wires.copy(sent.at[2, high], diag_y, to["y"])
    from_core[1].wait_recv()
    sent[0, high] = both(1, high).astype(bf16)
    y_high = wires.copy(sent.at[0, high], got_y.at[high], to["y"])
    from_core[2].wait_recv()
    sent[1, low] = both(2, low).astype(bf16)
    z_low = wires.copy(sent.at[1, low], got_z.at[low], to["z"])
    yield
    via_z.wait_recv()
    sent[0, low] = (both(1, low) + wide(diag_z[...])).astype(bf16)
    y_low = wires.copy(sent.at[0, low], got_y.at[low], to["y"])
    via_y.wait_recv()
    sent[1, high] = (both(2, high) + wide(diag_y[...])).astype(bf16)
    z_high = wires.copy(sent.at[1, high], got_z.at[high], to["z"])
    yield
    from_core[0].wait_recv()
    total = wide(own[0]) + wide(got_core[0])
    for one in (y_high, z_low, y_low, z_high):
        one.wait_recv()
    return total + wide(got_y[...]) + wide(got_z[...])


def result_of(steps):
    while True:
        try:
            next(steps)
        except StopIteration as done:
            return done.value


def gather_rank(wires, to, block, out):
    size = block.shape[0] // 2
    halves = [pl.ds(0, size), pl.ds(size, size)]
    rank = ranks()
    mine = wires.here(block, out.at[rank[0]])
    from_y = [wires.copy(block.at[h], out.at[rank[0], h], to["y"]) for h in halves]
    from_core = [wires.copy(block, out.at[rank[0]], to["core"])]
    yield
    for h, one in zip(halves, from_y):
        one.wait_recv()
        from_core.append(wires.copy(out.at[rank[2], h], out.at[rank[2], h], to["core"]))
    for one in from_core:
        one.wait_recv()
    mine.wait()


def gather_pair(wires, to, block, out, base):
    size = block.shape[0] // 2
    low, high = pl.ds(0, size), pl.ds(size, size)
    at = lambda j: out.at[base + j]
    from_z = wires.copy(block, at(2), to["z"])
    yield
    from_y = wires.copy(block, at(1), to["y"])
    from_core = [wires.copy(block, at(4), to["core"])]
    yield
    from_y.wait_recv()
    via_z = wires.copy(out.at[base + 1, low], out.at[base + 3, low], to["z"])
    from_core.append(wires.copy(at(1), at(5), to["core"]))
    from_z.wait_recv()
    via_y = wires.copy(out.at[base + 2, high], out.at[base + 3, high], to["y"])
    from_core.append(wires.copy(at(2), at(6), to["core"]))
    yield
    via_z.wait_recv()
    via_y.wait_recv()
    from_core.append(wires.copy(at(3), at(7), to["core"]))
    return from_core


def remote_call(kernel, name, key, args, outs, scratch, copies, in_vmem):
    ins, out_in = in_vmem
    spec = lambda inside: pl.BlockSpec(memory_space=pltpu.VMEM if inside else pl.ANY)
    return pl.pallas_call(
        kernel,
        name=name,
        out_shape=outs,
        in_specs=[spec(x) for x in ins],
        out_specs=[spec(x) for x in out_in],
        scratch_shapes=list(scratch)
        + [
            pltpu.SemaphoreType.DMA((copies,)),
            pltpu.SemaphoreType.DMA((copies,)),
            pltpu.SemaphoreType.DMA((8,)),
        ],
        compiler_params=pltpu.CompilerParams(
            collective_id=key, has_side_effects=True, vmem_limit_bytes=VMEM_LIMIT
        ),
    )(*args)


def kv_gather_kernel(own_ref, out_ref, *sems):
    wires, to = Wires(*sems), partners()
    kind = lax.rem(lax.axis_index("tensor"), 2)
    rows = own_ref.shape[0]
    block = lambda j: out_ref.at[kind, pl.ds(j * rows, rows)]
    meet([to[k] for k in ("core", "z", "far", "last")])
    mine = wires.here(own_ref, block(0))
    arrive = [wires.copy(own_ref, block(j), to[k]) for j, k in ((3, "last"), (2, "far"), (1, "z"))]
    from_core = [wires.copy(own_ref, block(0), to["core"])]
    for j, one in ((1, arrive[2]), (2, arrive[1]), (3, arrive[0])):
        one.wait_recv()
        from_core.append(wires.copy(block(j), block(j), to["core"]))
    for one in from_core:
        one.wait_recv()
    mine.wait()
    wires.finish()


def kv_gather(own):
    rows, width = own.shape
    n_c = lax.axis_size("context")
    return remote_call(
        kv_gather_kernel,
        "kv_gather",
        0,
        [own],
        [jax.ShapeDtypeStruct((2, n_c * rows, width), bf16)],
        [],
        8,
        ([False], [False]),
    )[0]


def kv_scatter_kernel(count, part_ref, *refs):
    args, dkv_ref, outs = refs[: 2 * count], refs[2 * count], refs[2 * count + 1 : 3 * count + 1]
    own, got_core, sent, got = refs[3 * count + 1 : 3 * count + 5]
    wires, to = Wires(*refs[-3:]), partners()
    fill = own_grads(count, args, outs, refs[3 * count + 5 : -3])
    kind = lax.rem(lax.axis_index("tensor"), 2)
    rows = dkv_ref.shape[0]
    block = lambda j: pl.ds(j * rows, rows)
    meet([to[k] for k in ("core", "z", "far", "last")])
    steps = ((3, "last"), (2, "far"), (1, "z"), (0, None))
    from_core = {
        j: wires.copy(part_ref.at[1 - kind, block(j)], got_core.at[block(j)], to["core"])
        for j, _ in steps
    }
    mine = wires.here(part_ref.at[kind], own)
    for one in fill:
        one.fetch(wires)
    mine.wait()
    arrive = []
    for j, k in steps[:3]:
        from_core[j].wait_recv()
        sent[block(j)] = (wide(own[block(j)]) + wide(got_core[block(j)])).astype(bf16)
        arrive.append(wires.copy(sent.at[block(j)], got.at[block(j)], to[k]))
    for one in fill:
        one.make(0, one.tiles)
    from_core[0].wait_recv()
    total = wide(own[block(0)]) + wide(got_core[block(0)])
    for one in arrive:
        one.wait_recv()
    for j in (1, 2, 3):
        total = total + wide(got[block(j)])
    dkv_ref[...] = total
    wires.finish()


def kv_scatter(part, fill, width):
    _, rows, depth = part.shape
    n_c = lax.axis_size("context")
    args, outs, scratch = own_grad_call(fill, width)
    return remote_call(
        functools.partial(kv_scatter_kernel, len(fill)),
        "kv_scatter",
        1,
        [part, *args],
        [jax.ShapeDtypeStruct((rows // n_c, depth), f32), *outs],
        [pltpu.VMEM((rows, depth), bf16)] * 4 + scratch,
        7,
        ([False] * (1 + len(args)), [True] * (1 + len(outs))),
    )


def middle_kernel(
    part,
    x_ref,
    gain_ref,
    dy_ref,
    dy_y,
    dy_z,
    dy_far,
    mid_ref,
    factor_ref,
    out,
    dys,
    own,
    core,
    sent,
    got,
    xn,
    *sems,
):
    wires, to = Wires(*sems), partners()
    blocks = out.shape[0] // 2
    size = xn.shape[0] // 2
    low, high = pl.ds(0, size), pl.ds(size, size)
    meet([to[k] for k in ("core", "y", "z", "far")])
    summed = scatter_rank(wires, to, part, own, core, sent, got)
    next(summed)
    mine = [
        wires.here(block, dys.at[k])
        for block, k in ((dy_ref, 0), (dy_y, 1), (dy_z, 2), (dy_far, blocks))
    ]
    via_z = wires.copy(dy_y.at[low], dys.at[3, low], to["z"])
    dy_last = gather_pair(wires, to, dy_far, dys, blocks)
    next(dy_last)
    next(summed)
    via_y = wires.copy(dy_z.at[high], dys.at[3, high], to["y"])
    ends = [
        wires.copy(block, dys.at[4 + k], to["core"])
        for k, block in enumerate((dy_ref, dy_y, dy_z))
    ]
    next(dy_last)
    middle = wide(x_ref[...]) + result_of(summed)
    mid_ref[...] = middle
    factor = lax.rsqrt(jnp.mean(middle * middle, axis=-1, keepdims=True) + EPSILON)
    factor_ref[...] = factor
    xn[...] = (middle * factor * gain_ref[...]).astype(bf16)
    mine.append(wires.here(xn, out.at[0]))
    xn_far = wires.copy(xn, out.at[blocks], to["far"])
    xn_near = gather_pair(wires, to, xn, out, 0)
    next(xn_near)
    next(xn_near)
    via_z.wait_recv()
    via_y.wait_recv()
    ends.append(wires.copy(dys.at[3], dys.at[7], to["core"]))
    next(dy_last)
    next(xn_near)
    xn_far.wait_recv()
    xn_last = gather_pair(wires, to, out.at[blocks], out, blocks)
    next(xn_last)
    next(xn_last)
    ends += result_of(dy_last) + result_of(xn_near)
    next(xn_last)
    ends += result_of(xn_last)
    for one in ends:
        one.wait_recv()
    for one in mine:
        one.wait()
    wires.finish()


def middle_norm(part, inputs_part, gain, dy_blocks):
    rows, width = inputs_part.shape
    return remote_call(
        middle_kernel,
        "middle_norm",
        2,
        [part.reshape(4, rows, width), inputs_part, gain, *dy_blocks],
        [
            jax.ShapeDtypeStruct((rows, width), f32),
            jax.ShapeDtypeStruct((rows, 1), f32),
            jax.ShapeDtypeStruct((16, rows, width), bf16),
            jax.ShapeDtypeStruct((16, rows, width), bf16),
        ],
        [
            pltpu.VMEM((2, rows, width), bf16),
            pltpu.VMEM((2, rows, width), bf16),
            pltpu.VMEM((rows, width), bf16),
            pltpu.VMEM((rows, width), bf16),
            pltpu.VMEM((rows, width), bf16),
        ],
        48,
        ([False] + [True] * 6, [True, True, False, False]),
    )


def norm_back_rows(values, factor, gain, grad_normed):
    gained = gain * grad_normed
    inner = jnp.mean(gained * values, axis=-1, keepdims=True)
    grad_values = factor * gained - values * (factor * factor * factor) * inner
    return grad_values, jnp.sum(grad_normed * values * factor, axis=0, keepdims=True)


def middle_back_kernel(count, part, mid_ref, factor_ref, gain_ref, dy_ref, *refs):
    args, refs = refs[: 2 * count], refs[2 * count :]
    got_ref, refs = (refs[0], refs[1:]) if count else (None, refs)
    (dmid_ref, dgain_ref, out), refs = refs[:3], refs[3:]
    outs, refs = refs[:count], refs[count:]
    (low_ref, half_ref), refs = (refs[:2], refs[2:]) if count else ((None, None), refs)
    low, first, wires, to = refs[0], refs[1:8], Wires(*refs[-3:]), partners()
    fill = own_grads(count, args, outs, refs[8:-3])
    meet([to[k] for k in ("core", "y", "z")])
    back = scatter_pair(wires, to, part, *first)
    next(back)
    for one in fill:
        one.fetch(wires)
    next(back)
    if fill:
        fill[0].make(0, 1)
    next(back)
    if fill:
        fill[0].make(1, fill[0].tiles)
        low_ref[...] = (wide(outs[0][...]) + wide(got_ref[...])).astype(bf16)
        near_half = wires.copy(low_ref.at[pl.ds(0, half_ref.shape[0])], half_ref, to["z"])
    grad_normed = result_of(back)
    du, dgain = norm_back_rows(mid_ref[...], factor_ref[...], gain_ref[...], grad_normed)
    dgain_ref[...] = dgain
    dmid = wide(dy_ref[...]) + du
    low[...] = dmid.astype(bf16)
    share = gather_rank(wires, to, low, out)
    next(share)
    dmid_ref[...] = dmid
    for one in fill[1:]:
        one.make(0, one.tiles)
    result_of(share)
    if fill:
        near_half.wait_recv()
    wires.finish()


def pair_scratch(rows, width):
    return [
        pltpu.VMEM((4, rows, width), bf16),
        pltpu.VMEM((4, rows, width), bf16),
        pltpu.VMEM((3, rows, width), bf16),
        pltpu.VMEM((rows, width), bf16),
        pltpu.VMEM((rows, width), bf16),
        pltpu.VMEM((rows // 2, width), bf16),
        pltpu.VMEM((rows // 2, width), bf16),
    ]


def middle_back(part, middle, factor, gain, dy_part, fill, got, shard):
    rows, width = middle.shape
    args, outs, scratch = own_grad_call(fill, shard)
    if fill:
        args = [*args, got]
        units = got.shape[0]
        outs = [*outs, *(jax.ShapeDtypeStruct((n, shard), bf16) for n in (units, units // 2))]
    return remote_call(
        functools.partial(middle_back_kernel, len(fill)),
        "middle_back",
        3,
        [part.reshape(8, rows, width), middle, factor, gain, dy_part, *args],
        [
            jax.ShapeDtypeStruct((rows, width), f32),
            jax.ShapeDtypeStruct((1, width), f32),
            jax.ShapeDtypeStruct((4, rows, width), bf16),
            *outs,
        ],
        [pltpu.VMEM((rows, width), bf16)] + pair_scratch(rows, width) + scratch,
        16,
        (
            [False] + [True] * 4 + ([False] * (len(args) - 1) + [True] if fill else []),
            [True, True, False] + ([True] * (len(outs) - 1) + [False] if fill else []),
        ),
    )


def add_all(wires, ways, value, slots):
    for k, device in enumerate(ways):
        one = wires.copy(value, slots.at[k], device)
        one.wait()
        wires.started = [x for x in wires.started if x is not one]
        value[...] = value[...] + slots[k]


def input_back_kernel(
    part, x_ref, factor_ref, gain_ref, dmid_ref, small_ref, sum_ref, out, *rest
):
    low, own, core, sent, got, slots = rest[:-3]
    wires, to = Wires(*rest[-3:]), partners()
    meet([to[k] for k in ("core", "y")])
    grad_normed = result_of(scatter_rank(wires, to, part, own, core, sent, got))
    du, dgain = norm_back_rows(wide(x_ref[...]), factor_ref[...], gain_ref[...], grad_normed)
    low[...] = (dmid_ref[...] + du).astype(bf16)
    share = gather_rank(wires, to, low, out)
    next(share)
    width = dgain.shape[1]
    sum_ref[:, width:] = small_ref[:, width:]
    sum_ref[:, :width] = dgain
    add_all(wires, [to["core"], to["y"]], sum_ref, slots)
    result_of(share)
    wires.finish()


def input_back(part, inputs_part, factor, gain, grad_middle, small):
    rows, width = inputs_part.shape
    return remote_call(
        input_back_kernel,
        "input_back",
        5,
        [part.reshape(4, rows, width), inputs_part, factor, gain, grad_middle, small],
        [
            jax.ShapeDtypeStruct(small.shape, f32),
            jax.ShapeDtypeStruct((4, rows, width), bf16),
        ],
        [
            pltpu.VMEM((rows, width), bf16),
            pltpu.VMEM((2, rows, width), bf16),
            pltpu.VMEM((2, rows, width), bf16),
            pltpu.VMEM((rows, width), bf16),
            pltpu.VMEM((rows, width), bf16),
            pltpu.VMEM((2,) + small.shape, f32),
        ],
        16,
        ([False, True, True, True, True, True], [True, False]),
    )


def context_sum_kernel(over_f, *refs):
    parts, small_ref, out_part, mid_ref = refs[:3], refs[3], refs[4], refs[5]
    outs, sum_ref, shared, outputs = refs[6:8], refs[8], refs[9], refs[10]
    lows, from_end, from_middle = refs[11:15], refs[15:19], refs[19:23]
    out_low, slot, scratch = refs[23], refs[24], refs[25:32]
    wires, to, c = Wires(*refs[32:]), partners(), lax.axis_index("context")
    end = (c == 0) | (c == lax.axis_size("context") - 1)
    inner = jnp.logical_not(end)
    greet = ["core", "y", "z", "last"]
    if over_f:
        to["f"] = {"fsdp": 1 - lax.axis_index("fsdp")}
        greet.append("f")
    meet([to[k] for k in greet])
    ahead = scatter_pair(wires, to, out_part, *scratch)
    next(ahead)
    sum_ref[...] = small_ref[...]
    from_f = wires.copy(small_ref, slot, to["f"]) if over_f else None
    next(ahead)
    sources = [*parts, sum_ref]
    chunks = []
    for i, cuts in ((2, 1), (0, 2), (1, 2), (3, 1)):
        size = sources[i].shape[0] // cuts
        chunks += [(i, pl.ds(k * size, size)) for k in range(cuts)]
    inward = [wires.plan(sources[i].at[at], from_end[i].at[at], to["z"]) for i, at in chunks]
    across = [wires.plan(lows[i].at[at], from_middle[i].at[at], to["last"]) for i, at in chunks]
    outward = [wires.plan(lows[i].at[at], lows[i].at[at], to["z"]) for i, at in chunks]
    small = len(chunks) - 1

    def send_in(k):
        @pl.when(end)
        def _():
            inward[k].start()

    def pass_on(first, past):
        @pl.when(inner)
        def _():
            for k in range(first, past):
                i, at = chunks[k]
                inward[k].wait_recv()
                total = wide(sources[i][at]) + wide(from_end[i][at])
                lows[i][at] = total.astype(lows[i].dtype)
                across[k].start()
                if k:
                    send_out(k - 1)

    def send_out(k):
        i, at = chunks[k]
        across[k].wait()
        lows[i][at] = (wide(lows[i][at]) + wide(from_middle[i][at])).astype(lows[i].dtype)
        outward[k].start()

    send_in(0)
    send_in(1)
    next(ahead)
    if over_f:
        from_f.wait_recv()
        sum_ref[...] = sum_ref[...] + slot[...]
    for k in range(2, small + 1):
        send_in(k)
    pass_on(0, 2)
    out_low[...] = (mid_ref[...] + result_of(ahead)).astype(bf16)
    out_share = gather_rank(wires, to, out_low, outputs)
    next(out_share)
    pass_on(2, small + 1)

    @pl.when(inner)
    def _():
        send_out(small)

    result_of(out_share)

    def arrived(k):
        @pl.when(end)
        def _():
            outward[k].wait_recv()

    arrived(0)
    share = gather_rank(wires, to, lows[2], shared)
    next(share)
    for k in range(1, len(chunks)):
        arrived(k)

    @pl.when(end)
    def _():
        for one in inward:
            one.wait_send()

    for i in (0, 1):
        outs[i][...] = wide(lows[i][...])
    sum_ref[...] = lows[3][...]
    result_of(share)

    @pl.when(inner)
    def _():
        for one in outward:
            one.wait_send()

    wires.finish()


def context_sum(over_f, parts, small, out_part, middle):
    rows, width = middle.shape
    lines = [pltpu.VMEM(x.shape, x.dtype) for x in (*parts, small)]
    return remote_call(
        functools.partial(context_sum_kernel, over_f),
        "context_sum",
        6,
        [*parts, small, out_part.reshape(8, rows, width), middle],
        [jax.ShapeDtypeStruct(x.shape, f32) for x in parts[:2]]
        + [jax.ShapeDtypeStruct(small.shape, f32)]
        + [jax.ShapeDtypeStruct((4,) + parts[2].shape, bf16)]
        + [jax.ShapeDtypeStruct((4, rows, width), bf16)],
        lines * 3
        + [pltpu.VMEM((rows, width), bf16), pltpu.VMEM(small.shape, f32)]
        + pair_scratch(rows, width),
        48,
        ([True] * 4 + [False, True], [True] * 3 + [False] * 2),
    )


def build(n_f, n_c, n_t):
    def flip(x, axis, bit):
        size = {"fsdp": n_f, "context": n_c, "tensor": n_t}[axis]
        return lax.ppermute(x, axis, [(i, i ^ bit) for i in range(size)])

    def by_bit(bit, x, other, axis):
        return jnp.where(
            bit == 0,
            jnp.concatenate([x, other], axis=axis),
            jnp.concatenate([other, x], axis=axis),
        )

    def after(x, *others):
        return lax.optimization_barrier((x, others))[0]

    def local(
        inputs,
        cotangent,
        blocks,
        attn_gain,
        w_query,
        b_query,
        w_key,
        b_key,
        w_value,
        b_value,
        w_out,
        ffn_gain,
        w_gate,
        w_up,
        w_down,
    ):
        rows, width = inputs.shape
        f = lax.axis_index("fsdp")
        c = lax.axis_index("context")
        t = lax.axis_index("tensor")
        core, parity, pair = t % 2, c % 2, c // 2
        heads = w_query.shape[1] // HD
        group = (t * heads) // (H // KV)
        part = rows // n_t
        units_all = w_gate.shape[1]
        units = units_all // 2

        def gather_f(x, axis):
            if n_f == 2:
                return by_bit(f, x, flip(x, "fsdp", 1), axis)
            return lax.all_gather(x, "fsdp", axis=axis, tiled=True)

        def grad_far(left, right, side):
            if n_f > 2:
                return None
            source = (left, right)[side]
            half = width // 2
            far = lax.dynamic_slice_in_dim(source, (1 - f) * half, half, 1)
            return (dot_rows(far, right) if side == 0 else dot_rows(left, far)).astype(bf16)

        def grad_sum(left, right, side, far, late):
            if n_f > 2:
                return lax.psum_scatter(
                    dot_rows(left, right).astype(bf16), "fsdp", scatter_dimension=side, tiled=True
                )
            source = (left, right)[side]
            half = width // 2
            own = lax.dynamic_slice_in_dim(source, f * half, half, 1)
            own = dot_rows(own, right) if side == 0 else dot_rows(left, own)
            return (own + after(flip(far, "fsdp", 1), late).astype(f32)).astype(bf16)

        small = jnp.concatenate(
            [v.reshape(1, -1) for v in (attn_gain, ffn_gain, b_query, b_key, b_value)], axis=1
        )
        column = lambda w: lax.dynamic_slice_in_dim(w, group * HD, HD, 1)
        w_kv_own = jnp.where(core == 0, column(w_key), column(w_value))
        pieces_f = lambda x, axis: (
            [x, flip(x, "fsdp", 1)]
            if n_f == 2
            else [lax.all_gather(x, "fsdp", axis=axis, tiled=True)]
        )
        meta = jnp.stack([f, 1 - f, core, pair]).astype(jnp.int32)
        w_q = pieces_f(w_query, 0)
        w_kv = pieces_f(w_kv_own, 0)
        small = gather_f(small, 0)
        w_out_all = gather_f(after(w_out, small, w_q, w_kv), 1)
        piece = attn_gain.shape[0]
        gain_first = small[:, :piece].reshape(1, width).astype(f32)
        gain_second = small[:, piece : 2 * piece].reshape(1, width).astype(f32)
        bias_of = lambda lo, n: (
            small[:, lo : lo + n * (HD // n_f)]
            .reshape(n_f, n, HD // n_f)
            .transpose(1, 0, 2)
            .reshape(n, HD)
            .astype(f32)
        )
        at = 2 * piece
        bq = bias_of(at, heads)
        bk = bias_of(at + heads * (HD // n_f), KV)
        bv = bias_of(at + (heads + KV) * (HD // n_f), KV)
        b_kv = lax.dynamic_index_in_dim(jnp.where(core == 0, bk, bv), group, 0)

        unit_slice = lambda w: lax.dynamic_slice_in_dim(w, parity * units, units, 0)
        own_gate_up = jnp.concatenate(
            [unit_slice(after(w, w_kv_own)) for w in (w_gate.T, w_up.T)], axis=0
        )
        own_down = unit_slice(w_down)

        dy_part = lax.dynamic_slice_in_dim(cotangent, t * part, part, 0)

        seq_blocks = blocks[0].reshape(n_c, -1)
        own_blocks = seq_blocks.shape[1]
        key_blocks = jnp.concatenate(
            [lax.dynamic_index_in_dim(seq_blocks, c ^ j, 0, keepdims=False) for j in range(n_c)]
        )
        positions = (
            key_blocks[:own_blocks, None] * BLOCK + jnp.arange(BLOCK, dtype=jnp.int32)[None, :]
        ).reshape(-1)
        cosine, sine = rope_tables(positions)
        bias = jnp.concatenate([bq.reshape(1, -1), b_kv], axis=1)
        dy_blocks = [
            dy_part,
            flip(dy_part, "tensor", 2),
            flip(dy_part, "context", 1),
            flip(dy_part, "context", 2),
        ]
        inputs_part = lax.dynamic_slice_in_dim(inputs, t * part, part, 0)
        bias = after(bias, dy_blocks[2:], own_gate_up, own_down, inputs_part)
        normed, factor_first, queries, kv_own = qkv(
            meta, inputs, gain_first, bias, cosine, sine, w_q, w_kv
        )
        far_gate_up = pieces_f(after(own_gate_up, kv_own, w_out_all), 1)[-1]
        w_gate_up = [own_gate_up, far_gate_up] if n_f == 2 else [far_gate_up]
        kv = kv_gather(after(kv_own, w_out_all))
        far_down = pieces_f(after(own_down, kv), 1)[-1]
        w_downs = [own_down, far_down] if n_f == 2 else [far_down]
        attended, lse = attention(key_blocks, queries, kv)
        middle, factor_second, normed2, dy_all = middle_norm(
            dot(attended, w_out_all).astype(bf16), inputs_part, gain_second, dy_blocks
        )

        hidden, slope, gated, *down_far = hidden_units(meta, normed2, dy_all, w_gate_up)
        grad_gate, grad_up, dx_part, out_part, *unit_far = hidden_back(
            meta, normed2, dy_all, hidden, slope, gated, w_gate_up, w_downs
        )
        unit_far = [*down_far, *unit_far]
        flat = lambda x: x.reshape(-1, width)
        if n_f == 2:
            down_got, gate_got, up_got = (flip(x, "fsdp", 1) for x in unit_far)
            early = [(hidden, flat(dy_all)), (grad_gate, flat(normed2))]
            later = [(grad_up, flat(normed2))]
        else:
            over_f = lambda x: lax.psum_scatter(x, "fsdp", scatter_dimension=1, tiled=True)
            owns = [
                over_f(unit_grads(meta, 0, 1, x, [unit]))
                for x, unit in ((dy_all, hidden), (normed2, grad_gate), (normed2, grad_up))
            ]
            down_got = gate_got = up_got = jnp.zeros_like(owns[0])
            early = later = []

        unit_whole = lambda low, *other: by_bit(
            parity, low, jnp.concatenate(other, axis=0), 0
        ).astype(f32)

        grad_middle, ffn_gain_grad, grad_middle_low, *first_owns = middle_back(
            dx_part, middle, factor_second, gain_second, dy_part, early, down_got, width // n_f
        )
        grad_middle_low = grad_middle_low.reshape(rows, width)
        add = lambda own, got: (own.astype(f32) + got.astype(f32)).astype(bf16)
        upper = units // 2
        if n_f == 2:
            _, gate_own, down_low, down_upper = first_owns
        else:
            down_low, gate_own = owns[:2]
            down_upper = flip(down_low[:upper], "context", 1)
        gate_low = add(gate_own, after(gate_got, grad_middle_low))
        down_lower = flip(down_low[upper:], "context", 1)
        gate_upper = flip(after(gate_low[:upper], down_low), "context", 1)
        grad_middle_low = after(grad_middle_low, gate_low)
        grad_attended = dot_cols(grad_middle_low, w_out_all).astype(bf16)

        dq_low, dkv = attention_back(key_blocks, queries, grad_attended, lse, cosine, sine, kv)
        attention_args = [(attended, after(grad_middle_low, dq_low), 1), (normed, dq_low, 0)]
        fars = [grad_far(*args) for args in attention_args]
        dkv, *last_owns = kv_scatter(
            after(dkv, fars, down_lower, gate_upper), later, width // n_f
        )
        (up_own,) = last_owns or owns[2:]
        gate_lower = flip(after(gate_low[upper:], dkv, gate_upper), "context", 1)
        up_low = add(up_own, after(up_got, dkv))
        dkv = after(dkv, up_low, gate_upper)
        dkv_low = jnp.where(core == 0, rotate_back(dkv, cosine, sine), dkv).astype(bf16)
        attention_args.append((normed, dkv_low, 0))
        fars.append(grad_far(*attention_args[-1]))
        dkv_low = after(dkv_low, fars)
        factor_part = lax.dynamic_slice_in_dim(factor_first, t * part, part, 0)
        own_biases = jnp.sum(
            jnp.concatenate([dq_low, dkv_low], axis=1).astype(f32), axis=0, keepdims=True
        )
        slots = lax.dynamic_update_slice(
            jnp.zeros((n_t, (heads + 1) * HD), f32), own_biases, (t, 0)
        )
        small_grads = jnp.concatenate(
            [jnp.zeros((1, width), f32), ffn_gain_grad, slots.reshape(1, -1)], axis=1
        )
        grad_qkv = qkv_back(meta, dq_low, dkv_low, w_q, w_kv)
        up_upper = flip(after(up_low[:upper], dkv_low), "context", 1)
        up_lower = flip(after(up_low[upper:], grad_qkv), "context", 1)
        small_grads, input_grad = input_back(
            grad_qkv,
            inputs_part,
            factor_part,
            gain_first,
            grad_middle,
            small_grads,
        )
        input_grad = input_grad.reshape(rows, width)
        if n_f > 2:
            small_grads = lax.psum(small_grads, "fsdp")
        small_grads = after(small_grads, gate_lower, up_upper)
        attention_parts = [
            grad_sum(*args, far, small_grads) for args, far in zip(attention_args, fars)
        ]
        wd_grad = unit_whole(*after((down_low, down_upper, down_lower), small_grads))
        wg_grad = unit_whole(*after((gate_low, gate_upper, gate_lower), small_grads))
        small_grads, up_lower, wg_grad, wd_grad = lax.optimization_barrier(
            (small_grads, up_lower, wg_grad, wd_grad)
        )
        wo_grad, wq_grad, packed, wkv_all, outputs = context_sum(
            n_f == 2, attention_parts, small_grads, out_part, middle
        )
        outputs = outputs.reshape(rows, width)
        wkv_all = wkv_all.astype(f32)
        wk_grad = jnp.concatenate([wkv_all[0], wkv_all[2]], axis=1)
        wv_grad = jnp.concatenate([wkv_all[1], wkv_all[3]], axis=1)
        packed = packed[0]
        attn_gain_grad = lax.dynamic_slice_in_dim(packed, f * piece, piece, 0)
        ffn_gain_grad = lax.dynamic_slice_in_dim(packed, width + f * piece, piece, 0)
        slots = packed[2 * width :].reshape(n_t, heads + 1, HD)
        slots = lax.dynamic_slice_in_dim(slots, f * (HD // n_f), HD // n_f, 2)
        bq_out = lax.dynamic_index_in_dim(slots, t, 0, keepdims=False)[:heads]
        bk_out = slots[0::2, heads]
        bv_out = slots[1::2, heads]

        wu_grad = unit_whole(up_low, up_upper, up_lower)
        wg_grad, wu_grad = wg_grad.T, wu_grad.T

        return (
            outputs,
            input_grad,
            attn_gain_grad,
            wq_grad,
            bq_out,
            wk_grad,
            bk_out,
            wv_grad,
            bv_out,
            wo_grad,
            ffn_gain_grad,
            wg_grad,
            wu_grad,
            wd_grad,
        )

    return local


def solution(mesh):
    in_specs = (
        P(("fsdp", "context"), None),
        P(("fsdp", "context"), None),
        P("fsdp", None),
        P("fsdp"),
        P("fsdp", "tensor"),
        P("tensor", "fsdp"),
        P("fsdp", None),
        P(None, "fsdp"),
        P("fsdp", None),
        P(None, "fsdp"),
        P("tensor", "fsdp"),
        P("fsdp"),
        P("fsdp", "tensor"),
        P("fsdp", "tensor"),
        P("tensor", "fsdp"),
    )
    out_specs = (
        P(("fsdp", "context"), None),
        P(("fsdp", "context"), None),
        P("fsdp"),
        P("fsdp", "tensor"),
        P("tensor", "fsdp"),
        P("fsdp", None),
        P(None, "fsdp"),
        P("fsdp", None),
        P(None, "fsdp"),
        P("tensor", "fsdp"),
        P("fsdp"),
        P("fsdp", "tensor"),
        P("fsdp", "tensor"),
        P("tensor", "fsdp"),
    )
    local = build(mesh.shape["fsdp"], mesh.shape["context"], mesh.shape["tensor"])
    return jax.shard_map(local, mesh=mesh, in_specs=in_specs, out_specs=out_specs, check_vma=False)
```

```python
import functools

import jax
import jax.numpy as jnp
from jax import lax
from jax.experimental import pallas as pl
from jax.experimental.pallas import tpu as pltpu
from jax.sharding import PartitionSpec as P

H = 12
KV = 2
HD = 128
BLOCK = 256

EPSILON = 1e-06
ROPE_BASE = 1000000.0
MASKED = -1e30
SCALING = HD ** (-0.5)
LANES = 128
VMEM_LIMIT = 60 << 20

f32 = jnp.float32
bf16 = jnp.bfloat16


def rope_tables(positions):
    halfway = HD // 2
    frequency = ROPE_BASE ** (-(jnp.arange(halfway, dtype=f32) * 2.0 / HD))
    angles = positions.astype(f32)[:, None] * frequency[None, :]
    cosine, sine = jnp.cos(angles), jnp.sin(angles)
    return (jnp.concatenate([cosine, cosine], axis=1), jnp.concatenate([sine, sine], axis=1))


def rotate(field, cosine, sine):
    halfway = HD // 2
    turned = jnp.concatenate([-field[..., halfway:], field[..., :halfway]], axis=-1)
    return field * cosine + turned * sine


def rotate_back(grad_field, cosine, sine):
    halfway = HD // 2
    moved = grad_field * sine
    turned = jnp.concatenate([moved[..., halfway:], -moved[..., :halfway]], axis=-1)
    return grad_field * cosine + turned


def dot(left, right):
    return jnp.dot(left, right, preferred_element_type=f32)


def dot_rows(left, right):
    return lax.dot_general(left, right, (((0,), (0,)), ((), ())), preferred_element_type=f32)


def dot_cols(left, right):
    return lax.dot_general(left, right, (((1,), (1,)), ((), ())), preferred_element_type=f32)


def mask_row(kb_ref, own_block, key_blocks):
    return jnp.concatenate(
        [
            jnp.full((1, BLOCK), jnp.where(kb_ref[j] <= own_block, 0.0, MASKED), f32)
            for j in range(key_blocks)
        ],
        axis=1,
    )


def attention_kernel(key_blocks, kb_ref, q_ref, k_ref, v_ref, o_ref, lse_ref):
    bias = mask_row(kb_ref, kb_ref[pl.program_id(1)], key_blocks)
    scores = dot_cols(q_ref[...], k_ref[...]) * SCALING + bias
    row_max = jnp.max(scores, axis=1, keepdims=True)
    expo = jnp.exp(scores - row_max)
    total = jnp.sum(expo, axis=1, keepdims=True)
    probability = (expo * (1.0 / total)).astype(bf16)
    o_ref[...] = dot(probability, v_ref[...]).astype(bf16)
    lse_ref[0] = row_max + jnp.log(total)


def attention(key_blocks, queries, kv):
    rows, width = queries.shape
    heads = width // HD
    whole = lambda kind: pl.BlockSpec((None,) + kv.shape[1:], lambda h, i, kb: (kind, 0, 0))
    tile = pl.BlockSpec((BLOCK, HD), lambda h, i, kb: (i, h))
    return pl.pallas_call(
        functools.partial(attention_kernel, kv.shape[1] // BLOCK),
        name="attention",
        grid_spec=pltpu.PrefetchScalarGridSpec(
            num_scalar_prefetch=1,
            grid=(heads, rows // BLOCK),
            in_specs=[tile, whole(0), whole(1)],
            out_specs=[tile, pl.BlockSpec((1, BLOCK, 1), lambda h, i, kb: (h, i, 0))],
        ),
        out_shape=[
            jax.ShapeDtypeStruct((rows, width), bf16),
            jax.ShapeDtypeStruct((heads, rows, 1), f32),
        ],
        compiler_params=pltpu.CompilerParams(vmem_limit_bytes=VMEM_LIMIT),
    )(key_blocks, queries, kv, kv)


def attention_back_kernel(
    key_blocks,
    kb_ref,
    q_ref,
    do_ref,
    lse_ref,
    cos_ref,
    sin_ref,
    k_ref,
    v_ref,
    dq_ref,
    dkv_ref,
    dk_ref,
    dv_ref,
):
    head, i = pl.program_id(0), pl.program_id(1)

    @pl.when((head == 0) & (i == 0))
    def _():
        dk_ref[...] = jnp.zeros_like(dk_ref)
        dv_ref[...] = jnp.zeros_like(dv_ref)

    bias = mask_row(kb_ref, kb_ref[i], key_blocks)
    scores = dot_cols(q_ref[...], k_ref[...]) * SCALING + bias
    probability = jnp.exp(scores - lse_ref[0])
    grad_probs = dot_cols(do_ref[...], v_ref[...])
    inner = jnp.sum(probability * grad_probs, axis=1, keepdims=True)
    grad_scores = (probability * (grad_probs - inner)).astype(bf16)
    grad_query = dot(grad_scores, k_ref[...]) * SCALING
    moved = grad_query * sin_ref[...]
    sign = jnp.where(lax.broadcasted_iota(jnp.int32, moved.shape, 1) < HD // 2, 1.0, -1.0)
    dq_ref[...] = (
        grad_query * cos_ref[...] + pltpu.roll(moved, HD // 2, 1) * sign
    ).astype(bf16)
    dk_ref[...] += dot_rows(grad_scores, q_ref[...]) * SCALING
    dv_ref[...] += dot_rows(probability.astype(bf16), do_ref[...])

    @pl.when((head == pl.num_programs(0) - 1) & (i == pl.num_programs(1) - 1))
    def _():
        dkv_ref[0] = dk_ref[...].astype(bf16)
        dkv_ref[1] = dv_ref[...].astype(bf16)


def attention_back(key_blocks, queries, grad_out, lse, cosine, sine, kv):
    rows, width = queries.shape
    heads = width // HD
    whole = lambda kind: pl.BlockSpec((None,) + kv.shape[1:], lambda h, i, kb: (kind, 0, 0))
    tile = pl.BlockSpec((BLOCK, HD), lambda h, i, kb: (i, h))
    table = pl.BlockSpec((BLOCK, HD), lambda h, i, kb: (i, 0))
    return pl.pallas_call(
        functools.partial(attention_back_kernel, kv.shape[1] // BLOCK),
        name="attention_back",
        grid_spec=pltpu.PrefetchScalarGridSpec(
            num_scalar_prefetch=1,
            grid=(heads, rows // BLOCK),
            in_specs=[
                tile,
                tile,
                pl.BlockSpec((1, BLOCK, 1), lambda h, i, kb: (h, i, 0)),
                table,
                table,
                whole(0),
                whole(1),
            ],
            out_specs=[tile, pl.BlockSpec(kv.shape, lambda h, i, kb: (0, 0, 0))],
            scratch_shapes=[pltpu.VMEM(kv.shape[1:], f32)] * 2,
        ),
        out_shape=[
            jax.ShapeDtypeStruct((rows, width), bf16),
            jax.ShapeDtypeStruct(kv.shape, bf16),
        ],
        compiler_params=pltpu.CompilerParams(vmem_limit_bytes=VMEM_LIMIT),
    )(key_blocks, queries, grad_out, lse, cosine, sine, kv, kv)


def qkv_kernel(pieces, meta_ref, x_ref, gain_ref, bias_ref, cos_ref, sin_ref, *refs):
    weights, (xn_ref, factor_ref, q_ref, kv_ref) = refs[: 2 * pieces], refs[2 * pieces :]
    values = x_ref[...].astype(f32)
    factor = lax.rsqrt(jnp.mean(values * values, axis=-1, keepdims=True) + EPSILON)
    factor_ref[...] = factor
    xn_ref[...] = (values * factor * gain_ref[...]).astype(bf16)
    depth = weights[0].shape[0]
    normed = [xn_ref[:, columns_of(meta_ref, j, depth, pieces)] for j in range(pieces)]
    cosine, sine = cos_ref[...], sin_ref[...]
    sign = jnp.where(lax.broadcasted_iota(jnp.int32, cosine.shape, 1) < HD // 2, -1.0, 1.0)
    sine = sine * sign
    width = q_ref.shape[1]
    total = bias_ref[:, :width] + sum(dot(x, w[...]) for x, w in zip(normed, weights[:pieces]))
    turn = lambda own: own * cosine + pltpu.roll(own, HD // 2, 1) * sine
    for h in range(width // HD):
        q_ref[:, h * HD : (h + 1) * HD] = turn(total[:, h * HD : (h + 1) * HD]).astype(bf16)
    own = bias_ref[:, width:] + sum(dot(x, w[...]) for x, w in zip(normed, weights[pieces:]))
    kv_ref[...] = jnp.where(meta_ref[2] == 0, turn(own), own).astype(bf16)


def columns_of(meta_ref, j, depth, pieces):
    if pieces == 1:
        return slice(None)
    return pl.ds(pl.multiple_of(meta_ref[j] * depth, LANES), depth)


def qkv(meta, inputs, gain, bias, cosine, sine, w_q, w_kv):
    rows, width = inputs.shape
    out = w_q[0].shape[1]
    tile = 256
    row = lambda n: pl.BlockSpec((tile, n), lambda i, m: (i, 0))
    fixed = lambda w: pl.BlockSpec(w.shape, lambda i, m: (0, 0))
    return pl.pallas_call(
        functools.partial(qkv_kernel, len(w_q)),
        name="qkv",
        grid_spec=pltpu.PrefetchScalarGridSpec(
            num_scalar_prefetch=1,
            grid=(rows // tile,),
            in_specs=[row(width), fixed(gain), fixed(bias), row(HD), row(HD)]
            + [fixed(w) for w in (*w_q, *w_kv)],
            out_specs=[row(width), row(1), row(out), row(HD)],
        ),
        out_shape=[
            jax.ShapeDtypeStruct((rows, width), bf16),
            jax.ShapeDtypeStruct((rows, 1), f32),
            jax.ShapeDtypeStruct((rows, out), bf16),
            jax.ShapeDtypeStruct((rows, HD), bf16),
        ],
        compiler_params=pltpu.CompilerParams(vmem_limit_bytes=VMEM_LIMIT),
    )(meta, inputs, gain, bias, cosine, sine, *w_q, *w_kv)


def qkv_back_kernel(pieces, meta_ref, dq_ref, dkv_ref, *refs):
    w_q, w_kv, out_ref = refs[:pieces], refs[pieces : 2 * pieces], refs[-1]
    for j in range(pieces):
        out_ref[:, columns_of(meta_ref, j, w_q[j].shape[0], pieces)] = (
            dot_cols(dq_ref[...], w_q[j][...]) + dot_cols(dkv_ref[...], w_kv[j][...])
        ).astype(bf16)


def qkv_back(meta, grad_q, grad_kv, w_q, w_kv):
    rows, width = grad_q.shape[0], sum(w.shape[0] for w in w_q)
    tile = 256
    row = lambda n: pl.BlockSpec((tile, n), lambda i, m: (i, 0))
    fixed = lambda w: pl.BlockSpec(w.shape, lambda i, m: (0, 0))
    return pl.pallas_call(
        functools.partial(qkv_back_kernel, len(w_q)),
        name="qkv_back",
        grid_spec=pltpu.PrefetchScalarGridSpec(
            num_scalar_prefetch=1,
            grid=(rows // tile,),
            in_specs=[row(grad_q.shape[1]), row(HD)] + [fixed(w) for w in (*w_q, *w_kv)],
            out_specs=row(width),
        ),
        out_shape=jax.ShapeDtypeStruct((rows, width), bf16),
        compiler_params=pltpu.CompilerParams(vmem_limit_bytes=VMEM_LIMIT),
    )(meta, grad_q, grad_kv, *w_q, *w_kv)


def add_rows(unit_refs, row_refs, columns, totals, outs):
    step = pl.program_id(0)

    @pl.when(step == 0)
    def _():
        for total in totals:
            total[...] = jnp.zeros_like(total)

    for total, unit, row in zip(totals, unit_refs, row_refs):
        total[...] += dot_rows(unit[...], row[:, columns])

    @pl.when(step == pl.num_programs(0) - 1)
    def _():
        for out, total in zip(outs, totals):
            out[...] = total[...].astype(bf16)


def hidden_kernel(pieces, meta_ref, x_ref, dy_ref, *refs):
    wg, wu, refs = refs[:pieces], refs[pieces : 2 * pieces], refs[2 * pieces :]
    hid_ref, slope_ref, gated_ref = refs[:3]
    columns = [columns_of(meta_ref, j, wg[j].shape[1], pieces) for j in range(pieces)]
    gate = sum(dot_cols(x_ref[:, at], w[...]) for at, w in zip(columns, wg))
    up = sum(dot_cols(x_ref[:, at], w[...]) for at, w in zip(columns, wu))
    sigma = 1.0 / (1.0 + jnp.exp(-gate))
    gated = gate * sigma
    hid_ref[...] = (gated * up).astype(bf16)
    slope_ref[...] = (up * (sigma + gated * (1.0 - sigma))).astype(bf16)
    gated_ref[...] = gated.astype(bf16)
    if pieces == 2:
        add_rows([hid_ref], [dy_ref], columns[1], refs[4:], refs[3:4])


def hidden_back_kernel(pieces, meta_ref, x_ref, dy_ref, hid_ref, slope_ref, gated_ref, *refs):
    wg, wu, wd = (refs[m * pieces : (m + 1) * pieces] for m in range(3))
    refs = refs[3 * pieces :]
    dg_ref, du_ref, dx_ref, out_ref = refs[:4]
    columns = [columns_of(meta_ref, j, wg[j].shape[1], pieces) for j in range(pieces)]
    grad_hidden = sum(dot_cols(dy_ref[:, at], w[...]) for at, w in zip(columns, wd))
    dg_ref[...] = (grad_hidden * slope_ref[...].astype(f32)).astype(bf16)
    du_ref[...] = (grad_hidden * gated_ref[...].astype(f32)).astype(bf16)

    @pl.when(pl.program_id(0) // (pl.num_programs(0) // 2) == meta_ref[3])
    def _():
        for at, g, u, d in zip(columns, wg, wu, wd):
            dx_ref[:, at] = (dot(dg_ref[...], g[...]) + dot(du_ref[...], u[...])).astype(bf16)
            out_ref[:, at] = dot(hid_ref[...], d[...]).astype(bf16)

    if pieces == 2:
        add_rows([dg_ref, du_ref], [x_ref, x_ref], columns[1], refs[6:], refs[4:6])


def hidden_specs(meta, normed, weights):
    width = normed.shape[-1]
    rows = normed.shape[0] * normed.shape[1]
    units, depth = weights[0].shape[0] // 2, weights[0].shape[1]
    tile = 512
    steps = rows // tile
    half = steps // 2
    once = pl.Buffered(1)
    inside = lambda i, m: jnp.clip(i - m[3] * half, 0, half - 1)
    return {
        "steps": steps,
        "flat": lambda x: x.reshape(-1, width),
        "row": pl.BlockSpec((tile, width), lambda i, m: (lax.rem(i + m[3] * half, steps), 0)),
        "unit": pl.BlockSpec((tile, units), lambda i, m: (i, 0)),
        "near_unit": pl.BlockSpec((tile, units), lambda i, m: (inside(i, m) + m[3] * half, 0)),
        "near_row": pl.BlockSpec((tile, width), lambda i, m: (inside(i, m), 0)),
        "weight": lambda k: pl.BlockSpec((units, depth), lambda i, m: (k, 0), pipeline_mode=once),
        "grad": pl.BlockSpec((units, depth), lambda i, m: (0, 0), pipeline_mode=once),
        "unit_shape": jax.ShapeDtypeStruct((rows, units), bf16),
        "near_shape": jax.ShapeDtypeStruct((rows // 2, width), bf16),
        "grad_shape": jax.ShapeDtypeStruct((units, depth), bf16),
        "total": pltpu.VMEM((units, depth), f32),
    }


def hidden_call(kernel, name, meta, args, in_specs, outs, grads, specs):
    return pl.pallas_call(
        kernel,
        name=name,
        grid_spec=pltpu.PrefetchScalarGridSpec(
            num_scalar_prefetch=1,
            grid=(specs["steps"],),
            in_specs=in_specs,
            out_specs=[specs[x] for x in outs] + [specs["grad"]] * grads,
            scratch_shapes=[specs["total"]] * grads,
        ),
        out_shape=[specs[x.split("_")[0] + "_shape"] for x in outs]
        + [specs["grad_shape"]] * grads,
        compiler_params=pltpu.CompilerParams(vmem_limit_bytes=VMEM_LIMIT),
    )(meta, *args)


def hidden_units(meta, normed, grad_out, weights):
    specs, pieces = hidden_specs(meta, normed, weights), len(weights)
    return hidden_call(
        functools.partial(hidden_kernel, pieces),
        "hidden_units",
        meta,
        [specs["flat"](normed), specs["flat"](grad_out)] + list(weights) * 2,
        [specs["row"]] * 2 + [specs["weight"](k) for k in range(2) for _ in weights],
        ["unit"] * 3,
        pieces == 2,
        specs,
    )


def hidden_back(meta, normed, grad_out, hidden, slope, gated, weights, down_weights):
    specs, pieces = hidden_specs(meta, normed, weights), len(weights)
    return hidden_call(
        functools.partial(hidden_back_kernel, pieces),
        "hidden_back",
        meta,
        [specs["flat"](normed), specs["flat"](grad_out), hidden, slope, gated]
        + list(weights) * 2
        + list(down_weights),
        [specs["row"]] * 2
        + [specs["near_unit"], specs["unit"], specs["unit"]]
        + [specs["weight"](k) for k in (0, 1, 0) for _ in weights],
        ["unit", "unit", "near_row", "near_row"],
        2 * (pieces == 2),
        specs,
    )


def unit_grads_kernel(count, meta_ref, near_ref, far_ref, *refs):
    units, out_ref, x_ref = refs[:count], refs[-2], refs[-1]
    half = near_ref.shape[0]
    x_ref[pl.ds(pl.multiple_of(meta_ref[3] * half, half), half)] = near_ref[...]
    x_ref[pl.ds(pl.multiple_of((1 - meta_ref[3]) * half, half), half)] = far_ref[...]
    for k, unit in enumerate(units):
        depth = unit.shape[1]
        out_ref[k * depth : (k + 1) * depth] = dot_rows(unit[...], x_ref[...]).astype(bf16)


def unit_grads(meta, which, pieces, x, units_of):
    width = x.shape[-1]
    count, (rows, units) = len(units_of), units_of[0].shape
    depth = width // pieces
    tile = 256
    steps = depth // tile
    shard = (lambda m: m[which]) if pieces > 1 else (lambda m: 0)
    feature = lambda half: pl.BlockSpec(
        (rows // 2, tile), lambda i, m: (half, shard(m) * steps + i)
    )
    unit = pl.BlockSpec((rows, units), lambda i, m: (0, 0), pipeline_mode=pl.Buffered(1))
    x = x.reshape(-1, width)
    return pl.pallas_call(
        functools.partial(unit_grads_kernel, count),
        name=f"unit_grads_{which}_{count}",
        grid_spec=pltpu.PrefetchScalarGridSpec(
            num_scalar_prefetch=1,
            grid=(steps,),
            in_specs=[feature(0), feature(1)] + [unit] * count,
            out_specs=pl.BlockSpec((count * units, tile), lambda i, m: (0, i)),
            scratch_shapes=[pltpu.VMEM((rows, tile), bf16)],
        ),
        out_shape=jax.ShapeDtypeStruct((count * units, depth), bf16),
        compiler_params=pltpu.CompilerParams(vmem_limit_bytes=VMEM_LIMIT),
    )(meta, x, x, *units_of)


class Wires:
    def __init__(self, sends, receives, locals_):
        self.sends, self.receives, self.locals = sends, receives, locals_
        self.used = self.used_local = 0
        self.started = []

    def plan(self, source, target, device):
        k = self.used
        self.used += 1
        return pltpu.make_async_remote_copy(
            source,
            target,
            self.sends.at[k],
            self.receives.at[k],
            device_id=device,
            device_id_type=pl.DeviceIdType.MESH,
        )

    def copy(self, source, target, device):
        one = self.plan(source, target, device)
        one.start()
        self.started.append(one)
        return one

    def here(self, source, target):
        k = self.used_local
        self.used_local += 1
        one = pltpu.make_async_copy(source, target, self.locals.at[k])
        one.start()
        return one

    def finish(self):
        for one in self.started:
            one.wait_send()


class OwnGrad:
    TILE = 256

    def __init__(self, units, rows, out, units_here, rows_here):
        self.units, self.rows, self.out = units, rows, out
        self.units_here, self.rows_here = units_here, rows_here
        self.tiles = out.shape[1] // self.TILE
        self.copies = None

    def fetch(self, wires):
        half, depth = self.rows.shape[0] // 2, self.out.shape[1]
        column = pl.multiple_of(lax.axis_index("fsdp") * depth, LANES)
        pair = lax.axis_index("context") // 2
        self.copies = [wires.here(self.units, self.units_here)]
        for k, place in ((0, pair), (1, 1 - pair)):
            self.copies.append(
                wires.here(
                    self.rows.at[pl.ds(k * half, half), pl.ds(column, depth)],
                    self.rows_here.at[pl.ds(pl.multiple_of(place * half, half), half)],
                )
            )

    def make(self, first, past):
        for one in self.copies:
            one.wait()
        self.copies = []

        @pl.loop(first, past)
        def _(k):
            at = pl.ds(pl.multiple_of(k * self.TILE, self.TILE), self.TILE)
            self.out[:, at] = dot_rows(self.units_here[...], self.rows_here[:, at]).astype(bf16)


def own_grad_call(fill, width):
    args = [x for pair in fill for x in pair]
    outs = [jax.ShapeDtypeStruct((units.shape[1], width), bf16) for units, _ in fill]
    scratch = []
    for units, rows in fill:
        scratch += [pltpu.VMEM(units.shape, bf16), pltpu.VMEM((rows.shape[0], width), bf16)]
    return args, outs, scratch


def own_grads(count, args, outs, scratch):
    return [
        OwnGrad(args[2 * k], args[2 * k + 1], outs[k], scratch[2 * k], scratch[2 * k + 1])
        for k in range(count)
    ]


def meet(devices):
    barrier = pltpu.get_barrier_semaphore()
    for device in devices:
        pl.semaphore_signal(barrier, inc=1, device_id=device, device_id_type=pl.DeviceIdType.MESH)
    pl.semaphore_wait(barrier, len(devices))


def partners():
    c, t = lax.axis_index("context"), lax.axis_index("tensor")
    flip = lambda x, bit: x + bit * (1 - 2 * lax.rem(x // bit, 2))
    return {
        "core": {"tensor": flip(t, 1)},
        "y": {"tensor": flip(t, 2)},
        "z": {"context": flip(c, 1)},
        "far": {"context": flip(c, 2)},
        "last": {"context": flip(flip(c, 1), 2)},
    }


def wide(x):
    return x.astype(f32)


def ranks():
    t = lax.axis_index("tensor")
    flip = lambda x, bit: x + bit * (1 - 2 * lax.rem(x // bit, 2))
    return (t, flip(t, 1), flip(t, 2), flip(flip(t, 1), 2))


def scatter_rank(wires, to, part, own, got_core, sent, got_y):
    size = part.shape[1] // 2
    halves = [pl.ds(0, size), pl.ds(size, size)]
    rank = ranks()
    from_core = {}
    for block in (1, 0):
        for k, at in enumerate(halves):
            from_core[block, k] = wires.copy(
                part.at[rank[1 + 2 * block], at], got_core.at[block, at], to["core"]
            )
    mine = [wires.here(part.at[rank[2 * block]], own.at[block]) for block in (0, 1)]
    yield
    for one in mine:
        one.wait()
    from_y = []
    for k, at in enumerate(halves):
        from_core[1, k].wait_recv()
        sent[at] = (wide(own[1, at]) + wide(got_core[1, at])).astype(bf16)
        from_y.append(wires.copy(sent.at[at], got_y.at[at], to["y"]))
    yield
    for k in range(2):
        from_core[0, k].wait_recv()
    total = wide(own[0]) + wide(got_core[0])
    for one in from_y:
        one.wait_recv()
    return total + wide(got_y[...])


def scatter_pair(wires, to, part, own, got_core, sent, got_y, got_z, diag_y, diag_z):
    size = part.shape[1] // 2
    low, high = pl.ds(0, size), pl.ds(size, size)
    from_core = {j: wires.copy(part.at[4 + j], got_core.at[j], to["core"]) for j in (3, 1, 2, 0)}
    mine = wires.here(part.at[pl.ds(0, 4)], own)
    yield
    mine.wait()
    both = lambda j, at: wide(own[j, at]) + wide(got_core[j, at])
    from_core[3].wait_recv()
    sent[2] = (wide(own[3]) + wide(got_core[3])).astype(bf16)
    via_z = wires.copy(sent.at[2, low], diag_z, to["z"])
    via_y = wires.copy(sent.at[2, high], diag_y, to["y"])
    from_core[1].wait_recv()
    sent[0, high] = both(1, high).astype(bf16)
    y_high = wires.copy(sent.at[0, high], got_y.at[high], to["y"])
    from_core[2].wait_recv()
    sent[1, low] = both(2, low).astype(bf16)
    z_low = wires.copy(sent.at[1, low], got_z.at[low], to["z"])
    yield
    via_z.wait_recv()
    sent[0, low] = (both(1, low) + wide(diag_z[...])).astype(bf16)
    y_low = wires.copy(sent.at[0, low], got_y.at[low], to["y"])
    via_y.wait_recv()
    sent[1, high] = (both(2, high) + wide(diag_y[...])).astype(bf16)
    z_high = wires.copy(sent.at[1, high], got_z.at[high], to["z"])
    yield
    from_core[0].wait_recv()
    total = wide(own[0]) + wide(got_core[0])
    for one in (y_high, z_low, y_low, z_high):
        one.wait_recv()
    return total + wide(got_y[...]) + wide(got_z[...])


def result_of(steps):
    while True:
        try:
            next(steps)
        except StopIteration as done:
            return done.value


def gather_rank(wires, to, block, out):
    size = block.shape[0] // 2
    halves = [pl.ds(0, size), pl.ds(size, size)]
    rank = ranks()
    mine = wires.here(block, out.at[rank[0]])
    from_y = [wires.copy(block.at[h], out.at[rank[0], h], to["y"]) for h in halves]
    from_core = [wires.copy(block, out.at[rank[0]], to["core"])]
    yield
    for h, one in zip(halves, from_y):
        one.wait_recv()
        from_core.append(wires.copy(out.at[rank[2], h], out.at[rank[2], h], to["core"]))
    for one in from_core:
        one.wait_recv()
    mine.wait()


def gather_pair(wires, to, block, out, base):
    size = block.shape[0] // 2
    low, high = pl.ds(0, size), pl.ds(size, size)
    at = lambda j: out.at[base + j]
    from_z = wires.copy(block, at(2), to["z"])
    yield
    from_y = wires.copy(block, at(1), to["y"])
    from_core = [wires.copy(block, at(4), to["core"])]
    yield
    from_y.wait_recv()
    via_z = wires.copy(out.at[base + 1, low], out.at[base + 3, low], to["z"])
    from_core.append(wires.copy(at(1), at(5), to["core"]))
    from_z.wait_recv()
    via_y = wires.copy(out.at[base + 2, high], out.at[base + 3, high], to["y"])
    from_core.append(wires.copy(at(2), at(6), to["core"]))
    yield
    via_z.wait_recv()
    via_y.wait_recv()
    from_core.append(wires.copy(at(3), at(7), to["core"]))
    return from_core


def remote_call(kernel, name, key, args, outs, scratch, copies, in_vmem):
    ins, out_in = in_vmem
    spec = lambda inside: pl.BlockSpec(memory_space=pltpu.VMEM if inside else pl.ANY)
    return pl.pallas_call(
        kernel,
        name=name,
        out_shape=outs,
        in_specs=[spec(x) for x in ins],
        out_specs=[spec(x) for x in out_in],
        scratch_shapes=list(scratch)
        + [
            pltpu.SemaphoreType.DMA((copies,)),
            pltpu.SemaphoreType.DMA((copies,)),
            pltpu.SemaphoreType.DMA((8,)),
        ],
        compiler_params=pltpu.CompilerParams(
            collective_id=key, has_side_effects=True, vmem_limit_bytes=VMEM_LIMIT
        ),
    )(*args)


def kv_gather_kernel(own_ref, out_ref, *sems):
    wires, to = Wires(*sems), partners()
    kind = lax.rem(lax.axis_index("tensor"), 2)
    rows = own_ref.shape[0]
    block = lambda j: out_ref.at[kind, pl.ds(j * rows, rows)]
    meet([to[k] for k in ("core", "z", "far", "last")])
    mine = wires.here(own_ref, block(0))
    arrive = [wires.copy(own_ref, block(j), to[k]) for j, k in ((3, "last"), (2, "far"), (1, "z"))]
    from_core = [wires.copy(own_ref, block(0), to["core"])]
    for j, one in ((1, arrive[2]), (2, arrive[1]), (3, arrive[0])):
        one.wait_recv()
        from_core.append(wires.copy(block(j), block(j), to["core"]))
    for one in from_core:
        one.wait_recv()
    mine.wait()
    wires.finish()


def kv_gather(own):
    rows, width = own.shape
    n_c = lax.axis_size("context")
    return remote_call(
        kv_gather_kernel,
        "kv_gather",
        0,
        [own],
        [jax.ShapeDtypeStruct((2, n_c * rows, width), bf16)],
        [],
        8,
        ([False], [False]),
    )[0]


def kv_scatter_kernel(count, part_ref, *refs):
    args, dkv_ref, outs = refs[: 2 * count], refs[2 * count], refs[2 * count + 1 : 3 * count + 1]
    own, got_core, sent, got = refs[3 * count + 1 : 3 * count + 5]
    wires, to = Wires(*refs[-3:]), partners()
    fill = own_grads(count, args, outs, refs[3 * count + 5 : -3])
    kind = lax.rem(lax.axis_index("tensor"), 2)
    rows = dkv_ref.shape[0]
    block = lambda j: pl.ds(j * rows, rows)
    meet([to[k] for k in ("core", "z", "far", "last")])
    steps = ((3, "last"), (2, "far"), (1, "z"), (0, None))
    from_core = {
        j: wires.copy(part_ref.at[1 - kind, block(j)], got_core.at[block(j)], to["core"])
        for j, _ in steps
    }
    mine = wires.here(part_ref.at[kind], own)
    for one in fill:
        one.fetch(wires)
    mine.wait()
    arrive = []
    for j, k in steps[:3]:
        from_core[j].wait_recv()
        sent[block(j)] = (wide(own[block(j)]) + wide(got_core[block(j)])).astype(bf16)
        arrive.append(wires.copy(sent.at[block(j)], got.at[block(j)], to[k]))
    for one in fill:
        one.make(0, one.tiles)
    from_core[0].wait_recv()
    total = wide(own[block(0)]) + wide(got_core[block(0)])
    for one in arrive:
        one.wait_recv()
    for j in (1, 2, 3):
        total = total + wide(got[block(j)])
    dkv_ref[...] = total
    wires.finish()


def kv_scatter(part, fill, width):
    _, rows, depth = part.shape
    n_c = lax.axis_size("context")
    args, outs, scratch = own_grad_call(fill, width)
    return remote_call(
        functools.partial(kv_scatter_kernel, len(fill)),
        "kv_scatter",
        1,
        [part, *args],
        [jax.ShapeDtypeStruct((rows // n_c, depth), f32), *outs],
        [pltpu.VMEM((rows, depth), bf16)] * 4 + scratch,
        7,
        ([False] * (1 + len(args)), [True] * (1 + len(outs))),
    )


def middle_kernel(
    part,
    x_ref,
    gain_ref,
    dy_ref,
    dy_y,
    dy_z,
    dy_far,
    mid_ref,
    factor_ref,
    out,
    dys,
    own,
    core,
    sent,
    got,
    xn,
    *sems,
):
    wires, to = Wires(*sems), partners()
    blocks = out.shape[0] // 2
    size = xn.shape[0] // 2
    low, high = pl.ds(0, size), pl.ds(size, size)
    meet([to[k] for k in ("core", "y", "z", "far")])
    summed = scatter_rank(wires, to, part, own, core, sent, got)
    next(summed)
    mine = [
        wires.here(block, dys.at[k])
        for block, k in ((dy_ref, 0), (dy_y, 1), (dy_z, 2), (dy_far, blocks))
    ]
    via_z = wires.copy(dy_y.at[low], dys.at[3, low], to["z"])
    dy_last = gather_pair(wires, to, dy_far, dys, blocks)
    next(dy_last)
    next(summed)
    via_y = wires.copy(dy_z.at[high], dys.at[3, high], to["y"])
    ends = [
        wires.copy(block, dys.at[4 + k], to["core"])
        for k, block in enumerate((dy_ref, dy_y, dy_z))
    ]
    next(dy_last)
    middle = wide(x_ref[...]) + result_of(summed)
    mid_ref[...] = middle
    factor = lax.rsqrt(jnp.mean(middle * middle, axis=-1, keepdims=True) + EPSILON)
    factor_ref[...] = factor
    xn[...] = (middle * factor * gain_ref[...]).astype(bf16)
    mine.append(wires.here(xn, out.at[0]))
    xn_far = wires.copy(xn, out.at[blocks], to["far"])
    xn_near = gather_pair(wires, to, xn, out, 0)
    next(xn_near)
    next(xn_near)
    via_z.wait_recv()
    via_y.wait_recv()
    ends.append(wires.copy(dys.at[3], dys.at[7], to["core"]))
    next(dy_last)
    next(xn_near)
    xn_far.wait_recv()
    xn_last = gather_pair(wires, to, out.at[blocks], out, blocks)
    next(xn_last)
    next(xn_last)
    ends += result_of(dy_last) + result_of(xn_near)
    next(xn_last)
    ends += result_of(xn_last)
    for one in ends:
        one.wait_recv()
    for one in mine:
        one.wait()
    wires.finish()


def middle_norm(part, inputs_part, gain, dy_blocks):
    rows, width = inputs_part.shape
    return remote_call(
        middle_kernel,
        "middle_norm",
        2,
        [part.reshape(4, rows, width), inputs_part, gain, *dy_blocks],
        [
            jax.ShapeDtypeStruct((rows, width), f32),
            jax.ShapeDtypeStruct((rows, 1), f32),
            jax.ShapeDtypeStruct((16, rows, width), bf16),
            jax.ShapeDtypeStruct((16, rows, width), bf16),
        ],
        [
            pltpu.VMEM((2, rows, width), bf16),
            pltpu.VMEM((2, rows, width), bf16),
            pltpu.VMEM((rows, width), bf16),
            pltpu.VMEM((rows, width), bf16),
            pltpu.VMEM((rows, width), bf16),
        ],
        48,
        ([False] + [True] * 6, [True, True, False, False]),
    )


def norm_back_rows(values, factor, gain, grad_normed):
    gained = gain * grad_normed
    inner = jnp.mean(gained * values, axis=-1, keepdims=True)
    grad_values = factor * gained - values * (factor * factor * factor) * inner
    return grad_values, jnp.sum(grad_normed * values * factor, axis=0, keepdims=True)


def middle_back_kernel(count, part, mid_ref, factor_ref, gain_ref, dy_ref, *refs):
    args, refs = refs[: 2 * count], refs[2 * count :]
    got_ref, refs = (refs[0], refs[1:]) if count else (None, refs)
    (dmid_ref, dgain_ref, out), refs = refs[:3], refs[3:]
    outs, refs = refs[:count], refs[count:]
    (upper_ref, lower_ref, far_ref), refs = (
        (refs[:3], refs[3:]) if count else ((None, None, None), refs)
    )
    low, first, wires, to = refs[0], refs[1:8], Wires(*refs[-3:]), partners()
    fill = own_grads(count, args, outs, refs[8:-3])
    meet([to[k] for k in ("core", "y", "z")])
    back = scatter_pair(wires, to, part, *first)
    next(back)
    for one in fill:
        one.fetch(wires)
    next(back)
    if fill:
        fill[0].make(0, 1)
    next(back)
    if fill:
        fill[0].make(1, fill[0].tiles)
        cut = upper_ref.shape[0]
        upper_ref[...] = (wide(outs[0][:cut]) + wide(got_ref[:cut])).astype(bf16)
        near_half = wires.copy(upper_ref, far_ref, to["z"])
        lower_ref[...] = (wide(outs[0][cut:]) + wide(got_ref[cut:])).astype(bf16)
    grad_normed = result_of(back)
    du, dgain = norm_back_rows(mid_ref[...], factor_ref[...], gain_ref[...], grad_normed)
    dgain_ref[...] = dgain
    dmid = wide(dy_ref[...]) + du
    low[...] = dmid.astype(bf16)
    share = gather_rank(wires, to, low, out)
    next(share)
    dmid_ref[...] = dmid
    for one in fill[1:]:
        one.make(0, one.tiles)
    result_of(share)
    if fill:
        near_half.wait_recv()
    wires.finish()


def pair_scratch(rows, width):
    return [
        pltpu.VMEM((4, rows, width), bf16),
        pltpu.VMEM((4, rows, width), bf16),
        pltpu.VMEM((3, rows, width), bf16),
        pltpu.VMEM((rows, width), bf16),
        pltpu.VMEM((rows, width), bf16),
        pltpu.VMEM((rows // 2, width), bf16),
        pltpu.VMEM((rows // 2, width), bf16),
    ]


def middle_back(part, middle, factor, gain, dy_part, fill, got, shard):
    rows, width = middle.shape
    args, outs, scratch = own_grad_call(fill, shard)
    if fill:
        args = [*args, got]
        units = got.shape[0]
        cut = units // 64 * 16
        outs = [*outs, *(jax.ShapeDtypeStruct((n, shard), bf16) for n in (cut, units - cut, cut))]
    return remote_call(
        functools.partial(middle_back_kernel, len(fill)),
        "middle_back",
        3,
        [part.reshape(8, rows, width), middle, factor, gain, dy_part, *args],
        [
            jax.ShapeDtypeStruct((rows, width), f32),
            jax.ShapeDtypeStruct((1, width), f32),
            jax.ShapeDtypeStruct((4, rows, width), bf16),
            *outs,
        ],
        [pltpu.VMEM((rows, width), bf16)] + pair_scratch(rows, width) + scratch,
        16,
        (
            [False] + [True] * 4 + ([False] * (len(args) - 1) + [True] if fill else []),
            [True, True, False] + ([True] * (len(outs) - 1) + [False] if fill else []),
        ),
    )


def add_all(wires, ways, value, slots):
    for k, device in enumerate(ways):
        one = wires.copy(value, slots.at[k], device)
        one.wait()
        wires.started = [x for x in wires.started if x is not one]
        value[...] = value[...] + slots[k]


def input_back_kernel(
    part, x_ref, factor_ref, gain_ref, dmid_ref, small_ref, sum_ref, out, *rest
):
    low, own, core, sent, got, slots = rest[:-3]
    wires, to = Wires(*rest[-3:]), partners()
    meet([to[k] for k in ("core", "y")])
    grad_normed = result_of(scatter_rank(wires, to, part, own, core, sent, got))
    du, dgain = norm_back_rows(wide(x_ref[...]), factor_ref[...], gain_ref[...], grad_normed)
    low[...] = (dmid_ref[...] + du).astype(bf16)
    share = gather_rank(wires, to, low, out)
    next(share)
    width = dgain.shape[1]
    sum_ref[:, width:] = small_ref[:, width:]
    sum_ref[:, :width] = dgain
    add_all(wires, [to["core"], to["y"]], sum_ref, slots)
    result_of(share)
    wires.finish()


def input_back(part, inputs_part, factor, gain, grad_middle, small):
    rows, width = inputs_part.shape
    return remote_call(
        input_back_kernel,
        "input_back",
        5,
        [part.reshape(4, rows, width), inputs_part, factor, gain, grad_middle, small],
        [
            jax.ShapeDtypeStruct(small.shape, f32),
            jax.ShapeDtypeStruct((4, rows, width), bf16),
        ],
        [
            pltpu.VMEM((rows, width), bf16),
            pltpu.VMEM((2, rows, width), bf16),
            pltpu.VMEM((2, rows, width), bf16),
            pltpu.VMEM((rows, width), bf16),
            pltpu.VMEM((rows, width), bf16),
            pltpu.VMEM((2,) + small.shape, f32),
        ],
        16,
        ([False, True, True, True, True, True], [True, False]),
    )


def context_sum_kernel(over_f, *refs):
    parts, small_ref, out_part, mid_ref = refs[:3], refs[3], refs[4], refs[5]
    outs, sum_ref, shared, outputs = refs[6:8], refs[8], refs[9], refs[10]
    lows, from_end, from_middle = refs[11:15], refs[15:19], refs[19:23]
    out_low, slot, scratch = refs[23], refs[24], refs[25:32]
    wires, to, c = Wires(*refs[32:]), partners(), lax.axis_index("context")
    end = (c == 0) | (c == lax.axis_size("context") - 1)
    inner = jnp.logical_not(end)
    greet = ["core", "y", "z", "last"]
    if over_f:
        to["f"] = {"fsdp": 1 - lax.axis_index("fsdp")}
        greet.append("f")
    meet([to[k] for k in greet])
    ahead = scatter_pair(wires, to, out_part, *scratch)
    next(ahead)
    sum_ref[...] = small_ref[...]
    from_f = wires.copy(small_ref, slot, to["f"]) if over_f else None
    next(ahead)
    sources = [*parts, sum_ref]
    chunks = []
    for i, cuts in ((2, 1), (0, 2), (1, 2), (3, 1)):
        size = sources[i].shape[0] // cuts
        chunks += [(i, pl.ds(k * size, size)) for k in range(cuts)]
    inward = [wires.plan(sources[i].at[at], from_end[i].at[at], to["z"]) for i, at in chunks]
    across = [wires.plan(lows[i].at[at], from_middle[i].at[at], to["last"]) for i, at in chunks]
    outward = [wires.plan(lows[i].at[at], lows[i].at[at], to["z"]) for i, at in chunks]
    small = len(chunks) - 1

    def send_in(k):
        @pl.when(end)
        def _():
            inward[k].start()

    def pass_on(first, past):
        @pl.when(inner)
        def _():
            for k in range(first, past):
                i, at = chunks[k]
                inward[k].wait_recv()
                total = wide(sources[i][at]) + wide(from_end[i][at])
                lows[i][at] = total.astype(lows[i].dtype)
                across[k].start()
                if k:
                    send_out(k - 1)

    def send_out(k):
        i, at = chunks[k]
        across[k].wait()
        lows[i][at] = (wide(lows[i][at]) + wide(from_middle[i][at])).astype(lows[i].dtype)
        outward[k].start()

    send_in(0)
    send_in(1)
    next(ahead)
    if over_f:
        from_f.wait_recv()
        sum_ref[...] = sum_ref[...] + slot[...]
    for k in range(2, small + 1):
        send_in(k)
    pass_on(0, 2)
    out_low[...] = (mid_ref[...] + result_of(ahead)).astype(bf16)
    out_share = gather_rank(wires, to, out_low, outputs)
    next(out_share)
    pass_on(2, small + 1)

    @pl.when(inner)
    def _():
        send_out(small)

    result_of(out_share)

    def arrived(k):
        @pl.when(end)
        def _():
            outward[k].wait_recv()

    arrived(0)
    share = gather_rank(wires, to, lows[2], shared)
    next(share)
    for k in range(1, len(chunks)):
        arrived(k)

    @pl.when(end)
    def _():
        for one in inward:
            one.wait_send()

    for i in (0, 1):
        outs[i][...] = wide(lows[i][...])
    sum_ref[...] = lows[3][...]
    result_of(share)

    @pl.when(inner)
    def _():
        for one in outward:
            one.wait_send()

    wires.finish()


def context_sum(over_f, parts, small, out_part, middle):
    rows, width = middle.shape
    lines = [pltpu.VMEM(x.shape, x.dtype) for x in (*parts, small)]
    return remote_call(
        functools.partial(context_sum_kernel, over_f),
        "context_sum",
        6,
        [*parts, small, out_part.reshape(8, rows, width), middle],
        [jax.ShapeDtypeStruct(x.shape, f32) for x in parts[:2]]
        + [jax.ShapeDtypeStruct(small.shape, f32)]
        + [jax.ShapeDtypeStruct((4,) + parts[2].shape, bf16)]
        + [jax.ShapeDtypeStruct((4, rows, width), bf16)],
        lines * 3
        + [pltpu.VMEM((rows, width), bf16), pltpu.VMEM(small.shape, f32)]
        + pair_scratch(rows, width),
        48,
        ([True] * 4 + [False, True], [True] * 3 + [False] * 2),
    )


def build(n_f, n_c, n_t):
    def flip(x, axis, bit):
        size = {"fsdp": n_f, "context": n_c, "tensor": n_t}[axis]
        return lax.ppermute(x, axis, [(i, i ^ bit) for i in range(size)])

    def by_bit(bit, x, other, axis):
        return jnp.where(
            bit == 0,
            jnp.concatenate([x, other], axis=axis),
            jnp.concatenate([other, x], axis=axis),
        )

    def after(x, *others):
        return lax.optimization_barrier((x, others))[0]

    def local(
        inputs,
        cotangent,
        blocks,
        attn_gain,
        w_query,
        b_query,
        w_key,
        b_key,
        w_value,
        b_value,
        w_out,
        ffn_gain,
        w_gate,
        w_up,
        w_down,
    ):
        rows, width = inputs.shape
        f = lax.axis_index("fsdp")
        c = lax.axis_index("context")
        t = lax.axis_index("tensor")
        core, parity, pair = t % 2, c % 2, c // 2
        heads = w_query.shape[1] // HD
        group = (t * heads) // (H // KV)
        part = rows // n_t
        units_all = w_gate.shape[1]
        units = units_all // 2

        def gather_f(x, axis):
            if n_f == 2:
                return by_bit(f, x, flip(x, "fsdp", 1), axis)
            return lax.all_gather(x, "fsdp", axis=axis, tiled=True)

        def grad_far(left, right, side):
            if n_f > 2:
                return None
            source = (left, right)[side]
            half = width // 2
            far = lax.dynamic_slice_in_dim(source, (1 - f) * half, half, 1)
            return (dot_rows(far, right) if side == 0 else dot_rows(left, far)).astype(bf16)

        def grad_sum(left, right, side, far, late):
            if n_f > 2:
                return lax.psum_scatter(
                    dot_rows(left, right).astype(bf16), "fsdp", scatter_dimension=side, tiled=True
                )
            source = (left, right)[side]
            half = width // 2
            own = lax.dynamic_slice_in_dim(source, f * half, half, 1)
            own = dot_rows(own, right) if side == 0 else dot_rows(left, own)
            return (own + after(flip(far, "fsdp", 1), late).astype(f32)).astype(bf16)

        small = jnp.concatenate(
            [v.reshape(1, -1) for v in (attn_gain, ffn_gain, b_query, b_key, b_value)], axis=1
        )
        column = lambda w: lax.dynamic_slice_in_dim(w, group * HD, HD, 1)
        w_kv_own = jnp.where(core == 0, column(w_key), column(w_value))
        pieces_f = lambda x, axis: (
            [x, flip(x, "fsdp", 1)]
            if n_f == 2
            else [lax.all_gather(x, "fsdp", axis=axis, tiled=True)]
        )
        meta = jnp.stack([f, 1 - f, core, pair]).astype(jnp.int32)
        w_q = pieces_f(w_query, 0)
        w_kv = pieces_f(w_kv_own, 0)
        small = gather_f(small, 0)
        w_out_all = gather_f(after(w_out, small, w_q, w_kv), 1)
        piece = attn_gain.shape[0]
        gain_first = small[:, :piece].reshape(1, width).astype(f32)
        gain_second = small[:, piece : 2 * piece].reshape(1, width).astype(f32)
        bias_of = lambda lo, n: (
            small[:, lo : lo + n * (HD // n_f)]
            .reshape(n_f, n, HD // n_f)
            .transpose(1, 0, 2)
            .reshape(n, HD)
            .astype(f32)
        )
        at = 2 * piece
        bq = bias_of(at, heads)
        bk = bias_of(at + heads * (HD // n_f), KV)
        bv = bias_of(at + (heads + KV) * (HD // n_f), KV)
        b_kv = lax.dynamic_index_in_dim(jnp.where(core == 0, bk, bv), group, 0)

        unit_slice = lambda w: lax.dynamic_slice_in_dim(w, parity * units, units, 0)
        own_gate_up = jnp.concatenate(
            [unit_slice(after(w, w_kv_own)) for w in (w_gate.T, w_up.T)], axis=0
        )
        own_down = unit_slice(w_down)

        dy_part = lax.dynamic_slice_in_dim(cotangent, t * part, part, 0)

        seq_blocks = blocks[0].reshape(n_c, -1)
        own_blocks = seq_blocks.shape[1]
        key_blocks = jnp.concatenate(
            [lax.dynamic_index_in_dim(seq_blocks, c ^ j, 0, keepdims=False) for j in range(n_c)]
        )
        positions = (
            key_blocks[:own_blocks, None] * BLOCK + jnp.arange(BLOCK, dtype=jnp.int32)[None, :]
        ).reshape(-1)
        cosine, sine = rope_tables(positions)
        bias = jnp.concatenate([bq.reshape(1, -1), b_kv], axis=1)
        dy_blocks = [
            dy_part,
            flip(dy_part, "tensor", 2),
            flip(dy_part, "context", 1),
            flip(dy_part, "context", 2),
        ]
        inputs_part = lax.dynamic_slice_in_dim(inputs, t * part, part, 0)
        bias = after(bias, dy_blocks[2:], own_gate_up, own_down, inputs_part)
        normed, factor_first, queries, kv_own = qkv(
            meta, inputs, gain_first, bias, cosine, sine, w_q, w_kv
        )
        far_gate_up = pieces_f(after(own_gate_up, kv_own, w_out_all), 1)[-1]
        w_gate_up = [own_gate_up, far_gate_up] if n_f == 2 else [far_gate_up]
        kv = kv_gather(after(kv_own, w_out_all))
        far_down = pieces_f(after(own_down, kv), 1)[-1]
        w_downs = [own_down, far_down] if n_f == 2 else [far_down]
        attended, lse = attention(key_blocks, queries, kv)
        middle, factor_second, normed2, dy_all = middle_norm(
            dot(attended, w_out_all).astype(bf16), inputs_part, gain_second, dy_blocks
        )

        hidden, slope, gated, *down_far = hidden_units(meta, normed2, dy_all, w_gate_up)
        grad_gate, grad_up, dx_part, out_part, *unit_far = hidden_back(
            meta, normed2, dy_all, hidden, slope, gated, w_gate_up, w_downs
        )
        unit_far = [*down_far, *unit_far]
        flat = lambda x: x.reshape(-1, width)
        if n_f == 2:
            down_got, gate_got, up_got = (flip(x, "fsdp", 1) for x in unit_far)
            early = [(hidden, flat(dy_all)), (grad_gate, flat(normed2))]
            later = [(grad_up, flat(normed2))]
        else:
            over_f = lambda x: lax.psum_scatter(x, "fsdp", scatter_dimension=1, tiled=True)
            owns = [
                over_f(unit_grads(meta, 0, 1, x, [unit]))
                for x, unit in ((dy_all, hidden), (normed2, grad_gate), (normed2, grad_up))
            ]
            down_got = gate_got = up_got = jnp.zeros_like(owns[0])
            early = later = []

        def unit_whole(own, other):
            own, other = (jnp.concatenate(x, axis=0) for x in (own, other))
            return by_bit(parity, own, other, 0).astype(f32)

        grad_middle, ffn_gain_grad, grad_middle_low, *first_owns = middle_back(
            dx_part, middle, factor_second, gain_second, dy_part, early, down_got, width // n_f
        )
        grad_middle_low = grad_middle_low.reshape(rows, width)
        add = lambda own, got: (own.astype(f32) + got.astype(f32)).astype(bf16)
        upper = units // 2
        if n_f == 2:
            _, gate_own, down_upper, down_lower, far_upper = first_owns
        else:
            down_low, gate_own = owns[:2]
            down_upper, down_lower = down_low[:upper], down_low[upper:]
            far_upper = flip(down_upper, "context", 1)
        gate_got = after(gate_got, grad_middle_low)
        gate_low = add(gate_own, gate_got)
        far_lower = flip(down_lower, "context", 1)
        grad_middle_low = after(grad_middle_low, gate_low)
        grad_attended = dot_cols(grad_middle_low, w_out_all).astype(bf16)

        dq_low, dkv = attention_back(key_blocks, queries, grad_attended, lse, cosine, sine, kv)
        attention_args = [(attended, after(grad_middle_low, dq_low), 1), (normed, dq_low, 0)]
        fars = [grad_far(*args) for args in attention_args]
        dkv, *last_owns = kv_scatter(
            after(dkv, fars), later, width // n_f
        )
        (up_own,) = last_owns or owns[2:]
        far_gate = flip(after(gate_low, dkv, far_lower), "context", 1)
        up_got = after(up_got, dkv)
        up_low = add(up_own, up_got)
        dkv = after(dkv, up_low, far_lower)
        dkv_low = jnp.where(core == 0, rotate_back(dkv, cosine, sine), dkv).astype(bf16)
        attention_args.append((normed, dkv_low, 0))
        fars.append(grad_far(*attention_args[-1]))
        dkv_low = after(dkv_low, fars)
        factor_part = lax.dynamic_slice_in_dim(factor_first, t * part, part, 0)
        own_biases = jnp.sum(
            jnp.concatenate([dq_low, dkv_low], axis=1).astype(f32), axis=0, keepdims=True
        )
        slots = lax.dynamic_update_slice(
            jnp.zeros((n_t, (heads + 1) * HD), f32), own_biases, (t, 0)
        )
        small_grads = jnp.concatenate(
            [jnp.zeros((1, width), f32), ffn_gain_grad, slots.reshape(1, -1)], axis=1
        )
        grad_qkv = qkv_back(meta, dq_low, dkv_low, w_q, w_kv)
        far_up = flip(after(up_low, dkv_low), "context", 1)
        small_grads, input_grad = input_back(
            grad_qkv,
            inputs_part,
            factor_part,
            gain_first,
            grad_middle,
            small_grads,
        )
        input_grad = input_grad.reshape(rows, width)
        if n_f > 2:
            small_grads = lax.psum(small_grads, "fsdp")
        zero = jnp.minimum(t, 0).astype(bf16)
        input_grad = input_grad + zero
        small_grads = after(small_grads, far_gate)
        attention_parts = [
            grad_sum(*args, far, small_grads) for args, far in zip(attention_args, fars)
        ]
        wd_grad = unit_whole(
            *after(((down_upper, down_lower), (far_upper, far_lower)), small_grads)
        )
        wg_grad = unit_whole(*after(((gate_low,), (far_gate,)), small_grads))
        small_grads, wd_grad, wg_grad, input_grad = lax.optimization_barrier(
            (small_grads, wd_grad, wg_grad, input_grad)
        )
        wo_grad, wq_grad, packed, wkv_all, outputs = context_sum(
            n_f == 2, attention_parts, small_grads, out_part, middle
        )
        wo_grad, wq_grad, packed, wkv_all, outputs, far_up = lax.optimization_barrier(
            (wo_grad, wq_grad, packed, wkv_all, outputs, far_up)
        )
        outputs = outputs.reshape(rows, width)
        wkv_all = wkv_all.astype(f32)
        wk_grad = jnp.concatenate([wkv_all[0], wkv_all[2]], axis=1)
        wv_grad = jnp.concatenate([wkv_all[1], wkv_all[3]], axis=1)
        packed = packed[0]
        attn_gain_grad = lax.dynamic_slice_in_dim(packed, f * piece, piece, 0)
        ffn_gain_grad = lax.dynamic_slice_in_dim(packed, width + f * piece, piece, 0)
        slots = packed[2 * width :].reshape(n_t, heads + 1, HD)
        slots = lax.dynamic_slice_in_dim(slots, f * (HD // n_f), HD // n_f, 2)
        bq_out = lax.dynamic_index_in_dim(slots, t, 0, keepdims=False)[:heads]
        bk_out = slots[0::2, heads]
        bv_out = slots[1::2, heads]

        wu_grad = unit_whole((up_low,), (far_up,))
        wg_grad, wu_grad = wg_grad.T, wu_grad.T

        return (
            outputs,
            input_grad,
            attn_gain_grad,
            wq_grad,
            bq_out,
            wk_grad,
            bk_out,
            wv_grad,
            bv_out,
            wo_grad,
            ffn_gain_grad,
            wg_grad,
            wu_grad,
            wd_grad,
        )

    return local


def solution(mesh):
    in_specs = (
        P(("fsdp", "context"), None),
        P(("fsdp", "context"), None),
        P("fsdp", None),
        P("fsdp"),
        P("fsdp", "tensor"),
        P("tensor", "fsdp"),
        P("fsdp", None),
        P(None, "fsdp"),
        P("fsdp", None),
        P(None, "fsdp"),
        P("tensor", "fsdp"),
        P("fsdp"),
        P("fsdp", "tensor"),
        P("fsdp", "tensor"),
        P("tensor", "fsdp"),
    )
    out_specs = (
        P(("fsdp", "context"), None),
        P(("fsdp", "context"), None),
        P("fsdp"),
        P("fsdp", "tensor"),
        P("tensor", "fsdp"),
        P("fsdp", None),
        P(None, "fsdp"),
        P("fsdp", None),
        P(None, "fsdp"),
        P("tensor", "fsdp"),
        P("fsdp"),
        P("fsdp", "tensor"),
        P("fsdp", "tensor"),
        P("tensor", "fsdp"),
    )
    local = build(mesh.shape["fsdp"], mesh.shape["context"], mesh.shape["tensor"])
    return jax.shard_map(local, mesh=mesh, in_specs=in_specs, out_specs=out_specs, check_vma=False)
```

```python
import functools

import jax
import jax.numpy as jnp
from jax import lax
from jax.experimental import pallas as pl
from jax.experimental.pallas import tpu as pltpu
from jax.sharding import PartitionSpec as P

H = 12
KV = 2
HD = 128
BLOCK = 256

EPSILON = 1e-06
ROPE_BASE = 1000000.0
MASKED = -1e30
SCALING = HD ** (-0.5)
LANES = 128
VMEM_LIMIT = 60 << 20

f32 = jnp.float32
bf16 = jnp.bfloat16


def rope_tables(positions):
    halfway = HD // 2
    frequency = ROPE_BASE ** (-(jnp.arange(halfway, dtype=f32) * 2.0 / HD))
    angles = positions.astype(f32)[:, None] * frequency[None, :]
    cosine, sine = jnp.cos(angles), jnp.sin(angles)
    return (jnp.concatenate([cosine, cosine], axis=1), jnp.concatenate([sine, sine], axis=1))


def rotate(field, cosine, sine):
    halfway = HD // 2
    turned = jnp.concatenate([-field[..., halfway:], field[..., :halfway]], axis=-1)
    return field * cosine + turned * sine


def rotate_back(grad_field, cosine, sine):
    halfway = HD // 2
    moved = grad_field * sine
    turned = jnp.concatenate([moved[..., halfway:], -moved[..., :halfway]], axis=-1)
    return grad_field * cosine + turned


def dot(left, right):
    return jnp.dot(left, right, preferred_element_type=f32)


def dot_rows(left, right):
    return lax.dot_general(left, right, (((0,), (0,)), ((), ())), preferred_element_type=f32)


def dot_cols(left, right):
    return lax.dot_general(left, right, (((1,), (1,)), ((), ())), preferred_element_type=f32)


def mask_row(kb_ref, own_block, key_blocks):
    return jnp.concatenate(
        [
            jnp.full((1, BLOCK), jnp.where(kb_ref[j] <= own_block, 0.0, MASKED), f32)
            for j in range(key_blocks)
        ],
        axis=1,
    )


def attention_kernel(key_blocks, kb_ref, q_ref, k_ref, v_ref, o_ref, lse_ref):
    bias = mask_row(kb_ref, kb_ref[pl.program_id(1)], key_blocks)
    scores = dot_cols(q_ref[...], k_ref[...]) * SCALING + bias
    row_max = jnp.max(scores, axis=1, keepdims=True)
    expo = jnp.exp(scores - row_max)
    total = jnp.sum(expo, axis=1, keepdims=True)
    probability = (expo * (1.0 / total)).astype(bf16)
    o_ref[...] = dot(probability, v_ref[...]).astype(bf16)
    lse_ref[0] = row_max + jnp.log(total)


def attention(key_blocks, queries, kv):
    rows, width = queries.shape
    heads = width // HD
    whole = lambda kind: pl.BlockSpec((None,) + kv.shape[1:], lambda h, i, kb: (kind, 0, 0))
    tile = pl.BlockSpec((BLOCK, HD), lambda h, i, kb: (i, h))
    return pl.pallas_call(
        functools.partial(attention_kernel, kv.shape[1] // BLOCK),
        name="attention",
        grid_spec=pltpu.PrefetchScalarGridSpec(
            num_scalar_prefetch=1,
            grid=(heads, rows // BLOCK),
            in_specs=[tile, whole(0), whole(1)],
            out_specs=[tile, pl.BlockSpec((1, BLOCK, 1), lambda h, i, kb: (h, i, 0))],
        ),
        out_shape=[
            jax.ShapeDtypeStruct((rows, width), bf16),
            jax.ShapeDtypeStruct((heads, rows, 1), f32),
        ],
        compiler_params=pltpu.CompilerParams(vmem_limit_bytes=VMEM_LIMIT),
    )(key_blocks, queries, kv, kv)


def attention_back_kernel(
    key_blocks,
    kb_ref,
    q_ref,
    do_ref,
    lse_ref,
    cos_ref,
    sin_ref,
    k_ref,
    v_ref,
    dq_ref,
    dkv_ref,
    dk_ref,
    dv_ref,
):
    head, i = pl.program_id(0), pl.program_id(1)

    @pl.when((head == 0) & (i == 0))
    def _():
        dk_ref[...] = jnp.zeros_like(dk_ref)
        dv_ref[...] = jnp.zeros_like(dv_ref)

    bias = mask_row(kb_ref, kb_ref[i], key_blocks)
    scores = dot_cols(q_ref[...], k_ref[...]) * SCALING + bias
    probability = jnp.exp(scores - lse_ref[0])
    grad_probs = dot_cols(do_ref[...], v_ref[...])
    inner = jnp.sum(probability * grad_probs, axis=1, keepdims=True)
    grad_scores = (probability * (grad_probs - inner)).astype(bf16)
    grad_query = dot(grad_scores, k_ref[...]) * SCALING
    moved = grad_query * sin_ref[...]
    sign = jnp.where(lax.broadcasted_iota(jnp.int32, moved.shape, 1) < HD // 2, 1.0, -1.0)
    dq_ref[...] = (
        grad_query * cos_ref[...] + pltpu.roll(moved, HD // 2, 1) * sign
    ).astype(bf16)
    dk_ref[...] += dot_rows(grad_scores, q_ref[...]) * SCALING
    dv_ref[...] += dot_rows(probability.astype(bf16), do_ref[...])

    @pl.when((head == pl.num_programs(0) - 1) & (i == pl.num_programs(1) - 1))
    def _():
        dkv_ref[0] = dk_ref[...].astype(bf16)
        dkv_ref[1] = dv_ref[...].astype(bf16)


def attention_back(key_blocks, queries, grad_out, lse, cosine, sine, kv):
    rows, width = queries.shape
    heads = width // HD
    whole = lambda kind: pl.BlockSpec((None,) + kv.shape[1:], lambda h, i, kb: (kind, 0, 0))
    tile = pl.BlockSpec((BLOCK, HD), lambda h, i, kb: (i, h))
    table = pl.BlockSpec((BLOCK, HD), lambda h, i, kb: (i, 0))
    return pl.pallas_call(
        functools.partial(attention_back_kernel, kv.shape[1] // BLOCK),
        name="attention_back",
        grid_spec=pltpu.PrefetchScalarGridSpec(
            num_scalar_prefetch=1,
            grid=(heads, rows // BLOCK),
            in_specs=[
                tile,
                tile,
                pl.BlockSpec((1, BLOCK, 1), lambda h, i, kb: (h, i, 0)),
                table,
                table,
                whole(0),
                whole(1),
            ],
            out_specs=[tile, pl.BlockSpec(kv.shape, lambda h, i, kb: (0, 0, 0))],
            scratch_shapes=[pltpu.VMEM(kv.shape[1:], f32)] * 2,
        ),
        out_shape=[
            jax.ShapeDtypeStruct((rows, width), bf16),
            jax.ShapeDtypeStruct(kv.shape, bf16),
        ],
        compiler_params=pltpu.CompilerParams(vmem_limit_bytes=VMEM_LIMIT),
    )(key_blocks, queries, grad_out, lse, cosine, sine, kv, kv)


def qkv_kernel(pieces, meta_ref, x_ref, gain_ref, bias_ref, cos_ref, sin_ref, *refs):
    weights, (xn_ref, factor_ref, q_ref, kv_ref) = refs[: 2 * pieces], refs[2 * pieces :]
    values = x_ref[...].astype(f32)
    factor = lax.rsqrt(jnp.mean(values * values, axis=-1, keepdims=True) + EPSILON)
    factor_ref[...] = factor
    xn_ref[...] = (values * factor * gain_ref[...]).astype(bf16)
    depth = weights[0].shape[0]
    normed = [xn_ref[:, columns_of(meta_ref, j, depth, pieces)] for j in range(pieces)]
    cosine, sine = cos_ref[...], sin_ref[...]
    sign = jnp.where(lax.broadcasted_iota(jnp.int32, cosine.shape, 1) < HD // 2, -1.0, 1.0)
    sine = sine * sign
    width = q_ref.shape[1]
    total = bias_ref[:, :width] + sum(dot(x, w[...]) for x, w in zip(normed, weights[:pieces]))
    turn = lambda own: own * cosine + pltpu.roll(own, HD // 2, 1) * sine
    for h in range(width // HD):
        q_ref[:, h * HD : (h + 1) * HD] = turn(total[:, h * HD : (h + 1) * HD]).astype(bf16)
    own = bias_ref[:, width:] + sum(dot(x, w[...]) for x, w in zip(normed, weights[pieces:]))
    kv_ref[...] = jnp.where(meta_ref[2] == 0, turn(own), own).astype(bf16)


def columns_of(meta_ref, j, depth, pieces):
    if pieces == 1:
        return slice(None)
    return pl.ds(pl.multiple_of(meta_ref[j] * depth, LANES), depth)


def qkv(meta, inputs, gain, bias, cosine, sine, w_q, w_kv):
    rows, width = inputs.shape
    out = w_q[0].shape[1]
    tile = 256
    row = lambda n: pl.BlockSpec((tile, n), lambda i, m: (i, 0))
    fixed = lambda w: pl.BlockSpec(w.shape, lambda i, m: (0, 0))
    return pl.pallas_call(
        functools.partial(qkv_kernel, len(w_q)),
        name="qkv",
        grid_spec=pltpu.PrefetchScalarGridSpec(
            num_scalar_prefetch=1,
            grid=(rows // tile,),
            in_specs=[row(width), fixed(gain), fixed(bias), row(HD), row(HD)]
            + [fixed(w) for w in (*w_q, *w_kv)],
            out_specs=[row(width), row(1), row(out), row(HD)],
        ),
        out_shape=[
            jax.ShapeDtypeStruct((rows, width), bf16),
            jax.ShapeDtypeStruct((rows, 1), f32),
            jax.ShapeDtypeStruct((rows, out), bf16),
            jax.ShapeDtypeStruct((rows, HD), bf16),
        ],
        compiler_params=pltpu.CompilerParams(vmem_limit_bytes=VMEM_LIMIT),
    )(meta, inputs, gain, bias, cosine, sine, *w_q, *w_kv)


def qkv_back_kernel(pieces, meta_ref, dq_ref, dkv_ref, *refs):
    w_q, w_kv, out_ref = refs[:pieces], refs[pieces : 2 * pieces], refs[-1]
    for j in range(pieces):
        out_ref[:, columns_of(meta_ref, j, w_q[j].shape[0], pieces)] = (
            dot_cols(dq_ref[...], w_q[j][...]) + dot_cols(dkv_ref[...], w_kv[j][...])
        ).astype(bf16)


def qkv_back(meta, grad_q, grad_kv, w_q, w_kv):
    rows, width = grad_q.shape[0], sum(w.shape[0] for w in w_q)
    tile = 256
    row = lambda n: pl.BlockSpec((tile, n), lambda i, m: (i, 0))
    fixed = lambda w: pl.BlockSpec(w.shape, lambda i, m: (0, 0))
    return pl.pallas_call(
        functools.partial(qkv_back_kernel, len(w_q)),
        name="qkv_back",
        grid_spec=pltpu.PrefetchScalarGridSpec(
            num_scalar_prefetch=1,
            grid=(rows // tile,),
            in_specs=[row(grad_q.shape[1]), row(HD)] + [fixed(w) for w in (*w_q, *w_kv)],
            out_specs=row(width),
        ),
        out_shape=jax.ShapeDtypeStruct((rows, width), bf16),
        compiler_params=pltpu.CompilerParams(vmem_limit_bytes=VMEM_LIMIT),
    )(meta, grad_q, grad_kv, *w_q, *w_kv)


def add_rows(unit_refs, row_refs, columns, totals, outs):
    step = pl.program_id(0)

    @pl.when(step == 0)
    def _():
        for total in totals:
            total[...] = jnp.zeros_like(total)

    for total, unit, row in zip(totals, unit_refs, row_refs):
        total[...] += dot_rows(unit[...], row[:, columns])

    @pl.when(step == pl.num_programs(0) - 1)
    def _():
        for out, total in zip(outs, totals):
            out[...] = total[...].astype(bf16)


def hidden_kernel(pieces, meta_ref, x_ref, dy_ref, *refs):
    wg, wu, refs = refs[:pieces], refs[pieces : 2 * pieces], refs[2 * pieces :]
    hid_ref, slope_ref, gated_ref = refs[:3]
    columns = [columns_of(meta_ref, j, wg[j].shape[1], pieces) for j in range(pieces)]
    gate = sum(dot_cols(x_ref[:, at], w[...]) for at, w in zip(columns, wg))
    up = sum(dot_cols(x_ref[:, at], w[...]) for at, w in zip(columns, wu))
    sigma = 1.0 / (1.0 + jnp.exp(-gate))
    gated = gate * sigma
    hid_ref[...] = (gated * up).astype(bf16)
    slope_ref[...] = (up * (sigma + gated * (1.0 - sigma))).astype(bf16)
    gated_ref[...] = gated.astype(bf16)
    if pieces == 2:
        add_rows([hid_ref], [dy_ref], columns[1], refs[4:], refs[3:4])


def hidden_back_kernel(pieces, meta_ref, x_ref, dy_ref, hid_ref, slope_ref, gated_ref, *refs):
    wg, wu, wd = (refs[m * pieces : (m + 1) * pieces] for m in range(3))
    refs = refs[3 * pieces :]
    dg_ref, du_ref, dx_ref, out_ref = refs[:4]
    columns = [columns_of(meta_ref, j, wg[j].shape[1], pieces) for j in range(pieces)]
    grad_hidden = sum(dot_cols(dy_ref[:, at], w[...]) for at, w in zip(columns, wd))
    dg_ref[...] = (grad_hidden * slope_ref[...].astype(f32)).astype(bf16)
    du_ref[...] = (grad_hidden * gated_ref[...].astype(f32)).astype(bf16)

    @pl.when(pl.program_id(0) // (pl.num_programs(0) // 2) == meta_ref[3])
    def _():
        for at, g, u, d in zip(columns, wg, wu, wd):
            dx_ref[:, at] = (dot(dg_ref[...], g[...]) + dot(du_ref[...], u[...])).astype(bf16)
            out_ref[:, at] = dot(hid_ref[...], d[...]).astype(bf16)

    if pieces == 2:
        add_rows([dg_ref, du_ref], [x_ref, x_ref], columns[1], refs[6:], refs[4:6])


def hidden_specs(meta, normed, weights):
    width = normed.shape[-1]
    rows = normed.shape[0] * normed.shape[1]
    units, depth = weights[0].shape[0] // 2, weights[0].shape[1]
    tile = 512
    steps = rows // tile
    half = steps // 2
    once = pl.Buffered(1)
    inside = lambda i, m: jnp.clip(i - m[3] * half, 0, half - 1)
    return {
        "steps": steps,
        "flat": lambda x: x.reshape(-1, width),
        "row": pl.BlockSpec((tile, width), lambda i, m: (lax.rem(i + m[3] * half, steps), 0)),
        "unit": pl.BlockSpec((tile, units), lambda i, m: (i, 0)),
        "near_unit": pl.BlockSpec((tile, units), lambda i, m: (inside(i, m) + m[3] * half, 0)),
        "near_row": pl.BlockSpec((tile, width), lambda i, m: (inside(i, m), 0)),
        "weight": lambda k: pl.BlockSpec((units, depth), lambda i, m: (k, 0), pipeline_mode=once),
        "grad": pl.BlockSpec((units, depth), lambda i, m: (0, 0), pipeline_mode=once),
        "unit_shape": jax.ShapeDtypeStruct((rows, units), bf16),
        "near_shape": jax.ShapeDtypeStruct((rows // 2, width), bf16),
        "grad_shape": jax.ShapeDtypeStruct((units, depth), bf16),
        "total": pltpu.VMEM((units, depth), f32),
    }


def hidden_call(kernel, name, meta, args, in_specs, outs, grads, specs):
    return pl.pallas_call(
        kernel,
        name=name,
        grid_spec=pltpu.PrefetchScalarGridSpec(
            num_scalar_prefetch=1,
            grid=(specs["steps"],),
            in_specs=in_specs,
            out_specs=[specs[x] for x in outs] + [specs["grad"]] * grads,
            scratch_shapes=[specs["total"]] * grads,
        ),
        out_shape=[specs[x.split("_")[0] + "_shape"] for x in outs]
        + [specs["grad_shape"]] * grads,
        compiler_params=pltpu.CompilerParams(vmem_limit_bytes=VMEM_LIMIT),
    )(meta, *args)


def hidden_units(meta, normed, grad_out, weights):
    specs, pieces = hidden_specs(meta, normed, weights), len(weights)
    return hidden_call(
        functools.partial(hidden_kernel, pieces),
        "hidden_units",
        meta,
        [specs["flat"](normed), specs["flat"](grad_out)] + list(weights) * 2,
        [specs["row"]] * 2 + [specs["weight"](k) for k in range(2) for _ in weights],
        ["unit"] * 3,
        pieces == 2,
        specs,
    )


def hidden_back(meta, normed, grad_out, hidden, slope, gated, weights, down_weights):
    specs, pieces = hidden_specs(meta, normed, weights), len(weights)
    return hidden_call(
        functools.partial(hidden_back_kernel, pieces),
        "hidden_back",
        meta,
        [specs["flat"](normed), specs["flat"](grad_out), hidden, slope, gated]
        + list(weights) * 2
        + list(down_weights),
        [specs["row"]] * 2
        + [specs["near_unit"], specs["unit"], specs["unit"]]
        + [specs["weight"](k) for k in (0, 1, 0) for _ in weights],
        ["unit", "unit", "near_row", "near_row"],
        2 * (pieces == 2),
        specs,
    )


def unit_grads_kernel(count, meta_ref, near_ref, far_ref, *refs):
    units, out_ref, x_ref = refs[:count], refs[-2], refs[-1]
    half = near_ref.shape[0]
    x_ref[pl.ds(pl.multiple_of(meta_ref[3] * half, half), half)] = near_ref[...]
    x_ref[pl.ds(pl.multiple_of((1 - meta_ref[3]) * half, half), half)] = far_ref[...]
    for k, unit in enumerate(units):
        depth = unit.shape[1]
        out_ref[k * depth : (k + 1) * depth] = dot_rows(unit[...], x_ref[...]).astype(bf16)


def unit_grads(meta, which, pieces, x, units_of):
    width = x.shape[-1]
    count, (rows, units) = len(units_of), units_of[0].shape
    depth = width // pieces
    tile = 256
    steps = depth // tile
    shard = (lambda m: m[which]) if pieces > 1 else (lambda m: 0)
    feature = lambda half: pl.BlockSpec(
        (rows // 2, tile), lambda i, m: (half, shard(m) * steps + i)
    )
    unit = pl.BlockSpec((rows, units), lambda i, m: (0, 0), pipeline_mode=pl.Buffered(1))
    x = x.reshape(-1, width)
    return pl.pallas_call(
        functools.partial(unit_grads_kernel, count),
        name=f"unit_grads_{which}_{count}",
        grid_spec=pltpu.PrefetchScalarGridSpec(
            num_scalar_prefetch=1,
            grid=(steps,),
            in_specs=[feature(0), feature(1)] + [unit] * count,
            out_specs=pl.BlockSpec((count * units, tile), lambda i, m: (0, i)),
            scratch_shapes=[pltpu.VMEM((rows, tile), bf16)],
        ),
        out_shape=jax.ShapeDtypeStruct((count * units, depth), bf16),
        compiler_params=pltpu.CompilerParams(vmem_limit_bytes=VMEM_LIMIT),
    )(meta, x, x, *units_of)


class Wires:
    def __init__(self, sends, receives, locals_):
        self.sends, self.receives, self.locals = sends, receives, locals_
        self.used = self.used_local = 0
        self.started = []

    def plan(self, source, target, device):
        k = self.used
        self.used += 1
        return pltpu.make_async_remote_copy(
            source,
            target,
            self.sends.at[k],
            self.receives.at[k],
            device_id=device,
            device_id_type=pl.DeviceIdType.MESH,
        )

    def copy(self, source, target, device):
        one = self.plan(source, target, device)
        one.start()
        self.started.append(one)
        return one

    def here(self, source, target):
        k = self.used_local
        self.used_local += 1
        one = pltpu.make_async_copy(source, target, self.locals.at[k])
        one.start()
        return one

    def finish(self):
        for one in self.started:
            one.wait_send()


class OwnGrad:
    TILE = 256

    def __init__(self, units, rows, out, units_here, rows_here):
        self.units, self.rows, self.out = units, rows, out
        self.units_here, self.rows_here = units_here, rows_here
        self.tiles = out.shape[1] // self.TILE
        self.copies = None

    def fetch(self, wires):
        half, depth = self.rows.shape[0] // 2, self.out.shape[1]
        column = pl.multiple_of(lax.axis_index("fsdp") * depth, LANES)
        pair = lax.axis_index("context") // 2
        self.copies = [wires.here(self.units, self.units_here)]
        for k, place in ((0, pair), (1, 1 - pair)):
            self.copies.append(
                wires.here(
                    self.rows.at[pl.ds(k * half, half), pl.ds(column, depth)],
                    self.rows_here.at[pl.ds(pl.multiple_of(place * half, half), half)],
                )
            )

    def make(self, first, past):
        for one in self.copies:
            one.wait()
        self.copies = []

        @pl.loop(first, past)
        def _(k):
            at = pl.ds(pl.multiple_of(k * self.TILE, self.TILE), self.TILE)
            self.out[:, at] = dot_rows(self.units_here[...], self.rows_here[:, at]).astype(bf16)


def own_grad_call(fill, width):
    args = [x for pair in fill for x in pair]
    outs = [jax.ShapeDtypeStruct((units.shape[1], width), bf16) for units, _ in fill]
    scratch = []
    for units, rows in fill:
        scratch += [pltpu.VMEM(units.shape, bf16), pltpu.VMEM((rows.shape[0], width), bf16)]
    return args, outs, scratch


def own_grads(count, args, outs, scratch):
    return [
        OwnGrad(args[2 * k], args[2 * k + 1], outs[k], scratch[2 * k], scratch[2 * k + 1])
        for k in range(count)
    ]


def meet(devices):
    barrier = pltpu.get_barrier_semaphore()
    for device in devices:
        pl.semaphore_signal(barrier, inc=1, device_id=device, device_id_type=pl.DeviceIdType.MESH)
    pl.semaphore_wait(barrier, len(devices))


def partners():
    c, t = lax.axis_index("context"), lax.axis_index("tensor")
    flip = lambda x, bit: x + bit * (1 - 2 * lax.rem(x // bit, 2))
    return {
        "core": {"tensor": flip(t, 1)},
        "y": {"tensor": flip(t, 2)},
        "z": {"context": flip(c, 1)},
        "far": {"context": flip(c, 2)},
        "last": {"context": flip(flip(c, 1), 2)},
    }


def wide(x):
    return x.astype(f32)


def ranks():
    t = lax.axis_index("tensor")
    flip = lambda x, bit: x + bit * (1 - 2 * lax.rem(x // bit, 2))
    return (t, flip(t, 1), flip(t, 2), flip(flip(t, 1), 2))


def scatter_rank(wires, to, part, own, got_core, sent, got_y):
    size = part.shape[1] // 2
    halves = [pl.ds(0, size), pl.ds(size, size)]
    rank = ranks()
    from_core = {}
    for block in (1, 0):
        for k, at in enumerate(halves):
            from_core[block, k] = wires.copy(
                part.at[rank[1 + 2 * block], at], got_core.at[block, at], to["core"]
            )
    mine = [wires.here(part.at[rank[2 * block]], own.at[block]) for block in (0, 1)]
    yield
    for one in mine:
        one.wait()
    from_y = []
    for k, at in enumerate(halves):
        from_core[1, k].wait_recv()
        sent[at] = (wide(own[1, at]) + wide(got_core[1, at])).astype(bf16)
        from_y.append(wires.copy(sent.at[at], got_y.at[at], to["y"]))
    yield
    for k in range(2):
        from_core[0, k].wait_recv()
    total = wide(own[0]) + wide(got_core[0])
    for one in from_y:
        one.wait_recv()
    return total + wide(got_y[...])


def scatter_pair(wires, to, part, own, got_core, sent, got_y, got_z, diag_y, diag_z):
    size = part.shape[1] // 2
    low, high = pl.ds(0, size), pl.ds(size, size)
    from_core = {j: wires.copy(part.at[4 + j], got_core.at[j], to["core"]) for j in (3, 1, 2, 0)}
    mine = wires.here(part.at[pl.ds(0, 4)], own)
    yield
    mine.wait()
    both = lambda j, at: wide(own[j, at]) + wide(got_core[j, at])
    from_core[3].wait_recv()
    sent[2] = (wide(own[3]) + wide(got_core[3])).astype(bf16)
    via_z = wires.copy(sent.at[2, low], diag_z, to["z"])
    via_y = wires.copy(sent.at[2, high], diag_y, to["y"])
    from_core[1].wait_recv()
    sent[0, high] = both(1, high).astype(bf16)
    y_high = wires.copy(sent.at[0, high], got_y.at[high], to["y"])
    from_core[2].wait_recv()
    sent[1, low] = both(2, low).astype(bf16)
    z_low = wires.copy(sent.at[1, low], got_z.at[low], to["z"])
    yield
    via_z.wait_recv()
    sent[0, low] = (both(1, low) + wide(diag_z[...])).astype(bf16)
    y_low = wires.copy(sent.at[0, low], got_y.at[low], to["y"])
    via_y.wait_recv()
    sent[1, high] = (both(2, high) + wide(diag_y[...])).astype(bf16)
    z_high = wires.copy(sent.at[1, high], got_z.at[high], to["z"])
    yield
    from_core[0].wait_recv()
    total = wide(own[0]) + wide(got_core[0])
    for one in (y_high, z_low, y_low, z_high):
        one.wait_recv()
    return total + wide(got_y[...]) + wide(got_z[...])


def result_of(steps):
    while True:
        try:
            next(steps)
        except StopIteration as done:
            return done.value


def gather_rank(wires, to, block, out):
    size = block.shape[0] // 2
    halves = [pl.ds(0, size), pl.ds(size, size)]
    rank = ranks()
    mine = wires.here(block, out.at[rank[0]])
    from_y = [wires.copy(block.at[h], out.at[rank[0], h], to["y"]) for h in halves]
    from_core = [wires.copy(block, out.at[rank[0]], to["core"])]
    yield
    for h, one in zip(halves, from_y):
        one.wait_recv()
        from_core.append(wires.copy(out.at[rank[2], h], out.at[rank[2], h], to["core"]))
    for one in from_core:
        one.wait_recv()
    mine.wait()


def gather_pair(wires, to, block, out, base):
    size = block.shape[0] // 2
    low, high = pl.ds(0, size), pl.ds(size, size)
    at = lambda j: out.at[base + j]
    from_z = wires.copy(block, at(2), to["z"])
    yield
    from_y = wires.copy(block, at(1), to["y"])
    from_core = [wires.copy(block, at(4), to["core"])]
    yield
    from_y.wait_recv()
    via_z = wires.copy(out.at[base + 1, low], out.at[base + 3, low], to["z"])
    from_core.append(wires.copy(at(1), at(5), to["core"]))
    from_z.wait_recv()
    via_y = wires.copy(out.at[base + 2, high], out.at[base + 3, high], to["y"])
    from_core.append(wires.copy(at(2), at(6), to["core"]))
    yield
    via_z.wait_recv()
    via_y.wait_recv()
    from_core.append(wires.copy(at(3), at(7), to["core"]))
    return from_core


def remote_call(kernel, name, key, args, outs, scratch, copies, in_vmem):
    ins, out_in = in_vmem
    spec = lambda inside: pl.BlockSpec(memory_space=pltpu.VMEM if inside else pl.ANY)
    return pl.pallas_call(
        kernel,
        name=name,
        out_shape=outs,
        in_specs=[spec(x) for x in ins],
        out_specs=[spec(x) for x in out_in],
        scratch_shapes=list(scratch)
        + [
            pltpu.SemaphoreType.DMA((copies,)),
            pltpu.SemaphoreType.DMA((copies,)),
            pltpu.SemaphoreType.DMA((8,)),
        ],
        compiler_params=pltpu.CompilerParams(
            collective_id=key, has_side_effects=True, vmem_limit_bytes=VMEM_LIMIT
        ),
    )(*args)


def kv_gather_kernel(own_ref, out_ref, *sems):
    wires, to = Wires(*sems), partners()
    kind = lax.rem(lax.axis_index("tensor"), 2)
    rows = own_ref.shape[0]
    block = lambda j: out_ref.at[kind, pl.ds(j * rows, rows)]
    meet([to[k] for k in ("core", "z", "far", "last")])
    mine = wires.here(own_ref, block(0))
    arrive = [wires.copy(own_ref, block(j), to[k]) for j, k in ((3, "last"), (2, "far"), (1, "z"))]
    from_core = [wires.copy(own_ref, block(0), to["core"])]
    for j, one in ((1, arrive[2]), (2, arrive[1]), (3, arrive[0])):
        one.wait_recv()
        from_core.append(wires.copy(block(j), block(j), to["core"]))
    for one in from_core:
        one.wait_recv()
    mine.wait()
    wires.finish()


def kv_gather(own):
    rows, width = own.shape
    n_c = lax.axis_size("context")
    return remote_call(
        kv_gather_kernel,
        "kv_gather",
        0,
        [own],
        [jax.ShapeDtypeStruct((2, n_c * rows, width), bf16)],
        [],
        8,
        ([False], [False]),
    )[0]


def kv_scatter_kernel(count, part_ref, *refs):
    args, dkv_ref, outs = refs[: 2 * count], refs[2 * count], refs[2 * count + 1 : 3 * count + 1]
    own, got_core, sent, got = refs[3 * count + 1 : 3 * count + 5]
    wires, to = Wires(*refs[-3:]), partners()
    fill = own_grads(count, args, outs, refs[3 * count + 5 : -3])
    kind = lax.rem(lax.axis_index("tensor"), 2)
    rows = dkv_ref.shape[0]
    block = lambda j: pl.ds(j * rows, rows)
    meet([to[k] for k in ("core", "z", "far", "last")])
    steps = ((3, "last"), (2, "far"), (1, "z"), (0, None))
    from_core = {
        j: wires.copy(part_ref.at[1 - kind, block(j)], got_core.at[block(j)], to["core"])
        for j, _ in steps
    }
    mine = wires.here(part_ref.at[kind], own)
    for one in fill:
        one.fetch(wires)
    mine.wait()
    arrive = []
    for j, k in steps[:3]:
        from_core[j].wait_recv()
        sent[block(j)] = (wide(own[block(j)]) + wide(got_core[block(j)])).astype(bf16)
        arrive.append(wires.copy(sent.at[block(j)], got.at[block(j)], to[k]))
    for one in fill:
        one.make(0, one.tiles)
    from_core[0].wait_recv()
    total = wide(own[block(0)]) + wide(got_core[block(0)])
    for one in arrive:
        one.wait_recv()
    for j in (1, 2, 3):
        total = total + wide(got[block(j)])
    dkv_ref[...] = total
    wires.finish()


def kv_scatter(part, fill, width):
    _, rows, depth = part.shape
    n_c = lax.axis_size("context")
    args, outs, scratch = own_grad_call(fill, width)
    return remote_call(
        functools.partial(kv_scatter_kernel, len(fill)),
        "kv_scatter",
        1,
        [part, *args],
        [jax.ShapeDtypeStruct((rows // n_c, depth), f32), *outs],
        [pltpu.VMEM((rows, depth), bf16)] * 4 + scratch,
        7,
        ([False] * (1 + len(args)), [True] * (1 + len(outs))),
    )


def middle_kernel(
    part,
    x_ref,
    gain_ref,
    dy_ref,
    dy_y,
    dy_z,
    dy_far,
    mid_ref,
    factor_ref,
    out,
    dys,
    own,
    core,
    sent,
    got,
    xn,
    *sems,
):
    wires, to = Wires(*sems), partners()
    blocks = out.shape[0] // 2
    size = xn.shape[0] // 2
    low, high = pl.ds(0, size), pl.ds(size, size)
    meet([to[k] for k in ("core", "y", "z", "far")])
    summed = scatter_rank(wires, to, part, own, core, sent, got)
    next(summed)
    mine = [
        wires.here(block, dys.at[k])
        for block, k in ((dy_ref, 0), (dy_y, 1), (dy_z, 2), (dy_far, blocks))
    ]
    via_z = wires.copy(dy_y.at[low], dys.at[3, low], to["z"])
    dy_last = gather_pair(wires, to, dy_far, dys, blocks)
    next(dy_last)
    next(summed)
    via_y = wires.copy(dy_z.at[high], dys.at[3, high], to["y"])
    ends = [
        wires.copy(block, dys.at[4 + k], to["core"])
        for k, block in enumerate((dy_ref, dy_y, dy_z))
    ]
    next(dy_last)
    middle = wide(x_ref[...]) + result_of(summed)
    mid_ref[...] = middle
    factor = lax.rsqrt(jnp.mean(middle * middle, axis=-1, keepdims=True) + EPSILON)
    factor_ref[...] = factor
    xn[...] = (middle * factor * gain_ref[...]).astype(bf16)
    mine.append(wires.here(xn, out.at[0]))
    xn_far = wires.copy(xn, out.at[blocks], to["far"])
    xn_near = gather_pair(wires, to, xn, out, 0)
    next(xn_near)
    next(xn_near)
    via_z.wait_recv()
    via_y.wait_recv()
    ends.append(wires.copy(dys.at[3], dys.at[7], to["core"]))
    next(dy_last)
    next(xn_near)
    xn_far.wait_recv()
    xn_last = gather_pair(wires, to, out.at[blocks], out, blocks)
    next(xn_last)
    next(xn_last)
    ends += result_of(dy_last) + result_of(xn_near)
    next(xn_last)
    ends += result_of(xn_last)
    for one in ends:
        one.wait_recv()
    for one in mine:
        one.wait()
    wires.finish()


def middle_norm(part, inputs_part, gain, dy_blocks):
    rows, width = inputs_part.shape
    return remote_call(
        middle_kernel,
        "middle_norm",
        2,
        [part.reshape(4, rows, width), inputs_part, gain, *dy_blocks],
        [
            jax.ShapeDtypeStruct((rows, width), f32),
            jax.ShapeDtypeStruct((rows, 1), f32),
            jax.ShapeDtypeStruct((16, rows, width), bf16),
            jax.ShapeDtypeStruct((16, rows, width), bf16),
        ],
        [
            pltpu.VMEM((2, rows, width), bf16),
            pltpu.VMEM((2, rows, width), bf16),
            pltpu.VMEM((rows, width), bf16),
            pltpu.VMEM((rows, width), bf16),
            pltpu.VMEM((rows, width), bf16),
        ],
        48,
        ([False] + [True] * 6, [True, True, False, False]),
    )


def norm_back_rows(values, factor, gain, grad_normed):
    gained = gain * grad_normed
    inner = jnp.mean(gained * values, axis=-1, keepdims=True)
    grad_values = factor * gained - values * (factor * factor * factor) * inner
    return grad_values, jnp.sum(grad_normed * values * factor, axis=0, keepdims=True)


def middle_back_kernel(count, part, mid_ref, factor_ref, gain_ref, dy_ref, *refs):
    args, refs = refs[: 2 * count], refs[2 * count :]
    got_ref, refs = (refs[0], refs[1:]) if count else (None, refs)
    (dmid_ref, dgain_ref, out), refs = refs[:3], refs[3:]
    outs, refs = refs[:count], refs[count:]
    (upper_ref, lower_ref, far_ref), refs = (
        (refs[:3], refs[3:]) if count else ((None, None, None), refs)
    )
    low, first, wires, to = refs[0], refs[1:8], Wires(*refs[-3:]), partners()
    fill = own_grads(count, args, outs, refs[8:-3])
    meet([to[k] for k in ("core", "y", "z")])
    back = scatter_pair(wires, to, part, *first)
    next(back)
    for one in fill:
        one.fetch(wires)
    next(back)
    if fill:
        fill[0].make(0, 1)
    next(back)
    if fill:
        fill[0].make(1, fill[0].tiles)
        cut = upper_ref.shape[0]
        upper_ref[...] = (wide(outs[0][:cut]) + wide(got_ref[:cut])).astype(bf16)
        near_half = wires.copy(upper_ref, far_ref, to["z"])
        lower_ref[...] = (wide(outs[0][cut:]) + wide(got_ref[cut:])).astype(bf16)
    grad_normed = result_of(back)
    du, dgain = norm_back_rows(mid_ref[...], factor_ref[...], gain_ref[...], grad_normed)
    dgain_ref[...] = dgain
    dmid = wide(dy_ref[...]) + du
    low[...] = dmid.astype(bf16)
    share = gather_rank(wires, to, low, out)
    next(share)
    dmid_ref[...] = dmid
    for one in fill[1:]:
        one.make(0, one.tiles)
    result_of(share)
    if fill:
        near_half.wait_recv()
    wires.finish()


def pair_scratch(rows, width):
    return [
        pltpu.VMEM((4, rows, width), bf16),
        pltpu.VMEM((4, rows, width), bf16),
        pltpu.VMEM((3, rows, width), bf16),
        pltpu.VMEM((rows, width), bf16),
        pltpu.VMEM((rows, width), bf16),
        pltpu.VMEM((rows // 2, width), bf16),
        pltpu.VMEM((rows // 2, width), bf16),
    ]


def middle_back(part, middle, factor, gain, dy_part, fill, got, shard):
    rows, width = middle.shape
    args, outs, scratch = own_grad_call(fill, shard)
    if fill:
        args = [*args, got]
        units = got.shape[0]
        cut = units // 64 * 16
        outs = [*outs, *(jax.ShapeDtypeStruct((n, shard), bf16) for n in (cut, units - cut, cut))]
    return remote_call(
        functools.partial(middle_back_kernel, len(fill)),
        "middle_back",
        3,
        [part.reshape(8, rows, width), middle, factor, gain, dy_part, *args],
        [
            jax.ShapeDtypeStruct((rows, width), f32),
            jax.ShapeDtypeStruct((1, width), f32),
            jax.ShapeDtypeStruct((4, rows, width), bf16),
            *outs,
        ],
        [pltpu.VMEM((rows, width), bf16)] + pair_scratch(rows, width) + scratch,
        16,
        (
            [False] + [True] * 4 + ([False] * (len(args) - 1) + [True] if fill else []),
            [True, True, False] + ([True] * (len(outs) - 1) + [False] if fill else []),
        ),
    )


def add_all(wires, ways, value, slots):
    for k, device in enumerate(ways):
        one = wires.copy(value, slots.at[k], device)
        one.wait()
        wires.started = [x for x in wires.started if x is not one]
        value[...] = value[...] + slots[k]


def input_back_kernel(
    part, x_ref, factor_ref, gain_ref, dmid_ref, small_ref, sum_ref, out, *rest
):
    low, own, core, sent, got, slots = rest[:-3]
    wires, to = Wires(*rest[-3:]), partners()
    meet([to[k] for k in ("core", "y")])
    grad_normed = result_of(scatter_rank(wires, to, part, own, core, sent, got))
    du, dgain = norm_back_rows(wide(x_ref[...]), factor_ref[...], gain_ref[...], grad_normed)
    low[...] = (dmid_ref[...] + du).astype(bf16)
    share = gather_rank(wires, to, low, out)
    next(share)
    width = dgain.shape[1]
    sum_ref[:, width:] = small_ref[:, width:]
    sum_ref[:, :width] = dgain
    add_all(wires, [to["core"], to["y"]], sum_ref, slots)
    result_of(share)
    wires.finish()


def input_back(part, inputs_part, factor, gain, grad_middle, small):
    rows, width = inputs_part.shape
    return remote_call(
        input_back_kernel,
        "input_back",
        5,
        [part.reshape(4, rows, width), inputs_part, factor, gain, grad_middle, small],
        [
            jax.ShapeDtypeStruct(small.shape, f32),
            jax.ShapeDtypeStruct((4, rows, width), bf16),
        ],
        [
            pltpu.VMEM((rows, width), bf16),
            pltpu.VMEM((2, rows, width), bf16),
            pltpu.VMEM((2, rows, width), bf16),
            pltpu.VMEM((rows, width), bf16),
            pltpu.VMEM((rows, width), bf16),
            pltpu.VMEM((2,) + small.shape, f32),
        ],
        16,
        ([False, True, True, True, True, True], [True, False]),
    )


def context_sum_kernel(over_f, *refs):
    parts, small_ref, out_part, mid_ref = refs[:3], refs[3], refs[4], refs[5]
    outs, sum_ref, shared, outputs = refs[6:8], refs[8], refs[9], refs[10]
    lows, from_end, from_middle = refs[11:15], refs[15:19], refs[19:23]
    out_low, slot, scratch = refs[23], refs[24], refs[25:32]
    wires, to, c = Wires(*refs[32:]), partners(), lax.axis_index("context")
    end = (c == 0) | (c == lax.axis_size("context") - 1)
    inner = jnp.logical_not(end)
    greet = ["core", "y", "z", "last"]
    if over_f:
        to["f"] = {"fsdp": 1 - lax.axis_index("fsdp")}
        greet.append("f")
    meet([to[k] for k in greet])
    ahead = scatter_pair(wires, to, out_part, *scratch)
    next(ahead)
    sum_ref[...] = small_ref[...]
    from_f = wires.copy(small_ref, slot, to["f"]) if over_f else None
    next(ahead)
    sources = [*parts, sum_ref]
    chunks = []
    for i, cuts in ((2, 1), (0, 2), (1, 4), (3, 1)):
        size = sources[i].shape[0] // cuts
        chunks += [(i, pl.ds(k * size, size)) for k in range(cuts)]
    inward = [wires.plan(sources[i].at[at], from_end[i].at[at], to["z"]) for i, at in chunks]
    across = [wires.plan(lows[i].at[at], from_middle[i].at[at], to["last"]) for i, at in chunks]
    outward = [wires.plan(lows[i].at[at], lows[i].at[at], to["z"]) for i, at in chunks]
    small = len(chunks) - 1

    def send_in(k):
        @pl.when(end)
        def _():
            inward[k].start()

    def pass_on(first, past):
        @pl.when(inner)
        def _():
            for k in range(first, past):
                i, at = chunks[k]
                inward[k].wait_recv()
                total = wide(sources[i][at]) + wide(from_end[i][at])
                lows[i][at] = total.astype(lows[i].dtype)
                across[k].start()
                if k:
                    send_out(k - 1)

    def send_out(k):
        i, at = chunks[k]
        across[k].wait()
        lows[i][at] = (wide(lows[i][at]) + wide(from_middle[i][at])).astype(lows[i].dtype)
        outward[k].start()

    send_in(0)
    send_in(1)
    next(ahead)
    if over_f:
        from_f.wait_recv()
        sum_ref[...] = sum_ref[...] + slot[...]
    for k in range(2, small + 1):
        send_in(k)
    pass_on(0, 2)
    out_low[...] = (mid_ref[...] + result_of(ahead)).astype(bf16)
    out_share = gather_rank(wires, to, out_low, outputs)
    next(out_share)
    pass_on(2, small + 1)

    @pl.when(inner)
    def _():
        send_out(small)

    result_of(out_share)

    def arrived(k):
        @pl.when(end)
        def _():
            outward[k].wait_recv()

    arrived(0)
    share = gather_rank(wires, to, lows[2], shared)
    next(share)
    for k in range(1, len(chunks)):
        arrived(k)

    @pl.when(end)
    def _():
        for one in inward:
            one.wait_send()

    for i in (0, 1):
        outs[i][...] = wide(lows[i][...])
    sum_ref[...] = lows[3][...]
    result_of(share)

    @pl.when(inner)
    def _():
        for one in outward:
            one.wait_send()

    wires.finish()


def context_sum(over_f, parts, small, out_part, middle):
    rows, width = middle.shape
    lines = [pltpu.VMEM(x.shape, x.dtype) for x in (*parts, small)]
    return remote_call(
        functools.partial(context_sum_kernel, over_f),
        "context_sum",
        6,
        [*parts, small, out_part.reshape(8, rows, width), middle],
        [jax.ShapeDtypeStruct(x.shape, f32) for x in parts[:2]]
        + [jax.ShapeDtypeStruct(small.shape, f32)]
        + [jax.ShapeDtypeStruct((4,) + parts[2].shape, bf16)]
        + [jax.ShapeDtypeStruct((4, rows, width), bf16)],
        lines * 3
        + [pltpu.VMEM((rows, width), bf16), pltpu.VMEM(small.shape, f32)]
        + pair_scratch(rows, width),
        48,
        ([True] * 4 + [False, True], [True] * 3 + [False] * 2),
    )


def build(n_f, n_c, n_t):
    def flip(x, axis, bit):
        size = {"fsdp": n_f, "context": n_c, "tensor": n_t}[axis]
        return lax.ppermute(x, axis, [(i, i ^ bit) for i in range(size)])

    def by_bit(bit, x, other, axis):
        return jnp.where(
            bit == 0,
            jnp.concatenate([x, other], axis=axis),
            jnp.concatenate([other, x], axis=axis),
        )

    def after(x, *others):
        return lax.optimization_barrier((x, others))[0]

    def local(
        inputs,
        cotangent,
        blocks,
        attn_gain,
        w_query,
        b_query,
        w_key,
        b_key,
        w_value,
        b_value,
        w_out,
        ffn_gain,
        w_gate,
        w_up,
        w_down,
    ):
        rows, width = inputs.shape
        f = lax.axis_index("fsdp")
        c = lax.axis_index("context")
        t = lax.axis_index("tensor")
        core, parity, pair = t % 2, c % 2, c // 2
        heads = w_query.shape[1] // HD
        group = (t * heads) // (H // KV)
        part = rows // n_t
        units_all = w_gate.shape[1]
        units = units_all // 2

        def gather_f(x, axis):
            if n_f == 2:
                return by_bit(f, x, flip(x, "fsdp", 1), axis)
            return lax.all_gather(x, "fsdp", axis=axis, tiled=True)

        def grad_far(left, right, side):
            if n_f > 2:
                return None
            source = (left, right)[side]
            half = width // 2
            far = lax.dynamic_slice_in_dim(source, (1 - f) * half, half, 1)
            return (dot_rows(far, right) if side == 0 else dot_rows(left, far)).astype(bf16)

        def grad_sum(left, right, side, far, late):
            if n_f > 2:
                return lax.psum_scatter(
                    dot_rows(left, right).astype(bf16), "fsdp", scatter_dimension=side, tiled=True
                )
            source = (left, right)[side]
            half = width // 2
            own = lax.dynamic_slice_in_dim(source, f * half, half, 1)
            own = dot_rows(own, right) if side == 0 else dot_rows(left, own)
            return (own + after(flip(far, "fsdp", 1), late).astype(f32)).astype(bf16)

        small = jnp.concatenate(
            [v.reshape(1, -1) for v in (attn_gain, ffn_gain, b_query, b_key, b_value)], axis=1
        )
        column = lambda w: lax.dynamic_slice_in_dim(w, group * HD, HD, 1)
        w_kv_own = jnp.where(core == 0, column(w_key), column(w_value))
        pieces_f = lambda x, axis: (
            [x, flip(x, "fsdp", 1)]
            if n_f == 2
            else [lax.all_gather(x, "fsdp", axis=axis, tiled=True)]
        )
        meta = jnp.stack([f, 1 - f, core, pair]).astype(jnp.int32)
        w_q = pieces_f(w_query, 0)
        w_kv = pieces_f(w_kv_own, 0)
        small = gather_f(small, 0)
        w_out_all = gather_f(after(w_out, small, w_q, w_kv), 1)
        piece = attn_gain.shape[0]
        gain_first = small[:, :piece].reshape(1, width).astype(f32)
        gain_second = small[:, piece : 2 * piece].reshape(1, width).astype(f32)
        bias_of = lambda lo, n: (
            small[:, lo : lo + n * (HD // n_f)]
            .reshape(n_f, n, HD // n_f)
            .transpose(1, 0, 2)
            .reshape(n, HD)
            .astype(f32)
        )
        at = 2 * piece
        bq = bias_of(at, heads)
        bk = bias_of(at + heads * (HD // n_f), KV)
        bv = bias_of(at + (heads + KV) * (HD // n_f), KV)
        b_kv = lax.dynamic_index_in_dim(jnp.where(core == 0, bk, bv), group, 0)

        unit_slice = lambda w: lax.dynamic_slice_in_dim(w, parity * units, units, 0)
        own_gate_up = jnp.concatenate(
            [unit_slice(after(w, w_kv_own)) for w in (w_gate.T, w_up.T)], axis=0
        )
        own_down = unit_slice(w_down)

        dy_part = lax.dynamic_slice_in_dim(cotangent, t * part, part, 0)

        seq_blocks = blocks[0].reshape(n_c, -1)
        own_blocks = seq_blocks.shape[1]
        key_blocks = jnp.concatenate(
            [lax.dynamic_index_in_dim(seq_blocks, c ^ j, 0, keepdims=False) for j in range(n_c)]
        )
        positions = (
            key_blocks[:own_blocks, None] * BLOCK + jnp.arange(BLOCK, dtype=jnp.int32)[None, :]
        ).reshape(-1)
        cosine, sine = rope_tables(positions)
        bias = jnp.concatenate([bq.reshape(1, -1), b_kv], axis=1)
        dy_blocks = [
            dy_part,
            flip(dy_part, "tensor", 2),
            flip(dy_part, "context", 1),
            flip(dy_part, "context", 2),
        ]
        inputs_part = lax.dynamic_slice_in_dim(inputs, t * part, part, 0)
        bias = after(bias, dy_blocks[2:], own_gate_up, own_down, inputs_part)
        normed, factor_first, queries, kv_own = qkv(
            meta, inputs, gain_first, bias, cosine, sine, w_q, w_kv
        )
        kv = after(kv_gather(kv_own), w_out_all)
        far_gate_up = pieces_f(after(own_gate_up, kv), 1)[-1]
        w_gate_up = [own_gate_up, far_gate_up] if n_f == 2 else [far_gate_up]
        far_down = pieces_f(after(own_down, kv), 1)[-1]
        w_downs = [own_down, far_down] if n_f == 2 else [far_down]
        attended, lse = attention(key_blocks, queries, kv)
        middle, factor_second, normed2, dy_all = middle_norm(
            dot(attended, w_out_all).astype(bf16), inputs_part, gain_second, dy_blocks
        )

        hidden, slope, gated, *down_far = hidden_units(meta, normed2, dy_all, w_gate_up)
        grad_gate, grad_up, dx_part, out_part, *unit_far = hidden_back(
            meta, normed2, dy_all, hidden, slope, gated, w_gate_up, w_downs
        )
        unit_far = [*down_far, *unit_far]
        flat = lambda x: x.reshape(-1, width)
        if n_f == 2:
            down_got, gate_got, up_got = (flip(x, "fsdp", 1) for x in unit_far)
            early = [(hidden, flat(dy_all)), (grad_gate, flat(normed2))]
            later = [(grad_up, flat(normed2))]
        else:
            over_f = lambda x: lax.psum_scatter(x, "fsdp", scatter_dimension=1, tiled=True)
            owns = [
                over_f(unit_grads(meta, 0, 1, x, [unit]))
                for x, unit in ((dy_all, hidden), (normed2, grad_gate), (normed2, grad_up))
            ]
            down_got = gate_got = up_got = jnp.zeros_like(owns[0])
            early = later = []

        def unit_whole(own, other):
            own, other = (jnp.concatenate(x, axis=0) for x in (own, other))
            return by_bit(parity, own, other, 0).astype(f32)

        grad_middle, ffn_gain_grad, grad_middle_low, *first_owns = middle_back(
            dx_part, middle, factor_second, gain_second, dy_part, early, down_got, width // n_f
        )
        grad_middle_low = grad_middle_low.reshape(rows, width)
        add = lambda own, got: (own.astype(f32) + got.astype(f32)).astype(bf16)
        upper = units // 2
        if n_f == 2:
            _, gate_own, down_upper, down_lower, far_upper = first_owns
        else:
            down_low, gate_own = owns[:2]
            down_upper, down_lower = down_low[:upper], down_low[upper:]
            far_upper = flip(down_upper, "context", 1)
        gate_got = after(gate_got, grad_middle_low)
        gate_low = add(gate_own, gate_got)
        far_lower = flip(down_lower, "context", 1)
        grad_middle_low = after(grad_middle_low, gate_low)
        grad_attended = dot_cols(grad_middle_low, w_out_all).astype(bf16)

        dq_low, dkv = attention_back(key_blocks, queries, grad_attended, lse, cosine, sine, kv)
        attention_args = [(attended, after(grad_middle_low, dq_low), 1), (normed, dq_low, 0)]
        fars = [grad_far(*args) for args in attention_args]
        dkv, *last_owns = kv_scatter(
            after(dkv, fars), later, width // n_f
        )
        (up_own,) = last_owns or owns[2:]
        far_gate = flip(after(gate_low, dkv, far_lower), "context", 1)
        up_got = after(up_got, dkv)
        up_low = add(up_own, up_got)
        dkv = after(dkv, up_low, far_lower)
        dkv_low = jnp.where(core == 0, rotate_back(dkv, cosine, sine), dkv).astype(bf16)
        attention_args.append((normed, dkv_low, 0))
        fars.append(grad_far(*attention_args[-1]))
        dkv_low = after(dkv_low, fars)
        factor_part = lax.dynamic_slice_in_dim(factor_first, t * part, part, 0)
        own_biases = jnp.sum(
            jnp.concatenate([dq_low, dkv_low], axis=1).astype(f32), axis=0, keepdims=True
        )
        slots = lax.dynamic_update_slice(
            jnp.zeros((n_t, (heads + 1) * HD), f32), own_biases, (t, 0)
        )
        small_grads = jnp.concatenate(
            [jnp.zeros((1, width), f32), ffn_gain_grad, slots.reshape(1, -1)], axis=1
        )
        grad_qkv = qkv_back(meta, dq_low, dkv_low, w_q, w_kv)
        far_up = flip(after(up_low, dkv_low), "context", 1)
        small_grads, input_grad = input_back(
            grad_qkv,
            inputs_part,
            factor_part,
            gain_first,
            grad_middle,
            small_grads,
        )
        input_grad = input_grad.reshape(rows, width)
        if n_f > 2:
            small_grads = lax.psum(small_grads, "fsdp")
        zero = jnp.minimum(t, 0).astype(bf16)
        input_grad = input_grad + zero
        small_grads = after(small_grads, far_gate)
        attention_parts = [
            grad_sum(*args, far, small_grads) for args, far in zip(attention_args, fars)
        ]
        wd_grad = unit_whole(
            *after(((down_upper, down_lower), (far_upper, far_lower)), small_grads)
        )
        wg_grad = unit_whole(*after(((gate_low,), (far_gate,)), small_grads))
        small_grads, wd_grad, wg_grad, input_grad = lax.optimization_barrier(
            (small_grads, wd_grad, wg_grad, input_grad)
        )
        wo_grad, wq_grad, packed, wkv_all, outputs = context_sum(
            n_f == 2, attention_parts, small_grads, out_part, middle
        )
        wo_grad, wq_grad, packed, wkv_all, outputs, far_up = lax.optimization_barrier(
            (wo_grad, wq_grad, packed, wkv_all, outputs, far_up)
        )
        outputs = outputs.reshape(rows, width)
        wkv_all = wkv_all.astype(f32)
        wk_grad = jnp.concatenate([wkv_all[0], wkv_all[2]], axis=1)
        wv_grad = jnp.concatenate([wkv_all[1], wkv_all[3]], axis=1)
        packed = packed[0]
        attn_gain_grad = lax.dynamic_slice_in_dim(packed, f * piece, piece, 0)
        ffn_gain_grad = lax.dynamic_slice_in_dim(packed, width + f * piece, piece, 0)
        slots = packed[2 * width :].reshape(n_t, heads + 1, HD)
        slots = lax.dynamic_slice_in_dim(slots, f * (HD // n_f), HD // n_f, 2)
        bq_out = lax.dynamic_index_in_dim(slots, t, 0, keepdims=False)[:heads]
        bk_out = slots[0::2, heads]
        bv_out = slots[1::2, heads]

        wu_grad = unit_whole((up_low,), (far_up,))
        wg_grad, wu_grad = wg_grad.T, wu_grad.T

        return (
            outputs,
            input_grad,
            attn_gain_grad,
            wq_grad,
            bq_out,
            wk_grad,
            bk_out,
            wv_grad,
            bv_out,
            wo_grad,
            ffn_gain_grad,
            wg_grad,
            wu_grad,
            wd_grad,
        )

    return local


def solution(mesh):
    in_specs = (
        P(("fsdp", "context"), None),
        P(("fsdp", "context"), None),
        P("fsdp", None),
        P("fsdp"),
        P("fsdp", "tensor"),
        P("tensor", "fsdp"),
        P("fsdp", None),
        P(None, "fsdp"),
        P("fsdp", None),
        P(None, "fsdp"),
        P("tensor", "fsdp"),
        P("fsdp"),
        P("fsdp", "tensor"),
        P("fsdp", "tensor"),
        P("tensor", "fsdp"),
    )
    out_specs = (
        P(("fsdp", "context"), None),
        P(("fsdp", "context"), None),
        P("fsdp"),
        P("fsdp", "tensor"),
        P("tensor", "fsdp"),
        P("fsdp", None),
        P(None, "fsdp"),
        P("fsdp", None),
        P(None, "fsdp"),
        P("tensor", "fsdp"),
        P("fsdp"),
        P("fsdp", "tensor"),
        P("fsdp", "tensor"),
        P("tensor", "fsdp"),
    )
    local = build(mesh.shape["fsdp"], mesh.shape["context"], mesh.shape["tensor"])
    return jax.shard_map(local, mesh=mesh, in_specs=in_specs, out_specs=out_specs, check_vma=False)
```

```python
import functools

import jax
import jax.numpy as jnp
from jax import lax
from jax.experimental import pallas as pl
from jax.experimental.pallas import tpu as pltpu
from jax.sharding import PartitionSpec as P

H = 12
KV = 2
HD = 128
BLOCK = 256

EPSILON = 1e-06
ROPE_BASE = 1000000.0
MASKED = -1e30
SCALING = HD ** (-0.5)
LANES = 128
VMEM_LIMIT = 60 << 20

f32 = jnp.float32
bf16 = jnp.bfloat16


def rope_tables(positions):
    halfway = HD // 2
    frequency = ROPE_BASE ** (-(jnp.arange(halfway, dtype=f32) * 2.0 / HD))
    angles = positions.astype(f32)[:, None] * frequency[None, :]
    cosine, sine = jnp.cos(angles), jnp.sin(angles)
    return (jnp.concatenate([cosine, cosine], axis=1), jnp.concatenate([sine, sine], axis=1))


def rotate(field, cosine, sine):
    halfway = HD // 2
    turned = jnp.concatenate([-field[..., halfway:], field[..., :halfway]], axis=-1)
    return field * cosine + turned * sine


def rotate_back(grad_field, cosine, sine):
    halfway = HD // 2
    moved = grad_field * sine
    turned = jnp.concatenate([moved[..., halfway:], -moved[..., :halfway]], axis=-1)
    return grad_field * cosine + turned


def dot(left, right):
    return jnp.dot(left, right, preferred_element_type=f32)


def dot_rows(left, right):
    return lax.dot_general(left, right, (((0,), (0,)), ((), ())), preferred_element_type=f32)


def dot_cols(left, right):
    return lax.dot_general(left, right, (((1,), (1,)), ((), ())), preferred_element_type=f32)


def mask_row(kb_ref, own_block, key_blocks):
    return jnp.concatenate(
        [
            jnp.full((1, BLOCK), jnp.where(kb_ref[j] <= own_block, 0.0, MASKED), f32)
            for j in range(key_blocks)
        ],
        axis=1,
    )


def attention_kernel(key_blocks, kb_ref, q_ref, k_ref, v_ref, o_ref, lse_ref):
    bias = mask_row(kb_ref, kb_ref[pl.program_id(1)], key_blocks)
    scores = dot_cols(q_ref[...], k_ref[...]) * SCALING + bias
    row_max = jnp.max(scores, axis=1, keepdims=True)
    expo = jnp.exp(scores - row_max)
    total = jnp.sum(expo, axis=1, keepdims=True)
    probability = (expo * (1.0 / total)).astype(bf16)
    o_ref[...] = dot(probability, v_ref[...]).astype(bf16)
    lse_ref[0] = row_max + jnp.log(total)


def attention(key_blocks, queries, kv):
    rows, width = queries.shape
    heads = width // HD
    whole = lambda kind: pl.BlockSpec((None,) + kv.shape[1:], lambda h, i, kb: (kind, 0, 0))
    tile = pl.BlockSpec((BLOCK, HD), lambda h, i, kb: (i, h))
    return pl.pallas_call(
        functools.partial(attention_kernel, kv.shape[1] // BLOCK),
        name="attention",
        grid_spec=pltpu.PrefetchScalarGridSpec(
            num_scalar_prefetch=1,
            grid=(heads, rows // BLOCK),
            in_specs=[tile, whole(0), whole(1)],
            out_specs=[tile, pl.BlockSpec((1, BLOCK, 1), lambda h, i, kb: (h, i, 0))],
        ),
        out_shape=[
            jax.ShapeDtypeStruct((rows, width), bf16),
            jax.ShapeDtypeStruct((heads, rows, 1), f32),
        ],
        compiler_params=pltpu.CompilerParams(vmem_limit_bytes=VMEM_LIMIT),
    )(key_blocks, queries, kv, kv)


def attention_back_kernel(
    key_blocks,
    kb_ref,
    q_ref,
    do_ref,
    lse_ref,
    cos_ref,
    sin_ref,
    k_ref,
    v_ref,
    dq_ref,
    dkv_ref,
    dk_ref,
    dv_ref,
):
    head, i = pl.program_id(0), pl.program_id(1)

    @pl.when((head == 0) & (i == 0))
    def _():
        dk_ref[...] = jnp.zeros_like(dk_ref)
        dv_ref[...] = jnp.zeros_like(dv_ref)

    bias = mask_row(kb_ref, kb_ref[i], key_blocks)
    scores = dot_cols(q_ref[...], k_ref[...]) * SCALING + bias
    probability = jnp.exp(scores - lse_ref[0])
    grad_probs = dot_cols(do_ref[...], v_ref[...])
    inner = jnp.sum(probability * grad_probs, axis=1, keepdims=True)
    grad_scores = (probability * (grad_probs - inner)).astype(bf16)
    grad_query = dot(grad_scores, k_ref[...]) * SCALING
    moved = grad_query * sin_ref[...]
    sign = jnp.where(lax.broadcasted_iota(jnp.int32, moved.shape, 1) < HD // 2, 1.0, -1.0)
    dq_ref[...] = (
        grad_query * cos_ref[...] + pltpu.roll(moved, HD // 2, 1) * sign
    ).astype(bf16)
    dk_ref[...] += dot_rows(grad_scores, q_ref[...]) * SCALING
    dv_ref[...] += dot_rows(probability.astype(bf16), do_ref[...])

    @pl.when((head == pl.num_programs(0) - 1) & (i == pl.num_programs(1) - 1))
    def _():
        dkv_ref[0] = dk_ref[...].astype(bf16)
        dkv_ref[1] = dv_ref[...].astype(bf16)


def attention_back(key_blocks, queries, grad_out, lse, cosine, sine, kv):
    rows, width = queries.shape
    heads = width // HD
    whole = lambda kind: pl.BlockSpec((None,) + kv.shape[1:], lambda h, i, kb: (kind, 0, 0))
    tile = pl.BlockSpec((BLOCK, HD), lambda h, i, kb: (i, h))
    table = pl.BlockSpec((BLOCK, HD), lambda h, i, kb: (i, 0))
    return pl.pallas_call(
        functools.partial(attention_back_kernel, kv.shape[1] // BLOCK),
        name="attention_back",
        grid_spec=pltpu.PrefetchScalarGridSpec(
            num_scalar_prefetch=1,
            grid=(heads, rows // BLOCK),
            in_specs=[
                tile,
                tile,
                pl.BlockSpec((1, BLOCK, 1), lambda h, i, kb: (h, i, 0)),
                table,
                table,
                whole(0),
                whole(1),
            ],
            out_specs=[tile, pl.BlockSpec(kv.shape, lambda h, i, kb: (0, 0, 0))],
            scratch_shapes=[pltpu.VMEM(kv.shape[1:], f32)] * 2,
        ),
        out_shape=[
            jax.ShapeDtypeStruct((rows, width), bf16),
            jax.ShapeDtypeStruct(kv.shape, bf16),
        ],
        compiler_params=pltpu.CompilerParams(vmem_limit_bytes=VMEM_LIMIT),
    )(key_blocks, queries, grad_out, lse, cosine, sine, kv, kv)


def qkv_kernel(pieces, meta_ref, x_ref, gain_ref, bias_ref, cos_ref, sin_ref, *refs):
    weights, (xn_ref, q_ref, kv_ref) = refs[: 2 * pieces], refs[2 * pieces :]
    values = x_ref[...].astype(f32)
    factor = lax.rsqrt(jnp.mean(values * values, axis=-1, keepdims=True) + EPSILON)
    xn_ref[...] = (values * factor * gain_ref[...]).astype(bf16)
    depth = weights[0].shape[0]
    normed = [xn_ref[:, columns_of(meta_ref, j, depth, pieces)] for j in range(pieces)]
    cosine, sine = cos_ref[...], sin_ref[...]
    sign = jnp.where(lax.broadcasted_iota(jnp.int32, cosine.shape, 1) < HD // 2, -1.0, 1.0)
    sine = sine * sign
    width = q_ref.shape[1]
    total = bias_ref[:, :width] + sum(dot(x, w[...]) for x, w in zip(normed, weights[:pieces]))
    turn = lambda own: own * cosine + pltpu.roll(own, HD // 2, 1) * sine
    for h in range(width // HD):
        q_ref[:, h * HD : (h + 1) * HD] = turn(total[:, h * HD : (h + 1) * HD]).astype(bf16)
    own = bias_ref[:, width:] + sum(dot(x, w[...]) for x, w in zip(normed, weights[pieces:]))
    kv_ref[...] = jnp.where(meta_ref[2] == 0, turn(own), own).astype(bf16)


def columns_of(meta_ref, j, depth, pieces):
    if pieces == 1:
        return slice(None)
    return pl.ds(pl.multiple_of(meta_ref[j] * depth, LANES), depth)


def qkv(meta, inputs, gain, bias, cosine, sine, w_q, w_kv):
    rows, width = inputs.shape
    out = w_q[0].shape[1]
    tile = 256
    row = lambda n: pl.BlockSpec((tile, n), lambda i, m: (i, 0))
    fixed = lambda w: pl.BlockSpec(w.shape, lambda i, m: (0, 0))
    return pl.pallas_call(
        functools.partial(qkv_kernel, len(w_q)),
        name="qkv",
        grid_spec=pltpu.PrefetchScalarGridSpec(
            num_scalar_prefetch=1,
            grid=(rows // tile,),
            in_specs=[row(width), fixed(gain), fixed(bias), row(HD), row(HD)]
            + [fixed(w) for w in (*w_q, *w_kv)],
            out_specs=[row(width), row(out), row(HD)],
        ),
        out_shape=[
            jax.ShapeDtypeStruct((rows, width), bf16),
            jax.ShapeDtypeStruct((rows, out), bf16),
            jax.ShapeDtypeStruct((rows, HD), bf16),
        ],
        compiler_params=pltpu.CompilerParams(vmem_limit_bytes=VMEM_LIMIT),
    )(meta, inputs, gain, bias, cosine, sine, *w_q, *w_kv)


def qkv_back_kernel(pieces, meta_ref, dq_ref, dkv_ref, *refs):
    w_q, w_kv, out_ref = refs[:pieces], refs[pieces : 2 * pieces], refs[-1]
    for j in range(pieces):
        out_ref[:, columns_of(meta_ref, j, w_q[j].shape[0], pieces)] = (
            dot_cols(dq_ref[...], w_q[j][...]) + dot_cols(dkv_ref[...], w_kv[j][...])
        ).astype(bf16)


def qkv_back(meta, grad_q, grad_kv, w_q, w_kv):
    rows, width = grad_q.shape[0], sum(w.shape[0] for w in w_q)
    tile = 256
    row = lambda n: pl.BlockSpec((tile, n), lambda i, m: (i, 0))
    fixed = lambda w: pl.BlockSpec(w.shape, lambda i, m: (0, 0))
    return pl.pallas_call(
        functools.partial(qkv_back_kernel, len(w_q)),
        name="qkv_back",
        grid_spec=pltpu.PrefetchScalarGridSpec(
            num_scalar_prefetch=1,
            grid=(rows // tile,),
            in_specs=[row(grad_q.shape[1]), row(HD)] + [fixed(w) for w in (*w_q, *w_kv)],
            out_specs=row(width),
        ),
        out_shape=jax.ShapeDtypeStruct((rows, width), bf16),
        compiler_params=pltpu.CompilerParams(vmem_limit_bytes=VMEM_LIMIT),
    )(meta, grad_q, grad_kv, *w_q, *w_kv)


def add_rows(unit_refs, row_refs, columns, totals, outs):
    step = pl.program_id(0)

    @pl.when(step == 0)
    def _():
        for total in totals:
            total[...] = jnp.zeros_like(total)

    for total, unit, row in zip(totals, unit_refs, row_refs):
        total[...] += dot_rows(unit[...], row[:, columns])

    @pl.when(step == pl.num_programs(0) - 1)
    def _():
        for out, total in zip(outs, totals):
            out[...] = total[...].astype(bf16)


def hidden_kernel(pieces, meta_ref, x_ref, dy_ref, *refs):
    wg, wu, refs = refs[:pieces], refs[pieces : 2 * pieces], refs[2 * pieces :]
    hid_ref, slope_ref, gated_ref = refs[:3]
    columns = [columns_of(meta_ref, j, wg[j].shape[1], pieces) for j in range(pieces)]
    gate = sum(dot_cols(x_ref[:, at], w[...]) for at, w in zip(columns, wg))
    up = sum(dot_cols(x_ref[:, at], w[...]) for at, w in zip(columns, wu))
    sigma = 1.0 / (1.0 + jnp.exp(-gate))
    gated = gate * sigma
    hid_ref[...] = (gated * up).astype(bf16)
    slope_ref[...] = (up * (sigma + gated * (1.0 - sigma))).astype(bf16)
    gated_ref[...] = gated.astype(bf16)
    if pieces == 2:
        add_rows([hid_ref], [dy_ref], columns[1], refs[4:], refs[3:4])


def hidden_back_kernel(pieces, meta_ref, x_ref, dy_ref, hid_ref, slope_ref, gated_ref, *refs):
    wg, wu, wd = (refs[m * pieces : (m + 1) * pieces] for m in range(3))
    refs = refs[3 * pieces :]
    dg_ref, du_ref, dx_ref, out_ref = refs[:4]
    columns = [columns_of(meta_ref, j, wg[j].shape[1], pieces) for j in range(pieces)]
    grad_hidden = sum(dot_cols(dy_ref[:, at], w[...]) for at, w in zip(columns, wd))
    dg_ref[...] = (grad_hidden * slope_ref[...].astype(f32)).astype(bf16)
    du_ref[...] = (grad_hidden * gated_ref[...].astype(f32)).astype(bf16)

    @pl.when(pl.program_id(0) // (pl.num_programs(0) // 2) == meta_ref[3])
    def _():
        for at, g, u, d in zip(columns, wg, wu, wd):
            dx_ref[:, at] = (dot(dg_ref[...], g[...]) + dot(du_ref[...], u[...])).astype(bf16)
            out_ref[:, at] = dot(hid_ref[...], d[...]).astype(bf16)

    if pieces == 2:
        add_rows([dg_ref, du_ref], [x_ref, x_ref], columns[1], refs[6:], refs[4:6])


def hidden_specs(meta, normed, weights):
    width = normed.shape[-1]
    rows = normed.shape[0] * normed.shape[1]
    units, depth = weights[0].shape[0] // 2, weights[0].shape[1]
    tile = 512
    steps = rows // tile
    half = steps // 2
    once = pl.Buffered(1)
    inside = lambda i, m: jnp.clip(i - m[3] * half, 0, half - 1)
    return {
        "steps": steps,
        "flat": lambda x: x.reshape(-1, width),
        "row": pl.BlockSpec((tile, width), lambda i, m: (lax.rem(i + m[3] * half, steps), 0)),
        "unit": pl.BlockSpec((tile, units), lambda i, m: (i, 0)),
        "near_unit": pl.BlockSpec((tile, units), lambda i, m: (inside(i, m) + m[3] * half, 0)),
        "near_row": pl.BlockSpec((tile, width), lambda i, m: (inside(i, m), 0)),
        "weight": lambda k: pl.BlockSpec((units, depth), lambda i, m: (k, 0), pipeline_mode=once),
        "grad": pl.BlockSpec((units, depth), lambda i, m: (0, 0), pipeline_mode=once),
        "unit_shape": jax.ShapeDtypeStruct((rows, units), bf16),
        "near_shape": jax.ShapeDtypeStruct((rows // 2, width), bf16),
        "grad_shape": jax.ShapeDtypeStruct((units, depth), bf16),
        "total": pltpu.VMEM((units, depth), f32),
    }


def hidden_call(kernel, name, meta, args, in_specs, outs, grads, specs):
    return pl.pallas_call(
        kernel,
        name=name,
        grid_spec=pltpu.PrefetchScalarGridSpec(
            num_scalar_prefetch=1,
            grid=(specs["steps"],),
            in_specs=in_specs,
            out_specs=[specs[x] for x in outs] + [specs["grad"]] * grads,
            scratch_shapes=[specs["total"]] * grads,
        ),
        out_shape=[specs[x.split("_")[0] + "_shape"] for x in outs]
        + [specs["grad_shape"]] * grads,
        compiler_params=pltpu.CompilerParams(vmem_limit_bytes=VMEM_LIMIT),
    )(meta, *args)


def hidden_units(meta, normed, grad_out, weights):
    specs, pieces = hidden_specs(meta, normed, weights), len(weights)
    return hidden_call(
        functools.partial(hidden_kernel, pieces),
        "hidden_units",
        meta,
        [specs["flat"](normed), specs["flat"](grad_out)] + list(weights) * 2,
        [specs["row"]] * 2 + [specs["weight"](k) for k in range(2) for _ in weights],
        ["unit"] * 3,
        pieces == 2,
        specs,
    )


def hidden_back(meta, normed, grad_out, hidden, slope, gated, weights, down_weights):
    specs, pieces = hidden_specs(meta, normed, weights), len(weights)
    return hidden_call(
        functools.partial(hidden_back_kernel, pieces),
        "hidden_back",
        meta,
        [specs["flat"](normed), specs["flat"](grad_out), hidden, slope, gated]
        + list(weights) * 2
        + list(down_weights),
        [specs["row"]] * 2
        + [specs["near_unit"], specs["unit"], specs["unit"]]
        + [specs["weight"](k) for k in (0, 1, 0) for _ in weights],
        ["unit", "unit", "near_row", "near_row"],
        2 * (pieces == 2),
        specs,
    )


def unit_grads_kernel(count, meta_ref, near_ref, far_ref, *refs):
    units, out_ref, x_ref = refs[:count], refs[-2], refs[-1]
    half = near_ref.shape[0]
    x_ref[pl.ds(pl.multiple_of(meta_ref[3] * half, half), half)] = near_ref[...]
    x_ref[pl.ds(pl.multiple_of((1 - meta_ref[3]) * half, half), half)] = far_ref[...]
    for k, unit in enumerate(units):
        depth = unit.shape[1]
        out_ref[k * depth : (k + 1) * depth] = dot_rows(unit[...], x_ref[...]).astype(bf16)


def unit_grads(meta, which, pieces, x, units_of):
    width = x.shape[-1]
    count, (rows, units) = len(units_of), units_of[0].shape
    depth = width // pieces
    tile = 256
    steps = depth // tile
    shard = (lambda m: m[which]) if pieces > 1 else (lambda m: 0)
    feature = lambda half: pl.BlockSpec(
        (rows // 2, tile), lambda i, m: (half, shard(m) * steps + i)
    )
    unit = pl.BlockSpec((rows, units), lambda i, m: (0, 0), pipeline_mode=pl.Buffered(1))
    x = x.reshape(-1, width)
    return pl.pallas_call(
        functools.partial(unit_grads_kernel, count),
        name=f"unit_grads_{which}_{count}",
        grid_spec=pltpu.PrefetchScalarGridSpec(
            num_scalar_prefetch=1,
            grid=(steps,),
            in_specs=[feature(0), feature(1)] + [unit] * count,
            out_specs=pl.BlockSpec((count * units, tile), lambda i, m: (0, i)),
            scratch_shapes=[pltpu.VMEM((rows, tile), bf16)],
        ),
        out_shape=jax.ShapeDtypeStruct((count * units, depth), bf16),
        compiler_params=pltpu.CompilerParams(vmem_limit_bytes=VMEM_LIMIT),
    )(meta, x, x, *units_of)


class Wires:
    def __init__(self, sends, receives, locals_):
        self.sends, self.receives, self.locals = sends, receives, locals_
        self.used = self.used_local = 0
        self.started = []

    def plan(self, source, target, device):
        k = self.used
        self.used += 1
        return pltpu.make_async_remote_copy(
            source,
            target,
            self.sends.at[k],
            self.receives.at[k],
            device_id=device,
            device_id_type=pl.DeviceIdType.MESH,
        )

    def copy(self, source, target, device):
        one = self.plan(source, target, device)
        one.start()
        self.started.append(one)
        return one

    def here(self, source, target):
        k = self.used_local
        self.used_local += 1
        one = pltpu.make_async_copy(source, target, self.locals.at[k])
        one.start()
        return one

    def finish(self):
        for one in self.started:
            one.wait_send()


class OwnGrad:
    TILE = 256

    def __init__(self, units, rows, out, units_here, rows_here):
        self.units, self.rows, self.out = units, rows, out
        self.units_here, self.rows_here = units_here, rows_here
        self.tiles = out.shape[1] // self.TILE
        self.copies = None

    def fetch(self, wires):
        half, depth = self.rows.shape[0] // 2, self.out.shape[1]
        column = pl.multiple_of(lax.axis_index("fsdp") * depth, LANES)
        pair = lax.axis_index("context") // 2
        self.copies = [wires.here(self.units, self.units_here)]
        for k, place in ((0, pair), (1, 1 - pair)):
            self.copies.append(
                wires.here(
                    self.rows.at[pl.ds(k * half, half), pl.ds(column, depth)],
                    self.rows_here.at[pl.ds(pl.multiple_of(place * half, half), half)],
                )
            )

    def make(self, first, past):
        for one in self.copies:
            one.wait()
        self.copies = []

        @pl.loop(first, past)
        def _(k):
            at = pl.ds(pl.multiple_of(k * self.TILE, self.TILE), self.TILE)
            self.out[:, at] = dot_rows(self.units_here[...], self.rows_here[:, at]).astype(bf16)


def own_grad_call(fill, width):
    args = [x for pair in fill for x in pair]
    outs = [jax.ShapeDtypeStruct((units.shape[1], width), bf16) for units, _ in fill]
    scratch = []
    for units, rows in fill:
        scratch += [pltpu.VMEM(units.shape, bf16), pltpu.VMEM((rows.shape[0], width), bf16)]
    return args, outs, scratch


def own_grads(count, args, outs, scratch):
    return [
        OwnGrad(args[2 * k], args[2 * k + 1], outs[k], scratch[2 * k], scratch[2 * k + 1])
        for k in range(count)
    ]


def meet(devices):
    barrier = pltpu.get_barrier_semaphore()
    for device in devices:
        pl.semaphore_signal(barrier, inc=1, device_id=device, device_id_type=pl.DeviceIdType.MESH)
    pl.semaphore_wait(barrier, len(devices))


def partners():
    c, t = lax.axis_index("context"), lax.axis_index("tensor")
    flip = lambda x, bit: x + bit * (1 - 2 * lax.rem(x // bit, 2))
    return {
        "core": {"tensor": flip(t, 1)},
        "y": {"tensor": flip(t, 2)},
        "z": {"context": flip(c, 1)},
        "far": {"context": flip(c, 2)},
        "last": {"context": flip(flip(c, 1), 2)},
    }


def wide(x):
    return x.astype(f32)


def ranks():
    t = lax.axis_index("tensor")
    flip = lambda x, bit: x + bit * (1 - 2 * lax.rem(x // bit, 2))
    return (t, flip(t, 1), flip(t, 2), flip(flip(t, 1), 2))


def scatter_rank(wires, to, part, own, got_core, sent, got_y):
    size = part.shape[1] // 2
    halves = [pl.ds(0, size), pl.ds(size, size)]
    rank = ranks()
    from_core = {}
    for block in (1, 0):
        for k, at in enumerate(halves):
            from_core[block, k] = wires.copy(
                part.at[rank[1 + 2 * block], at], got_core.at[block, at], to["core"]
            )
    mine = [wires.here(part.at[rank[2 * block]], own.at[block]) for block in (0, 1)]
    yield
    for one in mine:
        one.wait()
    from_y = []
    for k, at in enumerate(halves):
        from_core[1, k].wait_recv()
        sent[at] = (wide(own[1, at]) + wide(got_core[1, at])).astype(bf16)
        from_y.append(wires.copy(sent.at[at], got_y.at[at], to["y"]))
    yield
    for k in range(2):
        from_core[0, k].wait_recv()
    total = wide(own[0]) + wide(got_core[0])
    for one in from_y:
        one.wait_recv()
    return total + wide(got_y[...])


def scatter_pair(wires, to, part, own, got_core, sent, got_y, got_z, diag_y, diag_z):
    size = part.shape[1] // 2
    low, high = pl.ds(0, size), pl.ds(size, size)
    from_core = {j: wires.copy(part.at[4 + j], got_core.at[j], to["core"]) for j in (3, 1, 2, 0)}
    mine = wires.here(part.at[pl.ds(0, 4)], own)
    yield
    mine.wait()
    both = lambda j, at: wide(own[j, at]) + wide(got_core[j, at])
    from_core[3].wait_recv()
    sent[2] = (wide(own[3]) + wide(got_core[3])).astype(bf16)
    via_z = wires.copy(sent.at[2, low], diag_z, to["z"])
    via_y = wires.copy(sent.at[2, high], diag_y, to["y"])
    from_core[1].wait_recv()
    sent[0, high] = both(1, high).astype(bf16)
    y_high = wires.copy(sent.at[0, high], got_y.at[high], to["y"])
    from_core[2].wait_recv()
    sent[1, low] = both(2, low).astype(bf16)
    z_low = wires.copy(sent.at[1, low], got_z.at[low], to["z"])
    yield
    via_z.wait_recv()
    sent[0, low] = (both(1, low) + wide(diag_z[...])).astype(bf16)
    y_low = wires.copy(sent.at[0, low], got_y.at[low], to["y"])
    via_y.wait_recv()
    sent[1, high] = (both(2, high) + wide(diag_y[...])).astype(bf16)
    z_high = wires.copy(sent.at[1, high], got_z.at[high], to["z"])
    yield
    from_core[0].wait_recv()
    total = wide(own[0]) + wide(got_core[0])
    for one in (y_high, z_low, y_low, z_high):
        one.wait_recv()
    return total + wide(got_y[...]) + wide(got_z[...])


def result_of(steps):
    while True:
        try:
            next(steps)
        except StopIteration as done:
            return done.value


def gather_rank(wires, to, block, out):
    size = block.shape[0] // 2
    halves = [pl.ds(0, size), pl.ds(size, size)]
    rank = ranks()
    mine = wires.here(block, out.at[rank[0]])
    from_y = [wires.copy(block.at[h], out.at[rank[0], h], to["y"]) for h in halves]
    from_core = [wires.copy(block, out.at[rank[0]], to["core"])]
    yield
    for h, one in zip(halves, from_y):
        one.wait_recv()
        from_core.append(wires.copy(out.at[rank[2], h], out.at[rank[2], h], to["core"]))
    for one in from_core:
        one.wait_recv()
    mine.wait()


def gather_pair(wires, to, block, out, base):
    size = block.shape[0] // 2
    low, high = pl.ds(0, size), pl.ds(size, size)
    at = lambda j: out.at[base + j]
    from_z = wires.copy(block, at(2), to["z"])
    yield
    from_y = wires.copy(block, at(1), to["y"])
    from_core = [wires.copy(block, at(4), to["core"])]
    yield
    from_y.wait_recv()
    via_z = wires.copy(out.at[base + 1, low], out.at[base + 3, low], to["z"])
    from_core.append(wires.copy(at(1), at(5), to["core"]))
    from_z.wait_recv()
    via_y = wires.copy(out.at[base + 2, high], out.at[base + 3, high], to["y"])
    from_core.append(wires.copy(at(2), at(6), to["core"]))
    yield
    via_z.wait_recv()
    via_y.wait_recv()
    from_core.append(wires.copy(at(3), at(7), to["core"]))
    return from_core


def remote_call(kernel, name, key, args, outs, scratch, copies, in_vmem):
    ins, out_in = in_vmem
    spec = lambda inside: pl.BlockSpec(memory_space=pltpu.VMEM if inside else pl.ANY)
    return pl.pallas_call(
        kernel,
        name=name,
        out_shape=outs,
        in_specs=[spec(x) for x in ins],
        out_specs=[spec(x) for x in out_in],
        scratch_shapes=list(scratch)
        + [
            pltpu.SemaphoreType.DMA((copies,)),
            pltpu.SemaphoreType.DMA((copies,)),
            pltpu.SemaphoreType.DMA((10,)),
        ],
        compiler_params=pltpu.CompilerParams(
            collective_id=key, has_side_effects=True, vmem_limit_bytes=VMEM_LIMIT
        ),
    )(*args)


def kv_gather_kernel(own_ref, out_ref, *sems):
    wires, to = Wires(*sems), partners()
    kind = lax.rem(lax.axis_index("tensor"), 2)
    rows = own_ref.shape[0]
    block = lambda j: out_ref.at[kind, pl.ds(j * rows, rows)]
    meet([to[k] for k in ("core", "z", "far", "last")])
    mine = wires.here(own_ref, block(0))
    arrive = [wires.copy(own_ref, block(j), to[k]) for j, k in ((3, "last"), (2, "far"), (1, "z"))]
    from_core = [wires.copy(own_ref, block(0), to["core"])]
    for j, one in ((1, arrive[2]), (2, arrive[1]), (3, arrive[0])):
        one.wait_recv()
        from_core.append(wires.copy(block(j), block(j), to["core"]))
    for one in from_core:
        one.wait_recv()
    mine.wait()
    wires.finish()


def kv_gather(own):
    rows, width = own.shape
    n_c = lax.axis_size("context")
    return remote_call(
        kv_gather_kernel,
        "kv_gather",
        0,
        [own],
        [jax.ShapeDtypeStruct((2, n_c * rows, width), bf16)],
        [],
        8,
        ([False], [False]),
    )[0]


def kv_scatter_kernel(count, part_ref, *refs):
    args, dkv_ref, outs = refs[: 2 * count], refs[2 * count], refs[2 * count + 1 : 3 * count + 1]
    own, got_core, sent, got = refs[3 * count + 1 : 3 * count + 5]
    wires, to = Wires(*refs[-3:]), partners()
    fill = own_grads(count, args, outs, refs[3 * count + 5 : -3])
    kind = lax.rem(lax.axis_index("tensor"), 2)
    rows = dkv_ref.shape[0]
    block = lambda j: pl.ds(j * rows, rows)
    meet([to[k] for k in ("core", "z", "far", "last")])
    steps = ((3, "last"), (2, "far"), (1, "z"), (0, None))
    from_core = {
        j: wires.copy(part_ref.at[1 - kind, block(j)], got_core.at[block(j)], to["core"])
        for j, _ in steps
    }
    mine = wires.here(part_ref.at[kind], own)
    for one in fill:
        one.fetch(wires)
    mine.wait()
    arrive = []
    for j, k in steps[:3]:
        from_core[j].wait_recv()
        sent[block(j)] = (wide(own[block(j)]) + wide(got_core[block(j)])).astype(bf16)
        arrive.append(wires.copy(sent.at[block(j)], got.at[block(j)], to[k]))
    for one in fill:
        one.make(0, one.tiles)
    from_core[0].wait_recv()
    total = wide(own[block(0)]) + wide(got_core[block(0)])
    for one in arrive:
        one.wait_recv()
    for j in (1, 2, 3):
        total = total + wide(got[block(j)])
    dkv_ref[...] = total
    wires.finish()


def kv_scatter(part, fill, width):
    _, rows, depth = part.shape
    n_c = lax.axis_size("context")
    args, outs, scratch = own_grad_call(fill, width)
    return remote_call(
        functools.partial(kv_scatter_kernel, len(fill)),
        "kv_scatter",
        1,
        [part, *args],
        [jax.ShapeDtypeStruct((rows // n_c, depth), f32), *outs],
        [pltpu.VMEM((rows, depth), bf16)] * 4 + scratch,
        7,
        ([False] * (1 + len(args)), [True] * (1 + len(outs))),
    )


def middle_kernel(
    part,
    x_ref,
    gain_ref,
    dy_ref,
    dy_y,
    dy_z,
    dy_far,
    mid_ref,
    factor_ref,
    out,
    dys,
    own,
    core,
    sent,
    got,
    xn,
    *sems,
):
    wires, to = Wires(*sems), partners()
    blocks = out.shape[0] // 2
    size = xn.shape[0] // 2
    low, high = pl.ds(0, size), pl.ds(size, size)
    meet([to[k] for k in ("core", "y", "z", "far")])
    summed = scatter_rank(wires, to, part, own, core, sent, got)
    next(summed)
    mine = [
        wires.here(block, dys.at[k])
        for block, k in ((dy_ref, 0), (dy_y, 1), (dy_z, 2), (dy_far, blocks))
    ]
    via_z = wires.copy(dy_y.at[low], dys.at[3, low], to["z"])
    dy_last = gather_pair(wires, to, dy_far, dys, blocks)
    next(dy_last)
    next(summed)
    via_y = wires.copy(dy_z.at[high], dys.at[3, high], to["y"])
    ends = [
        wires.copy(block, dys.at[4 + k], to["core"])
        for k, block in enumerate((dy_ref, dy_y, dy_z))
    ]
    next(dy_last)
    middle = wide(x_ref[...]) + result_of(summed)
    mid_ref[...] = middle
    factor = lax.rsqrt(jnp.mean(middle * middle, axis=-1, keepdims=True) + EPSILON)
    factor_ref[...] = factor
    xn[...] = (middle * factor * gain_ref[...]).astype(bf16)
    mine.append(wires.here(xn, out.at[0]))
    xn_far = wires.copy(xn, out.at[blocks], to["far"])
    xn_near = gather_pair(wires, to, xn, out, 0)
    next(xn_near)
    next(xn_near)
    via_z.wait_recv()
    via_y.wait_recv()
    ends.append(wires.copy(dys.at[3], dys.at[7], to["core"]))
    next(dy_last)
    next(xn_near)
    xn_far.wait_recv()
    xn_last = gather_pair(wires, to, out.at[blocks], out, blocks)
    next(xn_last)
    next(xn_last)
    ends += result_of(dy_last) + result_of(xn_near)
    next(xn_last)
    ends += result_of(xn_last)
    for one in ends:
        one.wait_recv()
    for one in mine:
        one.wait()
    wires.finish()


def middle_norm(part, inputs_part, gain, dy_blocks):
    rows, width = inputs_part.shape
    return remote_call(
        middle_kernel,
        "middle_norm",
        2,
        [part.reshape(4, rows, width), inputs_part, gain, *dy_blocks],
        [
            jax.ShapeDtypeStruct((rows, width), f32),
            jax.ShapeDtypeStruct((rows, 1), f32),
            jax.ShapeDtypeStruct((16, rows, width), bf16),
            jax.ShapeDtypeStruct((16, rows, width), bf16),
        ],
        [
            pltpu.VMEM((2, rows, width), bf16),
            pltpu.VMEM((2, rows, width), bf16),
            pltpu.VMEM((rows, width), bf16),
            pltpu.VMEM((rows, width), bf16),
            pltpu.VMEM((rows, width), bf16),
        ],
        48,
        ([False] + [True] * 6, [True, True, False, False]),
    )


def norm_back_rows(values, factor, gain, grad_normed):
    gained = gain * grad_normed
    inner = jnp.mean(gained * values, axis=-1, keepdims=True)
    grad_values = factor * gained - values * (factor * factor * factor) * inner
    return grad_values, jnp.sum(grad_normed * values * factor, axis=0, keepdims=True)


def middle_back_kernel(count, part, mid_ref, factor_ref, gain_ref, dy_ref, *refs):
    args, refs = refs[: 2 * count], refs[2 * count :]
    source_ref, refs = (refs[0], refs[1:]) if count else (None, refs)
    (dmid_ref, dgain_ref, out), refs = refs[:3], refs[3:]
    outs, refs = refs[:count], refs[count:]
    (upper_ref, lower_ref, far_ref), refs = (
        (refs[:3], refs[3:]) if count else ((None, None, None), refs)
    )
    low, first, wires, to = refs[0], refs[1:8], Wires(*refs[-3:]), partners()
    fill = own_grads(count, args, outs, refs[8 : 8 + 2 * count])
    meet([to[k] for k in ("core", "y", "z")])
    back = scatter_pair(wires, to, part, *first)
    next(back)
    for one in fill:
        one.fetch(wires)
    if fill:
        got_ref = refs[8 + 2 * count]
        fetched = wires.here(source_ref, got_ref)
    next(back)
    if fill:
        fill[0].make(0, 1)
    next(back)
    if fill:
        fill[0].make(1, fill[0].tiles)
        fetched.wait()
        cut = upper_ref.shape[0]
        upper_ref[...] = (wide(outs[0][:cut]) + wide(got_ref[:cut])).astype(bf16)
        near_half = wires.copy(upper_ref, far_ref, to["z"])
        lower_ref[...] = (wide(outs[0][cut:]) + wide(got_ref[cut:])).astype(bf16)
    grad_normed = result_of(back)
    du, dgain = norm_back_rows(mid_ref[...], factor_ref[...], gain_ref[...], grad_normed)
    dgain_ref[...] = dgain
    dmid = wide(dy_ref[...]) + du
    low[...] = dmid.astype(bf16)
    share = gather_rank(wires, to, low, out)
    next(share)
    dmid_ref[...] = dmid
    for one in fill[1:]:
        one.make(0, one.tiles)
    result_of(share)
    if fill:
        near_half.wait_recv()
    wires.finish()


def pair_scratch(rows, width):
    return [
        pltpu.VMEM((4, rows, width), bf16),
        pltpu.VMEM((4, rows, width), bf16),
        pltpu.VMEM((3, rows, width), bf16),
        pltpu.VMEM((rows, width), bf16),
        pltpu.VMEM((rows, width), bf16),
        pltpu.VMEM((rows // 2, width), bf16),
        pltpu.VMEM((rows // 2, width), bf16),
    ]


def middle_back(part, middle, factor, gain, dy_part, fill, got, shard):
    rows, width = middle.shape
    args, outs, scratch = own_grad_call(fill, shard)
    if fill:
        args = [*args, got]
        scratch = [*scratch, pltpu.VMEM(got.shape, bf16)]
        units = got.shape[0]
        cut = units // 64 * 16
        outs = [*outs, *(jax.ShapeDtypeStruct((n, shard), bf16) for n in (cut, units - cut, cut))]
    return remote_call(
        functools.partial(middle_back_kernel, len(fill)),
        "middle_back",
        3,
        [part.reshape(8, rows, width), middle, factor, gain, dy_part, *args],
        [
            jax.ShapeDtypeStruct((rows, width), f32),
            jax.ShapeDtypeStruct((1, width), f32),
            jax.ShapeDtypeStruct((4, rows, width), bf16),
            *outs,
        ],
        [pltpu.VMEM((rows, width), bf16)] + pair_scratch(rows, width) + scratch,
        16,
        (
            [False] + [True] * 4 + [False] * len(args),
            [True, True, False] + ([True] * (len(outs) - 1) + [False] if fill else []),
        ),
    )


def add_all(wires, ways, value, slots):
    for k, device in enumerate(ways):
        one = wires.copy(value, slots.at[k], device)
        one.wait()
        wires.started = [x for x in wires.started if x is not one]
        value[...] = value[...] + slots[k]


def input_back_kernel(
    part, x_ref, gain_ref, dmid_ref, small_ref, sum_ref, out, *rest
):
    low, own, core, sent, got, slots = rest[:-3]
    wires, to = Wires(*rest[-3:]), partners()
    meet([to[k] for k in ("core", "y")])
    grad_normed = result_of(scatter_rank(wires, to, part, own, core, sent, got))
    values = wide(x_ref[...])
    factor = lax.rsqrt(jnp.mean(values * values, axis=-1, keepdims=True) + EPSILON)
    du, dgain = norm_back_rows(values, factor, gain_ref[...], grad_normed)
    low[...] = (dmid_ref[...] + du).astype(bf16)
    share = gather_rank(wires, to, low, out)
    next(share)
    width = dgain.shape[1]
    sum_ref[:, width:] = small_ref[:, width:]
    sum_ref[:, :width] = dgain
    add_all(wires, [to["core"], to["y"]], sum_ref, slots)
    result_of(share)
    wires.finish()


def input_back(part, inputs_part, gain, grad_middle, small):
    rows, width = inputs_part.shape
    return remote_call(
        input_back_kernel,
        "input_back",
        5,
        [part.reshape(4, rows, width), inputs_part, gain, grad_middle, small],
        [
            jax.ShapeDtypeStruct(small.shape, f32),
            jax.ShapeDtypeStruct((4, rows, width), bf16),
        ],
        [
            pltpu.VMEM((rows, width), bf16),
            pltpu.VMEM((2, rows, width), bf16),
            pltpu.VMEM((2, rows, width), bf16),
            pltpu.VMEM((rows, width), bf16),
            pltpu.VMEM((rows, width), bf16),
            pltpu.VMEM((2,) + small.shape, f32),
        ],
        16,
        ([False, True, True, True, True], [True, False]),
    )


def context_sum_kernel(over_f, *refs):
    parts, small_ref, out_part, mid_ref = refs[:3], refs[3], refs[4], refs[5]
    outs, sum_ref, shared, outputs = refs[6:8], refs[8], refs[9], refs[10]
    lows, from_end, from_middle = refs[11:15], refs[15:19], refs[19:23]
    out_low, slot, scratch = refs[23], refs[24], refs[25:32]
    wires, to, c = Wires(*refs[32:]), partners(), lax.axis_index("context")
    end = (c == 0) | (c == lax.axis_size("context") - 1)
    inner = jnp.logical_not(end)
    greet = ["core", "y", "z", "last"]
    if over_f:
        to["f"] = {"fsdp": 1 - lax.axis_index("fsdp")}
        greet.append("f")
    meet([to[k] for k in greet])
    ahead = scatter_pair(wires, to, out_part, *scratch)
    next(ahead)
    sum_ref[...] = small_ref[...]
    from_f = wires.copy(small_ref, slot, to["f"]) if over_f else None
    next(ahead)
    sources = [*parts, sum_ref]
    chunks = []
    for i, cuts in ((2, 1), (0, 2), (1, 4), (3, 1)):
        size = sources[i].shape[0] // cuts
        chunks += [(i, pl.ds(k * size, size)) for k in range(cuts)]
    inward = [wires.plan(sources[i].at[at], from_end[i].at[at], to["z"]) for i, at in chunks]
    across = [wires.plan(lows[i].at[at], from_middle[i].at[at], to["last"]) for i, at in chunks]
    outward = [wires.plan(lows[i].at[at], lows[i].at[at], to["z"]) for i, at in chunks]
    small = len(chunks) - 1

    def send_in(k):
        @pl.when(end)
        def _():
            inward[k].start()

    def pass_on(first, past):
        @pl.when(inner)
        def _():
            for k in range(first, past):
                i, at = chunks[k]
                inward[k].wait_recv()
                total = wide(sources[i][at]) + wide(from_end[i][at])
                lows[i][at] = total.astype(lows[i].dtype)
                across[k].start()
                if k:
                    send_out(k - 1)

    def send_out(k):
        i, at = chunks[k]
        across[k].wait()
        lows[i][at] = (wide(lows[i][at]) + wide(from_middle[i][at])).astype(lows[i].dtype)
        outward[k].start()

    send_in(0)
    send_in(1)
    next(ahead)
    if over_f:
        from_f.wait_recv()
        sum_ref[...] = sum_ref[...] + slot[...]
    for k in range(2, small + 1):
        send_in(k)
    pass_on(0, 2)
    out_low[...] = (mid_ref[...] + result_of(ahead)).astype(bf16)
    out_share = gather_rank(wires, to, out_low, outputs)
    next(out_share)
    pass_on(2, small + 1)

    @pl.when(inner)
    def _():
        send_out(small)

    result_of(out_share)

    def arrived(k):
        @pl.when(end)
        def _():
            outward[k].wait_recv()

    arrived(0)
    share = gather_rank(wires, to, lows[2], shared)
    next(share)
    for k in range(1, len(chunks)):
        arrived(k)

    @pl.when(end)
    def _():
        for one in inward:
            one.wait_send()

    for i in (0, 1):
        outs[i][...] = wide(lows[i][...])
    sum_ref[...] = lows[3][...]
    result_of(share)

    @pl.when(inner)
    def _():
        for one in outward:
            one.wait_send()

    wires.finish()


def context_sum(over_f, parts, small, out_part, middle):
    rows, width = middle.shape
    lines = [pltpu.VMEM(x.shape, x.dtype) for x in (*parts, small)]
    return remote_call(
        functools.partial(context_sum_kernel, over_f),
        "context_sum",
        6,
        [*parts, small, out_part.reshape(8, rows, width), middle],
        [jax.ShapeDtypeStruct(x.shape, f32) for x in parts[:2]]
        + [jax.ShapeDtypeStruct(small.shape, f32)]
        + [jax.ShapeDtypeStruct((4,) + parts[2].shape, bf16)]
        + [jax.ShapeDtypeStruct((4, rows, width), bf16)],
        lines * 3
        + [pltpu.VMEM((rows, width), bf16), pltpu.VMEM(small.shape, f32)]
        + pair_scratch(rows, width),
        48,
        ([True] * 4 + [False, True], [True] * 3 + [False] * 2),
    )


def build(n_f, n_c, n_t):
    def flip(x, axis, bit):
        size = {"fsdp": n_f, "context": n_c, "tensor": n_t}[axis]
        return lax.ppermute(x, axis, [(i, i ^ bit) for i in range(size)])

    def by_bit(bit, x, other, axis):
        return jnp.where(
            bit == 0,
            jnp.concatenate([x, other], axis=axis),
            jnp.concatenate([other, x], axis=axis),
        )

    def after(x, *others):
        return lax.optimization_barrier((x, others))[0]

    def local(
        inputs,
        cotangent,
        blocks,
        attn_gain,
        w_query,
        b_query,
        w_key,
        b_key,
        w_value,
        b_value,
        w_out,
        ffn_gain,
        w_gate,
        w_up,
        w_down,
    ):
        rows, width = inputs.shape
        f = lax.axis_index("fsdp")
        c = lax.axis_index("context")
        t = lax.axis_index("tensor")
        core, parity, pair = t % 2, c % 2, c // 2
        heads = w_query.shape[1] // HD
        group = (t * heads) // (H // KV)
        part = rows // n_t
        units_all = w_gate.shape[1]
        units = units_all // 2

        def gather_f(x, axis):
            if n_f == 2:
                return by_bit(f, x, flip(x, "fsdp", 1), axis)
            return lax.all_gather(x, "fsdp", axis=axis, tiled=True)

        def grad_far(left, right, side):
            if n_f > 2:
                return None
            source = (left, right)[side]
            half = width // 2
            far = lax.dynamic_slice_in_dim(source, (1 - f) * half, half, 1)
            return (dot_rows(far, right) if side == 0 else dot_rows(left, far)).astype(bf16)

        def grad_sum(left, right, side, far, late):
            if n_f > 2:
                return lax.psum_scatter(
                    dot_rows(left, right).astype(bf16), "fsdp", scatter_dimension=side, tiled=True
                )
            source = (left, right)[side]
            half = width // 2
            own = lax.dynamic_slice_in_dim(source, f * half, half, 1)
            own = dot_rows(own, right) if side == 0 else dot_rows(left, own)
            return (own + after(flip(far, "fsdp", 1), late).astype(f32)).astype(bf16)

        small = jnp.concatenate(
            [v.reshape(1, -1) for v in (attn_gain, ffn_gain, b_query, b_key, b_value)], axis=1
        )
        column = lambda w: lax.dynamic_slice_in_dim(w, group * HD, HD, 1)
        w_kv_own = jnp.where(core == 0, column(w_key), column(w_value))
        pieces_f = lambda x, axis: (
            [x, flip(x, "fsdp", 1)]
            if n_f == 2
            else [lax.all_gather(x, "fsdp", axis=axis, tiled=True)]
        )
        meta = jnp.stack([f, 1 - f, core, pair]).astype(jnp.int32)
        w_q = pieces_f(w_query, 0)
        w_kv = pieces_f(w_kv_own, 0)
        small = gather_f(small, 0)
        w_out_all = gather_f(after(w_out, small, w_q, w_kv), 1)
        piece = attn_gain.shape[0]
        gain_first = small[:, :piece].reshape(1, width).astype(f32)
        gain_second = small[:, piece : 2 * piece].reshape(1, width).astype(f32)
        bias_of = lambda lo, n: (
            small[:, lo : lo + n * (HD // n_f)]
            .reshape(n_f, n, HD // n_f)
            .transpose(1, 0, 2)
            .reshape(n, HD)
            .astype(f32)
        )
        at = 2 * piece
        bq = bias_of(at, heads)
        bk = bias_of(at + heads * (HD // n_f), KV)
        bv = bias_of(at + (heads + KV) * (HD // n_f), KV)
        b_kv = lax.dynamic_index_in_dim(jnp.where(core == 0, bk, bv), group, 0)

        unit_slice = lambda w: lax.dynamic_slice_in_dim(w, parity * units, units, 0)
        own_gate_up = jnp.concatenate(
            [unit_slice(after(w, w_kv_own)) for w in (w_gate.T, w_up.T)], axis=0
        )
        own_down = unit_slice(w_down)

        dy_part = lax.dynamic_slice_in_dim(cotangent, t * part, part, 0)

        seq_blocks = blocks[0].reshape(n_c, -1)
        own_blocks = seq_blocks.shape[1]
        key_blocks = jnp.concatenate(
            [lax.dynamic_index_in_dim(seq_blocks, c ^ j, 0, keepdims=False) for j in range(n_c)]
        )
        positions = (
            key_blocks[:own_blocks, None] * BLOCK + jnp.arange(BLOCK, dtype=jnp.int32)[None, :]
        ).reshape(-1)
        cosine, sine = rope_tables(positions)
        bias = jnp.concatenate([bq.reshape(1, -1), b_kv], axis=1)
        dy_blocks = [
            dy_part,
            flip(dy_part, "tensor", 2),
            flip(dy_part, "context", 1),
            flip(dy_part, "context", 2),
        ]
        inputs_part = lax.dynamic_slice_in_dim(inputs, t * part, part, 0)
        bias = after(bias, dy_blocks[2:], own_gate_up, own_down, inputs_part)
        normed, queries, kv_own = qkv(
            meta, inputs, gain_first, bias, cosine, sine, w_q, w_kv
        )
        kv = after(kv_gather(kv_own), w_out_all)
        far_gate_up = pieces_f(after(own_gate_up, kv), 1)[-1]
        w_gate_up = [own_gate_up, far_gate_up] if n_f == 2 else [far_gate_up]
        far_down = pieces_f(after(own_down, kv), 1)[-1]
        w_downs = [own_down, far_down] if n_f == 2 else [far_down]
        attended, lse = attention(key_blocks, queries, kv)
        middle, factor_second, normed2, dy_all = middle_norm(
            dot(attended, w_out_all).astype(bf16), inputs_part, gain_second, dy_blocks
        )

        hidden, slope, gated, *down_far = hidden_units(meta, normed2, dy_all, w_gate_up)
        grad_gate, grad_up, dx_part, out_part, *unit_far = hidden_back(
            meta, normed2, dy_all, hidden, slope, gated, w_gate_up, w_downs
        )
        unit_far = [*down_far, *unit_far]
        flat = lambda x: x.reshape(-1, width)
        if n_f == 2:
            down_got, gate_got, up_got = (flip(x, "fsdp", 1) for x in unit_far)
            early = [(hidden, flat(dy_all)), (grad_gate, flat(normed2))]
            later = [(grad_up, flat(normed2))]
        else:
            over_f = lambda x: lax.psum_scatter(x, "fsdp", scatter_dimension=1, tiled=True)
            owns = [
                over_f(unit_grads(meta, 0, 1, x, [unit]))
                for x, unit in ((dy_all, hidden), (normed2, grad_gate), (normed2, grad_up))
            ]
            down_got = gate_got = up_got = jnp.zeros_like(owns[0])
            early = later = []

        def unit_whole(own, other):
            own, other = (jnp.concatenate(x, axis=0) for x in (own, other))
            return by_bit(parity, own, other, 0).astype(f32)

        grad_middle, ffn_gain_grad, grad_middle_low, *first_owns = middle_back(
            dx_part, middle, factor_second, gain_second, dy_part, early, down_got, width // n_f
        )
        grad_middle_low = grad_middle_low.reshape(rows, width)
        add = lambda own, got: (own.astype(f32) + got.astype(f32)).astype(bf16)
        upper = units // 2
        if n_f == 2:
            _, gate_own, down_upper, down_lower, far_upper = first_owns
        else:
            down_low, gate_own = owns[:2]
            down_upper, down_lower = down_low[:upper], down_low[upper:]
            far_upper = flip(down_upper, "context", 1)
        gate_got = after(gate_got, grad_middle_low)
        gate_low = add(gate_own, gate_got)
        far_lower = flip(down_lower, "context", 1)
        grad_middle_low = after(grad_middle_low, gate_low)
        grad_attended = dot_cols(grad_middle_low, w_out_all).astype(bf16)

        dq_low, dkv = attention_back(key_blocks, queries, grad_attended, lse, cosine, sine, kv)
        attention_args = [(attended, after(grad_middle_low, dq_low), 1), (normed, dq_low, 0)]
        fars = [grad_far(*args) for args in attention_args]
        dkv, *last_owns = kv_scatter(
            after(dkv, fars), later, width // n_f
        )
        (up_own,) = last_owns or owns[2:]
        far_gate = flip(after(gate_low, dkv, far_lower), "context", 1)
        dkv = after(dkv, far_lower)
        dkv_low = jnp.where(core == 0, rotate_back(dkv, cosine, sine), dkv).astype(bf16)
        own_biases = jnp.sum(
            jnp.concatenate([dq_low, dkv_low], axis=1).astype(f32), axis=0, keepdims=True
        )
        slots = lax.dynamic_update_slice(
            jnp.zeros((n_t, (heads + 1) * HD), f32), own_biases, (t, 0)
        )
        small_grads = jnp.concatenate(
            [jnp.zeros((1, width), f32), ffn_gain_grad, slots.reshape(1, -1)], axis=1
        )
        grad_qkv = qkv_back(meta, dq_low, dkv_low, w_q, w_kv)
        up_low = add(up_own, after(up_got, grad_qkv))
        attention_args.append((after(normed, grad_qkv), dkv_low, 0))
        fars.append(grad_far(*attention_args[-1]))
        far_up = flip(up_low, "context", 1)
        small_grads, input_grad = input_back(
            after(grad_qkv, up_low, fars),
            inputs_part,
            gain_first,
            grad_middle,
            small_grads,
        )
        input_grad = input_grad.reshape(rows, width)
        if n_f > 2:
            small_grads = lax.psum(small_grads, "fsdp")
        zero = jnp.minimum(t, 0).astype(bf16)
        input_grad = input_grad + zero
        small_grads = after(small_grads, far_gate)
        attention_parts = [
            grad_sum(*args, far, small_grads) for args, far in zip(attention_args, fars)
        ]
        wd_grad = unit_whole(
            *after(((down_upper, down_lower), (far_upper, far_lower)), small_grads)
        )
        wg_grad = unit_whole(*after(((gate_low,), (far_gate,)), small_grads))
        small_grads, wd_grad, wg_grad, input_grad = lax.optimization_barrier(
            (small_grads, wd_grad, wg_grad, input_grad)
        )
        wo_grad, wq_grad, packed, wkv_all, outputs = context_sum(
            n_f == 2, attention_parts, small_grads, out_part, middle
        )
        wo_grad, wq_grad, packed, wkv_all, outputs, far_up = lax.optimization_barrier(
            (wo_grad, wq_grad, packed, wkv_all, outputs, far_up)
        )
        outputs = outputs.reshape(rows, width)
        wk_grad = jnp.concatenate([wkv_all[0], wkv_all[2]], axis=1).astype(f32)
        wv_grad = jnp.concatenate([wkv_all[1], wkv_all[3]], axis=1).astype(f32)
        packed = packed[0]
        attn_gain_grad = lax.dynamic_slice_in_dim(packed, f * piece, piece, 0)
        ffn_gain_grad = lax.dynamic_slice_in_dim(packed, width + f * piece, piece, 0)
        slots = packed[2 * width :].reshape(n_t, heads + 1, HD)
        slots = lax.dynamic_slice_in_dim(slots, f * (HD // n_f), HD // n_f, 2)
        bq_out = lax.dynamic_index_in_dim(slots, t, 0, keepdims=False)[:heads]
        bk_out = slots[0::2, heads]
        bv_out = slots[1::2, heads]

        wu_grad = unit_whole((up_low,), (far_up,))
        wg_grad, wu_grad = wg_grad.T, wu_grad.T

        return (
            outputs,
            input_grad,
            attn_gain_grad,
            wq_grad,
            bq_out,
            wk_grad,
            bk_out,
            wv_grad,
            bv_out,
            wo_grad,
            ffn_gain_grad,
            wg_grad,
            wu_grad,
            wd_grad,
        )

    return local


def solution(mesh):
    in_specs = (
        P(("fsdp", "context"), None),
        P(("fsdp", "context"), None),
        P("fsdp", None),
        P("fsdp"),
        P("fsdp", "tensor"),
        P("tensor", "fsdp"),
        P("fsdp", None),
        P(None, "fsdp"),
        P("fsdp", None),
        P(None, "fsdp"),
        P("tensor", "fsdp"),
        P("fsdp"),
        P("fsdp", "tensor"),
        P("fsdp", "tensor"),
        P("tensor", "fsdp"),
    )
    out_specs = (
        P(("fsdp", "context"), None),
        P(("fsdp", "context"), None),
        P("fsdp"),
        P("fsdp", "tensor"),
        P("tensor", "fsdp"),
        P("fsdp", None),
        P(None, "fsdp"),
        P("fsdp", None),
        P(None, "fsdp"),
        P("tensor", "fsdp"),
        P("fsdp"),
        P("fsdp", "tensor"),
        P("fsdp", "tensor"),
        P("tensor", "fsdp"),
    )
    local = build(mesh.shape["fsdp"], mesh.shape["context"], mesh.shape["tensor"])
    return jax.shard_map(local, mesh=mesh, in_specs=in_specs, out_specs=out_specs, check_vma=False)
```

```python
import functools

import jax
import jax.numpy as jnp
from jax import lax
from jax.experimental import pallas as pl
from jax.experimental.pallas import tpu as pltpu
from jax.sharding import PartitionSpec as P

H = 12
KV = 2
HD = 128
BLOCK = 256

EPSILON = 1e-06
ROPE_BASE = 1000000.0
MASKED = -1e30
SCALING = HD ** (-0.5)
LANES = 128
VMEM_LIMIT = 60 << 20

f32 = jnp.float32
bf16 = jnp.bfloat16


def rope_tables(positions):
    halfway = HD // 2
    frequency = ROPE_BASE ** (-(jnp.arange(halfway, dtype=f32) * 2.0 / HD))
    angles = positions.astype(f32)[:, None] * frequency[None, :]
    cosine, sine = jnp.cos(angles), jnp.sin(angles)
    return (jnp.concatenate([cosine, cosine], axis=1), jnp.concatenate([sine, sine], axis=1))


def rotate(field, cosine, sine):
    halfway = HD // 2
    turned = jnp.concatenate([-field[..., halfway:], field[..., :halfway]], axis=-1)
    return field * cosine + turned * sine


def rotate_back(grad_field, cosine, sine):
    halfway = HD // 2
    moved = grad_field * sine
    turned = jnp.concatenate([moved[..., halfway:], -moved[..., :halfway]], axis=-1)
    return grad_field * cosine + turned


def dot(left, right):
    return jnp.dot(left, right, preferred_element_type=f32)


def dot_rows(left, right):
    return lax.dot_general(left, right, (((0,), (0,)), ((), ())), preferred_element_type=f32)


def dot_cols(left, right):
    return lax.dot_general(left, right, (((1,), (1,)), ((), ())), preferred_element_type=f32)


def mask_row(kb_ref, own_block, key_blocks):
    return jnp.concatenate(
        [
            jnp.full((1, BLOCK), jnp.where(kb_ref[j] <= own_block, 0.0, MASKED), f32)
            for j in range(key_blocks)
        ],
        axis=1,
    )


def attention_kernel(key_blocks, kb_ref, q_ref, k_ref, v_ref, o_ref, lse_ref):
    bias = mask_row(kb_ref, kb_ref[pl.program_id(1)], key_blocks)
    scores = dot_cols(q_ref[...], k_ref[...]) * SCALING + bias
    row_max = jnp.max(scores, axis=1, keepdims=True)
    expo = jnp.exp(scores - row_max)
    total = jnp.sum(expo, axis=1, keepdims=True)
    probability = (expo * (1.0 / total)).astype(bf16)
    o_ref[...] = dot(probability, v_ref[...]).astype(bf16)
    lse_ref[0] = row_max + jnp.log(total)


def attention(key_blocks, queries, kv):
    rows, width = queries.shape
    heads = width // HD
    whole = lambda kind: pl.BlockSpec((None,) + kv.shape[1:], lambda h, i, kb: (kind, 0, 0))
    tile = pl.BlockSpec((BLOCK, HD), lambda h, i, kb: (i, h))
    return pl.pallas_call(
        functools.partial(attention_kernel, kv.shape[1] // BLOCK),
        name="attention",
        grid_spec=pltpu.PrefetchScalarGridSpec(
            num_scalar_prefetch=1,
            grid=(heads, rows // BLOCK),
            in_specs=[tile, whole(0), whole(1)],
            out_specs=[tile, pl.BlockSpec((1, BLOCK, 1), lambda h, i, kb: (h, i, 0))],
        ),
        out_shape=[
            jax.ShapeDtypeStruct((rows, width), bf16),
            jax.ShapeDtypeStruct((heads, rows, 1), f32),
        ],
        compiler_params=pltpu.CompilerParams(vmem_limit_bytes=VMEM_LIMIT),
    )(key_blocks, queries, kv, kv)


def attention_back_kernel(
    key_blocks,
    kb_ref,
    q_ref,
    do_ref,
    lse_ref,
    cos_ref,
    sin_ref,
    k_ref,
    v_ref,
    dq_ref,
    dkv_ref,
    dk_ref,
    dv_ref,
):
    head, i = pl.program_id(0), pl.program_id(1)

    @pl.when((head == 0) & (i == 0))
    def _():
        dk_ref[...] = jnp.zeros_like(dk_ref)
        dv_ref[...] = jnp.zeros_like(dv_ref)

    bias = mask_row(kb_ref, kb_ref[i], key_blocks)
    scores = dot_cols(q_ref[...], k_ref[...]) * SCALING + bias
    probability = jnp.exp(scores - lse_ref[0])
    grad_probs = dot_cols(do_ref[...], v_ref[...])
    inner = jnp.sum(probability * grad_probs, axis=1, keepdims=True)
    grad_scores = (probability * (grad_probs - inner)).astype(bf16)
    grad_query = dot(grad_scores, k_ref[...]) * SCALING
    moved = grad_query * sin_ref[...]
    sign = jnp.where(lax.broadcasted_iota(jnp.int32, moved.shape, 1) < HD // 2, 1.0, -1.0)
    dq_ref[...] = (
        grad_query * cos_ref[...] + pltpu.roll(moved, HD // 2, 1) * sign
    ).astype(bf16)
    dk_ref[...] += dot_rows(grad_scores, q_ref[...]) * SCALING
    dv_ref[...] += dot_rows(probability.astype(bf16), do_ref[...])

    @pl.when((head == pl.num_programs(0) - 1) & (i == pl.num_programs(1) - 1))
    def _():
        dkv_ref[0] = dk_ref[...].astype(bf16)
        dkv_ref[1] = dv_ref[...].astype(bf16)


def attention_back(key_blocks, queries, grad_out, lse, cosine, sine, kv):
    rows, width = queries.shape
    heads = width // HD
    whole = lambda kind: pl.BlockSpec((None,) + kv.shape[1:], lambda h, i, kb: (kind, 0, 0))
    tile = pl.BlockSpec((BLOCK, HD), lambda h, i, kb: (i, h))
    table = pl.BlockSpec((BLOCK, HD), lambda h, i, kb: (i, 0))
    return pl.pallas_call(
        functools.partial(attention_back_kernel, kv.shape[1] // BLOCK),
        name="attention_back",
        grid_spec=pltpu.PrefetchScalarGridSpec(
            num_scalar_prefetch=1,
            grid=(heads, rows // BLOCK),
            in_specs=[
                tile,
                tile,
                pl.BlockSpec((1, BLOCK, 1), lambda h, i, kb: (h, i, 0)),
                table,
                table,
                whole(0),
                whole(1),
            ],
            out_specs=[tile, pl.BlockSpec(kv.shape, lambda h, i, kb: (0, 0, 0))],
            scratch_shapes=[pltpu.VMEM(kv.shape[1:], f32)] * 2,
        ),
        out_shape=[
            jax.ShapeDtypeStruct((rows, width), bf16),
            jax.ShapeDtypeStruct(kv.shape, bf16),
        ],
        compiler_params=pltpu.CompilerParams(vmem_limit_bytes=VMEM_LIMIT),
    )(key_blocks, queries, grad_out, lse, cosine, sine, kv, kv)


def qkv_kernel(pieces, meta_ref, x_ref, gain_ref, bias_ref, cos_ref, sin_ref, *refs):
    weights, (xn_ref, q_ref, kv_ref) = refs[: 2 * pieces], refs[2 * pieces :]
    values = x_ref[...].astype(f32)
    factor = lax.rsqrt(jnp.mean(values * values, axis=-1, keepdims=True) + EPSILON)
    xn_ref[...] = (values * factor * gain_ref[...]).astype(bf16)
    depth = weights[0].shape[0]
    normed = [xn_ref[:, columns_of(meta_ref, j, depth, pieces)] for j in range(pieces)]
    cosine, sine = cos_ref[...], sin_ref[...]
    sign = jnp.where(lax.broadcasted_iota(jnp.int32, cosine.shape, 1) < HD // 2, -1.0, 1.0)
    sine = sine * sign
    width = q_ref.shape[1]
    total = bias_ref[:, :width] + sum(dot(x, w[...]) for x, w in zip(normed, weights[:pieces]))
    turn = lambda own: own * cosine + pltpu.roll(own, HD // 2, 1) * sine
    for h in range(width // HD):
        q_ref[:, h * HD : (h + 1) * HD] = turn(total[:, h * HD : (h + 1) * HD]).astype(bf16)
    own = bias_ref[:, width:] + sum(dot(x, w[...]) for x, w in zip(normed, weights[pieces:]))
    kv_ref[...] = jnp.where(meta_ref[2] == 0, turn(own), own).astype(bf16)


def columns_of(meta_ref, j, depth, pieces):
    if pieces == 1:
        return slice(None)
    return pl.ds(pl.multiple_of(meta_ref[j] * depth, LANES), depth)


def qkv(meta, inputs, gain, bias, cosine, sine, w_q, w_kv):
    rows, width = inputs.shape
    out = w_q[0].shape[1]
    tile = 256
    row = lambda n: pl.BlockSpec((tile, n), lambda i, m: (i, 0))
    fixed = lambda w: pl.BlockSpec(w.shape, lambda i, m: (0, 0))
    return pl.pallas_call(
        functools.partial(qkv_kernel, len(w_q)),
        name="qkv",
        grid_spec=pltpu.PrefetchScalarGridSpec(
            num_scalar_prefetch=1,
            grid=(rows // tile,),
            in_specs=[row(width), fixed(gain), fixed(bias), row(HD), row(HD)]
            + [fixed(w) for w in (*w_q, *w_kv)],
            out_specs=[row(width), row(out), row(HD)],
        ),
        out_shape=[
            jax.ShapeDtypeStruct((rows, width), bf16),
            jax.ShapeDtypeStruct((rows, out), bf16),
            jax.ShapeDtypeStruct((rows, HD), bf16),
        ],
        compiler_params=pltpu.CompilerParams(vmem_limit_bytes=VMEM_LIMIT),
    )(meta, inputs, gain, bias, cosine, sine, *w_q, *w_kv)


def qkv_back_kernel(pieces, meta_ref, dq_ref, dkv_ref, *refs):
    w_q, w_kv, out_ref = refs[:pieces], refs[pieces : 2 * pieces], refs[-1]
    for j in range(pieces):
        out_ref[:, columns_of(meta_ref, j, w_q[j].shape[0], pieces)] = (
            dot_cols(dq_ref[...], w_q[j][...]) + dot_cols(dkv_ref[...], w_kv[j][...])
        ).astype(bf16)


def qkv_back(meta, grad_q, grad_kv, w_q, w_kv):
    rows, width = grad_q.shape[0], sum(w.shape[0] for w in w_q)
    tile = 256
    row = lambda n: pl.BlockSpec((tile, n), lambda i, m: (i, 0))
    fixed = lambda w: pl.BlockSpec(w.shape, lambda i, m: (0, 0))
    return pl.pallas_call(
        functools.partial(qkv_back_kernel, len(w_q)),
        name="qkv_back",
        grid_spec=pltpu.PrefetchScalarGridSpec(
            num_scalar_prefetch=1,
            grid=(rows // tile,),
            in_specs=[row(grad_q.shape[1]), row(HD)] + [fixed(w) for w in (*w_q, *w_kv)],
            out_specs=row(width),
        ),
        out_shape=jax.ShapeDtypeStruct((rows, width), bf16),
        compiler_params=pltpu.CompilerParams(vmem_limit_bytes=VMEM_LIMIT),
    )(meta, grad_q, grad_kv, *w_q, *w_kv)


def add_rows(unit_refs, row_refs, columns, totals, outs):
    step = pl.program_id(0)

    @pl.when(step == 0)
    def _():
        for total in totals:
            total[...] = jnp.zeros_like(total)

    for total, unit, row in zip(totals, unit_refs, row_refs):
        total[...] += dot_rows(unit[...], row[:, columns])

    @pl.when(step == pl.num_programs(0) - 1)
    def _():
        for out, total in zip(outs, totals):
            out[...] = total[...].astype(bf16)


def hidden_kernel(pieces, meta_ref, x_ref, dy_ref, *refs):
    wg, wu, refs = refs[:pieces], refs[pieces : 2 * pieces], refs[2 * pieces :]
    hid_ref, slope_ref, gated_ref = refs[:3]
    columns = [columns_of(meta_ref, j, wg[j].shape[1], pieces) for j in range(pieces)]
    gate = sum(dot_cols(x_ref[:, at], w[...]) for at, w in zip(columns, wg))
    up = sum(dot_cols(x_ref[:, at], w[...]) for at, w in zip(columns, wu))
    sigma = 1.0 / (1.0 + jnp.exp(-gate))
    gated = gate * sigma
    hid_ref[...] = (gated * up).astype(bf16)
    slope_ref[...] = (up * (sigma + gated * (1.0 - sigma))).astype(bf16)
    gated_ref[...] = gated.astype(bf16)
    if pieces == 2:
        add_rows([hid_ref], [dy_ref], columns[1], refs[4:], refs[3:4])


def hidden_back_kernel(pieces, meta_ref, x_ref, dy_ref, hid_ref, slope_ref, gated_ref, *refs):
    wg, wu, wd = (refs[m * pieces : (m + 1) * pieces] for m in range(3))
    refs = refs[3 * pieces :]
    dg_ref, du_ref, dx_ref, out_ref = refs[:4]
    columns = [columns_of(meta_ref, j, wg[j].shape[1], pieces) for j in range(pieces)]
    grad_hidden = sum(dot_cols(dy_ref[:, at], w[...]) for at, w in zip(columns, wd))
    dg_ref[...] = (grad_hidden * slope_ref[...].astype(f32)).astype(bf16)
    du_ref[...] = (grad_hidden * gated_ref[...].astype(f32)).astype(bf16)

    @pl.when(pl.program_id(0) // (pl.num_programs(0) // 2) == meta_ref[3])
    def _():
        for at, g, u, d in zip(columns, wg, wu, wd):
            dx_ref[:, at] = (dot(dg_ref[...], g[...]) + dot(du_ref[...], u[...])).astype(bf16)
            out_ref[:, at] = dot(hid_ref[...], d[...]).astype(bf16)

    if pieces == 2:
        add_rows([dg_ref, du_ref], [x_ref, x_ref], columns[1], refs[6:], refs[4:6])


def hidden_specs(meta, normed, weights):
    width = normed.shape[-1]
    rows = normed.shape[0] * normed.shape[1]
    units, depth = weights[0].shape[0] // 2, weights[0].shape[1]
    tile = 512
    steps = rows // tile
    half = steps // 2
    once = pl.Buffered(1)
    inside = lambda i, m: jnp.clip(i - m[3] * half, 0, half - 1)
    return {
        "steps": steps,
        "flat": lambda x: x.reshape(-1, width),
        "row": pl.BlockSpec((tile, width), lambda i, m: (lax.rem(i + m[3] * half, steps), 0)),
        "unit": pl.BlockSpec((tile, units), lambda i, m: (i, 0)),
        "near_unit": pl.BlockSpec((tile, units), lambda i, m: (inside(i, m) + m[3] * half, 0)),
        "near_row": pl.BlockSpec((tile, width), lambda i, m: (inside(i, m), 0)),
        "weight": lambda k: pl.BlockSpec((units, depth), lambda i, m: (k, 0), pipeline_mode=once),
        "grad": pl.BlockSpec((units, depth), lambda i, m: (0, 0), pipeline_mode=once),
        "unit_shape": jax.ShapeDtypeStruct((rows, units), bf16),
        "near_shape": jax.ShapeDtypeStruct((rows // 2, width), bf16),
        "grad_shape": jax.ShapeDtypeStruct((units, depth), bf16),
        "total": pltpu.VMEM((units, depth), f32),
    }


def hidden_call(kernel, name, meta, args, in_specs, outs, grads, specs):
    return pl.pallas_call(
        kernel,
        name=name,
        grid_spec=pltpu.PrefetchScalarGridSpec(
            num_scalar_prefetch=1,
            grid=(specs["steps"],),
            in_specs=in_specs,
            out_specs=[specs[x] for x in outs] + [specs["grad"]] * grads,
            scratch_shapes=[specs["total"]] * grads,
        ),
        out_shape=[specs[x.split("_")[0] + "_shape"] for x in outs]
        + [specs["grad_shape"]] * grads,
        compiler_params=pltpu.CompilerParams(vmem_limit_bytes=VMEM_LIMIT),
    )(meta, *args)


def hidden_units(meta, normed, grad_out, weights):
    specs, pieces = hidden_specs(meta, normed, weights), len(weights)
    return hidden_call(
        functools.partial(hidden_kernel, pieces),
        "hidden_units",
        meta,
        [specs["flat"](normed), specs["flat"](grad_out)] + list(weights) * 2,
        [specs["row"]] * 2 + [specs["weight"](k) for k in range(2) for _ in weights],
        ["unit"] * 3,
        pieces == 2,
        specs,
    )


def hidden_back(meta, normed, grad_out, hidden, slope, gated, weights, down_weights):
    specs, pieces = hidden_specs(meta, normed, weights), len(weights)
    return hidden_call(
        functools.partial(hidden_back_kernel, pieces),
        "hidden_back",
        meta,
        [specs["flat"](normed), specs["flat"](grad_out), hidden, slope, gated]
        + list(weights) * 2
        + list(down_weights),
        [specs["row"]] * 2
        + [specs["near_unit"], specs["unit"], specs["unit"]]
        + [specs["weight"](k) for k in (0, 1, 0) for _ in weights],
        ["unit", "unit", "near_row", "near_row"],
        2 * (pieces == 2),
        specs,
    )


def unit_grads_kernel(count, meta_ref, near_ref, far_ref, *refs):
    units, out_ref, x_ref = refs[:count], refs[-2], refs[-1]
    half = near_ref.shape[0]
    x_ref[pl.ds(pl.multiple_of(meta_ref[3] * half, half), half)] = near_ref[...]
    x_ref[pl.ds(pl.multiple_of((1 - meta_ref[3]) * half, half), half)] = far_ref[...]
    for k, unit in enumerate(units):
        depth = unit.shape[1]
        out_ref[k * depth : (k + 1) * depth] = dot_rows(unit[...], x_ref[...]).astype(bf16)


def unit_grads(meta, which, pieces, x, units_of):
    width = x.shape[-1]
    count, (rows, units) = len(units_of), units_of[0].shape
    depth = width // pieces
    tile = 256
    steps = depth // tile
    shard = (lambda m: m[which]) if pieces > 1 else (lambda m: 0)
    feature = lambda half: pl.BlockSpec(
        (rows // 2, tile), lambda i, m: (half, shard(m) * steps + i)
    )
    unit = pl.BlockSpec((rows, units), lambda i, m: (0, 0), pipeline_mode=pl.Buffered(1))
    x = x.reshape(-1, width)
    return pl.pallas_call(
        functools.partial(unit_grads_kernel, count),
        name=f"unit_grads_{which}_{count}",
        grid_spec=pltpu.PrefetchScalarGridSpec(
            num_scalar_prefetch=1,
            grid=(steps,),
            in_specs=[feature(0), feature(1)] + [unit] * count,
            out_specs=pl.BlockSpec((count * units, tile), lambda i, m: (0, i)),
            scratch_shapes=[pltpu.VMEM((rows, tile), bf16)],
        ),
        out_shape=jax.ShapeDtypeStruct((count * units, depth), bf16),
        compiler_params=pltpu.CompilerParams(vmem_limit_bytes=VMEM_LIMIT),
    )(meta, x, x, *units_of)


class Wires:
    def __init__(self, sends, receives, locals_):
        self.sends, self.receives, self.locals = sends, receives, locals_
        self.used = self.used_local = 0
        self.started = []

    def plan(self, source, target, device):
        k = self.used
        self.used += 1
        return pltpu.make_async_remote_copy(
            source,
            target,
            self.sends.at[k],
            self.receives.at[k],
            device_id=device,
            device_id_type=pl.DeviceIdType.MESH,
        )

    def copy(self, source, target, device):
        one = self.plan(source, target, device)
        one.start()
        self.started.append(one)
        return one

    def here(self, source, target):
        k = self.used_local
        self.used_local += 1
        one = pltpu.make_async_copy(source, target, self.locals.at[k])
        one.start()
        return one

    def finish(self):
        for one in self.started:
            one.wait_send()


class OwnGrad:
    TILE = 256

    def __init__(self, units, rows, out, units_here, rows_here):
        self.units, self.rows, self.out = units, rows, out
        self.units_here, self.rows_here = units_here, rows_here
        self.tiles = out.shape[1] // self.TILE
        self.copies = None

    def fetch(self, wires):
        half, depth = self.rows.shape[0] // 2, self.out.shape[1]
        column = pl.multiple_of(lax.axis_index("fsdp") * depth, LANES)
        pair = lax.axis_index("context") // 2
        self.copies = [wires.here(self.units, self.units_here)]
        for k, place in ((0, pair), (1, 1 - pair)):
            self.copies.append(
                wires.here(
                    self.rows.at[pl.ds(k * half, half), pl.ds(column, depth)],
                    self.rows_here.at[pl.ds(pl.multiple_of(place * half, half), half)],
                )
            )

    def make(self, first, past):
        for one in self.copies:
            one.wait()
        self.copies = []

        @pl.loop(first, past)
        def _(k):
            at = pl.ds(pl.multiple_of(k * self.TILE, self.TILE), self.TILE)
            self.out[:, at] = dot_rows(self.units_here[...], self.rows_here[:, at]).astype(bf16)


def own_grad_call(fill, width):
    args = [x for pair in fill for x in pair]
    outs = [jax.ShapeDtypeStruct((units.shape[1], width), bf16) for units, _ in fill]
    scratch = []
    for units, rows in fill:
        scratch += [pltpu.VMEM(units.shape, bf16), pltpu.VMEM((rows.shape[0], width), bf16)]
    return args, outs, scratch


def own_grads(count, args, outs, scratch):
    return [
        OwnGrad(args[2 * k], args[2 * k + 1], outs[k], scratch[2 * k], scratch[2 * k + 1])
        for k in range(count)
    ]


def meet(devices):
    barrier = pltpu.get_barrier_semaphore()
    for device in devices:
        pl.semaphore_signal(barrier, inc=1, device_id=device, device_id_type=pl.DeviceIdType.MESH)
    pl.semaphore_wait(barrier, len(devices))


def partners():
    c, t = lax.axis_index("context"), lax.axis_index("tensor")
    flip = lambda x, bit: x + bit * (1 - 2 * lax.rem(x // bit, 2))
    return {
        "core": {"tensor": flip(t, 1)},
        "y": {"tensor": flip(t, 2)},
        "z": {"context": flip(c, 1)},
        "far": {"context": flip(c, 2)},
        "last": {"context": flip(flip(c, 1), 2)},
    }


def wide(x):
    return x.astype(f32)


def ranks():
    t = lax.axis_index("tensor")
    flip = lambda x, bit: x + bit * (1 - 2 * lax.rem(x // bit, 2))
    return (t, flip(t, 1), flip(t, 2), flip(flip(t, 1), 2))


def scatter_rank(wires, to, part, own, got_core, sent, got_y):
    size = part.shape[1] // 2
    halves = [pl.ds(0, size), pl.ds(size, size)]
    rank = ranks()
    from_core = {}
    for block in (1, 0):
        for k, at in enumerate(halves):
            from_core[block, k] = wires.copy(
                part.at[rank[1 + 2 * block], at], got_core.at[block, at], to["core"]
            )
    mine = [wires.here(part.at[rank[2 * block]], own.at[block]) for block in (0, 1)]
    yield
    for one in mine:
        one.wait()
    from_y = []
    for k, at in enumerate(halves):
        from_core[1, k].wait_recv()
        sent[at] = (wide(own[1, at]) + wide(got_core[1, at])).astype(bf16)
        from_y.append(wires.copy(sent.at[at], got_y.at[at], to["y"]))
    yield
    for k in range(2):
        from_core[0, k].wait_recv()
    total = wide(own[0]) + wide(got_core[0])
    for one in from_y:
        one.wait_recv()
    return total + wide(got_y[...])


def scatter_pair(wires, to, part, own, got_core, sent, got_y, got_z, diag_y, diag_z):
    size = part.shape[1] // 2
    low, high = pl.ds(0, size), pl.ds(size, size)
    from_core = {j: wires.copy(part.at[4 + j], got_core.at[j], to["core"]) for j in (3, 1, 2, 0)}
    mine = wires.here(part.at[pl.ds(0, 4)], own)
    yield
    mine.wait()
    both = lambda j, at: wide(own[j, at]) + wide(got_core[j, at])
    from_core[3].wait_recv()
    sent[2] = (wide(own[3]) + wide(got_core[3])).astype(bf16)
    via_z = wires.copy(sent.at[2, low], diag_z, to["z"])
    via_y = wires.copy(sent.at[2, high], diag_y, to["y"])
    from_core[1].wait_recv()
    sent[0, high] = both(1, high).astype(bf16)
    y_high = wires.copy(sent.at[0, high], got_y.at[high], to["y"])
    from_core[2].wait_recv()
    sent[1, low] = both(2, low).astype(bf16)
    z_low = wires.copy(sent.at[1, low], got_z.at[low], to["z"])
    yield
    via_z.wait_recv()
    sent[0, low] = (both(1, low) + wide(diag_z[...])).astype(bf16)
    y_low = wires.copy(sent.at[0, low], got_y.at[low], to["y"])
    via_y.wait_recv()
    sent[1, high] = (both(2, high) + wide(diag_y[...])).astype(bf16)
    z_high = wires.copy(sent.at[1, high], got_z.at[high], to["z"])
    yield
    from_core[0].wait_recv()
    total = wide(own[0]) + wide(got_core[0])
    for one in (y_high, z_low, y_low, z_high):
        one.wait_recv()
    return total + wide(got_y[...]) + wide(got_z[...])


def result_of(steps):
    while True:
        try:
            next(steps)
        except StopIteration as done:
            return done.value


def gather_rank(wires, to, block, out):
    size = block.shape[0] // 2
    halves = [pl.ds(0, size), pl.ds(size, size)]
    rank = ranks()
    mine = wires.here(block, out.at[rank[0]])
    from_y = [wires.copy(block.at[h], out.at[rank[0], h], to["y"]) for h in halves]
    from_core = [wires.copy(block, out.at[rank[0]], to["core"])]
    yield
    for h, one in zip(halves, from_y):
        one.wait_recv()
        from_core.append(wires.copy(out.at[rank[2], h], out.at[rank[2], h], to["core"]))
    for one in from_core:
        one.wait_recv()
    mine.wait()


def gather_pair(wires, to, block, out, base):
    size = block.shape[0] // 2
    low, high = pl.ds(0, size), pl.ds(size, size)
    at = lambda j: out.at[base + j]
    from_z = wires.copy(block, at(2), to["z"])
    yield
    from_y = wires.copy(block, at(1), to["y"])
    from_core = [wires.copy(block, at(4), to["core"])]
    yield
    from_y.wait_recv()
    via_z = wires.copy(out.at[base + 1, low], out.at[base + 3, low], to["z"])
    from_core.append(wires.copy(at(1), at(5), to["core"]))
    from_z.wait_recv()
    via_y = wires.copy(out.at[base + 2, high], out.at[base + 3, high], to["y"])
    from_core.append(wires.copy(at(2), at(6), to["core"]))
    yield
    via_z.wait_recv()
    via_y.wait_recv()
    from_core.append(wires.copy(at(3), at(7), to["core"]))
    return from_core


def remote_call(kernel, name, key, args, outs, scratch, copies, in_vmem):
    ins, out_in = in_vmem
    spaces = {True: pltpu.VMEM, False: pl.ANY, None: pltpu.HBM}
    spec = lambda inside: pl.BlockSpec(memory_space=spaces[inside])
    return pl.pallas_call(
        kernel,
        name=name,
        out_shape=outs,
        in_specs=[spec(x) for x in ins],
        out_specs=[spec(x) for x in out_in],
        scratch_shapes=list(scratch)
        + [
            pltpu.SemaphoreType.DMA((copies,)),
            pltpu.SemaphoreType.DMA((copies,)),
            pltpu.SemaphoreType.DMA((10,)),
        ],
        compiler_params=pltpu.CompilerParams(
            collective_id=key, has_side_effects=True, vmem_limit_bytes=VMEM_LIMIT
        ),
    )(*args)


def kv_gather_kernel(own_ref, out_ref, *sems):
    wires, to = Wires(*sems), partners()
    kind = lax.rem(lax.axis_index("tensor"), 2)
    rows = own_ref.shape[0]
    block = lambda j: out_ref.at[kind, pl.ds(j * rows, rows)]
    meet([to[k] for k in ("core", "z", "far", "last")])
    mine = wires.here(own_ref, block(0))
    arrive = [wires.copy(own_ref, block(j), to[k]) for j, k in ((3, "last"), (2, "far"), (1, "z"))]
    from_core = [wires.copy(own_ref, block(0), to["core"])]
    for j, one in ((1, arrive[2]), (2, arrive[1]), (3, arrive[0])):
        one.wait_recv()
        from_core.append(wires.copy(block(j), block(j), to["core"]))
    for one in from_core:
        one.wait_recv()
    mine.wait()
    wires.finish()


def kv_gather(own):
    rows, width = own.shape
    n_c = lax.axis_size("context")
    return remote_call(
        kv_gather_kernel,
        "kv_gather",
        0,
        [own],
        [jax.ShapeDtypeStruct((2, n_c * rows, width), bf16)],
        [],
        8,
        ([False], [False]),
    )[0]


def kv_scatter_kernel(count, part_ref, *refs):
    args, dkv_ref, outs = refs[: 2 * count], refs[2 * count], refs[2 * count + 1 : 3 * count + 1]
    own, got_core, sent, got = refs[3 * count + 1 : 3 * count + 5]
    wires, to = Wires(*refs[-3:]), partners()
    fill = own_grads(count, args, outs, refs[3 * count + 5 : -3])
    kind = lax.rem(lax.axis_index("tensor"), 2)
    rows = dkv_ref.shape[0]
    block = lambda j: pl.ds(j * rows, rows)
    meet([to[k] for k in ("core", "z", "far", "last")])
    steps = ((3, "last"), (2, "far"), (1, "z"), (0, None))
    from_core = {
        j: wires.copy(part_ref.at[1 - kind, block(j)], got_core.at[block(j)], to["core"])
        for j, _ in steps
    }
    mine = wires.here(part_ref.at[kind], own)
    for one in fill:
        one.fetch(wires)
    mine.wait()
    arrive = []
    for j, k in steps[:3]:
        from_core[j].wait_recv()
        sent[block(j)] = (wide(own[block(j)]) + wide(got_core[block(j)])).astype(bf16)
        arrive.append(wires.copy(sent.at[block(j)], got.at[block(j)], to[k]))
    for one in fill:
        one.make(0, one.tiles)
    from_core[0].wait_recv()
    total = wide(own[block(0)]) + wide(got_core[block(0)])
    for one in arrive:
        one.wait_recv()
    for j in (1, 2, 3):
        total = total + wide(got[block(j)])
    dkv_ref[...] = total
    wires.finish()


def kv_scatter(part, fill, width):
    _, rows, depth = part.shape
    n_c = lax.axis_size("context")
    args, outs, scratch = own_grad_call(fill, width)
    return remote_call(
        functools.partial(kv_scatter_kernel, len(fill)),
        "kv_scatter",
        1,
        [part, *args],
        [jax.ShapeDtypeStruct((rows // n_c, depth), f32), *outs],
        [pltpu.VMEM((rows, depth), bf16)] * 4 + scratch,
        7,
        ([False] * (1 + len(args)), [True] * (1 + len(outs))),
    )


def middle_kernel(
    part,
    x_ref,
    gain_ref,
    dy_ref,
    dy_y,
    dy_z,
    dy_far,
    mid_ref,
    factor_ref,
    out,
    dys,
    own,
    core,
    sent,
    got,
    xn,
    *sems,
):
    wires, to = Wires(*sems), partners()
    blocks = out.shape[0] // 2
    size = xn.shape[0] // 2
    low, high = pl.ds(0, size), pl.ds(size, size)
    meet([to[k] for k in ("core", "y", "z", "far")])
    summed = scatter_rank(wires, to, part, own, core, sent, got)
    next(summed)
    mine = [
        wires.here(block, dys.at[k])
        for block, k in ((dy_ref, 0), (dy_y, 1), (dy_z, 2), (dy_far, blocks))
    ]
    via_z = wires.copy(dy_y.at[low], dys.at[3, low], to["z"])
    dy_last = gather_pair(wires, to, dy_far, dys, blocks)
    next(dy_last)
    next(summed)
    via_y = wires.copy(dy_z.at[high], dys.at[3, high], to["y"])
    ends = [
        wires.copy(block, dys.at[4 + k], to["core"])
        for k, block in enumerate((dy_ref, dy_y, dy_z))
    ]
    next(dy_last)
    middle = wide(x_ref[...]) + result_of(summed)
    mid_ref[...] = middle
    factor = lax.rsqrt(jnp.mean(middle * middle, axis=-1, keepdims=True) + EPSILON)
    factor_ref[...] = factor
    xn[...] = (middle * factor * gain_ref[...]).astype(bf16)
    mine.append(wires.here(xn, out.at[0]))
    xn_far = wires.copy(xn, out.at[blocks], to["far"])
    xn_near = gather_pair(wires, to, xn, out, 0)
    next(xn_near)
    next(xn_near)
    via_z.wait_recv()
    via_y.wait_recv()
    ends.append(wires.copy(dys.at[3], dys.at[7], to["core"]))
    next(dy_last)
    next(xn_near)
    xn_far.wait_recv()
    xn_last = gather_pair(wires, to, out.at[blocks], out, blocks)
    next(xn_last)
    next(xn_last)
    ends += result_of(dy_last) + result_of(xn_near)
    next(xn_last)
    ends += result_of(xn_last)
    for one in ends:
        one.wait_recv()
    for one in mine:
        one.wait()
    wires.finish()


def middle_norm(part, inputs_part, gain, dy_blocks):
    rows, width = inputs_part.shape
    return remote_call(
        middle_kernel,
        "middle_norm",
        2,
        [part.reshape(4, rows, width), inputs_part, gain, *dy_blocks],
        [
            jax.ShapeDtypeStruct((rows, width), f32),
            jax.ShapeDtypeStruct((rows, 1), f32),
            jax.ShapeDtypeStruct((16, rows, width), bf16),
            jax.ShapeDtypeStruct((16, rows, width), bf16),
        ],
        [
            pltpu.VMEM((2, rows, width), bf16),
            pltpu.VMEM((2, rows, width), bf16),
            pltpu.VMEM((rows, width), bf16),
            pltpu.VMEM((rows, width), bf16),
            pltpu.VMEM((rows, width), bf16),
        ],
        48,
        ([False] + [True] * 6, [True, True, False, False]),
    )


def norm_back_rows(values, factor, gain, grad_normed):
    gained = gain * grad_normed
    inner = jnp.mean(gained * values, axis=-1, keepdims=True)
    grad_values = factor * gained - values * (factor * factor * factor) * inner
    return grad_values, jnp.sum(grad_normed * values * factor, axis=0, keepdims=True)


def middle_back_kernel(count, part, mid_ref, factor_ref, gain_ref, dy_ref, *refs):
    args, refs = refs[: 2 * count], refs[2 * count :]
    source_ref, refs = (refs[0], refs[1:]) if count else (None, refs)
    (dmid_ref, dgain_ref, out), refs = refs[:3], refs[3:]
    outs, refs = refs[:count], refs[count:]
    (upper_ref, lower_ref, far_ref), refs = (
        (refs[:3], refs[3:]) if count else ((None, None, None), refs)
    )
    low, first, wires, to = refs[0], refs[1:8], Wires(*refs[-3:]), partners()
    fill = own_grads(count, args, outs, refs[8 : 8 + 2 * count])
    meet([to[k] for k in ("core", "y", "z")])
    back = scatter_pair(wires, to, part, *first)
    next(back)
    for one in fill:
        one.fetch(wires)
    if fill:
        got_ref = refs[8 + 2 * count]
        fetched = wires.here(source_ref, got_ref)
    next(back)
    if fill:
        fill[0].make(0, 1)
    next(back)
    if fill:
        fill[0].make(1, fill[0].tiles)
        fetched.wait()
        cut = upper_ref.shape[0]
        upper_ref[...] = (wide(outs[0][:cut]) + wide(got_ref[:cut])).astype(bf16)
        near_half = wires.copy(upper_ref, far_ref, to["z"])
        lower_ref[...] = (wide(outs[0][cut:]) + wide(got_ref[cut:])).astype(bf16)
    grad_normed = result_of(back)
    du, dgain = norm_back_rows(mid_ref[...], factor_ref[...], gain_ref[...], grad_normed)
    dgain_ref[...] = dgain
    dmid = wide(dy_ref[...]) + du
    low[...] = dmid.astype(bf16)
    share = gather_rank(wires, to, low, out)
    next(share)
    dmid_ref[...] = dmid
    for one in fill[1:]:
        one.make(0, one.tiles)
    result_of(share)
    if fill:
        near_half.wait_recv()
    wires.finish()


def pair_scratch(rows, width):
    return [
        pltpu.VMEM((4, rows, width), bf16),
        pltpu.VMEM((4, rows, width), bf16),
        pltpu.VMEM((3, rows, width), bf16),
        pltpu.VMEM((rows, width), bf16),
        pltpu.VMEM((rows, width), bf16),
        pltpu.VMEM((rows // 2, width), bf16),
        pltpu.VMEM((rows // 2, width), bf16),
    ]


def middle_back(part, middle, factor, gain, dy_part, fill, got, shard):
    rows, width = middle.shape
    args, outs, scratch = own_grad_call(fill, shard)
    if fill:
        args = [*args, got]
        scratch = [*scratch, pltpu.VMEM(got.shape, bf16)]
        units = got.shape[0]
        cut = units // 64 * 16
        outs = [*outs, *(jax.ShapeDtypeStruct((n, shard), bf16) for n in (cut, units - cut, cut))]
    return remote_call(
        functools.partial(middle_back_kernel, len(fill)),
        "middle_back",
        3,
        [part.reshape(8, rows, width), middle, factor, gain, dy_part, *args],
        [
            jax.ShapeDtypeStruct((rows, width), f32),
            jax.ShapeDtypeStruct((1, width), f32),
            jax.ShapeDtypeStruct((4, rows, width), bf16),
            *outs,
        ],
        [pltpu.VMEM((rows, width), bf16)] + pair_scratch(rows, width) + scratch,
        16,
        (
            [False] + [True] * 4 + [None] * len(args),
            [True, True, False] + ([True] * (len(outs) - 1) + [False] if fill else []),
        ),
    )


def add_all(wires, ways, value, slots):
    for k, device in enumerate(ways):
        one = wires.copy(value, slots.at[k], device)
        one.wait()
        wires.started = [x for x in wires.started if x is not one]
        value[...] = value[...] + slots[k]


def input_back_kernel(
    part, x_ref, gain_ref, dmid_ref, small_ref, sum_ref, out, *rest
):
    low, own, core, sent, got, slots = rest[:-3]
    wires, to = Wires(*rest[-3:]), partners()
    meet([to[k] for k in ("core", "y")])
    grad_normed = result_of(scatter_rank(wires, to, part, own, core, sent, got))
    values = wide(x_ref[...])
    factor = lax.rsqrt(jnp.mean(values * values, axis=-1, keepdims=True) + EPSILON)
    du, dgain = norm_back_rows(values, factor, gain_ref[...], grad_normed)
    low[...] = (dmid_ref[...] + du).astype(bf16)
    share = gather_rank(wires, to, low, out)
    next(share)
    width = dgain.shape[1]
    sum_ref[:, width:] = small_ref[:, width:]
    sum_ref[:, :width] = dgain
    add_all(wires, [to["core"], to["y"]], sum_ref, slots)
    result_of(share)
    wires.finish()


def input_back(part, inputs_part, gain, grad_middle, small):
    rows, width = inputs_part.shape
    return remote_call(
        input_back_kernel,
        "input_back",
        5,
        [part.reshape(4, rows, width), inputs_part, gain, grad_middle, small],
        [
            jax.ShapeDtypeStruct(small.shape, f32),
            jax.ShapeDtypeStruct((4, rows, width), bf16),
        ],
        [
            pltpu.VMEM((rows, width), bf16),
            pltpu.VMEM((2, rows, width), bf16),
            pltpu.VMEM((2, rows, width), bf16),
            pltpu.VMEM((rows, width), bf16),
            pltpu.VMEM((rows, width), bf16),
            pltpu.VMEM((2,) + small.shape, f32),
        ],
        16,
        ([False, True, True, True, True], [True, False]),
    )


def context_sum_kernel(over_f, *refs):
    parts, small_ref, out_part, mid_ref = refs[:3], refs[3], refs[4], refs[5]
    outs, sum_ref, shared, outputs = refs[6:8], refs[8], refs[9], refs[10]
    lows, from_end, from_middle = refs[11:15], refs[15:19], refs[19:23]
    out_low, slot, scratch = refs[23], refs[24], refs[25:32]
    wires, to, c = Wires(*refs[32:]), partners(), lax.axis_index("context")
    end = (c == 0) | (c == lax.axis_size("context") - 1)
    inner = jnp.logical_not(end)
    greet = ["core", "y", "z", "last"]
    if over_f:
        to["f"] = {"fsdp": 1 - lax.axis_index("fsdp")}
        greet.append("f")
    meet([to[k] for k in greet])
    ahead = scatter_pair(wires, to, out_part, *scratch)
    next(ahead)
    sum_ref[...] = small_ref[...]
    from_f = wires.copy(small_ref, slot, to["f"]) if over_f else None
    sources = [*parts, sum_ref]
    chunks = []
    for i, cuts in ((2, 1), (0, 2), (1, 4), (3, 1)):
        size = sources[i].shape[0] // cuts
        chunks += [(i, pl.ds(k * size, size)) for k in range(cuts)]
    inward = [wires.plan(sources[i].at[at], from_end[i].at[at], to["z"]) for i, at in chunks]
    across = [wires.plan(lows[i].at[at], from_middle[i].at[at], to["last"]) for i, at in chunks]
    outward = [wires.plan(lows[i].at[at], lows[i].at[at], to["z"]) for i, at in chunks]
    small = len(chunks) - 1

    def send_in(k):
        @pl.when(end)
        def _():
            inward[k].start()

    def pass_on(first, past):
        @pl.when(inner)
        def _():
            for k in range(first, past):
                i, at = chunks[k]
                inward[k].wait_recv()
                total = wide(sources[i][at]) + wide(from_end[i][at])
                lows[i][at] = total.astype(lows[i].dtype)
                across[k].start()
                if k:
                    send_out(k - 1)

    def send_out(k):
        i, at = chunks[k]
        across[k].wait()
        lows[i][at] = (wide(lows[i][at]) + wide(from_middle[i][at])).astype(lows[i].dtype)
        outward[k].start()

    early = 3
    for k in range(early):
        send_in(k)
    next(ahead)
    for k in range(early, small):
        send_in(k)
    pass_on(0, early)
    next(ahead)
    if over_f:
        from_f.wait_recv()
        sum_ref[...] = sum_ref[...] + slot[...]
    send_in(small)
    pass_on(early, small + 1)
    out_low[...] = (mid_ref[...] + result_of(ahead)).astype(bf16)
    out_share = gather_rank(wires, to, out_low, outputs)
    next(out_share)

    @pl.when(inner)
    def _():
        send_out(small)

    result_of(out_share)

    def arrived(k):
        @pl.when(end)
        def _():
            outward[k].wait_recv()

    arrived(0)
    share = gather_rank(wires, to, lows[2], shared)
    next(share)
    for k in range(1, len(chunks)):
        arrived(k)

    @pl.when(end)
    def _():
        for one in inward:
            one.wait_send()

    for i in (0, 1):
        outs[i][...] = wide(lows[i][...])
    sum_ref[...] = lows[3][...]
    result_of(share)

    @pl.when(inner)
    def _():
        for one in outward:
            one.wait_send()

    wires.finish()


def context_sum(over_f, parts, small, out_part, middle):
    rows, width = middle.shape
    lines = [pltpu.VMEM(x.shape, x.dtype) for x in (*parts, small)]
    return remote_call(
        functools.partial(context_sum_kernel, over_f),
        "context_sum",
        6,
        [*parts, small, out_part.reshape(8, rows, width), middle],
        [jax.ShapeDtypeStruct(x.shape, f32) for x in parts[:2]]
        + [jax.ShapeDtypeStruct(small.shape, f32)]
        + [jax.ShapeDtypeStruct((4,) + parts[2].shape, bf16)]
        + [jax.ShapeDtypeStruct((4, rows, width), bf16)],
        lines * 3
        + [pltpu.VMEM((rows, width), bf16), pltpu.VMEM(small.shape, f32)]
        + pair_scratch(rows, width),
        48,
        ([True] * 4 + [False, True], [True] * 3 + [False] * 2),
    )


def build(n_f, n_c, n_t):
    def flip(x, axis, bit):
        size = {"fsdp": n_f, "context": n_c, "tensor": n_t}[axis]
        return lax.ppermute(x, axis, [(i, i ^ bit) for i in range(size)])

    def by_bit(bit, x, other, axis):
        return jnp.where(
            bit == 0,
            jnp.concatenate([x, other], axis=axis),
            jnp.concatenate([other, x], axis=axis),
        )

    def after(x, *others):
        return lax.optimization_barrier((x, others))[0]

    def local(
        inputs,
        cotangent,
        blocks,
        attn_gain,
        w_query,
        b_query,
        w_key,
        b_key,
        w_value,
        b_value,
        w_out,
        ffn_gain,
        w_gate,
        w_up,
        w_down,
    ):
        rows, width = inputs.shape
        f = lax.axis_index("fsdp")
        c = lax.axis_index("context")
        t = lax.axis_index("tensor")
        core, parity, pair = t % 2, c % 2, c // 2
        heads = w_query.shape[1] // HD
        group = (t * heads) // (H // KV)
        part = rows // n_t
        units_all = w_gate.shape[1]
        units = units_all // 2

        def gather_f(x, axis):
            if n_f == 2:
                return by_bit(f, x, flip(x, "fsdp", 1), axis)
            return lax.all_gather(x, "fsdp", axis=axis, tiled=True)

        def grad_far(left, right, side):
            if n_f > 2:
                return None
            source = (left, right)[side]
            half = width // 2
            far = lax.dynamic_slice_in_dim(source, (1 - f) * half, half, 1)
            return (dot_rows(far, right) if side == 0 else dot_rows(left, far)).astype(bf16)

        def grad_sum(left, right, side, far, late):
            if n_f > 2:
                return lax.psum_scatter(
                    dot_rows(left, right).astype(bf16), "fsdp", scatter_dimension=side, tiled=True
                )
            source = (left, right)[side]
            half = width // 2
            own = lax.dynamic_slice_in_dim(source, f * half, half, 1)
            own = dot_rows(own, right) if side == 0 else dot_rows(left, own)
            return (own + after(flip(far, "fsdp", 1), late).astype(f32)).astype(bf16)

        small = jnp.concatenate(
            [v.reshape(1, -1) for v in (attn_gain, ffn_gain, b_query, b_key, b_value)], axis=1
        )
        column = lambda w: lax.dynamic_slice_in_dim(w, group * HD, HD, 1)
        w_kv_own = jnp.where(core == 0, column(w_key), column(w_value))
        pieces_f = lambda x, axis: (
            [x, flip(x, "fsdp", 1)]
            if n_f == 2
            else [lax.all_gather(x, "fsdp", axis=axis, tiled=True)]
        )
        meta = jnp.stack([f, 1 - f, core, pair]).astype(jnp.int32)
        w_q = pieces_f(w_query, 0)
        w_kv = pieces_f(w_kv_own, 0)
        small = gather_f(small, 0)
        w_out_all = gather_f(after(w_out, small, w_q, w_kv), 1)
        piece = attn_gain.shape[0]
        gain_first = small[:, :piece].reshape(1, width).astype(f32)
        gain_second = small[:, piece : 2 * piece].reshape(1, width).astype(f32)
        bias_of = lambda lo, n: (
            small[:, lo : lo + n * (HD // n_f)]
            .reshape(n_f, n, HD // n_f)
            .transpose(1, 0, 2)
            .reshape(n, HD)
            .astype(f32)
        )
        at = 2 * piece
        bq = bias_of(at, heads)
        bk = bias_of(at + heads * (HD // n_f), KV)
        bv = bias_of(at + (heads + KV) * (HD // n_f), KV)
        b_kv = lax.dynamic_index_in_dim(jnp.where(core == 0, bk, bv), group, 0)

        unit_slice = lambda w: lax.dynamic_slice_in_dim(w, parity * units, units, 0)
        own_gate_up = jnp.concatenate(
            [unit_slice(after(w, w_kv_own)) for w in (w_gate.T, w_up.T)], axis=0
        )
        own_down = unit_slice(w_down)

        dy_part = lax.dynamic_slice_in_dim(cotangent, t * part, part, 0)

        seq_blocks = blocks[0].reshape(n_c, -1)
        own_blocks = seq_blocks.shape[1]
        key_blocks = jnp.concatenate(
            [lax.dynamic_index_in_dim(seq_blocks, c ^ j, 0, keepdims=False) for j in range(n_c)]
        )
        positions = (
            key_blocks[:own_blocks, None] * BLOCK + jnp.arange(BLOCK, dtype=jnp.int32)[None, :]
        ).reshape(-1)
        cosine, sine = rope_tables(positions)
        bias = jnp.concatenate([bq.reshape(1, -1), b_kv], axis=1)
        dy_blocks = [
            dy_part,
            flip(dy_part, "tensor", 2),
            flip(dy_part, "context", 1),
            flip(dy_part, "context", 2),
        ]
        inputs_part = lax.dynamic_slice_in_dim(inputs, t * part, part, 0)
        bias = after(bias, dy_blocks[2:], own_gate_up, own_down, inputs_part)
        normed, queries, kv_own = qkv(
            meta, inputs, gain_first, bias, cosine, sine, w_q, w_kv
        )
        kv = after(kv_gather(kv_own), w_out_all)
        far_gate_up = pieces_f(after(own_gate_up, kv), 1)[-1]
        w_gate_up = [own_gate_up, far_gate_up] if n_f == 2 else [far_gate_up]
        far_down = pieces_f(after(own_down, kv), 1)[-1]
        w_downs = [own_down, far_down] if n_f == 2 else [far_down]
        attended, lse = attention(key_blocks, queries, kv)
        middle, factor_second, normed2, dy_all = middle_norm(
            dot(attended, w_out_all).astype(bf16), inputs_part, gain_second, dy_blocks
        )

        hidden, slope, gated, *down_far = hidden_units(meta, normed2, dy_all, w_gate_up)
        grad_gate, grad_up, dx_part, out_part, *unit_far = hidden_back(
            meta, normed2, dy_all, hidden, slope, gated, w_gate_up, w_downs
        )
        unit_far = [*down_far, *unit_far]
        flat = lambda x: x.reshape(-1, width)
        if n_f == 2:
            down_got, gate_got, up_got = (flip(x, "fsdp", 1) for x in unit_far)
            early = [(hidden, flat(dy_all)), (grad_gate, flat(normed2))]
            later = [(grad_up, flat(normed2))]
        else:
            over_f = lambda x: lax.psum_scatter(x, "fsdp", scatter_dimension=1, tiled=True)
            owns = [
                over_f(unit_grads(meta, 0, 1, x, [unit]))
                for x, unit in ((dy_all, hidden), (normed2, grad_gate), (normed2, grad_up))
            ]
            down_got = gate_got = up_got = jnp.zeros_like(owns[0])
            early = later = []

        def unit_whole(own, other):
            own, other = (jnp.concatenate(x, axis=0) for x in (own, other))
            return by_bit(parity, own, other, 0).astype(f32)

        grad_middle, ffn_gain_grad, grad_middle_low, *first_owns = middle_back(
            dx_part, middle, factor_second, gain_second, dy_part, early, down_got, width // n_f
        )
        grad_middle_low = grad_middle_low.reshape(rows, width)
        add = lambda own, got: (own.astype(f32) + got.astype(f32)).astype(bf16)
        upper = units // 2
        if n_f == 2:
            _, gate_own, down_upper, down_lower, far_upper = first_owns
        else:
            down_low, gate_own = owns[:2]
            down_upper, down_lower = down_low[:upper], down_low[upper:]
            far_upper = flip(down_upper, "context", 1)
        far_lower = flip(down_lower, "context", 1)
        grad_attended = dot_cols(grad_middle_low, w_out_all).astype(bf16)

        dq_low, dkv = attention_back(key_blocks, queries, grad_attended, lse, cosine, sine, kv)
        attention_args = [(attended, after(grad_middle_low, dq_low), 1), (normed, dq_low, 0)]
        fars = [grad_far(*args) for args in attention_args]
        gate_low = add(gate_own, after(gate_got, dq_low))
        dkv, *last_owns = kv_scatter(
            after(dkv, fars, gate_low, far_lower), later, width // n_f
        )
        (up_own,) = last_owns or owns[2:]
        far_gate = flip(after(gate_low, dkv, far_lower), "context", 1)
        dkv = after(dkv, far_lower)
        dkv_low = jnp.where(core == 0, rotate_back(dkv, cosine, sine), dkv).astype(bf16)
        own_biases = jnp.sum(
            jnp.concatenate([dq_low, dkv_low], axis=1).astype(f32), axis=0, keepdims=True
        )
        slots = lax.dynamic_update_slice(
            jnp.zeros((n_t, (heads + 1) * HD), f32), own_biases, (t, 0)
        )
        small_grads = jnp.concatenate(
            [jnp.zeros((1, width), f32), ffn_gain_grad, slots.reshape(1, -1)], axis=1
        )
        grad_qkv = qkv_back(meta, dq_low, dkv_low, w_q, w_kv)
        up_low = add(up_own, after(up_got, grad_qkv))
        attention_args.append((after(normed, grad_qkv), dkv_low, 0))
        fars.append(grad_far(*attention_args[-1]))
        far_up = flip(up_low, "context", 1)
        small_grads, input_grad = input_back(
            after(grad_qkv, up_low, fars),
            inputs_part,
            gain_first,
            grad_middle,
            small_grads,
        )
        input_grad = input_grad.reshape(rows, width)
        if n_f > 2:
            small_grads = lax.psum(small_grads, "fsdp")
        zero = jnp.minimum(t, 0).astype(bf16)
        input_grad = input_grad + zero
        small_grads = after(small_grads, far_gate)
        attention_parts = [
            grad_sum(*args, far, small_grads) for args, far in zip(attention_args, fars)
        ]
        wd_grad = unit_whole(
            *after(((down_upper, down_lower), (far_upper, far_lower)), small_grads)
        )
        wg_grad = unit_whole(*after(((gate_low,), (far_gate,)), small_grads))
        small_grads, wd_grad, wg_grad, input_grad = lax.optimization_barrier(
            (small_grads, wd_grad, wg_grad, input_grad)
        )
        wo_grad, wq_grad, packed, wkv_all, outputs = context_sum(
            n_f == 2, attention_parts, small_grads, out_part, middle
        )
        wo_grad, wq_grad, packed, wkv_all, outputs, far_up = lax.optimization_barrier(
            (wo_grad, wq_grad, packed, wkv_all, outputs, far_up)
        )
        outputs = outputs.reshape(rows, width)
        wk_grad = jnp.concatenate([wkv_all[0], wkv_all[2]], axis=1).astype(f32)
        wv_grad = jnp.concatenate([wkv_all[1], wkv_all[3]], axis=1).astype(f32)
        packed = packed[0]
        attn_gain_grad = lax.dynamic_slice_in_dim(packed, f * piece, piece, 0)
        ffn_gain_grad = lax.dynamic_slice_in_dim(packed, width + f * piece, piece, 0)
        slots = packed[2 * width :].reshape(n_t, heads + 1, HD)
        slots = lax.dynamic_slice_in_dim(slots, f * (HD // n_f), HD // n_f, 2)
        bq_out = lax.dynamic_index_in_dim(slots, t, 0, keepdims=False)[:heads]
        bk_out = slots[0::2, heads]
        bv_out = slots[1::2, heads]

        wu_grad = unit_whole((up_low,), (far_up,))
        wg_grad, wu_grad = wg_grad.T, wu_grad.T

        return (
            outputs,
            input_grad,
            attn_gain_grad,
            wq_grad,
            bq_out,
            wk_grad,
            bk_out,
            wv_grad,
            bv_out,
            wo_grad,
            ffn_gain_grad,
            wg_grad,
            wu_grad,
            wd_grad,
        )

    return local


def solution(mesh):
    in_specs = (
        P(("fsdp", "context"), None),
        P(("fsdp", "context"), None),
        P("fsdp", None),
        P("fsdp"),
        P("fsdp", "tensor"),
        P("tensor", "fsdp"),
        P("fsdp", None),
        P(None, "fsdp"),
        P("fsdp", None),
        P(None, "fsdp"),
        P("tensor", "fsdp"),
        P("fsdp"),
        P("fsdp", "tensor"),
        P("fsdp", "tensor"),
        P("tensor", "fsdp"),
    )
    out_specs = (
        P(("fsdp", "context"), None),
        P(("fsdp", "context"), None),
        P("fsdp"),
        P("fsdp", "tensor"),
        P("tensor", "fsdp"),
        P("fsdp", None),
        P(None, "fsdp"),
        P("fsdp", None),
        P(None, "fsdp"),
        P("tensor", "fsdp"),
        P("fsdp"),
        P("fsdp", "tensor"),
        P("fsdp", "tensor"),
        P("tensor", "fsdp"),
    )
    local = build(mesh.shape["fsdp"], mesh.shape["context"], mesh.shape["tensor"])
    return jax.shard_map(local, mesh=mesh, in_specs=in_specs, out_specs=out_specs, check_vma=False)
```

```python
import functools

import jax
import jax.numpy as jnp
from jax import lax
from jax.experimental import pallas as pl
from jax.experimental.pallas import tpu as pltpu
from jax.sharding import PartitionSpec as P

H = 12
KV = 2
HD = 128
BLOCK = 256

EPSILON = 1e-06
ROPE_BASE = 1000000.0
MASKED = -1e30
SCALING = HD ** (-0.5)
LANES = 128
VMEM_LIMIT = 60 << 20

f32 = jnp.float32
bf16 = jnp.bfloat16


def rope_tables(positions):
    halfway = HD // 2
    frequency = ROPE_BASE ** (-(jnp.arange(halfway, dtype=f32) * 2.0 / HD))
    angles = positions.astype(f32)[:, None] * frequency[None, :]
    cosine, sine = jnp.cos(angles), jnp.sin(angles)
    return (jnp.concatenate([cosine, cosine], axis=1), jnp.concatenate([sine, sine], axis=1))


def rotate(field, cosine, sine):
    halfway = HD // 2
    turned = jnp.concatenate([-field[..., halfway:], field[..., :halfway]], axis=-1)
    return field * cosine + turned * sine


def rotate_back(grad_field, cosine, sine):
    halfway = HD // 2
    moved = grad_field * sine
    turned = jnp.concatenate([moved[..., halfway:], -moved[..., :halfway]], axis=-1)
    return grad_field * cosine + turned


def dot(left, right):
    return jnp.dot(left, right, preferred_element_type=f32)


def dot_rows(left, right):
    return lax.dot_general(left, right, (((0,), (0,)), ((), ())), preferred_element_type=f32)


def dot_cols(left, right):
    return lax.dot_general(left, right, (((1,), (1,)), ((), ())), preferred_element_type=f32)


def mask_row(kb_ref, own_block, key_blocks):
    return jnp.concatenate(
        [
            jnp.full((1, BLOCK), jnp.where(kb_ref[j] <= own_block, 0.0, MASKED), f32)
            for j in range(key_blocks)
        ],
        axis=1,
    )


def attention_kernel(key_blocks, kb_ref, q_ref, k_ref, v_ref, o_ref, lse_ref):
    bias = mask_row(kb_ref, kb_ref[pl.program_id(1)], key_blocks)
    scores = dot_cols(q_ref[...], k_ref[...]) * SCALING + bias
    row_max = jnp.max(scores, axis=1, keepdims=True)
    expo = jnp.exp(scores - row_max)
    total = jnp.sum(expo, axis=1, keepdims=True)
    probability = (expo * (1.0 / total)).astype(bf16)
    o_ref[...] = dot(probability, v_ref[...]).astype(bf16)
    lse_ref[0] = row_max + jnp.log(total)


def attention(key_blocks, queries, kv):
    rows, width = queries.shape
    heads = width // HD
    whole = lambda kind: pl.BlockSpec((None,) + kv.shape[1:], lambda h, i, kb: (kind, 0, 0))
    tile = pl.BlockSpec((BLOCK, HD), lambda h, i, kb: (i, h))
    return pl.pallas_call(
        functools.partial(attention_kernel, kv.shape[1] // BLOCK),
        name="attention",
        grid_spec=pltpu.PrefetchScalarGridSpec(
            num_scalar_prefetch=1,
            grid=(heads, rows // BLOCK),
            in_specs=[tile, whole(0), whole(1)],
            out_specs=[tile, pl.BlockSpec((1, BLOCK, 1), lambda h, i, kb: (h, i, 0))],
        ),
        out_shape=[
            jax.ShapeDtypeStruct((rows, width), bf16),
            jax.ShapeDtypeStruct((heads, rows, 1), f32),
        ],
        compiler_params=pltpu.CompilerParams(vmem_limit_bytes=VMEM_LIMIT),
    )(key_blocks, queries, kv, kv)


def attention_back_kernel(
    key_blocks,
    kb_ref,
    q_ref,
    do_ref,
    lse_ref,
    cos_ref,
    sin_ref,
    k_ref,
    v_ref,
    dq_ref,
    dkv_ref,
    dk_ref,
    dv_ref,
):
    head, i = pl.program_id(0), pl.program_id(1)

    @pl.when((head == 0) & (i == 0))
    def _():
        dk_ref[...] = jnp.zeros_like(dk_ref)
        dv_ref[...] = jnp.zeros_like(dv_ref)

    bias = mask_row(kb_ref, kb_ref[i], key_blocks)
    scores = dot_cols(q_ref[...], k_ref[...]) * SCALING + bias
    probability = jnp.exp(scores - lse_ref[0])
    grad_probs = dot_cols(do_ref[...], v_ref[...])
    inner = jnp.sum(probability * grad_probs, axis=1, keepdims=True)
    grad_scores = (probability * (grad_probs - inner)).astype(bf16)
    grad_query = dot(grad_scores, k_ref[...]) * SCALING
    moved = grad_query * sin_ref[...]
    sign = jnp.where(lax.broadcasted_iota(jnp.int32, moved.shape, 1) < HD // 2, 1.0, -1.0)
    dq_ref[...] = (
        grad_query * cos_ref[...] + pltpu.roll(moved, HD // 2, 1) * sign
    ).astype(bf16)
    dk_ref[...] += dot_rows(grad_scores, q_ref[...]) * SCALING
    dv_ref[...] += dot_rows(probability.astype(bf16), do_ref[...])

    @pl.when((head == pl.num_programs(0) - 1) & (i == pl.num_programs(1) - 1))
    def _():
        dkv_ref[0] = dk_ref[...].astype(bf16)
        dkv_ref[1] = dv_ref[...].astype(bf16)


def attention_back(key_blocks, queries, grad_out, lse, cosine, sine, kv):
    rows, width = queries.shape
    heads = width // HD
    whole = lambda kind: pl.BlockSpec((None,) + kv.shape[1:], lambda h, i, kb: (kind, 0, 0))
    tile = pl.BlockSpec((BLOCK, HD), lambda h, i, kb: (i, h))
    table = pl.BlockSpec((BLOCK, HD), lambda h, i, kb: (i, 0))
    return pl.pallas_call(
        functools.partial(attention_back_kernel, kv.shape[1] // BLOCK),
        name="attention_back",
        grid_spec=pltpu.PrefetchScalarGridSpec(
            num_scalar_prefetch=1,
            grid=(heads, rows // BLOCK),
            in_specs=[
                tile,
                tile,
                pl.BlockSpec((1, BLOCK, 1), lambda h, i, kb: (h, i, 0)),
                table,
                table,
                whole(0),
                whole(1),
            ],
            out_specs=[tile, pl.BlockSpec(kv.shape, lambda h, i, kb: (0, 0, 0))],
            scratch_shapes=[pltpu.VMEM(kv.shape[1:], f32)] * 2,
        ),
        out_shape=[
            jax.ShapeDtypeStruct((rows, width), bf16),
            jax.ShapeDtypeStruct(kv.shape, bf16),
        ],
        compiler_params=pltpu.CompilerParams(vmem_limit_bytes=VMEM_LIMIT),
    )(key_blocks, queries, grad_out, lse, cosine, sine, kv, kv)


def qkv_kernel(pieces, meta_ref, x_ref, gain_ref, bias_ref, cos_ref, sin_ref, *refs):
    weights, (xn_ref, q_ref, kv_ref) = refs[: 2 * pieces], refs[2 * pieces :]
    values = x_ref[...].astype(f32)
    factor = lax.rsqrt(jnp.mean(values * values, axis=-1, keepdims=True) + EPSILON)
    xn_ref[...] = (values * factor * gain_ref[...]).astype(bf16)
    depth = weights[0].shape[0]
    normed = [xn_ref[:, columns_of(meta_ref, j, depth, pieces)] for j in range(pieces)]
    cosine, sine = cos_ref[...], sin_ref[...]
    sign = jnp.where(lax.broadcasted_iota(jnp.int32, cosine.shape, 1) < HD // 2, -1.0, 1.0)
    sine = sine * sign
    width = q_ref.shape[1]
    total = bias_ref[:, :width] + sum(dot(x, w[...]) for x, w in zip(normed, weights[:pieces]))
    turn = lambda own: own * cosine + pltpu.roll(own, HD // 2, 1) * sine
    for h in range(width // HD):
        q_ref[:, h * HD : (h + 1) * HD] = turn(total[:, h * HD : (h + 1) * HD]).astype(bf16)
    own = bias_ref[:, width:] + sum(dot(x, w[...]) for x, w in zip(normed, weights[pieces:]))
    kv_ref[...] = jnp.where(meta_ref[2] == 0, turn(own), own).astype(bf16)


def columns_of(meta_ref, j, depth, pieces):
    if pieces == 1:
        return slice(None)
    return pl.ds(pl.multiple_of(meta_ref[j] * depth, LANES), depth)


def qkv(meta, inputs, gain, bias, cosine, sine, w_q, w_kv):
    rows, width = inputs.shape
    out = w_q[0].shape[1]
    tile = 256
    row = lambda n: pl.BlockSpec((tile, n), lambda i, m: (i, 0))
    fixed = lambda w: pl.BlockSpec(w.shape, lambda i, m: (0, 0))
    return pl.pallas_call(
        functools.partial(qkv_kernel, len(w_q)),
        name="qkv",
        grid_spec=pltpu.PrefetchScalarGridSpec(
            num_scalar_prefetch=1,
            grid=(rows // tile,),
            in_specs=[row(width), fixed(gain), fixed(bias), row(HD), row(HD)]
            + [fixed(w) for w in (*w_q, *w_kv)],
            out_specs=[row(width), row(out), row(HD)],
        ),
        out_shape=[
            jax.ShapeDtypeStruct((rows, width), bf16),
            jax.ShapeDtypeStruct((rows, out), bf16),
            jax.ShapeDtypeStruct((rows, HD), bf16),
        ],
        compiler_params=pltpu.CompilerParams(vmem_limit_bytes=VMEM_LIMIT),
    )(meta, inputs, gain, bias, cosine, sine, *w_q, *w_kv)


def qkv_back_kernel(pieces, meta_ref, dq_ref, dkv_ref, *refs):
    w_q, w_kv, out_ref = refs[:pieces], refs[pieces : 2 * pieces], refs[-1]
    for j in range(pieces):
        out_ref[:, columns_of(meta_ref, j, w_q[j].shape[0], pieces)] = (
            dot_cols(dq_ref[...], w_q[j][...]) + dot_cols(dkv_ref[...], w_kv[j][...])
        ).astype(bf16)


def qkv_back(meta, grad_q, grad_kv, w_q, w_kv):
    rows, width = grad_q.shape[0], sum(w.shape[0] for w in w_q)
    tile = 256
    row = lambda n: pl.BlockSpec((tile, n), lambda i, m: (i, 0))
    fixed = lambda w: pl.BlockSpec(w.shape, lambda i, m: (0, 0))
    return pl.pallas_call(
        functools.partial(qkv_back_kernel, len(w_q)),
        name="qkv_back",
        grid_spec=pltpu.PrefetchScalarGridSpec(
            num_scalar_prefetch=1,
            grid=(rows // tile,),
            in_specs=[row(grad_q.shape[1]), row(HD)] + [fixed(w) for w in (*w_q, *w_kv)],
            out_specs=row(width),
        ),
        out_shape=jax.ShapeDtypeStruct((rows, width), bf16),
        compiler_params=pltpu.CompilerParams(vmem_limit_bytes=VMEM_LIMIT),
    )(meta, grad_q, grad_kv, *w_q, *w_kv)


def add_rows(unit_refs, row_refs, columns, totals, outs):
    step = pl.program_id(0)

    @pl.when(step == 0)
    def _():
        for total in totals:
            total[...] = jnp.zeros_like(total)

    for total, unit, row in zip(totals, unit_refs, row_refs):
        total[...] += dot_rows(unit[...], row[:, columns])

    @pl.when(step == pl.num_programs(0) - 1)
    def _():
        for out, total in zip(outs, totals):
            out[...] = total[...].astype(bf16)


def hidden_kernel(pieces, meta_ref, x_ref, dy_ref, *refs):
    wg, wu, refs = refs[:pieces], refs[pieces : 2 * pieces], refs[2 * pieces :]
    hid_ref, slope_ref, gated_ref = refs[:3]
    columns = [columns_of(meta_ref, j, wg[j].shape[1], pieces) for j in range(pieces)]
    gate = sum(dot_cols(x_ref[:, at], w[...]) for at, w in zip(columns, wg))
    up = sum(dot_cols(x_ref[:, at], w[...]) for at, w in zip(columns, wu))
    sigma = 1.0 / (1.0 + jnp.exp(-gate))
    gated = gate * sigma
    hid_ref[...] = (gated * up).astype(bf16)
    slope_ref[...] = (up * (sigma + gated * (1.0 - sigma))).astype(bf16)
    gated_ref[...] = gated.astype(bf16)
    if pieces == 2:
        add_rows([hid_ref], [dy_ref], columns[1], refs[4:], refs[3:4])


def hidden_back_kernel(pieces, meta_ref, x_ref, dy_ref, hid_ref, slope_ref, gated_ref, *refs):
    wg, wu, wd = (refs[m * pieces : (m + 1) * pieces] for m in range(3))
    refs = refs[3 * pieces :]
    dg_ref, du_ref, dx_ref, out_ref = refs[:4]
    columns = [columns_of(meta_ref, j, wg[j].shape[1], pieces) for j in range(pieces)]
    grad_hidden = sum(dot_cols(dy_ref[:, at], w[...]) for at, w in zip(columns, wd))
    dg_ref[...] = (grad_hidden * slope_ref[...].astype(f32)).astype(bf16)
    du_ref[...] = (grad_hidden * gated_ref[...].astype(f32)).astype(bf16)

    @pl.when(pl.program_id(0) // (pl.num_programs(0) // 2) == meta_ref[3])
    def _():
        for at, g, u, d in zip(columns, wg, wu, wd):
            dx_ref[:, at] = (dot(dg_ref[...], g[...]) + dot(du_ref[...], u[...])).astype(bf16)
            out_ref[:, at] = dot(hid_ref[...], d[...]).astype(bf16)

    if pieces == 2:
        add_rows([dg_ref, du_ref], [x_ref, x_ref], columns[1], refs[6:], refs[4:6])


def hidden_specs(meta, normed, weights):
    width = normed.shape[-1]
    rows = normed.shape[0] * normed.shape[1]
    units, depth = weights[0].shape[0] // 2, weights[0].shape[1]
    tile = 512
    steps = rows // tile
    half = steps // 2
    once = pl.Buffered(1)
    inside = lambda i, m: jnp.clip(i - m[3] * half, 0, half - 1)
    return {
        "steps": steps,
        "flat": lambda x: x.reshape(-1, width),
        "row": pl.BlockSpec((tile, width), lambda i, m: (lax.rem(i + m[3] * half, steps), 0)),
        "unit": pl.BlockSpec((tile, units), lambda i, m: (i, 0)),
        "near_unit": pl.BlockSpec((tile, units), lambda i, m: (inside(i, m) + m[3] * half, 0)),
        "near_row": pl.BlockSpec((tile, width), lambda i, m: (inside(i, m), 0)),
        "weight": lambda k: pl.BlockSpec((units, depth), lambda i, m: (k, 0), pipeline_mode=once),
        "grad": pl.BlockSpec((units, depth), lambda i, m: (0, 0), pipeline_mode=once),
        "unit_shape": jax.ShapeDtypeStruct((rows, units), bf16),
        "near_shape": jax.ShapeDtypeStruct((rows // 2, width), bf16),
        "grad_shape": jax.ShapeDtypeStruct((units, depth), bf16),
        "total": pltpu.VMEM((units, depth), f32),
    }


def hidden_call(kernel, name, meta, args, in_specs, outs, grads, specs):
    return pl.pallas_call(
        kernel,
        name=name,
        grid_spec=pltpu.PrefetchScalarGridSpec(
            num_scalar_prefetch=1,
            grid=(specs["steps"],),
            in_specs=in_specs,
            out_specs=[specs[x] for x in outs] + [specs["grad"]] * grads,
            scratch_shapes=[specs["total"]] * grads,
        ),
        out_shape=[specs[x.split("_")[0] + "_shape"] for x in outs]
        + [specs["grad_shape"]] * grads,
        compiler_params=pltpu.CompilerParams(vmem_limit_bytes=VMEM_LIMIT),
    )(meta, *args)


def hidden_units(meta, normed, grad_out, weights):
    specs, pieces = hidden_specs(meta, normed, weights), len(weights)
    return hidden_call(
        functools.partial(hidden_kernel, pieces),
        "hidden_units",
        meta,
        [specs["flat"](normed), specs["flat"](grad_out)] + list(weights) * 2,
        [specs["row"]] * 2 + [specs["weight"](k) for k in range(2) for _ in weights],
        ["unit"] * 3,
        pieces == 2,
        specs,
    )


def hidden_back(meta, normed, grad_out, hidden, slope, gated, weights, down_weights):
    specs, pieces = hidden_specs(meta, normed, weights), len(weights)
    return hidden_call(
        functools.partial(hidden_back_kernel, pieces),
        "hidden_back",
        meta,
        [specs["flat"](normed), specs["flat"](grad_out), hidden, slope, gated]
        + list(weights) * 2
        + list(down_weights),
        [specs["row"]] * 2
        + [specs["near_unit"], specs["unit"], specs["unit"]]
        + [specs["weight"](k) for k in (0, 1, 0) for _ in weights],
        ["unit", "unit", "near_row", "near_row"],
        2 * (pieces == 2),
        specs,
    )


def unit_grads_kernel(count, meta_ref, near_ref, far_ref, *refs):
    units, out_ref, x_ref = refs[:count], refs[-2], refs[-1]
    half = near_ref.shape[0]
    x_ref[pl.ds(pl.multiple_of(meta_ref[3] * half, half), half)] = near_ref[...]
    x_ref[pl.ds(pl.multiple_of((1 - meta_ref[3]) * half, half), half)] = far_ref[...]
    for k, unit in enumerate(units):
        depth = unit.shape[1]
        out_ref[k * depth : (k + 1) * depth] = dot_rows(unit[...], x_ref[...]).astype(bf16)


def unit_grads(meta, which, pieces, x, units_of):
    width = x.shape[-1]
    count, (rows, units) = len(units_of), units_of[0].shape
    depth = width // pieces
    tile = 256
    steps = depth // tile
    shard = (lambda m: m[which]) if pieces > 1 else (lambda m: 0)
    feature = lambda half: pl.BlockSpec(
        (rows // 2, tile), lambda i, m: (half, shard(m) * steps + i)
    )
    unit = pl.BlockSpec((rows, units), lambda i, m: (0, 0), pipeline_mode=pl.Buffered(1))
    x = x.reshape(-1, width)
    return pl.pallas_call(
        functools.partial(unit_grads_kernel, count),
        name=f"unit_grads_{which}_{count}",
        grid_spec=pltpu.PrefetchScalarGridSpec(
            num_scalar_prefetch=1,
            grid=(steps,),
            in_specs=[feature(0), feature(1)] + [unit] * count,
            out_specs=pl.BlockSpec((count * units, tile), lambda i, m: (0, i)),
            scratch_shapes=[pltpu.VMEM((rows, tile), bf16)],
        ),
        out_shape=jax.ShapeDtypeStruct((count * units, depth), bf16),
        compiler_params=pltpu.CompilerParams(vmem_limit_bytes=VMEM_LIMIT),
    )(meta, x, x, *units_of)


class Wires:
    def __init__(self, sends, receives, locals_):
        self.sends, self.receives, self.locals = sends, receives, locals_
        self.used = self.used_local = 0
        self.started = []

    def plan(self, source, target, device):
        k = self.used
        self.used += 1
        return pltpu.make_async_remote_copy(
            source,
            target,
            self.sends.at[k],
            self.receives.at[k],
            device_id=device,
            device_id_type=pl.DeviceIdType.MESH,
        )

    def copy(self, source, target, device):
        one = self.plan(source, target, device)
        one.start()
        self.started.append(one)
        return one

    def here(self, source, target):
        k = self.used_local
        self.used_local += 1
        one = pltpu.make_async_copy(source, target, self.locals.at[k])
        one.start()
        return one

    def finish(self):
        for one in self.started:
            one.wait_send()


class OwnGrad:
    TILE = 256

    def __init__(self, units, rows, out, units_here, rows_here):
        self.units, self.rows, self.out = units, rows, out
        self.units_here, self.rows_here = units_here, rows_here
        self.tiles = out.shape[1] // self.TILE
        self.copies = None

    def fetch(self, wires):
        half, depth = self.rows.shape[0] // 2, self.out.shape[1]
        column = pl.multiple_of(lax.axis_index("fsdp") * depth, LANES)
        pair = lax.axis_index("context") // 2
        self.copies = [wires.here(self.units, self.units_here)]
        for k, place in ((0, pair), (1, 1 - pair)):
            self.copies.append(
                wires.here(
                    self.rows.at[pl.ds(k * half, half), pl.ds(column, depth)],
                    self.rows_here.at[pl.ds(pl.multiple_of(place * half, half), half)],
                )
            )

    def make(self, first, past):
        for one in self.copies:
            one.wait()
        self.copies = []

        @pl.loop(first, past)
        def _(k):
            at = pl.ds(pl.multiple_of(k * self.TILE, self.TILE), self.TILE)
            self.out[:, at] = dot_rows(self.units_here[...], self.rows_here[:, at]).astype(bf16)


def own_grad_call(fill, width):
    args = [x for pair in fill for x in pair]
    outs = [jax.ShapeDtypeStruct((units.shape[1], width), bf16) for units, _ in fill]
    scratch = []
    for units, rows in fill:
        scratch += [pltpu.VMEM(units.shape, bf16), pltpu.VMEM((rows.shape[0], width), bf16)]
    return args, outs, scratch


def own_grads(count, args, outs, scratch):
    return [
        OwnGrad(args[2 * k], args[2 * k + 1], outs[k], scratch[2 * k], scratch[2 * k + 1])
        for k in range(count)
    ]


def meet(devices):
    barrier = pltpu.get_barrier_semaphore()
    for device in devices:
        pl.semaphore_signal(barrier, inc=1, device_id=device, device_id_type=pl.DeviceIdType.MESH)
    pl.semaphore_wait(barrier, len(devices))


def partners():
    c, t = lax.axis_index("context"), lax.axis_index("tensor")
    flip = lambda x, bit: x + bit * (1 - 2 * lax.rem(x // bit, 2))
    return {
        "core": {"tensor": flip(t, 1)},
        "y": {"tensor": flip(t, 2)},
        "z": {"context": flip(c, 1)},
        "far": {"context": flip(c, 2)},
        "last": {"context": flip(flip(c, 1), 2)},
    }


def wide(x):
    return x.astype(f32)


def ranks():
    t = lax.axis_index("tensor")
    flip = lambda x, bit: x + bit * (1 - 2 * lax.rem(x // bit, 2))
    return (t, flip(t, 1), flip(t, 2), flip(flip(t, 1), 2))


def scatter_rank(wires, to, part, own, got_core, sent, got_y):
    size = part.shape[1] // 2
    halves = [pl.ds(0, size), pl.ds(size, size)]
    rank = ranks()
    from_core = {}
    for block in (1, 0):
        for k, at in enumerate(halves):
            from_core[block, k] = wires.copy(
                part.at[rank[1 + 2 * block], at], got_core.at[block, at], to["core"]
            )
    mine = [wires.here(part.at[rank[2 * block]], own.at[block]) for block in (0, 1)]
    yield
    for one in mine:
        one.wait()
    from_y = []
    for k, at in enumerate(halves):
        from_core[1, k].wait_recv()
        sent[at] = (wide(own[1, at]) + wide(got_core[1, at])).astype(bf16)
        from_y.append(wires.copy(sent.at[at], got_y.at[at], to["y"]))
    yield
    for k in range(2):
        from_core[0, k].wait_recv()
    total = wide(own[0]) + wide(got_core[0])
    for one in from_y:
        one.wait_recv()
    return total + wide(got_y[...])


def scatter_pair(wires, to, part, own, got_core, sent, got_y, got_z, diag_y, diag_z):
    size = part.shape[1] // 2
    low, high = pl.ds(0, size), pl.ds(size, size)
    from_core = {j: wires.copy(part.at[4 + j], got_core.at[j], to["core"]) for j in (3, 1, 2, 0)}
    mine = wires.here(part.at[pl.ds(0, 4)], own)
    yield
    mine.wait()
    both = lambda j, at: wide(own[j, at]) + wide(got_core[j, at])
    from_core[3].wait_recv()
    sent[2] = (wide(own[3]) + wide(got_core[3])).astype(bf16)
    via_z = wires.copy(sent.at[2, low], diag_z, to["z"])
    via_y = wires.copy(sent.at[2, high], diag_y, to["y"])
    from_core[1].wait_recv()
    sent[0, high] = both(1, high).astype(bf16)
    y_high = wires.copy(sent.at[0, high], got_y.at[high], to["y"])
    from_core[2].wait_recv()
    sent[1, low] = both(2, low).astype(bf16)
    z_low = wires.copy(sent.at[1, low], got_z.at[low], to["z"])
    yield
    via_z.wait_recv()
    sent[0, low] = (both(1, low) + wide(diag_z[...])).astype(bf16)
    y_low = wires.copy(sent.at[0, low], got_y.at[low], to["y"])
    via_y.wait_recv()
    sent[1, high] = (both(2, high) + wide(diag_y[...])).astype(bf16)
    z_high = wires.copy(sent.at[1, high], got_z.at[high], to["z"])
    yield
    from_core[0].wait_recv()
    total = wide(own[0]) + wide(got_core[0])
    for one in (y_high, z_low, y_low, z_high):
        one.wait_recv()
    return total + wide(got_y[...]) + wide(got_z[...])


def result_of(steps):
    while True:
        try:
            next(steps)
        except StopIteration as done:
            return done.value


def gather_rank(wires, to, block, out):
    size = block.shape[0] // 2
    halves = [pl.ds(0, size), pl.ds(size, size)]
    rank = ranks()
    mine = wires.here(block, out.at[rank[0]])
    from_y = [wires.copy(block.at[h], out.at[rank[0], h], to["y"]) for h in halves]
    from_core = [wires.copy(block, out.at[rank[0]], to["core"])]
    yield
    for h, one in zip(halves, from_y):
        one.wait_recv()
        from_core.append(wires.copy(out.at[rank[2], h], out.at[rank[2], h], to["core"]))
    for one in from_core:
        one.wait_recv()
    mine.wait()


def gather_pair(wires, to, block, out, base):
    size = block.shape[0] // 2
    low, high = pl.ds(0, size), pl.ds(size, size)
    at = lambda j: out.at[base + j]
    from_z = wires.copy(block, at(2), to["z"])
    yield
    from_y = wires.copy(block, at(1), to["y"])
    from_core = [wires.copy(block, at(4), to["core"])]
    yield
    from_y.wait_recv()
    via_z = wires.copy(out.at[base + 1, low], out.at[base + 3, low], to["z"])
    from_core.append(wires.copy(at(1), at(5), to["core"]))
    from_z.wait_recv()
    via_y = wires.copy(out.at[base + 2, high], out.at[base + 3, high], to["y"])
    from_core.append(wires.copy(at(2), at(6), to["core"]))
    yield
    via_z.wait_recv()
    via_y.wait_recv()
    from_core.append(wires.copy(at(3), at(7), to["core"]))
    return from_core


def remote_call(kernel, name, key, args, outs, scratch, copies, in_vmem):
    ins, out_in = in_vmem
    spec = lambda inside: pl.BlockSpec(memory_space=pltpu.VMEM if inside else pl.ANY)
    return pl.pallas_call(
        kernel,
        name=name,
        out_shape=outs,
        in_specs=[spec(x) for x in ins],
        out_specs=[spec(x) for x in out_in],
        scratch_shapes=list(scratch)
        + [
            pltpu.SemaphoreType.DMA((copies,)),
            pltpu.SemaphoreType.DMA((copies,)),
            pltpu.SemaphoreType.DMA((10,)),
        ],
        compiler_params=pltpu.CompilerParams(
            collective_id=key, has_side_effects=True, vmem_limit_bytes=VMEM_LIMIT
        ),
    )(*args)


def kv_gather_kernel(own_ref, out_ref, *sems):
    wires, to = Wires(*sems), partners()
    kind = lax.rem(lax.axis_index("tensor"), 2)
    rows = own_ref.shape[0]
    block = lambda j: out_ref.at[kind, pl.ds(j * rows, rows)]
    meet([to[k] for k in ("core", "z", "far", "last")])
    mine = wires.here(own_ref, block(0))
    arrive = [wires.copy(own_ref, block(j), to[k]) for j, k in ((3, "last"), (2, "far"), (1, "z"))]
    from_core = [wires.copy(own_ref, block(0), to["core"])]
    for j, one in ((1, arrive[2]), (2, arrive[1]), (3, arrive[0])):
        one.wait_recv()
        from_core.append(wires.copy(block(j), block(j), to["core"]))
    for one in from_core:
        one.wait_recv()
    mine.wait()
    wires.finish()


def kv_gather(own):
    rows, width = own.shape
    n_c = lax.axis_size("context")
    return remote_call(
        kv_gather_kernel,
        "kv_gather",
        0,
        [own],
        [jax.ShapeDtypeStruct((2, n_c * rows, width), bf16)],
        [],
        8,
        ([False], [False]),
    )[0]


def kv_scatter_kernel(count, part_ref, *refs):
    args, dkv_ref, outs = refs[: 2 * count], refs[2 * count], refs[2 * count + 1 : 3 * count + 1]
    own, got_core, sent, got = refs[3 * count + 1 : 3 * count + 5]
    wires, to = Wires(*refs[-3:]), partners()
    fill = own_grads(count, args, outs, refs[3 * count + 5 : -3])
    kind = lax.rem(lax.axis_index("tensor"), 2)
    rows = dkv_ref.shape[0]
    block = lambda j: pl.ds(j * rows, rows)
    meet([to[k] for k in ("core", "z", "far", "last")])
    steps = ((3, "last"), (2, "far"), (1, "z"), (0, None))
    from_core = {
        j: wires.copy(part_ref.at[1 - kind, block(j)], got_core.at[block(j)], to["core"])
        for j, _ in steps
    }
    mine = wires.here(part_ref.at[kind], own)
    for one in fill:
        one.fetch(wires)
    mine.wait()
    arrive = []
    for j, k in steps[:3]:
        from_core[j].wait_recv()
        sent[block(j)] = (wide(own[block(j)]) + wide(got_core[block(j)])).astype(bf16)
        arrive.append(wires.copy(sent.at[block(j)], got.at[block(j)], to[k]))
    for one in fill:
        one.make(0, one.tiles)
    from_core[0].wait_recv()
    total = wide(own[block(0)]) + wide(got_core[block(0)])
    for one in arrive:
        one.wait_recv()
    for j in (1, 2, 3):
        total = total + wide(got[block(j)])
    dkv_ref[...] = total
    wires.finish()


def kv_scatter(part, fill, width):
    _, rows, depth = part.shape
    n_c = lax.axis_size("context")
    args, outs, scratch = own_grad_call(fill, width)
    return remote_call(
        functools.partial(kv_scatter_kernel, len(fill)),
        "kv_scatter",
        1,
        [part, *args],
        [jax.ShapeDtypeStruct((rows // n_c, depth), f32), *outs],
        [pltpu.VMEM((rows, depth), bf16)] * 4 + scratch,
        7,
        ([False] * (1 + len(args)), [True] * (1 + len(outs))),
    )


def middle_kernel(
    part,
    x_ref,
    gain_ref,
    dy_ref,
    dy_y,
    dy_z,
    dy_far,
    mid_ref,
    factor_ref,
    out,
    dys,
    own,
    core,
    sent,
    got,
    xn,
    *sems,
):
    wires, to = Wires(*sems), partners()
    blocks = out.shape[0] // 2
    size = xn.shape[0] // 2
    low, high = pl.ds(0, size), pl.ds(size, size)
    meet([to[k] for k in ("core", "y", "z", "far")])
    summed = scatter_rank(wires, to, part, own, core, sent, got)
    next(summed)
    mine = [
        wires.here(block, dys.at[k])
        for block, k in ((dy_ref, 0), (dy_y, 1), (dy_z, 2), (dy_far, blocks))
    ]
    via_z = wires.copy(dy_y.at[low], dys.at[3, low], to["z"])
    dy_last = gather_pair(wires, to, dy_far, dys, blocks)
    next(dy_last)
    next(summed)
    via_y = wires.copy(dy_z.at[high], dys.at[3, high], to["y"])
    ends = [
        wires.copy(block, dys.at[4 + k], to["core"])
        for k, block in enumerate((dy_ref, dy_y, dy_z))
    ]
    next(dy_last)
    middle = wide(x_ref[...]) + result_of(summed)
    mid_ref[...] = middle
    factor = lax.rsqrt(jnp.mean(middle * middle, axis=-1, keepdims=True) + EPSILON)
    factor_ref[...] = factor
    xn[...] = (middle * factor * gain_ref[...]).astype(bf16)
    mine.append(wires.here(xn, out.at[0]))
    xn_far = wires.copy(xn, out.at[blocks], to["far"])
    xn_near = gather_pair(wires, to, xn, out, 0)
    next(xn_near)
    next(xn_near)
    via_z.wait_recv()
    via_y.wait_recv()
    ends.append(wires.copy(dys.at[3], dys.at[7], to["core"]))
    next(dy_last)
    next(xn_near)
    xn_far.wait_recv()
    xn_last = gather_pair(wires, to, out.at[blocks], out, blocks)
    next(xn_last)
    next(xn_last)
    ends += result_of(dy_last) + result_of(xn_near)
    next(xn_last)
    ends += result_of(xn_last)
    for one in ends:
        one.wait_recv()
    for one in mine:
        one.wait()
    wires.finish()


def middle_norm(part, inputs_part, gain, dy_blocks):
    rows, width = inputs_part.shape
    return remote_call(
        middle_kernel,
        "middle_norm",
        2,
        [part.reshape(4, rows, width), inputs_part, gain, *dy_blocks],
        [
            jax.ShapeDtypeStruct((rows, width), f32),
            jax.ShapeDtypeStruct((rows, 1), f32),
            jax.ShapeDtypeStruct((16, rows, width), bf16),
            jax.ShapeDtypeStruct((16, rows, width), bf16),
        ],
        [
            pltpu.VMEM((2, rows, width), bf16),
            pltpu.VMEM((2, rows, width), bf16),
            pltpu.VMEM((rows, width), bf16),
            pltpu.VMEM((rows, width), bf16),
            pltpu.VMEM((rows, width), bf16),
        ],
        48,
        ([False] + [True] * 6, [True, True, False, False]),
    )


def norm_back_rows(values, factor, gain, grad_normed):
    gained = gain * grad_normed
    inner = jnp.mean(gained * values, axis=-1, keepdims=True)
    grad_values = factor * gained - values * (factor * factor * factor) * inner
    return grad_values, jnp.sum(grad_normed * values * factor, axis=0, keepdims=True)


def middle_back_kernel(count, part, mid_ref, factor_ref, gain_ref, dy_ref, *refs):
    args, refs = refs[: 2 * count], refs[2 * count :]
    source_ref, refs = (refs[0], refs[1:]) if count else (None, refs)
    (dmid_ref, dgain_ref, out), refs = refs[:3], refs[3:]
    outs, refs = refs[:count], refs[count:]
    (upper_ref, lower_ref, far_ref), refs = (
        (refs[:3], refs[3:]) if count else ((None, None, None), refs)
    )
    low, first, wires, to = refs[0], refs[1:8], Wires(*refs[-3:]), partners()
    fill = own_grads(count, args, outs, refs[8 : 8 + 2 * count])
    meet([to[k] for k in ("core", "y", "z")])
    back = scatter_pair(wires, to, part, *first)
    next(back)
    for one in fill:
        one.fetch(wires)
    if fill:
        got_ref = refs[8 + 2 * count]
        fetched = wires.here(source_ref, got_ref)
    next(back)
    if fill:
        fill[0].make(0, 1)
    next(back)
    if fill:
        fill[0].make(1, fill[0].tiles)
        fetched.wait()
        cut = upper_ref.shape[0]
        upper_ref[...] = (wide(outs[0][:cut]) + wide(got_ref[:cut])).astype(bf16)
        near_half = wires.copy(upper_ref, far_ref, to["z"])
        lower_ref[...] = (wide(outs[0][cut:]) + wide(got_ref[cut:])).astype(bf16)
    grad_normed = result_of(back)
    du, dgain = norm_back_rows(mid_ref[...], factor_ref[...], gain_ref[...], grad_normed)
    dgain_ref[...] = dgain
    dmid = wide(dy_ref[...]) + du
    low[...] = dmid.astype(bf16)
    share = gather_rank(wires, to, low, out)
    next(share)
    dmid_ref[...] = dmid
    for one in fill[1:]:
        one.make(0, one.tiles)
    result_of(share)
    if fill:
        near_half.wait_recv()
    wires.finish()


def pair_scratch(rows, width):
    return [
        pltpu.VMEM((4, rows, width), bf16),
        pltpu.VMEM((4, rows, width), bf16),
        pltpu.VMEM((3, rows, width), bf16),
        pltpu.VMEM((rows, width), bf16),
        pltpu.VMEM((rows, width), bf16),
        pltpu.VMEM((rows // 2, width), bf16),
        pltpu.VMEM((rows // 2, width), bf16),
    ]


def middle_back(part, middle, factor, gain, dy_part, fill, got, shard):
    rows, width = middle.shape
    args, outs, scratch = own_grad_call(fill, shard)
    if fill:
        args = [*args, got]
        scratch = [*scratch, pltpu.VMEM(got.shape, bf16)]
        units = got.shape[0]
        cut = units // 64 * 16
        outs = [*outs, *(jax.ShapeDtypeStruct((n, shard), bf16) for n in (cut, units - cut, cut))]
    return remote_call(
        functools.partial(middle_back_kernel, len(fill)),
        "middle_back",
        3,
        [part.reshape(8, rows, width), middle, factor, gain, dy_part, *args],
        [
            jax.ShapeDtypeStruct((rows, width), f32),
            jax.ShapeDtypeStruct((1, width), f32),
            jax.ShapeDtypeStruct((4, rows, width), bf16),
            *outs,
        ],
        [pltpu.VMEM((rows, width), bf16)] + pair_scratch(rows, width) + scratch,
        16,
        (
            [False] + [True] * 4 + [False] * len(args),
            [True, True, False] + ([True] * (len(outs) - 1) + [False] if fill else []),
        ),
    )


def add_all(wires, ways, value, slots):
    for k, device in enumerate(ways):
        one = wires.copy(value, slots.at[k], device)
        one.wait()
        wires.started = [x for x in wires.started if x is not one]
        value[...] = value[...] + slots[k]


def input_back_kernel(
    part, x_ref, gain_ref, dmid_ref, small_ref, sum_ref, out, *rest
):
    low, own, core, sent, got, slots = rest[:-3]
    wires, to = Wires(*rest[-3:]), partners()
    meet([to[k] for k in ("core", "y")])
    grad_normed = result_of(scatter_rank(wires, to, part, own, core, sent, got))
    values = wide(x_ref[...])
    factor = lax.rsqrt(jnp.mean(values * values, axis=-1, keepdims=True) + EPSILON)
    du, dgain = norm_back_rows(values, factor, gain_ref[...], grad_normed)
    low[...] = (dmid_ref[...] + du).astype(bf16)
    share = gather_rank(wires, to, low, out)
    next(share)
    width = dgain.shape[1]
    sum_ref[:, width:] = small_ref[:, width:]
    sum_ref[:, :width] = dgain
    add_all(wires, [to["core"], to["y"]], sum_ref, slots)
    result_of(share)
    wires.finish()


def input_back(part, inputs_part, gain, grad_middle, small):
    rows, width = inputs_part.shape
    return remote_call(
        input_back_kernel,
        "input_back",
        5,
        [part.reshape(4, rows, width), inputs_part, gain, grad_middle, small],
        [
            jax.ShapeDtypeStruct(small.shape, f32),
            jax.ShapeDtypeStruct((4, rows, width), bf16),
        ],
        [
            pltpu.VMEM((rows, width), bf16),
            pltpu.VMEM((2, rows, width), bf16),
            pltpu.VMEM((2, rows, width), bf16),
            pltpu.VMEM((rows, width), bf16),
            pltpu.VMEM((rows, width), bf16),
            pltpu.VMEM((2,) + small.shape, f32),
        ],
        16,
        ([False, True, True, True, True], [True, False]),
    )


def context_sum_kernel(over_f, *refs):
    parts, small_ref, out_part, mid_ref = refs[:3], refs[3], refs[4], refs[5]
    outs, sum_ref, shared, outputs = refs[6:8], refs[8], refs[9], refs[10]
    lows, from_end, from_middle = refs[11:15], refs[15:19], refs[19:23]
    out_low, slot, scratch = refs[23], refs[24], refs[25:32]
    wires, to, c = Wires(*refs[32:]), partners(), lax.axis_index("context")
    end = (c == 0) | (c == lax.axis_size("context") - 1)
    inner = jnp.logical_not(end)
    greet = ["core", "y", "z", "last"]
    if over_f:
        to["f"] = {"fsdp": 1 - lax.axis_index("fsdp")}
        greet.append("f")
    meet([to[k] for k in greet])
    ahead = scatter_pair(wires, to, out_part, *scratch)
    next(ahead)
    sum_ref[...] = small_ref[...]
    from_f = wires.copy(small_ref, slot, to["f"]) if over_f else None
    sources = [*parts, sum_ref]
    chunks = []
    for i, cuts in ((2, 1), (0, 2), (1, 4), (3, 1)):
        size = sources[i].shape[0] // cuts
        chunks += [(i, pl.ds(k * size, size)) for k in range(cuts)]
    inward = [wires.plan(sources[i].at[at], from_end[i].at[at], to["z"]) for i, at in chunks]
    across = [wires.plan(lows[i].at[at], from_middle[i].at[at], to["last"]) for i, at in chunks]
    outward = [wires.plan(lows[i].at[at], lows[i].at[at], to["z"]) for i, at in chunks]
    small = len(chunks) - 1

    def send_in(k):
        @pl.when(end)
        def _():
            inward[k].start()

    def pass_on(first, past):
        @pl.when(inner)
        def _():
            for k in range(first, past):
                i, at = chunks[k]
                inward[k].wait_recv()
                total = wide(sources[i][at]) + wide(from_end[i][at])
                lows[i][at] = total.astype(lows[i].dtype)
                across[k].start()
                if k:
                    send_out(k - 1)

    def send_out(k):
        i, at = chunks[k]
        across[k].wait()
        lows[i][at] = (wide(lows[i][at]) + wide(from_middle[i][at])).astype(lows[i].dtype)
        outward[k].start()

    early, late = 3, 5
    for k in range(early):
        send_in(k)
    next(ahead)
    for k in range(early, late):
        send_in(k)
    pass_on(0, early)
    next(ahead)
    if over_f:
        from_f.wait_recv()
        sum_ref[...] = sum_ref[...] + slot[...]
    for k in range(late, small + 1):
        send_in(k)
    pass_on(early, late)
    out_low[...] = (mid_ref[...] + result_of(ahead)).astype(bf16)
    out_share = gather_rank(wires, to, out_low, outputs)
    next(out_share)
    pass_on(late, small + 1)

    @pl.when(inner)
    def _():
        send_out(small)

    result_of(out_share)

    def arrived(k):
        @pl.when(end)
        def _():
            outward[k].wait_recv()

    arrived(0)
    share = gather_rank(wires, to, lows[2], shared)
    next(share)
    for k in range(1, len(chunks)):
        arrived(k)

    @pl.when(end)
    def _():
        for one in inward:
            one.wait_send()

    for i in (0, 1):
        outs[i][...] = wide(lows[i][...])
    sum_ref[...] = lows[3][...]
    result_of(share)

    @pl.when(inner)
    def _():
        for one in outward:
            one.wait_send()

    wires.finish()


def context_sum(over_f, parts, small, out_part, middle):
    rows, width = middle.shape
    lines = [pltpu.VMEM(x.shape, x.dtype) for x in (*parts, small)]
    return remote_call(
        functools.partial(context_sum_kernel, over_f),
        "context_sum",
        6,
        [*parts, small, out_part.reshape(8, rows, width), middle],
        [jax.ShapeDtypeStruct(x.shape, f32) for x in parts[:2]]
        + [jax.ShapeDtypeStruct(small.shape, f32)]
        + [jax.ShapeDtypeStruct((4,) + parts[2].shape, bf16)]
        + [jax.ShapeDtypeStruct((4, rows, width), bf16)],
        lines * 3
        + [pltpu.VMEM((rows, width), bf16), pltpu.VMEM(small.shape, f32)]
        + pair_scratch(rows, width),
        48,
        ([True] * 4 + [False, True], [True] * 3 + [False] * 2),
    )


def build(n_f, n_c, n_t):
    def flip(x, axis, bit):
        size = {"fsdp": n_f, "context": n_c, "tensor": n_t}[axis]
        return lax.ppermute(x, axis, [(i, i ^ bit) for i in range(size)])

    def by_bit(bit, x, other, axis):
        return jnp.where(
            bit == 0,
            jnp.concatenate([x, other], axis=axis),
            jnp.concatenate([other, x], axis=axis),
        )

    def after(x, *others):
        return lax.optimization_barrier((x, others))[0]

    def local(
        inputs,
        cotangent,
        blocks,
        attn_gain,
        w_query,
        b_query,
        w_key,
        b_key,
        w_value,
        b_value,
        w_out,
        ffn_gain,
        w_gate,
        w_up,
        w_down,
    ):
        rows, width = inputs.shape
        f = lax.axis_index("fsdp")
        c = lax.axis_index("context")
        t = lax.axis_index("tensor")
        core, parity, pair = t % 2, c % 2, c // 2
        heads = w_query.shape[1] // HD
        group = (t * heads) // (H // KV)
        part = rows // n_t
        units_all = w_gate.shape[1]
        units = units_all // 2

        def gather_f(x, axis):
            if n_f == 2:
                return by_bit(f, x, flip(x, "fsdp", 1), axis)
            return lax.all_gather(x, "fsdp", axis=axis, tiled=True)

        def grad_far(left, right, side):
            if n_f > 2:
                return None
            source = (left, right)[side]
            half = width // 2
            far = lax.dynamic_slice_in_dim(source, (1 - f) * half, half, 1)
            return (dot_rows(far, right) if side == 0 else dot_rows(left, far)).astype(bf16)

        def grad_sum(left, right, side, far, late):
            if n_f > 2:
                return lax.psum_scatter(
                    dot_rows(left, right).astype(bf16), "fsdp", scatter_dimension=side, tiled=True
                )
            source = (left, right)[side]
            half = width // 2
            own = lax.dynamic_slice_in_dim(source, f * half, half, 1)
            own = dot_rows(own, right) if side == 0 else dot_rows(left, own)
            return (own + after(flip(far, "fsdp", 1), late).astype(f32)).astype(bf16)

        small = jnp.concatenate(
            [v.reshape(1, -1) for v in (attn_gain, ffn_gain, b_query, b_key, b_value)], axis=1
        )
        column = lambda w: lax.dynamic_slice_in_dim(w, group * HD, HD, 1)
        w_kv_own = jnp.where(core == 0, column(w_key), column(w_value))
        pieces_f = lambda x, axis: (
            [x, flip(x, "fsdp", 1)]
            if n_f == 2
            else [lax.all_gather(x, "fsdp", axis=axis, tiled=True)]
        )
        meta = jnp.stack([f, 1 - f, core, pair]).astype(jnp.int32)
        w_q = pieces_f(w_query, 0)
        w_kv = pieces_f(w_kv_own, 0)
        small = gather_f(small, 0)
        w_out_all = gather_f(after(w_out, small, w_q, w_kv), 1)
        piece = attn_gain.shape[0]
        gain_first = small[:, :piece].reshape(1, width).astype(f32)
        gain_second = small[:, piece : 2 * piece].reshape(1, width).astype(f32)
        bias_of = lambda lo, n: (
            small[:, lo : lo + n * (HD // n_f)]
            .reshape(n_f, n, HD // n_f)
            .transpose(1, 0, 2)
            .reshape(n, HD)
            .astype(f32)
        )
        at = 2 * piece
        bq = bias_of(at, heads)
        bk = bias_of(at + heads * (HD // n_f), KV)
        bv = bias_of(at + (heads + KV) * (HD // n_f), KV)
        b_kv = lax.dynamic_index_in_dim(jnp.where(core == 0, bk, bv), group, 0)

        unit_slice = lambda w: lax.dynamic_slice_in_dim(w, parity * units, units, 0)
        own_gate_up = jnp.concatenate(
            [unit_slice(after(w, w_kv_own)) for w in (w_gate.T, w_up.T)], axis=0
        )
        own_down = unit_slice(w_down)

        dy_part = lax.dynamic_slice_in_dim(cotangent, t * part, part, 0)

        seq_blocks = blocks[0].reshape(n_c, -1)
        own_blocks = seq_blocks.shape[1]
        key_blocks = jnp.concatenate(
            [lax.dynamic_index_in_dim(seq_blocks, c ^ j, 0, keepdims=False) for j in range(n_c)]
        )
        positions = (
            key_blocks[:own_blocks, None] * BLOCK + jnp.arange(BLOCK, dtype=jnp.int32)[None, :]
        ).reshape(-1)
        cosine, sine = rope_tables(positions)
        bias = jnp.concatenate([bq.reshape(1, -1), b_kv], axis=1)
        dy_blocks = [
            dy_part,
            flip(dy_part, "tensor", 2),
            flip(dy_part, "context", 1),
            flip(dy_part, "context", 2),
        ]
        inputs_part = lax.dynamic_slice_in_dim(inputs, t * part, part, 0)
        bias = after(bias, dy_blocks[2:], own_gate_up, own_down, inputs_part)
        normed, queries, kv_own = qkv(
            meta, inputs, gain_first, bias, cosine, sine, w_q, w_kv
        )
        kv = after(kv_gather(kv_own), w_out_all)
        far_gate_up = pieces_f(after(own_gate_up, kv), 1)[-1]
        w_gate_up = [own_gate_up, far_gate_up] if n_f == 2 else [far_gate_up]
        far_down = pieces_f(after(own_down, kv), 1)[-1]
        w_downs = [own_down, far_down] if n_f == 2 else [far_down]
        attended, lse = attention(key_blocks, queries, kv)
        middle, factor_second, normed2, dy_all = middle_norm(
            dot(attended, w_out_all).astype(bf16), inputs_part, gain_second, dy_blocks
        )

        hidden, slope, gated, *down_far = hidden_units(meta, normed2, dy_all, w_gate_up)
        grad_gate, grad_up, dx_part, out_part, *unit_far = hidden_back(
            meta, normed2, dy_all, hidden, slope, gated, w_gate_up, w_downs
        )
        unit_far = [*down_far, *unit_far]
        flat = lambda x: x.reshape(-1, width)
        if n_f == 2:
            down_got, gate_got, up_got = (flip(x, "fsdp", 1) for x in unit_far)
            early = [(hidden, flat(dy_all)), (grad_gate, flat(normed2))]
            later = [(grad_up, flat(normed2))]
        else:
            over_f = lambda x: lax.psum_scatter(x, "fsdp", scatter_dimension=1, tiled=True)
            owns = [
                over_f(unit_grads(meta, 0, 1, x, [unit]))
                for x, unit in ((dy_all, hidden), (normed2, grad_gate), (normed2, grad_up))
            ]
            down_got = gate_got = up_got = jnp.zeros_like(owns[0])
            early = later = []

        def unit_whole(own, other):
            own, other = (jnp.concatenate(x, axis=0) for x in (own, other))
            return by_bit(parity, own, other, 0).astype(f32)

        grad_middle, ffn_gain_grad, grad_middle_low, *first_owns = middle_back(
            dx_part, middle, factor_second, gain_second, dy_part, early, down_got, width // n_f
        )
        grad_middle_low = grad_middle_low.reshape(rows, width)
        add = lambda own, got: (own.astype(f32) + got.astype(f32)).astype(bf16)
        upper = units // 2
        if n_f == 2:
            _, gate_own, down_upper, down_lower, far_upper = first_owns
        else:
            down_low, gate_own = owns[:2]
            down_upper, down_lower = down_low[:upper], down_low[upper:]
            far_upper = flip(down_upper, "context", 1)
        gate_got = after(gate_got, grad_middle_low)
        gate_low = add(gate_own, gate_got)
        far_lower = flip(down_lower, "context", 1)
        grad_middle_low = after(grad_middle_low, gate_low)
        grad_attended = dot_cols(grad_middle_low, w_out_all).astype(bf16)

        dq_low, dkv = attention_back(key_blocks, queries, grad_attended, lse, cosine, sine, kv)
        attention_args = [(attended, after(grad_middle_low, dq_low), 1), (normed, dq_low, 0)]
        fars = [grad_far(*args) for args in attention_args]
        dkv, *last_owns = kv_scatter(
            after(dkv, fars), later, width // n_f
        )
        (up_own,) = last_owns or owns[2:]
        far_gate = flip(after(gate_low, dkv, far_lower), "context", 1)
        dkv = after(dkv, far_lower)
        dkv_low = jnp.where(core == 0, rotate_back(dkv, cosine, sine), dkv).astype(bf16)
        own_biases = jnp.sum(
            jnp.concatenate([dq_low, dkv_low], axis=1).astype(f32), axis=0, keepdims=True
        )
        slots = lax.dynamic_update_slice(
            jnp.zeros((n_t, (heads + 1) * HD), f32), own_biases, (t, 0)
        )
        small_grads = jnp.concatenate(
            [jnp.zeros((1, width), f32), ffn_gain_grad, slots.reshape(1, -1)], axis=1
        )
        grad_qkv = qkv_back(meta, dq_low, dkv_low, w_q, w_kv)
        up_low = add(up_own, after(up_got, grad_qkv))
        attention_args.append((after(normed, grad_qkv), dkv_low, 0))
        fars.append(grad_far(*attention_args[-1]))
        far_up = flip(up_low, "context", 1)
        small_grads, input_grad = input_back(
            after(grad_qkv, up_low, fars),
            inputs_part,
            gain_first,
            grad_middle,
            small_grads,
        )
        input_grad = input_grad.reshape(rows, width)
        if n_f > 2:
            small_grads = lax.psum(small_grads, "fsdp")
        zero = jnp.minimum(t, 0).astype(bf16)
        input_grad = input_grad + zero
        small_grads = after(small_grads, far_gate)
        attention_parts = [
            grad_sum(*args, far, small_grads) for args, far in zip(attention_args, fars)
        ]
        wd_grad = unit_whole(
            *after(((down_upper, down_lower), (far_upper, far_lower)), small_grads)
        )
        wg_grad = unit_whole(*after(((gate_low,), (far_gate,)), small_grads))
        small_grads, wd_grad, wg_grad, input_grad = lax.optimization_barrier(
            (small_grads, wd_grad, wg_grad, input_grad)
        )
        wo_grad, wq_grad, packed, wkv_all, outputs = context_sum(
            n_f == 2, attention_parts, small_grads, out_part, middle
        )
        wo_grad, wq_grad, packed, wkv_all, outputs, far_up = lax.optimization_barrier(
            (wo_grad, wq_grad, packed, wkv_all, outputs, far_up)
        )
        outputs = outputs.reshape(rows, width)
        wk_grad = jnp.concatenate([wkv_all[0], wkv_all[2]], axis=1).astype(f32)
        wv_grad = jnp.concatenate([wkv_all[1], wkv_all[3]], axis=1).astype(f32)
        packed = packed[0]
        attn_gain_grad = lax.dynamic_slice_in_dim(packed, f * piece, piece, 0)
        ffn_gain_grad = lax.dynamic_slice_in_dim(packed, width + f * piece, piece, 0)
        slots = packed[2 * width :].reshape(n_t, heads + 1, HD)
        slots = lax.dynamic_slice_in_dim(slots, f * (HD // n_f), HD // n_f, 2)
        bq_out = lax.dynamic_index_in_dim(slots, t, 0, keepdims=False)[:heads]
        bk_out = slots[0::2, heads]
        bv_out = slots[1::2, heads]

        wu_grad = unit_whole((up_low,), (far_up,))
        wg_grad, wu_grad = wg_grad.T, wu_grad.T

        return (
            outputs,
            input_grad,
            attn_gain_grad,
            wq_grad,
            bq_out,
            wk_grad,
            bk_out,
            wv_grad,
            bv_out,
            wo_grad,
            ffn_gain_grad,
            wg_grad,
            wu_grad,
            wd_grad,
        )

    return local


def solution(mesh):
    in_specs = (
        P(("fsdp", "context"), None),
        P(("fsdp", "context"), None),
        P("fsdp", None),
        P("fsdp"),
        P("fsdp", "tensor"),
        P("tensor", "fsdp"),
        P("fsdp", None),
        P(None, "fsdp"),
        P("fsdp", None),
        P(None, "fsdp"),
        P("tensor", "fsdp"),
        P("fsdp"),
        P("fsdp", "tensor"),
        P("fsdp", "tensor"),
        P("tensor", "fsdp"),
    )
    out_specs = (
        P(("fsdp", "context"), None),
        P(("fsdp", "context"), None),
        P("fsdp"),
        P("fsdp", "tensor"),
        P("tensor", "fsdp"),
        P("fsdp", None),
        P(None, "fsdp"),
        P("fsdp", None),
        P(None, "fsdp"),
        P("tensor", "fsdp"),
        P("fsdp"),
        P("fsdp", "tensor"),
        P("fsdp", "tensor"),
        P("tensor", "fsdp"),
    )
    local = build(mesh.shape["fsdp"], mesh.shape["context"], mesh.shape["tensor"])
    return jax.shard_map(local, mesh=mesh, in_specs=in_specs, out_specs=out_specs, check_vma=False)
```

```python
import functools

import jax
import jax.numpy as jnp
from jax import lax
from jax.experimental import pallas as pl
from jax.experimental.pallas import tpu as pltpu
from jax.sharding import PartitionSpec as P

H = 12
KV = 2
HD = 128
BLOCK = 256

EPSILON = 1e-06
ROPE_BASE = 1000000.0
MASKED = -1e30
SCALING = HD ** (-0.5)
LANES = 128
VMEM_LIMIT = 60 << 20

f32 = jnp.float32
bf16 = jnp.bfloat16


def rope_tables(positions):
    halfway = HD // 2
    frequency = ROPE_BASE ** (-(jnp.arange(halfway, dtype=f32) * 2.0 / HD))
    angles = positions.astype(f32)[:, None] * frequency[None, :]
    cosine, sine = jnp.cos(angles), jnp.sin(angles)
    return (jnp.concatenate([cosine, cosine], axis=1), jnp.concatenate([sine, sine], axis=1))


def rotate(field, cosine, sine):
    halfway = HD // 2
    turned = jnp.concatenate([-field[..., halfway:], field[..., :halfway]], axis=-1)
    return field * cosine + turned * sine


def rotate_back(grad_field, cosine, sine):
    halfway = HD // 2
    moved = grad_field * sine
    turned = jnp.concatenate([moved[..., halfway:], -moved[..., :halfway]], axis=-1)
    return grad_field * cosine + turned


def dot(left, right):
    return jnp.dot(left, right, preferred_element_type=f32)


def dot_rows(left, right):
    return lax.dot_general(left, right, (((0,), (0,)), ((), ())), preferred_element_type=f32)


def dot_cols(left, right):
    return lax.dot_general(left, right, (((1,), (1,)), ((), ())), preferred_element_type=f32)


def mask_row(kb_ref, own_block, key_blocks):
    return jnp.concatenate(
        [
            jnp.full((1, BLOCK), jnp.where(kb_ref[j] <= own_block, 0.0, MASKED), f32)
            for j in range(key_blocks)
        ],
        axis=1,
    )


def attention_kernel(key_blocks, kb_ref, q_ref, k_ref, v_ref, o_ref, lse_ref):
    bias = mask_row(kb_ref, kb_ref[pl.program_id(1)], key_blocks)
    scores = dot_cols(q_ref[...], k_ref[...]) * SCALING + bias
    row_max = jnp.max(scores, axis=1, keepdims=True)
    expo = jnp.exp(scores - row_max)
    total = jnp.sum(expo, axis=1, keepdims=True)
    probability = (expo * (1.0 / total)).astype(bf16)
    o_ref[...] = dot(probability, v_ref[...]).astype(bf16)
    lse_ref[0] = row_max + jnp.log(total)


def attention(key_blocks, queries, kv):
    rows, width = queries.shape
    heads = width // HD
    whole = lambda kind: pl.BlockSpec((None,) + kv.shape[1:], lambda h, i, kb: (kind, 0, 0))
    tile = pl.BlockSpec((BLOCK, HD), lambda h, i, kb: (i, h))
    return pl.pallas_call(
        functools.partial(attention_kernel, kv.shape[1] // BLOCK),
        name="attention",
        grid_spec=pltpu.PrefetchScalarGridSpec(
            num_scalar_prefetch=1,
            grid=(heads, rows // BLOCK),
            in_specs=[tile, whole(0), whole(1)],
            out_specs=[tile, pl.BlockSpec((1, BLOCK, 1), lambda h, i, kb: (h, i, 0))],
        ),
        out_shape=[
            jax.ShapeDtypeStruct((rows, width), bf16),
            jax.ShapeDtypeStruct((heads, rows, 1), f32),
        ],
        compiler_params=pltpu.CompilerParams(vmem_limit_bytes=VMEM_LIMIT),
    )(key_blocks, queries, kv, kv)


def attention_back_kernel(
    key_blocks,
    kb_ref,
    q_ref,
    do_ref,
    lse_ref,
    cos_ref,
    sin_ref,
    k_ref,
    v_ref,
    dq_ref,
    dkv_ref,
    dk_ref,
    dv_ref,
):
    head, i = pl.program_id(0), pl.program_id(1)

    @pl.when((head == 0) & (i == 0))
    def _():
        dk_ref[...] = jnp.zeros_like(dk_ref)
        dv_ref[...] = jnp.zeros_like(dv_ref)

    bias = mask_row(kb_ref, kb_ref[i], key_blocks)
    scores = dot_cols(q_ref[...], k_ref[...]) * SCALING + bias
    probability = jnp.exp(scores - lse_ref[0])
    grad_probs = dot_cols(do_ref[...], v_ref[...])
    inner = jnp.sum(probability * grad_probs, axis=1, keepdims=True)
    grad_scores = (probability * (grad_probs - inner)).astype(bf16)
    grad_query = dot(grad_scores, k_ref[...]) * SCALING
    moved = grad_query * sin_ref[...]
    sign = jnp.where(lax.broadcasted_iota(jnp.int32, moved.shape, 1) < HD // 2, 1.0, -1.0)
    dq_ref[...] = (
        grad_query * cos_ref[...] + pltpu.roll(moved, HD // 2, 1) * sign
    ).astype(bf16)
    dk_ref[...] += dot_rows(grad_scores, q_ref[...]) * SCALING
    dv_ref[...] += dot_rows(probability.astype(bf16), do_ref[...])

    @pl.when((head == pl.num_programs(0) - 1) & (i == pl.num_programs(1) - 1))
    def _():
        dkv_ref[0] = dk_ref[...].astype(bf16)
        dkv_ref[1] = dv_ref[...].astype(bf16)


def attention_back(key_blocks, queries, grad_out, lse, cosine, sine, kv):
    rows, width = queries.shape
    heads = width // HD
    whole = lambda kind: pl.BlockSpec((None,) + kv.shape[1:], lambda h, i, kb: (kind, 0, 0))
    tile = pl.BlockSpec((BLOCK, HD), lambda h, i, kb: (i, h))
    table = pl.BlockSpec((BLOCK, HD), lambda h, i, kb: (i, 0))
    return pl.pallas_call(
        functools.partial(attention_back_kernel, kv.shape[1] // BLOCK),
        name="attention_back",
        grid_spec=pltpu.PrefetchScalarGridSpec(
            num_scalar_prefetch=1,
            grid=(heads, rows // BLOCK),
            in_specs=[
                tile,
                tile,
                pl.BlockSpec((1, BLOCK, 1), lambda h, i, kb: (h, i, 0)),
                table,
                table,
                whole(0),
                whole(1),
            ],
            out_specs=[tile, pl.BlockSpec(kv.shape, lambda h, i, kb: (0, 0, 0))],
            scratch_shapes=[pltpu.VMEM(kv.shape[1:], f32)] * 2,
        ),
        out_shape=[
            jax.ShapeDtypeStruct((rows, width), bf16),
            jax.ShapeDtypeStruct(kv.shape, bf16),
        ],
        compiler_params=pltpu.CompilerParams(vmem_limit_bytes=VMEM_LIMIT),
    )(key_blocks, queries, grad_out, lse, cosine, sine, kv, kv)


def qkv_kernel(pieces, meta_ref, x_ref, gain_ref, bias_ref, cos_ref, sin_ref, *refs):
    weights, (xn_ref, q_ref, kv_ref) = refs[: 2 * pieces], refs[2 * pieces :]
    values = x_ref[...].astype(f32)
    factor = lax.rsqrt(jnp.mean(values * values, axis=-1, keepdims=True) + EPSILON)
    xn_ref[...] = (values * factor * gain_ref[...]).astype(bf16)
    depth = weights[0].shape[0]
    normed = [xn_ref[:, columns_of(meta_ref, j, depth, pieces)] for j in range(pieces)]
    cosine, sine = cos_ref[...], sin_ref[...]
    sign = jnp.where(lax.broadcasted_iota(jnp.int32, cosine.shape, 1) < HD // 2, -1.0, 1.0)
    sine = sine * sign
    width = q_ref.shape[1]
    total = bias_ref[:, :width] + sum(dot(x, w[...]) for x, w in zip(normed, weights[:pieces]))
    turn = lambda own: own * cosine + pltpu.roll(own, HD // 2, 1) * sine
    for h in range(width // HD):
        q_ref[:, h * HD : (h + 1) * HD] = turn(total[:, h * HD : (h + 1) * HD]).astype(bf16)
    own = bias_ref[:, width:] + sum(dot(x, w[...]) for x, w in zip(normed, weights[pieces:]))
    kv_ref[...] = jnp.where(meta_ref[2] == 0, turn(own), own).astype(bf16)


def columns_of(meta_ref, j, depth, pieces):
    if pieces == 1:
        return slice(None)
    return pl.ds(pl.multiple_of(meta_ref[j] * depth, LANES), depth)


def qkv(meta, inputs, gain, bias, cosine, sine, w_q, w_kv):
    rows, width = inputs.shape
    out = w_q[0].shape[1]
    tile = 256
    row = lambda n: pl.BlockSpec((tile, n), lambda i, m: (i, 0))
    fixed = lambda w: pl.BlockSpec(w.shape, lambda i, m: (0, 0))
    return pl.pallas_call(
        functools.partial(qkv_kernel, len(w_q)),
        name="qkv",
        grid_spec=pltpu.PrefetchScalarGridSpec(
            num_scalar_prefetch=1,
            grid=(rows // tile,),
            in_specs=[row(width), fixed(gain), fixed(bias), row(HD), row(HD)]
            + [fixed(w) for w in (*w_q, *w_kv)],
            out_specs=[row(width), row(out), row(HD)],
        ),
        out_shape=[
            jax.ShapeDtypeStruct((rows, width), bf16),
            jax.ShapeDtypeStruct((rows, out), bf16),
            jax.ShapeDtypeStruct((rows, HD), bf16),
        ],
        compiler_params=pltpu.CompilerParams(vmem_limit_bytes=VMEM_LIMIT),
    )(meta, inputs, gain, bias, cosine, sine, *w_q, *w_kv)


def qkv_back_kernel(pieces, meta_ref, dq_ref, dkv_ref, *refs):
    w_q, w_kv, out_ref = refs[:pieces], refs[pieces : 2 * pieces], refs[-1]
    for j in range(pieces):
        out_ref[:, columns_of(meta_ref, j, w_q[j].shape[0], pieces)] = (
            dot_cols(dq_ref[...], w_q[j][...]) + dot_cols(dkv_ref[...], w_kv[j][...])
        ).astype(bf16)


def qkv_back(meta, grad_q, grad_kv, w_q, w_kv):
    rows, width = grad_q.shape[0], sum(w.shape[0] for w in w_q)
    tile = 256
    row = lambda n: pl.BlockSpec((tile, n), lambda i, m: (i, 0))
    fixed = lambda w: pl.BlockSpec(w.shape, lambda i, m: (0, 0))
    return pl.pallas_call(
        functools.partial(qkv_back_kernel, len(w_q)),
        name="qkv_back",
        grid_spec=pltpu.PrefetchScalarGridSpec(
            num_scalar_prefetch=1,
            grid=(rows // tile,),
            in_specs=[row(grad_q.shape[1]), row(HD)] + [fixed(w) for w in (*w_q, *w_kv)],
            out_specs=row(width),
        ),
        out_shape=jax.ShapeDtypeStruct((rows, width), bf16),
        compiler_params=pltpu.CompilerParams(vmem_limit_bytes=VMEM_LIMIT),
    )(meta, grad_q, grad_kv, *w_q, *w_kv)


def add_rows(unit_refs, row_refs, columns, totals, outs):
    step = pl.program_id(0)

    @pl.when(step == 0)
    def _():
        for total in totals:
            total[...] = jnp.zeros_like(total)

    for total, unit, row in zip(totals, unit_refs, row_refs):
        total[...] += dot_rows(unit[...], row[:, columns])

    @pl.when(step == pl.num_programs(0) - 1)
    def _():
        for out, total in zip(outs, totals):
            out[...] = total[...].astype(bf16)


def hidden_kernel(pieces, meta_ref, x_ref, dy_ref, *refs):
    wg, wu, refs = refs[:pieces], refs[pieces : 2 * pieces], refs[2 * pieces :]
    hid_ref, slope_ref, gated_ref = refs[:3]
    columns = [columns_of(meta_ref, j, wg[j].shape[1], pieces) for j in range(pieces)]
    gate = sum(dot_cols(x_ref[:, at], w[...]) for at, w in zip(columns, wg))
    up = sum(dot_cols(x_ref[:, at], w[...]) for at, w in zip(columns, wu))
    sigma = 1.0 / (1.0 + jnp.exp(-gate))
    gated = gate * sigma
    hid_ref[...] = (gated * up).astype(bf16)
    slope_ref[...] = (up * (sigma + gated * (1.0 - sigma))).astype(bf16)
    gated_ref[...] = gated.astype(bf16)
    if pieces == 2:
        add_rows([hid_ref], [dy_ref], columns[1], refs[4:], refs[3:4])


def hidden_back_kernel(pieces, meta_ref, x_ref, dy_ref, hid_ref, slope_ref, gated_ref, *refs):
    wg, wu, wd = (refs[m * pieces : (m + 1) * pieces] for m in range(3))
    refs = refs[3 * pieces :]
    dg_ref, du_ref, dx_ref, out_ref = refs[:4]
    columns = [columns_of(meta_ref, j, wg[j].shape[1], pieces) for j in range(pieces)]
    grad_hidden = sum(dot_cols(dy_ref[:, at], w[...]) for at, w in zip(columns, wd))
    dg_ref[...] = (grad_hidden * slope_ref[...].astype(f32)).astype(bf16)
    du_ref[...] = (grad_hidden * gated_ref[...].astype(f32)).astype(bf16)

    @pl.when(pl.program_id(0) // (pl.num_programs(0) // 2) == meta_ref[3])
    def _():
        for at, g, u, d in zip(columns, wg, wu, wd):
            dx_ref[:, at] = (dot(dg_ref[...], g[...]) + dot(du_ref[...], u[...])).astype(bf16)
            out_ref[:, at] = dot(hid_ref[...], d[...]).astype(bf16)

    if pieces == 2:
        add_rows([dg_ref, du_ref], [x_ref, x_ref], columns[1], refs[6:], refs[4:6])


def hidden_specs(meta, normed, weights):
    width = normed.shape[-1]
    rows = normed.shape[0] * normed.shape[1]
    units, depth = weights[0].shape[0] // 2, weights[0].shape[1]
    tile = 512
    steps = rows // tile
    half = steps // 2
    once = pl.Buffered(1)
    inside = lambda i, m: jnp.clip(i - m[3] * half, 0, half - 1)
    return {
        "steps": steps,
        "flat": lambda x: x.reshape(-1, width),
        "row": pl.BlockSpec((tile, width), lambda i, m: (lax.rem(i + m[3] * half, steps), 0)),
        "unit": pl.BlockSpec((tile, units), lambda i, m: (i, 0)),
        "near_unit": pl.BlockSpec((tile, units), lambda i, m: (inside(i, m) + m[3] * half, 0)),
        "near_row": pl.BlockSpec((tile, width), lambda i, m: (inside(i, m), 0)),
        "weight": lambda k: pl.BlockSpec((units, depth), lambda i, m: (k, 0), pipeline_mode=once),
        "grad": pl.BlockSpec((units, depth), lambda i, m: (0, 0), pipeline_mode=once),
        "unit_shape": jax.ShapeDtypeStruct((rows, units), bf16),
        "near_shape": jax.ShapeDtypeStruct((rows // 2, width), bf16),
        "grad_shape": jax.ShapeDtypeStruct((units, depth), bf16),
        "total": pltpu.VMEM((units, depth), f32),
    }


def hidden_call(kernel, name, meta, args, in_specs, outs, grads, specs):
    return pl.pallas_call(
        kernel,
        name=name,
        grid_spec=pltpu.PrefetchScalarGridSpec(
            num_scalar_prefetch=1,
            grid=(specs["steps"],),
            in_specs=in_specs,
            out_specs=[specs[x] for x in outs] + [specs["grad"]] * grads,
            scratch_shapes=[specs["total"]] * grads,
        ),
        out_shape=[specs[x.split("_")[0] + "_shape"] for x in outs]
        + [specs["grad_shape"]] * grads,
        compiler_params=pltpu.CompilerParams(vmem_limit_bytes=VMEM_LIMIT),
    )(meta, *args)


def hidden_units(meta, normed, grad_out, weights):
    specs, pieces = hidden_specs(meta, normed, weights), len(weights)
    return hidden_call(
        functools.partial(hidden_kernel, pieces),
        "hidden_units",
        meta,
        [specs["flat"](normed), specs["flat"](grad_out)] + list(weights) * 2,
        [specs["row"]] * 2 + [specs["weight"](k) for k in range(2) for _ in weights],
        ["unit"] * 3,
        pieces == 2,
        specs,
    )


def hidden_back(meta, normed, grad_out, hidden, slope, gated, weights, down_weights):
    specs, pieces = hidden_specs(meta, normed, weights), len(weights)
    return hidden_call(
        functools.partial(hidden_back_kernel, pieces),
        "hidden_back",
        meta,
        [specs["flat"](normed), specs["flat"](grad_out), hidden, slope, gated]
        + list(weights) * 2
        + list(down_weights),
        [specs["row"]] * 2
        + [specs["near_unit"], specs["unit"], specs["unit"]]
        + [specs["weight"](k) for k in (0, 1, 0) for _ in weights],
        ["unit", "unit", "near_row", "near_row"],
        2 * (pieces == 2),
        specs,
    )


def unit_grads_kernel(count, meta_ref, near_ref, far_ref, *refs):
    units, out_ref, x_ref = refs[:count], refs[-2], refs[-1]
    half = near_ref.shape[0]
    x_ref[pl.ds(pl.multiple_of(meta_ref[3] * half, half), half)] = near_ref[...]
    x_ref[pl.ds(pl.multiple_of((1 - meta_ref[3]) * half, half), half)] = far_ref[...]
    for k, unit in enumerate(units):
        depth = unit.shape[1]
        out_ref[k * depth : (k + 1) * depth] = dot_rows(unit[...], x_ref[...]).astype(bf16)


def unit_grads(meta, which, pieces, x, units_of):
    width = x.shape[-1]
    count, (rows, units) = len(units_of), units_of[0].shape
    depth = width // pieces
    tile = 256
    steps = depth // tile
    shard = (lambda m: m[which]) if pieces > 1 else (lambda m: 0)
    feature = lambda half: pl.BlockSpec(
        (rows // 2, tile), lambda i, m: (half, shard(m) * steps + i)
    )
    unit = pl.BlockSpec((rows, units), lambda i, m: (0, 0), pipeline_mode=pl.Buffered(1))
    x = x.reshape(-1, width)
    return pl.pallas_call(
        functools.partial(unit_grads_kernel, count),
        name=f"unit_grads_{which}_{count}",
        grid_spec=pltpu.PrefetchScalarGridSpec(
            num_scalar_prefetch=1,
            grid=(steps,),
            in_specs=[feature(0), feature(1)] + [unit] * count,
            out_specs=pl.BlockSpec((count * units, tile), lambda i, m: (0, i)),
            scratch_shapes=[pltpu.VMEM((rows, tile), bf16)],
        ),
        out_shape=jax.ShapeDtypeStruct((count * units, depth), bf16),
        compiler_params=pltpu.CompilerParams(vmem_limit_bytes=VMEM_LIMIT),
    )(meta, x, x, *units_of)


class Wires:
    def __init__(self, sends, receives, locals_):
        self.sends, self.receives, self.locals = sends, receives, locals_
        self.used = self.used_local = 0
        self.started = []

    def plan(self, source, target, device):
        k = self.used
        self.used += 1
        return pltpu.make_async_remote_copy(
            source,
            target,
            self.sends.at[k],
            self.receives.at[k],
            device_id=device,
            device_id_type=pl.DeviceIdType.MESH,
        )

    def copy(self, source, target, device):
        one = self.plan(source, target, device)
        one.start()
        self.started.append(one)
        return one

    def here(self, source, target):
        k = self.used_local
        self.used_local += 1
        one = pltpu.make_async_copy(source, target, self.locals.at[k])
        one.start()
        return one

    def finish(self):
        for one in self.started:
            one.wait_send()


class OwnGrad:
    TILE = 256

    def __init__(self, units, rows, out, units_here, rows_here):
        self.units, self.rows, self.out = units, rows, out
        self.units_here, self.rows_here = units_here, rows_here
        self.tiles = out.shape[1] // self.TILE
        self.copies = None

    def fetch(self, wires):
        half, depth = self.rows.shape[0] // 2, self.out.shape[1]
        column = pl.multiple_of(lax.axis_index("fsdp") * depth, LANES)
        pair = lax.axis_index("context") // 2
        self.copies = [wires.here(self.units, self.units_here)]
        for k, place in ((0, pair), (1, 1 - pair)):
            self.copies.append(
                wires.here(
                    self.rows.at[pl.ds(k * half, half), pl.ds(column, depth)],
                    self.rows_here.at[pl.ds(pl.multiple_of(place * half, half), half)],
                )
            )

    def make(self, first, past):
        for one in self.copies:
            one.wait()
        self.copies = []

        @pl.loop(first, past)
        def _(k):
            at = pl.ds(pl.multiple_of(k * self.TILE, self.TILE), self.TILE)
            self.out[:, at] = dot_rows(self.units_here[...], self.rows_here[:, at]).astype(bf16)


def own_grad_call(fill, width):
    args = [x for pair in fill for x in pair]
    outs = [jax.ShapeDtypeStruct((units.shape[1], width), bf16) for units, _ in fill]
    scratch = []
    for units, rows in fill:
        scratch += [pltpu.VMEM(units.shape, bf16), pltpu.VMEM((rows.shape[0], width), bf16)]
    return args, outs, scratch


def own_grads(count, args, outs, scratch):
    return [
        OwnGrad(args[2 * k], args[2 * k + 1], outs[k], scratch[2 * k], scratch[2 * k + 1])
        for k in range(count)
    ]


def meet(devices):
    barrier = pltpu.get_barrier_semaphore()
    for device in devices:
        pl.semaphore_signal(barrier, inc=1, device_id=device, device_id_type=pl.DeviceIdType.MESH)
    pl.semaphore_wait(barrier, len(devices))


def partners():
    c, t = lax.axis_index("context"), lax.axis_index("tensor")
    flip = lambda x, bit: x + bit * (1 - 2 * lax.rem(x // bit, 2))
    return {
        "core": {"tensor": flip(t, 1)},
        "y": {"tensor": flip(t, 2)},
        "z": {"context": flip(c, 1)},
        "far": {"context": flip(c, 2)},
        "last": {"context": flip(flip(c, 1), 2)},
    }


def wide(x):
    return x.astype(f32)


def ranks():
    t = lax.axis_index("tensor")
    flip = lambda x, bit: x + bit * (1 - 2 * lax.rem(x // bit, 2))
    return (t, flip(t, 1), flip(t, 2), flip(flip(t, 1), 2))


def scatter_rank(wires, to, part, own, got_core, sent, got_y):
    size = part.shape[1] // 2
    halves = [pl.ds(0, size), pl.ds(size, size)]
    rank = ranks()
    from_core = {}
    for block in (1, 0):
        for k, at in enumerate(halves):
            from_core[block, k] = wires.copy(
                part.at[rank[1 + 2 * block], at], got_core.at[block, at], to["core"]
            )
    mine = [wires.here(part.at[rank[2 * block]], own.at[block]) for block in (0, 1)]
    yield
    for one in mine:
        one.wait()
    from_y = []
    for k, at in enumerate(halves):
        from_core[1, k].wait_recv()
        sent[at] = (wide(own[1, at]) + wide(got_core[1, at])).astype(bf16)
        from_y.append(wires.copy(sent.at[at], got_y.at[at], to["y"]))
    yield
    for k in range(2):
        from_core[0, k].wait_recv()
    total = wide(own[0]) + wide(got_core[0])
    for one in from_y:
        one.wait_recv()
    return total + wide(got_y[...])


def scatter_pair(wires, to, part, own, got_core, sent, got_y, got_z, diag_y, diag_z):
    size = part.shape[1] // 2
    low, high = pl.ds(0, size), pl.ds(size, size)
    from_core = {j: wires.copy(part.at[4 + j], got_core.at[j], to["core"]) for j in (3, 1, 2, 0)}
    mine = wires.here(part.at[pl.ds(0, 4)], own)
    yield
    mine.wait()
    both = lambda j, at: wide(own[j, at]) + wide(got_core[j, at])
    from_core[3].wait_recv()
    sent[2] = (wide(own[3]) + wide(got_core[3])).astype(bf16)
    via_z = wires.copy(sent.at[2, low], diag_z, to["z"])
    via_y = wires.copy(sent.at[2, high], diag_y, to["y"])
    from_core[1].wait_recv()
    sent[0, high] = both(1, high).astype(bf16)
    y_high = wires.copy(sent.at[0, high], got_y.at[high], to["y"])
    from_core[2].wait_recv()
    sent[1, low] = both(2, low).astype(bf16)
    z_low = wires.copy(sent.at[1, low], got_z.at[low], to["z"])
    yield
    via_z.wait_recv()
    sent[0, low] = (both(1, low) + wide(diag_z[...])).astype(bf16)
    y_low = wires.copy(sent.at[0, low], got_y.at[low], to["y"])
    via_y.wait_recv()
    sent[1, high] = (both(2, high) + wide(diag_y[...])).astype(bf16)
    z_high = wires.copy(sent.at[1, high], got_z.at[high], to["z"])
    yield
    from_core[0].wait_recv()
    total = wide(own[0]) + wide(got_core[0])
    for one in (y_high, z_low, y_low, z_high):
        one.wait_recv()
    return total + wide(got_y[...]) + wide(got_z[...])


def result_of(steps):
    while True:
        try:
            next(steps)
        except StopIteration as done:
            return done.value


def gather_rank(wires, to, block, out):
    size = block.shape[0] // 2
    halves = [pl.ds(0, size), pl.ds(size, size)]
    rank = ranks()
    mine = wires.here(block, out.at[rank[0]])
    from_y = [wires.copy(block.at[h], out.at[rank[0], h], to["y"]) for h in halves]
    from_core = [wires.copy(block, out.at[rank[0]], to["core"])]
    yield
    for h, one in zip(halves, from_y):
        one.wait_recv()
        from_core.append(wires.copy(out.at[rank[2], h], out.at[rank[2], h], to["core"]))
    for one in from_core:
        one.wait_recv()
    mine.wait()


def gather_pair(wires, to, block, out, base):
    size = block.shape[0] // 2
    low, high = pl.ds(0, size), pl.ds(size, size)
    at = lambda j: out.at[base + j]
    from_z = wires.copy(block, at(2), to["z"])
    yield
    from_y = wires.copy(block, at(1), to["y"])
    from_core = [wires.copy(block, at(4), to["core"])]
    yield
    from_y.wait_recv()
    via_z = wires.copy(out.at[base + 1, low], out.at[base + 3, low], to["z"])
    from_core.append(wires.copy(at(1), at(5), to["core"]))
    from_z.wait_recv()
    via_y = wires.copy(out.at[base + 2, high], out.at[base + 3, high], to["y"])
    from_core.append(wires.copy(at(2), at(6), to["core"]))
    yield
    via_z.wait_recv()
    via_y.wait_recv()
    from_core.append(wires.copy(at(3), at(7), to["core"]))
    return from_core


def remote_call(kernel, name, key, args, outs, scratch, copies, in_vmem):
    ins, out_in = in_vmem
    spec = lambda inside: pl.BlockSpec(memory_space=pltpu.VMEM if inside else pl.ANY)
    return pl.pallas_call(
        kernel,
        name=name,
        out_shape=outs,
        in_specs=[spec(x) for x in ins],
        out_specs=[spec(x) for x in out_in],
        scratch_shapes=list(scratch)
        + [
            pltpu.SemaphoreType.DMA((copies,)),
            pltpu.SemaphoreType.DMA((copies,)),
            pltpu.SemaphoreType.DMA((10,)),
        ],
        compiler_params=pltpu.CompilerParams(
            collective_id=key, has_side_effects=True, vmem_limit_bytes=VMEM_LIMIT
        ),
    )(*args)


def kv_gather_kernel(own_ref, out_ref, *sems):
    wires, to = Wires(*sems), partners()
    kind = lax.rem(lax.axis_index("tensor"), 2)
    rows = own_ref.shape[0]
    block = lambda j: out_ref.at[kind, pl.ds(j * rows, rows)]
    meet([to[k] for k in ("core", "z", "far", "last")])
    mine = wires.here(own_ref, block(0))
    arrive = [wires.copy(own_ref, block(j), to[k]) for j, k in ((3, "last"), (2, "far"), (1, "z"))]
    from_core = [wires.copy(own_ref, block(0), to["core"])]
    for j, one in ((1, arrive[2]), (2, arrive[1]), (3, arrive[0])):
        one.wait_recv()
        from_core.append(wires.copy(block(j), block(j), to["core"]))
    for one in from_core:
        one.wait_recv()
    mine.wait()
    wires.finish()


def kv_gather(own):
    rows, width = own.shape
    n_c = lax.axis_size("context")
    return remote_call(
        kv_gather_kernel,
        "kv_gather",
        0,
        [own],
        [jax.ShapeDtypeStruct((2, n_c * rows, width), bf16)],
        [],
        8,
        ([False], [False]),
    )[0]


def kv_scatter_kernel(count, part_ref, *refs):
    args, dkv_ref, outs = refs[: 2 * count], refs[2 * count], refs[2 * count + 1 : 3 * count + 1]
    own, got_core, sent, got = refs[3 * count + 1 : 3 * count + 5]
    wires, to = Wires(*refs[-3:]), partners()
    fill = own_grads(count, args, outs, refs[3 * count + 5 : -3])
    kind = lax.rem(lax.axis_index("tensor"), 2)
    rows = dkv_ref.shape[0]
    block = lambda j: pl.ds(j * rows, rows)
    meet([to[k] for k in ("core", "z", "far", "last")])
    steps = ((3, "last"), (2, "far"), (1, "z"), (0, None))
    from_core = {
        j: wires.copy(part_ref.at[1 - kind, block(j)], got_core.at[block(j)], to["core"])
        for j, _ in steps
    }
    mine = wires.here(part_ref.at[kind], own)
    for one in fill:
        one.fetch(wires)
    mine.wait()
    arrive = []
    for j, k in steps[:3]:
        from_core[j].wait_recv()
        sent[block(j)] = (wide(own[block(j)]) + wide(got_core[block(j)])).astype(bf16)
        arrive.append(wires.copy(sent.at[block(j)], got.at[block(j)], to[k]))
    for one in fill:
        one.make(0, one.tiles)
    from_core[0].wait_recv()
    total = wide(own[block(0)]) + wide(got_core[block(0)])
    for one in arrive:
        one.wait_recv()
    for j in (1, 2, 3):
        total = total + wide(got[block(j)])
    dkv_ref[...] = total
    wires.finish()


def kv_scatter(part, fill, width):
    _, rows, depth = part.shape
    n_c = lax.axis_size("context")
    args, outs, scratch = own_grad_call(fill, width)
    return remote_call(
        functools.partial(kv_scatter_kernel, len(fill)),
        "kv_scatter",
        1,
        [part, *args],
        [jax.ShapeDtypeStruct((rows // n_c, depth), f32), *outs],
        [pltpu.VMEM((rows, depth), bf16)] * 4 + scratch,
        7,
        ([False] * (1 + len(args)), [True] * (1 + len(outs))),
    )


def middle_kernel(
    part,
    x_ref,
    gain_ref,
    dy_ref,
    dy_y,
    dy_z,
    dy_far,
    mid_ref,
    factor_ref,
    out,
    dys,
    own,
    core,
    sent,
    got,
    xn,
    *sems,
):
    wires, to = Wires(*sems), partners()
    blocks = out.shape[0] // 2
    size = xn.shape[0] // 2
    low, high = pl.ds(0, size), pl.ds(size, size)
    meet([to[k] for k in ("core", "y", "z", "far")])
    summed = scatter_rank(wires, to, part, own, core, sent, got)
    next(summed)
    mine = [
        wires.here(block, dys.at[k])
        for block, k in ((dy_ref, 0), (dy_y, 1), (dy_z, 2), (dy_far, blocks))
    ]
    via_z = wires.copy(dy_y.at[low], dys.at[3, low], to["z"])
    dy_last = gather_pair(wires, to, dy_far, dys, blocks)
    next(dy_last)
    next(summed)
    via_y = wires.copy(dy_z.at[high], dys.at[3, high], to["y"])
    ends = [
        wires.copy(block, dys.at[4 + k], to["core"])
        for k, block in enumerate((dy_ref, dy_y, dy_z))
    ]
    next(dy_last)
    middle = wide(x_ref[...]) + result_of(summed)
    mid_ref[...] = middle
    factor = lax.rsqrt(jnp.mean(middle * middle, axis=-1, keepdims=True) + EPSILON)
    factor_ref[...] = factor
    xn[...] = (middle * factor * gain_ref[...]).astype(bf16)
    mine.append(wires.here(xn, out.at[0]))
    xn_far = wires.copy(xn, out.at[blocks], to["far"])
    xn_near = gather_pair(wires, to, xn, out, 0)
    next(xn_near)
    next(xn_near)
    via_z.wait_recv()
    via_y.wait_recv()
    ends.append(wires.copy(dys.at[3], dys.at[7], to["core"]))
    next(dy_last)
    next(xn_near)
    xn_far.wait_recv()
    xn_last = gather_pair(wires, to, out.at[blocks], out, blocks)
    next(xn_last)
    next(xn_last)
    ends += result_of(dy_last) + result_of(xn_near)
    next(xn_last)
    ends += result_of(xn_last)
    for one in ends:
        one.wait_recv()
    for one in mine:
        one.wait()
    wires.finish()


def middle_norm(part, inputs_part, gain, dy_blocks):
    rows, width = inputs_part.shape
    return remote_call(
        middle_kernel,
        "middle_norm",
        2,
        [part.reshape(4, rows, width), inputs_part, gain, *dy_blocks],
        [
            jax.ShapeDtypeStruct((rows, width), f32),
            jax.ShapeDtypeStruct((rows, 1), f32),
            jax.ShapeDtypeStruct((16, rows, width), bf16),
            jax.ShapeDtypeStruct((16, rows, width), bf16),
        ],
        [
            pltpu.VMEM((2, rows, width), bf16),
            pltpu.VMEM((2, rows, width), bf16),
            pltpu.VMEM((rows, width), bf16),
            pltpu.VMEM((rows, width), bf16),
            pltpu.VMEM((rows, width), bf16),
        ],
        48,
        ([False] + [True] * 6, [True, True, False, False]),
    )


def norm_back_rows(values, factor, gain, grad_normed):
    gained = gain * grad_normed
    inner = jnp.mean(gained * values, axis=-1, keepdims=True)
    grad_values = factor * gained - values * (factor * factor * factor) * inner
    return grad_values, jnp.sum(grad_normed * values * factor, axis=0, keepdims=True)


def middle_back_kernel(count, part, mid_ref, factor_ref, gain_ref, dy_ref, *refs):
    args, refs = refs[: 2 * count], refs[2 * count :]
    source_ref, refs = (refs[0], refs[1:]) if count else (None, refs)
    (dmid_ref, dgain_ref, out), refs = refs[:3], refs[3:]
    outs, refs = refs[:count], refs[count:]
    (upper_ref, lower_ref, far_ref), refs = (
        (refs[:3], refs[3:]) if count else ((None, None, None), refs)
    )
    low, first, wires, to = refs[0], refs[1:8], Wires(*refs[-3:]), partners()
    fill = own_grads(count, args, outs, refs[8 : 8 + 2 * count])
    meet([to[k] for k in ("core", "y", "z")])
    back = scatter_pair(wires, to, part, *first)
    next(back)
    for one in fill:
        one.fetch(wires)
    if fill:
        got_ref = refs[8 + 2 * count]
        fetched = wires.here(source_ref, got_ref)
    next(back)
    if fill:
        fill[0].make(0, 1)
    next(back)
    if fill:
        fill[0].make(1, fill[0].tiles)
        fetched.wait()
        cut = upper_ref.shape[0]
        upper_ref[...] = (wide(outs[0][:cut]) + wide(got_ref[:cut])).astype(bf16)
        near_half = wires.copy(upper_ref, far_ref, to["z"])
        lower_ref[...] = (wide(outs[0][cut:]) + wide(got_ref[cut:])).astype(bf16)
    grad_normed = result_of(back)
    du, dgain = norm_back_rows(mid_ref[...], factor_ref[...], gain_ref[...], grad_normed)
    dgain_ref[...] = dgain
    dmid = wide(dy_ref[...]) + du
    low[...] = dmid.astype(bf16)
    share = gather_rank(wires, to, low, out)
    next(share)
    dmid_ref[...] = dmid
    for one in fill[1:]:
        one.make(0, one.tiles)
    result_of(share)
    if fill:
        near_half.wait_recv()
    wires.finish()


def pair_scratch(rows, width):
    return [
        pltpu.VMEM((4, rows, width), bf16),
        pltpu.VMEM((4, rows, width), bf16),
        pltpu.VMEM((3, rows, width), bf16),
        pltpu.VMEM((rows, width), bf16),
        pltpu.VMEM((rows, width), bf16),
        pltpu.VMEM((rows // 2, width), bf16),
        pltpu.VMEM((rows // 2, width), bf16),
    ]


def middle_back(part, middle, factor, gain, dy_part, fill, got, shard):
    rows, width = middle.shape
    args, outs, scratch = own_grad_call(fill, shard)
    if fill:
        args = [*args, got]
        scratch = [*scratch, pltpu.VMEM(got.shape, bf16)]
        units = got.shape[0]
        cut = units * 3 // 128 * 16
        outs = [*outs, *(jax.ShapeDtypeStruct((n, shard), bf16) for n in (cut, units - cut, cut))]
    return remote_call(
        functools.partial(middle_back_kernel, len(fill)),
        "middle_back",
        3,
        [part.reshape(8, rows, width), middle, factor, gain, dy_part, *args],
        [
            jax.ShapeDtypeStruct((rows, width), f32),
            jax.ShapeDtypeStruct((1, width), f32),
            jax.ShapeDtypeStruct((4, rows, width), bf16),
            *outs,
        ],
        [pltpu.VMEM((rows, width), bf16)] + pair_scratch(rows, width) + scratch,
        16,
        (
            [False] + [True] * 4 + [False] * len(args),
            [True, True, False] + ([True] * (len(outs) - 1) + [False] if fill else []),
        ),
    )


def add_all(wires, ways, value, slots):
    for k, device in enumerate(ways):
        one = wires.copy(value, slots.at[k], device)
        one.wait()
        wires.started = [x for x in wires.started if x is not one]
        value[...] = value[...] + slots[k]


def input_back_kernel(
    part, x_ref, gain_ref, dmid_ref, small_ref, sum_ref, out, *rest
):
    low, own, core, sent, got, slots = rest[:-3]
    wires, to = Wires(*rest[-3:]), partners()
    meet([to[k] for k in ("core", "y")])
    grad_normed = result_of(scatter_rank(wires, to, part, own, core, sent, got))
    values = wide(x_ref[...])
    factor = lax.rsqrt(jnp.mean(values * values, axis=-1, keepdims=True) + EPSILON)
    du, dgain = norm_back_rows(values, factor, gain_ref[...], grad_normed)
    low[...] = (dmid_ref[...] + du).astype(bf16)
    share = gather_rank(wires, to, low, out)
    next(share)
    width = dgain.shape[1]
    sum_ref[:, width:] = small_ref[:, width:]
    sum_ref[:, :width] = dgain
    add_all(wires, [to["core"], to["y"]], sum_ref, slots)
    result_of(share)
    wires.finish()


def input_back(part, inputs_part, gain, grad_middle, small):
    rows, width = inputs_part.shape
    return remote_call(
        input_back_kernel,
        "input_back",
        5,
        [part.reshape(4, rows, width), inputs_part, gain, grad_middle, small],
        [
            jax.ShapeDtypeStruct(small.shape, f32),
            jax.ShapeDtypeStruct((4, rows, width), bf16),
        ],
        [
            pltpu.VMEM((rows, width), bf16),
            pltpu.VMEM((2, rows, width), bf16),
            pltpu.VMEM((2, rows, width), bf16),
            pltpu.VMEM((rows, width), bf16),
            pltpu.VMEM((rows, width), bf16),
            pltpu.VMEM((2,) + small.shape, f32),
        ],
        16,
        ([False, True, True, True, True], [True, False]),
    )


def context_sum_kernel(over_f, *refs):
    parts, small_ref, out_part, mid_ref = refs[:3], refs[3], refs[4], refs[5]
    outs, sum_ref, shared, outputs = refs[6:8], refs[8], refs[9], refs[10]
    lows, from_end, from_middle = refs[11:15], refs[15:19], refs[19:23]
    out_low, slot, scratch = refs[23], refs[24], refs[25:32]
    wires, to, c = Wires(*refs[32:]), partners(), lax.axis_index("context")
    end = (c == 0) | (c == lax.axis_size("context") - 1)
    inner = jnp.logical_not(end)
    greet = ["core", "y", "z", "last"]
    if over_f:
        to["f"] = {"fsdp": 1 - lax.axis_index("fsdp")}
        greet.append("f")
    meet([to[k] for k in greet])
    ahead = scatter_pair(wires, to, out_part, *scratch)
    next(ahead)
    sum_ref[...] = small_ref[...]
    from_f = wires.copy(small_ref, slot, to["f"]) if over_f else None
    sources = [*parts, sum_ref]
    chunks = []
    for i, cuts in ((2, 1), (0, 2), (1, 4), (3, 1)):
        size = sources[i].shape[0] // cuts
        chunks += [(i, pl.ds(k * size, size)) for k in range(cuts)]
    inward = [wires.plan(sources[i].at[at], from_end[i].at[at], to["z"]) for i, at in chunks]
    across = [wires.plan(lows[i].at[at], from_middle[i].at[at], to["last"]) for i, at in chunks]
    outward = [wires.plan(lows[i].at[at], lows[i].at[at], to["z"]) for i, at in chunks]
    small = len(chunks) - 1

    def send_in(k):
        @pl.when(end)
        def _():
            inward[k].start()

    def pass_on(first, past):
        @pl.when(inner)
        def _():
            for k in range(first, past):
                i, at = chunks[k]
                inward[k].wait_recv()
                total = wide(sources[i][at]) + wide(from_end[i][at])
                lows[i][at] = total.astype(lows[i].dtype)
                across[k].start()
                if k:
                    send_out(k - 1)

    def send_out(k):
        i, at = chunks[k]
        across[k].wait()
        lows[i][at] = (wide(lows[i][at]) + wide(from_middle[i][at])).astype(lows[i].dtype)
        outward[k].start()

    early, late = 3, 5
    for k in range(early):
        send_in(k)
    next(ahead)
    for k in range(early, late):
        send_in(k)
    pass_on(0, early)
    next(ahead)
    if over_f:
        from_f.wait_recv()
        sum_ref[...] = sum_ref[...] + slot[...]
    for k in range(late, small + 1):
        send_in(k)
    pass_on(early, late)
    out_low[...] = (mid_ref[...] + result_of(ahead)).astype(bf16)
    out_share = gather_rank(wires, to, out_low, outputs)
    next(out_share)
    pass_on(late, small + 1)

    @pl.when(inner)
    def _():
        send_out(small)

    result_of(out_share)

    def arrived(k):
        @pl.when(end)
        def _():
            outward[k].wait_recv()

    arrived(0)
    share = gather_rank(wires, to, lows[2], shared)
    next(share)
    for k in range(1, len(chunks)):
        arrived(k)

    @pl.when(end)
    def _():
        for one in inward:
            one.wait_send()

    for i in (0, 1):
        outs[i][...] = wide(lows[i][...])
    sum_ref[...] = lows[3][...]
    result_of(share)

    @pl.when(inner)
    def _():
        for one in outward:
            one.wait_send()

    wires.finish()


def context_sum(over_f, parts, small, out_part, middle):
    rows, width = middle.shape
    lines = [pltpu.VMEM(x.shape, x.dtype) for x in (*parts, small)]
    return remote_call(
        functools.partial(context_sum_kernel, over_f),
        "context_sum",
        6,
        [*parts, small, out_part.reshape(8, rows, width), middle],
        [jax.ShapeDtypeStruct(x.shape, f32) for x in parts[:2]]
        + [jax.ShapeDtypeStruct(small.shape, f32)]
        + [jax.ShapeDtypeStruct((4,) + parts[2].shape, bf16)]
        + [jax.ShapeDtypeStruct((4, rows, width), bf16)],
        lines * 3
        + [pltpu.VMEM((rows, width), bf16), pltpu.VMEM(small.shape, f32)]
        + pair_scratch(rows, width),
        48,
        ([True] * 4 + [False, True], [True] * 3 + [False] * 2),
    )


def build(n_f, n_c, n_t):
    def flip(x, axis, bit):
        size = {"fsdp": n_f, "context": n_c, "tensor": n_t}[axis]
        return lax.ppermute(x, axis, [(i, i ^ bit) for i in range(size)])

    def by_bit(bit, x, other, axis):
        return jnp.where(
            bit == 0,
            jnp.concatenate([x, other], axis=axis),
            jnp.concatenate([other, x], axis=axis),
        )

    def after(x, *others):
        return lax.optimization_barrier((x, others))[0]

    def local(
        inputs,
        cotangent,
        blocks,
        attn_gain,
        w_query,
        b_query,
        w_key,
        b_key,
        w_value,
        b_value,
        w_out,
        ffn_gain,
        w_gate,
        w_up,
        w_down,
    ):
        rows, width = inputs.shape
        f = lax.axis_index("fsdp")
        c = lax.axis_index("context")
        t = lax.axis_index("tensor")
        core, parity, pair = t % 2, c % 2, c // 2
        heads = w_query.shape[1] // HD
        group = (t * heads) // (H // KV)
        part = rows // n_t
        units_all = w_gate.shape[1]
        units = units_all // 2

        def gather_f(x, axis):
            if n_f == 2:
                return by_bit(f, x, flip(x, "fsdp", 1), axis)
            return lax.all_gather(x, "fsdp", axis=axis, tiled=True)

        def grad_far(left, right, side):
            if n_f > 2:
                return None
            source = (left, right)[side]
            half = width // 2
            far = lax.dynamic_slice_in_dim(source, (1 - f) * half, half, 1)
            return (dot_rows(far, right) if side == 0 else dot_rows(left, far)).astype(bf16)

        def grad_sum(left, right, side, far, late):
            if n_f > 2:
                return lax.psum_scatter(
                    dot_rows(left, right).astype(bf16), "fsdp", scatter_dimension=side, tiled=True
                )
            source = (left, right)[side]
            half = width // 2
            own = lax.dynamic_slice_in_dim(source, f * half, half, 1)
            own = dot_rows(own, right) if side == 0 else dot_rows(left, own)
            return (own + after(flip(far, "fsdp", 1), late).astype(f32)).astype(bf16)

        small = jnp.concatenate(
            [v.reshape(1, -1) for v in (attn_gain, ffn_gain, b_query, b_key, b_value)], axis=1
        )
        column = lambda w: lax.dynamic_slice_in_dim(w, group * HD, HD, 1)
        w_kv_own = jnp.where(core == 0, column(w_key), column(w_value))
        pieces_f = lambda x, axis: (
            [x, flip(x, "fsdp", 1)]
            if n_f == 2
            else [lax.all_gather(x, "fsdp", axis=axis, tiled=True)]
        )
        meta = jnp.stack([f, 1 - f, core, pair]).astype(jnp.int32)
        w_q = pieces_f(w_query, 0)
        w_kv = pieces_f(w_kv_own, 0)
        small = gather_f(small, 0)
        w_out_all = gather_f(after(w_out, small, w_q, w_kv), 1)
        piece = attn_gain.shape[0]
        gain_first = small[:, :piece].reshape(1, width).astype(f32)
        gain_second = small[:, piece : 2 * piece].reshape(1, width).astype(f32)
        bias_of = lambda lo, n: (
            small[:, lo : lo + n * (HD // n_f)]
            .reshape(n_f, n, HD // n_f)
            .transpose(1, 0, 2)
            .reshape(n, HD)
            .astype(f32)
        )
        at = 2 * piece
        bq = bias_of(at, heads)
        bk = bias_of(at + heads * (HD // n_f), KV)
        bv = bias_of(at + (heads + KV) * (HD // n_f), KV)
        b_kv = lax.dynamic_index_in_dim(jnp.where(core == 0, bk, bv), group, 0)

        unit_slice = lambda w: lax.dynamic_slice_in_dim(w, parity * units, units, 0)
        own_gate_up = jnp.concatenate(
            [unit_slice(after(w, w_kv_own)) for w in (w_gate.T, w_up.T)], axis=0
        )
        own_down = unit_slice(w_down)

        dy_part = lax.dynamic_slice_in_dim(cotangent, t * part, part, 0)

        seq_blocks = blocks[0].reshape(n_c, -1)
        own_blocks = seq_blocks.shape[1]
        key_blocks = jnp.concatenate(
            [lax.dynamic_index_in_dim(seq_blocks, c ^ j, 0, keepdims=False) for j in range(n_c)]
        )
        positions = (
            key_blocks[:own_blocks, None] * BLOCK + jnp.arange(BLOCK, dtype=jnp.int32)[None, :]
        ).reshape(-1)
        cosine, sine = rope_tables(positions)
        bias = jnp.concatenate([bq.reshape(1, -1), b_kv], axis=1)
        dy_blocks = [
            dy_part,
            flip(dy_part, "tensor", 2),
            flip(dy_part, "context", 1),
            flip(dy_part, "context", 2),
        ]
        inputs_part = lax.dynamic_slice_in_dim(inputs, t * part, part, 0)
        bias = after(bias, dy_blocks[2:], own_gate_up, own_down, inputs_part)
        normed, queries, kv_own = qkv(
            meta, inputs, gain_first, bias, cosine, sine, w_q, w_kv
        )
        kv = after(kv_gather(kv_own), w_out_all)
        far_gate_up = pieces_f(after(own_gate_up, kv), 1)[-1]
        w_gate_up = [own_gate_up, far_gate_up] if n_f == 2 else [far_gate_up]
        far_down = pieces_f(after(own_down, kv), 1)[-1]
        w_downs = [own_down, far_down] if n_f == 2 else [far_down]
        attended, lse = attention(key_blocks, queries, kv)
        middle, factor_second, normed2, dy_all = middle_norm(
            dot(attended, w_out_all).astype(bf16), inputs_part, gain_second, dy_blocks
        )

        hidden, slope, gated, *down_far = hidden_units(meta, normed2, dy_all, w_gate_up)
        grad_gate, grad_up, dx_part, out_part, *unit_far = hidden_back(
            meta, normed2, dy_all, hidden, slope, gated, w_gate_up, w_downs
        )
        unit_far = [*down_far, *unit_far]
        flat = lambda x: x.reshape(-1, width)
        if n_f == 2:
            down_got, gate_got, up_got = (flip(x, "fsdp", 1) for x in unit_far)
            early = [(hidden, flat(dy_all)), (grad_gate, flat(normed2))]
            later = [(grad_up, flat(normed2))]
        else:
            over_f = lambda x: lax.psum_scatter(x, "fsdp", scatter_dimension=1, tiled=True)
            owns = [
                over_f(unit_grads(meta, 0, 1, x, [unit]))
                for x, unit in ((dy_all, hidden), (normed2, grad_gate), (normed2, grad_up))
            ]
            down_got = gate_got = up_got = jnp.zeros_like(owns[0])
            early = later = []

        def unit_whole(own, other):
            own, other = (jnp.concatenate(x, axis=0) for x in (own, other))
            return by_bit(parity, own, other, 0).astype(f32)

        grad_middle, ffn_gain_grad, grad_middle_low, *first_owns = middle_back(
            dx_part, middle, factor_second, gain_second, dy_part, early, down_got, width // n_f
        )
        grad_middle_low = grad_middle_low.reshape(rows, width)
        add = lambda own, got: (own.astype(f32) + got.astype(f32)).astype(bf16)
        upper = units // 2
        if n_f == 2:
            _, gate_own, down_upper, down_lower, far_upper = first_owns
        else:
            down_low, gate_own = owns[:2]
            down_upper, down_lower = down_low[:upper], down_low[upper:]
            far_upper = flip(down_upper, "context", 1)
        far_lower = flip(down_lower, "context", 1)
        grad_attended = dot_cols(grad_middle_low, w_out_all).astype(bf16)

        dq_low, dkv = attention_back(key_blocks, queries, grad_attended, lse, cosine, sine, kv)
        attention_args = [(attended, after(grad_middle_low, dq_low), 1), (normed, dq_low, 0)]
        fars = [grad_far(*args) for args in attention_args]
        gate_low = add(gate_own, after(gate_got, dq_low))
        dkv, *last_owns = kv_scatter(
            after(dkv, fars, gate_low, far_lower), later, width // n_f
        )
        (up_own,) = last_owns or owns[2:]
        far_gate = flip(after(gate_low, dkv, far_lower), "context", 1)
        dkv = after(dkv, far_lower)
        dkv_low = jnp.where(core == 0, rotate_back(dkv, cosine, sine), dkv).astype(bf16)
        own_biases = jnp.sum(
            jnp.concatenate([dq_low, dkv_low], axis=1).astype(f32), axis=0, keepdims=True
        )
        slots = lax.dynamic_update_slice(
            jnp.zeros((n_t, (heads + 1) * HD), f32), own_biases, (t, 0)
        )
        small_grads = jnp.concatenate(
            [jnp.zeros((1, width), f32), ffn_gain_grad, slots.reshape(1, -1)], axis=1
        )
        grad_qkv = qkv_back(meta, dq_low, dkv_low, w_q, w_kv)
        up_low = add(up_own, after(up_got, grad_qkv))
        attention_args.append((after(normed, grad_qkv), dkv_low, 0))
        fars.append(grad_far(*attention_args[-1]))
        far_up = flip(up_low, "context", 1)
        small_grads, input_grad = input_back(
            after(grad_qkv, up_low, fars),
            inputs_part,
            gain_first,
            grad_middle,
            small_grads,
        )
        input_grad = input_grad.reshape(rows, width)
        if n_f > 2:
            small_grads = lax.psum(small_grads, "fsdp")
        zero = jnp.minimum(t, 0).astype(bf16)
        input_grad = input_grad + zero
        small_grads = after(small_grads, far_gate)
        attention_parts = [
            grad_sum(*args, far, small_grads) for args, far in zip(attention_args, fars)
        ]
        wd_grad = unit_whole(
            *after(((down_upper, down_lower), (far_upper, far_lower)), small_grads)
        )
        wg_grad = unit_whole(*after(((gate_low,), (far_gate,)), small_grads))
        small_grads, wd_grad, wg_grad, input_grad = lax.optimization_barrier(
            (small_grads, wd_grad, wg_grad, input_grad)
        )
        wo_grad, wq_grad, packed, wkv_all, outputs = context_sum(
            n_f == 2, attention_parts, small_grads, out_part, middle
        )
        wo_grad, wq_grad, packed, wkv_all, outputs, far_up = lax.optimization_barrier(
            (wo_grad, wq_grad, packed, wkv_all, outputs, far_up)
        )
        outputs = outputs.reshape(rows, width)
        wk_grad = jnp.concatenate([wkv_all[0], wkv_all[2]], axis=1).astype(f32)
        wv_grad = jnp.concatenate([wkv_all[1], wkv_all[3]], axis=1).astype(f32)
        packed = packed[0]
        attn_gain_grad = lax.dynamic_slice_in_dim(packed, f * piece, piece, 0)
        ffn_gain_grad = lax.dynamic_slice_in_dim(packed, width + f * piece, piece, 0)
        slots = packed[2 * width :].reshape(n_t, heads + 1, HD)
        slots = lax.dynamic_slice_in_dim(slots, f * (HD // n_f), HD // n_f, 2)
        bq_out = lax.dynamic_index_in_dim(slots, t, 0, keepdims=False)[:heads]
        bk_out = slots[0::2, heads]
        bv_out = slots[1::2, heads]

        wu_grad = unit_whole((up_low,), (far_up,))
        wg_grad, wu_grad = wg_grad.T, wu_grad.T

        return (
            outputs,
            input_grad,
            attn_gain_grad,
            wq_grad,
            bq_out,
            wk_grad,
            bk_out,
            wv_grad,
            bv_out,
            wo_grad,
            ffn_gain_grad,
            wg_grad,
            wu_grad,
            wd_grad,
        )

    return local


def solution(mesh):
    in_specs = (
        P(("fsdp", "context"), None),
        P(("fsdp", "context"), None),
        P("fsdp", None),
        P("fsdp"),
        P("fsdp", "tensor"),
        P("tensor", "fsdp"),
        P("fsdp", None),
        P(None, "fsdp"),
        P("fsdp", None),
        P(None, "fsdp"),
        P("tensor", "fsdp"),
        P("fsdp"),
        P("fsdp", "tensor"),
        P("fsdp", "tensor"),
        P("tensor", "fsdp"),
    )
    out_specs = (
        P(("fsdp", "context"), None),
        P(("fsdp", "context"), None),
        P("fsdp"),
        P("fsdp", "tensor"),
        P("tensor", "fsdp"),
        P("fsdp", None),
        P(None, "fsdp"),
        P("fsdp", None),
        P(None, "fsdp"),
        P("tensor", "fsdp"),
        P("fsdp"),
        P("fsdp", "tensor"),
        P("fsdp", "tensor"),
        P("tensor", "fsdp"),
    )
    local = build(mesh.shape["fsdp"], mesh.shape["context"], mesh.shape["tensor"])
    return jax.shard_map(local, mesh=mesh, in_specs=in_specs, out_specs=out_specs, check_vma=False)
```

```python
import functools

import jax
import jax.numpy as jnp
from jax import lax
from jax.experimental import pallas as pl
from jax.experimental.pallas import tpu as pltpu
from jax.sharding import PartitionSpec as P

H = 12
KV = 2
HD = 128
BLOCK = 256

EPSILON = 1e-06
ROPE_BASE = 1000000.0
MASKED = -1e30
SCALING = HD ** (-0.5)
LANES = 128
VMEM_LIMIT = 60 << 20

f32 = jnp.float32
bf16 = jnp.bfloat16


def rope_tables(positions):
    halfway = HD // 2
    frequency = ROPE_BASE ** (-(jnp.arange(halfway, dtype=f32) * 2.0 / HD))
    angles = positions.astype(f32)[:, None] * frequency[None, :]
    cosine, sine = jnp.cos(angles), jnp.sin(angles)
    return (jnp.concatenate([cosine, cosine], axis=1), jnp.concatenate([sine, sine], axis=1))


def rotate(field, cosine, sine):
    halfway = HD // 2
    turned = jnp.concatenate([-field[..., halfway:], field[..., :halfway]], axis=-1)
    return field * cosine + turned * sine


def rotate_back(grad_field, cosine, sine):
    halfway = HD // 2
    moved = grad_field * sine
    turned = jnp.concatenate([moved[..., halfway:], -moved[..., :halfway]], axis=-1)
    return grad_field * cosine + turned


def dot(left, right):
    return jnp.dot(left, right, preferred_element_type=f32)


def dot_rows(left, right):
    return lax.dot_general(left, right, (((0,), (0,)), ((), ())), preferred_element_type=f32)


def dot_cols(left, right):
    return lax.dot_general(left, right, (((1,), (1,)), ((), ())), preferred_element_type=f32)


def mask_row(kb_ref, own_block, key_blocks):
    return jnp.concatenate(
        [
            jnp.full((1, BLOCK), jnp.where(kb_ref[j] <= own_block, 0.0, MASKED), f32)
            for j in range(key_blocks)
        ],
        axis=1,
    )


def attention_kernel(key_blocks, kb_ref, q_ref, k_ref, v_ref, o_ref, lse_ref):
    bias = mask_row(kb_ref, kb_ref[pl.program_id(1)], key_blocks)
    scores = dot_cols(q_ref[...], k_ref[...]) * SCALING + bias
    row_max = jnp.max(scores, axis=1, keepdims=True)
    expo = jnp.exp(scores - row_max)
    total = jnp.sum(expo, axis=1, keepdims=True)
    probability = (expo * (1.0 / total)).astype(bf16)
    o_ref[...] = dot(probability, v_ref[...]).astype(bf16)
    lse_ref[0] = row_max + jnp.log(total)


def attention(key_blocks, queries, kv):
    rows, width = queries.shape
    heads = width // HD
    whole = lambda kind: pl.BlockSpec((None,) + kv.shape[1:], lambda h, i, kb: (kind, 0, 0))
    tile = pl.BlockSpec((BLOCK, HD), lambda h, i, kb: (i, h))
    return pl.pallas_call(
        functools.partial(attention_kernel, kv.shape[1] // BLOCK),
        name="attention",
        grid_spec=pltpu.PrefetchScalarGridSpec(
            num_scalar_prefetch=1,
            grid=(heads, rows // BLOCK),
            in_specs=[tile, whole(0), whole(1)],
            out_specs=[tile, pl.BlockSpec((1, BLOCK, 1), lambda h, i, kb: (h, i, 0))],
        ),
        out_shape=[
            jax.ShapeDtypeStruct((rows, width), bf16),
            jax.ShapeDtypeStruct((heads, rows, 1), f32),
        ],
        compiler_params=pltpu.CompilerParams(vmem_limit_bytes=VMEM_LIMIT),
    )(key_blocks, queries, kv, kv)


def attention_back_kernel(
    key_blocks,
    kb_ref,
    q_ref,
    do_ref,
    lse_ref,
    cos_ref,
    sin_ref,
    k_ref,
    v_ref,
    dq_ref,
    dkv_ref,
    dk_ref,
    dv_ref,
):
    head, i = pl.program_id(0), pl.program_id(1)

    @pl.when((head == 0) & (i == 0))
    def _():
        dk_ref[...] = jnp.zeros_like(dk_ref)
        dv_ref[...] = jnp.zeros_like(dv_ref)

    bias = mask_row(kb_ref, kb_ref[i], key_blocks)
    scores = dot_cols(q_ref[...], k_ref[...]) * SCALING + bias
    probability = jnp.exp(scores - lse_ref[0])
    grad_probs = dot_cols(do_ref[...], v_ref[...])
    inner = jnp.sum(probability * grad_probs, axis=1, keepdims=True)
    grad_scores = (probability * (grad_probs - inner)).astype(bf16)
    grad_query = dot(grad_scores, k_ref[...]) * SCALING
    moved = grad_query * sin_ref[...]
    sign = jnp.where(lax.broadcasted_iota(jnp.int32, moved.shape, 1) < HD // 2, 1.0, -1.0)
    dq_ref[...] = (
        grad_query * cos_ref[...] + pltpu.roll(moved, HD // 2, 1) * sign
    ).astype(bf16)
    dk_ref[...] += dot_rows(grad_scores, q_ref[...]) * SCALING
    dv_ref[...] += dot_rows(probability.astype(bf16), do_ref[...])

    @pl.when((head == pl.num_programs(0) - 1) & (i == pl.num_programs(1) - 1))
    def _():
        dkv_ref[0] = dk_ref[...].astype(bf16)
        dkv_ref[1] = dv_ref[...].astype(bf16)


def attention_back(key_blocks, queries, grad_out, lse, cosine, sine, kv):
    rows, width = queries.shape
    heads = width // HD
    whole = lambda kind: pl.BlockSpec((None,) + kv.shape[1:], lambda h, i, kb: (kind, 0, 0))
    tile = pl.BlockSpec((BLOCK, HD), lambda h, i, kb: (i, h))
    table = pl.BlockSpec((BLOCK, HD), lambda h, i, kb: (i, 0))
    return pl.pallas_call(
        functools.partial(attention_back_kernel, kv.shape[1] // BLOCK),
        name="attention_back",
        grid_spec=pltpu.PrefetchScalarGridSpec(
            num_scalar_prefetch=1,
            grid=(heads, rows // BLOCK),
            in_specs=[
                tile,
                tile,
                pl.BlockSpec((1, BLOCK, 1), lambda h, i, kb: (h, i, 0)),
                table,
                table,
                whole(0),
                whole(1),
            ],
            out_specs=[tile, pl.BlockSpec(kv.shape, lambda h, i, kb: (0, 0, 0))],
            scratch_shapes=[pltpu.VMEM(kv.shape[1:], f32)] * 2,
        ),
        out_shape=[
            jax.ShapeDtypeStruct((rows, width), bf16),
            jax.ShapeDtypeStruct(kv.shape, bf16),
        ],
        compiler_params=pltpu.CompilerParams(vmem_limit_bytes=VMEM_LIMIT),
    )(key_blocks, queries, grad_out, lse, cosine, sine, kv, kv)


def qkv_kernel(pieces, meta_ref, x_ref, gain_ref, bias_ref, cos_ref, sin_ref, *refs):
    weights, (xn_ref, q_ref, kv_ref) = refs[: 2 * pieces], refs[2 * pieces :]
    values = x_ref[...].astype(f32)
    factor = lax.rsqrt(jnp.mean(values * values, axis=-1, keepdims=True) + EPSILON)
    xn_ref[...] = (values * factor * gain_ref[...]).astype(bf16)
    depth = weights[0].shape[0]
    normed = [xn_ref[:, columns_of(meta_ref, j, depth, pieces)] for j in range(pieces)]
    cosine, sine = cos_ref[...], sin_ref[...]
    sign = jnp.where(lax.broadcasted_iota(jnp.int32, cosine.shape, 1) < HD // 2, -1.0, 1.0)
    sine = sine * sign
    width = q_ref.shape[1]
    total = bias_ref[:, :width] + sum(dot(x, w[...]) for x, w in zip(normed, weights[:pieces]))
    turn = lambda own: own * cosine + pltpu.roll(own, HD // 2, 1) * sine
    for h in range(width // HD):
        q_ref[:, h * HD : (h + 1) * HD] = turn(total[:, h * HD : (h + 1) * HD]).astype(bf16)
    own = bias_ref[:, width:] + sum(dot(x, w[...]) for x, w in zip(normed, weights[pieces:]))
    kv_ref[...] = jnp.where(meta_ref[2] == 0, turn(own), own).astype(bf16)


def columns_of(meta_ref, j, depth, pieces):
    if pieces == 1:
        return slice(None)
    return pl.ds(pl.multiple_of(meta_ref[j] * depth, LANES), depth)


def qkv(meta, inputs, gain, bias, cosine, sine, w_q, w_kv):
    rows, width = inputs.shape
    out = w_q[0].shape[1]
    tile = 256
    row = lambda n: pl.BlockSpec((tile, n), lambda i, m: (i, 0))
    fixed = lambda w: pl.BlockSpec(w.shape, lambda i, m: (0, 0))
    return pl.pallas_call(
        functools.partial(qkv_kernel, len(w_q)),
        name="qkv",
        grid_spec=pltpu.PrefetchScalarGridSpec(
            num_scalar_prefetch=1,
            grid=(rows // tile,),
            in_specs=[row(width), fixed(gain), fixed(bias), row(HD), row(HD)]
            + [fixed(w) for w in (*w_q, *w_kv)],
            out_specs=[row(width), row(out), row(HD)],
        ),
        out_shape=[
            jax.ShapeDtypeStruct((rows, width), bf16),
            jax.ShapeDtypeStruct((rows, out), bf16),
            jax.ShapeDtypeStruct((rows, HD), bf16),
        ],
        compiler_params=pltpu.CompilerParams(vmem_limit_bytes=VMEM_LIMIT),
    )(meta, inputs, gain, bias, cosine, sine, *w_q, *w_kv)


def qkv_back_kernel(pieces, meta_ref, dq_ref, dkv_ref, *refs):
    w_q, w_kv, out_ref = refs[:pieces], refs[pieces : 2 * pieces], refs[-1]
    for j in range(pieces):
        out_ref[:, columns_of(meta_ref, j, w_q[j].shape[0], pieces)] = (
            dot_cols(dq_ref[...], w_q[j][...]) + dot_cols(dkv_ref[...], w_kv[j][...])
        ).astype(bf16)


def qkv_back(meta, grad_q, grad_kv, w_q, w_kv):
    rows, width = grad_q.shape[0], sum(w.shape[0] for w in w_q)
    tile = 256
    row = lambda n: pl.BlockSpec((tile, n), lambda i, m: (i, 0))
    fixed = lambda w: pl.BlockSpec(w.shape, lambda i, m: (0, 0))
    return pl.pallas_call(
        functools.partial(qkv_back_kernel, len(w_q)),
        name="qkv_back",
        grid_spec=pltpu.PrefetchScalarGridSpec(
            num_scalar_prefetch=1,
            grid=(rows // tile,),
            in_specs=[row(grad_q.shape[1]), row(HD)] + [fixed(w) for w in (*w_q, *w_kv)],
            out_specs=row(width),
        ),
        out_shape=jax.ShapeDtypeStruct((rows, width), bf16),
        compiler_params=pltpu.CompilerParams(vmem_limit_bytes=VMEM_LIMIT),
    )(meta, grad_q, grad_kv, *w_q, *w_kv)


def add_rows(unit_refs, row_refs, columns, totals, outs):
    step = pl.program_id(0)

    @pl.when(step == 0)
    def _():
        for total in totals:
            total[...] = jnp.zeros_like(total)

    for total, unit, row in zip(totals, unit_refs, row_refs):
        total[...] += dot_rows(unit[...], row[:, columns])

    @pl.when(step == pl.num_programs(0) - 1)
    def _():
        for out, total in zip(outs, totals):
            out[...] = total[...].astype(bf16)


def hidden_kernel(pieces, meta_ref, x_ref, dy_ref, *refs):
    wg, wu, refs = refs[:pieces], refs[pieces : 2 * pieces], refs[2 * pieces :]
    hid_ref, slope_ref, gated_ref = refs[:3]
    columns = [columns_of(meta_ref, j, wg[j].shape[1], pieces) for j in range(pieces)]
    gate = sum(dot_cols(x_ref[:, at], w[...]) for at, w in zip(columns, wg))
    up = sum(dot_cols(x_ref[:, at], w[...]) for at, w in zip(columns, wu))
    sigma = 1.0 / (1.0 + jnp.exp(-gate))
    gated = gate * sigma
    hid_ref[...] = (gated * up).astype(bf16)
    slope_ref[...] = (up * (sigma + gated * (1.0 - sigma))).astype(bf16)
    gated_ref[...] = gated.astype(bf16)
    if pieces == 2:
        add_rows([hid_ref], [dy_ref], columns[1], refs[4:], refs[3:4])


def hidden_back_kernel(pieces, meta_ref, x_ref, dy_ref, hid_ref, slope_ref, gated_ref, *refs):
    wg, wu, wd = (refs[m * pieces : (m + 1) * pieces] for m in range(3))
    refs = refs[3 * pieces :]
    dg_ref, du_ref, dx_ref, out_ref = refs[:4]
    columns = [columns_of(meta_ref, j, wg[j].shape[1], pieces) for j in range(pieces)]
    grad_hidden = sum(dot_cols(dy_ref[:, at], w[...]) for at, w in zip(columns, wd))
    dg_ref[...] = (grad_hidden * slope_ref[...].astype(f32)).astype(bf16)
    du_ref[...] = (grad_hidden * gated_ref[...].astype(f32)).astype(bf16)

    @pl.when(pl.program_id(0) // (pl.num_programs(0) // 2) == meta_ref[3])
    def _():
        for at, g, u, d in zip(columns, wg, wu, wd):
            dx_ref[:, at] = (dot(dg_ref[...], g[...]) + dot(du_ref[...], u[...])).astype(bf16)
            out_ref[:, at] = dot(hid_ref[...], d[...]).astype(bf16)

    if pieces == 2:
        add_rows([dg_ref, du_ref], [x_ref, x_ref], columns[1], refs[6:], refs[4:6])


def hidden_specs(meta, normed, weights):
    width = normed.shape[-1]
    rows = normed.shape[0] * normed.shape[1]
    units, depth = weights[0].shape[0] // 2, weights[0].shape[1]
    tile = 512
    steps = rows // tile
    half = steps // 2
    once = pl.Buffered(1)
    inside = lambda i, m: jnp.clip(i - m[3] * half, 0, half - 1)
    return {
        "steps": steps,
        "flat": lambda x: x.reshape(-1, width),
        "row": pl.BlockSpec((tile, width), lambda i, m: (lax.rem(i + m[3] * half, steps), 0)),
        "unit": pl.BlockSpec((tile, units), lambda i, m: (i, 0)),
        "near_unit": pl.BlockSpec((tile, units), lambda i, m: (inside(i, m) + m[3] * half, 0)),
        "near_row": pl.BlockSpec((tile, width), lambda i, m: (inside(i, m), 0)),
        "weight": lambda k: pl.BlockSpec((units, depth), lambda i, m: (k, 0), pipeline_mode=once),
        "grad": pl.BlockSpec((units, depth), lambda i, m: (0, 0), pipeline_mode=once),
        "unit_shape": jax.ShapeDtypeStruct((rows, units), bf16),
        "near_shape": jax.ShapeDtypeStruct((rows // 2, width), bf16),
        "grad_shape": jax.ShapeDtypeStruct((units, depth), bf16),
        "total": pltpu.VMEM((units, depth), f32),
    }


def hidden_call(kernel, name, meta, args, in_specs, outs, grads, specs):
    return pl.pallas_call(
        kernel,
        name=name,
        grid_spec=pltpu.PrefetchScalarGridSpec(
            num_scalar_prefetch=1,
            grid=(specs["steps"],),
            in_specs=in_specs,
            out_specs=[specs[x] for x in outs] + [specs["grad"]] * grads,
            scratch_shapes=[specs["total"]] * grads,
        ),
        out_shape=[specs[x.split("_")[0] + "_shape"] for x in outs]
        + [specs["grad_shape"]] * grads,
        compiler_params=pltpu.CompilerParams(vmem_limit_bytes=VMEM_LIMIT),
    )(meta, *args)


def hidden_units(meta, normed, grad_out, weights):
    specs, pieces = hidden_specs(meta, normed, weights), len(weights)
    return hidden_call(
        functools.partial(hidden_kernel, pieces),
        "hidden_units",
        meta,
        [specs["flat"](normed), specs["flat"](grad_out)] + list(weights) * 2,
        [specs["row"]] * 2 + [specs["weight"](k) for k in range(2) for _ in weights],
        ["unit"] * 3,
        pieces == 2,
        specs,
    )


def hidden_back(meta, normed, grad_out, hidden, slope, gated, weights, down_weights):
    specs, pieces = hidden_specs(meta, normed, weights), len(weights)
    return hidden_call(
        functools.partial(hidden_back_kernel, pieces),
        "hidden_back",
        meta,
        [specs["flat"](normed), specs["flat"](grad_out), hidden, slope, gated]
        + list(weights) * 2
        + list(down_weights),
        [specs["row"]] * 2
        + [specs["near_unit"], specs["unit"], specs["unit"]]
        + [specs["weight"](k) for k in (0, 1, 0) for _ in weights],
        ["unit", "unit", "near_row", "near_row"],
        2 * (pieces == 2),
        specs,
    )


def unit_grads_kernel(count, meta_ref, near_ref, far_ref, *refs):
    units, out_ref, x_ref = refs[:count], refs[-2], refs[-1]
    half = near_ref.shape[0]
    x_ref[pl.ds(pl.multiple_of(meta_ref[3] * half, half), half)] = near_ref[...]
    x_ref[pl.ds(pl.multiple_of((1 - meta_ref[3]) * half, half), half)] = far_ref[...]
    for k, unit in enumerate(units):
        depth = unit.shape[1]
        out_ref[k * depth : (k + 1) * depth] = dot_rows(unit[...], x_ref[...]).astype(bf16)


def unit_grads(meta, which, pieces, x, units_of):
    width = x.shape[-1]
    count, (rows, units) = len(units_of), units_of[0].shape
    depth = width // pieces
    tile = 256
    steps = depth // tile
    shard = (lambda m: m[which]) if pieces > 1 else (lambda m: 0)
    feature = lambda half: pl.BlockSpec(
        (rows // 2, tile), lambda i, m: (half, shard(m) * steps + i)
    )
    unit = pl.BlockSpec((rows, units), lambda i, m: (0, 0), pipeline_mode=pl.Buffered(1))
    x = x.reshape(-1, width)
    return pl.pallas_call(
        functools.partial(unit_grads_kernel, count),
        name=f"unit_grads_{which}_{count}",
        grid_spec=pltpu.PrefetchScalarGridSpec(
            num_scalar_prefetch=1,
            grid=(steps,),
            in_specs=[feature(0), feature(1)] + [unit] * count,
            out_specs=pl.BlockSpec((count * units, tile), lambda i, m: (0, i)),
            scratch_shapes=[pltpu.VMEM((rows, tile), bf16)],
        ),
        out_shape=jax.ShapeDtypeStruct((count * units, depth), bf16),
        compiler_params=pltpu.CompilerParams(vmem_limit_bytes=VMEM_LIMIT),
    )(meta, x, x, *units_of)


class Wires:
    def __init__(self, sends, receives, locals_):
        self.sends, self.receives, self.locals = sends, receives, locals_
        self.used = self.used_local = 0
        self.started = []

    def plan(self, source, target, device):
        k = self.used
        self.used += 1
        return pltpu.make_async_remote_copy(
            source,
            target,
            self.sends.at[k],
            self.receives.at[k],
            device_id=device,
            device_id_type=pl.DeviceIdType.MESH,
        )

    def copy(self, source, target, device):
        one = self.plan(source, target, device)
        one.start()
        self.started.append(one)
        return one

    def here(self, source, target):
        k = self.used_local
        self.used_local += 1
        one = pltpu.make_async_copy(source, target, self.locals.at[k])
        one.start()
        return one

    def finish(self):
        for one in self.started:
            one.wait_send()


class OwnGrad:
    TILE = 256

    def __init__(self, units, rows, out, units_here, rows_here):
        self.units, self.rows, self.out = units, rows, out
        self.units_here, self.rows_here = units_here, rows_here
        self.tiles = out.shape[1] // self.TILE
        self.copies = None

    def fetch(self, wires):
        half, depth = self.rows.shape[0] // 2, self.out.shape[1]
        column = pl.multiple_of(lax.axis_index("fsdp") * depth, LANES)
        pair = lax.axis_index("context") // 2
        self.copies = [wires.here(self.units, self.units_here)]
        for k, place in ((0, pair), (1, 1 - pair)):
            self.copies.append(
                wires.here(
                    self.rows.at[pl.ds(k * half, half), pl.ds(column, depth)],
                    self.rows_here.at[pl.ds(pl.multiple_of(place * half, half), half)],
                )
            )

    def make(self, first, past):
        for one in self.copies:
            one.wait()
        self.copies = []

        @pl.loop(first, past)
        def _(k):
            at = pl.ds(pl.multiple_of(k * self.TILE, self.TILE), self.TILE)
            self.out[:, at] = dot_rows(self.units_here[...], self.rows_here[:, at]).astype(bf16)


def own_grad_call(fill, width):
    args = [x for pair in fill for x in pair]
    outs = [jax.ShapeDtypeStruct((units.shape[1], width), bf16) for units, _ in fill]
    scratch = []
    for units, rows in fill:
        scratch += [pltpu.VMEM(units.shape, bf16), pltpu.VMEM((rows.shape[0], width), bf16)]
    return args, outs, scratch


def own_grads(count, args, outs, scratch):
    return [
        OwnGrad(args[2 * k], args[2 * k + 1], outs[k], scratch[2 * k], scratch[2 * k + 1])
        for k in range(count)
    ]


def meet(devices):
    barrier = pltpu.get_barrier_semaphore()
    for device in devices:
        pl.semaphore_signal(barrier, inc=1, device_id=device, device_id_type=pl.DeviceIdType.MESH)
    pl.semaphore_wait(barrier, len(devices))


def partners():
    c, t = lax.axis_index("context"), lax.axis_index("tensor")
    flip = lambda x, bit: x + bit * (1 - 2 * lax.rem(x // bit, 2))
    return {
        "core": {"tensor": flip(t, 1)},
        "y": {"tensor": flip(t, 2)},
        "z": {"context": flip(c, 1)},
        "far": {"context": flip(c, 2)},
        "last": {"context": flip(flip(c, 1), 2)},
    }


def wide(x):
    return x.astype(f32)


def ranks():
    t = lax.axis_index("tensor")
    flip = lambda x, bit: x + bit * (1 - 2 * lax.rem(x // bit, 2))
    return (t, flip(t, 1), flip(t, 2), flip(flip(t, 1), 2))


def scatter_rank(wires, to, part, own, got_core, sent, got_y):
    size = part.shape[1] // 2
    halves = [pl.ds(0, size), pl.ds(size, size)]
    rank = ranks()
    from_core = {}
    for block in (1, 0):
        for k, at in enumerate(halves):
            from_core[block, k] = wires.copy(
                part.at[rank[1 + 2 * block], at], got_core.at[block, at], to["core"]
            )
    mine = [wires.here(part.at[rank[2 * block]], own.at[block]) for block in (0, 1)]
    yield
    for one in mine:
        one.wait()
    from_y = []
    for k, at in enumerate(halves):
        from_core[1, k].wait_recv()
        sent[at] = (wide(own[1, at]) + wide(got_core[1, at])).astype(bf16)
        from_y.append(wires.copy(sent.at[at], got_y.at[at], to["y"]))
    yield
    for k in range(2):
        from_core[0, k].wait_recv()
    total = wide(own[0]) + wide(got_core[0])
    for one in from_y:
        one.wait_recv()
    return total + wide(got_y[...])


def scatter_pair(wires, to, part, own, got_core, sent, got_y, got_z, diag_y, diag_z):
    size = part.shape[1] // 2
    low, high = pl.ds(0, size), pl.ds(size, size)
    from_core = {j: wires.copy(part.at[4 + j], got_core.at[j], to["core"]) for j in (3, 1, 2, 0)}
    mine = wires.here(part.at[pl.ds(0, 4)], own)
    yield
    mine.wait()
    both = lambda j, at: wide(own[j, at]) + wide(got_core[j, at])
    from_core[3].wait_recv()
    sent[2] = (wide(own[3]) + wide(got_core[3])).astype(bf16)
    via_z = wires.copy(sent.at[2, low], diag_z, to["z"])
    via_y = wires.copy(sent.at[2, high], diag_y, to["y"])
    from_core[1].wait_recv()
    sent[0, high] = both(1, high).astype(bf16)
    y_high = wires.copy(sent.at[0, high], got_y.at[high], to["y"])
    from_core[2].wait_recv()
    sent[1, low] = both(2, low).astype(bf16)
    z_low = wires.copy(sent.at[1, low], got_z.at[low], to["z"])
    yield
    via_z.wait_recv()
    sent[0, low] = (both(1, low) + wide(diag_z[...])).astype(bf16)
    y_low = wires.copy(sent.at[0, low], got_y.at[low], to["y"])
    via_y.wait_recv()
    sent[1, high] = (both(2, high) + wide(diag_y[...])).astype(bf16)
    z_high = wires.copy(sent.at[1, high], got_z.at[high], to["z"])
    yield
    from_core[0].wait_recv()
    total = wide(own[0]) + wide(got_core[0])
    for one in (y_high, z_low, y_low, z_high):
        one.wait_recv()
    return total + wide(got_y[...]) + wide(got_z[...])


def result_of(steps):
    while True:
        try:
            next(steps)
        except StopIteration as done:
            return done.value


def gather_rank(wires, to, block, out):
    size = block.shape[0] // 2
    halves = [pl.ds(0, size), pl.ds(size, size)]
    rank = ranks()
    mine = wires.here(block, out.at[rank[0]])
    from_y = [wires.copy(block.at[h], out.at[rank[0], h], to["y"]) for h in halves]
    from_core = [wires.copy(block, out.at[rank[0]], to["core"])]
    yield
    for h, one in zip(halves, from_y):
        one.wait_recv()
        from_core.append(wires.copy(out.at[rank[2], h], out.at[rank[2], h], to["core"]))
    for one in from_core:
        one.wait_recv()
    mine.wait()


def gather_pair(wires, to, block, out, base):
    size = block.shape[0] // 2
    low, high = pl.ds(0, size), pl.ds(size, size)
    at = lambda j: out.at[base + j]
    from_z = wires.copy(block, at(2), to["z"])
    yield
    from_y = wires.copy(block, at(1), to["y"])
    from_core = [wires.copy(block, at(4), to["core"])]
    yield
    from_y.wait_recv()
    via_z = wires.copy(out.at[base + 1, low], out.at[base + 3, low], to["z"])
    from_core.append(wires.copy(at(1), at(5), to["core"]))
    from_z.wait_recv()
    via_y = wires.copy(out.at[base + 2, high], out.at[base + 3, high], to["y"])
    from_core.append(wires.copy(at(2), at(6), to["core"]))
    yield
    via_z.wait_recv()
    via_y.wait_recv()
    from_core.append(wires.copy(at(3), at(7), to["core"]))
    return from_core


def remote_call(kernel, name, key, args, outs, scratch, copies, in_vmem):
    ins, out_in = in_vmem
    spec = lambda inside: pl.BlockSpec(memory_space=pltpu.VMEM if inside else pl.ANY)
    return pl.pallas_call(
        kernel,
        name=name,
        out_shape=outs,
        in_specs=[spec(x) for x in ins],
        out_specs=[spec(x) for x in out_in],
        scratch_shapes=list(scratch)
        + [
            pltpu.SemaphoreType.DMA((copies,)),
            pltpu.SemaphoreType.DMA((copies,)),
            pltpu.SemaphoreType.DMA((10,)),
        ],
        compiler_params=pltpu.CompilerParams(
            collective_id=key, has_side_effects=True, vmem_limit_bytes=VMEM_LIMIT
        ),
    )(*args)


def kv_gather_kernel(own_ref, out_ref, *sems):
    wires, to = Wires(*sems), partners()
    kind = lax.rem(lax.axis_index("tensor"), 2)
    rows = own_ref.shape[0]
    block = lambda j: out_ref.at[kind, pl.ds(j * rows, rows)]
    meet([to[k] for k in ("core", "z", "far", "last")])
    mine = wires.here(own_ref, block(0))
    arrive = [wires.copy(own_ref, block(j), to[k]) for j, k in ((3, "last"), (2, "far"), (1, "z"))]
    from_core = [wires.copy(own_ref, block(0), to["core"])]
    for j, one in ((1, arrive[2]), (2, arrive[1]), (3, arrive[0])):
        one.wait_recv()
        from_core.append(wires.copy(block(j), block(j), to["core"]))
    for one in from_core:
        one.wait_recv()
    mine.wait()
    wires.finish()


def kv_gather(own):
    rows, width = own.shape
    n_c = lax.axis_size("context")
    return remote_call(
        kv_gather_kernel,
        "kv_gather",
        0,
        [own],
        [jax.ShapeDtypeStruct((2, n_c * rows, width), bf16)],
        [],
        8,
        ([False], [False]),
    )[0]


def kv_scatter_kernel(count, part_ref, *refs):
    args, dkv_ref, outs = refs[: 2 * count], refs[2 * count], refs[2 * count + 1 : 3 * count + 1]
    own, got_core, sent, got = refs[3 * count + 1 : 3 * count + 5]
    wires, to = Wires(*refs[-3:]), partners()
    fill = own_grads(count, args, outs, refs[3 * count + 5 : -3])
    kind = lax.rem(lax.axis_index("tensor"), 2)
    rows = dkv_ref.shape[0]
    block = lambda j: pl.ds(j * rows, rows)
    meet([to[k] for k in ("core", "z", "far", "last")])
    steps = ((3, "last"), (2, "far"), (1, "z"), (0, None))
    from_core = {
        j: wires.copy(part_ref.at[1 - kind, block(j)], got_core.at[block(j)], to["core"])
        for j, _ in steps
    }
    mine = wires.here(part_ref.at[kind], own)
    for one in fill:
        one.fetch(wires)
    mine.wait()
    arrive = []
    for j, k in steps[:3]:
        from_core[j].wait_recv()
        sent[block(j)] = (wide(own[block(j)]) + wide(got_core[block(j)])).astype(bf16)
        arrive.append(wires.copy(sent.at[block(j)], got.at[block(j)], to[k]))
    for one in fill:
        one.make(0, one.tiles)
    from_core[0].wait_recv()
    total = wide(own[block(0)]) + wide(got_core[block(0)])
    for one in arrive:
        one.wait_recv()
    for j in (1, 2, 3):
        total = total + wide(got[block(j)])
    dkv_ref[...] = total
    wires.finish()


def kv_scatter(part, fill, width):
    _, rows, depth = part.shape
    n_c = lax.axis_size("context")
    args, outs, scratch = own_grad_call(fill, width)
    return remote_call(
        functools.partial(kv_scatter_kernel, len(fill)),
        "kv_scatter",
        1,
        [part, *args],
        [jax.ShapeDtypeStruct((rows // n_c, depth), f32), *outs],
        [pltpu.VMEM((rows, depth), bf16)] * 4 + scratch,
        7,
        ([False] * (1 + len(args)), [True] * (1 + len(outs))),
    )


def middle_kernel(
    part,
    x_ref,
    gain_ref,
    dy_ref,
    dy_y,
    dy_z,
    dy_far,
    mid_ref,
    factor_ref,
    out,
    dys,
    own,
    core,
    sent,
    got,
    xn,
    *sems,
):
    wires, to = Wires(*sems), partners()
    blocks = out.shape[0] // 2
    size = xn.shape[0] // 2
    low, high = pl.ds(0, size), pl.ds(size, size)
    meet([to[k] for k in ("core", "y", "z", "far")])
    summed = scatter_rank(wires, to, part, own, core, sent, got)
    next(summed)
    mine = [
        wires.here(block, dys.at[k])
        for block, k in ((dy_ref, 0), (dy_y, 1), (dy_z, 2), (dy_far, blocks))
    ]
    via_z = wires.copy(dy_y.at[low], dys.at[3, low], to["z"])
    dy_last = gather_pair(wires, to, dy_far, dys, blocks)
    next(dy_last)
    next(summed)
    via_y = wires.copy(dy_z.at[high], dys.at[3, high], to["y"])
    ends = [
        wires.copy(block, dys.at[4 + k], to["core"])
        for k, block in enumerate((dy_ref, dy_y, dy_z))
    ]
    next(dy_last)
    middle = wide(x_ref[...]) + result_of(summed)
    mid_ref[...] = middle
    factor = lax.rsqrt(jnp.mean(middle * middle, axis=-1, keepdims=True) + EPSILON)
    factor_ref[...] = factor
    xn[...] = (middle * factor * gain_ref[...]).astype(bf16)
    mine.append(wires.here(xn, out.at[0]))
    xn_far = wires.copy(xn, out.at[blocks], to["far"])
    xn_near = gather_pair(wires, to, xn, out, 0)
    next(xn_near)
    next(xn_near)
    via_z.wait_recv()
    via_y.wait_recv()
    ends.append(wires.copy(dys.at[3], dys.at[7], to["core"]))
    next(dy_last)
    next(xn_near)
    xn_far.wait_recv()
    xn_last = gather_pair(wires, to, out.at[blocks], out, blocks)
    next(xn_last)
    next(xn_last)
    ends += result_of(dy_last) + result_of(xn_near)
    next(xn_last)
    ends += result_of(xn_last)
    for one in ends:
        one.wait_recv()
    for one in mine:
        one.wait()
    wires.finish()


def middle_norm(part, inputs_part, gain, dy_blocks):
    rows, width = inputs_part.shape
    return remote_call(
        middle_kernel,
        "middle_norm",
        2,
        [part.reshape(4, rows, width), inputs_part, gain, *dy_blocks],
        [
            jax.ShapeDtypeStruct((rows, width), f32),
            jax.ShapeDtypeStruct((rows, 1), f32),
            jax.ShapeDtypeStruct((16, rows, width), bf16),
            jax.ShapeDtypeStruct((16, rows, width), bf16),
        ],
        [
            pltpu.VMEM((2, rows, width), bf16),
            pltpu.VMEM((2, rows, width), bf16),
            pltpu.VMEM((rows, width), bf16),
            pltpu.VMEM((rows, width), bf16),
            pltpu.VMEM((rows, width), bf16),
        ],
        48,
        ([False] + [True] * 6, [True, True, False, False]),
    )


def norm_back_rows(values, factor, gain, grad_normed):
    gained = gain * grad_normed
    inner = jnp.mean(gained * values, axis=-1, keepdims=True)
    grad_values = factor * gained - values * (factor * factor * factor) * inner
    return grad_values, jnp.sum(grad_normed * values * factor, axis=0, keepdims=True)


def middle_back_kernel(count, part, mid_ref, factor_ref, gain_ref, dy_ref, *refs):
    args, refs = refs[: 2 * count], refs[2 * count :]
    source_ref, refs = (refs[0], refs[1:]) if count else (None, refs)
    (dmid_ref, dgain_ref, out), refs = refs[:3], refs[3:]
    outs, refs = refs[:count], refs[count:]
    (upper_ref, lower_ref, far_ref), refs = (
        (refs[:3], refs[3:]) if count else ((None, None, None), refs)
    )
    low, first, wires, to = refs[0], refs[1:8], Wires(*refs[-3:]), partners()
    fill = own_grads(count, args, outs, refs[8 : 8 + 2 * count])
    meet([to[k] for k in ("core", "y", "z")])
    back = scatter_pair(wires, to, part, *first)
    next(back)
    for one in fill:
        one.fetch(wires)
    if fill:
        got_ref = refs[8 + 2 * count]
        fetched = wires.here(source_ref, got_ref)
    next(back)
    if fill:
        fill[0].make(0, 1)
    next(back)
    if fill:
        fill[0].make(1, fill[0].tiles)
        fetched.wait()
        cut = upper_ref.shape[0]
        upper_ref[...] = (wide(outs[0][:cut]) + wide(got_ref[:cut])).astype(bf16)
        near_half = wires.copy(upper_ref, far_ref, to["z"])
        lower_ref[...] = (wide(outs[0][cut:]) + wide(got_ref[cut:])).astype(bf16)
    grad_normed = result_of(back)
    du, dgain = norm_back_rows(mid_ref[...], factor_ref[...], gain_ref[...], grad_normed)
    dgain_ref[...] = dgain
    dmid = wide(dy_ref[...]) + du
    low[...] = dmid.astype(bf16)
    share = gather_rank(wires, to, low, out)
    next(share)
    dmid_ref[...] = dmid
    for one in fill[1:]:
        one.make(0, one.tiles)
    result_of(share)
    if fill:
        near_half.wait_recv()
    wires.finish()


def pair_scratch(rows, width):
    return [
        pltpu.VMEM((4, rows, width), bf16),
        pltpu.VMEM((4, rows, width), bf16),
        pltpu.VMEM((3, rows, width), bf16),
        pltpu.VMEM((rows, width), bf16),
        pltpu.VMEM((rows, width), bf16),
        pltpu.VMEM((rows // 2, width), bf16),
        pltpu.VMEM((rows // 2, width), bf16),
    ]


def middle_back(part, middle, factor, gain, dy_part, fill, got, shard):
    rows, width = middle.shape
    args, outs, scratch = own_grad_call(fill, shard)
    if fill:
        args = [*args, got]
        scratch = [*scratch, pltpu.VMEM(got.shape, bf16)]
        units = got.shape[0]
        cut = units // 64 * 16
        outs = [*outs, *(jax.ShapeDtypeStruct((n, shard), bf16) for n in (cut, units - cut, cut))]
    return remote_call(
        functools.partial(middle_back_kernel, len(fill)),
        "middle_back",
        3,
        [part.reshape(8, rows, width), middle, factor, gain, dy_part, *args],
        [
            jax.ShapeDtypeStruct((rows, width), f32),
            jax.ShapeDtypeStruct((1, width), f32),
            jax.ShapeDtypeStruct((4, rows, width), bf16),
            *outs,
        ],
        [pltpu.VMEM((rows, width), bf16)] + pair_scratch(rows, width) + scratch,
        16,
        (
            [False] + [True] * 4 + [False] * len(args),
            [True, True, False] + ([True] * (len(outs) - 1) + [False] if fill else []),
        ),
    )


def add_all(wires, ways, value, slots):
    for k, device in enumerate(ways):
        one = wires.copy(value, slots.at[k], device)
        one.wait()
        wires.started = [x for x in wires.started if x is not one]
        value[...] = value[...] + slots[k]


def input_back_kernel(
    part, x_ref, gain_ref, dmid_ref, small_ref, sum_ref, out, *rest
):
    low, own, core, sent, got, slots = rest[:-3]
    wires, to = Wires(*rest[-3:]), partners()
    meet([to[k] for k in ("core", "y")])
    grad_normed = result_of(scatter_rank(wires, to, part, own, core, sent, got))
    values = wide(x_ref[...])
    factor = lax.rsqrt(jnp.mean(values * values, axis=-1, keepdims=True) + EPSILON)
    du, dgain = norm_back_rows(values, factor, gain_ref[...], grad_normed)
    low[...] = (dmid_ref[...] + du).astype(bf16)
    share = gather_rank(wires, to, low, out)
    next(share)
    width = dgain.shape[1]
    sum_ref[:, width:] = small_ref[:, width:]
    sum_ref[:, :width] = dgain
    add_all(wires, [to["core"], to["y"]], sum_ref, slots)
    result_of(share)
    wires.finish()


def input_back(part, inputs_part, gain, grad_middle, small):
    rows, width = inputs_part.shape
    return remote_call(
        input_back_kernel,
        "input_back",
        5,
        [part.reshape(4, rows, width), inputs_part, gain, grad_middle, small],
        [
            jax.ShapeDtypeStruct(small.shape, f32),
            jax.ShapeDtypeStruct((4, rows, width), bf16),
        ],
        [
            pltpu.VMEM((rows, width), bf16),
            pltpu.VMEM((2, rows, width), bf16),
            pltpu.VMEM((2, rows, width), bf16),
            pltpu.VMEM((rows, width), bf16),
            pltpu.VMEM((rows, width), bf16),
            pltpu.VMEM((2,) + small.shape, f32),
        ],
        16,
        ([False, True, True, True, True], [True, False]),
    )


def context_sum_kernel(over_f, *refs):
    parts, small_ref, out_part, mid_ref = refs[:3], refs[3], refs[4], refs[5]
    outs, sum_ref, shared, outputs = refs[6:8], refs[8], refs[9], refs[10]
    lows, from_end, from_middle = refs[11:15], refs[15:19], refs[19:23]
    out_low, slot, scratch = refs[23], refs[24], refs[25:32]
    wires, to, c = Wires(*refs[32:]), partners(), lax.axis_index("context")
    end = (c == 0) | (c == lax.axis_size("context") - 1)
    inner = jnp.logical_not(end)
    greet = ["core", "y", "z", "last"]
    if over_f:
        to["f"] = {"fsdp": 1 - lax.axis_index("fsdp")}
        greet.append("f")
    meet([to[k] for k in greet])
    ahead = scatter_pair(wires, to, out_part, *scratch)
    next(ahead)
    sum_ref[...] = small_ref[...]
    from_f = wires.copy(small_ref, slot, to["f"]) if over_f else None
    sources = [*parts, sum_ref]
    chunks = []
    for i, cuts in ((2, 1), (0, 2), (1, 4), (3, 1)):
        size = sources[i].shape[0] // cuts
        chunks += [(i, pl.ds(k * size, size)) for k in range(cuts)]
    inward = [wires.plan(sources[i].at[at], from_end[i].at[at], to["z"]) for i, at in chunks]
    across = [wires.plan(lows[i].at[at], from_middle[i].at[at], to["last"]) for i, at in chunks]
    outward = [wires.plan(lows[i].at[at], lows[i].at[at], to["z"]) for i, at in chunks]
    small = len(chunks) - 1

    def send_in(k):
        @pl.when(end)
        def _():
            inward[k].start()

    def pass_on(first, past):
        @pl.when(inner)
        def _():
            for k in range(first, past):
                i, at = chunks[k]
                inward[k].wait_recv()
                total = wide(sources[i][at]) + wide(from_end[i][at])
                lows[i][at] = total.astype(lows[i].dtype)
                across[k].start()
                if k:
                    send_out(k - 1)

    def send_out(k):
        i, at = chunks[k]
        across[k].wait()
        lows[i][at] = (wide(lows[i][at]) + wide(from_middle[i][at])).astype(lows[i].dtype)
        outward[k].start()

    early, late = 3, 5
    for k in range(early):
        send_in(k)
    next(ahead)
    for k in range(early, late):
        send_in(k)
    pass_on(0, early)
    next(ahead)
    if over_f:
        from_f.wait_recv()
        sum_ref[...] = sum_ref[...] + slot[...]
    for k in range(late, small + 1):
        send_in(k)
    pass_on(early, late)
    out_low[...] = (mid_ref[...] + result_of(ahead)).astype(bf16)
    out_share = gather_rank(wires, to, out_low, outputs)
    next(out_share)
    pass_on(late, small + 1)

    @pl.when(inner)
    def _():
        send_out(small)

    result_of(out_share)

    def arrived(k):
        @pl.when(end)
        def _():
            outward[k].wait_recv()

    arrived(0)
    share = gather_rank(wires, to, lows[2], shared)
    next(share)
    for k in range(1, len(chunks)):
        arrived(k)

    @pl.when(end)
    def _():
        for one in inward:
            one.wait_send()

    for i in (0, 1):
        outs[i][...] = wide(lows[i][...])
    sum_ref[...] = lows[3][...]
    result_of(share)

    @pl.when(inner)
    def _():
        for one in outward:
            one.wait_send()

    wires.finish()


def context_sum(over_f, parts, small, out_part, middle):
    rows, width = middle.shape
    lines = [pltpu.VMEM(x.shape, x.dtype) for x in (*parts, small)]
    return remote_call(
        functools.partial(context_sum_kernel, over_f),
        "context_sum",
        6,
        [*parts, small, out_part.reshape(8, rows, width), middle],
        [jax.ShapeDtypeStruct(x.shape, f32) for x in parts[:2]]
        + [jax.ShapeDtypeStruct(small.shape, f32)]
        + [jax.ShapeDtypeStruct((4,) + parts[2].shape, bf16)]
        + [jax.ShapeDtypeStruct((4, rows, width), bf16)],
        lines * 3
        + [pltpu.VMEM((rows, width), bf16), pltpu.VMEM(small.shape, f32)]
        + pair_scratch(rows, width),
        48,
        ([True] * 4 + [False, True], [True] * 3 + [False] * 2),
    )


def build(n_f, n_c, n_t):
    def flip(x, axis, bit):
        size = {"fsdp": n_f, "context": n_c, "tensor": n_t}[axis]
        return lax.ppermute(x, axis, [(i, i ^ bit) for i in range(size)])

    def by_bit(bit, x, other, axis):
        return jnp.where(
            bit == 0,
            jnp.concatenate([x, other], axis=axis),
            jnp.concatenate([other, x], axis=axis),
        )

    def after(x, *others):
        return lax.optimization_barrier((x, others))[0]

    def local(
        inputs,
        cotangent,
        blocks,
        attn_gain,
        w_query,
        b_query,
        w_key,
        b_key,
        w_value,
        b_value,
        w_out,
        ffn_gain,
        w_gate,
        w_up,
        w_down,
    ):
        rows, width = inputs.shape
        f = lax.axis_index("fsdp")
        c = lax.axis_index("context")
        t = lax.axis_index("tensor")
        core, parity, pair = t % 2, c % 2, c // 2
        heads = w_query.shape[1] // HD
        group = (t * heads) // (H // KV)
        part = rows // n_t
        units_all = w_gate.shape[1]
        units = units_all // 2

        def gather_f(x, axis):
            if n_f == 2:
                return by_bit(f, x, flip(x, "fsdp", 1), axis)
            return lax.all_gather(x, "fsdp", axis=axis, tiled=True)

        def grad_far(left, right, side):
            if n_f > 2:
                return None
            source = (left, right)[side]
            half = width // 2
            far = lax.dynamic_slice_in_dim(source, (1 - f) * half, half, 1)
            return (dot_rows(far, right) if side == 0 else dot_rows(left, far)).astype(bf16)

        def grad_sum(left, right, side, far, late):
            if n_f > 2:
                return lax.psum_scatter(
                    dot_rows(left, right).astype(bf16), "fsdp", scatter_dimension=side, tiled=True
                )
            source = (left, right)[side]
            half = width // 2
            own = lax.dynamic_slice_in_dim(source, f * half, half, 1)
            own = dot_rows(own, right) if side == 0 else dot_rows(left, own)
            return (own + after(flip(far, "fsdp", 1), late).astype(f32)).astype(bf16)

        small = jnp.concatenate(
            [v.reshape(1, -1) for v in (attn_gain, ffn_gain, b_query, b_key, b_value)], axis=1
        )
        column = lambda w: lax.dynamic_slice_in_dim(w, group * HD, HD, 1)
        w_kv_own = jnp.where(core == 0, column(w_key), column(w_value))
        pieces_f = lambda x, axis: (
            [x, flip(x, "fsdp", 1)]
            if n_f == 2
            else [lax.all_gather(x, "fsdp", axis=axis, tiled=True)]
        )
        meta = jnp.stack([f, 1 - f, core, pair]).astype(jnp.int32)
        w_q = pieces_f(w_query, 0)
        w_kv = pieces_f(w_kv_own, 0)
        small = gather_f(small, 0)
        w_out_all = gather_f(after(w_out, small, w_q, w_kv), 1)
        piece = attn_gain.shape[0]
        gain_first = small[:, :piece].reshape(1, width).astype(f32)
        gain_second = small[:, piece : 2 * piece].reshape(1, width).astype(f32)
        bias_of = lambda lo, n: (
            small[:, lo : lo + n * (HD // n_f)]
            .reshape(n_f, n, HD // n_f)
            .transpose(1, 0, 2)
            .reshape(n, HD)
            .astype(f32)
        )
        at = 2 * piece
        bq = bias_of(at, heads)
        bk = bias_of(at + heads * (HD // n_f), KV)
        bv = bias_of(at + (heads + KV) * (HD // n_f), KV)
        b_kv = lax.dynamic_index_in_dim(jnp.where(core == 0, bk, bv), group, 0)

        unit_slice = lambda w: lax.dynamic_slice_in_dim(w, parity * units, units, 0)
        own_gate_up = jnp.concatenate(
            [unit_slice(after(w, w_kv_own)) for w in (w_gate.T, w_up.T)], axis=0
        )
        own_down = unit_slice(w_down)

        dy_part = lax.dynamic_slice_in_dim(cotangent, t * part, part, 0)

        seq_blocks = blocks[0].reshape(n_c, -1)
        own_blocks = seq_blocks.shape[1]
        key_blocks = jnp.concatenate(
            [lax.dynamic_index_in_dim(seq_blocks, c ^ j, 0, keepdims=False) for j in range(n_c)]
        )
        positions = (
            key_blocks[:own_blocks, None] * BLOCK + jnp.arange(BLOCK, dtype=jnp.int32)[None, :]
        ).reshape(-1)
        cosine, sine = rope_tables(positions)
        bias = jnp.concatenate([bq.reshape(1, -1), b_kv], axis=1)
        dy_blocks = [
            dy_part,
            flip(dy_part, "tensor", 2),
            flip(dy_part, "context", 1),
            flip(dy_part, "context", 2),
        ]
        inputs_part = lax.dynamic_slice_in_dim(inputs, t * part, part, 0)
        bias = after(bias, dy_blocks[2:], own_gate_up, own_down, inputs_part)
        normed, queries, kv_own = qkv(
            meta, inputs, gain_first, bias, cosine, sine, w_q, w_kv
        )
        kv = after(kv_gather(kv_own), w_out_all)
        far_gate_up = pieces_f(after(own_gate_up, kv), 1)[-1]
        w_gate_up = [own_gate_up, far_gate_up] if n_f == 2 else [far_gate_up]
        far_down = pieces_f(after(own_down, kv), 1)[-1]
        w_downs = [own_down, far_down] if n_f == 2 else [far_down]
        attended, lse = attention(key_blocks, queries, kv)
        middle, factor_second, normed2, dy_all = middle_norm(
            dot(attended, w_out_all).astype(bf16), inputs_part, gain_second, dy_blocks
        )

        hidden, slope, gated, *down_far = hidden_units(meta, normed2, dy_all, w_gate_up)
        grad_gate, grad_up, dx_part, out_part, *unit_far = hidden_back(
            meta, normed2, dy_all, hidden, slope, gated, w_gate_up, w_downs
        )
        unit_far = [*down_far, *unit_far]
        flat = lambda x: x.reshape(-1, width)
        if n_f == 2:
            down_got, gate_got, up_got = (flip(x, "fsdp", 1) for x in unit_far)
            early = [(hidden, flat(dy_all)), (grad_gate, flat(normed2))]
            later = [(grad_up, flat(normed2))]
        else:
            over_f = lambda x: lax.psum_scatter(x, "fsdp", scatter_dimension=1, tiled=True)
            owns = [
                over_f(unit_grads(meta, 0, 1, x, [unit]))
                for x, unit in ((dy_all, hidden), (normed2, grad_gate), (normed2, grad_up))
            ]
            down_got = gate_got = up_got = jnp.zeros_like(owns[0])
            early = later = []

        def unit_whole(own, other):
            own, other = (jnp.concatenate(x, axis=0) for x in (own, other))
            return by_bit(parity, own, other, 0).astype(f32)

        grad_middle, ffn_gain_grad, grad_middle_low, *first_owns = middle_back(
            dx_part, middle, factor_second, gain_second, dy_part, early, down_got, width // n_f
        )
        grad_middle_low = grad_middle_low.reshape(rows, width)
        add = lambda own, got: (own.astype(f32) + got.astype(f32)).astype(bf16)
        upper = units // 2
        if n_f == 2:
            _, gate_own, down_upper, down_lower, far_upper = first_owns
        else:
            down_low, gate_own = owns[:2]
            down_upper, down_lower = down_low[:upper], down_low[upper:]
            far_upper = flip(down_upper, "context", 1)
        far_lower = flip(down_lower, "context", 1)
        grad_attended = dot_cols(grad_middle_low, w_out_all).astype(bf16)
        gate_low = add(gate_own, after(gate_got, grad_attended))
        grad_attended = after(grad_attended, gate_low)

        dq_low, dkv = attention_back(key_blocks, queries, grad_attended, lse, cosine, sine, kv)
        attention_args = [(attended, after(grad_middle_low, dq_low), 1), (normed, dq_low, 0)]
        fars = [grad_far(*args) for args in attention_args]
        dkv, *last_owns = kv_scatter(
            after(dkv, fars), later, width // n_f
        )
        (up_own,) = last_owns or owns[2:]
        far_gate = flip(after(gate_low, dkv, far_lower), "context", 1)
        dkv = after(dkv, far_lower)
        dkv_low = jnp.where(core == 0, rotate_back(dkv, cosine, sine), dkv).astype(bf16)
        own_biases = jnp.sum(
            jnp.concatenate([dq_low, dkv_low], axis=1).astype(f32), axis=0, keepdims=True
        )
        slots = lax.dynamic_update_slice(
            jnp.zeros((n_t, (heads + 1) * HD), f32), own_biases, (t, 0)
        )
        small_grads = jnp.concatenate(
            [jnp.zeros((1, width), f32), ffn_gain_grad, slots.reshape(1, -1)], axis=1
        )
        grad_qkv = qkv_back(meta, dq_low, dkv_low, w_q, w_kv)
        up_low = add(up_own, after(up_got, grad_qkv))
        attention_args.append((after(normed, grad_qkv), dkv_low, 0))
        fars.append(grad_far(*attention_args[-1]))
        far_up = flip(up_low, "context", 1)
        small_grads, input_grad = input_back(
            after(grad_qkv, up_low, fars),
            inputs_part,
            gain_first,
            grad_middle,
            small_grads,
        )
        input_grad = input_grad.reshape(rows, width)
        if n_f > 2:
            small_grads = lax.psum(small_grads, "fsdp")
        zero = jnp.minimum(t, 0).astype(bf16)
        input_grad = input_grad + zero
        small_grads = after(small_grads, far_gate)
        attention_parts = [
            grad_sum(*args, far, small_grads) for args, far in zip(attention_args, fars)
        ]
        wd_grad = unit_whole(
            *after(((down_upper, down_lower), (far_upper, far_lower)), small_grads)
        )
        wg_grad = unit_whole(*after(((gate_low,), (far_gate,)), small_grads))
        small_grads, wd_grad, wg_grad, input_grad = lax.optimization_barrier(
            (small_grads, wd_grad, wg_grad, input_grad)
        )
        wo_grad, wq_grad, packed, wkv_all, outputs = context_sum(
            n_f == 2, attention_parts, small_grads, out_part, middle
        )
        wo_grad, wq_grad, packed, wkv_all, outputs, far_up = lax.optimization_barrier(
            (wo_grad, wq_grad, packed, wkv_all, outputs, far_up)
        )
        outputs = outputs.reshape(rows, width)
        wk_grad = jnp.concatenate([wkv_all[0], wkv_all[2]], axis=1).astype(f32)
        wv_grad = jnp.concatenate([wkv_all[1], wkv_all[3]], axis=1).astype(f32)
        packed = packed[0]
        attn_gain_grad = lax.dynamic_slice_in_dim(packed, f * piece, piece, 0)
        ffn_gain_grad = lax.dynamic_slice_in_dim(packed, width + f * piece, piece, 0)
        slots = packed[2 * width :].reshape(n_t, heads + 1, HD)
        slots = lax.dynamic_slice_in_dim(slots, f * (HD // n_f), HD // n_f, 2)
        bq_out = lax.dynamic_index_in_dim(slots, t, 0, keepdims=False)[:heads]
        bk_out = slots[0::2, heads]
        bv_out = slots[1::2, heads]

        wu_grad = unit_whole((up_low,), (far_up,))
        wg_grad, wu_grad = wg_grad.T, wu_grad.T

        return (
            outputs,
            input_grad,
            attn_gain_grad,
            wq_grad,
            bq_out,
            wk_grad,
            bk_out,
            wv_grad,
            bv_out,
            wo_grad,
            ffn_gain_grad,
            wg_grad,
            wu_grad,
            wd_grad,
        )

    return local


def solution(mesh):
    in_specs = (
        P(("fsdp", "context"), None),
        P(("fsdp", "context"), None),
        P("fsdp", None),
        P("fsdp"),
        P("fsdp", "tensor"),
        P("tensor", "fsdp"),
        P("fsdp", None),
        P(None, "fsdp"),
        P("fsdp", None),
        P(None, "fsdp"),
        P("tensor", "fsdp"),
        P("fsdp"),
        P("fsdp", "tensor"),
        P("fsdp", "tensor"),
        P("tensor", "fsdp"),
    )
    out_specs = (
        P(("fsdp", "context"), None),
        P(("fsdp", "context"), None),
        P("fsdp"),
        P("fsdp", "tensor"),
        P("tensor", "fsdp"),
        P("fsdp", None),
        P(None, "fsdp"),
        P("fsdp", None),
        P(None, "fsdp"),
        P("tensor", "fsdp"),
        P("fsdp"),
        P("fsdp", "tensor"),
        P("fsdp", "tensor"),
        P("tensor", "fsdp"),
    )
    local = build(mesh.shape["fsdp"], mesh.shape["context"], mesh.shape["tensor"])
    return jax.shard_map(local, mesh=mesh, in_specs=in_specs, out_specs=out_specs, check_vma=False)
```
